32 devices in a mesh: dp: 8 (over y, x, core), mp: 4 (over z).
Axes of the slice: x: 2, y: 2, z: 4, core: 2. Of those that a mesh axis runs over, the one named last changes fastest.
Arguments:
- tokens: bfloat16 [12288, 1792], P(('dp', 'mp')), may hold values from -6 to 6
- cotangent: bfloat16 [12288, 1792], P(('dp', 'mp')), may hold values from -6 to 6
- route: int32 [12288], P(('dp', 'mp')), may hold values from 0 to 12287, as said below
- lengths: int32 [8, 3], P('dp'), may hold values from 1 to 1024, 1536 in all within a row
- key_mask: int32 [12288], P('dp'), may hold values 0 or 1
- norm1_gain: float32 [1792], replicated, may hold values from 0.1 to 1.9
- norm2_gain: float32 [1792], replicated, may hold values from 0.1 to 1.9
- w_query: bfloat16 [1792, 1792], P(None, 'mp'), may hold values from -0.1875 to 0.1875
- w_key: bfloat16 [1792, 1792], P(None, 'mp'), may hold values from -0.1875 to 0.1875
- w_value: bfloat16 [1792, 1792], P(None, 'mp'), may hold values from -0.125 to 0.125
- w_out: bfloat16 [1792, 1792], P('mp'), may hold values from -0.375 to 0.375
- w_gate: bfloat16 [1792, 4096], P(None, 'mp'), may hold values from -0.125 to 0.125
- w_up: bfloat16 [1792, 4096], P(None, 'mp'), may hold values from -0.125 to 0.125
- w_down: bfloat16 [4096, 1792], P('mp'), may hold values from -0.125 to 0.125
Outputs:
- output: bfloat16 [12288, 1792], P(('dp', 'mp'))
- input_grad: bfloat16 [12288, 1792], P(('dp', 'mp'))
- norm1_gain_grad: float32 [1792], replicated
- norm2_gain_grad: float32 [1792], replicated
- w_query_grad: float32 [1792, 1792], P(None, 'mp')
- w_key_grad: float32 [1792, 1792], P(None, 'mp')
- w_value_grad: float32 [1792, 1792], P(None, 'mp')
- w_out_grad: float32 [1792, 1792], P('mp')
- w_gate_grad: float32 [1792, 4096], P(None, 'mp')
- w_up_grad: float32 [1792, 4096], P(None, 'mp')
- w_down_grad: float32 [4096, 1792], P('mp')
The draws below stay inside these ranges and needn't reach their ends.
Inputs may be any that keep to these rules, and one draw needn't show every extreme that they name: route is a permutation of the 12288 slots. For every row r, slot s = route[r] lies on index s // 1536 of dp and on index (s // 384) % (number of mp indices) of mp, and that mp index equals the mp index of the device that holds row r in given order; every device holds exactly 48 rows bound for each index of dp. Each row of lengths sums to 1536; its largest entry is exactly 1024.
All inputs are finite; a program needn't handle non-finite values. No bound on the sum of `key_mask` on one device may be relied on, other than what follows from the above.
Results may differ from the reference program's by a relative error of at most 0.019.
Values may be sent and summed in bfloat16 or wider, within the bound.
A program may use at most 192 MiB of HBM per device.

```python
import math
import jax
import jax.numpy as jnp
import numpy as np
from jax import lax

D = 1792
HEADS = 16
HEAD_DIM = 112
FF = 4096
WINDOW = 64
SEQS = 3
TOK_DEV = 1536
MAX_LEN = 1024
GROUPS = 8
TOKENS = 12288
TM = 384
CAP = 48


def shuffle_rows(seed_key):
    return jax.random.permutation(seed_key, TM).astype(jnp.int32)


def draw_route(key, part):
    devices_all = TOKENS // TM
    members = TOK_DEV // TM
    groups = TOKENS // TOK_DEV
    first_key, second_key = jax.random.split(jax.random.fold_in(key, 17))
    dealing = jax.vmap(shuffle_rows)(jax.random.split(first_key, devices_all))
    placing = jax.vmap(shuffle_rows)(jax.random.split(second_key, devices_all))
    source = jnp.arange(devices_all, dtype=jnp.int32)[:, None]
    group = source // members
    member = source % members
    target = dealing % groups
    arrival = group * CAP + dealing // groups
    place = placing[target * members + member, arrival]
    return (target * TOK_DEV + member * TM + place).reshape(TOKENS).astype(jnp.int32)


def place_ends(values, stream_key, smallest, high):
    longest = values.shape.index(max(values.shape))
    spots = []
    for shift in (0, 1):
        where = [jax.random.randint(jax.random.fold_in(stream_key, axis), (), 0, length) for axis, length in enumerate(values.shape)]
        where[longest] = (where[longest] + shift) % values.shape[longest]
        spots.append(tuple(where))
    return values.at[spots[0]].set(smallest).at[spots[1]].set(high)


def block_levels(own_key, dims, cuts, least, high):
    def one(axis_at, blocks):
        steps = jax.random.uniform(jax.random.fold_in(jax.random.fold_in(own_key, 6), axis_at), (blocks,), jnp.float32, least / len(cuts), high / len(cuts))
        return jnp.repeat(jnp.exp(steps), dims[axis_at] // blocks).reshape((-1,) + (1,) * (len(dims) - axis_at - 1))

    loudness = one(*cuts[0])
    for cut in cuts[1:]:
        loudness = loudness * one(*cut)
    return loudness


def split_up(count, total, most, slope):
    weights = [(1 << 20) // math.isqrt(rank ** slope) + 1 for rank in range(2, count + 1)]
    surplus, holding = total - most - (count - 1), [1] * (count - 1)
    while surplus > 0:
        movable = [i for i in range(count - 1) if holding[i] < most]
        whole, budget = sum([weights[i] for i in movable]), surplus
        for i in movable:
            extra = min(most - holding[i], max(1, budget * weights[i] // whole), surplus)
            holding[i] = holding[i] + extra
            surplus = surplus - extra
    return np.array([most] + holding)


def ragged_sizes(stream_key, amount, total, bound, slope):
    if amount == 2:
        one = jax.random.randint(stream_key, (), max(1, total - bound), min(bound, total - 1) + 1)
        return jnp.stack([one, total - one])
    sizes = jnp.asarray(split_up(amount, total, bound, slope), jnp.int32)
    pairs = (amount - 1) // 2
    giver, taker = sizes[1:1 + 2 * pairs:2], sizes[2:2 + 2 * pairs:2]
    room = jnp.minimum(giver - 1, bound - taker)
    passed = jax.random.randint(jax.random.fold_in(stream_key, 1), (pairs,), 0, 1 << 20) % (room + 1)
    sizes = sizes.at[1:1 + 2 * pairs:2].set(giver - passed).at[2:2 + 2 * pairs:2].set(taker + passed)
    return sizes[jax.random.permutation(jax.random.fold_in(stream_key, 2), amount)]


def normal_values(stream_key, dims, deviation, bound, pieces=(), kind=jnp.bfloat16):
    values = jax.random.normal(stream_key, dims, jnp.float32) * deviation
    if len(pieces) > 0:
        values = block_levels(stream_key, dims, pieces, -0.22, 0.18) * values
    return jnp.clip(values, min=-bound, max=bound).astype(kind)


def setup_inputs(seed: int = 0) -> dict:
    splits = jax.random.split(jax.random.key(seed), 15)
    return {
        "tokens": normal_values(splits[0], (TOKENS, D), 1.0, 6.0, ((0, 32),)),
        "cotangent": normal_values(splits[1], (TOKENS, D), 1.0, 6.0, ((0, 32),)),
        "route": draw_route(jax.random.fold_in(splits[14], 71), 0),
        "lengths": jax.vmap(lambda own: ragged_sizes(own, SEQS, TOK_DEV, MAX_LEN, 2))(jax.random.split(splits[3], GROUPS)).reshape((GROUPS, SEQS)).astype(jnp.int32),
        "key_mask": place_ends((jax.random.randint(splits[4], (TOKENS,), 0, 8) < 7).astype(jnp.int32), jax.random.fold_in(splits[4], 1), 0, 1),
        "norm1_gain": jnp.clip(1.0 + 0.18 * jax.random.normal(splits[5], (D,), jnp.float32), 0.1, 1.9),
        "norm2_gain": jnp.clip(1.0 + 0.18 * jax.random.normal(splits[6], (D,), jnp.float32), 0.1, 1.9),
        "w_query": normal_values(splits[7], (D, HEADS * HEAD_DIM), (D // 2) ** -0.5, 0.1875, ((1, 4),)),
        "w_key": normal_values(splits[8], (D, HEADS * HEAD_DIM), (D // 2) ** -0.5, 0.1875, ((1, 4),)),
        "w_value": normal_values(splits[9], (D, HEADS * HEAD_DIM), D ** -0.5, 0.125, ((1, 4),)),
        "w_out": normal_values(splits[10], (HEADS * HEAD_DIM, D), (HEADS * HEAD_DIM // 8) ** -0.5, 0.375, ((0, 4),)),
        "w_gate": normal_values(splits[11], (D, FF), D ** -0.5, 0.125, ((1, 4),)),
        "w_up": normal_values(splits[12], (D, FF), D ** -0.5, 0.125, ((1, 4),)),
        "w_down": normal_values(splits[13], (FF, D), (FF // 2) ** -0.5, 0.125, ((0, 4),)),
    }


@jax.custom_vjp
def low(v):
    return lax.optimization_barrier(v.astype(jnp.bfloat16)).astype(jnp.float32)

@jax.custom_vjp
def low_back(v):
    return v

def low_keep(v):
    return (low(v), None)

def low_pass(kept, grad):
    return (grad,)

def back_keep(v):
    return (v, None)

def back_low(kept, grad):
    return (low(grad),)
low.defvjp(low_keep, low_pass)
low_back.defvjp(back_keep, back_low)
EPSILON = 1e-05
MASKED = 1e+30
HIGHEST = lax.Precision.HIGHEST

def product(left, right):
    return jnp.dot(left, right, precision=HIGHEST)

def norm_scale(values, norm_gain):
    return values * lax.rsqrt(lax.optimization_barrier(jnp.mean(values * values, axis=-1, keepdims=True)) + EPSILON) * norm_gain

def padded(values, filler):
    front = jnp.full((WINDOW,) + values.shape[1:], filler, values.dtype)
    return jnp.concatenate([front, values], axis=0)

def attention(query, key_all, value_all, segment, key_live):
    token_count = query.shape[0]
    block_rows = min(512, token_count)
    score_scale = HEAD_DIM ** (-0.5)
    key_pad = padded(key_all, 0.0)
    value_pad = padded(value_all, 0.0)
    seg_pad = padded(segment, -1)
    live_pad = padded(key_live, 0)

    def one_block(block_index):
        first_row = block_index * block_rows
        query_block = lax.dynamic_slice_in_dim(query, first_row, block_rows, 0)
        key_block = lax.dynamic_slice_in_dim(key_pad, first_row, block_rows + WINDOW, 0)
        value_block = lax.dynamic_slice_in_dim(value_pad, first_row, block_rows + WINDOW, 0)
        query_seg = lax.dynamic_slice_in_dim(segment, first_row, block_rows, 0)
        key_seg = lax.dynamic_slice_in_dim(seg_pad, first_row, block_rows + WINDOW, 0)
        key_flag = lax.dynamic_slice_in_dim(live_pad, first_row, block_rows + WINDOW, 0)
        query_pos = first_row + jnp.arange(block_rows, dtype=jnp.int32)
        key_pos = first_row - WINDOW + jnp.arange(block_rows + WINDOW, dtype=jnp.int32)
        distance = query_pos[:, None] - key_pos[None, :]
        allowed = (distance >= 0) & (distance < WINDOW) & (query_seg[:, None] == key_seg[None, :])
        allowed = allowed & ((key_flag[None, :] == 1) | (distance == 0))
        raw_scores = jnp.einsum('qhd,khd->hqk', query_block, key_block, precision=HIGHEST) * score_scale
        scores = jnp.where(allowed[None], low_back(raw_scores), -MASKED)
        chances = low(jax.nn.softmax(scores, axis=-1))
        return jnp.einsum('hqk,khd->qhd', chances, value_block, precision=HIGHEST)
    mixed = lax.map(jax.checkpoint(one_block), jnp.arange(token_count // block_rows, dtype=jnp.int32))
    return mixed.reshape(token_count, HEADS * HEAD_DIM)

def block_layer(placed, gain_one, gain_two, w_query, w_key, w_value, w_out, w_gate, w_up, w_down, segments, mask_rows):

    def one_group(inputs):
        group_rows, segment, key_live = inputs
        hidden_one = low(norm_scale(group_rows, gain_one))
        query = low_back(low(product(hidden_one, w_query))).reshape(-1, HEADS, HEAD_DIM)
        keys = low_back(low(product(hidden_one, w_key))).reshape(-1, HEADS, HEAD_DIM)
        values = low_back(low(product(hidden_one, w_value))).reshape(-1, HEADS, HEAD_DIM)
        mixed = low_back(low(attention(query, keys, values, segment, key_live)))
        middle = group_rows + low_back(product(mixed, w_out))
        hidden_two = low(norm_scale(middle, gain_two))
        gate_value = low_back(product(hidden_two, w_gate))
        upward = low_back(product(hidden_two, w_up))
        activated = low(jax.nn.silu(gate_value) * upward)
        return middle + low_back(product(activated, w_down))
    stacked = lax.map(jax.checkpoint(one_group), (placed.reshape(GROUPS, TOK_DEV, D), segments, mask_rows))
    return stacked.reshape(TOKENS, D)

def reference(tokens, cotangent, route, lengths, key_mask, norm1_gain, norm2_gain, w_query, w_key, w_value, w_out, w_gate, w_up, w_down):
    placed = jnp.zeros((TOKENS, D), jnp.float32).at[route].set(tokens.astype(jnp.float32))
    placed_grad = jnp.zeros((TOKENS, D), jnp.float32).at[route].set(cotangent.astype(jnp.float32))
    seq_ends = jnp.cumsum(lengths, axis=1)
    positions = jnp.arange(TOK_DEV, dtype=jnp.int32)
    segments = lax.optimization_barrier(jnp.sum((positions[None, :, None] >= seq_ends[:, None, :]).astype(jnp.int32), axis=2)).astype(jnp.int32)
    mask_rows = key_mask.reshape(GROUPS, TOK_DEV)

    def forward(*values):
        return block_layer(*values, segments, mask_rows)
    result, pull_back = jax.vjp(forward, placed, norm1_gain.astype(jnp.float32), norm2_gain.astype(jnp.float32), w_query.astype(jnp.float32), w_key.astype(jnp.float32), w_value.astype(jnp.float32), w_out.astype(jnp.float32), w_gate.astype(jnp.float32), w_up.astype(jnp.float32), w_down.astype(jnp.float32))
    gradients = pull_back(placed_grad)
    output = result.astype(jnp.bfloat16)[route]
    input_grad = gradients[0].astype(jnp.bfloat16)[route]
    return (output, input_grad, gradients[1], gradients[2], gradients[3], gradients[4], gradients[5], gradients[6], gradients[7], gradients[8], gradients[9])
```

```python
import functools

import jax
import jax.numpy as jnp
from jax import lax
from jax.experimental import pallas as pl
from jax.experimental.pallas import tpu as pltpu
from jax.sharding import PartitionSpec as P

HEAD_DIM = 112
WINDOW = 64
TOK_DEV = 1536


EPSILON = 1e-05
MASKED = 1e30


def norm_rows(values):
    inverse = lax.rsqrt(jnp.mean(values * values, axis=-1, keepdims=True) + EPSILON)
    return (values * inverse, inverse)


def norm_back(gradient, normed, inverse, norm_gain):
    scaled = gradient * norm_gain
    result = inverse * (scaled - normed * jnp.mean(scaled * normed, axis=-1, keepdims=True))
    return (result, jnp.sum(gradient * normed, axis=0))


def padded(values, filler):
    front = jnp.full((WINDOW,) + values.shape[1:], filler, values.dtype)
    return jnp.concatenate([front, values], axis=0)


def block_scores(query_block, key_block, query_seg, key_seg, key_flag, first_row, score_scale):
    query_pos = first_row + jnp.arange(query_block.shape[0], dtype=jnp.int32)
    key_pos = first_row - WINDOW + jnp.arange(key_block.shape[0], dtype=jnp.int32)
    distance = query_pos[:, None] - key_pos[None, :]
    allowed = (distance >= 0) & (distance < WINDOW) & (query_seg[:, None] == key_seg[None, :])
    allowed = allowed & ((key_flag[None, :] == 1) | (distance == 0))
    raw_scores = (
        jnp.einsum("qhd,khd->hqk", query_block, key_block, preferred_element_type=jnp.float32)
        * score_scale
    )
    return jnp.where(allowed[None], raw_scores, -MASKED)


def block_inputs(query, key_pad, value_pad, segment, seg_pad, live_pad, first_row, block_rows):
    key_span = block_rows + WINDOW
    return (
        lax.dynamic_slice_in_dim(query, first_row, block_rows, 0),
        lax.dynamic_slice_in_dim(key_pad, first_row, key_span, 0),
        lax.dynamic_slice_in_dim(value_pad, first_row, key_span, 0),
        lax.dynamic_slice_in_dim(segment, first_row, block_rows, 0),
        lax.dynamic_slice_in_dim(seg_pad, first_row, key_span, 0),
        lax.dynamic_slice_in_dim(live_pad, first_row, key_span, 0),
    )


def attend_forward(query, key_all, value_all, segment, key_live):
    token_count, head_count, head_width = query.shape
    block_rows = min(512, token_count)
    score_scale = head_width ** (-0.5)
    key_pad = padded(key_all, 0.0)
    value_pad = padded(value_all, 0.0)
    seg_pad = padded(segment, -1)
    live_pad = padded(key_live, 0)

    def one_block(running, block_index):
        first_row = block_index * block_rows
        query_block, key_block, value_block, query_seg, key_seg, key_flag = block_inputs(
            query, key_pad, value_pad, segment, seg_pad, live_pad, first_row, block_rows
        )
        scores = block_scores(
            query_block, key_block, query_seg, key_seg, key_flag, first_row, score_scale
        )
        row_max = jnp.max(scores, axis=-1, keepdims=True)
        weights = jnp.exp(scores - row_max)
        denominator = jnp.sum(weights, axis=-1, keepdims=True)
        chances = (weights / denominator).astype(jnp.bfloat16)
        mixed = jnp.einsum("hqk,khd->qhd", chances, value_block, preferred_element_type=jnp.float32)
        return (
            running,
            (mixed.astype(jnp.bfloat16), row_max[..., 0] + jnp.log(denominator[..., 0])),
        )

    _, (mixed, logsum) = lax.scan(
        one_block, jnp.zeros((), jnp.int32), jnp.arange(token_count // block_rows, dtype=jnp.int32)
    )
    return (mixed.reshape(token_count, head_count * head_width), logsum)


def attend_backward(query, key_all, value_all, segment, key_live, logsum, mixed_grad):
    token_count, head_count, head_width = query.shape
    block_rows = min(512, token_count)
    key_span = block_rows + WINDOW
    score_scale = head_width ** (-0.5)
    key_pad = padded(key_all, 0.0)
    value_pad = padded(value_all, 0.0)
    seg_pad = padded(segment, -1)
    live_pad = padded(key_live, 0)

    def one_block(running, inputs):
        key_grad, value_grad = running
        block_index, block_logsum = inputs
        first_row = block_index * block_rows
        query_block, key_block, value_block, query_seg, key_seg, key_flag = block_inputs(
            query, key_pad, value_pad, segment, seg_pad, live_pad, first_row, block_rows
        )
        grad_block = lax.dynamic_slice_in_dim(mixed_grad, first_row, block_rows, 0)
        scores = block_scores(
            query_block, key_block, query_seg, key_seg, key_flag, first_row, score_scale
        )
        chances = jnp.exp(scores - block_logsum[..., None])
        chance_grad = jnp.einsum(
            "qhd,khd->hqk", grad_block, value_block, preferred_element_type=jnp.float32
        )
        row_dot = jnp.sum(chances * chance_grad, axis=-1, keepdims=True)
        score_grad = (chances * (chance_grad - row_dot)).astype(jnp.bfloat16)
        query_grad = (
            jnp.einsum("hqk,khd->qhd", score_grad, key_block, preferred_element_type=jnp.float32)
            * score_scale
        )
        key_part = (
            jnp.einsum("hqk,qhd->khd", score_grad, query_block, preferred_element_type=jnp.float32)
            * score_scale
        )
        value_part = jnp.einsum(
            "hqk,qhd->khd",
            chances.astype(jnp.bfloat16),
            grad_block,
            preferred_element_type=jnp.float32,
        )
        key_grad = lax.dynamic_update_slice_in_dim(
            key_grad,
            lax.dynamic_slice_in_dim(key_grad, first_row, key_span, 0) + key_part,
            first_row,
            0,
        )
        value_grad = lax.dynamic_update_slice_in_dim(
            value_grad,
            lax.dynamic_slice_in_dim(value_grad, first_row, key_span, 0) + value_part,
            first_row,
            0,
        )
        return ((key_grad, value_grad), query_grad)

    empty_grad = jnp.zeros((token_count + WINDOW, head_count, head_width), jnp.float32)
    (key_grad, value_grad), query_grad = lax.scan(
        one_block,
        (empty_grad, empty_grad),
        (jnp.arange(token_count // block_rows, dtype=jnp.int32), logsum),
    )
    flat_width = head_count * head_width
    return (
        query_grad.reshape(token_count, flat_width).astype(jnp.bfloat16),
        key_grad[WINDOW:].reshape(token_count, flat_width).astype(jnp.bfloat16),
        value_grad[WINDOW:].reshape(token_count, flat_width).astype(jnp.bfloat16),
    )


def local(
    tokens,
    cotangent,
    route,
    lengths,
    key_mask,
    norm1_gain,
    norm2_gain,
    w_query,
    w_key,
    w_value,
    w_out,
    w_gate,
    w_up,
    w_down,
):
    groups = lax.axis_size("dp")
    members = lax.axis_size("mp")
    member = lax.axis_index("mp")
    local_rows = tokens.shape[0]
    group_rows = local_rows * members
    bucket = local_rows // groups
    target = route // TOK_DEV
    chosen = (target[:, None] == jnp.arange(groups, dtype=jnp.int32)[None, :]).astype(jnp.int32)
    ranking = jnp.sum((jnp.cumsum(chosen, axis=0) - chosen) * chosen, axis=1)
    send_at = target * bucket + ranking
    arrival, arrival_grad, arrival_slot = (
        lax.all_to_all(
            jnp.zeros_like(tokens).at[send_at].set(tokens),
            "dp",
            split_axis=0,
            concat_axis=0,
            tiled=True,
        ),
        lax.all_to_all(
            jnp.zeros_like(cotangent).at[send_at].set(cotangent),
            "dp",
            split_axis=0,
            concat_axis=0,
            tiled=True,
        ),
        lax.all_to_all(
            jnp.zeros_like(route).at[send_at].set(route % local_rows),
            "dp",
            split_axis=0,
            concat_axis=0,
            tiled=True,
        ),
    )
    token_rows = jnp.zeros_like(arrival).at[arrival_slot].set(arrival)
    grad_rows = jnp.zeros_like(arrival_grad).at[arrival_slot].set(arrival_grad)
    seq_ends = jnp.cumsum(lengths[0])
    positions = jnp.arange(group_rows, dtype=jnp.int32)
    segment = jnp.sum((positions[:, None] >= seq_ends[None, :]).astype(jnp.int32), axis=1)
    input_rows = token_rows.astype(jnp.float32)
    normed_one, inverse_one = norm_rows(input_rows)
    leading_all, grad_all = (
        lax.all_gather(token_rows, "mp", axis=0, tiled=True),
        lax.all_gather(grad_rows, "mp", axis=0, tiled=True),
    )
    input_all = leading_all.astype(jnp.float32)
    normed_all, _ = norm_rows(input_all)
    hidden_one = (normed_all * norm1_gain).astype(jnp.bfloat16)
    head_count = w_query.shape[1] // HEAD_DIM
    query = jnp.dot(hidden_one, w_query, preferred_element_type=jnp.float32).astype(jnp.bfloat16)
    keys = jnp.dot(hidden_one, w_key, preferred_element_type=jnp.float32).astype(jnp.bfloat16)
    values = jnp.dot(hidden_one, w_value, preferred_element_type=jnp.float32).astype(jnp.bfloat16)
    query_heads = query.reshape(group_rows, head_count, HEAD_DIM)
    key_heads = keys.reshape(group_rows, head_count, HEAD_DIM)
    value_heads = values.reshape(group_rows, head_count, HEAD_DIM)
    mixed_flat, logsum = attend_forward(query_heads, key_heads, value_heads, segment, key_mask)
    attention_all = lax.psum(jnp.dot(mixed_flat, w_out, preferred_element_type=jnp.float32), "mp")
    middle_all = input_all + attention_all
    middle_rows = lax.dynamic_slice_in_dim(middle_all, member * local_rows, local_rows, 0)
    normed_mid, _ = norm_rows(middle_all)
    hidden_two = (normed_mid * norm2_gain).astype(jnp.bfloat16)
    normed_two, inverse_two = norm_rows(middle_rows)
    gate_value = jnp.dot(hidden_two, w_gate, preferred_element_type=jnp.float32)
    upward = jnp.dot(hidden_two, w_up, preferred_element_type=jnp.float32)
    sigmoid = jax.nn.sigmoid(gate_value)
    activated = (gate_value * sigmoid * upward).astype(jnp.bfloat16)
    out_rows = middle_rows + lax.psum_scatter(
        jnp.dot(activated, w_down, preferred_element_type=jnp.float32).astype(jnp.bfloat16),
        "mp",
        scatter_dimension=0,
        tiled=True,
    ).astype(jnp.float32)
    activated_grad = jnp.einsum("td,fd->tf", grad_all, w_down, preferred_element_type=jnp.float32)
    gate_grad = (activated_grad * upward * sigmoid * (1.0 + gate_value * (1.0 - sigmoid))).astype(
        jnp.bfloat16
    )
    upward_grad = (activated_grad * gate_value * sigmoid).astype(jnp.bfloat16)
    down_sum = jnp.einsum("tf,td->fd", activated, grad_all, preferred_element_type=jnp.float32)
    gate_sum = jnp.einsum("td,tf->df", hidden_two, gate_grad, preferred_element_type=jnp.float32)
    upward_sum = jnp.einsum(
        "td,tf->df", hidden_two, upward_grad, preferred_element_type=jnp.float32
    )
    hidden_two_grad = lax.psum_scatter(
        jnp.einsum("tf,df->td", gate_grad, w_gate, preferred_element_type=jnp.float32)
        + jnp.einsum("tf,df->td", upward_grad, w_up, preferred_element_type=jnp.float32),
        "mp",
        scatter_dimension=0,
        tiled=True,
    )
    norm_part_two, gain_two_grad = norm_back(hidden_two_grad, normed_two, inverse_two, norm2_gain)
    middle_grad = grad_rows.astype(jnp.float32) + norm_part_two
    branch_all = lax.all_gather(middle_grad.astype(jnp.bfloat16), "mp", axis=0, tiled=True)
    output_sum = jnp.einsum("tc,td->cd", mixed_flat, branch_all, preferred_element_type=jnp.float32)
    mixed_grad = jnp.einsum(
        "td,cd->tc", branch_all, w_out, preferred_element_type=jnp.float32
    ).astype(jnp.bfloat16)
    query_grad, key_grad, value_grad = attend_backward(
        query_heads,
        key_heads,
        value_heads,
        segment,
        key_mask,
        logsum,
        mixed_grad.reshape(group_rows, head_count, HEAD_DIM),
    )
    query_sum = jnp.einsum("td,tc->dc", hidden_one, query_grad, preferred_element_type=jnp.float32)
    key_sum = jnp.einsum("td,tc->dc", hidden_one, key_grad, preferred_element_type=jnp.float32)
    value_sum = jnp.einsum("td,tc->dc", hidden_one, value_grad, preferred_element_type=jnp.float32)
    hidden_one_grad = lax.psum_scatter(
        (
            jnp.einsum("tc,dc->td", query_grad, w_query, preferred_element_type=jnp.float32)
            + jnp.einsum("tc,dc->td", key_grad, w_key, preferred_element_type=jnp.float32)
            + jnp.einsum("tc,dc->td", value_grad, w_value, preferred_element_type=jnp.float32)
        ).astype(jnp.bfloat16),
        "mp",
        scatter_dimension=0,
        tiled=True,
    ).astype(jnp.float32)
    norm_part_one, gain_one_grad = norm_back(hidden_one_grad, normed_one, inverse_one, norm1_gain)
    input_grad = middle_grad + norm_part_one
    gain_one_sum, gain_two_sum = lax.psum((gain_one_grad, gain_two_grad), ("dp", "mp"))
    weight_sums = (
        lax.psum(query_sum.astype(jnp.bfloat16), "dp").astype(jnp.float32),
        lax.psum(key_sum.astype(jnp.bfloat16), "dp").astype(jnp.float32),
        lax.psum(value_sum.astype(jnp.bfloat16), "dp").astype(jnp.float32),
        lax.psum(output_sum.astype(jnp.bfloat16), "dp").astype(jnp.float32),
        lax.psum(gate_sum.astype(jnp.bfloat16), "dp").astype(jnp.float32),
        lax.psum(upward_sum.astype(jnp.bfloat16), "dp").astype(jnp.float32),
        lax.psum(down_sum.astype(jnp.bfloat16), "dp").astype(jnp.float32),
    )
    back_out, back_grad = (
        lax.all_to_all(
            out_rows.astype(jnp.bfloat16)[arrival_slot],
            "dp",
            split_axis=0,
            concat_axis=0,
            tiled=True,
        ),
        lax.all_to_all(
            input_grad.astype(jnp.bfloat16)[arrival_slot],
            "dp",
            split_axis=0,
            concat_axis=0,
            tiled=True,
        ),
    )
    return (
        back_out[send_at],
        back_grad[send_at],
        gain_one_sum,
        gain_two_sum,
        weight_sums[0],
        weight_sums[1],
        weight_sums[2],
        weight_sums[3],
        weight_sums[4],
        weight_sums[5],
        weight_sums[6],
    )


MESH = pl.DeviceIdType.MESH
LANES = 128
F32 = jnp.float32
BF16 = jnp.bfloat16
VMEM_LIMIT = 56 * 1024 * 1024


def plane():
    me = lax.axis_index("dp")
    side = me + 1 - 2 * lax.rem(me, 2)
    over_x = me + 2 - 4 * lax.rem(lax.div(me, 2), 2)
    over_y = me + 4 - 8 * lax.rem(lax.div(me, 4), 2)
    corner = over_x + 4 - 8 * lax.rem(lax.div(over_x, 4), 2)
    return (me, side, over_x, over_y, corner)


def to_dp(source, target, send_sem, recv_sem, index):
    return pltpu.make_async_remote_copy(
        src_ref=source,
        dst_ref=target,
        send_sem=send_sem,
        recv_sem=recv_sem,
        device_id={"dp": index},
        device_id_type=MESH,
    )


def to_mp(source, target, send_sem, recv_sem, index):
    return pltpu.make_async_remote_copy(
        src_ref=source,
        dst_ref=target,
        send_sem=send_sem,
        recv_sem=recv_sem,
        device_id={"mp": index},
        device_id_type=MESH,
    )


def greet_plane():
    _, side, over_x, over_y, _ = plane()
    barrier = pltpu.get_barrier_semaphore()
    for other in (side, over_x, over_y):
        pl.semaphore_signal(barrier, inc=1, device_id={"dp": other}, device_id_type=MESH)
    return barrier


class Gather:
    COUNT = 13

    def __init__(self, own, out, send, recv, local):
        me, side, over_x, over_y, corner = plane()
        half = own.shape[0] // 2
        low, high = pl.ds(0, half), pl.ds(half, half)

        def hop(number, source, target, index):
            return to_dp(source, target, send.at[number], recv.at[number], index)

        self.keep = pltpu.make_async_copy(own, out.at[me], local)
        self.first = [
            hop(0, own.at[low], out.at[me, low], over_x),
            hop(1, own.at[high], out.at[me, high], over_y),
            hop(2, own.at[high], out.at[me, high], over_x),
            hop(3, own.at[low], out.at[me, low], over_y),
            hop(4, own, out.at[me], side),
        ]
        self.onward = [
            (0, hop(5, out.at[over_x, low], out.at[over_x, low], over_y)),
            (0, hop(6, out.at[over_x, low], out.at[over_x, low], side)),
            (1, hop(7, out.at[over_y, high], out.at[over_y, high], over_x)),
            (1, hop(8, out.at[over_y, high], out.at[over_y, high], side)),
            (2, hop(9, out.at[over_x, high], out.at[over_x, high], side)),
            (3, hop(10, out.at[over_y, low], out.at[over_y, low], side)),
        ]
        self.last = [
            (5, hop(11, out.at[corner, low], out.at[corner, low], side)),
            (7, hop(12, out.at[corner, high], out.at[corner, high], side)),
        ]
        self.by_number = dict(enumerate(self.first))
        for number, copy in zip((5, 6, 7, 8, 9, 10), [c for _, c in self.onward]):
            self.by_number[number] = copy
        for number, copy in zip((11, 12), [c for _, c in self.last]):
            self.by_number[number] = copy

    def start(self):
        for copy in self.first:
            copy.start()
        self.keep.start()

    def pass_on(self):
        seen = set()
        for after, copy in self.onward:
            if after not in seen:
                self.by_number[after].wait_recv()
                seen.add(after)
            copy.start()

    def finish(self):
        for after, copy in self.last:
            self.by_number[after].wait_recv()
            copy.start()
        for number in (4, 6, 8, 9, 10, 11, 12):
            self.by_number[number].wait_recv()
        for number in range(self.COUNT):
            self.by_number[number].wait_send()
        self.keep.wait()


def first_kernel(
    hidden, cotangent, qkv_share, out_share,
    hidden_all, cotangent_all, w_qkv, w_out,
    send_a, recv_a, send_b, recv_b, send_w, recv_w, local,
):
    me, _, _, _, _ = plane()
    z = lax.axis_index("mp")
    core = lax.rem(me, 2)
    barrier = greet_plane()
    for step in (1, 2, 3):
        pl.semaphore_signal(
            barrier, inc=1, device_id={"mp": lax.rem(z + step, 4)}, device_id_type=MESH
        )
    pl.semaphore_wait(barrier, 6)
    first = Gather(hidden, hidden_all, send_a, recv_a, local.at[0])
    second = Gather(cotangent, cotangent_all, send_b, recv_b, local.at[1])
    first.start()
    place = lax.rem(z, 2)
    owner = lax.div(z, 2) == core

    def pieces(slot):
        found = []
        for part in range(3):
            columns = pl.ds(pl.multiple_of((2 * part + slot) * LANES, LANES), LANES)
            found.append((qkv_share.at[part], w_qkv.at[:, columns]))
        rows = pl.ds(pl.multiple_of(slot * LANES, LANES), LANES)
        found.append((out_share, w_out.at[rows]))
        return found

    @pl.when(owner)
    def _():
        for number, (source, target) in enumerate(pieces(place)):
            pltpu.make_async_copy(source, target, local.at[2 + number]).start()
        for step in (1, 2, 3):
            other = lax.rem(z + step, 4)
            for number, (source, target) in enumerate(pieces(place)):
                index = (step - 1) * 4 + number
                to_mp(source, target, send_w.at[index], recv_w.at[index], other).start()

    second.start()
    first.pass_on()
    second.pass_on()
    first.finish()
    second.finish()

    for step in (1, 2, 3):
        source_z = lax.rem(z + 4 - step, 4)

        @pl.when(lax.div(source_z, 2) == core)
        def _():
            for number, (source, target) in enumerate(pieces(lax.rem(source_z, 2))):
                index = (step - 1) * 4 + number
                to_mp(source, target, send_w.at[index], recv_w.at[index], source_z).wait_recv()

    @pl.when(owner)
    def _():
        for step in (1, 2, 3):
            other = lax.rem(z + step, 4)
            for number, (source, target) in enumerate(pieces(place)):
                index = (step - 1) * 4 + number
                to_mp(source, target, send_w.at[index], recv_w.at[index], other).wait_send()
        for number, (source, target) in enumerate(pieces(place)):
            pltpu.make_async_copy(source, target, local.at[2 + number]).wait()


def anywhere():
    return pl.BlockSpec(memory_space=pl.ANY)


def on_chip():
    return pl.BlockSpec(memory_space=pltpu.VMEM)


def in_scalar():
    return pl.BlockSpec(memory_space=pltpu.SMEM)


def remote_params(number, limit=VMEM_LIMIT):
    return pltpu.CompilerParams(
        collective_id=number, has_side_effects=True, vmem_limit_bytes=limit
    )


def gather_first(hidden, cotangent, qkv_share, out_share):
    rows, width = hidden.shape
    groups = lax.axis_size("dp")
    dma = pltpu.SemaphoreType.DMA
    return pl.pallas_call(
        first_kernel,
        out_shape=(
            jax.ShapeDtypeStruct((groups, rows, width), BF16),
            jax.ShapeDtypeStruct((groups, rows, width), BF16),
            jax.ShapeDtypeStruct((width, 6 * LANES), BF16),
            jax.ShapeDtypeStruct((2 * LANES, width), BF16),
        ),
        in_specs=[anywhere()] * 4,
        out_specs=(anywhere(),) * 4,
        scratch_shapes=[
            dma((13,)), dma((13,)), dma((13,)), dma((13,)), dma((12,)), dma((12,)), dma((6,)),
        ],
        compiler_params=remote_params(1),
        cost_estimate=pl.CostEstimate(flops=0, bytes_accessed=300_000_000, transcendentals=0),
        name="gather_first",
    )(hidden, cotangent, qkv_share, out_share)


def one_hot(slots, k, size):
    row = slots[pl.ds(k, 1), :]
    place = lax.broadcasted_iota(jnp.int32, (size, size), 0)
    return (place == row).astype(BF16)


def block_mask(lengths, flags, k, block, z, rows):
    position = rows * z + block * 128 + lax.broadcasted_iota(jnp.int32, (128, 1), 0)
    first_end = lengths[k, 0]
    second_end = first_end + lengths[k, 1]
    begin = jnp.where(position >= first_end, first_end, 0)
    begin = jnp.where(position >= second_end, second_end, begin)
    column = lax.broadcasted_iota(jnp.int32, (128, 192), 1)
    distance = 64 + lax.broadcasted_iota(jnp.int32, (128, 192), 0) - column
    key_position = rows * z + block * 128 - 64 + column
    live = flags[pl.ds(k, 1), block * 128 : block * 128 + 192]
    allowed = (distance >= 0) & (distance < WINDOW) & (key_position >= begin)
    return allowed & ((live == 1) | (distance == 0))


NT = (((1,), (1,)), ((), ()))
TN = (((0,), (0,)), ((), ()))


def forward_kernel(
    lengths, qkv, slots, flags, mixed, kept, send, recv, *, scale, groups, rows
):
    z = lax.axis_index("mp")
    members = lax.axis_size("mp")
    barrier = pltpu.get_barrier_semaphore()

    @pl.when(z > 0)
    def _():
        pl.semaphore_signal(barrier, inc=1, device_id={"mp": z - 1}, device_id_type=MESH)

    @pl.when(z < members - 1)
    def _():
        pl.semaphore_wait(barrier, 1)

    def halo(k, other):
        return to_mp(
            kept.at[k, pl.ds(rows, 64), pl.ds(256, 512)],
            kept.at[k, pl.ds(0, 64), pl.ds(256, 512)],
            send.at[k],
            recv.at[k],
            other,
        )

    def order(k, carry):
        hot = one_hot(slots, k, rows)
        given = qkv[:, pl.ds(k, 1)].reshape(rows, 768)
        kept[k, pl.ds(64, rows), :] = jnp.dot(hot, given, preferred_element_type=F32).astype(BF16)
        kept[k, pl.ds(0, 64), pl.ds(0, 256)] = jnp.zeros((64, 256), BF16)

        @pl.when(z < members - 1)
        def _():
            halo(k, z + 1).start()

        @pl.when(z == 0)
        def _():
            kept[k, pl.ds(0, 64), pl.ds(256, 512)] = jnp.zeros((64, 512), BF16)

        return carry

    lax.fori_loop(0, groups, order, 0)

    def attend(k, carry):
        @pl.when(z > 0)
        def _():
            halo(k, z).wait_recv()

        hot = one_hot(slots, k, rows)
        found = []
        for block in range(rows // 128):
            allowed = block_mask(lengths, flags, k, block, z, rows)
            heads = []
            for head in range(2):
                query = kept[k, pl.ds(64 + block * 128, 128), pl.ds(head * 128, 128)]
                keys = kept[k, pl.ds(block * 128, 192), pl.ds(256 + head * 128, 128)]
                values = kept[k, pl.ds(block * 128, 192), pl.ds(512 + head * 128, 128)]
                scores = lax.dot_general(query, keys, NT, preferred_element_type=F32) * scale
                scores = jnp.where(allowed, scores, -MASKED)
                weights = jnp.exp(scores - jnp.max(scores, axis=-1, keepdims=True))
                total = jnp.sum(weights, axis=-1, keepdims=True)
                chances = (weights / total).astype(BF16)
                heads.append(jnp.dot(chances, values, preferred_element_type=F32).astype(BF16))
            found.append(jnp.concatenate(heads, axis=1))
        ordered = jnp.concatenate(found, axis=0)
        back = lax.dot_general(hot, ordered, TN, preferred_element_type=F32).astype(BF16)
        mixed[:, pl.ds(k, 1)] = back.reshape(groups, 1, rows // groups, 256)
        return carry

    lax.fori_loop(0, groups, attend, 0)

    @pl.when(z < members - 1)
    def _():
        def done(k, carry):
            halo(k, z + 1).wait_send()
            return carry

        lax.fori_loop(0, groups, done, 0)


def attend_ahead(lengths, qkv, slots, flags, scale):
    groups = qkv.shape[0]
    rows = slots.shape[1]
    dma = pltpu.SemaphoreType.DMA
    return pl.pallas_call(
        functools.partial(forward_kernel, scale=scale, groups=groups, rows=rows),
        out_shape=(
            jax.ShapeDtypeStruct((groups, groups, rows // groups, 256), BF16),
            jax.ShapeDtypeStruct((groups, rows + 64, 768), BF16),
        ),
        in_specs=[in_scalar(), on_chip(), on_chip(), on_chip()],
        out_specs=(on_chip(), on_chip()),
        scratch_shapes=[dma((groups,)), dma((groups,))],
        compiler_params=remote_params(2),
        cost_estimate=pl.CostEstimate(flops=0, bytes_accessed=70_000_000, transcendentals=0),
        name="attend_ahead",
    )(lengths, qkv, slots, flags)


def backward_kernel(
    lengths, kept, mixed_grad, slots, flags, out,
    totals, query_part, key_value, leaving, arriving, send, recv,
    *, scale, groups, rows,
):
    z = lax.axis_index("mp")
    members = lax.axis_size("mp")
    barrier = pltpu.get_barrier_semaphore()

    @pl.when(z < members - 1)
    def _():
        pl.semaphore_signal(barrier, inc=1, device_id={"mp": z + 1}, device_id_type=MESH)

    @pl.when(z > 0)
    def _():
        pl.semaphore_wait(barrier, 1)

    def halo(k, other):
        return to_mp(leaving.at[k], arriving.at[k], send.at[k], recv.at[k], other)

    def attend(k, carry):
        hot = one_hot(slots, k, rows)
        given = mixed_grad[:, pl.ds(k, 1)].reshape(rows, 256)
        grad_ordered = jnp.dot(hot, given, preferred_element_type=F32).astype(BF16)
        totals[...] = jnp.zeros_like(totals)
        for block in range(rows // 128):
            allowed = block_mask(lengths, flags, k, block, z, rows)
            for head in range(2):
                query = kept[k, pl.ds(64 + block * 128, 128), pl.ds(head * 128, 128)]
                keys = kept[k, pl.ds(block * 128, 192), pl.ds(256 + head * 128, 128)]
                values = kept[k, pl.ds(block * 128, 192), pl.ds(512 + head * 128, 128)]
                grad = grad_ordered[block * 128 : block * 128 + 128, head * 128 : head * 128 + 128]
                scores = lax.dot_general(query, keys, NT, preferred_element_type=F32) * scale
                scores = jnp.where(allowed, scores, -MASKED)
                weights = jnp.exp(scores - jnp.max(scores, axis=-1, keepdims=True))
                again = weights / jnp.sum(weights, axis=-1, keepdims=True)
                chance_grad = lax.dot_general(grad, values, NT, preferred_element_type=F32)
                row_dot = jnp.sum(again * chance_grad, axis=-1, keepdims=True)
                score_grad = (again * (chance_grad - row_dot)).astype(BF16)
                query_part[k, pl.ds(block * 128, 128), pl.ds(head * 128, 128)] = (
                    jnp.dot(score_grad, keys, preferred_element_type=F32) * scale
                ).astype(BF16)
                totals[pl.ds(block * 128, 192), pl.ds(head * 128, 128)] += (
                    lax.dot_general(score_grad, query, TN, preferred_element_type=F32) * scale
                )
                totals[pl.ds(block * 128, 192), pl.ds(256 + head * 128, 128)] += lax.dot_general(
                    again.astype(BF16), grad, TN, preferred_element_type=F32
                )
        key_value[k] = totals[pl.ds(64, rows), :]

        @pl.when(z > 0)
        def _():
            leaving[k] = totals[pl.ds(0, 64), :].astype(BF16)
            halo(k, z - 1).start()

        return carry

    lax.fori_loop(0, groups, attend, 0)

    def restore(k, carry):
        @pl.when(z < members - 1)
        def _():
            halo(k, z).wait_recv()
            key_value[k, pl.ds(rows - 64, 64), :] += arriving[k].astype(F32)

        hot = one_hot(slots, k, rows)
        ordered = jnp.concatenate([query_part[k], key_value[k].astype(BF16)], axis=1)
        back = lax.dot_general(hot, ordered, TN, preferred_element_type=F32).astype(BF16)
        out[:, pl.ds(k, 1)] = back.reshape(groups, 1, rows // groups, 768)
        return carry

    lax.fori_loop(0, groups, restore, 0)

    @pl.when(z > 0)
    def _():
        def done(k, carry):
            halo(k, z - 1).wait_send()
            return carry

        lax.fori_loop(0, groups, done, 0)


def attend_back(lengths, kept, mixed_grad, slots, flags, scale):
    groups = kept.shape[0]
    rows = slots.shape[1]
    dma = pltpu.SemaphoreType.DMA
    return pl.pallas_call(
        functools.partial(backward_kernel, scale=scale, groups=groups, rows=rows),
        out_shape=jax.ShapeDtypeStruct((groups, groups, rows // groups, 768), BF16),
        in_specs=[in_scalar()] + [on_chip()] * 4,
        out_specs=on_chip(),
        scratch_shapes=[
            pltpu.VMEM((rows + 64, 512), F32),
            pltpu.VMEM((groups, rows, 256), BF16),
            pltpu.VMEM((groups, rows, 512), F32),
            pltpu.VMEM((groups, 64, 512), BF16),
            pltpu.VMEM((groups, 64, 512), BF16),
            dma((groups,)),
            dma((groups,)),
        ],
        compiler_params=remote_params(3),
        cost_estimate=pl.CostEstimate(flops=0, bytes_accessed=120_000_000, transcendentals=0),
        name="attend_back",
    )(lengths, kept, mixed_grad, slots, flags)


def feed_kernel(hidden, cotangent, w_both, w_down, both_grad, activated, *, members):
    rows = hidden[...]
    raw = jnp.dot(rows, w_both[...], preferred_element_type=F32)
    grad = lax.dot_general(cotangent[...], w_down[...], NT, preferred_element_type=F32)
    for part in range(members):
        gate = raw[:, part * 256 : part * 256 + 128]
        upward = raw[:, part * 256 + 128 : part * 256 + 256]
        active_grad = grad[:, part * 128 : part * 128 + 128]
        sigmoid = jax.nn.sigmoid(gate)
        activated[:, part * 128 : part * 128 + 128] = (gate * sigmoid * upward).astype(BF16)
        both_grad[:, part * 256 : part * 256 + 128] = (
            active_grad * upward * sigmoid * (1.0 + gate * (1.0 - sigmoid))
        ).astype(BF16)
        both_grad[:, part * 256 + 128 : part * 256 + 256] = (
            active_grad * gate * sigmoid
        ).astype(BF16)


def feed(hidden, cotangent, w_both, w_down):
    count, width = hidden.shape
    wide = w_both.shape[1]
    units = w_down.shape[0]
    tile = 256
    return pl.pallas_call(
        functools.partial(feed_kernel, members=wide // 256),
        grid=(count // tile,),
        out_shape=(
            jax.ShapeDtypeStruct((count, wide), BF16),
            jax.ShapeDtypeStruct((count, units), BF16),
        ),
        in_specs=[
            pl.BlockSpec((tile, width), lambda i: (i, 0)),
            pl.BlockSpec((tile, width), lambda i: (i, 0)),
            pl.BlockSpec((width, wide), lambda i: (0, 0)),
            pl.BlockSpec((units, width), lambda i: (0, 0)),
        ],
        out_specs=(
            pl.BlockSpec((tile, wide), lambda i: (i, 0)),
            pl.BlockSpec((tile, units), lambda i: (i, 0)),
        ),
        compiler_params=pltpu.CompilerParams(vmem_limit_bytes=VMEM_LIMIT),
        cost_estimate=pl.CostEstimate(
            flops=2 * count * width * (wide + units), bytes_accessed=50_000_000, transcendentals=0
        ),
        name="feed",
    )(hidden, cotangent, w_both, w_down)


CHUNK = 32


def each_chunk(rows, body):
    def step(i, carry):
        body(pl.ds(pl.multiple_of(i * CHUNK, CHUNK), CHUNK))
        return carry

    lax.fori_loop(0, rows // CHUNK, step, 0)


class Reduce:
    COUNT = 10

    def __init__(self, left, right, across, part, from_side, from_corner, from_near, send, recv):
        self.left, self.right, self.across, self.part = left, right, across, part
        self.from_side, self.from_corner, self.from_near = from_side, from_corner, from_near
        self.send, self.recv = send, recv
        self.rows = part.shape[1]

    def product(self, owner, slot):
        rows, width = self.rows, self.part.shape[2]
        picked = pl.ds(pl.multiple_of(owner * rows, rows), rows)

        def tile(t, carry):
            columns = pl.ds(pl.multiple_of(t * 256, 256), 256)
            if self.across:
                value = lax.dot_general(
                    self.left[picked, :], self.right[columns, :], NT, preferred_element_type=F32
                )
            else:
                value = jnp.dot(
                    self.left[picked, :], self.right[:, columns], preferred_element_type=F32
                )
            self.part[slot, :, columns] = value.astype(BF16)
            return carry

        lax.fori_loop(0, width // 256, tile, 0)

    def run(self):
        me, side, over_x, over_y, corner = plane()
        part, near, rows = self.part, self.from_near, self.rows
        half = rows // 2
        low, high = pl.ds(0, half), pl.ds(half, half)

        def hop(number, source, target, index):
            return to_dp(source, target, self.send.at[number], self.recv.at[number], index)

        shares = [hop(i, part.at[4 + i], self.from_side.at[i], side) for i in range(4)]
        corners = [
            hop(4, part.at[0, low], self.from_corner.at[0], over_x),
            hop(5, part.at[0, high], self.from_corner.at[1], over_y),
        ]
        nears = [
            hop(6, part.at[1, low], near.at[0, low], over_x),
            hop(7, part.at[1, high], near.at[0, high], over_x),
            hop(8, part.at[2, high], near.at[1, high], over_y),
            hop(9, part.at[2, low], near.at[1, low], over_y),
        ]
        owners = [corner, over_x, over_y, me]
        for slot in range(4):
            other = owners[slot] + 1 - 2 * lax.rem(me, 2)
            self.product(other, 4 + slot)
            shares[slot].start()

        def add_side(slot):
            shares[slot].wait_recv()

            def body(span):
                part[slot, span, :] = (
                    part[slot, span, :].astype(F32) + self.from_side[slot, span, :].astype(F32)
                ).astype(BF16)

            each_chunk(rows, body)

        self.product(corner, 0)
        add_side(0)
        corners[0].start()
        corners[1].start()
        self.product(over_x, 1)
        add_side(1)
        nears[0].start()
        self.product(over_y, 2)
        add_side(2)
        nears[2].start()
        self.product(me, 3)

        def add_corner(slot, offset, which):
            def body(span):
                target = pl.ds(pl.multiple_of(offset + span.start, CHUNK), CHUNK)
                part[slot, target, :] = (
                    part[slot, target, :].astype(F32)
                    + self.from_corner[which, span, :].astype(F32)
                ).astype(BF16)

            each_chunk(half, body)

        corners[0].wait_recv()
        add_corner(2, 0, 0)
        nears[3].start()
        corners[1].wait_recv()
        add_corner(1, half, 1)
        nears[1].start()
        shares[3].wait_recv()
        for copy in nears:
            copy.wait_recv()
        self.pending = shares + corners + nears

    def rows_of(self, span):
        return (
            self.part[3, span, :].astype(F32)
            + self.from_side[3, span, :].astype(F32)
            + self.from_near[0, span, :].astype(F32)
            + self.from_near[1, span, :].astype(F32)
        )

    def finish(self):
        for copy in self.pending:
            copy.wait_send()


def reduce_scratch(rows, width):
    dma = pltpu.SemaphoreType.DMA
    return [
        pltpu.VMEM((8, rows, width), BF16),
        pltpu.VMEM((4, rows, width), BF16),
        pltpu.VMEM((2, rows // 2, width), BF16),
        pltpu.VMEM((2, rows, width), BF16),
        dma((10,)),
        dma((10,)),
    ]


def gather_scratch(rows, width):
    dma = pltpu.SemaphoreType.DMA
    return [pltpu.VMEM((rows, width), BF16), dma((13,)), dma((13,)), dma(())]


def mean_rows(values):
    return jnp.mean(values, axis=-1, keepdims=True)


def middle_kernel(
    mixed, w_out, tokens, gain, middle, hidden_all,
    part, from_side, from_corner, from_near, send, recv, own, send_g, recv_g, local,
):
    pl.semaphore_wait(greet_plane(), 3)
    reduce = Reduce(mixed, w_out, False, part, from_side, from_corner, from_near, send, recv)
    reduce.run()

    def body(span):
        values = tokens[span, :].astype(F32) + reduce.rows_of(span)
        middle[span, :] = values
        inverse = lax.rsqrt(mean_rows(values * values) + EPSILON)
        own[span, :] = (values * inverse * gain[...]).astype(BF16)

    each_chunk(own.shape[0], body)
    gather = Gather(own, hidden_all, send_g, recv_g, local)
    gather.start()
    gather.pass_on()
    gather.finish()
    reduce.finish()


def project_middle(mixed, w_out, tokens, gain):
    rows, width = tokens.shape
    groups = lax.axis_size("dp")
    return pl.pallas_call(
        middle_kernel,
        out_shape=(
            jax.ShapeDtypeStruct((rows, width), F32),
            jax.ShapeDtypeStruct((groups, rows, width), BF16),
        ),
        in_specs=[on_chip()] * 4,
        out_specs=(on_chip(), anywhere()),
        scratch_shapes=reduce_scratch(rows, width) + gather_scratch(rows, width),
        compiler_params=remote_params(4),
        cost_estimate=pl.CostEstimate(flops=0, bytes_accessed=300_000_000, transcendentals=0),
        name="project_middle",
    )(mixed, w_out, tokens, gain)


def norm_back_rows(gradient, values, gain, sums, span):
    inverse = lax.rsqrt(mean_rows(values * values) + EPSILON)
    normed = values * inverse
    product = gradient * normed
    folded = product[0:8]
    for step in range(1, CHUNK // 8):
        folded = folded + product[step * 8 : step * 8 + 8]
    sums[...] += folded
    scaled = gradient * gain
    return inverse * (scaled - normed * mean_rows(scaled * normed))


def branch_kernel(
    both_grad, w_both, middle, cotangent, gain, middle_grad, branch_all, sums,
    part, from_side, from_corner, from_near, send, recv, own, send_g, recv_g, local,
):
    pl.semaphore_wait(greet_plane(), 3)
    reduce = Reduce(both_grad, w_both, True, part, from_side, from_corner, from_near, send, recv)
    reduce.run()
    sums[...] = jnp.zeros_like(sums)

    def body(span):
        change = norm_back_rows(reduce.rows_of(span), middle[span, :], gain[...], sums, span)
        total = cotangent[span, :].astype(F32) + change
        middle_grad[span, :] = total
        own[span, :] = total.astype(BF16)

    each_chunk(own.shape[0], body)
    gather = Gather(own, branch_all, send_g, recv_g, local)
    gather.start()
    gather.pass_on()
    gather.finish()
    reduce.finish()


def project_branch(both_grad, w_both, middle, cotangent, gain):
    rows, width = middle.shape
    groups = lax.axis_size("dp")
    return pl.pallas_call(
        branch_kernel,
        out_shape=(
            jax.ShapeDtypeStruct((rows, width), F32),
            jax.ShapeDtypeStruct((groups, rows, width), BF16),
            jax.ShapeDtypeStruct((8, width), F32),
        ),
        in_specs=[on_chip()] * 5,
        out_specs=(on_chip(), anywhere(), on_chip()),
        scratch_shapes=reduce_scratch(rows, width) + gather_scratch(rows, width),
        compiler_params=remote_params(5),
        cost_estimate=pl.CostEstimate(flops=0, bytes_accessed=300_000_000, transcendentals=0),
        name="project_branch",
    )(both_grad, w_both, middle, cotangent, gain)


def input_kernel(
    qkv_grad, w_qkv, tokens, middle_grad, gain, result, sums,
    part, from_side, from_corner, from_near, send, recv,
):
    pl.semaphore_wait(greet_plane(), 3)
    reduce = Reduce(qkv_grad, w_qkv, True, part, from_side, from_corner, from_near, send, recv)
    reduce.run()
    sums[...] = jnp.zeros_like(sums)

    def body(span):
        values = tokens[span, :].astype(F32)
        change = norm_back_rows(reduce.rows_of(span), values, gain[...], sums, span)
        result[span, :] = (middle_grad[span, :] + change).astype(BF16)

    each_chunk(result.shape[0], body)
    reduce.finish()


def project_input(qkv_grad, w_qkv, tokens, middle_grad, gain):
    rows, width = tokens.shape
    return pl.pallas_call(
        input_kernel,
        out_shape=(
            jax.ShapeDtypeStruct((rows, width), BF16),
            jax.ShapeDtypeStruct((8, width), F32),
        ),
        in_specs=[on_chip()] * 5,
        out_specs=(on_chip(), on_chip()),
        scratch_shapes=reduce_scratch(rows, width),
        compiler_params=remote_params(6),
        cost_estimate=pl.CostEstimate(flops=0, bytes_accessed=150_000_000, transcendentals=0),
        name="project_input",
    )(qkv_grad, w_qkv, tokens, middle_grad, gain)


def output_kernel(
    activated, w_down, middle, result, part, from_side, from_corner, from_near, send, recv
):
    pl.semaphore_wait(greet_plane(), 3)
    reduce = Reduce(activated, w_down, False, part, from_side, from_corner, from_near, send, recv)
    reduce.run()

    def body(span):
        result[span, :] = (middle[span, :] + reduce.rows_of(span)).astype(BF16)

    each_chunk(result.shape[0], body)
    reduce.finish()


def project_output(activated, w_down, middle):
    rows, width = middle.shape
    return pl.pallas_call(
        output_kernel,
        out_shape=jax.ShapeDtypeStruct((rows, width), BF16),
        in_specs=[on_chip()] * 3,
        out_specs=on_chip(),
        scratch_shapes=reduce_scratch(rows, width),
        compiler_params=remote_params(7),
        cost_estimate=pl.CostEstimate(flops=0, bytes_accessed=150_000_000, transcendentals=0),
        name="project_output",
    )(activated, w_down, middle)


def swapped(
    tokens, cotangent, route, lengths, key_mask, norm1_gain, norm2_gain,
    w_query, w_key, w_value, w_out, w_gate, w_up, w_down,
):
    groups = lax.axis_size("dp")
    members = lax.axis_size("mp")
    me = lax.axis_index("dp")
    z = lax.axis_index("mp")
    rows, width = tokens.shape
    bucket = rows // groups
    units = w_down.shape[0] // groups
    chip, core = me // 2, me % 2
    pad_head = LANES - HEAD_DIM

    target = route // TOK_DEV
    earlier = jnp.arange(rows, dtype=jnp.int32)
    same = (target[:, None] == target[None, :]) & (earlier[None, :] < earlier[:, None])
    send_at = target * bucket + jnp.sum(same.astype(jnp.int32), axis=1)
    sorting = send_at[None, :] == earlier[:, None]
    slots_own = jnp.sum(jnp.where(sorting, (route % rows)[None, :], 0), axis=1)
    sort_hot = sorting.astype(BF16)
    tokens_b = jnp.dot(sort_hot, tokens, preferred_element_type=F32).astype(BF16)
    cotangent_b = jnp.dot(sort_hot, cotangent, preferred_element_type=F32).astype(BF16)

    mask_window = lax.dynamic_slice_in_dim(
        jnp.concatenate([jnp.zeros((WINDOW,), jnp.int32), key_mask]), z * rows, rows + WINDOW
    )
    notes = jnp.concatenate([slots_own, mask_window, lengths[0]])
    notes = jnp.pad(notes, (0, -notes.shape[0] % LANES))
    notes_all = lax.all_gather(notes, "dp")
    slots = (
        notes_all[:, :rows].reshape(groups, groups, bucket).transpose(1, 0, 2).reshape(groups, rows)
    )
    flags = notes_all[:, rows : 2 * rows + WINDOW]
    lengths_all = notes_all[:, 2 * rows + WINDOW : 2 * rows + WINDOW + 3]

    def unit_columns(weight):
        return lax.dynamic_slice_in_dim(weight, me * units, units, 1)

    both_own = jnp.concatenate([unit_columns(w_gate), unit_columns(w_up)], axis=1)
    down_own = lax.dynamic_slice_in_dim(w_down, me * units, units, 0)
    both_all = lax.all_gather(both_own, "mp")
    down_all = lax.all_gather(down_own, "mp", axis=0, tiled=True)
    w_both = both_all.transpose(1, 0, 2).reshape(width, members * 2 * units)

    def head_columns(weight):
        head = lax.dynamic_slice_in_dim(weight, chip * HEAD_DIM, HEAD_DIM, 1)
        return jnp.pad(head, ((0, 0), (0, pad_head)))

    qkv_share = jnp.stack([head_columns(w_query), head_columns(w_key), head_columns(w_value)])
    out_share = jnp.pad(
        lax.dynamic_slice_in_dim(w_out, chip * HEAD_DIM, HEAD_DIM, 0), ((0, pad_head), (0, 0))
    )

    normed, _ = norm_rows(tokens_b.astype(F32))
    hidden_own = (normed * norm1_gain).astype(BF16)
    hidden_one, cotangent_all, w_qkv, w_proj = gather_first(
        hidden_own, cotangent_b, qkv_share, out_share
    )
    count = groups * rows
    hidden_one = hidden_one.reshape(count, width)
    cotangent_all = cotangent_all.reshape(count, width)
    qkv = jnp.dot(hidden_one, w_qkv, preferred_element_type=F32).astype(BF16)
    scale = HEAD_DIM ** (-0.5)
    mixed, kept = attend_ahead(
        lengths_all, qkv.reshape(groups, groups, bucket, 6 * LANES), slots, flags, scale
    )
    mixed = mixed.reshape(count, 2 * LANES)
    middle, hidden_two = project_middle(mixed, w_proj, tokens_b, norm2_gain[None])
    hidden_two = hidden_two.reshape(count, width)
    both_grad, activated = feed(hidden_two, cotangent_all, w_both, down_all)

    down_sum = jnp.einsum("tf,td->fd", activated, cotangent_all, preferred_element_type=F32)
    both_sum = jnp.einsum("td,tf->df", hidden_two, both_grad, preferred_element_type=F32)
    both_sum = both_sum.astype(BF16).reshape(width, members, 2 * units).transpose(1, 0, 2)
    down_part = lax.psum_scatter(down_sum.astype(BF16), "mp", scatter_dimension=0, tiled=True)
    both_part = lax.psum_scatter(both_sum, "mp", scatter_dimension=0)

    middle_grad, branch_all, sums_two = project_branch(
        both_grad, w_both, middle, cotangent_b, norm2_gain[None]
    )
    branch_all = branch_all.reshape(count, width)
    mixed_grad = jnp.einsum(
        "td,cd->tc", branch_all, w_proj, preferred_element_type=F32
    ).astype(BF16)
    qkv_grad = attend_back(
        lengths_all, kept, mixed_grad.reshape(groups, groups, bucket, 2 * LANES), slots, flags, scale
    ).reshape(count, 6 * LANES)
    proj_sum = jnp.einsum("tc,td->cd", mixed, branch_all, preferred_element_type=F32).astype(BF16)
    qkv_sum = jnp.einsum("td,tc->dc", hidden_one, qkv_grad, preferred_element_type=F32).astype(BF16)

    spread = jnp.arange(members, dtype=jnp.int32)
    mine = (spread // 2 == core)[:, None, None]
    qkv_heads = qkv_sum.reshape(width, 3, 2, LANES)[..., :HEAD_DIM].transpose(2, 0, 1, 3)
    qkv_heads = qkv_heads.reshape(2, width, 3 * HEAD_DIM)
    proj_heads = proj_sum.reshape(2, LANES, width)[:, :HEAD_DIM]
    none = jnp.zeros((), BF16)
    qkv_part = lax.psum_scatter(
        jnp.where(mine, jnp.tile(qkv_heads, (2, 1, 1)), none), "mp", scatter_dimension=0
    )
    proj_part = lax.psum_scatter(
        jnp.where(mine, jnp.tile(proj_heads, (2, 1, 1)), none), "mp", scatter_dimension=0
    )
    input_rows, sums_one = project_input(qkv_grad, w_qkv, tokens_b, middle_grad, norm1_gain[None])
    output_rows = project_output(activated, down_all, middle)

    gain_sums = lax.psum(
        jnp.stack([jnp.sum(sums_one, axis=0), jnp.sum(sums_two, axis=0)]), ("dp", "mp")
    )
    pick = z // 2
    both_whole = lax.all_gather(both_part, "dp").astype(F32)
    down_grad = lax.all_gather(down_part, "dp", axis=0, tiled=True).astype(F32)
    gate_grad = both_whole[:, :, :units].transpose(1, 0, 2).reshape(width, groups * units)
    up_grad = both_whole[:, :, units:].transpose(1, 0, 2).reshape(width, groups * units)
    qkv_whole = lax.all_gather(qkv_part, "dp").reshape(groups // 2, 2, width, 3, HEAD_DIM)
    qkv_whole = lax.dynamic_index_in_dim(qkv_whole, pick, 1, keepdims=False).astype(F32)
    proj_whole = lax.all_gather(proj_part, "dp").reshape(groups // 2, 2, HEAD_DIM, width)
    proj_whole = lax.dynamic_index_in_dim(proj_whole, pick, 1, keepdims=False).astype(F32)
    head_grads = qkv_whole.transpose(2, 1, 0, 3).reshape(3, width, groups // 2 * HEAD_DIM)

    unsort = (((0,), (0,)), ((), ()))
    return (
        lax.dot_general(sort_hot, output_rows, unsort, preferred_element_type=F32).astype(BF16),
        lax.dot_general(sort_hot, input_rows, unsort, preferred_element_type=F32).astype(BF16),
        gain_sums[0],
        gain_sums[1],
        head_grads[0],
        head_grads[1],
        head_grads[2],
        proj_whole.reshape(groups // 2 * HEAD_DIM, width),
        gate_grad,
        up_grad,
        down_grad,
    )


def solution(mesh):
    in_specs = (
        P(("dp", "mp"), None),
        P(("dp", "mp"), None),
        P(("dp", "mp")),
        P("dp", None),
        P("dp"),
        P(),
        P(),
        P(None, "mp"),
        P(None, "mp"),
        P(None, "mp"),
        P("mp", None),
        P(None, "mp"),
        P(None, "mp"),
        P("mp", None),
    )
    out_specs = (
        P(("dp", "mp"), None),
        P(("dp", "mp"), None),
        P(),
        P(),
        P(None, "mp"),
        P(None, "mp"),
        P(None, "mp"),
        P("mp", None),
        P(None, "mp"),
        P(None, "mp"),
        P("mp", None),
    )
    body = swapped if (mesh.shape["dp"], mesh.shape["mp"]) == (8, 4) else local
    return jax.shard_map(body, mesh=mesh, in_specs=in_specs, out_specs=out_specs, check_vma=False)
```

```python
import functools

import jax
import jax.numpy as jnp
from jax import lax
from jax.experimental import pallas as pl
from jax.experimental.pallas import tpu as pltpu
from jax.sharding import PartitionSpec as P

HEAD_DIM = 112
WINDOW = 64
TOK_DEV = 1536


EPSILON = 1e-05
MASKED = 1e30


def norm_rows(values):
    inverse = lax.rsqrt(jnp.mean(values * values, axis=-1, keepdims=True) + EPSILON)
    return (values * inverse, inverse)


def norm_back(gradient, normed, inverse, norm_gain):
    scaled = gradient * norm_gain
    result = inverse * (scaled - normed * jnp.mean(scaled * normed, axis=-1, keepdims=True))
    return (result, jnp.sum(gradient * normed, axis=0))


def padded(values, filler):
    front = jnp.full((WINDOW,) + values.shape[1:], filler, values.dtype)
    return jnp.concatenate([front, values], axis=0)


def block_scores(query_block, key_block, query_seg, key_seg, key_flag, first_row, score_scale):
    query_pos = first_row + jnp.arange(query_block.shape[0], dtype=jnp.int32)
    key_pos = first_row - WINDOW + jnp.arange(key_block.shape[0], dtype=jnp.int32)
    distance = query_pos[:, None] - key_pos[None, :]
    allowed = (distance >= 0) & (distance < WINDOW) & (query_seg[:, None] == key_seg[None, :])
    allowed = allowed & ((key_flag[None, :] == 1) | (distance == 0))
    raw_scores = (
        jnp.einsum("qhd,khd->hqk", query_block, key_block, preferred_element_type=jnp.float32)
        * score_scale
    )
    return jnp.where(allowed[None], raw_scores, -MASKED)


def block_inputs(query, key_pad, value_pad, segment, seg_pad, live_pad, first_row, block_rows):
    key_span = block_rows + WINDOW
    return (
        lax.dynamic_slice_in_dim(query, first_row, block_rows, 0),
        lax.dynamic_slice_in_dim(key_pad, first_row, key_span, 0),
        lax.dynamic_slice_in_dim(value_pad, first_row, key_span, 0),
        lax.dynamic_slice_in_dim(segment, first_row, block_rows, 0),
        lax.dynamic_slice_in_dim(seg_pad, first_row, key_span, 0),
        lax.dynamic_slice_in_dim(live_pad, first_row, key_span, 0),
    )


def attend_forward(query, key_all, value_all, segment, key_live):
    token_count, head_count, head_width = query.shape
    block_rows = min(512, token_count)
    score_scale = head_width ** (-0.5)
    key_pad = padded(key_all, 0.0)
    value_pad = padded(value_all, 0.0)
    seg_pad = padded(segment, -1)
    live_pad = padded(key_live, 0)

    def one_block(running, block_index):
        first_row = block_index * block_rows
        query_block, key_block, value_block, query_seg, key_seg, key_flag = block_inputs(
            query, key_pad, value_pad, segment, seg_pad, live_pad, first_row, block_rows
        )
        scores = block_scores(
            query_block, key_block, query_seg, key_seg, key_flag, first_row, score_scale
        )
        row_max = jnp.max(scores, axis=-1, keepdims=True)
        weights = jnp.exp(scores - row_max)
        denominator = jnp.sum(weights, axis=-1, keepdims=True)
        chances = (weights / denominator).astype(jnp.bfloat16)
        mixed = jnp.einsum("hqk,khd->qhd", chances, value_block, preferred_element_type=jnp.float32)
        return (
            running,
            (mixed.astype(jnp.bfloat16), row_max[..., 0] + jnp.log(denominator[..., 0])),
        )

    _, (mixed, logsum) = lax.scan(
        one_block, jnp.zeros((), jnp.int32), jnp.arange(token_count // block_rows, dtype=jnp.int32)
    )
    return (mixed.reshape(token_count, head_count * head_width), logsum)


def attend_backward(query, key_all, value_all, segment, key_live, logsum, mixed_grad):
    token_count, head_count, head_width = query.shape
    block_rows = min(512, token_count)
    key_span = block_rows + WINDOW
    score_scale = head_width ** (-0.5)
    key_pad = padded(key_all, 0.0)
    value_pad = padded(value_all, 0.0)
    seg_pad = padded(segment, -1)
    live_pad = padded(key_live, 0)

    def one_block(running, inputs):
        key_grad, value_grad = running
        block_index, block_logsum = inputs
        first_row = block_index * block_rows
        query_block, key_block, value_block, query_seg, key_seg, key_flag = block_inputs(
            query, key_pad, value_pad, segment, seg_pad, live_pad, first_row, block_rows
        )
        grad_block = lax.dynamic_slice_in_dim(mixed_grad, first_row, block_rows, 0)
        scores = block_scores(
            query_block, key_block, query_seg, key_seg, key_flag, first_row, score_scale
        )
        chances = jnp.exp(scores - block_logsum[..., None])
        chance_grad = jnp.einsum(
            "qhd,khd->hqk", grad_block, value_block, preferred_element_type=jnp.float32
        )
        row_dot = jnp.sum(chances * chance_grad, axis=-1, keepdims=True)
        score_grad = (chances * (chance_grad - row_dot)).astype(jnp.bfloat16)
        query_grad = (
            jnp.einsum("hqk,khd->qhd", score_grad, key_block, preferred_element_type=jnp.float32)
            * score_scale
        )
        key_part = (
            jnp.einsum("hqk,qhd->khd", score_grad, query_block, preferred_element_type=jnp.float32)
            * score_scale
        )
        value_part = jnp.einsum(
            "hqk,qhd->khd",
            chances.astype(jnp.bfloat16),
            grad_block,
            preferred_element_type=jnp.float32,
        )
        key_grad = lax.dynamic_update_slice_in_dim(
            key_grad,
            lax.dynamic_slice_in_dim(key_grad, first_row, key_span, 0) + key_part,
            first_row,
            0,
        )
        value_grad = lax.dynamic_update_slice_in_dim(
            value_grad,
            lax.dynamic_slice_in_dim(value_grad, first_row, key_span, 0) + value_part,
            first_row,
            0,
        )
        return ((key_grad, value_grad), query_grad)

    empty_grad = jnp.zeros((token_count + WINDOW, head_count, head_width), jnp.float32)
    (key_grad, value_grad), query_grad = lax.scan(
        one_block,
        (empty_grad, empty_grad),
        (jnp.arange(token_count // block_rows, dtype=jnp.int32), logsum),
    )
    flat_width = head_count * head_width
    return (
        query_grad.reshape(token_count, flat_width).astype(jnp.bfloat16),
        key_grad[WINDOW:].reshape(token_count, flat_width).astype(jnp.bfloat16),
        value_grad[WINDOW:].reshape(token_count, flat_width).astype(jnp.bfloat16),
    )


def local(
    tokens,
    cotangent,
    route,
    lengths,
    key_mask,
    norm1_gain,
    norm2_gain,
    w_query,
    w_key,
    w_value,
    w_out,
    w_gate,
    w_up,
    w_down,
):
    groups = lax.axis_size("dp")
    members = lax.axis_size("mp")
    member = lax.axis_index("mp")
    local_rows = tokens.shape[0]
    group_rows = local_rows * members
    bucket = local_rows // groups
    target = route // TOK_DEV
    chosen = (target[:, None] == jnp.arange(groups, dtype=jnp.int32)[None, :]).astype(jnp.int32)
    ranking = jnp.sum((jnp.cumsum(chosen, axis=0) - chosen) * chosen, axis=1)
    send_at = target * bucket + ranking
    arrival, arrival_grad, arrival_slot = (
        lax.all_to_all(
            jnp.zeros_like(tokens).at[send_at].set(tokens),
            "dp",
            split_axis=0,
            concat_axis=0,
            tiled=True,
        ),
        lax.all_to_all(
            jnp.zeros_like(cotangent).at[send_at].set(cotangent),
            "dp",
            split_axis=0,
            concat_axis=0,
            tiled=True,
        ),
        lax.all_to_all(
            jnp.zeros_like(route).at[send_at].set(route % local_rows),
            "dp",
            split_axis=0,
            concat_axis=0,
            tiled=True,
        ),
    )
    token_rows = jnp.zeros_like(arrival).at[arrival_slot].set(arrival)
    grad_rows = jnp.zeros_like(arrival_grad).at[arrival_slot].set(arrival_grad)
    seq_ends = jnp.cumsum(lengths[0])
    positions = jnp.arange(group_rows, dtype=jnp.int32)
    segment = jnp.sum((positions[:, None] >= seq_ends[None, :]).astype(jnp.int32), axis=1)
    input_rows = token_rows.astype(jnp.float32)
    normed_one, inverse_one = norm_rows(input_rows)
    leading_all, grad_all = (
        lax.all_gather(token_rows, "mp", axis=0, tiled=True),
        lax.all_gather(grad_rows, "mp", axis=0, tiled=True),
    )
    input_all = leading_all.astype(jnp.float32)
    normed_all, _ = norm_rows(input_all)
    hidden_one = (normed_all * norm1_gain).astype(jnp.bfloat16)
    head_count = w_query.shape[1] // HEAD_DIM
    query = jnp.dot(hidden_one, w_query, preferred_element_type=jnp.float32).astype(jnp.bfloat16)
    keys = jnp.dot(hidden_one, w_key, preferred_element_type=jnp.float32).astype(jnp.bfloat16)
    values = jnp.dot(hidden_one, w_value, preferred_element_type=jnp.float32).astype(jnp.bfloat16)
    query_heads = query.reshape(group_rows, head_count, HEAD_DIM)
    key_heads = keys.reshape(group_rows, head_count, HEAD_DIM)
    value_heads = values.reshape(group_rows, head_count, HEAD_DIM)
    mixed_flat, logsum = attend_forward(query_heads, key_heads, value_heads, segment, key_mask)
    attention_all = lax.psum(jnp.dot(mixed_flat, w_out, preferred_element_type=jnp.float32), "mp")
    middle_all = input_all + attention_all
    middle_rows = lax.dynamic_slice_in_dim(middle_all, member * local_rows, local_rows, 0)
    normed_mid, _ = norm_rows(middle_all)
    hidden_two = (normed_mid * norm2_gain).astype(jnp.bfloat16)
    normed_two, inverse_two = norm_rows(middle_rows)
    gate_value = jnp.dot(hidden_two, w_gate, preferred_element_type=jnp.float32)
    upward = jnp.dot(hidden_two, w_up, preferred_element_type=jnp.float32)
    sigmoid = jax.nn.sigmoid(gate_value)
    activated = (gate_value * sigmoid * upward).astype(jnp.bfloat16)
    out_rows = middle_rows + lax.psum_scatter(
        jnp.dot(activated, w_down, preferred_element_type=jnp.float32).astype(jnp.bfloat16),
        "mp",
        scatter_dimension=0,
        tiled=True,
    ).astype(jnp.float32)
    activated_grad = jnp.einsum("td,fd->tf", grad_all, w_down, preferred_element_type=jnp.float32)
    gate_grad = (activated_grad * upward * sigmoid * (1.0 + gate_value * (1.0 - sigmoid))).astype(
        jnp.bfloat16
    )
    upward_grad = (activated_grad * gate_value * sigmoid).astype(jnp.bfloat16)
    down_sum = jnp.einsum("tf,td->fd", activated, grad_all, preferred_element_type=jnp.float32)
    gate_sum = jnp.einsum("td,tf->df", hidden_two, gate_grad, preferred_element_type=jnp.float32)
    upward_sum = jnp.einsum(
        "td,tf->df", hidden_two, upward_grad, preferred_element_type=jnp.float32
    )
    hidden_two_grad = lax.psum_scatter(
        jnp.einsum("tf,df->td", gate_grad, w_gate, preferred_element_type=jnp.float32)
        + jnp.einsum("tf,df->td", upward_grad, w_up, preferred_element_type=jnp.float32),
        "mp",
        scatter_dimension=0,
        tiled=True,
    )
    norm_part_two, gain_two_grad = norm_back(hidden_two_grad, normed_two, inverse_two, norm2_gain)
    middle_grad = grad_rows.astype(jnp.float32) + norm_part_two
    branch_all = lax.all_gather(middle_grad.astype(jnp.bfloat16), "mp", axis=0, tiled=True)
    output_sum = jnp.einsum("tc,td->cd", mixed_flat, branch_all, preferred_element_type=jnp.float32)
    mixed_grad = jnp.einsum(
        "td,cd->tc", branch_all, w_out, preferred_element_type=jnp.float32
    ).astype(jnp.bfloat16)
    query_grad, key_grad, value_grad = attend_backward(
        query_heads,
        key_heads,
        value_heads,
        segment,
        key_mask,
        logsum,
        mixed_grad.reshape(group_rows, head_count, HEAD_DIM),
    )
    query_sum = jnp.einsum("td,tc->dc", hidden_one, query_grad, preferred_element_type=jnp.float32)
    key_sum = jnp.einsum("td,tc->dc", hidden_one, key_grad, preferred_element_type=jnp.float32)
    value_sum = jnp.einsum("td,tc->dc", hidden_one, value_grad, preferred_element_type=jnp.float32)
    hidden_one_grad = lax.psum_scatter(
        (
            jnp.einsum("tc,dc->td", query_grad, w_query, preferred_element_type=jnp.float32)
            + jnp.einsum("tc,dc->td", key_grad, w_key, preferred_element_type=jnp.float32)
            + jnp.einsum("tc,dc->td", value_grad, w_value, preferred_element_type=jnp.float32)
        ).astype(jnp.bfloat16),
        "mp",
        scatter_dimension=0,
        tiled=True,
    ).astype(jnp.float32)
    norm_part_one, gain_one_grad = norm_back(hidden_one_grad, normed_one, inverse_one, norm1_gain)
    input_grad = middle_grad + norm_part_one
    gain_one_sum, gain_two_sum = lax.psum((gain_one_grad, gain_two_grad), ("dp", "mp"))
    weight_sums = (
        lax.psum(query_sum.astype(jnp.bfloat16), "dp").astype(jnp.float32),
        lax.psum(key_sum.astype(jnp.bfloat16), "dp").astype(jnp.float32),
        lax.psum(value_sum.astype(jnp.bfloat16), "dp").astype(jnp.float32),
        lax.psum(output_sum.astype(jnp.bfloat16), "dp").astype(jnp.float32),
        lax.psum(gate_sum.astype(jnp.bfloat16), "dp").astype(jnp.float32),
        lax.psum(upward_sum.astype(jnp.bfloat16), "dp").astype(jnp.float32),
        lax.psum(down_sum.astype(jnp.bfloat16), "dp").astype(jnp.float32),
    )
    back_out, back_grad = (
        lax.all_to_all(
            out_rows.astype(jnp.bfloat16)[arrival_slot],
            "dp",
            split_axis=0,
            concat_axis=0,
            tiled=True,
        ),
        lax.all_to_all(
            input_grad.astype(jnp.bfloat16)[arrival_slot],
            "dp",
            split_axis=0,
            concat_axis=0,
            tiled=True,
        ),
    )
    return (
        back_out[send_at],
        back_grad[send_at],
        gain_one_sum,
        gain_two_sum,
        weight_sums[0],
        weight_sums[1],
        weight_sums[2],
        weight_sums[3],
        weight_sums[4],
        weight_sums[5],
        weight_sums[6],
    )


MESH = pl.DeviceIdType.MESH
LANES = 128
F32 = jnp.float32
BF16 = jnp.bfloat16
VMEM_LIMIT = 56 * 1024 * 1024


def plane():
    me = lax.axis_index("dp")
    side = me + 1 - 2 * lax.rem(me, 2)
    over_x = me + 2 - 4 * lax.rem(lax.div(me, 2), 2)
    over_y = me + 4 - 8 * lax.rem(lax.div(me, 4), 2)
    corner = over_x + 4 - 8 * lax.rem(lax.div(over_x, 4), 2)
    return (me, side, over_x, over_y, corner)


def to_dp(source, target, send_sem, recv_sem, index):
    return pltpu.make_async_remote_copy(
        src_ref=source,
        dst_ref=target,
        send_sem=send_sem,
        recv_sem=recv_sem,
        device_id={"dp": index},
        device_id_type=MESH,
    )


def to_mp(source, target, send_sem, recv_sem, index):
    return pltpu.make_async_remote_copy(
        src_ref=source,
        dst_ref=target,
        send_sem=send_sem,
        recv_sem=recv_sem,
        device_id={"mp": index},
        device_id_type=MESH,
    )


def greet_plane():
    _, side, over_x, over_y, _ = plane()
    barrier = pltpu.get_barrier_semaphore()
    for other in (side, over_x, over_y):
        pl.semaphore_signal(barrier, inc=1, device_id={"dp": other}, device_id_type=MESH)
    return barrier


class Gather:
    COUNT = 13

    def __init__(self, own, out, send, recv, local):
        me, side, over_x, over_y, corner = plane()
        half = own.shape[0] // 2
        low, high = pl.ds(0, half), pl.ds(half, half)

        def hop(number, source, target, index):
            return to_dp(source, target, send.at[number], recv.at[number], index)

        self.keep = pltpu.make_async_copy(own, out.at[me], local)
        self.first = [
            hop(0, own.at[low], out.at[me, low], over_x),
            hop(1, own.at[high], out.at[me, high], over_y),
            hop(2, own.at[high], out.at[me, high], over_x),
            hop(3, own.at[low], out.at[me, low], over_y),
            hop(4, own, out.at[me], side),
        ]
        self.onward = [
            (0, hop(5, out.at[over_x, low], out.at[over_x, low], over_y)),
            (0, hop(6, out.at[over_x, low], out.at[over_x, low], side)),
            (1, hop(7, out.at[over_y, high], out.at[over_y, high], over_x)),
            (1, hop(8, out.at[over_y, high], out.at[over_y, high], side)),
            (2, hop(9, out.at[over_x, high], out.at[over_x, high], side)),
            (3, hop(10, out.at[over_y, low], out.at[over_y, low], side)),
        ]
        self.last = [
            (5, hop(11, out.at[corner, low], out.at[corner, low], side)),
            (7, hop(12, out.at[corner, high], out.at[corner, high], side)),
        ]
        self.by_number = dict(enumerate(self.first))
        for number, copy in zip((5, 6, 7, 8, 9, 10), [c for _, c in self.onward]):
            self.by_number[number] = copy
        for number, copy in zip((11, 12), [c for _, c in self.last]):
            self.by_number[number] = copy

    def start(self):
        for copy in self.first:
            copy.start()
        self.keep.start()

    def pass_on(self):
        seen = set()
        for after, copy in self.onward:
            if after not in seen:
                self.by_number[after].wait_recv()
                seen.add(after)
            copy.start()

    def finish(self):
        for after, copy in self.last:
            self.by_number[after].wait_recv()
            copy.start()
        for number in (4, 6, 8, 9, 10, 11, 12):
            self.by_number[number].wait_recv()
        for number in range(self.COUNT):
            self.by_number[number].wait_send()
        self.keep.wait()


def greet_all(barrier):
    me, z = lax.axis_index("dp"), lax.axis_index("mp")
    for step in range(1, 8):
        pl.semaphore_signal(
            barrier, inc=1, device_id={"dp": lax.rem(me + step, 8)}, device_id_type=MESH
        )
    core = lax.rem(me, 2)
    for step in range(1, 4):
        for other in (me, me + 1 - 2 * core):
            pl.semaphore_signal(
                barrier,
                inc=1,
                device_id={"dp": other, "mp": lax.rem(z + step, 4)},
                device_id_type=MESH,
            )
    pl.semaphore_wait(barrier, 13)


def swap_all(source, target, send, recv):
    me = lax.axis_index("dp")
    return [
        to_dp(source, target.at[me], send.at[step - 1], recv.at[step - 1], lax.rem(me + step, 8))
        for step in range(1, 8)
    ]


class Spread:
    def __init__(self, qkv_share, out_share, w_qkv, w_out, send, recv, local):
        me, z = lax.axis_index("dp"), lax.axis_index("mp")
        core = lax.rem(me, 2)
        self.place = z + core * (3 - 2 * z)
        self.send, self.recv, self.local = send, recv, local
        self.shares = [qkv_share.at[0], qkv_share.at[1], qkv_share.at[2], out_share]
        self.slots = (core, 1 - core)
        self.core = core
        self.w_qkv, self.w_out = w_qkv, w_out

    def target(self, which, piece):
        slot = self.slots[which]
        if piece == 3:
            return self.w_out.at[pl.ds(pl.multiple_of(slot * LANES, LANES), LANES)]
        columns = pl.ds(pl.multiple_of((2 * piece + slot) * LANES, LANES), LANES)
        return self.w_qkv.at[:, columns]

    def hop(self, which, piece, number, place, own):
        source = self.shares[piece] if own else self.target(which, piece)
        z = place + self.core * (3 - 2 * place)
        return to_mp(
            source,
            self.target(which, piece),
            self.send.at[number * 4 + piece],
            self.recv.at[which * 4 + piece],
            z,
        )

    def keep(self, which, piece):
        return pltpu.make_async_copy(
            self.shares[piece], self.target(which, piece), self.local.at[piece]
        )

    def start(self):
        @pl.when(self.place == 0)
        def _():
            for piece in range(4):
                self.hop(0, piece, 0, 1, True).start()
                self.keep(0, piece).start()

        @pl.when(self.place == 1)
        def _():
            for piece in range(4):
                self.hop(1, piece, 0, 0, True).start()
                self.hop(1, piece, 1, 2, True).start()
                self.keep(1, piece).start()

    def pass_on(self):
        @pl.when(self.place == 1)
        def _():
            for piece in range(4):
                self.hop(0, piece, 2, 2, False).wait_recv()
                self.hop(0, piece, 2, 2, False).start()

        @pl.when(self.place == 2)
        def _():
            for piece in range(4):
                for which in (1, 0):
                    self.hop(which, piece, which, 3, False).wait_recv()
                    self.hop(which, piece, which, 3, False).start()

    def finish(self):
        @pl.when(self.place == 0)
        def _():
            for piece in range(4):
                self.hop(1, piece, 0, 1, False).wait_recv()
                self.hop(0, piece, 0, 1, True).wait_send()
                self.keep(0, piece).wait()

        @pl.when(self.place == 1)
        def _():
            for piece in range(4):
                self.hop(1, piece, 0, 0, True).wait_send()
                self.hop(1, piece, 1, 2, True).wait_send()
                self.hop(0, piece, 2, 2, False).wait_send()
                self.keep(1, piece).wait()

        @pl.when(self.place == 2)
        def _():
            for piece in range(4):
                for which in (1, 0):
                    self.hop(which, piece, which, 3, False).wait_send()

        @pl.when(self.place == 3)
        def _():
            for piece in range(4):
                for which in (1, 0):
                    self.hop(which, piece, which, 3, False).wait_recv()


def first_kernel(
    hidden, qkv_share, out_share, notes,
    hidden_all, w_qkv, w_out, notes_all,
    send_a, recv_a, send_w, recv_w, send_n, recv_n, local,
):
    greet_all(pltpu.get_barrier_semaphore())
    spread = Spread(qkv_share, out_share, w_qkv, w_out, send_w, recv_w, local)
    gather = Gather(hidden, hidden_all, send_a, recv_a, local.at[4])
    spread.start()
    gather.start()
    swaps = swap_all(notes, notes_all, send_n, recv_n)
    for copy in swaps:
        copy.start()
    keep = pltpu.make_async_copy(notes, notes_all.at[lax.axis_index("dp")], local.at[5])
    keep.start()
    spread.pass_on()
    gather.pass_on()
    gather.finish()
    spread.finish()
    for copy in swaps:
        copy.wait()
    keep.wait()


def anywhere():
    return pl.BlockSpec(memory_space=pl.ANY)


def on_chip():
    return pl.BlockSpec(memory_space=pltpu.VMEM)


def in_scalar():
    return pl.BlockSpec(memory_space=pltpu.SMEM)


def remote_params(number, limit=VMEM_LIMIT):
    return pltpu.CompilerParams(
        collective_id=number, has_side_effects=True, vmem_limit_bytes=limit
    )


def gather_first(hidden, qkv_share, out_share, notes):
    rows, width = hidden.shape
    groups = lax.axis_size("dp")
    dma = pltpu.SemaphoreType.DMA
    return pl.pallas_call(
        first_kernel,
        out_shape=(
            jax.ShapeDtypeStruct((groups, rows, width), BF16),
            jax.ShapeDtypeStruct((width, 6 * LANES), BF16),
            jax.ShapeDtypeStruct((2 * LANES, width), BF16),
            jax.ShapeDtypeStruct((groups,) + notes.shape, notes.dtype),
        ),
        in_specs=[on_chip()] * 4,
        out_specs=(anywhere(),) * 4,
        scratch_shapes=[
            dma((13,)), dma((13,)), dma((12,)), dma((8,)), dma((7,)), dma((7,)), dma((6,)),
        ],
        compiler_params=remote_params(1),
        cost_estimate=pl.CostEstimate(flops=0, bytes_accessed=200_000_000, transcendentals=0),
        name="gather_first",
    )(hidden, qkv_share, out_share, notes)


def one_hot(slots, k, size):
    row = slots[pl.ds(k, 1), :]
    place = lax.broadcasted_iota(jnp.int32, (size, size), 0)
    return (place == row).astype(BF16)


def block_mask(lengths, flags, k, block, z, rows):
    position = rows * z + block * 128 + lax.broadcasted_iota(jnp.int32, (128, 1), 0)
    first_end = lengths[k, 0]
    second_end = first_end + lengths[k, 1]
    begin = jnp.where(position >= first_end, first_end, 0)
    begin = jnp.where(position >= second_end, second_end, begin)
    column = lax.broadcasted_iota(jnp.int32, (128, 192), 1)
    distance = 64 + lax.broadcasted_iota(jnp.int32, (128, 192), 0) - column
    key_position = rows * z + block * 128 - 64 + column
    live = flags[pl.ds(k, 1), block * 128 : block * 128 + 192]
    allowed = (distance >= 0) & (distance < WINDOW) & (key_position >= begin)
    return allowed & ((live == 1) | (distance == 0))


NT = (((1,), (1,)), ((), ()))
TN = (((0,), (0,)), ((), ()))


def forward_kernel(
    lengths, qkv, slots, flags, cotangent, mixed, kept, cotangent_all,
    send, recv, send_g, recv_g, local, *, scale, groups, rows
):
    z = lax.axis_index("mp")
    members = lax.axis_size("mp")
    barrier = greet_plane()

    @pl.when(z > 0)
    def _():
        pl.semaphore_signal(barrier, inc=1, device_id={"mp": z - 1}, device_id_type=MESH)

    @pl.when(z < members - 1)
    def _():
        pl.semaphore_wait(barrier, 4)

    @pl.when(z == members - 1)
    def _():
        pl.semaphore_wait(barrier, 3)

    gather = Gather(cotangent, cotangent_all, send_g, recv_g, local)
    gather.start()

    def halo(k, other):
        return to_mp(
            kept.at[k, pl.ds(rows, 64), pl.ds(256, 512)],
            kept.at[k, pl.ds(0, 64), pl.ds(256, 512)],
            send.at[k],
            recv.at[k],
            other,
        )

    def order(k, carry):
        hot = one_hot(slots, k, rows)
        given = qkv[:, pl.ds(k, 1)].reshape(rows, 768)
        kept[k, pl.ds(64, rows), :] = jnp.dot(hot, given, preferred_element_type=F32).astype(BF16)
        kept[k, pl.ds(0, 64), pl.ds(0, 256)] = jnp.zeros((64, 256), BF16)

        @pl.when(z < members - 1)
        def _():
            halo(k, z + 1).start()

        @pl.when(z == 0)
        def _():
            kept[k, pl.ds(0, 64), pl.ds(256, 512)] = jnp.zeros((64, 512), BF16)

        return carry

    lax.fori_loop(0, groups, order, 0)

    def attend(k, carry):
        @pl.when(z > 0)
        def _():
            halo(k, z).wait_recv()

        hot = one_hot(slots, k, rows)
        found = []
        for block in range(rows // 128):
            allowed = block_mask(lengths, flags, k, block, z, rows)
            heads = []
            for head in range(2):
                query = kept[k, pl.ds(64 + block * 128, 128), pl.ds(head * 128, 128)]
                keys = kept[k, pl.ds(block * 128, 192), pl.ds(256 + head * 128, 128)]
                values = kept[k, pl.ds(block * 128, 192), pl.ds(512 + head * 128, 128)]
                scores = lax.dot_general(query, keys, NT, preferred_element_type=F32) * scale
                scores = jnp.where(allowed, scores, -MASKED)
                weights = jnp.exp(scores - jnp.max(scores, axis=-1, keepdims=True))
                total = jnp.sum(weights, axis=-1, keepdims=True)
                chances = (weights / total).astype(BF16)
                heads.append(jnp.dot(chances, values, preferred_element_type=F32).astype(BF16))
            found.append(jnp.concatenate(heads, axis=1))
        ordered = jnp.concatenate(found, axis=0)
        back = lax.dot_general(hot, ordered, TN, preferred_element_type=F32).astype(BF16)
        mixed[:, pl.ds(k, 1)] = back.reshape(groups, 1, rows // groups, 256)
        return carry

    lax.fori_loop(0, groups - 2, attend, 0)
    gather.pass_on()
    lax.fori_loop(groups - 2, groups, attend, 0)
    gather.finish()

    @pl.when(z < members - 1)
    def _():
        def done(k, carry):
            halo(k, z + 1).wait_send()
            return carry

        lax.fori_loop(0, groups, done, 0)


def attend_ahead(lengths, qkv, slots, flags, cotangent, scale):
    groups = qkv.shape[0]
    rows = slots.shape[1]
    dma = pltpu.SemaphoreType.DMA
    return pl.pallas_call(
        functools.partial(forward_kernel, scale=scale, groups=groups, rows=rows),
        out_shape=(
            jax.ShapeDtypeStruct((groups, groups, rows // groups, 256), BF16),
            jax.ShapeDtypeStruct((groups, rows + 64, 768), BF16),
            jax.ShapeDtypeStruct((groups,) + cotangent.shape, BF16),
        ),
        in_specs=[in_scalar()] + [on_chip()] * 4,
        out_specs=(on_chip(), on_chip(), anywhere()),
        scratch_shapes=[dma((groups,)), dma((groups,)), dma((13,)), dma((13,)), dma(())],
        compiler_params=remote_params(2),
        cost_estimate=pl.CostEstimate(flops=0, bytes_accessed=150_000_000, transcendentals=0),
        name="attend_ahead",
    )(lengths, qkv, slots, flags, cotangent)


def feed_kernel(hidden, cotangent, w_both, w_down, both_grad, activated, *, members):
    rows = hidden[...]
    grad = lax.dot_general(cotangent[...], w_down[...], NT, preferred_element_type=F32)
    for part in range(members):
        raw = jnp.dot(rows, w_both[part], preferred_element_type=F32)
        gate, upward = raw[:, :128], raw[:, 128:]
        active_grad = grad[:, part * 128 : part * 128 + 128]
        sigmoid = jax.nn.sigmoid(gate)
        activated[:, part * 128 : part * 128 + 128] = (gate * sigmoid * upward).astype(BF16)
        both_grad[:, part * 256 : part * 256 + 128] = (
            active_grad * upward * sigmoid * (1.0 + gate * (1.0 - sigmoid))
        ).astype(BF16)
        both_grad[:, part * 256 + 128 : part * 256 + 256] = (
            active_grad * gate * sigmoid
        ).astype(BF16)


def feed(hidden, cotangent, w_both, w_down):
    count, width = hidden.shape
    wide = w_both.shape[0] * 256
    units = w_down.shape[0]
    tile = 256
    return pl.pallas_call(
        functools.partial(feed_kernel, members=wide // 256),
        grid=(count // tile,),
        out_shape=(
            jax.ShapeDtypeStruct((count, wide), BF16),
            jax.ShapeDtypeStruct((count, units), BF16),
        ),
        in_specs=[
            pl.BlockSpec((tile, width), lambda i: (i, 0)),
            pl.BlockSpec((tile, width), lambda i: (i, 0)),
            pl.BlockSpec(w_both.shape, lambda i: (0, 0, 0)),
            pl.BlockSpec((units, width), lambda i: (0, 0)),
        ],
        out_specs=(
            pl.BlockSpec((tile, wide), lambda i: (i, 0)),
            pl.BlockSpec((tile, units), lambda i: (i, 0)),
        ),
        compiler_params=pltpu.CompilerParams(vmem_limit_bytes=VMEM_LIMIT),
        cost_estimate=pl.CostEstimate(
            flops=2 * count * width * (wide + units), bytes_accessed=50_000_000, transcendentals=0
        ),
        name="feed",
    )(hidden, cotangent, w_both, w_down)


CHUNK = 32


def each_chunk(rows, body):
    def step(i, carry):
        body(pl.ds(pl.multiple_of(i * CHUNK, CHUNK), CHUNK))
        return carry

    lax.fori_loop(0, rows // CHUNK, step, 0)


class Reduce:
    COUNT = 10

    def __init__(self, left, right, across, part, from_side, from_corner, from_near, send, recv):
        self.left, self.right, self.across, self.part = left, right, across, part
        self.from_side, self.from_corner, self.from_near = from_side, from_corner, from_near
        self.send, self.recv = send, recv
        self.rows = part.shape[1]

    def product(self, owner, slot):
        rows, width = self.rows, self.part.shape[2]
        picked = pl.ds(pl.multiple_of(owner * rows, rows), rows)

        def tile(t, carry):
            columns = pl.ds(pl.multiple_of(t * 256, 256), 256)
            if self.across == 3:
                value = sum(
                    lax.dot_general(
                        self.left[picked, part * 256 : part * 256 + 256],
                        self.right[part, columns, :],
                        NT,
                        preferred_element_type=F32,
                    )
                    for part in range(self.right.shape[0])
                )
            elif self.across == 2:
                value = lax.dot_general(
                    self.left[picked, :], self.right[columns, :], NT, preferred_element_type=F32
                )
            else:
                value = jnp.dot(
                    self.left[picked, :], self.right[:, columns], preferred_element_type=F32
                )
            self.part[slot, :, columns] = value.astype(BF16)
            return carry

        lax.fori_loop(0, width // 256, tile, 0)

    def prepare(self):
        _, side, over_x, over_y, corner = plane()
        part, near = self.part, self.from_near
        half = self.rows // 2
        low, high = pl.ds(0, half), pl.ds(half, half)

        def hop(number, source, target, index):
            return to_dp(source, target, self.send.at[number], self.recv.at[number], index)

        self.shares = [hop(i, part.at[4 + i], self.from_side.at[i], side) for i in range(4)]
        self.corners = [
            hop(4, part.at[0, low], self.from_corner.at[0], over_x),
            hop(5, part.at[0, high], self.from_corner.at[1], over_y),
        ]
        self.nears = [
            hop(6, part.at[1, low], near.at[0, low], over_x),
            hop(7, part.at[1, high], near.at[0, high], over_x),
            hop(8, part.at[2, high], near.at[1, high], over_y),
            hop(9, part.at[2, low], near.at[1, low], over_y),
        ]

    def add_side(self, slot):
        self.shares[slot].wait_recv()

        def body(span):
            self.part[slot, span, :] = (
                self.part[slot, span, :].astype(F32) + self.from_side[slot, span, :].astype(F32)
            ).astype(BF16)

        each_chunk(self.rows, body)

    def add_corner(self, slot, offset, which):
        self.corners[which].wait_recv()

        def body(span):
            target = pl.ds(pl.multiple_of(offset + span.start, CHUNK), CHUNK)
            self.part[slot, target, :] = (
                self.part[slot, target, :].astype(F32)
                + self.from_corner[which, span, :].astype(F32)
            ).astype(BF16)

        each_chunk(self.rows // 2, body)

    def begin(self):
        self.prepare()
        me, _, over_x, over_y, corner = plane()
        owners = (corner, over_x, over_y, me)
        turn = 1 - 2 * lax.rem(me, 2)
        self.product(corner + turn, 4)
        self.shares[0].start()
        self.product(corner, 0)
        self.product(over_x + turn, 5)
        self.shares[1].start()
        self.add_side(0)
        self.corners[0].start()
        self.corners[1].start()
        self.product(over_x, 1)
        self.product(over_y + turn, 6)
        self.shares[2].start()
        self.add_side(1)
        self.nears[0].start()
        self.product(over_y, 2)
        self.product(me + turn, 7)
        self.shares[3].start()
        self.add_side(2)
        self.nears[2].start()
        self.product(me, 3)

    def middle(self):
        self.add_corner(2, 0, 0)
        self.nears[3].start()
        self.add_corner(1, self.rows // 2, 1)
        self.nears[1].start()

    def end(self):
        self.shares[3].wait_recv()
        for copy in self.nears:
            copy.wait_recv()

    def run(self):
        self.begin()
        self.middle()
        self.end()

    def rows_of(self, span):
        return (
            self.part[3, span, :].astype(F32)
            + self.from_side[3, span, :].astype(F32)
            + self.from_near[0, span, :].astype(F32)
            + self.from_near[1, span, :].astype(F32)
        )

    def finish(self):
        for copy in self.shares + self.corners + self.nears:
            copy.wait_send()


def reduce_scratch(rows, width):
    dma = pltpu.SemaphoreType.DMA
    return [
        pltpu.VMEM((8, rows, width), BF16),
        pltpu.VMEM((4, rows, width), BF16),
        pltpu.VMEM((2, rows // 2, width), BF16),
        pltpu.VMEM((2, rows, width), BF16),
        dma((10,)),
        dma((10,)),
    ]


def gather_scratch(rows, width):
    dma = pltpu.SemaphoreType.DMA
    return [pltpu.VMEM((rows, width), BF16), dma((13,)), dma((13,)), dma(())]


def mean_rows(values):
    return jnp.mean(values, axis=-1, keepdims=True)


class Heads:
    def __init__(self, source, arrive, send, recv, views):
        me, z = lax.axis_index("dp"), lax.axis_index("mp")
        self.me, self.z = me, z
        self.core = lax.rem(me, 2)
        self.source, self.arrive, self.send, self.recv, self.views = source, arrive, send, recv, views
        self.owner = lax.div(z, 2)

    def copy(self, slot, half, number):
        target_z = 2 * self.core + slot
        index = (slot * 2 + half) * self.views + number
        return to_at(
            self.view(slot, half, number),
            self.arrive.at[self.z, number],
            self.send.at[index],
            self.recv.at[self.z * self.views + number],
            self.me - self.core + half,
            target_z,
        )

    def view(self, slot, half, number):
        if self.views == 1:
            rows = pl.ds(pl.multiple_of(slot * LANES, LANES), LANES)
            return self.source.at[rows, pl.ds(half * 896, 896)]
        columns = pl.ds(pl.multiple_of((2 * number + slot) * LANES, LANES), LANES)
        return self.source.at[pl.ds(half * 896, 896), columns]

    def each(self, action):
        for slot in range(2):
            for half in range(2):
                mine = (2 * self.core + slot == self.z) & (self.core == half)

                @pl.when(jnp.logical_not(mine))
                def _():
                    for number in range(self.views):
                        action(self.copy(slot, half, number))

    def start(self):
        self.each(lambda copy: copy.start())

    def finish_send(self):
        self.each(lambda copy: copy.wait_send())

    def total(self, out):
        me, z = self.me, self.z
        for number in range(self.views):
            for other in range(4):
                waiting = to_at(
                    self.view(0, 0, number),
                    self.arrive.at[other, number],
                    self.send.at[0],
                    self.recv.at[other * self.views + number],
                    me,
                    other,
                )

                @pl.when((z != other) | (self.core != self.owner))
                def _():
                    waiting.wait_recv()

                @pl.when((z == other) & (self.core == self.owner))
                def _():
                    half = self.core
                    slot = lax.rem(z, 2)
                    if self.views == 1:
                        rows = pl.ds(pl.multiple_of(slot * LANES, LANES), LANES)
                        columns = pl.ds(pl.multiple_of(half * 896, LANES), 896)
                        self.arrive[other, number] = self.source[rows, columns]
                    else:
                        rows = pl.ds(pl.multiple_of(half * 896, LANES), 896)
                        columns = pl.ds(pl.multiple_of((2 * number + slot) * LANES, LANES), LANES)
                        self.arrive[other, number] = self.source[rows, columns]

            count = self.arrive.shape[2]

            def body(span):
                found = self.arrive[0, number, span, :].astype(F32)
                for other in range(1, 4):
                    found = found + self.arrive[other, number, span, :].astype(F32)
                out[number, span, :] = found.astype(BF16)

            each_chunk(count, body)


def to_at(source, target, send_sem, recv_sem, dp, mp):
    return pltpu.make_async_remote_copy(
        src_ref=source,
        dst_ref=target,
        send_sem=send_sem,
        recv_sem=recv_sem,
        device_id={"dp": dp, "mp": mp},
        device_id_type=MESH,
    )


def backward_kernel(
    lengths, kept, mixed_grad, slots, flags, activated, w_down, middle, proj_sum,
    out, result, proj_part,
    totals, query_part, key_value, ending, leaving, arriving, send, recv,
    part, from_side, from_corner, from_near, send_r, recv_r, arrive, send_h, recv_h,
    *, scale, groups, rows,
):
    z = lax.axis_index("mp")
    members = lax.axis_size("mp")
    greet_all(pltpu.get_barrier_semaphore())
    heads = Heads(proj_sum, arrive, send_h, recv_h, 1)
    heads.start()
    reduce = Reduce(activated, w_down, 0, part, from_side, from_corner, from_near, send_r, recv_r)
    reduce.begin()

    def halo(k, other):
        return to_mp(leaving.at[k], arriving.at[k], send.at[k], recv.at[k], other)

    def attend(k, carry):
        hot = one_hot(slots, k, rows)
        given = mixed_grad[:, pl.ds(k, 1)].reshape(rows, 256)
        grad_ordered = jnp.dot(hot, given, preferred_element_type=F32).astype(BF16)
        totals[...] = jnp.zeros_like(totals)
        for block in range(rows // 128):
            allowed = block_mask(lengths, flags, k, block, z, rows)
            for head in range(2):
                query = kept[k, pl.ds(64 + block * 128, 128), pl.ds(head * 128, 128)]
                keys = kept[k, pl.ds(block * 128, 192), pl.ds(256 + head * 128, 128)]
                values = kept[k, pl.ds(block * 128, 192), pl.ds(512 + head * 128, 128)]
                grad = grad_ordered[block * 128 : block * 128 + 128, head * 128 : head * 128 + 128]
                scores = lax.dot_general(query, keys, NT, preferred_element_type=F32) * scale
                scores = jnp.where(allowed, scores, -MASKED)
                weights = jnp.exp(scores - jnp.max(scores, axis=-1, keepdims=True))
                again = weights / jnp.sum(weights, axis=-1, keepdims=True)
                chance_grad = lax.dot_general(grad, values, NT, preferred_element_type=F32)
                row_dot = jnp.sum(again * chance_grad, axis=-1, keepdims=True)
                score_grad = (again * (chance_grad - row_dot)).astype(BF16)
                query_part[k, pl.ds(block * 128, 128), pl.ds(head * 128, 128)] = (
                    jnp.dot(score_grad, keys, preferred_element_type=F32) * scale
                ).astype(BF16)
                totals[pl.ds(block * 128, 192), pl.ds(head * 128, 128)] += (
                    lax.dot_general(score_grad, query, TN, preferred_element_type=F32) * scale
                )
                totals[pl.ds(block * 128, 192), pl.ds(256 + head * 128, 128)] += lax.dot_general(
                    again.astype(BF16), grad, TN, preferred_element_type=F32
                )
        key_value[k] = totals[pl.ds(64, rows), :].astype(BF16)
        ending[k] = totals[pl.ds(rows, 64), :]

        @pl.when(z > 0)
        def _():
            leaving[k] = totals[pl.ds(0, 64), :].astype(BF16)
            halo(k, z - 1).start()

        return carry

    lax.fori_loop(0, groups - 5, attend, 0)
    reduce.middle()
    lax.fori_loop(groups - 5, groups, attend, 0)

    def restore(k, carry):
        @pl.when(z < members - 1)
        def _():
            halo(k, z).wait_recv()
            key_value[k, pl.ds(rows - 64, 64), :] = (
                ending[k] + arriving[k].astype(F32)
            ).astype(BF16)

        hot = one_hot(slots, k, rows)
        ordered = jnp.concatenate([query_part[k], key_value[k]], axis=1)
        back = lax.dot_general(hot, ordered, TN, preferred_element_type=F32).astype(BF16)
        out[:, pl.ds(k, 1)] = back.reshape(groups, 1, rows // groups, 768)
        return carry

    lax.fori_loop(0, groups, restore, 0)
    reduce.end()

    def body(span):
        result[span, :] = (middle[span, :] + reduce.rows_of(span)).astype(BF16)

    each_chunk(rows, body)
    heads.total(proj_part)
    heads.finish_send()
    reduce.finish()

    @pl.when(z > 0)
    def _():
        def done(k, carry):
            halo(k, z - 1).wait_send()
            return carry

        lax.fori_loop(0, groups, done, 0)


def attend_back(
    lengths, kept, mixed_grad, slots, flags, activated, w_down, middle, proj_sum, scale
):
    groups = kept.shape[0]
    rows, width = middle.shape
    dma = pltpu.SemaphoreType.DMA
    return pl.pallas_call(
        functools.partial(backward_kernel, scale=scale, groups=groups, rows=rows),
        out_shape=(
            jax.ShapeDtypeStruct((groups, groups, rows // groups, 768), BF16),
            jax.ShapeDtypeStruct((rows, width), BF16),
            jax.ShapeDtypeStruct((1, LANES, width // 2), BF16),
        ),
        in_specs=[in_scalar()] + [on_chip()] * 8,
        out_specs=(on_chip(), on_chip(), on_chip()),
        scratch_shapes=[
            pltpu.VMEM((rows + 64, 512), F32),
            pltpu.VMEM((groups, rows, 256), BF16),
            pltpu.VMEM((groups, rows, 512), BF16),
            pltpu.VMEM((groups, 64, 512), F32),
            pltpu.VMEM((groups, 64, 512), BF16),
            pltpu.VMEM((groups, 64, 512), BF16),
            dma((groups,)),
            dma((groups,)),
        ]
        + reduce_scratch(rows, width)
        + [pltpu.VMEM((4, 1, LANES, width // 2), BF16), dma((4,)), dma((4,))],
        compiler_params=remote_params(3, 62 * 1024 * 1024),
        cost_estimate=pl.CostEstimate(flops=0, bytes_accessed=200_000_000, transcendentals=0),
        name="attend_back",
    )(lengths, kept, mixed_grad, slots, flags, activated, w_down, middle, proj_sum)


def middle_kernel(
    mixed, w_out, tokens, gain, middle, hidden_all,
    part, from_side, from_corner, from_near, send, recv, own, send_g, recv_g, local,
):
    pl.semaphore_wait(greet_plane(), 3)
    reduce = Reduce(mixed, w_out, 0, part, from_side, from_corner, from_near, send, recv)
    reduce.run()

    def body(span):
        values = tokens[span, :].astype(F32) + reduce.rows_of(span)
        middle[span, :] = values
        inverse = lax.rsqrt(mean_rows(values * values) + EPSILON)
        own[span, :] = (values * inverse * gain[...]).astype(BF16)

    each_chunk(own.shape[0], body)
    gather = Gather(own, hidden_all, send_g, recv_g, local)
    gather.start()
    gather.pass_on()
    gather.finish()
    reduce.finish()


def project_middle(mixed, w_out, tokens, gain):
    rows, width = tokens.shape
    groups = lax.axis_size("dp")
    return pl.pallas_call(
        middle_kernel,
        out_shape=(
            jax.ShapeDtypeStruct((rows, width), F32),
            jax.ShapeDtypeStruct((groups, rows, width), BF16),
        ),
        in_specs=[on_chip()] * 4,
        out_specs=(on_chip(), anywhere()),
        scratch_shapes=reduce_scratch(rows, width) + gather_scratch(rows, width),
        compiler_params=remote_params(4),
        cost_estimate=pl.CostEstimate(flops=0, bytes_accessed=300_000_000, transcendentals=0),
        name="project_middle",
    )(mixed, w_out, tokens, gain)


def norm_back_rows(gradient, values, gain, sums, span):
    inverse = lax.rsqrt(mean_rows(values * values) + EPSILON)
    normed = values * inverse
    product = gradient * normed
    folded = product[0:8]
    for step in range(1, CHUNK // 8):
        folded = folded + product[step * 8 : step * 8 + 8]
    sums[...] += folded
    scaled = gradient * gain
    return inverse * (scaled - normed * mean_rows(scaled * normed))


def branch_kernel(
    both_grad, w_both, middle, cotangent, gain, middle_grad, branch_all, sums,
    part, from_side, from_corner, from_near, send, recv, own, send_g, recv_g, local,
):
    pl.semaphore_wait(greet_plane(), 3)
    reduce = Reduce(both_grad, w_both, 3, part, from_side, from_corner, from_near, send, recv)
    reduce.run()
    sums[...] = jnp.zeros_like(sums)

    def body(span):
        change = norm_back_rows(reduce.rows_of(span), middle[span, :], gain[...], sums, span)
        total = cotangent[span, :].astype(F32) + change
        middle_grad[span, :] = total
        own[span, :] = total.astype(BF16)

    each_chunk(own.shape[0], body)
    gather = Gather(own, branch_all, send_g, recv_g, local)
    gather.start()
    gather.pass_on()
    gather.finish()
    reduce.finish()


def project_branch(both_grad, w_both, middle, cotangent, gain):
    rows, width = middle.shape
    groups = lax.axis_size("dp")
    return pl.pallas_call(
        branch_kernel,
        out_shape=(
            jax.ShapeDtypeStruct((rows, width), F32),
            jax.ShapeDtypeStruct((groups, rows, width), BF16),
            jax.ShapeDtypeStruct((8, width), F32),
        ),
        in_specs=[on_chip()] * 5,
        out_specs=(on_chip(), anywhere(), on_chip()),
        scratch_shapes=reduce_scratch(rows, width) + gather_scratch(rows, width),
        compiler_params=remote_params(5),
        cost_estimate=pl.CostEstimate(flops=0, bytes_accessed=300_000_000, transcendentals=0),
        name="project_branch",
    )(both_grad, w_both, middle, cotangent, gain)


def input_kernel(
    qkv_grad, w_qkv, tokens, middle_grad, gain, sums_two, qkv_sum, result, qkv_part, gains,
    part, from_side, from_corner, from_near, send, recv, sums,
    arrive, send_h, recv_h, own, plane_sums, column_sums, send_s, recv_s,
):
    me, z = lax.axis_index("dp"), lax.axis_index("mp")
    greet_all(pltpu.get_barrier_semaphore())
    heads = Heads(qkv_sum, arrive, send_h, recv_h, 3)
    heads.start()
    reduce = Reduce(qkv_grad, w_qkv, 2, part, from_side, from_corner, from_near, send, recv)
    reduce.run()
    sums[...] = jnp.zeros_like(sums)

    def body(span):
        values = tokens[span, :].astype(F32)
        change = norm_back_rows(reduce.rows_of(span), values, gain[...], sums, span)
        result[span, :] = (middle_grad[span, :] + change).astype(BF16)

    each_chunk(result.shape[0], body)
    own[...] = jnp.concatenate(
        [
            jnp.sum(sums[...], axis=0, keepdims=True),
            jnp.sum(sums_two[...], axis=0, keepdims=True),
        ],
        axis=0,
    )
    swaps = swap_all(own, plane_sums, send_s, recv_s)
    for copy in swaps:
        copy.start()
    plane_sums[me] = own[...]
    for copy in swaps:
        copy.wait()
    found = plane_sums[0]
    for other in range(1, 8):
        found = found + plane_sums[other]
    column_sums[z] = found
    passes = [
        to_mp(
            column_sums.at[z],
            column_sums.at[z],
            send_s.at[6 + step],
            recv_s.at[6 + step],
            lax.rem(z + step, 4),
        )
        for step in range(1, 4)
    ]
    for copy in passes:
        copy.start()
    for copy in passes:
        copy.wait()
    gains[...] = (column_sums[0] + column_sums[1]) + (column_sums[2] + column_sums[3])
    heads.total(qkv_part)
    heads.finish_send()
    reduce.finish()


def project_input(qkv_grad, w_qkv, tokens, middle_grad, gain, sums_two, qkv_sum):
    rows, width = tokens.shape
    dma = pltpu.SemaphoreType.DMA
    return pl.pallas_call(
        input_kernel,
        out_shape=(
            jax.ShapeDtypeStruct((rows, width), BF16),
            jax.ShapeDtypeStruct((3, width // 2, LANES), BF16),
            jax.ShapeDtypeStruct((2, width), F32),
        ),
        in_specs=[on_chip()] * 7,
        out_specs=(on_chip(),) * 3,
        scratch_shapes=reduce_scratch(rows, width)
        + [
            pltpu.VMEM((8, width), F32),
            pltpu.VMEM((4, 3, width // 2, LANES), BF16),
            dma((12,)),
            dma((12,)),
            pltpu.VMEM((2, width), F32),
            pltpu.VMEM((8, 2, width), F32),
            pltpu.VMEM((4, 2, width), F32),
            dma((10,)),
            dma((10,)),
        ],
        compiler_params=remote_params(6),
        cost_estimate=pl.CostEstimate(flops=0, bytes_accessed=200_000_000, transcendentals=0),
        name="project_input",
    )(qkv_grad, w_qkv, tokens, middle_grad, gain, sums_two, qkv_sum)


def units_kernel(both, gate, upward):
    for d in range(both.shape[0]):
        gate[:, d * 128 : d * 128 + 128] = both[d, :, :128].astype(F32)
        upward[:, d * 128 : d * 128 + 128] = both[d, :, 128:].astype(F32)


def assemble_units(both):
    groups, width, wide = both.shape
    tile = 256
    shape = jax.ShapeDtypeStruct((width, groups * wide // 2), F32)
    spec = pl.BlockSpec((tile, groups * wide // 2), lambda i: (i, 0))
    return pl.pallas_call(
        units_kernel,
        grid=(width // tile,),
        out_shape=(shape, shape),
        in_specs=[pl.BlockSpec((groups, tile, wide), lambda i: (0, i, 0))],
        out_specs=(spec, spec),
        cost_estimate=pl.CostEstimate(flops=0, bytes_accessed=22_000_000, transcendentals=0),
        name="assemble_units",
    )(both)


def heads_kernel(whole, query, keys, values):
    for part, out in enumerate((query, keys, values)):
        out[...] = jnp.concatenate(
            [whole[c, 0, part, :, :HEAD_DIM].astype(F32) for c in range(whole.shape[0])], axis=1
        )


def assemble_heads(whole):
    chips, halves, _, rows, _ = whole.shape
    tile = 448
    count = rows // tile
    shape = jax.ShapeDtypeStruct((halves * rows, chips * HEAD_DIM), F32)
    spec = pl.BlockSpec((tile, chips * HEAD_DIM), lambda h, i: (h * count + i, 0))
    return pl.pallas_call(
        heads_kernel,
        grid=(halves, count),
        out_shape=(shape,) * 3,
        in_specs=[pl.BlockSpec((chips, 1, 3, tile, LANES), lambda h, i: (0, h, 0, i, 0))],
        out_specs=(spec,) * 3,
        cost_estimate=pl.CostEstimate(flops=0, bytes_accessed=15_000_000, transcendentals=0),
        name="assemble_heads",
    )(whole)


def swapped(
    tokens, cotangent, route, lengths, key_mask, norm1_gain, norm2_gain,
    w_query, w_key, w_value, w_out, w_gate, w_up, w_down,
):
    groups = lax.axis_size("dp")
    members = lax.axis_size("mp")
    me = lax.axis_index("dp")
    z = lax.axis_index("mp")
    rows, width = tokens.shape
    bucket = rows // groups
    units = w_down.shape[0] // groups
    chip, core = me // 2, me % 2
    pad_head = LANES - HEAD_DIM

    target = route // TOK_DEV
    earlier = jnp.arange(rows, dtype=jnp.int32)
    same = (target[:, None] == target[None, :]) & (earlier[None, :] < earlier[:, None])
    send_at = target * bucket + jnp.sum(same.astype(jnp.int32), axis=1)
    sorting = send_at[None, :] == earlier[:, None]
    slots_own = jnp.sum(jnp.where(sorting, (route % rows)[None, :], 0), axis=1)
    sort_hot = sorting.astype(BF16)
    tokens_b = jnp.dot(sort_hot, tokens, preferred_element_type=F32).astype(BF16)
    cotangent_b = jnp.dot(sort_hot, cotangent, preferred_element_type=F32).astype(BF16)

    mask_window = lax.dynamic_slice_in_dim(
        jnp.concatenate([jnp.zeros((WINDOW,), jnp.int32), key_mask]), z * rows, rows + WINDOW
    )
    notes = jnp.concatenate([slots_own, mask_window, lengths[0]])
    notes = jnp.pad(notes, (0, 8 * LANES - notes.shape[0])).reshape(8, LANES)

    def head_columns(weight):
        head = lax.dynamic_slice_in_dim(weight, chip * HEAD_DIM, HEAD_DIM, 1)
        return jnp.pad(head, ((0, 0), (0, pad_head)))

    qkv_share = jnp.stack([head_columns(w_query), head_columns(w_key), head_columns(w_value)])
    out_share = jnp.pad(
        lax.dynamic_slice_in_dim(w_out, chip * HEAD_DIM, HEAD_DIM, 0), ((0, pad_head), (0, 0))
    )

    normed, _ = norm_rows(tokens_b.astype(F32))
    hidden_own = (normed * norm1_gain).astype(BF16)
    hidden_one, w_qkv, w_proj, notes_all = gather_first(hidden_own, qkv_share, out_share, notes)
    notes_all = notes_all.reshape(groups, 8 * LANES)
    slots = (
        notes_all[:, :rows].reshape(groups, groups, bucket).transpose(1, 0, 2).reshape(groups, rows)
    )
    flags = notes_all[:, rows : 2 * rows + WINDOW]
    lengths_all = notes_all[:, 2 * rows + WINDOW : 2 * rows + WINDOW + 3]

    w_gate, w_up, w_down, hidden_one = lax.optimization_barrier((w_gate, w_up, w_down, hidden_one))

    def unit_columns(weight):
        return lax.dynamic_slice_in_dim(weight, me * units, units, 1)

    both_own = jnp.concatenate([unit_columns(w_gate), unit_columns(w_up)], axis=1)
    down_own = lax.dynamic_slice_in_dim(w_down, me * units, units, 0)
    w_both = lax.all_gather(both_own, "mp")
    down_all = lax.all_gather(down_own, "mp", axis=0, tiled=True)

    count = groups * rows
    hidden_one = hidden_one.reshape(count, width)
    qkv = jnp.dot(hidden_one, w_qkv, preferred_element_type=F32).astype(BF16)
    scale = HEAD_DIM ** (-0.5)
    mixed, kept, cotangent_all = attend_ahead(
        lengths_all,
        qkv.reshape(groups, groups, bucket, 6 * LANES),
        slots,
        flags,
        cotangent_b,
        scale,
    )
    cotangent_all = cotangent_all.reshape(count, width)
    mixed = mixed.reshape(count, 2 * LANES)
    middle, hidden_two = project_middle(mixed, w_proj, tokens_b, norm2_gain[None])
    hidden_two = hidden_two.reshape(count, width)
    both_grad, activated = feed(hidden_two, cotangent_all, w_both, down_all)

    down_sum = jnp.einsum("tf,td->fd", activated, cotangent_all, preferred_element_type=F32)
    both_sum = jnp.einsum("td,tf->df", hidden_two, both_grad, preferred_element_type=F32)
    both_sum = both_sum.astype(BF16).reshape(width, members, 2 * units).transpose(1, 0, 2)
    down_sum, both_sum, both_grad = lax.optimization_barrier(
        (down_sum.astype(BF16), both_sum, both_grad)
    )
    down_part = lax.psum_scatter(down_sum, "mp", scatter_dimension=0, tiled=True)
    both_part = lax.psum_scatter(both_sum, "mp", scatter_dimension=0)

    middle_grad, branch_all, sums_two = project_branch(
        both_grad, w_both, middle, cotangent_b, norm2_gain[None]
    )
    down_part, both_part, branch_all = lax.optimization_barrier((down_part, both_part, branch_all))
    both_whole = lax.all_gather(both_part, "dp")
    down_whole = lax.all_gather(down_part, "dp", axis=0, tiled=True)
    branch_all = branch_all.reshape(count, width)
    mixed_grad = jnp.einsum(
        "td,cd->tc", branch_all, w_proj, preferred_element_type=F32
    ).astype(BF16)
    proj_sum = jnp.einsum("tc,td->cd", mixed, branch_all, preferred_element_type=F32).astype(BF16)
    qkv_grad, output_rows, proj_part = attend_back(
        lengths_all,
        kept,
        mixed_grad.reshape(groups, groups, bucket, 2 * LANES),
        slots,
        flags,
        activated,
        down_all,
        middle,
        proj_sum,
        scale,
    )
    qkv_grad = qkv_grad.reshape(count, 6 * LANES)
    qkv_sum = jnp.einsum("td,tc->dc", hidden_one, qkv_grad, preferred_element_type=F32).astype(BF16)
    input_rows, qkv_part, gain_sums = project_input(
        qkv_grad, w_qkv, tokens_b, middle_grad, norm1_gain[None], sums_two, qkv_sum
    )
    proj_part, qkv_part, both_whole, down_whole = lax.optimization_barrier(
        (proj_part, qkv_part, both_whole, down_whole)
    )
    chips = groups // 2
    qkv_whole = lax.all_gather(qkv_part.reshape(3 * width // 2, LANES), "dp")
    proj_whole = lax.all_gather(proj_part[0], "dp")
    gate_grad, up_grad = assemble_units(both_whole)
    down_grad = down_whole.astype(F32)
    query_grad, key_grad, value_grad = assemble_heads(
        qkv_whole.reshape(chips, 2, 3, width // 2, LANES)
    )
    proj_grad = proj_whole.reshape(chips, 2, LANES, width // 2)[:, :, :HEAD_DIM]
    proj_grad = proj_grad.transpose(0, 2, 1, 3).reshape(chips * HEAD_DIM, width).astype(F32)

    unsort = (((0,), (0,)), ((), ()))
    return (
        lax.dot_general(sort_hot, output_rows, unsort, preferred_element_type=F32).astype(BF16),
        lax.dot_general(sort_hot, input_rows, unsort, preferred_element_type=F32).astype(BF16),
        gain_sums[0],
        gain_sums[1],
        query_grad,
        key_grad,
        value_grad,
        proj_grad,
        gate_grad,
        up_grad,
        down_grad,
    )


def solution(mesh):
    in_specs = (
        P(("dp", "mp"), None),
        P(("dp", "mp"), None),
        P(("dp", "mp")),
        P("dp", None),
        P("dp"),
        P(),
        P(),
        P(None, "mp"),
        P(None, "mp"),
        P(None, "mp"),
        P("mp", None),
        P(None, "mp"),
        P(None, "mp"),
        P("mp", None),
    )
    out_specs = (
        P(("dp", "mp"), None),
        P(("dp", "mp"), None),
        P(),
        P(),
        P(None, "mp"),
        P(None, "mp"),
        P(None, "mp"),
        P("mp", None),
        P(None, "mp"),
        P(None, "mp"),
        P("mp", None),
    )
    body = swapped if (mesh.shape["dp"], mesh.shape["mp"]) == (8, 4) else local
    return jax.shard_map(body, mesh=mesh, in_specs=in_specs, out_specs=out_specs, check_vma=False)
```

```python
import functools

import jax
import jax.numpy as jnp
from jax import lax
from jax.experimental import pallas as pl
from jax.experimental.pallas import tpu as pltpu
from jax.sharding import PartitionSpec as P

HEAD_DIM = 112
WINDOW = 64
TOK_DEV = 1536


EPSILON = 1e-05
MASKED = 1e30


def norm_rows(values):
    inverse = lax.rsqrt(jnp.mean(values * values, axis=-1, keepdims=True) + EPSILON)
    return (values * inverse, inverse)


def norm_back(gradient, normed, inverse, norm_gain):
    scaled = gradient * norm_gain
    result = inverse * (scaled - normed * jnp.mean(scaled * normed, axis=-1, keepdims=True))
    return (result, jnp.sum(gradient * normed, axis=0))


def padded(values, filler):
    front = jnp.full((WINDOW,) + values.shape[1:], filler, values.dtype)
    return jnp.concatenate([front, values], axis=0)


def block_scores(query_block, key_block, query_seg, key_seg, key_flag, first_row, score_scale):
    query_pos = first_row + jnp.arange(query_block.shape[0], dtype=jnp.int32)
    key_pos = first_row - WINDOW + jnp.arange(key_block.shape[0], dtype=jnp.int32)
    distance = query_pos[:, None] - key_pos[None, :]
    allowed = (distance >= 0) & (distance < WINDOW) & (query_seg[:, None] == key_seg[None, :])
    allowed = allowed & ((key_flag[None, :] == 1) | (distance == 0))
    raw_scores = (
        jnp.einsum("qhd,khd->hqk", query_block, key_block, preferred_element_type=jnp.float32)
        * score_scale
    )
    return jnp.where(allowed[None], raw_scores, -MASKED)


def block_inputs(query, key_pad, value_pad, segment, seg_pad, live_pad, first_row, block_rows):
    key_span = block_rows + WINDOW
    return (
        lax.dynamic_slice_in_dim(query, first_row, block_rows, 0),
        lax.dynamic_slice_in_dim(key_pad, first_row, key_span, 0),
        lax.dynamic_slice_in_dim(value_pad, first_row, key_span, 0),
        lax.dynamic_slice_in_dim(segment, first_row, block_rows, 0),
        lax.dynamic_slice_in_dim(seg_pad, first_row, key_span, 0),
        lax.dynamic_slice_in_dim(live_pad, first_row, key_span, 0),
    )


def attend_forward(query, key_all, value_all, segment, key_live):
    token_count, head_count, head_width = query.shape
    block_rows = min(512, token_count)
    score_scale = head_width ** (-0.5)
    key_pad = padded(key_all, 0.0)
    value_pad = padded(value_all, 0.0)
    seg_pad = padded(segment, -1)
    live_pad = padded(key_live, 0)

    def one_block(running, block_index):
        first_row = block_index * block_rows
        query_block, key_block, value_block, query_seg, key_seg, key_flag = block_inputs(
            query, key_pad, value_pad, segment, seg_pad, live_pad, first_row, block_rows
        )
        scores = block_scores(
            query_block, key_block, query_seg, key_seg, key_flag, first_row, score_scale
        )
        row_max = jnp.max(scores, axis=-1, keepdims=True)
        weights = jnp.exp(scores - row_max)
        denominator = jnp.sum(weights, axis=-1, keepdims=True)
        chances = (weights / denominator).astype(jnp.bfloat16)
        mixed = jnp.einsum("hqk,khd->qhd", chances, value_block, preferred_element_type=jnp.float32)
        return (
            running,
            (mixed.astype(jnp.bfloat16), row_max[..., 0] + jnp.log(denominator[..., 0])),
        )

    _, (mixed, logsum) = lax.scan(
        one_block, jnp.zeros((), jnp.int32), jnp.arange(token_count // block_rows, dtype=jnp.int32)
    )
    return (mixed.reshape(token_count, head_count * head_width), logsum)


def attend_backward(query, key_all, value_all, segment, key_live, logsum, mixed_grad):
    token_count, head_count, head_width = query.shape
    block_rows = min(512, token_count)
    key_span = block_rows + WINDOW
    score_scale = head_width ** (-0.5)
    key_pad = padded(key_all, 0.0)
    value_pad = padded(value_all, 0.0)
    seg_pad = padded(segment, -1)
    live_pad = padded(key_live, 0)

    def one_block(running, inputs):
        key_grad, value_grad = running
        block_index, block_logsum = inputs
        first_row = block_index * block_rows
        query_block, key_block, value_block, query_seg, key_seg, key_flag = block_inputs(
            query, key_pad, value_pad, segment, seg_pad, live_pad, first_row, block_rows
        )
        grad_block = lax.dynamic_slice_in_dim(mixed_grad, first_row, block_rows, 0)
        scores = block_scores(
            query_block, key_block, query_seg, key_seg, key_flag, first_row, score_scale
        )
        chances = jnp.exp(scores - block_logsum[..., None])
        chance_grad = jnp.einsum(
            "qhd,khd->hqk", grad_block, value_block, preferred_element_type=jnp.float32
        )
        row_dot = jnp.sum(chances * chance_grad, axis=-1, keepdims=True)
        score_grad = (chances * (chance_grad - row_dot)).astype(jnp.bfloat16)
        query_grad = (
            jnp.einsum("hqk,khd->qhd", score_grad, key_block, preferred_element_type=jnp.float32)
            * score_scale
        )
        key_part = (
            jnp.einsum("hqk,qhd->khd", score_grad, query_block, preferred_element_type=jnp.float32)
            * score_scale
        )
        value_part = jnp.einsum(
            "hqk,qhd->khd",
            chances.astype(jnp.bfloat16),
            grad_block,
            preferred_element_type=jnp.float32,
        )
        key_grad = lax.dynamic_update_slice_in_dim(
            key_grad,
            lax.dynamic_slice_in_dim(key_grad, first_row, key_span, 0) + key_part,
            first_row,
            0,
        )
        value_grad = lax.dynamic_update_slice_in_dim(
            value_grad,
            lax.dynamic_slice_in_dim(value_grad, first_row, key_span, 0) + value_part,
            first_row,
            0,
        )
        return ((key_grad, value_grad), query_grad)

    empty_grad = jnp.zeros((token_count + WINDOW, head_count, head_width), jnp.float32)
    (key_grad, value_grad), query_grad = lax.scan(
        one_block,
        (empty_grad, empty_grad),
        (jnp.arange(token_count // block_rows, dtype=jnp.int32), logsum),
    )
    flat_width = head_count * head_width
    return (
        query_grad.reshape(token_count, flat_width).astype(jnp.bfloat16),
        key_grad[WINDOW:].reshape(token_count, flat_width).astype(jnp.bfloat16),
        value_grad[WINDOW:].reshape(token_count, flat_width).astype(jnp.bfloat16),
    )


def local(
    tokens,
    cotangent,
    route,
    lengths,
    key_mask,
    norm1_gain,
    norm2_gain,
    w_query,
    w_key,
    w_value,
    w_out,
    w_gate,
    w_up,
    w_down,
):
    groups = lax.axis_size("dp")
    members = lax.axis_size("mp")
    member = lax.axis_index("mp")
    local_rows = tokens.shape[0]
    group_rows = local_rows * members
    bucket = local_rows // groups
    target = route // TOK_DEV
    chosen = (target[:, None] == jnp.arange(groups, dtype=jnp.int32)[None, :]).astype(jnp.int32)
    ranking = jnp.sum((jnp.cumsum(chosen, axis=0) - chosen) * chosen, axis=1)
    send_at = target * bucket + ranking
    arrival, arrival_grad, arrival_slot = (
        lax.all_to_all(
            jnp.zeros_like(tokens).at[send_at].set(tokens),
            "dp",
            split_axis=0,
            concat_axis=0,
            tiled=True,
        ),
        lax.all_to_all(
            jnp.zeros_like(cotangent).at[send_at].set(cotangent),
            "dp",
            split_axis=0,
            concat_axis=0,
            tiled=True,
        ),
        lax.all_to_all(
            jnp.zeros_like(route).at[send_at].set(route % local_rows),
            "dp",
            split_axis=0,
            concat_axis=0,
            tiled=True,
        ),
    )
    token_rows = jnp.zeros_like(arrival).at[arrival_slot].set(arrival)
    grad_rows = jnp.zeros_like(arrival_grad).at[arrival_slot].set(arrival_grad)
    seq_ends = jnp.cumsum(lengths[0])
    positions = jnp.arange(group_rows, dtype=jnp.int32)
    segment = jnp.sum((positions[:, None] >= seq_ends[None, :]).astype(jnp.int32), axis=1)
    input_rows = token_rows.astype(jnp.float32)
    normed_one, inverse_one = norm_rows(input_rows)
    leading_all, grad_all = (
        lax.all_gather(token_rows, "mp", axis=0, tiled=True),
        lax.all_gather(grad_rows, "mp", axis=0, tiled=True),
    )
    input_all = leading_all.astype(jnp.float32)
    normed_all, _ = norm_rows(input_all)
    hidden_one = (normed_all * norm1_gain).astype(jnp.bfloat16)
    head_count = w_query.shape[1] // HEAD_DIM
    query = jnp.dot(hidden_one, w_query, preferred_element_type=jnp.float32).astype(jnp.bfloat16)
    keys = jnp.dot(hidden_one, w_key, preferred_element_type=jnp.float32).astype(jnp.bfloat16)
    values = jnp.dot(hidden_one, w_value, preferred_element_type=jnp.float32).astype(jnp.bfloat16)
    query_heads = query.reshape(group_rows, head_count, HEAD_DIM)
    key_heads = keys.reshape(group_rows, head_count, HEAD_DIM)
    value_heads = values.reshape(group_rows, head_count, HEAD_DIM)
    mixed_flat, logsum = attend_forward(query_heads, key_heads, value_heads, segment, key_mask)
    attention_all = lax.psum(jnp.dot(mixed_flat, w_out, preferred_element_type=jnp.float32), "mp")
    middle_all = input_all + attention_all
    middle_rows = lax.dynamic_slice_in_dim(middle_all, member * local_rows, local_rows, 0)
    normed_mid, _ = norm_rows(middle_all)
    hidden_two = (normed_mid * norm2_gain).astype(jnp.bfloat16)
    normed_two, inverse_two = norm_rows(middle_rows)
    gate_value = jnp.dot(hidden_two, w_gate, preferred_element_type=jnp.float32)
    upward = jnp.dot(hidden_two, w_up, preferred_element_type=jnp.float32)
    sigmoid = jax.nn.sigmoid(gate_value)
    activated = (gate_value * sigmoid * upward).astype(jnp.bfloat16)
    out_rows = middle_rows + lax.psum_scatter(
        jnp.dot(activated, w_down, preferred_element_type=jnp.float32).astype(jnp.bfloat16),
        "mp",
        scatter_dimension=0,
        tiled=True,
    ).astype(jnp.float32)
    activated_grad = jnp.einsum("td,fd->tf", grad_all, w_down, preferred_element_type=jnp.float32)
    gate_grad = (activated_grad * upward * sigmoid * (1.0 + gate_value * (1.0 - sigmoid))).astype(
        jnp.bfloat16
    )
    upward_grad = (activated_grad * gate_value * sigmoid).astype(jnp.bfloat16)
    down_sum = jnp.einsum("tf,td->fd", activated, grad_all, preferred_element_type=jnp.float32)
    gate_sum = jnp.einsum("td,tf->df", hidden_two, gate_grad, preferred_element_type=jnp.float32)
    upward_sum = jnp.einsum(
        "td,tf->df", hidden_two, upward_grad, preferred_element_type=jnp.float32
    )
    hidden_two_grad = lax.psum_scatter(
        jnp.einsum("tf,df->td", gate_grad, w_gate, preferred_element_type=jnp.float32)
        + jnp.einsum("tf,df->td", upward_grad, w_up, preferred_element_type=jnp.float32),
        "mp",
        scatter_dimension=0,
        tiled=True,
    )
    norm_part_two, gain_two_grad = norm_back(hidden_two_grad, normed_two, inverse_two, norm2_gain)
    middle_grad = grad_rows.astype(jnp.float32) + norm_part_two
    branch_all = lax.all_gather(middle_grad.astype(jnp.bfloat16), "mp", axis=0, tiled=True)
    output_sum = jnp.einsum("tc,td->cd", mixed_flat, branch_all, preferred_element_type=jnp.float32)
    mixed_grad = jnp.einsum(
        "td,cd->tc", branch_all, w_out, preferred_element_type=jnp.float32
    ).astype(jnp.bfloat16)
    query_grad, key_grad, value_grad = attend_backward(
        query_heads,
        key_heads,
        value_heads,
        segment,
        key_mask,
        logsum,
        mixed_grad.reshape(group_rows, head_count, HEAD_DIM),
    )
    query_sum = jnp.einsum("td,tc->dc", hidden_one, query_grad, preferred_element_type=jnp.float32)
    key_sum = jnp.einsum("td,tc->dc", hidden_one, key_grad, preferred_element_type=jnp.float32)
    value_sum = jnp.einsum("td,tc->dc", hidden_one, value_grad, preferred_element_type=jnp.float32)
    hidden_one_grad = lax.psum_scatter(
        (
            jnp.einsum("tc,dc->td", query_grad, w_query, preferred_element_type=jnp.float32)
            + jnp.einsum("tc,dc->td", key_grad, w_key, preferred_element_type=jnp.float32)
            + jnp.einsum("tc,dc->td", value_grad, w_value, preferred_element_type=jnp.float32)
        ).astype(jnp.bfloat16),
        "mp",
        scatter_dimension=0,
        tiled=True,
    ).astype(jnp.float32)
    norm_part_one, gain_one_grad = norm_back(hidden_one_grad, normed_one, inverse_one, norm1_gain)
    input_grad = middle_grad + norm_part_one
    gain_one_sum, gain_two_sum = lax.psum((gain_one_grad, gain_two_grad), ("dp", "mp"))
    weight_sums = (
        lax.psum(query_sum.astype(jnp.bfloat16), "dp").astype(jnp.float32),
        lax.psum(key_sum.astype(jnp.bfloat16), "dp").astype(jnp.float32),
        lax.psum(value_sum.astype(jnp.bfloat16), "dp").astype(jnp.float32),
        lax.psum(output_sum.astype(jnp.bfloat16), "dp").astype(jnp.float32),
        lax.psum(gate_sum.astype(jnp.bfloat16), "dp").astype(jnp.float32),
        lax.psum(upward_sum.astype(jnp.bfloat16), "dp").astype(jnp.float32),
        lax.psum(down_sum.astype(jnp.bfloat16), "dp").astype(jnp.float32),
    )
    back_out, back_grad = (
        lax.all_to_all(
            out_rows.astype(jnp.bfloat16)[arrival_slot],
            "dp",
            split_axis=0,
            concat_axis=0,
            tiled=True,
        ),
        lax.all_to_all(
            input_grad.astype(jnp.bfloat16)[arrival_slot],
            "dp",
            split_axis=0,
            concat_axis=0,
            tiled=True,
        ),
    )
    return (
        back_out[send_at],
        back_grad[send_at],
        gain_one_sum,
        gain_two_sum,
        weight_sums[0],
        weight_sums[1],
        weight_sums[2],
        weight_sums[3],
        weight_sums[4],
        weight_sums[5],
        weight_sums[6],
    )


MESH = pl.DeviceIdType.MESH
LANES = 128
F32 = jnp.float32
BF16 = jnp.bfloat16
VMEM_LIMIT = 56 * 1024 * 1024


def plane():
    me = lax.axis_index("dp")
    side = me + 1 - 2 * lax.rem(me, 2)
    over_x = me + 2 - 4 * lax.rem(lax.div(me, 2), 2)
    over_y = me + 4 - 8 * lax.rem(lax.div(me, 4), 2)
    corner = over_x + 4 - 8 * lax.rem(lax.div(over_x, 4), 2)
    return (me, side, over_x, over_y, corner)


def to_dp(source, target, send_sem, recv_sem, index):
    return pltpu.make_async_remote_copy(
        src_ref=source,
        dst_ref=target,
        send_sem=send_sem,
        recv_sem=recv_sem,
        device_id={"dp": index},
        device_id_type=MESH,
    )


def to_mp(source, target, send_sem, recv_sem, index):
    return pltpu.make_async_remote_copy(
        src_ref=source,
        dst_ref=target,
        send_sem=send_sem,
        recv_sem=recv_sem,
        device_id={"mp": index},
        device_id_type=MESH,
    )


def greet_plane():
    _, side, over_x, over_y, _ = plane()
    barrier = pltpu.get_barrier_semaphore()
    for other in (side, over_x, over_y):
        pl.semaphore_signal(barrier, inc=1, device_id={"dp": other}, device_id_type=MESH)
    return barrier


class Gather:
    AFTER = {0: (5, 6), 1: (7, 8), 2: (9,), 3: (10,), 5: (11,), 7: (12,)}

    def __init__(self, own, out, send, recv, local=None):
        me, side, over_x, over_y, corner = plane()
        half = out.shape[1] // 2
        low, high = pl.ds(0, half), pl.ds(half, half)
        self.keep = None if own is None else pltpu.make_async_copy(own, out.at[me], local)
        own = out.at[me] if own is None else own

        def hop(number, source, target, index):
            return to_dp(source, target, send.at[number], recv.at[number], index)

        def onward(number, owner, part, index):
            place = out.at[owner, part]
            return hop(number, place, place, index)

        self.copies = [
            hop(0, own.at[low], out.at[me, low], over_x),
            hop(1, own.at[high], out.at[me, high], over_y),
            hop(2, own.at[high], out.at[me, high], over_x),
            hop(3, own.at[low], out.at[me, low], over_y),
            hop(4, own, out.at[me], side),
            onward(5, over_x, low, over_y),
            onward(6, over_x, low, side),
            onward(7, over_y, high, over_x),
            onward(8, over_y, high, side),
            onward(9, over_x, high, side),
            onward(10, over_y, low, side),
            onward(11, corner, low, side),
            onward(12, corner, high, side),
        ]

    def start(self):
        for number in range(5):
            self.copies[number].start()
        if self.keep is not None:
            self.keep.start()

    def arrive(self, *numbers):
        for number in numbers:
            self.copies[number].wait_recv()
            for later in self.AFTER.get(number, ()):
                self.copies[later].start()

    def pass_on(self):
        self.arrive(0, 1, 2, 3)

    def sent(self):
        for copy in self.copies:
            copy.wait_send()
        if self.keep is not None:
            self.keep.wait()

    def finish(self):
        self.arrive(5, 7, 4, 6, 8, 9, 10, 11, 12)
        self.sent()


def greet_all(barrier):
    me, z = lax.axis_index("dp"), lax.axis_index("mp")
    for step in range(1, 8):
        pl.semaphore_signal(
            barrier, inc=1, device_id={"dp": lax.rem(me + step, 8)}, device_id_type=MESH
        )
    core = lax.rem(me, 2)
    for step in range(1, 4):
        for other in (me, me + 1 - 2 * core):
            pl.semaphore_signal(
                barrier,
                inc=1,
                device_id={"dp": other, "mp": lax.rem(z + step, 4)},
                device_id_type=MESH,
            )
    pl.semaphore_wait(barrier, 13)


def swap_all(source, target, send, recv):
    me = lax.axis_index("dp")
    return [
        to_dp(source, target.at[me], send.at[step - 1], recv.at[step - 1], lax.rem(me + step, 8))
        for step in range(1, 8)
    ]


class Spread:
    def __init__(self, share, w_qkv, w_out, send, recv, local):
        me, z = lax.axis_index("dp"), lax.axis_index("mp")
        core = lax.rem(me, 2)
        self.place = z + core * (3 - 2 * z)
        self.send, self.recv, self.local = send, recv, local
        self.shares = [share.at[0], share.at[1], share.at[2], share.at[3]]
        self.slots = (core, 1 - core)
        self.core = core
        self.w_qkv, self.w_out = w_qkv, w_out

    def target(self, which, piece):
        slot = self.slots[which]
        block = slot if piece == 3 else 2 * piece + slot
        rows = pl.ds(pl.multiple_of(block * LANES, LANES), HEAD_DIM)
        return (self.w_out if piece == 3 else self.w_qkv).at[rows]

    def hop(self, which, piece, number, place, own):
        source = self.shares[piece] if own else self.target(which, piece)
        z = place + self.core * (3 - 2 * place)
        return to_mp(
            source,
            self.target(which, piece),
            self.send.at[number * 4 + piece],
            self.recv.at[which * 4 + piece],
            z,
        )

    def keep(self, which, piece):
        return pltpu.make_async_copy(
            self.shares[piece], self.target(which, piece), self.local.at[piece]
        )

    def start(self):
        @pl.when(self.place == 0)
        def _():
            for piece in range(4):
                self.hop(0, piece, 0, 1, True).start()
                self.keep(0, piece).start()

        @pl.when(self.place == 1)
        def _():
            for piece in range(4):
                self.hop(1, piece, 0, 0, True).start()
                self.hop(1, piece, 1, 2, True).start()
                self.keep(1, piece).start()

    def pass_on(self):
        @pl.when(self.place == 1)
        def _():
            for piece in range(4):
                self.hop(0, piece, 2, 2, False).wait_recv()
                self.hop(0, piece, 2, 2, False).start()

        @pl.when(self.place == 2)
        def _():
            for piece in range(4):
                for which in (1, 0):
                    self.hop(which, piece, which, 3, False).wait_recv()
                    self.hop(which, piece, which, 3, False).start()

    def finish(self):
        @pl.when(self.place == 0)
        def _():
            for piece in range(4):
                self.hop(1, piece, 0, 1, False).wait_recv()
                self.hop(0, piece, 0, 1, True).wait_send()
                self.keep(0, piece).wait()

        @pl.when(self.place == 1)
        def _():
            for piece in range(4):
                self.hop(1, piece, 0, 0, True).wait_send()
                self.hop(1, piece, 1, 2, True).wait_send()
                self.hop(0, piece, 2, 2, False).wait_send()
                self.keep(1, piece).wait()

        @pl.when(self.place == 2)
        def _():
            for piece in range(4):
                for which in (1, 0):
                    self.hop(which, piece, which, 3, False).wait_send()

        @pl.when(self.place == 3)
        def _():
            for piece in range(4):
                for which in (1, 0):
                    self.hop(which, piece, which, 3, False).wait_recv()


def first_kernel(
    hidden, query, keys, values, project, notes,
    hidden_all, w_qkv, w_out, notes_all,
    share, none, send_a, recv_a, send_w, recv_w, send_n, recv_n, local,
):
    me = lax.axis_index("dp")
    head = pl.ds(pl.multiple_of(lax.div(me, 2) * HEAD_DIM, 16), HEAD_DIM)
    loads = [
        pltpu.make_async_copy(source.at[head], share.at[piece], local.at[piece])
        for piece, source in enumerate((query, keys, values, project))
    ]
    for copy in loads:
        copy.start()
    none[...] = jnp.zeros_like(none)
    greet_all(pltpu.get_barrier_semaphore())
    gather = Gather(hidden, hidden_all, send_a, recv_a, local.at[4])
    gather.start()
    swaps = swap_all(notes, notes_all, send_n, recv_n)
    for copy in swaps:
        copy.start()
    keep = pltpu.make_async_copy(notes, notes_all.at[me], local.at[5])
    keep.start()
    pads = [
        pltpu.make_async_copy(
            none, weight.at[pl.ds(block * LANES + HEAD_DIM, LANES - HEAD_DIM)], local.at[6 + number]
        )
        for number, (weight, block) in enumerate(
            [(w_qkv, block) for block in range(6)] + [(w_out, block) for block in range(2)]
        )
    ]
    for copy in pads:
        copy.start()
    for copy in loads:
        copy.wait()
    spread = Spread(share, w_qkv, w_out, send_w, recv_w, local)
    spread.start()
    spread.pass_on()
    gather.pass_on()
    gather.finish()
    spread.finish()
    for copy in swaps:
        copy.wait()
    for copy in pads:
        copy.wait()
    keep.wait()


def anywhere():
    return pl.BlockSpec(memory_space=pl.ANY)


def on_chip():
    return pl.BlockSpec(memory_space=pltpu.VMEM)


def in_scalar():
    return pl.BlockSpec(memory_space=pltpu.SMEM)


def remote_params(number, limit=VMEM_LIMIT):
    return pltpu.CompilerParams(
        collective_id=number, has_side_effects=True, vmem_limit_bytes=limit
    )


def gather_first(hidden, query, keys, values, project, notes):
    rows, width = hidden.shape
    groups = lax.axis_size("dp")
    dma = pltpu.SemaphoreType.DMA
    return pl.pallas_call(
        first_kernel,
        out_shape=(
            jax.ShapeDtypeStruct((groups, rows, width), BF16),
            jax.ShapeDtypeStruct((6 * LANES, width), BF16),
            jax.ShapeDtypeStruct((2 * LANES, width), BF16),
            jax.ShapeDtypeStruct((groups,) + notes.shape, notes.dtype),
        ),
        in_specs=[on_chip()] + [anywhere()] * 4 + [on_chip()],
        out_specs=(anywhere(),) * 4,
        scratch_shapes=[
            pltpu.VMEM((4, HEAD_DIM, width), BF16),
            pltpu.VMEM((LANES - HEAD_DIM, width), BF16),
            dma((13,)), dma((13,)), dma((12,)), dma((8,)), dma((7,)), dma((7,)), dma((14,)),
        ],
        compiler_params=remote_params(1),
        cost_estimate=pl.CostEstimate(flops=0, bytes_accessed=200_000_000, transcendentals=0),
        name="gather_first",
    )(hidden, query, keys, values, project, notes)


def one_hot(slots, k, size):
    row = slots[pl.ds(k, 1), :]
    place = lax.broadcasted_iota(jnp.int32, (size, size), 0)
    return (place == row).astype(BF16)


def block_mask(lengths, flags, k, block, z, rows):
    position = rows * z + block * 128 + lax.broadcasted_iota(jnp.int32, (128, 1), 0)
    first_end = lengths[k, 0]
    second_end = first_end + lengths[k, 1]
    begin = jnp.where(position >= first_end, first_end, 0)
    begin = jnp.where(position >= second_end, second_end, begin)
    column = lax.broadcasted_iota(jnp.int32, (128, 192), 1)
    distance = 64 + lax.broadcasted_iota(jnp.int32, (128, 192), 0) - column
    key_position = rows * z + block * 128 - 64 + column
    live = flags[pl.ds(k, 1), block * 128 : block * 128 + 192]
    allowed = (distance >= 0) & (distance < WINDOW) & (key_position >= begin)
    return allowed & ((live == 1) | (distance == 0))


NT = (((1,), (1,)), ((), ()))
TN = (((0,), (0,)), ((), ()))


def forward_kernel(
    lengths, hidden_all, w_qkv, slots, flags, cotangent, mixed, kept, cotangent_all,
    qkv, shard, shard_sem, send, recv, send_g, recv_g, local, *, scale, groups, rows
):
    z = lax.axis_index("mp")
    members = lax.axis_size("mp")
    barrier = greet_plane()

    @pl.when(z > 0)
    def _():
        pl.semaphore_signal(barrier, inc=1, device_id={"mp": z - 1}, device_id_type=MESH)

    @pl.when(z < members - 1)
    def _():
        pl.semaphore_wait(barrier, 4)

    @pl.when(z == members - 1)
    def _():
        pl.semaphore_wait(barrier, 3)

    gather = Gather(cotangent, cotangent_all, send_g, recv_g, local)
    gather.start()

    def load(g):
        slot = lax.rem(g, 2)
        return pltpu.make_async_copy(hidden_all.at[g], shard.at[slot], shard_sem.at[slot])

    load(0).start()

    def multiply(g, carry):
        @pl.when(g < groups - 1)
        def _():
            load(g + 1).start()

        load(g).wait()
        product = lax.dot_general(
            shard[lax.rem(g, 2)], w_qkv[...], NT, preferred_element_type=F32
        ).astype(BF16)
        qkv[g] = product.reshape(groups, rows // groups, 768)
        return carry

    lax.fori_loop(0, groups, multiply, 0)

    def halo(k, other):
        return to_mp(
            kept.at[k, pl.ds(rows, 64), pl.ds(256, 512)],
            kept.at[k, pl.ds(0, 64), pl.ds(256, 512)],
            send.at[k],
            recv.at[k],
            other,
        )

    def order(k, carry):
        hot = one_hot(slots, k, rows)
        given = qkv[:, pl.ds(k, 1)].reshape(rows, 768)
        kept[k, pl.ds(64, rows), :] = jnp.dot(hot, given, preferred_element_type=F32).astype(BF16)
        kept[k, pl.ds(0, 64), pl.ds(0, 256)] = jnp.zeros((64, 256), BF16)

        @pl.when(z < members - 1)
        def _():
            halo(k, z + 1).start()

        @pl.when(z == 0)
        def _():
            kept[k, pl.ds(0, 64), pl.ds(256, 512)] = jnp.zeros((64, 512), BF16)

        return carry

    lax.fori_loop(0, groups, order, 0)

    def attend(k, carry):
        @pl.when(z > 0)
        def _():
            halo(k, z).wait_recv()

        hot = one_hot(slots, k, rows)
        found = []
        for block in range(rows // 128):
            allowed = block_mask(lengths, flags, k, block, z, rows)
            heads = []
            for head in range(2):
                query = kept[k, pl.ds(64 + block * 128, 128), pl.ds(head * 128, 128)]
                keys = kept[k, pl.ds(block * 128, 192), pl.ds(256 + head * 128, 128)]
                values = kept[k, pl.ds(block * 128, 192), pl.ds(512 + head * 128, 128)]
                scores = lax.dot_general(query, keys, NT, preferred_element_type=F32) * scale
                scores = jnp.where(allowed, scores, -MASKED)
                weights = jnp.exp(scores - jnp.max(scores, axis=-1, keepdims=True))
                total = jnp.sum(weights, axis=-1, keepdims=True)
                chances = (weights / total).astype(BF16)
                heads.append(jnp.dot(chances, values, preferred_element_type=F32).astype(BF16))
            found.append(jnp.concatenate(heads, axis=1))
        ordered = jnp.concatenate(found, axis=0)
        back = lax.dot_general(hot, ordered, TN, preferred_element_type=F32).astype(BF16)
        mixed[:, pl.ds(k, 1)] = back.reshape(groups, 1, rows // groups, 256)
        return carry

    lax.fori_loop(0, groups // 4, attend, 0)
    gather.pass_on()
    lax.fori_loop(groups // 4, groups, attend, 0)
    gather.finish()

    @pl.when(z < members - 1)
    def _():
        def done(k, carry):
            halo(k, z + 1).wait_send()
            return carry

        lax.fori_loop(0, groups, done, 0)


def attend_ahead(lengths, hidden_all, w_qkv, slots, flags, cotangent, scale):
    groups, rows, width = hidden_all.shape
    dma = pltpu.SemaphoreType.DMA
    return pl.pallas_call(
        functools.partial(forward_kernel, scale=scale, groups=groups, rows=rows),
        out_shape=(
            jax.ShapeDtypeStruct((groups, groups, rows // groups, 256), BF16),
            jax.ShapeDtypeStruct((groups, rows + 64, 768), BF16),
            jax.ShapeDtypeStruct((groups,) + cotangent.shape, BF16),
        ),
        in_specs=[in_scalar(), anywhere()] + [on_chip()] * 4,
        out_specs=(on_chip(), on_chip(), anywhere()),
        scratch_shapes=[
            pltpu.VMEM((groups, groups, rows // groups, 768), BF16),
            pltpu.VMEM((2, rows, width), BF16),
            dma((2,)),
            dma((groups,)),
            dma((groups,)),
            dma((13,)),
            dma((13,)),
            dma(()),
        ],
        compiler_params=remote_params(2),
        cost_estimate=pl.CostEstimate(flops=0, bytes_accessed=200_000_000, transcendentals=0),
        name="attend_ahead",
    )(lengths, hidden_all, w_qkv, slots, flags, cotangent)


CHUNK = 32


def each_chunk(rows, body, chunk=CHUNK):
    def step(i, carry):
        body(pl.ds(pl.multiple_of(i * chunk, chunk), chunk))
        return carry

    lax.fori_loop(0, rows // chunk, step, 0)


class Reduce:
    COUNT = 10

    def __init__(self, left, right, across, part, from_side, from_corner, from_near, send, recv):
        self.left, self.right, self.across, self.part = left, right, across, part
        self.from_side, self.from_corner, self.from_near = from_side, from_corner, from_near
        self.send, self.recv = send, recv
        self.rows = part.shape[1]

    def product(self, owner, slot):
        rows, width = self.rows, self.part.shape[2]
        picked = pl.ds(pl.multiple_of(owner * rows, rows), rows)

        def tile(t, carry):
            columns = pl.ds(pl.multiple_of(t * 256, 256), 256)
            if self.across:
                value = lax.dot_general(
                    self.left[picked, :], self.right[columns, :], NT, preferred_element_type=F32
                )
            else:
                value = jnp.dot(
                    self.left[picked, :], self.right[:, columns], preferred_element_type=F32
                )
            self.part[slot, :, columns] = value.astype(BF16)
            return carry

        lax.fori_loop(0, width // 256, tile, 0)

    def prepare(self):
        _, side, over_x, over_y, corner = plane()
        part, near = self.part, self.from_near
        half = self.rows // 2
        low, high = pl.ds(0, half), pl.ds(half, half)

        def hop(number, source, target, index):
            return to_dp(source, target, self.send.at[number], self.recv.at[number], index)

        self.shares = [hop(i, part.at[4 + i], self.from_side.at[i], side) for i in range(4)]
        self.corners = [
            hop(4, part.at[0, low], self.from_corner.at[0], over_x),
            hop(5, part.at[0, high], self.from_corner.at[1], over_y),
        ]
        self.nears = [
            hop(6, part.at[1, low], near.at[0, low], over_x),
            hop(7, part.at[1, high], near.at[0, high], over_x),
            hop(8, part.at[2, high], near.at[1, high], over_y),
            hop(9, part.at[2, low], near.at[1, low], over_y),
        ]

    def add_side(self, slot):
        self.shares[slot].wait_recv()

        def body(span):
            self.part[slot, span, :] = (
                self.part[slot, span, :].astype(F32) + self.from_side[slot, span, :].astype(F32)
            ).astype(BF16)

        each_chunk(self.rows, body)

    def add_corner(self, slot, offset, which):
        self.corners[which].wait_recv()

        def body(span):
            target = pl.ds(pl.multiple_of(offset + span.start, CHUNK), CHUNK)
            self.part[slot, target, :] = (
                self.part[slot, target, :].astype(F32)
                + self.from_corner[which, span, :].astype(F32)
            ).astype(BF16)

        each_chunk(self.rows // 2, body)

    def begin(self):
        self.prepare()
        me, _, over_x, over_y, corner = plane()
        owners = (corner, over_x, over_y, me)
        turn = 1 - 2 * lax.rem(me, 2)
        self.product(corner + turn, 4)
        self.shares[0].start()
        self.product(corner, 0)
        self.product(over_x + turn, 5)
        self.shares[1].start()
        self.add_side(0)
        self.corners[0].start()
        self.corners[1].start()
        self.product(over_x, 1)
        self.product(over_y + turn, 6)
        self.shares[2].start()
        self.add_side(1)
        self.nears[0].start()
        self.product(over_y, 2)
        self.product(me + turn, 7)
        self.shares[3].start()
        self.add_side(2)
        self.nears[2].start()
        self.product(me, 3)

    def middle(self):
        self.add_corner(2, 0, 0)
        self.nears[3].start()
        self.add_corner(1, self.rows // 2, 1)
        self.nears[1].start()

    def end(self):
        self.shares[3].wait_recv()
        for copy in self.nears:
            copy.wait_recv()

    def run(self):
        self.begin()
        self.middle()
        self.end()

    def rows_of(self, span):
        return (
            self.part[3, span, :].astype(F32)
            + self.from_side[3, span, :].astype(F32)
            + self.from_near[0, span, :].astype(F32)
            + self.from_near[1, span, :].astype(F32)
        )

    def finish(self):
        for copy in self.shares + self.corners + self.nears:
            copy.wait_send()


def reduce_scratch(rows, width):
    dma = pltpu.SemaphoreType.DMA
    return [
        pltpu.VMEM((8, rows, width), BF16),
        pltpu.VMEM((4, rows, width), BF16),
        pltpu.VMEM((2, rows // 2, width), BF16),
        pltpu.VMEM((2, rows, width), BF16),
        dma((10,)),
        dma((10,)),
    ]


def gather_scratch(rows, width):
    dma = pltpu.SemaphoreType.DMA
    return [pltpu.VMEM((rows, width), BF16), dma((13,)), dma((13,)), dma(())]


def mean_rows(values):
    return jnp.mean(values, axis=-1, keepdims=True)


class Heads:
    def __init__(self, source, arrive, send, recv, views):
        me, z = lax.axis_index("dp"), lax.axis_index("mp")
        self.me, self.z = me, z
        self.core = lax.rem(me, 2)
        self.source, self.arrive, self.send, self.recv, self.views = source, arrive, send, recv, views
        self.owner = lax.div(z, 2)

    def copy(self, slot, half, number):
        target_z = 2 * self.core + slot
        index = (slot * 2 + half) * self.views + number
        return to_at(
            self.view(slot, half, number),
            self.arrive.at[self.z, number],
            self.send.at[index],
            self.recv.at[self.z * self.views + number],
            self.me - self.core + half,
            target_z,
        )

    def view(self, slot, half, number):
        rows = pl.ds(pl.multiple_of((2 * number + slot) * LANES, LANES), HEAD_DIM)
        columns = self.source.shape[1] // 2
        return self.source.at[rows, pl.ds(pl.multiple_of(half * columns, LANES), columns)]

    def each(self, action):
        for slot in range(2):
            for half in range(2):
                mine = (2 * self.core + slot == self.z) & (self.core == half)

                @pl.when(jnp.logical_not(mine))
                def _():
                    for number in range(self.views):
                        action(self.copy(slot, half, number))

    def start(self):
        self.each(lambda copy: copy.start())

    def finish_send(self):
        self.each(lambda copy: copy.wait_send())

    def total(self, out):
        me, z = self.me, self.z
        for number in range(self.views):
            for other in range(4):
                waiting = to_at(
                    self.view(0, 0, number),
                    self.arrive.at[other, number],
                    self.send.at[0],
                    self.recv.at[other * self.views + number],
                    me,
                    other,
                )

                @pl.when((z != other) | (self.core != self.owner))
                def _():
                    waiting.wait_recv()

                @pl.when((z == other) & (self.core == self.owner))
                def _():
                    self.arrive[other, number] = self.view(lax.rem(z, 2), self.core, number)[...]

            count = self.arrive.shape[2]

            def body(span):
                found = self.arrive[0, number, span, :].astype(F32)
                for other in range(1, 4):
                    found = found + self.arrive[other, number, span, :].astype(F32)
                out[number, span, :] = found.astype(BF16)

            each_chunk(count, body, 16)


def to_at(source, target, send_sem, recv_sem, dp, mp):
    return pltpu.make_async_remote_copy(
        src_ref=source,
        dst_ref=target,
        send_sem=send_sem,
        recv_sem=recv_sem,
        device_id={"dp": dp, "mp": mp},
        device_id_type=MESH,
    )


def backward_kernel(
    lengths, kept, mixed_grad, slots, flags, activated, w_down, middle, proj_sum,
    out, result, proj_part,
    totals, query_part, key_value, ending, leaving, arriving, send, recv,
    part, from_side, from_corner, from_near, send_r, recv_r, arrive, send_h, recv_h,
    *, scale, groups, rows,
):
    z = lax.axis_index("mp")
    members = lax.axis_size("mp")
    greet_all(pltpu.get_barrier_semaphore())
    heads = Heads(proj_sum, arrive, send_h, recv_h, 1)
    heads.start()
    reduce = Reduce(activated, w_down, False, part, from_side, from_corner, from_near, send_r, recv_r)
    reduce.begin()

    def halo(k, other):
        return to_mp(leaving.at[k], arriving.at[k], send.at[k], recv.at[k], other)

    def attend(k, carry):
        hot = one_hot(slots, k, rows)
        given = mixed_grad[:, pl.ds(k, 1)].reshape(rows, 256)
        grad_ordered = jnp.dot(hot, given, preferred_element_type=F32).astype(BF16)
        totals[...] = jnp.zeros_like(totals)
        for block in range(rows // 128):
            allowed = block_mask(lengths, flags, k, block, z, rows)
            for head in range(2):
                query = kept[k, pl.ds(64 + block * 128, 128), pl.ds(head * 128, 128)]
                keys = kept[k, pl.ds(block * 128, 192), pl.ds(256 + head * 128, 128)]
                values = kept[k, pl.ds(block * 128, 192), pl.ds(512 + head * 128, 128)]
                grad = grad_ordered[block * 128 : block * 128 + 128, head * 128 : head * 128 + 128]
                scores = lax.dot_general(query, keys, NT, preferred_element_type=F32) * scale
                scores = jnp.where(allowed, scores, -MASKED)
                weights = jnp.exp(scores - jnp.max(scores, axis=-1, keepdims=True))
                again = weights / jnp.sum(weights, axis=-1, keepdims=True)
                chance_grad = lax.dot_general(grad, values, NT, preferred_element_type=F32)
                row_dot = jnp.sum(again * chance_grad, axis=-1, keepdims=True)
                score_grad = (again * (chance_grad - row_dot)).astype(BF16)
                query_part[k, pl.ds(block * 128, 128), pl.ds(head * 128, 128)] = (
                    jnp.dot(score_grad, keys, preferred_element_type=F32) * scale
                ).astype(BF16)
                totals[pl.ds(block * 128, 192), pl.ds(head * 128, 128)] += (
                    lax.dot_general(score_grad, query, TN, preferred_element_type=F32) * scale
                )
                totals[pl.ds(block * 128, 192), pl.ds(256 + head * 128, 128)] += lax.dot_general(
                    again.astype(BF16), grad, TN, preferred_element_type=F32
                )
        key_value[k] = totals[pl.ds(64, rows), :].astype(BF16)
        ending[k] = totals[pl.ds(rows, 64), :]

        @pl.when(z > 0)
        def _():
            leaving[k] = totals[pl.ds(0, 64), :].astype(BF16)
            halo(k, z - 1).start()

        return carry

    lax.fori_loop(0, groups - 5, attend, 0)
    reduce.middle()
    lax.fori_loop(groups - 5, groups, attend, 0)

    def restore(k, carry):
        @pl.when(z < members - 1)
        def _():
            halo(k, z).wait_recv()
            key_value[k, pl.ds(rows - 64, 64), :] = (
                ending[k] + arriving[k].astype(F32)
            ).astype(BF16)

        hot = one_hot(slots, k, rows)
        ordered = jnp.concatenate([query_part[k], key_value[k]], axis=1)
        back = lax.dot_general(hot, ordered, TN, preferred_element_type=F32).astype(BF16)
        out[:, pl.ds(k, 1)] = back.reshape(groups, 1, rows // groups, 768)
        return carry

    lax.fori_loop(0, groups, restore, 0)
    reduce.end()

    def body(span):
        result[span, :] = (middle[span, :] + reduce.rows_of(span)).astype(BF16)

    each_chunk(rows, body)
    heads.total(proj_part)
    heads.finish_send()
    reduce.finish()

    @pl.when(z > 0)
    def _():
        def done(k, carry):
            halo(k, z - 1).wait_send()
            return carry

        lax.fori_loop(0, groups, done, 0)


def attend_back(
    lengths, kept, mixed_grad, slots, flags, activated, w_down, middle, proj_sum, scale
):
    groups = kept.shape[0]
    rows, width = middle.shape
    dma = pltpu.SemaphoreType.DMA
    return pl.pallas_call(
        functools.partial(backward_kernel, scale=scale, groups=groups, rows=rows),
        out_shape=(
            jax.ShapeDtypeStruct((groups, groups, rows // groups, 768), BF16),
            jax.ShapeDtypeStruct((rows, width), BF16),
            jax.ShapeDtypeStruct((1, HEAD_DIM, width // 2), BF16),
        ),
        in_specs=[in_scalar()] + [on_chip()] * 8,
        out_specs=(on_chip(), on_chip(), on_chip()),
        scratch_shapes=[
            pltpu.VMEM((rows + 64, 512), F32),
            pltpu.VMEM((groups, rows, 256), BF16),
            pltpu.VMEM((groups, rows, 512), BF16),
            pltpu.VMEM((groups, 64, 512), F32),
            pltpu.VMEM((groups, 64, 512), BF16),
            pltpu.VMEM((groups, 64, 512), BF16),
            dma((groups,)),
            dma((groups,)),
        ]
        + reduce_scratch(rows, width)
        + [pltpu.VMEM((4, 1, HEAD_DIM, width // 2), BF16), dma((4,)), dma((4,))],
        compiler_params=remote_params(3, 62 * 1024 * 1024),
        cost_estimate=pl.CostEstimate(flops=0, bytes_accessed=200_000_000, transcendentals=0),
        name="attend_back",
    )(lengths, kept, mixed_grad, slots, flags, activated, w_down, middle, proj_sum)


def middle_kernel(
    mixed, w_out, tokens, gain, middle, hidden,
    part, from_side, from_corner, from_near, send, recv,
):
    pl.semaphore_wait(greet_plane(), 3)
    reduce = Reduce(mixed, w_out, False, part, from_side, from_corner, from_near, send, recv)
    reduce.run()

    def body(span):
        values = tokens[span, :].astype(F32) + reduce.rows_of(span)
        middle[span, :] = values
        inverse = lax.rsqrt(mean_rows(values * values) + EPSILON)
        hidden[span, :] = (values * inverse * gain[...]).astype(BF16)

    each_chunk(hidden.shape[0], body)
    reduce.finish()


def project_middle(mixed, w_out, tokens, gain):
    rows, width = tokens.shape
    return pl.pallas_call(
        middle_kernel,
        out_shape=(
            jax.ShapeDtypeStruct((rows, width), F32),
            jax.ShapeDtypeStruct((rows, width), BF16),
        ),
        in_specs=[on_chip()] * 4,
        out_specs=(on_chip(), on_chip()),
        scratch_shapes=reduce_scratch(rows, width),
        compiler_params=remote_params(4),
        cost_estimate=pl.CostEstimate(flops=0, bytes_accessed=150_000_000, transcendentals=0),
        name="project_middle",
    )(mixed, w_out, tokens, gain)


def norm_back_rows(gradient, values, gain, sums, span):
    inverse = lax.rsqrt(mean_rows(values * values) + EPSILON)
    normed = values * inverse
    product = gradient * normed
    folded = product[0:8]
    for step in range(1, CHUNK // 8):
        folded = folded + product[step * 8 : step * 8 + 8]
    sums[...] += folded
    scaled = gradient * gain
    return inverse * (scaled - normed * mean_rows(scaled * normed))


def feed_kernel(
    hidden_own, cotangent_all, middle, cotangent, gain, w_both, w_down,
    middle_grad, branch_all, sums, activated, both_sum, down_sum,
    hidden_all, both_grad, part, from_side, from_corner, from_near, send_r, recv_r,
    send_a, recv_a, send_b, recv_b, cot_half, cot_tile, stage_both, stage_down, load_sem, local,
):
    groups, rows, width = hidden_all.shape
    members = w_both.shape[0]
    half_rows = rows // 2
    me, side, over_x, over_y, _ = plane()
    own = pltpu.make_async_copy(hidden_own, hidden_all.at[me], local.at[0])
    own.start()
    start_middle = pltpu.make_async_copy(middle, middle_grad, local.at[1])
    start_middle.start()

    def place_of(step):
        block = step // 4
        near = ((block + 1) // 2) % 2
        far = block // 3
        mixed_order = near * (1 - block // 2)
        second = mixed_order * (step % 2) + (1 - mixed_order) * ((step // 2) % 2)
        half = mixed_order * ((step % 2 + (step // 2) % 2) % 2) + (1 - mixed_order) * (step % 2)
        other = (1 - near) * second + (block // 2) * near
        in_x = near * (1 - second) + far
        in_y = near * second + far
        owner = me + in_x * (over_x - me) + in_y * (over_y - me) + other * (side - me)
        slot = 4 * other + 3 * (1 - near) * (1 - far) + near * (1 + second)
        return owner, half, slot

    def load_cotangent(step):
        owner, half, _ = place_of(step)
        span = pl.ds(pl.multiple_of(half * half_rows, half_rows), half_rows)
        return pltpu.make_async_copy(
            cotangent_all.at[owner, span], cot_half.at[step % 2], load_sem.at[step % 2]
        )

    load_cotangent(0).start()
    pl.semaphore_wait(greet_plane(), 3)
    own.wait()
    gather = Gather(None, hidden_all, send_a, recv_a)
    gather.start()
    reduce = Reduce(None, None, False, part, from_side, from_corner, from_near, send_r, recv_r)
    reduce.prepare()

    def before(step, *numbers):
        return (step, lambda: gather.arrive(*numbers))

    def nears():
        reduce.add_side(1)
        reduce.nears[0].start()
        reduce.add_side(2)
        reduce.nears[2].start()

    early = [
        before(2, 4),
        before(4, 0),
        before(5, 1),
        before(6, 2),
        before(7, 3),
        before(8, 6, 9),
        before(10, 8, 10),
        before(12, 5, 7),
        (13, nears),
        before(14, 11, 12),
    ]
    late = [(3, 3), (9, 1), (11, 2), (15, 0)]

    def unit(step, carry):
        for number, action in early:
            pl.when(step == number)(action)

        @pl.when(step < 15)
        def _():
            load_cotangent(step + 1).start()

        load_cotangent(step).wait()
        owner, half, slot = place_of(step)
        span = pl.ds(pl.multiple_of(half * half_rows, half_rows), half_rows)
        mine = hidden_all[owner, span, :]
        grads = cot_half[step % 2]
        for z in range(members):
            raw = jnp.dot(mine, w_both[z], preferred_element_type=F32)
            units = pl.ds(z * 128, 128)
            if z % 2 == 0:
                pair = lax.dot_general(
                    grads, w_down[pl.ds(z * 128, 256), :], NT, preferred_element_type=F32
                )
            active_grad = pair[:, 128 * (z % 2) : 128 * (z % 2) + 128]
            gate, upward = raw[:, :128], raw[:, 128:]
            sigmoid = jax.nn.sigmoid(gate)
            activated[owner, span, units] = (gate * sigmoid * upward).astype(BF16)
            both_grad[owner, span, pl.ds(z * 256, 128)] = (
                active_grad * upward * sigmoid * (1.0 + gate * (1.0 - sigmoid))
            ).astype(BF16)
            both_grad[owner, span, pl.ds(z * 256 + 128, 128)] = (
                active_grad * gate * sigmoid
            ).astype(BF16)

        def tile(t, inner):
            columns = pl.ds(pl.multiple_of(t * 256, 256), 256)
            value = sum(
                lax.dot_general(
                    both_grad[owner, span, pl.ds(z * 256, 256)],
                    w_both[z, columns, :],
                    NT,
                    preferred_element_type=F32,
                )
                for z in range(members)
            )
            part[slot, span, columns] = value.astype(BF16)
            return inner

        lax.fori_loop(0, width // 256, tile, 0)
        for number, share in late:
            pl.when(step == number)(reduce.shares[share].start)
        return carry

    lax.fori_loop(0, 16, unit, 0)

    def load_tile(t):
        columns = pl.ds(pl.multiple_of(t * 256, 256), 256)
        return pltpu.make_async_copy(
            cotangent_all.at[:, :, columns], cot_tile.at[t % 2], load_sem.at[2 + t % 2]
        )

    def store_both(t):
        columns = pl.ds(pl.multiple_of(t * 256, 256), 256)
        return pltpu.make_async_copy(
            stage_both.at[t % 2], both_sum.at[:, columns], load_sem.at[4 + t % 2]
        )

    def store_down(t):
        columns = pl.ds(pl.multiple_of(t * 256, 256), 256)
        return pltpu.make_async_copy(
            stage_down.at[t % 2], down_sum.at[:, columns], load_sem.at[6 + t % 2]
        )

    tiles = width // 256
    count = groups * rows

    def weight_tile(t, carry):
        columns = pl.ds(pl.multiple_of(t * 256, 256), 256)

        @pl.when(t < tiles - 1)
        def _():
            load_tile(t + 1).start()

        load_tile(t).wait()

        @pl.when(t >= 2)
        def _():
            store_both(t - 2).wait()
            store_down(t - 2).wait()

        value = lax.dot_general(
            hidden_all[:, :, columns].reshape(count, 256),
            both_grad[...].reshape(count, members * 256),
            TN,
            preferred_element_type=F32,
        )
        for z in range(members):
            stage_both[t % 2, z] = value[:, z * 256 : z * 256 + 256].astype(BF16)
        stage_down[t % 2] = lax.dot_general(
            activated[...].reshape(count, members * 128),
            cot_tile[t % 2].reshape(count, 256),
            TN,
            preferred_element_type=F32,
        ).astype(BF16)
        store_both(t).start()
        store_down(t).start()
        return carry

    load_tile(0).start()
    reduce.add_side(0)
    reduce.corners[0].start()
    reduce.corners[1].start()
    lax.fori_loop(0, 4, weight_tile, 0)
    reduce.middle()
    lax.fori_loop(4, tiles, weight_tile, 0)
    reduce.end()
    start_middle.wait()
    sums[...] = jnp.zeros_like(sums)
    for copy in reduce.corners:
        copy.wait_send()

    def body(span):
        change = norm_back_rows(reduce.rows_of(span), middle_grad[span, :], gain[...], sums, span)
        total = cotangent[span, :].astype(F32) + change
        middle_grad[span, :] = total
        part[0, span, :] = total.astype(BF16)

    each_chunk(rows, body)
    branch = Gather(part.at[0], branch_all, send_b, recv_b, local.at[2])
    branch.start()
    branch.pass_on()
    branch.finish()
    for copy in reduce.shares + reduce.nears:
        copy.wait_send()
    gather.sent()
    for t in (tiles - 2, tiles - 1):
        store_both(t).wait()
        store_down(t).wait()


def feed(hidden_own, cotangent_all, middle, cotangent, gain, w_both, w_down):
    groups, rows, width = cotangent_all.shape
    members = w_both.shape[0]
    dma = pltpu.SemaphoreType.DMA
    units = members * 128
    return pl.pallas_call(
        feed_kernel,
        out_shape=(
            jax.ShapeDtypeStruct((rows, width), F32),
            jax.ShapeDtypeStruct((groups, rows, width), BF16),
            jax.ShapeDtypeStruct((8, width), F32),
            jax.ShapeDtypeStruct((groups, rows, units), BF16),
            jax.ShapeDtypeStruct((members, width, 256), BF16),
            jax.ShapeDtypeStruct((units, width), BF16),
        ),
        in_specs=[anywhere()] * 3 + [on_chip()] * 4,
        out_specs=(on_chip(), anywhere(), on_chip(), on_chip(), anywhere(), anywhere()),
        scratch_shapes=[
            pltpu.VMEM((groups, rows, width), BF16),
            pltpu.VMEM((groups, rows, 2 * units), BF16),
        ]
        + reduce_scratch(rows, width)
        + [
            dma((13,)),
            dma((13,)),
            dma((13,)),
            dma((13,)),
            pltpu.VMEM((2, rows // 2, width), BF16),
            pltpu.VMEM((2, groups, rows, 256), BF16),
            pltpu.VMEM((2, members, 256, 256), BF16),
            pltpu.VMEM((2, units, 256), BF16),
            dma((8,)),
            dma((3,)),
        ],
        compiler_params=remote_params(5, 62 * 1024 * 1024),
        cost_estimate=pl.CostEstimate(flops=0, bytes_accessed=400_000_000, transcendentals=0),
        name="feed",
    )(hidden_own, cotangent_all, middle, cotangent, gain, w_both, w_down)


def input_kernel(
    qkv_grad, w_qkv, hidden_all, tokens, middle_grad, gain, sums_two, proj_part, result, heads_part, gains,
    part, from_side, from_corner, from_near, send, recv, sums,
    arrive, send_h, recv_h, own, plane_sums, column_sums, send_s, recv_s,
    qkv_sum, hidden_tile, tile_sem,
):
    me, z = lax.axis_index("dp"), lax.axis_index("mp")
    count = qkv_grad.shape[0]
    tiles = tokens.shape[1] // 256

    def load(t):
        columns = pl.ds(pl.multiple_of(t * 256, 256), 256)
        return pltpu.make_async_copy(
            hidden_all.at[:, :, columns], hidden_tile.at[t % 2], tile_sem.at[t % 2]
        )

    load(0).start()

    def weight_tile(t, carry):
        columns = pl.ds(pl.multiple_of(t * 256, 256), 256)

        @pl.when(t < tiles - 1)
        def _():
            load(t + 1).start()

        load(t).wait()
        qkv_sum[:, columns] = lax.dot_general(
            qkv_grad[...], hidden_tile[t % 2].reshape(count, 256), TN, preferred_element_type=F32
        ).astype(BF16)
        return carry

    lax.fori_loop(0, tiles, weight_tile, 0)
    greet_all(pltpu.get_barrier_semaphore())
    heads = Heads(qkv_sum, arrive, send_h, recv_h, 3)
    heads.start()
    heads_part[3] = proj_part[0]
    reduce = Reduce(qkv_grad, w_qkv, False, part, from_side, from_corner, from_near, send, recv)
    reduce.run()
    sums[...] = jnp.zeros_like(sums)

    def body(span):
        values = tokens[span, :].astype(F32)
        change = norm_back_rows(reduce.rows_of(span), values, gain[...], sums, span)
        result[span, :] = (middle_grad[span, :] + change).astype(BF16)

    each_chunk(result.shape[0], body)
    own[...] = jnp.concatenate(
        [
            jnp.sum(sums[...], axis=0, keepdims=True),
            jnp.sum(sums_two[...], axis=0, keepdims=True),
        ],
        axis=0,
    )
    swaps = swap_all(own, plane_sums, send_s, recv_s)
    for copy in swaps:
        copy.start()
    plane_sums[me] = own[...]
    for copy in swaps:
        copy.wait()
    found = plane_sums[0]
    for other in range(1, 8):
        found = found + plane_sums[other]
    column_sums[z] = found
    passes = [
        to_mp(
            column_sums.at[z],
            column_sums.at[z],
            send_s.at[6 + step],
            recv_s.at[6 + step],
            lax.rem(z + step, 4),
        )
        for step in range(1, 4)
    ]
    for copy in passes:
        copy.start()
    for copy in passes:
        copy.wait()
    gains[...] = (column_sums[0] + column_sums[1]) + (column_sums[2] + column_sums[3])
    heads.total(heads_part)
    heads.finish_send()
    reduce.finish()


def project_input(qkv_grad, w_qkv, hidden_all, tokens, middle_grad, gain, sums_two, proj_part):
    rows, width = tokens.shape
    groups = hidden_all.shape[0]
    dma = pltpu.SemaphoreType.DMA
    return pl.pallas_call(
        input_kernel,
        out_shape=(
            jax.ShapeDtypeStruct((rows, width), BF16),
            jax.ShapeDtypeStruct((4, HEAD_DIM, width // 2), BF16),
            jax.ShapeDtypeStruct((2, width), F32),
        ),
        in_specs=[on_chip()] * 2 + [anywhere()] + [on_chip()] * 5,
        out_specs=(on_chip(),) * 3,
        scratch_shapes=reduce_scratch(rows, width)
        + [
            pltpu.VMEM((8, width), F32),
            pltpu.VMEM((4, 3, HEAD_DIM, width // 2), BF16),
            dma((12,)),
            dma((12,)),
            pltpu.VMEM((2, width), F32),
            pltpu.VMEM((8, 2, width), F32),
            pltpu.VMEM((4, 2, width), F32),
            dma((10,)),
            dma((10,)),
            pltpu.VMEM((6 * LANES, width), BF16),
            pltpu.VMEM((2, groups, rows, 256), BF16),
            dma((2,)),
        ],
        compiler_params=remote_params(6),
        cost_estimate=pl.CostEstimate(flops=0, bytes_accessed=250_000_000, transcendentals=0),
        name="project_input",
    )(qkv_grad, w_qkv, hidden_all, tokens, middle_grad, gain, sums_two, proj_part)


def units_gather_kernel(both, both_all, send, recv, local):
    pl.semaphore_wait(greet_plane(), 3)
    gather = Gather(both, both_all, send, recv, local)
    gather.start()
    gather.pass_on()
    gather.finish()


def gather_units(part, number):
    groups = lax.axis_size("dp")
    dma = pltpu.SemaphoreType.DMA
    return pl.pallas_call(
        units_gather_kernel,
        out_shape=jax.ShapeDtypeStruct((groups,) + part.shape, BF16),
        in_specs=[on_chip()],
        out_specs=anywhere(),
        scratch_shapes=[dma((13,)), dma((13,)), dma(())],
        compiler_params=remote_params(number),
        cost_estimate=pl.CostEstimate(flops=0, bytes_accessed=100_000_000, transcendentals=0),
        name="gather_units",
    )(part)


def units_kernel(both, gate, upward):
    for d in range(both.shape[0]):
        gate[:, d * 128 : d * 128 + 128] = both[d, :, :128].astype(F32)
        upward[:, d * 128 : d * 128 + 128] = both[d, :, 128:].astype(F32)


def assemble_units(both):
    groups, width, wide = both.shape
    tile = 256
    shape = jax.ShapeDtypeStruct((width, groups * wide // 2), F32)
    spec = pl.BlockSpec((tile, groups * wide // 2), lambda i: (i, 0))
    return pl.pallas_call(
        units_kernel,
        grid=(width // tile,),
        out_shape=(shape, shape),
        in_specs=[pl.BlockSpec((groups, tile, wide), lambda i: (0, i, 0))],
        out_specs=(spec, spec),
        cost_estimate=pl.CostEstimate(flops=0, bytes_accessed=22_000_000, transcendentals=0),
        name="assemble_units",
    )(both)


def heads_kernel(whole, *outs):
    columns = whole.shape[4]
    for kind, out in enumerate(outs):
        for half in range(whole.shape[1]):
            out[:, half * columns : half * columns + columns] = whole[0, half, kind].astype(F32)


def assemble_heads(whole):
    chips, halves, kinds, rows, columns = whole.shape
    shape = jax.ShapeDtypeStruct((chips * rows, halves * columns), F32)
    spec = pl.BlockSpec((rows, halves * columns), lambda c: (c, 0))
    return pl.pallas_call(
        heads_kernel,
        grid=(chips,),
        out_shape=(shape,) * kinds,
        in_specs=[pl.BlockSpec((1, halves, kinds, rows, columns), lambda c: (c, 0, 0, 0, 0))],
        out_specs=(spec,) * kinds,
        cost_estimate=pl.CostEstimate(flops=0, bytes_accessed=20_000_000, transcendentals=0),
        name="assemble_heads",
    )(whole)


def swapped(
    tokens, cotangent, route, lengths, key_mask, norm1_gain, norm2_gain,
    w_query, w_key, w_value, w_out, w_gate, w_up, w_down,
):
    groups = lax.axis_size("dp")
    members = lax.axis_size("mp")
    me = lax.axis_index("dp")
    z = lax.axis_index("mp")
    rows, width = tokens.shape
    bucket = rows // groups
    units = w_down.shape[0] // groups

    target = route // TOK_DEV
    earlier = jnp.arange(rows, dtype=jnp.int32)
    same = (target[:, None] == target[None, :]) & (earlier[None, :] < earlier[:, None])
    send_at = target * bucket + jnp.sum(same.astype(jnp.int32), axis=1)
    sorting = send_at[None, :] == earlier[:, None]
    slots_own = jnp.sum(jnp.where(sorting, (route % rows)[None, :], 0), axis=1)
    sort_hot = sorting.astype(BF16)
    tokens_b = jnp.dot(sort_hot, tokens, preferred_element_type=F32).astype(BF16)
    cotangent_b = jnp.dot(sort_hot, cotangent, preferred_element_type=F32).astype(BF16)

    mask_window = lax.dynamic_slice_in_dim(
        jnp.concatenate([jnp.zeros((WINDOW,), jnp.int32), key_mask]), z * rows, rows + WINDOW
    )
    notes = jnp.concatenate([slots_own, mask_window, lengths[0]])
    notes = jnp.pad(notes, (0, 8 * LANES - notes.shape[0])).reshape(8, LANES)

    normed, _ = norm_rows(tokens_b.astype(F32))
    hidden_own = (normed * norm1_gain).astype(BF16)
    hidden_one, w_qkv, w_proj, notes_all = gather_first(
        hidden_own, w_query.T, w_key.T, w_value.T, w_out, notes
    )
    notes_all = notes_all.reshape(groups, 8 * LANES)
    slots = (
        notes_all[:, :rows].reshape(groups, groups, bucket).transpose(1, 0, 2).reshape(groups, rows)
    )
    flags = notes_all[:, rows : 2 * rows + WINDOW]
    lengths_all = notes_all[:, 2 * rows + WINDOW : 2 * rows + WINDOW + 3]

    w_gate, w_up, w_down, hidden_one = lax.optimization_barrier((w_gate, w_up, w_down, hidden_one))

    def unit_columns(weight):
        return lax.dynamic_slice_in_dim(weight, me * units, units, 1)

    both_own = jnp.concatenate([unit_columns(w_gate), unit_columns(w_up)], axis=1)
    down_own = lax.dynamic_slice_in_dim(w_down, me * units, units, 0)
    w_both = lax.all_gather(both_own, "mp")
    down_all = lax.all_gather(down_own, "mp", axis=0, tiled=True)

    count = groups * rows
    scale = HEAD_DIM ** (-0.5)
    mixed, kept, cotangent_all = attend_ahead(
        lengths_all, hidden_one, w_qkv, slots, flags, cotangent_b, scale
    )
    mixed = mixed.reshape(count, 2 * LANES)
    middle, hidden_two = project_middle(mixed, w_proj, tokens_b, norm2_gain[None])
    middle_grad, branch_all, sums_two, activated, both_sum, down_sum = feed(
        hidden_two, cotangent_all, middle, cotangent_b, norm2_gain[None], w_both, down_all
    )
    down_part = lax.psum_scatter(down_sum, "mp", scatter_dimension=0, tiled=True)
    both_part = lax.psum_scatter(both_sum, "mp", scatter_dimension=0)

    branch_rows = branch_all.reshape(count, width)
    mixed_grad = jnp.einsum(
        "td,cd->tc", branch_rows, w_proj, preferred_element_type=F32
    ).astype(BF16)
    proj_sum = jnp.einsum("tc,td->cd", mixed, branch_rows, preferred_element_type=F32).astype(BF16)
    qkv_grad, output_rows, proj_part = attend_back(
        lengths_all,
        kept,
        mixed_grad.reshape(groups, groups, bucket, 2 * LANES),
        slots,
        flags,
        activated.reshape(count, units * members),
        down_all,
        middle,
        proj_sum,
        scale,
    )
    qkv_grad = qkv_grad.reshape(count, 6 * LANES)
    input_rows, heads_part, gain_sums = project_input(
        qkv_grad, w_qkv, hidden_one, tokens_b, middle_grad, norm1_gain[None], sums_two, proj_part
    )
    down_part, both_part, heads_part = lax.optimization_barrier((down_part, both_part, heads_part))
    heads_whole = lax.all_gather(heads_part.reshape(4 * HEAD_DIM, width // 2), "dp")
    both_whole = gather_units(both_part, 7)
    down_whole = gather_units(down_part, 8)
    gate_grad, up_grad = assemble_units(both_whole)
    down_grad = down_whole.astype(F32).reshape(groups * units, width)
    query_grad, key_grad, value_grad, proj_grad = assemble_heads(
        heads_whole.reshape(groups // 2, 2, 4, HEAD_DIM, width // 2)
    )

    unsort = (((0,), (0,)), ((), ()))
    return (
        lax.dot_general(sort_hot, output_rows, unsort, preferred_element_type=F32).astype(BF16),
        lax.dot_general(sort_hot, input_rows, unsort, preferred_element_type=F32).astype(BF16),
        gain_sums[0],
        gain_sums[1],
        query_grad.T,
        key_grad.T,
        value_grad.T,
        proj_grad,
        gate_grad,
        up_grad,
        down_grad,
    )


def solution(mesh):
    in_specs = (
        P(("dp", "mp"), None),
        P(("dp", "mp"), None),
        P(("dp", "mp")),
        P("dp", None),
        P("dp"),
        P(),
        P(),
        P(None, "mp"),
        P(None, "mp"),
        P(None, "mp"),
        P("mp", None),
        P(None, "mp"),
        P(None, "mp"),
        P("mp", None),
    )
    out_specs = (
        P(("dp", "mp"), None),
        P(("dp", "mp"), None),
        P(),
        P(),
        P(None, "mp"),
        P(None, "mp"),
        P(None, "mp"),
        P("mp", None),
        P(None, "mp"),
        P(None, "mp"),
        P("mp", None),
    )
    body = swapped if (mesh.shape["dp"], mesh.shape["mp"]) == (8, 4) else local
    return jax.shard_map(body, mesh=mesh, in_specs=in_specs, out_specs=out_specs, check_vma=False)
```

```python
import functools

import jax
import jax.numpy as jnp
from jax import lax
from jax.experimental import pallas as pl
from jax.experimental.pallas import tpu as pltpu
from jax.sharding import PartitionSpec as P

HEAD_DIM = 112
WINDOW = 64
TOK_DEV = 1536


EPSILON = 1e-05
MASKED = 1e30


def norm_rows(values):
    inverse = lax.rsqrt(jnp.mean(values * values, axis=-1, keepdims=True) + EPSILON)
    return (values * inverse, inverse)


def norm_back(gradient, normed, inverse, norm_gain):
    scaled = gradient * norm_gain
    result = inverse * (scaled - normed * jnp.mean(scaled * normed, axis=-1, keepdims=True))
    return (result, jnp.sum(gradient * normed, axis=0))


def padded(values, filler):
    front = jnp.full((WINDOW,) + values.shape[1:], filler, values.dtype)
    return jnp.concatenate([front, values], axis=0)


def block_scores(query_block, key_block, query_seg, key_seg, key_flag, first_row, score_scale):
    query_pos = first_row + jnp.arange(query_block.shape[0], dtype=jnp.int32)
    key_pos = first_row - WINDOW + jnp.arange(key_block.shape[0], dtype=jnp.int32)
    distance = query_pos[:, None] - key_pos[None, :]
    allowed = (distance >= 0) & (distance < WINDOW) & (query_seg[:, None] == key_seg[None, :])
    allowed = allowed & ((key_flag[None, :] == 1) | (distance == 0))
    raw_scores = (
        jnp.einsum("qhd,khd->hqk", query_block, key_block, preferred_element_type=jnp.float32)
        * score_scale
    )
    return jnp.where(allowed[None], raw_scores, -MASKED)


def block_inputs(query, key_pad, value_pad, segment, seg_pad, live_pad, first_row, block_rows):
    key_span = block_rows + WINDOW
    return (
        lax.dynamic_slice_in_dim(query, first_row, block_rows, 0),
        lax.dynamic_slice_in_dim(key_pad, first_row, key_span, 0),
        lax.dynamic_slice_in_dim(value_pad, first_row, key_span, 0),
        lax.dynamic_slice_in_dim(segment, first_row, block_rows, 0),
        lax.dynamic_slice_in_dim(seg_pad, first_row, key_span, 0),
        lax.dynamic_slice_in_dim(live_pad, first_row, key_span, 0),
    )


def attend_forward(query, key_all, value_all, segment, key_live):
    token_count, head_count, head_width = query.shape
    block_rows = min(512, token_count)
    score_scale = head_width ** (-0.5)
    key_pad = padded(key_all, 0.0)
    value_pad = padded(value_all, 0.0)
    seg_pad = padded(segment, -1)
    live_pad = padded(key_live, 0)

    def one_block(running, block_index):
        first_row = block_index * block_rows
        query_block, key_block, value_block, query_seg, key_seg, key_flag = block_inputs(
            query, key_pad, value_pad, segment, seg_pad, live_pad, first_row, block_rows
        )
        scores = block_scores(
            query_block, key_block, query_seg, key_seg, key_flag, first_row, score_scale
        )
        row_max = jnp.max(scores, axis=-1, keepdims=True)
        weights = jnp.exp(scores - row_max)
        denominator = jnp.sum(weights, axis=-1, keepdims=True)
        chances = (weights / denominator).astype(jnp.bfloat16)
        mixed = jnp.einsum("hqk,khd->qhd", chances, value_block, preferred_element_type=jnp.float32)
        return (
            running,
            (mixed.astype(jnp.bfloat16), row_max[..., 0] + jnp.log(denominator[..., 0])),
        )

    _, (mixed, logsum) = lax.scan(
        one_block, jnp.zeros((), jnp.int32), jnp.arange(token_count // block_rows, dtype=jnp.int32)
    )
    return (mixed.reshape(token_count, head_count * head_width), logsum)


def attend_backward(query, key_all, value_all, segment, key_live, logsum, mixed_grad):
    token_count, head_count, head_width = query.shape
    block_rows = min(512, token_count)
    key_span = block_rows + WINDOW
    score_scale = head_width ** (-0.5)
    key_pad = padded(key_all, 0.0)
    value_pad = padded(value_all, 0.0)
    seg_pad = padded(segment, -1)
    live_pad = padded(key_live, 0)

    def one_block(running, inputs):
        key_grad, value_grad = running
        block_index, block_logsum = inputs
        first_row = block_index * block_rows
        query_block, key_block, value_block, query_seg, key_seg, key_flag = block_inputs(
            query, key_pad, value_pad, segment, seg_pad, live_pad, first_row, block_rows
        )
        grad_block = lax.dynamic_slice_in_dim(mixed_grad, first_row, block_rows, 0)
        scores = block_scores(
            query_block, key_block, query_seg, key_seg, key_flag, first_row, score_scale
        )
        chances = jnp.exp(scores - block_logsum[..., None])
        chance_grad = jnp.einsum(
            "qhd,khd->hqk", grad_block, value_block, preferred_element_type=jnp.float32
        )
        row_dot = jnp.sum(chances * chance_grad, axis=-1, keepdims=True)
        score_grad = (chances * (chance_grad - row_dot)).astype(jnp.bfloat16)
        query_grad = (
            jnp.einsum("hqk,khd->qhd", score_grad, key_block, preferred_element_type=jnp.float32)
            * score_scale
        )
        key_part = (
            jnp.einsum("hqk,qhd->khd", score_grad, query_block, preferred_element_type=jnp.float32)
            * score_scale
        )
        value_part = jnp.einsum(
            "hqk,qhd->khd",
            chances.astype(jnp.bfloat16),
            grad_block,
            preferred_element_type=jnp.float32,
        )
        key_grad = lax.dynamic_update_slice_in_dim(
            key_grad,
            lax.dynamic_slice_in_dim(key_grad, first_row, key_span, 0) + key_part,
            first_row,
            0,
        )
        value_grad = lax.dynamic_update_slice_in_dim(
            value_grad,
            lax.dynamic_slice_in_dim(value_grad, first_row, key_span, 0) + value_part,
            first_row,
            0,
        )
        return ((key_grad, value_grad), query_grad)

    empty_grad = jnp.zeros((token_count + WINDOW, head_count, head_width), jnp.float32)
    (key_grad, value_grad), query_grad = lax.scan(
        one_block,
        (empty_grad, empty_grad),
        (jnp.arange(token_count // block_rows, dtype=jnp.int32), logsum),
    )
    flat_width = head_count * head_width
    return (
        query_grad.reshape(token_count, flat_width).astype(jnp.bfloat16),
        key_grad[WINDOW:].reshape(token_count, flat_width).astype(jnp.bfloat16),
        value_grad[WINDOW:].reshape(token_count, flat_width).astype(jnp.bfloat16),
    )


def local(
    tokens,
    cotangent,
    route,
    lengths,
    key_mask,
    norm1_gain,
    norm2_gain,
    w_query,
    w_key,
    w_value,
    w_out,
    w_gate,
    w_up,
    w_down,
):
    groups = lax.axis_size("dp")
    members = lax.axis_size("mp")
    member = lax.axis_index("mp")
    local_rows = tokens.shape[0]
    group_rows = local_rows * members
    bucket = local_rows // groups
    target = route // TOK_DEV
    chosen = (target[:, None] == jnp.arange(groups, dtype=jnp.int32)[None, :]).astype(jnp.int32)
    ranking = jnp.sum((jnp.cumsum(chosen, axis=0) - chosen) * chosen, axis=1)
    send_at = target * bucket + ranking
    arrival, arrival_grad, arrival_slot = (
        lax.all_to_all(
            jnp.zeros_like(tokens).at[send_at].set(tokens),
            "dp",
            split_axis=0,
            concat_axis=0,
            tiled=True,
        ),
        lax.all_to_all(
            jnp.zeros_like(cotangent).at[send_at].set(cotangent),
            "dp",
            split_axis=0,
            concat_axis=0,
            tiled=True,
        ),
        lax.all_to_all(
            jnp.zeros_like(route).at[send_at].set(route % local_rows),
            "dp",
            split_axis=0,
            concat_axis=0,
            tiled=True,
        ),
    )
    token_rows = jnp.zeros_like(arrival).at[arrival_slot].set(arrival)
    grad_rows = jnp.zeros_like(arrival_grad).at[arrival_slot].set(arrival_grad)
    seq_ends = jnp.cumsum(lengths[0])
    positions = jnp.arange(group_rows, dtype=jnp.int32)
    segment = jnp.sum((positions[:, None] >= seq_ends[None, :]).astype(jnp.int32), axis=1)
    input_rows = token_rows.astype(jnp.float32)
    normed_one, inverse_one = norm_rows(input_rows)
    leading_all, grad_all = (
        lax.all_gather(token_rows, "mp", axis=0, tiled=True),
        lax.all_gather(grad_rows, "mp", axis=0, tiled=True),
    )
    input_all = leading_all.astype(jnp.float32)
    normed_all, _ = norm_rows(input_all)
    hidden_one = (normed_all * norm1_gain).astype(jnp.bfloat16)
    head_count = w_query.shape[1] // HEAD_DIM
    query = jnp.dot(hidden_one, w_query, preferred_element_type=jnp.float32).astype(jnp.bfloat16)
    keys = jnp.dot(hidden_one, w_key, preferred_element_type=jnp.float32).astype(jnp.bfloat16)
    values = jnp.dot(hidden_one, w_value, preferred_element_type=jnp.float32).astype(jnp.bfloat16)
    query_heads = query.reshape(group_rows, head_count, HEAD_DIM)
    key_heads = keys.reshape(group_rows, head_count, HEAD_DIM)
    value_heads = values.reshape(group_rows, head_count, HEAD_DIM)
    mixed_flat, logsum = attend_forward(query_heads, key_heads, value_heads, segment, key_mask)
    attention_all = lax.psum(jnp.dot(mixed_flat, w_out, preferred_element_type=jnp.float32), "mp")
    middle_all = input_all + attention_all
    middle_rows = lax.dynamic_slice_in_dim(middle_all, member * local_rows, local_rows, 0)
    normed_mid, _ = norm_rows(middle_all)
    hidden_two = (normed_mid * norm2_gain).astype(jnp.bfloat16)
    normed_two, inverse_two = norm_rows(middle_rows)
    gate_value = jnp.dot(hidden_two, w_gate, preferred_element_type=jnp.float32)
    upward = jnp.dot(hidden_two, w_up, preferred_element_type=jnp.float32)
    sigmoid = jax.nn.sigmoid(gate_value)
    activated = (gate_value * sigmoid * upward).astype(jnp.bfloat16)
    out_rows = middle_rows + lax.psum_scatter(
        jnp.dot(activated, w_down, preferred_element_type=jnp.float32).astype(jnp.bfloat16),
        "mp",
        scatter_dimension=0,
        tiled=True,
    ).astype(jnp.float32)
    activated_grad = jnp.einsum("td,fd->tf", grad_all, w_down, preferred_element_type=jnp.float32)
    gate_grad = (activated_grad * upward * sigmoid * (1.0 + gate_value * (1.0 - sigmoid))).astype(
        jnp.bfloat16
    )
    upward_grad = (activated_grad * gate_value * sigmoid).astype(jnp.bfloat16)
    down_sum = jnp.einsum("tf,td->fd", activated, grad_all, preferred_element_type=jnp.float32)
    gate_sum = jnp.einsum("td,tf->df", hidden_two, gate_grad, preferred_element_type=jnp.float32)
    upward_sum = jnp.einsum(
        "td,tf->df", hidden_two, upward_grad, preferred_element_type=jnp.float32
    )
    hidden_two_grad = lax.psum_scatter(
        jnp.einsum("tf,df->td", gate_grad, w_gate, preferred_element_type=jnp.float32)
        + jnp.einsum("tf,df->td", upward_grad, w_up, preferred_element_type=jnp.float32),
        "mp",
        scatter_dimension=0,
        tiled=True,
    )
    norm_part_two, gain_two_grad = norm_back(hidden_two_grad, normed_two, inverse_two, norm2_gain)
    middle_grad = grad_rows.astype(jnp.float32) + norm_part_two
    branch_all = lax.all_gather(middle_grad.astype(jnp.bfloat16), "mp", axis=0, tiled=True)
    output_sum = jnp.einsum("tc,td->cd", mixed_flat, branch_all, preferred_element_type=jnp.float32)
    mixed_grad = jnp.einsum(
        "td,cd->tc", branch_all, w_out, preferred_element_type=jnp.float32
    ).astype(jnp.bfloat16)
    query_grad, key_grad, value_grad = attend_backward(
        query_heads,
        key_heads,
        value_heads,
        segment,
        key_mask,
        logsum,
        mixed_grad.reshape(group_rows, head_count, HEAD_DIM),
    )
    query_sum = jnp.einsum("td,tc->dc", hidden_one, query_grad, preferred_element_type=jnp.float32)
    key_sum = jnp.einsum("td,tc->dc", hidden_one, key_grad, preferred_element_type=jnp.float32)
    value_sum = jnp.einsum("td,tc->dc", hidden_one, value_grad, preferred_element_type=jnp.float32)
    hidden_one_grad = lax.psum_scatter(
        (
            jnp.einsum("tc,dc->td", query_grad, w_query, preferred_element_type=jnp.float32)
            + jnp.einsum("tc,dc->td", key_grad, w_key, preferred_element_type=jnp.float32)
            + jnp.einsum("tc,dc->td", value_grad, w_value, preferred_element_type=jnp.float32)
        ).astype(jnp.bfloat16),
        "mp",
        scatter_dimension=0,
        tiled=True,
    ).astype(jnp.float32)
    norm_part_one, gain_one_grad = norm_back(hidden_one_grad, normed_one, inverse_one, norm1_gain)
    input_grad = middle_grad + norm_part_one
    gain_one_sum, gain_two_sum = lax.psum((gain_one_grad, gain_two_grad), ("dp", "mp"))
    weight_sums = (
        lax.psum(query_sum.astype(jnp.bfloat16), "dp").astype(jnp.float32),
        lax.psum(key_sum.astype(jnp.bfloat16), "dp").astype(jnp.float32),
        lax.psum(value_sum.astype(jnp.bfloat16), "dp").astype(jnp.float32),
        lax.psum(output_sum.astype(jnp.bfloat16), "dp").astype(jnp.float32),
        lax.psum(gate_sum.astype(jnp.bfloat16), "dp").astype(jnp.float32),
        lax.psum(upward_sum.astype(jnp.bfloat16), "dp").astype(jnp.float32),
        lax.psum(down_sum.astype(jnp.bfloat16), "dp").astype(jnp.float32),
    )
    back_out, back_grad = (
        lax.all_to_all(
            out_rows.astype(jnp.bfloat16)[arrival_slot],
            "dp",
            split_axis=0,
            concat_axis=0,
            tiled=True,
        ),
        lax.all_to_all(
            input_grad.astype(jnp.bfloat16)[arrival_slot],
            "dp",
            split_axis=0,
            concat_axis=0,
            tiled=True,
        ),
    )
    return (
        back_out[send_at],
        back_grad[send_at],
        gain_one_sum,
        gain_two_sum,
        weight_sums[0],
        weight_sums[1],
        weight_sums[2],
        weight_sums[3],
        weight_sums[4],
        weight_sums[5],
        weight_sums[6],
    )


MESH = pl.DeviceIdType.MESH
LANES = 128
F32 = jnp.float32
BF16 = jnp.bfloat16
VMEM_LIMIT = 56 * 1024 * 1024


def plane():
    me = lax.axis_index("dp")
    side = me + 1 - 2 * lax.rem(me, 2)
    over_x = me + 2 - 4 * lax.rem(lax.div(me, 2), 2)
    over_y = me + 4 - 8 * lax.rem(lax.div(me, 4), 2)
    corner = over_x + 4 - 8 * lax.rem(lax.div(over_x, 4), 2)
    return (me, side, over_x, over_y, corner)


def to_dp(source, target, send_sem, recv_sem, index):
    return pltpu.make_async_remote_copy(
        src_ref=source,
        dst_ref=target,
        send_sem=send_sem,
        recv_sem=recv_sem,
        device_id={"dp": index},
        device_id_type=MESH,
    )


def to_mp(source, target, send_sem, recv_sem, index):
    return pltpu.make_async_remote_copy(
        src_ref=source,
        dst_ref=target,
        send_sem=send_sem,
        recv_sem=recv_sem,
        device_id={"mp": index},
        device_id_type=MESH,
    )


def greet_plane():
    _, side, over_x, over_y, _ = plane()
    barrier = pltpu.get_barrier_semaphore()
    for other in (side, over_x, over_y):
        pl.semaphore_signal(barrier, inc=1, device_id={"dp": other}, device_id_type=MESH)
    return barrier


class Gather:
    AFTER = {0: (5, 6), 1: (7, 8), 2: (9,), 3: (10,), 5: (11,), 7: (12,)}

    def __init__(self, own, out, send, recv, local=None):
        me, side, over_x, over_y, corner = plane()
        half = out.shape[1] // 2
        low, high = pl.ds(0, half), pl.ds(half, half)
        self.keep = None if own is None else pltpu.make_async_copy(own, out.at[me], local)
        own = out.at[me] if own is None else own

        def hop(number, source, target, index):
            return to_dp(source, target, send.at[number], recv.at[number], index)

        def onward(number, owner, part, index):
            place = out.at[owner, part]
            return hop(number, place, place, index)

        self.copies = [
            hop(0, own.at[low], out.at[me, low], over_x),
            hop(1, own.at[high], out.at[me, high], over_y),
            hop(2, own.at[high], out.at[me, high], over_x),
            hop(3, own.at[low], out.at[me, low], over_y),
            hop(4, own, out.at[me], side),
            onward(5, over_x, low, over_y),
            onward(6, over_x, low, side),
            onward(7, over_y, high, over_x),
            onward(8, over_y, high, side),
            onward(9, over_x, high, side),
            onward(10, over_y, low, side),
            onward(11, corner, low, side),
            onward(12, corner, high, side),
        ]

    def start(self):
        for number in range(5):
            self.copies[number].start()
        if self.keep is not None:
            self.keep.start()

    def arrive(self, *numbers):
        for number in numbers:
            self.copies[number].wait_recv()
            for later in self.AFTER.get(number, ()):
                self.copies[later].start()

    def pass_on(self):
        self.arrive(0, 1, 2, 3)

    def sent(self):
        for copy in self.copies:
            copy.wait_send()
        if self.keep is not None:
            self.keep.wait()

    def finish(self):
        self.arrive(5, 7, 4, 6, 8, 9, 10, 11, 12)
        self.sent()


def greet_all(barrier):
    me, z = lax.axis_index("dp"), lax.axis_index("mp")
    for step in range(1, 8):
        pl.semaphore_signal(
            barrier, inc=1, device_id={"dp": lax.rem(me + step, 8)}, device_id_type=MESH
        )
    core = lax.rem(me, 2)
    for step in range(1, 4):
        for other in (me, me + 1 - 2 * core):
            pl.semaphore_signal(
                barrier,
                inc=1,
                device_id={"dp": other, "mp": lax.rem(z + step, 4)},
                device_id_type=MESH,
            )
    pl.semaphore_wait(barrier, 13)


def swap_all(source, target, send, recv):
    me = lax.axis_index("dp")
    return [
        to_dp(source, target.at[me], send.at[step - 1], recv.at[step - 1], lax.rem(me + step, 8))
        for step in range(1, 8)
    ]


class Spread:
    def __init__(self, share, w_qkv, w_out, send, recv, local):
        me, z = lax.axis_index("dp"), lax.axis_index("mp")
        core = lax.rem(me, 2)
        self.place = z + core * (3 - 2 * z)
        self.send, self.recv, self.local = send, recv, local
        self.shares = [share.at[0], share.at[1], share.at[2], share.at[3]]
        self.slots = (core, 1 - core)
        self.core = core
        self.w_qkv, self.w_out = w_qkv, w_out

    def target(self, which, piece):
        slot = self.slots[which]
        block = slot if piece == 3 else 2 * piece + slot
        rows = pl.ds(pl.multiple_of(block * LANES, LANES), HEAD_DIM)
        return (self.w_out if piece == 3 else self.w_qkv).at[rows]

    def hop(self, which, piece, number, place, own):
        source = self.shares[piece] if own else self.target(which, piece)
        z = place + self.core * (3 - 2 * place)
        return to_mp(
            source,
            self.target(which, piece),
            self.send.at[number * 4 + piece],
            self.recv.at[which * 4 + piece],
            z,
        )

    def keep(self, which, piece):
        return pltpu.make_async_copy(
            self.shares[piece], self.target(which, piece), self.local.at[piece]
        )

    def start(self):
        @pl.when(self.place == 0)
        def _():
            for piece in range(4):
                self.hop(0, piece, 0, 1, True).start()
                self.keep(0, piece).start()

        @pl.when(self.place == 1)
        def _():
            for piece in range(4):
                self.hop(1, piece, 0, 0, True).start()
                self.hop(1, piece, 1, 2, True).start()
                self.keep(1, piece).start()

    def pass_on(self):
        @pl.when(self.place == 1)
        def _():
            for piece in range(4):
                self.hop(0, piece, 2, 2, False).wait_recv()
                self.hop(0, piece, 2, 2, False).start()

        @pl.when(self.place == 2)
        def _():
            for piece in range(4):
                for which in (1, 0):
                    self.hop(which, piece, which, 3, False).wait_recv()
                    self.hop(which, piece, which, 3, False).start()

    def finish(self):
        @pl.when(self.place == 0)
        def _():
            for piece in range(4):
                self.hop(1, piece, 0, 1, False).wait_recv()
                self.hop(0, piece, 0, 1, True).wait_send()
                self.keep(0, piece).wait()

        @pl.when(self.place == 1)
        def _():
            for piece in range(4):
                self.hop(1, piece, 0, 0, True).wait_send()
                self.hop(1, piece, 1, 2, True).wait_send()
                self.hop(0, piece, 2, 2, False).wait_send()
                self.keep(1, piece).wait()

        @pl.when(self.place == 2)
        def _():
            for piece in range(4):
                for which in (1, 0):
                    self.hop(which, piece, which, 3, False).wait_send()

        @pl.when(self.place == 3)
        def _():
            for piece in range(4):
                for which in (1, 0):
                    self.hop(which, piece, which, 3, False).wait_recv()


def first_kernel(
    hidden, query, keys, values, project, gate, upward, down, notes,
    hidden_all, w_qkv, w_out, notes_all, both_own, down_own,
    share, none, send_a, recv_a, send_w, recv_w, send_n, recv_n, local,
):
    me = lax.axis_index("dp")
    head = pl.ds(pl.multiple_of(lax.div(me, 2) * HEAD_DIM, 16), HEAD_DIM)
    loads = [
        pltpu.make_async_copy(source.at[head], share.at[piece], local.at[piece])
        for piece, source in enumerate((query, keys, values, project))
    ]
    units = pl.ds(pl.multiple_of(me * LANES, LANES), LANES)
    loads += [
        pltpu.make_async_copy(gate.at[:, units], both_own.at[:, pl.ds(0, LANES)], local.at[14]),
        pltpu.make_async_copy(upward.at[:, units], both_own.at[:, pl.ds(LANES, LANES)], local.at[15]),
        pltpu.make_async_copy(down.at[units], down_own, local.at[16]),
    ]
    for copy in loads:
        copy.start()
    none[...] = jnp.zeros_like(none)
    greet_all(pltpu.get_barrier_semaphore())
    gather = Gather(hidden, hidden_all, send_a, recv_a, local.at[4])
    gather.start()
    swaps = swap_all(notes, notes_all, send_n, recv_n)
    for copy in swaps:
        copy.start()
    keep = pltpu.make_async_copy(notes, notes_all.at[me], local.at[5])
    keep.start()
    pads = [
        pltpu.make_async_copy(
            none, weight.at[pl.ds(block * LANES + HEAD_DIM, LANES - HEAD_DIM)], local.at[6 + number]
        )
        for number, (weight, block) in enumerate(
            [(w_qkv, block) for block in range(6)] + [(w_out, block) for block in range(2)]
        )
    ]
    for copy in pads:
        copy.start()
    for copy in loads[:4]:
        copy.wait()
    spread = Spread(share, w_qkv, w_out, send_w, recv_w, local)
    spread.start()
    spread.pass_on()
    gather.pass_on()
    gather.finish()
    spread.finish()
    for copy in swaps:
        copy.wait()
    for copy in pads + loads[4:]:
        copy.wait()
    keep.wait()


def anywhere():
    return pl.BlockSpec(memory_space=pl.ANY)


def on_chip():
    return pl.BlockSpec(memory_space=pltpu.VMEM)


def in_scalar():
    return pl.BlockSpec(memory_space=pltpu.SMEM)


def remote_params(number, limit=VMEM_LIMIT):
    return pltpu.CompilerParams(
        collective_id=number, has_side_effects=True, vmem_limit_bytes=limit
    )


def gather_first(hidden, query, keys, values, project, gate, upward, down, notes):
    rows, width = hidden.shape
    groups = lax.axis_size("dp")
    dma = pltpu.SemaphoreType.DMA
    return pl.pallas_call(
        first_kernel,
        out_shape=(
            jax.ShapeDtypeStruct((groups, rows, width), BF16),
            jax.ShapeDtypeStruct((6 * LANES, width), BF16),
            jax.ShapeDtypeStruct((2 * LANES, width), BF16),
            jax.ShapeDtypeStruct((groups,) + notes.shape, notes.dtype),
            jax.ShapeDtypeStruct((width, 2 * LANES), BF16),
            jax.ShapeDtypeStruct((LANES, width), BF16),
        ),
        in_specs=[on_chip()] + [anywhere()] * 7 + [on_chip()],
        out_specs=(anywhere(),) * 4 + (on_chip(),) * 2,
        scratch_shapes=[
            pltpu.VMEM((4, HEAD_DIM, width), BF16),
            pltpu.VMEM((LANES - HEAD_DIM, width), BF16),
            dma((13,)), dma((13,)), dma((12,)), dma((8,)), dma((7,)), dma((7,)), dma((17,)),
        ],
        compiler_params=remote_params(1),
        cost_estimate=pl.CostEstimate(flops=0, bytes_accessed=200_000_000, transcendentals=0),
        name="gather_first",
    )(hidden, query, keys, values, project, gate, upward, down, notes)


def one_hot(slots, k, size):
    row = slots[pl.ds(k, 1), :]
    place = lax.broadcasted_iota(jnp.int32, (size, size), 0)
    return (place == row).astype(BF16)


def block_mask(lengths, flags, k, block, z, rows):
    position = rows * z + block * 128 + lax.broadcasted_iota(jnp.int32, (128, 1), 0)
    first_end = lengths[k, 0]
    second_end = first_end + lengths[k, 1]
    begin = jnp.where(position >= first_end, first_end, 0)
    begin = jnp.where(position >= second_end, second_end, begin)
    column = lax.broadcasted_iota(jnp.int32, (128, 192), 1)
    distance = 64 + lax.broadcasted_iota(jnp.int32, (128, 192), 0) - column
    key_position = rows * z + block * 128 - 64 + column
    live = flags[pl.ds(k, 1), block * 128 : block * 128 + 192]
    allowed = (distance >= 0) & (distance < WINDOW) & (key_position >= begin)
    return allowed & ((live == 1) | (distance == 0))


NT = (((1,), (1,)), ((), ()))
TN = (((0,), (0,)), ((), ()))


def forward_kernel(
    lengths, hidden_all, w_qkv, slots, flags, cotangent, mixed, kept, cotangent_all,
    qkv, shard, shard_sem, send, recv, send_g, recv_g, local, *, scale, groups, rows
):
    z = lax.axis_index("mp")
    members = lax.axis_size("mp")
    barrier = greet_plane()

    @pl.when(z > 0)
    def _():
        pl.semaphore_signal(barrier, inc=1, device_id={"mp": z - 1}, device_id_type=MESH)

    @pl.when(z < members - 1)
    def _():
        pl.semaphore_wait(barrier, 4)

    @pl.when(z == members - 1)
    def _():
        pl.semaphore_wait(barrier, 3)

    gather = Gather(cotangent, cotangent_all, send_g, recv_g, local)
    gather.start()

    def load(g):
        slot = lax.rem(g, 2)
        return pltpu.make_async_copy(hidden_all.at[g], shard.at[slot], shard_sem.at[slot])

    load(0).start()

    def multiply(g, carry):
        @pl.when(g < groups - 1)
        def _():
            load(g + 1).start()

        load(g).wait()
        product = lax.dot_general(
            shard[lax.rem(g, 2)], w_qkv[...], NT, preferred_element_type=F32
        ).astype(BF16)
        qkv[g] = product.reshape(groups, rows // groups, 768)
        return carry

    lax.fori_loop(0, groups, multiply, 0)

    def halo(k, other):
        return to_mp(
            kept.at[k, pl.ds(rows, 64), pl.ds(256, 512)],
            kept.at[k, pl.ds(0, 64), pl.ds(256, 512)],
            send.at[k],
            recv.at[k],
            other,
        )

    def order(k, carry):
        hot = one_hot(slots, k, rows)
        given = qkv[:, pl.ds(k, 1)].reshape(rows, 768)
        kept[k, pl.ds(64, rows), :] = jnp.dot(hot, given, preferred_element_type=F32).astype(BF16)
        kept[k, pl.ds(0, 64), pl.ds(0, 256)] = jnp.zeros((64, 256), BF16)

        @pl.when(z < members - 1)
        def _():
            halo(k, z + 1).start()

        @pl.when(z == 0)
        def _():
            kept[k, pl.ds(0, 64), pl.ds(256, 512)] = jnp.zeros((64, 512), BF16)

        return carry

    lax.fori_loop(0, groups, order, 0)

    def attend(k, carry):
        @pl.when(z > 0)
        def _():
            halo(k, z).wait_recv()

        hot = one_hot(slots, k, rows)
        found = []
        for block in range(rows // 128):
            allowed = block_mask(lengths, flags, k, block, z, rows)
            heads = []
            for head in range(2):
                query = kept[k, pl.ds(64 + block * 128, 128), pl.ds(head * 128, 128)]
                keys = kept[k, pl.ds(block * 128, 192), pl.ds(256 + head * 128, 128)]
                values = kept[k, pl.ds(block * 128, 192), pl.ds(512 + head * 128, 128)]
                scores = lax.dot_general(query, keys, NT, preferred_element_type=F32) * scale
                scores = jnp.where(allowed, scores, -MASKED)
                weights = jnp.exp(scores - jnp.max(scores, axis=-1, keepdims=True))
                total = jnp.sum(weights, axis=-1, keepdims=True)
                chances = (weights / total).astype(BF16)
                heads.append(jnp.dot(chances, values, preferred_element_type=F32).astype(BF16))
            found.append(jnp.concatenate(heads, axis=1))
        ordered = jnp.concatenate(found, axis=0)
        back = lax.dot_general(hot, ordered, TN, preferred_element_type=F32).astype(BF16)
        mixed[:, pl.ds(k, 1)] = back.reshape(groups, 1, rows // groups, 256)
        return carry

    lax.fori_loop(0, groups // 4, attend, 0)
    gather.pass_on()
    lax.fori_loop(groups // 4, groups, attend, 0)
    gather.finish()

    @pl.when(z < members - 1)
    def _():
        def done(k, carry):
            halo(k, z + 1).wait_send()
            return carry

        lax.fori_loop(0, groups, done, 0)


def attend_ahead(lengths, hidden_all, w_qkv, slots, flags, cotangent, scale):
    groups, rows, width = hidden_all.shape
    dma = pltpu.SemaphoreType.DMA
    return pl.pallas_call(
        functools.partial(forward_kernel, scale=scale, groups=groups, rows=rows),
        out_shape=(
            jax.ShapeDtypeStruct((groups, groups, rows // groups, 256), BF16),
            jax.ShapeDtypeStruct((groups, rows + 64, 768), BF16),
            jax.ShapeDtypeStruct((groups,) + cotangent.shape, BF16),
        ),
        in_specs=[in_scalar(), anywhere()] + [on_chip()] * 4,
        out_specs=(on_chip(), on_chip(), anywhere()),
        scratch_shapes=[
            pltpu.VMEM((groups, groups, rows // groups, 768), BF16),
            pltpu.VMEM((2, rows, width), BF16),
            dma((2,)),
            dma((groups,)),
            dma((groups,)),
            dma((13,)),
            dma((13,)),
            dma(()),
        ],
        compiler_params=remote_params(2),
        cost_estimate=pl.CostEstimate(flops=0, bytes_accessed=200_000_000, transcendentals=0),
        name="attend_ahead",
    )(lengths, hidden_all, w_qkv, slots, flags, cotangent)


CHUNK = 32


def each_chunk(rows, body, chunk=CHUNK):
    def step(i, carry):
        body(pl.ds(pl.multiple_of(i * chunk, chunk), chunk))
        return carry

    lax.fori_loop(0, rows // chunk, step, 0)


class Reduce:
    COUNT = 10

    def __init__(self, left, right, across, part, from_side, from_corner, from_near, send, recv):
        self.left, self.right, self.across, self.part = left, right, across, part
        self.from_side, self.from_corner, self.from_near = from_side, from_corner, from_near
        self.send, self.recv = send, recv
        self.rows = part.shape[1]

    def product(self, owner, slot):
        rows, width = self.rows, self.part.shape[2]
        picked = pl.ds(pl.multiple_of(owner * rows, rows), rows)

        def tile(t, carry):
            columns = pl.ds(pl.multiple_of(t * 256, 256), 256)
            if self.across:
                value = lax.dot_general(
                    self.left[picked, :], self.right[columns, :], NT, preferred_element_type=F32
                )
            else:
                value = jnp.dot(
                    self.left[picked, :], self.right[:, columns], preferred_element_type=F32
                )
            self.part[slot, :, columns] = value.astype(BF16)
            return carry

        lax.fori_loop(0, width // 256, tile, 0)

    def prepare(self):
        _, side, over_x, over_y, corner = plane()
        part, near = self.part, self.from_near
        half = self.rows // 2
        low, high = pl.ds(0, half), pl.ds(half, half)

        def hop(number, source, target, index):
            return to_dp(source, target, self.send.at[number], self.recv.at[number], index)

        self.shares = [hop(i, part.at[4 + i], self.from_side.at[i], side) for i in range(4)]
        self.corners = [
            hop(4, part.at[0, low], self.from_corner.at[0], over_x),
            hop(5, part.at[0, high], self.from_corner.at[1], over_y),
        ]
        self.nears = [
            hop(6, part.at[1, low], near.at[0, low], over_x),
            hop(7, part.at[1, high], near.at[0, high], over_x),
            hop(8, part.at[2, high], near.at[1, high], over_y),
            hop(9, part.at[2, low], near.at[1, low], over_y),
        ]

    def add_side(self, slot):
        self.shares[slot].wait_recv()

        def body(span):
            self.part[slot, span, :] = (
                self.part[slot, span, :].astype(F32) + self.from_side[slot, span, :].astype(F32)
            ).astype(BF16)

        each_chunk(self.rows, body)

    def add_corner(self, slot, offset, which):
        self.corners[which].wait_recv()

        def body(span):
            target = pl.ds(pl.multiple_of(offset + span.start, CHUNK), CHUNK)
            self.part[slot, target, :] = (
                self.part[slot, target, :].astype(F32)
                + self.from_corner[which, span, :].astype(F32)
            ).astype(BF16)

        each_chunk(self.rows // 2, body)

    def begin(self):
        self.prepare()
        me, _, over_x, over_y, corner = plane()
        owners = (corner, over_x, over_y, me)
        turn = 1 - 2 * lax.rem(me, 2)
        self.product(corner + turn, 4)
        self.shares[0].start()
        self.product(corner, 0)
        self.product(over_x + turn, 5)
        self.shares[1].start()
        self.add_side(0)
        self.corners[0].start()
        self.corners[1].start()
        self.product(over_x, 1)
        self.product(over_y + turn, 6)
        self.shares[2].start()
        self.add_side(1)
        self.nears[0].start()
        self.product(over_y, 2)
        self.product(me + turn, 7)
        self.shares[3].start()
        self.add_side(2)
        self.nears[2].start()
        self.product(me, 3)

    def middle(self):
        self.add_corner(2, 0, 0)
        self.nears[3].start()
        self.add_corner(1, self.rows // 2, 1)
        self.nears[1].start()

    def end(self):
        self.shares[3].wait_recv()
        for copy in self.nears:
            copy.wait_recv()

    def run(self):
        self.begin()
        self.middle()
        self.end()

    def rows_of(self, span):
        return (
            self.part[3, span, :].astype(F32)
            + self.from_side[3, span, :].astype(F32)
            + self.from_near[0, span, :].astype(F32)
            + self.from_near[1, span, :].astype(F32)
        )

    def finish(self):
        for copy in self.shares + self.corners + self.nears:
            copy.wait_send()


def reduce_scratch(rows, width):
    dma = pltpu.SemaphoreType.DMA
    return [
        pltpu.VMEM((8, rows, width), BF16),
        pltpu.VMEM((4, rows, width), BF16),
        pltpu.VMEM((2, rows // 2, width), BF16),
        pltpu.VMEM((2, rows, width), BF16),
        dma((10,)),
        dma((10,)),
    ]


def gather_scratch(rows, width):
    dma = pltpu.SemaphoreType.DMA
    return [pltpu.VMEM((rows, width), BF16), dma((13,)), dma((13,)), dma(())]


def mean_rows(values):
    return jnp.mean(values, axis=-1, keepdims=True)


class Heads:
    def __init__(self, source, arrive, send, recv, views):
        me, z = lax.axis_index("dp"), lax.axis_index("mp")
        self.me, self.z = me, z
        self.core = lax.rem(me, 2)
        self.source, self.arrive, self.send, self.recv, self.views = source, arrive, send, recv, views
        self.owner = lax.div(z, 2)

    def copy(self, slot, half, number):
        target_z = 2 * self.core + slot
        index = (slot * 2 + half) * self.views + number
        return to_at(
            self.view(slot, half, number),
            self.arrive.at[self.z, number],
            self.send.at[index],
            self.recv.at[self.z * self.views + number],
            self.me - self.core + half,
            target_z,
        )

    def view(self, slot, half, number):
        rows = pl.ds(pl.multiple_of((2 * number + slot) * LANES, LANES), HEAD_DIM)
        columns = self.source.shape[1] // 2
        return self.source.at[rows, pl.ds(pl.multiple_of(half * columns, LANES), columns)]

    def each(self, action):
        for slot in range(2):
            for half in range(2):
                mine = (2 * self.core + slot == self.z) & (self.core == half)

                @pl.when(jnp.logical_not(mine))
                def _():
                    for number in range(self.views):
                        action(self.copy(slot, half, number))

    def start(self):
        self.each(lambda copy: copy.start())

    def finish_send(self):
        self.each(lambda copy: copy.wait_send())

    def total(self, out):
        me, z = self.me, self.z
        for number in range(self.views):
            for other in range(4):
                waiting = to_at(
                    self.view(0, 0, number),
                    self.arrive.at[other, number],
                    self.send.at[0],
                    self.recv.at[other * self.views + number],
                    me,
                    other,
                )

                @pl.when((z != other) | (self.core != self.owner))
                def _():
                    waiting.wait_recv()

                @pl.when((z == other) & (self.core == self.owner))
                def _():
                    self.arrive[other, number] = self.view(lax.rem(z, 2), self.core, number)[...]

            count = self.arrive.shape[2]

            def body(span):
                found = self.arrive[0, number, span, :].astype(F32)
                for other in range(1, 4):
                    found = found + self.arrive[other, number, span, :].astype(F32)
                out[number, span, :] = found.astype(BF16)

            each_chunk(count, body, 16)


def to_at(source, target, send_sem, recv_sem, dp, mp):
    return pltpu.make_async_remote_copy(
        src_ref=source,
        dst_ref=target,
        send_sem=send_sem,
        recv_sem=recv_sem,
        device_id={"dp": dp, "mp": mp},
        device_id_type=MESH,
    )


def backward_kernel(
    lengths, kept, mixed_grad, slots, flags, activated, w_down, middle, proj_sum,
    out, result, proj_part,
    totals, query_part, key_value, ending, leaving, arriving, send, recv,
    part, from_side, from_corner, from_near, send_r, recv_r, arrive, send_h, recv_h,
    *, scale, groups, rows,
):
    z = lax.axis_index("mp")
    members = lax.axis_size("mp")
    greet_all(pltpu.get_barrier_semaphore())
    heads = Heads(proj_sum, arrive, send_h, recv_h, 1)
    heads.start()
    reduce = Reduce(activated, w_down, False, part, from_side, from_corner, from_near, send_r, recv_r)
    reduce.begin()

    def halo(k, other):
        return to_mp(leaving.at[k], arriving.at[k], send.at[k], recv.at[k], other)

    def attend(k, carry):
        hot = one_hot(slots, k, rows)
        given = mixed_grad[:, pl.ds(k, 1)].reshape(rows, 256)
        grad_ordered = jnp.dot(hot, given, preferred_element_type=F32).astype(BF16)
        totals[...] = jnp.zeros_like(totals)
        for block in range(rows // 128):
            allowed = block_mask(lengths, flags, k, block, z, rows)
            for head in range(2):
                query = kept[k, pl.ds(64 + block * 128, 128), pl.ds(head * 128, 128)]
                keys = kept[k, pl.ds(block * 128, 192), pl.ds(256 + head * 128, 128)]
                values = kept[k, pl.ds(block * 128, 192), pl.ds(512 + head * 128, 128)]
                grad = grad_ordered[block * 128 : block * 128 + 128, head * 128 : head * 128 + 128]
                scores = lax.dot_general(query, keys, NT, preferred_element_type=F32) * scale
                scores = jnp.where(allowed, scores, -MASKED)
                weights = jnp.exp(scores - jnp.max(scores, axis=-1, keepdims=True))
                again = weights / jnp.sum(weights, axis=-1, keepdims=True)
                chance_grad = lax.dot_general(grad, values, NT, preferred_element_type=F32)
                row_dot = jnp.sum(again * chance_grad, axis=-1, keepdims=True)
                score_grad = (again * (chance_grad - row_dot)).astype(BF16)
                query_part[k, pl.ds(block * 128, 128), pl.ds(head * 128, 128)] = (
                    jnp.dot(score_grad, keys, preferred_element_type=F32) * scale
                ).astype(BF16)
                totals[pl.ds(block * 128, 192), pl.ds(head * 128, 128)] += (
                    lax.dot_general(score_grad, query, TN, preferred_element_type=F32) * scale
                )
                totals[pl.ds(block * 128, 192), pl.ds(256 + head * 128, 128)] += lax.dot_general(
                    again.astype(BF16), grad, TN, preferred_element_type=F32
                )
        key_value[k] = totals[pl.ds(64, rows), :].astype(BF16)
        ending[k] = totals[pl.ds(rows, 64), :]

        @pl.when(z > 0)
        def _():
            leaving[k] = totals[pl.ds(0, 64), :].astype(BF16)
            halo(k, z - 1).start()

        return carry

    lax.fori_loop(0, groups - 5, attend, 0)
    reduce.middle()
    lax.fori_loop(groups - 5, groups, attend, 0)

    def restore(k, carry):
        @pl.when(z < members - 1)
        def _():
            halo(k, z).wait_recv()
            key_value[k, pl.ds(rows - 64, 64), :] = (
                ending[k] + arriving[k].astype(F32)
            ).astype(BF16)

        hot = one_hot(slots, k, rows)
        ordered = jnp.concatenate([query_part[k], key_value[k]], axis=1)
        back = lax.dot_general(hot, ordered, TN, preferred_element_type=F32).astype(BF16)
        out[:, pl.ds(k, 1)] = back.reshape(groups, 1, rows // groups, 768)
        return carry

    lax.fori_loop(0, groups, restore, 0)
    reduce.end()

    def body(span):
        result[span, :] = (middle[span, :] + reduce.rows_of(span)).astype(BF16)

    each_chunk(rows, body)
    heads.total(proj_part)
    heads.finish_send()
    reduce.finish()

    @pl.when(z > 0)
    def _():
        def done(k, carry):
            halo(k, z - 1).wait_send()
            return carry

        lax.fori_loop(0, groups, done, 0)


def attend_back(
    lengths, kept, mixed_grad, slots, flags, activated, w_down, middle, proj_sum, scale
):
    groups = kept.shape[0]
    rows, width = middle.shape
    dma = pltpu.SemaphoreType.DMA
    return pl.pallas_call(
        functools.partial(backward_kernel, scale=scale, groups=groups, rows=rows),
        out_shape=(
            jax.ShapeDtypeStruct((groups, groups, rows // groups, 768), BF16),
            jax.ShapeDtypeStruct((rows, width), BF16),
            jax.ShapeDtypeStruct((1, HEAD_DIM, width // 2), BF16),
        ),
        in_specs=[in_scalar()] + [on_chip()] * 8,
        out_specs=(on_chip(), on_chip(), on_chip()),
        scratch_shapes=[
            pltpu.VMEM((rows + 64, 512), F32),
            pltpu.VMEM((groups, rows, 256), BF16),
            pltpu.VMEM((groups, rows, 512), BF16),
            pltpu.VMEM((groups, 64, 512), F32),
            pltpu.VMEM((groups, 64, 512), BF16),
            pltpu.VMEM((groups, 64, 512), BF16),
            dma((groups,)),
            dma((groups,)),
        ]
        + reduce_scratch(rows, width)
        + [pltpu.VMEM((4, 1, HEAD_DIM, width // 2), BF16), dma((4,)), dma((4,))],
        compiler_params=remote_params(3, 62 * 1024 * 1024),
        cost_estimate=pl.CostEstimate(flops=0, bytes_accessed=200_000_000, transcendentals=0),
        name="attend_back",
    )(lengths, kept, mixed_grad, slots, flags, activated, w_down, middle, proj_sum)


def middle_kernel(
    mixed, w_out, tokens, gain, middle, hidden,
    part, from_side, from_corner, from_near, send, recv,
):
    pl.semaphore_wait(greet_plane(), 3)
    reduce = Reduce(mixed, w_out, False, part, from_side, from_corner, from_near, send, recv)
    reduce.run()

    def body(span):
        values = tokens[span, :].astype(F32) + reduce.rows_of(span)
        middle[span, :] = values
        inverse = lax.rsqrt(mean_rows(values * values) + EPSILON)
        hidden[span, :] = (values * inverse * gain[...]).astype(BF16)

    each_chunk(hidden.shape[0], body)
    reduce.finish()


def project_middle(mixed, w_out, tokens, gain):
    rows, width = tokens.shape
    return pl.pallas_call(
        middle_kernel,
        out_shape=(
            jax.ShapeDtypeStruct((rows, width), F32),
            jax.ShapeDtypeStruct((rows, width), BF16),
        ),
        in_specs=[on_chip()] * 4,
        out_specs=(on_chip(), on_chip()),
        scratch_shapes=reduce_scratch(rows, width),
        compiler_params=remote_params(4),
        cost_estimate=pl.CostEstimate(flops=0, bytes_accessed=150_000_000, transcendentals=0),
        name="project_middle",
    )(mixed, w_out, tokens, gain)


def norm_back_rows(gradient, values, gain, sums, span):
    inverse = lax.rsqrt(mean_rows(values * values) + EPSILON)
    normed = values * inverse
    product = gradient * normed
    folded = product[0:8]
    for step in range(1, CHUNK // 8):
        folded = folded + product[step * 8 : step * 8 + 8]
    sums[...] += folded
    scaled = gradient * gain
    return inverse * (scaled - normed * mean_rows(scaled * normed))


def feed_kernel(
    hidden_own, cotangent_all, middle, cotangent, gain, w_both, w_down, mixed, w_out,
    middle_grad, mixed_grad, sums, activated, both_sum, down_sum, proj_sum,
    hidden_all, both_grad, part, from_side, from_corner, from_near, send_r, recv_r,
    send_a, recv_a, send_b, recv_b, cot_half, cot_tile, stage_both, stage_down, load_sem, local, ready,
):
    groups, rows, width = hidden_all.shape
    members = w_both.shape[0]
    half_rows = rows // 2
    me, side, over_x, over_y, _ = plane()
    own = pltpu.make_async_copy(hidden_own, hidden_all.at[me], local.at[0])
    own.start()
    start_middle = pltpu.make_async_copy(middle, middle_grad, local.at[1])
    start_middle.start()

    def place_of(step):
        block = step // 4
        near = ((block + 1) // 2) % 2
        far = block // 3
        mixed_order = near * (1 - block // 2)
        second = mixed_order * (step % 2) + (1 - mixed_order) * ((step // 2) % 2)
        half = mixed_order * ((step % 2 + (step // 2) % 2) % 2) + (1 - mixed_order) * (step % 2)
        other = (1 - near) * second + (block // 2) * near
        in_x = near * (1 - second) + far
        in_y = near * second + far
        owner = me + in_x * (over_x - me) + in_y * (over_y - me) + other * (side - me)
        slot = 4 * other + 3 * (1 - near) * (1 - far) + near * (1 + second)
        return owner, half, slot

    def load_cotangent(step):
        owner, half, _ = place_of(step)
        span = pl.ds(pl.multiple_of(half * half_rows, half_rows), half_rows)
        return pltpu.make_async_copy(
            cotangent_all.at[owner, span], cot_half.at[step % 2], load_sem.at[step % 2]
        )

    load_cotangent(0).start()
    pl.semaphore_wait(greet_plane(), 3)
    own.wait()
    gather = Gather(None, hidden_all, send_a, recv_a)
    gather.start()
    reduce = Reduce(None, None, False, part, from_side, from_corner, from_near, send_r, recv_r)
    reduce.prepare()

    def before(step, *numbers):
        return (step, lambda: gather.arrive(*numbers))

    def nears():
        reduce.add_side(1)
        reduce.nears[0].start()
        reduce.add_side(2)
        reduce.nears[2].start()

    early = [
        before(2, 4),
        before(4, 0),
        before(5, 1),
        before(6, 2),
        before(7, 3),
        before(8, 6, 9),
        before(10, 8, 10),
        before(12, 5, 7),
        (13, nears),
        before(14, 11, 12),
    ]
    late = [(3, 3), (9, 1), (11, 2), (15, 0)]

    def unit(step, carry):
        for number, action in early:
            pl.when(step == number)(action)

        @pl.when(step < 15)
        def _():
            load_cotangent(step + 1).start()

        load_cotangent(step).wait()
        owner, half, slot = place_of(step)
        span = pl.ds(pl.multiple_of(half * half_rows, half_rows), half_rows)
        mine = hidden_all[owner, span, :]
        grads = cot_half[step % 2]
        for z in range(members):
            raw = jnp.dot(mine, w_both[z], preferred_element_type=F32)
            units = pl.ds(z * 128, 128)
            if z % 2 == 0:
                pair = lax.dot_general(
                    grads, w_down[pl.ds(z * 128, 256), :], NT, preferred_element_type=F32
                )
            active_grad = pair[:, 128 * (z % 2) : 128 * (z % 2) + 128]
            gate, upward = raw[:, :128], raw[:, 128:]
            sigmoid = jax.nn.sigmoid(gate)
            activated[owner, span, units] = (gate * sigmoid * upward).astype(BF16)
            both_grad[owner, span, pl.ds(z * 256, 128)] = (
                active_grad * upward * sigmoid * (1.0 + gate * (1.0 - sigmoid))
            ).astype(BF16)
            both_grad[owner, span, pl.ds(z * 256 + 128, 128)] = (
                active_grad * gate * sigmoid
            ).astype(BF16)

        def tile(t, inner):
            columns = pl.ds(pl.multiple_of(t * 256, 256), 256)
            value = sum(
                lax.dot_general(
                    both_grad[owner, span, pl.ds(z * 256, 256)],
                    w_both[z, columns, :],
                    NT,
                    preferred_element_type=F32,
                )
                for z in range(members)
            )
            part[slot, span, columns] = value.astype(BF16)
            return inner

        lax.fori_loop(0, width // 256, tile, 0)
        for number, share in late:
            pl.when(step == number)(reduce.shares[share].start)
        return carry

    lax.fori_loop(0, 16, unit, 0)

    def load_tile(t):
        columns = pl.ds(pl.multiple_of(t * 256, 256), 256)
        return pltpu.make_async_copy(
            cotangent_all.at[:, :, columns], cot_tile.at[t % 2], load_sem.at[2 + t % 2]
        )

    def store_both(t):
        columns = pl.ds(pl.multiple_of(t * 256, 256), 256)
        return pltpu.make_async_copy(
            stage_both.at[t % 2], both_sum.at[:, columns], load_sem.at[4 + t % 2]
        )

    def store_down(t):
        columns = pl.ds(pl.multiple_of(t * 256, 256), 256)
        return pltpu.make_async_copy(
            stage_down.at[t % 2], down_sum.at[:, columns], load_sem.at[6 + t % 2]
        )

    tiles = width // 256
    count = groups * rows

    def weight_tile(t, carry):
        columns = pl.ds(pl.multiple_of(t * 256, 256), 256)

        @pl.when(t < tiles - 1)
        def _():
            load_tile(t + 1).start()

        load_tile(t).wait()

        @pl.when(t >= 2)
        def _():
            store_both(t - 2).wait()
            store_down(t - 2).wait()

        value = lax.dot_general(
            hidden_all[:, :, columns].reshape(count, 256),
            both_grad[...].reshape(count, members * 256),
            TN,
            preferred_element_type=F32,
        )
        for z in range(members):
            stage_both[t % 2, z] = value[:, z * 256 : z * 256 + 256].astype(BF16)
        stage_down[t % 2] = lax.dot_general(
            activated[...].reshape(count, members * 128),
            cot_tile[t % 2].reshape(count, 256),
            TN,
            preferred_element_type=F32,
        ).astype(BF16)
        store_both(t).start()
        store_down(t).start()
        return carry

    load_tile(0).start()
    reduce.add_side(0)
    reduce.corners[0].start()
    reduce.corners[1].start()
    lax.fori_loop(0, 4, weight_tile, 0)
    reduce.middle()
    lax.fori_loop(4, tiles, weight_tile, 0)
    reduce.end()
    start_middle.wait()
    sums[...] = jnp.zeros_like(sums)

    gather.sent()
    for other in (side, over_x, over_y):
        pl.semaphore_signal(ready, inc=1, device_id={"dp": other}, device_id_type=MESH)

    def body(span):
        change = norm_back_rows(reduce.rows_of(span), middle_grad[span, :], gain[...], sums, span)
        total = cotangent[span, :].astype(F32) + change
        middle_grad[span, :] = total
        hidden_all[me, span, :] = total.astype(BF16)

    each_chunk(rows, body)
    pl.semaphore_wait(ready, 3)
    branch = Gather(None, hidden_all, send_b, recv_b)
    branch.start()
    arrivals = [
        (1, (4,)),
        (2, (0, 1, 2)),
        (3, (3,)),
        (4, (6, 9)),
        (5, (8, 10)),
        (6, (5, 7)),
        (7, (11, 12)),
    ]

    def spread_back(turn, carry):
        for number, numbers in arrivals:
            pl.when(turn == number)(functools.partial(branch.arrive, *numbers))
        block = turn // 2
        near = ((block + 1) // 2) % 2
        far = block // 3
        second = turn % 2
        other = (1 - near) * second + (block // 2) * near
        owner = me + (near * (1 - second) + far) * (over_x - me)
        owner = owner + (near * second + far) * (over_y - me) + other * (side - me)
        mixed_grad[owner] = lax.dot_general(
            hidden_all[owner], w_out[...], NT, preferred_element_type=F32
        ).astype(BF16)
        return carry

    lax.fori_loop(0, 8, spread_back, 0)

    def project_tile(t, carry):
        columns = pl.ds(pl.multiple_of(t * 256, 256), 256)
        proj_sum[:, columns] = lax.dot_general(
            mixed[...],
            hidden_all[:, :, columns].reshape(count, 256),
            TN,
            preferred_element_type=F32,
        ).astype(BF16)
        return carry

    lax.fori_loop(0, tiles, project_tile, 0)
    branch.sent()
    reduce.finish()
    for t in (tiles - 2, tiles - 1):
        store_both(t).wait()
        store_down(t).wait()


def feed(hidden_own, cotangent_all, middle, cotangent, gain, w_both, w_down, mixed, w_out):
    groups, rows, width = cotangent_all.shape
    members = w_both.shape[0]
    dma = pltpu.SemaphoreType.DMA
    units = members * 128
    return pl.pallas_call(
        feed_kernel,
        out_shape=(
            jax.ShapeDtypeStruct((rows, width), F32),
            jax.ShapeDtypeStruct((groups, rows, 2 * LANES), BF16),
            jax.ShapeDtypeStruct((8, width), F32),
            jax.ShapeDtypeStruct((groups, rows, units), BF16),
            jax.ShapeDtypeStruct((members, width, 256), BF16),
            jax.ShapeDtypeStruct((units, width), BF16),
            jax.ShapeDtypeStruct((2 * LANES, width), BF16),
        ),
        in_specs=[anywhere()] * 3 + [on_chip()] * 6,
        out_specs=(on_chip(),) * 4 + (anywhere(),) * 2 + (on_chip(),),
        scratch_shapes=[
            pltpu.VMEM((groups, rows, width), BF16),
            pltpu.VMEM((groups, rows, 2 * units), BF16),
        ]
        + reduce_scratch(rows, width)
        + [
            dma((13,)),
            dma((13,)),
            dma((13,)),
            dma((13,)),
            pltpu.VMEM((2, rows // 2, width), BF16),
            pltpu.VMEM((2, groups, rows, 256), BF16),
            pltpu.VMEM((2, members, 256, 256), BF16),
            pltpu.VMEM((2, units, 256), BF16),
            dma((8,)),
            dma((2,)),
            pltpu.SemaphoreType.REGULAR,
        ],
        compiler_params=remote_params(5, 62 * 1024 * 1024),
        cost_estimate=pl.CostEstimate(flops=0, bytes_accessed=400_000_000, transcendentals=0),
        name="feed",
    )(hidden_own, cotangent_all, middle, cotangent, gain, w_both, w_down, mixed, w_out)


def input_kernel(
    qkv_grad, w_qkv, hidden_all, tokens, middle_grad, gain, sums_two, proj_part, down_part,
    result, heads_part, gains, down_all,
    part, from_side, from_corner, from_near, send, recv, sums,
    arrive, send_h, recv_h, own, plane_sums, column_sums, send_s, recv_s,
    qkv_sum, hidden_tile, tile_sem, send_g, recv_g, local,
):
    me, z = lax.axis_index("dp"), lax.axis_index("mp")
    count = qkv_grad.shape[0]
    tiles = tokens.shape[1] // 256

    def load(t):
        columns = pl.ds(pl.multiple_of(t * 256, 256), 256)
        return pltpu.make_async_copy(
            hidden_all.at[:, :, columns], hidden_tile.at[t % 2], tile_sem.at[t % 2]
        )

    load(0).start()

    def weight_tile(t, carry):
        columns = pl.ds(pl.multiple_of(t * 256, 256), 256)

        @pl.when(t < tiles - 1)
        def _():
            load(t + 1).start()

        load(t).wait()
        qkv_sum[:, columns] = lax.dot_general(
            qkv_grad[...], hidden_tile[t % 2].reshape(count, 256), TN, preferred_element_type=F32
        ).astype(BF16)
        return carry

    greet_all(pltpu.get_barrier_semaphore())
    down = Gather(down_part, down_all, send_g, recv_g, local)
    down.start()
    lax.fori_loop(0, tiles, weight_tile, 0)
    down.pass_on()
    heads = Heads(qkv_sum, arrive, send_h, recv_h, 3)
    heads.start()
    heads_part[3] = proj_part[0]
    reduce = Reduce(qkv_grad, w_qkv, False, part, from_side, from_corner, from_near, send, recv)
    reduce.run()
    sums[...] = jnp.zeros_like(sums)

    def body(span):
        values = tokens[span, :].astype(F32)
        change = norm_back_rows(reduce.rows_of(span), values, gain[...], sums, span)
        result[span, :] = (middle_grad[span, :] + change).astype(BF16)

    each_chunk(result.shape[0], body)
    own[...] = jnp.concatenate(
        [
            jnp.sum(sums[...], axis=0, keepdims=True),
            jnp.sum(sums_two[...], axis=0, keepdims=True),
        ],
        axis=0,
    )
    swaps = swap_all(own, plane_sums, send_s, recv_s)
    for copy in swaps:
        copy.start()
    plane_sums[me] = own[...]
    down.finish()
    for copy in swaps:
        copy.wait()
    found = plane_sums[0]
    for other in range(1, 8):
        found = found + plane_sums[other]
    column_sums[z] = found
    passes = [
        to_mp(
            column_sums.at[z],
            column_sums.at[z],
            send_s.at[6 + step],
            recv_s.at[6 + step],
            lax.rem(z + step, 4),
        )
        for step in range(1, 4)
    ]
    for copy in passes:
        copy.start()
    heads.total(heads_part)
    for copy in passes:
        copy.wait()
    gains[...] = (column_sums[0] + column_sums[1]) + (column_sums[2] + column_sums[3])
    heads.finish_send()
    reduce.finish()


def project_input(
    qkv_grad, w_qkv, hidden_all, tokens, middle_grad, gain, sums_two, proj_part, down_part
):
    rows, width = tokens.shape
    groups = hidden_all.shape[0]
    dma = pltpu.SemaphoreType.DMA
    return pl.pallas_call(
        input_kernel,
        out_shape=(
            jax.ShapeDtypeStruct((rows, width), BF16),
            jax.ShapeDtypeStruct((4, HEAD_DIM, width // 2), BF16),
            jax.ShapeDtypeStruct((2, width), F32),
            jax.ShapeDtypeStruct((groups,) + down_part.shape, BF16),
        ),
        in_specs=[on_chip()] * 2 + [anywhere()] + [on_chip()] * 6,
        out_specs=(on_chip(),) * 3 + (anywhere(),),
        scratch_shapes=reduce_scratch(rows, width)
        + [
            pltpu.VMEM((8, width), F32),
            pltpu.VMEM((4, 3, HEAD_DIM, width // 2), BF16),
            dma((12,)),
            dma((12,)),
            pltpu.VMEM((2, width), F32),
            pltpu.VMEM((8, 2, width), F32),
            pltpu.VMEM((4, 2, width), F32),
            dma((10,)),
            dma((10,)),
            pltpu.VMEM((6 * LANES, width), BF16),
            pltpu.VMEM((2, groups, rows, 256), BF16),
            dma((2,)),
            dma((13,)),
            dma((13,)),
            dma(()),
        ],
        compiler_params=remote_params(6),
        cost_estimate=pl.CostEstimate(flops=0, bytes_accessed=250_000_000, transcendentals=0),
        name="project_input",
    )(qkv_grad, w_qkv, hidden_all, tokens, middle_grad, gain, sums_two, proj_part, down_part)


def units_gather_kernel(both, both_all, send, recv, local):
    pl.semaphore_wait(greet_plane(), 3)
    gather = Gather(both, both_all, send, recv, local)
    gather.start()
    gather.pass_on()
    gather.finish()


def gather_units(part, number):
    groups = lax.axis_size("dp")
    dma = pltpu.SemaphoreType.DMA
    return pl.pallas_call(
        units_gather_kernel,
        out_shape=jax.ShapeDtypeStruct((groups,) + part.shape, BF16),
        in_specs=[on_chip()],
        out_specs=anywhere(),
        scratch_shapes=[dma((13,)), dma((13,)), dma(())],
        compiler_params=remote_params(number),
        cost_estimate=pl.CostEstimate(flops=0, bytes_accessed=100_000_000, transcendentals=0),
        name="gather_units",
    )(part)


def units_kernel(both, gate, upward):
    for d in range(both.shape[0]):
        gate[:, d * 128 : d * 128 + 128] = both[d, :, :128].astype(F32)
        upward[:, d * 128 : d * 128 + 128] = both[d, :, 128:].astype(F32)


def assemble_units(both):
    groups, width, wide = both.shape
    tile = 256
    shape = jax.ShapeDtypeStruct((width, groups * wide // 2), F32)
    spec = pl.BlockSpec((tile, groups * wide // 2), lambda i: (i, 0))
    return pl.pallas_call(
        units_kernel,
        grid=(width // tile,),
        out_shape=(shape, shape),
        in_specs=[pl.BlockSpec((groups, tile, wide), lambda i: (0, i, 0))],
        out_specs=(spec, spec),
        cost_estimate=pl.CostEstimate(flops=0, bytes_accessed=22_000_000, transcendentals=0),
        name="assemble_units",
    )(both)


def heads_kernel(whole, *outs):
    columns = whole.shape[4]
    for kind, out in enumerate(outs):
        for half in range(whole.shape[1]):
            out[:, half * columns : half * columns + columns] = whole[0, half, kind].astype(F32)


def assemble_heads(whole):
    chips, halves, kinds, rows, columns = whole.shape
    shape = jax.ShapeDtypeStruct((chips * rows, halves * columns), F32)
    spec = pl.BlockSpec((rows, halves * columns), lambda c: (c, 0))
    return pl.pallas_call(
        heads_kernel,
        grid=(chips,),
        out_shape=(shape,) * kinds,
        in_specs=[pl.BlockSpec((1, halves, kinds, rows, columns), lambda c: (c, 0, 0, 0, 0))],
        out_specs=(spec,) * kinds,
        cost_estimate=pl.CostEstimate(flops=0, bytes_accessed=20_000_000, transcendentals=0),
        name="assemble_heads",
    )(whole)


def swapped(
    tokens, cotangent, route, lengths, key_mask, norm1_gain, norm2_gain,
    w_query, w_key, w_value, w_out, w_gate, w_up, w_down,
):
    groups = lax.axis_size("dp")
    members = lax.axis_size("mp")
    me = lax.axis_index("dp")
    z = lax.axis_index("mp")
    rows, width = tokens.shape
    bucket = rows // groups
    units = w_down.shape[0] // groups

    target = route // TOK_DEV
    earlier = jnp.arange(rows, dtype=jnp.int32)
    same = (target[:, None] == target[None, :]) & (earlier[None, :] < earlier[:, None])
    send_at = target * bucket + jnp.sum(same.astype(jnp.int32), axis=1)
    sorting = send_at[None, :] == earlier[:, None]
    slots_own = jnp.sum(jnp.where(sorting, (route % rows)[None, :], 0), axis=1)
    sort_hot = sorting.astype(BF16)
    tokens_b = jnp.dot(sort_hot, tokens, preferred_element_type=F32).astype(BF16)
    cotangent_b = jnp.dot(sort_hot, cotangent, preferred_element_type=F32).astype(BF16)

    mask_window = lax.dynamic_slice_in_dim(
        jnp.concatenate([jnp.zeros((WINDOW,), jnp.int32), key_mask]), z * rows, rows + WINDOW
    )
    notes = jnp.concatenate([slots_own, mask_window, lengths[0]])
    notes = jnp.pad(notes, (0, 8 * LANES - notes.shape[0])).reshape(8, LANES)

    normed, _ = norm_rows(tokens_b.astype(F32))
    hidden_own = (normed * norm1_gain).astype(BF16)
    hidden_one, w_qkv, w_proj, notes_all, both_own, down_own = gather_first(
        hidden_own, w_query.T, w_key.T, w_value.T, w_out, w_gate, w_up, w_down, notes
    )
    notes_all = notes_all.reshape(groups, 8 * LANES)
    slots = (
        notes_all[:, :rows].reshape(groups, groups, bucket).transpose(1, 0, 2).reshape(groups, rows)
    )
    flags = notes_all[:, rows : 2 * rows + WINDOW]
    lengths_all = notes_all[:, 2 * rows + WINDOW : 2 * rows + WINDOW + 3]

    w_both = lax.all_gather(both_own, "mp")
    down_all = lax.all_gather(down_own, "mp", axis=0, tiled=True)

    count = groups * rows
    scale = HEAD_DIM ** (-0.5)
    mixed, kept, cotangent_all = attend_ahead(
        lengths_all, hidden_one, w_qkv, slots, flags, cotangent_b, scale
    )
    mixed = mixed.reshape(count, 2 * LANES)
    middle, hidden_two = project_middle(mixed, w_proj, tokens_b, norm2_gain[None])
    middle_grad, mixed_grad, sums_two, activated, both_sum, down_sum, proj_sum = feed(
        hidden_two,
        cotangent_all,
        middle,
        cotangent_b,
        norm2_gain[None],
        w_both,
        down_all,
        mixed,
        w_proj,
    )
    down_part = lax.psum_scatter(down_sum, "mp", scatter_dimension=0, tiled=True)
    both_part = lax.psum_scatter(both_sum, "mp", scatter_dimension=0)

    qkv_grad, output_rows, proj_part = attend_back(
        lengths_all,
        kept,
        mixed_grad.reshape(groups, groups, bucket, 2 * LANES),
        slots,
        flags,
        activated.reshape(count, units * members),
        down_all,
        middle,
        proj_sum,
        scale,
    )
    qkv_grad = qkv_grad.reshape(count, 6 * LANES)
    input_rows, heads_part, gain_sums, down_whole = project_input(
        qkv_grad,
        w_qkv,
        hidden_one,
        tokens_b,
        middle_grad,
        norm1_gain[None],
        sums_two,
        proj_part,
        down_part,
    )
    both_part, heads_part = lax.optimization_barrier((both_part, heads_part))
    heads_whole = lax.all_gather(heads_part.reshape(4 * HEAD_DIM, width // 2), "dp")
    both_whole = gather_units(both_part, 7)
    gate_grad, up_grad = assemble_units(both_whole)
    down_grad = down_whole.astype(F32).reshape(groups * units, width)
    query_grad, key_grad, value_grad, proj_grad = assemble_heads(
        heads_whole.reshape(groups // 2, 2, 4, HEAD_DIM, width // 2)
    )

    unsort = (((0,), (0,)), ((), ()))
    return (
        lax.dot_general(sort_hot, output_rows, unsort, preferred_element_type=F32).astype(BF16),
        lax.dot_general(sort_hot, input_rows, unsort, preferred_element_type=F32).astype(BF16),
        gain_sums[0],
        gain_sums[1],
        query_grad.T,
        key_grad.T,
        value_grad.T,
        proj_grad,
        gate_grad,
        up_grad,
        down_grad,
    )


def solution(mesh):
    in_specs = (
        P(("dp", "mp"), None),
        P(("dp", "mp"), None),
        P(("dp", "mp")),
        P("dp", None),
        P("dp"),
        P(),
        P(),
        P(None, "mp"),
        P(None, "mp"),
        P(None, "mp"),
        P("mp", None),
        P(None, "mp"),
        P(None, "mp"),
        P("mp", None),
    )
    out_specs = (
        P(("dp", "mp"), None),
        P(("dp", "mp"), None),
        P(),
        P(),
        P(None, "mp"),
        P(None, "mp"),
        P(None, "mp"),
        P("mp", None),
        P(None, "mp"),
        P(None, "mp"),
        P("mp", None),
    )
    body = swapped if (mesh.shape["dp"], mesh.shape["mp"]) == (8, 4) else local
    return jax.shard_map(body, mesh=mesh, in_specs=in_specs, out_specs=out_specs, check_vma=False)
```

```python
import functools

import jax
import jax.numpy as jnp
from jax import lax
from jax.experimental import pallas as pl
from jax.experimental.pallas import tpu as pltpu
from jax.sharding import PartitionSpec as P

HEAD_DIM = 112
WINDOW = 64
TOK_DEV = 1536


EPSILON = 1e-05
MASKED = 1e30


def norm_rows(values):
    inverse = lax.rsqrt(jnp.mean(values * values, axis=-1, keepdims=True) + EPSILON)
    return (values * inverse, inverse)


def norm_back(gradient, normed, inverse, norm_gain):
    scaled = gradient * norm_gain
    result = inverse * (scaled - normed * jnp.mean(scaled * normed, axis=-1, keepdims=True))
    return (result, jnp.sum(gradient * normed, axis=0))


def padded(values, filler):
    front = jnp.full((WINDOW,) + values.shape[1:], filler, values.dtype)
    return jnp.concatenate([front, values], axis=0)


def block_scores(query_block, key_block, query_seg, key_seg, key_flag, first_row, score_scale):
    query_pos = first_row + jnp.arange(query_block.shape[0], dtype=jnp.int32)
    key_pos = first_row - WINDOW + jnp.arange(key_block.shape[0], dtype=jnp.int32)
    distance = query_pos[:, None] - key_pos[None, :]
    allowed = (distance >= 0) & (distance < WINDOW) & (query_seg[:, None] == key_seg[None, :])
    allowed = allowed & ((key_flag[None, :] == 1) | (distance == 0))
    raw_scores = (
        jnp.einsum("qhd,khd->hqk", query_block, key_block, preferred_element_type=jnp.float32)
        * score_scale
    )
    return jnp.where(allowed[None], raw_scores, -MASKED)


def block_inputs(query, key_pad, value_pad, segment, seg_pad, live_pad, first_row, block_rows):
    key_span = block_rows + WINDOW
    return (
        lax.dynamic_slice_in_dim(query, first_row, block_rows, 0),
        lax.dynamic_slice_in_dim(key_pad, first_row, key_span, 0),
        lax.dynamic_slice_in_dim(value_pad, first_row, key_span, 0),
        lax.dynamic_slice_in_dim(segment, first_row, block_rows, 0),
        lax.dynamic_slice_in_dim(seg_pad, first_row, key_span, 0),
        lax.dynamic_slice_in_dim(live_pad, first_row, key_span, 0),
    )


def attend_forward(query, key_all, value_all, segment, key_live):
    token_count, head_count, head_width = query.shape
    block_rows = min(512, token_count)
    score_scale = head_width ** (-0.5)
    key_pad = padded(key_all, 0.0)
    value_pad = padded(value_all, 0.0)
    seg_pad = padded(segment, -1)
    live_pad = padded(key_live, 0)

    def one_block(running, block_index):
        first_row = block_index * block_rows
        query_block, key_block, value_block, query_seg, key_seg, key_flag = block_inputs(
            query, key_pad, value_pad, segment, seg_pad, live_pad, first_row, block_rows
        )
        scores = block_scores(
            query_block, key_block, query_seg, key_seg, key_flag, first_row, score_scale
        )
        row_max = jnp.max(scores, axis=-1, keepdims=True)
        weights = jnp.exp(scores - row_max)
        denominator = jnp.sum(weights, axis=-1, keepdims=True)
        chances = (weights / denominator).astype(jnp.bfloat16)
        mixed = jnp.einsum("hqk,khd->qhd", chances, value_block, preferred_element_type=jnp.float32)
        return (
            running,
            (mixed.astype(jnp.bfloat16), row_max[..., 0] + jnp.log(denominator[..., 0])),
        )

    _, (mixed, logsum) = lax.scan(
        one_block, jnp.zeros((), jnp.int32), jnp.arange(token_count // block_rows, dtype=jnp.int32)
    )
    return (mixed.reshape(token_count, head_count * head_width), logsum)


def attend_backward(query, key_all, value_all, segment, key_live, logsum, mixed_grad):
    token_count, head_count, head_width = query.shape
    block_rows = min(512, token_count)
    key_span = block_rows + WINDOW
    score_scale = head_width ** (-0.5)
    key_pad = padded(key_all, 0.0)
    value_pad = padded(value_all, 0.0)
    seg_pad = padded(segment, -1)
    live_pad = padded(key_live, 0)

    def one_block(running, inputs):
        key_grad, value_grad = running
        block_index, block_logsum = inputs
        first_row = block_index * block_rows
        query_block, key_block, value_block, query_seg, key_seg, key_flag = block_inputs(
            query, key_pad, value_pad, segment, seg_pad, live_pad, first_row, block_rows
        )
        grad_block = lax.dynamic_slice_in_dim(mixed_grad, first_row, block_rows, 0)
        scores = block_scores(
            query_block, key_block, query_seg, key_seg, key_flag, first_row, score_scale
        )
        chances = jnp.exp(scores - block_logsum[..., None])
        chance_grad = jnp.einsum(
            "qhd,khd->hqk", grad_block, value_block, preferred_element_type=jnp.float32
        )
        row_dot = jnp.sum(chances * chance_grad, axis=-1, keepdims=True)
        score_grad = (chances * (chance_grad - row_dot)).astype(jnp.bfloat16)
        query_grad = (
            jnp.einsum("hqk,khd->qhd", score_grad, key_block, preferred_element_type=jnp.float32)
            * score_scale
        )
        key_part = (
            jnp.einsum("hqk,qhd->khd", score_grad, query_block, preferred_element_type=jnp.float32)
            * score_scale
        )
        value_part = jnp.einsum(
            "hqk,qhd->khd",
            chances.astype(jnp.bfloat16),
            grad_block,
            preferred_element_type=jnp.float32,
        )
        key_grad = lax.dynamic_update_slice_in_dim(
            key_grad,
            lax.dynamic_slice_in_dim(key_grad, first_row, key_span, 0) + key_part,
            first_row,
            0,
        )
        value_grad = lax.dynamic_update_slice_in_dim(
            value_grad,
            lax.dynamic_slice_in_dim(value_grad, first_row, key_span, 0) + value_part,
            first_row,
            0,
        )
        return ((key_grad, value_grad), query_grad)

    empty_grad = jnp.zeros((token_count + WINDOW, head_count, head_width), jnp.float32)
    (key_grad, value_grad), query_grad = lax.scan(
        one_block,
        (empty_grad, empty_grad),
        (jnp.arange(token_count // block_rows, dtype=jnp.int32), logsum),
    )
    flat_width = head_count * head_width
    return (
        query_grad.reshape(token_count, flat_width).astype(jnp.bfloat16),
        key_grad[WINDOW:].reshape(token_count, flat_width).astype(jnp.bfloat16),
        value_grad[WINDOW:].reshape(token_count, flat_width).astype(jnp.bfloat16),
    )


def local(
    tokens,
    cotangent,
    route,
    lengths,
    key_mask,
    norm1_gain,
    norm2_gain,
    w_query,
    w_key,
    w_value,
    w_out,
    w_gate,
    w_up,
    w_down,
):
    groups = lax.axis_size("dp")
    members = lax.axis_size("mp")
    member = lax.axis_index("mp")
    local_rows = tokens.shape[0]
    group_rows = local_rows * members
    bucket = local_rows // groups
    target = route // TOK_DEV
    chosen = (target[:, None] == jnp.arange(groups, dtype=jnp.int32)[None, :]).astype(jnp.int32)
    ranking = jnp.sum((jnp.cumsum(chosen, axis=0) - chosen) * chosen, axis=1)
    send_at = target * bucket + ranking
    arrival, arrival_grad, arrival_slot = (
        lax.all_to_all(
            jnp.zeros_like(tokens).at[send_at].set(tokens),
            "dp",
            split_axis=0,
            concat_axis=0,
            tiled=True,
        ),
        lax.all_to_all(
            jnp.zeros_like(cotangent).at[send_at].set(cotangent),
            "dp",
            split_axis=0,
            concat_axis=0,
            tiled=True,
        ),
        lax.all_to_all(
            jnp.zeros_like(route).at[send_at].set(route % local_rows),
            "dp",
            split_axis=0,
            concat_axis=0,
            tiled=True,
        ),
    )
    token_rows = jnp.zeros_like(arrival).at[arrival_slot].set(arrival)
    grad_rows = jnp.zeros_like(arrival_grad).at[arrival_slot].set(arrival_grad)
    seq_ends = jnp.cumsum(lengths[0])
    positions = jnp.arange(group_rows, dtype=jnp.int32)
    segment = jnp.sum((positions[:, None] >= seq_ends[None, :]).astype(jnp.int32), axis=1)
    input_rows = token_rows.astype(jnp.float32)
    normed_one, inverse_one = norm_rows(input_rows)
    leading_all, grad_all = (
        lax.all_gather(token_rows, "mp", axis=0, tiled=True),
        lax.all_gather(grad_rows, "mp", axis=0, tiled=True),
    )
    input_all = leading_all.astype(jnp.float32)
    normed_all, _ = norm_rows(input_all)
    hidden_one = (normed_all * norm1_gain).astype(jnp.bfloat16)
    head_count = w_query.shape[1] // HEAD_DIM
    query = jnp.dot(hidden_one, w_query, preferred_element_type=jnp.float32).astype(jnp.bfloat16)
    keys = jnp.dot(hidden_one, w_key, preferred_element_type=jnp.float32).astype(jnp.bfloat16)
    values = jnp.dot(hidden_one, w_value, preferred_element_type=jnp.float32).astype(jnp.bfloat16)
    query_heads = query.reshape(group_rows, head_count, HEAD_DIM)
    key_heads = keys.reshape(group_rows, head_count, HEAD_DIM)
    value_heads = values.reshape(group_rows, head_count, HEAD_DIM)
    mixed_flat, logsum = attend_forward(query_heads, key_heads, value_heads, segment, key_mask)
    attention_all = lax.psum(jnp.dot(mixed_flat, w_out, preferred_element_type=jnp.float32), "mp")
    middle_all = input_all + attention_all
    middle_rows = lax.dynamic_slice_in_dim(middle_all, member * local_rows, local_rows, 0)
    normed_mid, _ = norm_rows(middle_all)
    hidden_two = (normed_mid * norm2_gain).astype(jnp.bfloat16)
    normed_two, inverse_two = norm_rows(middle_rows)
    gate_value = jnp.dot(hidden_two, w_gate, preferred_element_type=jnp.float32)
    upward = jnp.dot(hidden_two, w_up, preferred_element_type=jnp.float32)
    sigmoid = jax.nn.sigmoid(gate_value)
    activated = (gate_value * sigmoid * upward).astype(jnp.bfloat16)
    out_rows = middle_rows + lax.psum_scatter(
        jnp.dot(activated, w_down, preferred_element_type=jnp.float32).astype(jnp.bfloat16),
        "mp",
        scatter_dimension=0,
        tiled=True,
    ).astype(jnp.float32)
    activated_grad = jnp.einsum("td,fd->tf", grad_all, w_down, preferred_element_type=jnp.float32)
    gate_grad = (activated_grad * upward * sigmoid * (1.0 + gate_value * (1.0 - sigmoid))).astype(
        jnp.bfloat16
    )
    upward_grad = (activated_grad * gate_value * sigmoid).astype(jnp.bfloat16)
    down_sum = jnp.einsum("tf,td->fd", activated, grad_all, preferred_element_type=jnp.float32)
    gate_sum = jnp.einsum("td,tf->df", hidden_two, gate_grad, preferred_element_type=jnp.float32)
    upward_sum = jnp.einsum(
        "td,tf->df", hidden_two, upward_grad, preferred_element_type=jnp.float32
    )
    hidden_two_grad = lax.psum_scatter(
        jnp.einsum("tf,df->td", gate_grad, w_gate, preferred_element_type=jnp.float32)
        + jnp.einsum("tf,df->td", upward_grad, w_up, preferred_element_type=jnp.float32),
        "mp",
        scatter_dimension=0,
        tiled=True,
    )
    norm_part_two, gain_two_grad = norm_back(hidden_two_grad, normed_two, inverse_two, norm2_gain)
    middle_grad = grad_rows.astype(jnp.float32) + norm_part_two
    branch_all = lax.all_gather(middle_grad.astype(jnp.bfloat16), "mp", axis=0, tiled=True)
    output_sum = jnp.einsum("tc,td->cd", mixed_flat, branch_all, preferred_element_type=jnp.float32)
    mixed_grad = jnp.einsum(
        "td,cd->tc", branch_all, w_out, preferred_element_type=jnp.float32
    ).astype(jnp.bfloat16)
    query_grad, key_grad, value_grad = attend_backward(
        query_heads,
        key_heads,
        value_heads,
        segment,
        key_mask,
        logsum,
        mixed_grad.reshape(group_rows, head_count, HEAD_DIM),
    )
    query_sum = jnp.einsum("td,tc->dc", hidden_one, query_grad, preferred_element_type=jnp.float32)
    key_sum = jnp.einsum("td,tc->dc", hidden_one, key_grad, preferred_element_type=jnp.float32)
    value_sum = jnp.einsum("td,tc->dc", hidden_one, value_grad, preferred_element_type=jnp.float32)
    hidden_one_grad = lax.psum_scatter(
        (
            jnp.einsum("tc,dc->td", query_grad, w_query, preferred_element_type=jnp.float32)
            + jnp.einsum("tc,dc->td", key_grad, w_key, preferred_element_type=jnp.float32)
            + jnp.einsum("tc,dc->td", value_grad, w_value, preferred_element_type=jnp.float32)
        ).astype(jnp.bfloat16),
        "mp",
        scatter_dimension=0,
        tiled=True,
    ).astype(jnp.float32)
    norm_part_one, gain_one_grad = norm_back(hidden_one_grad, normed_one, inverse_one, norm1_gain)
    input_grad = middle_grad + norm_part_one
    gain_one_sum, gain_two_sum = lax.psum((gain_one_grad, gain_two_grad), ("dp", "mp"))
    weight_sums = (
        lax.psum(query_sum.astype(jnp.bfloat16), "dp").astype(jnp.float32),
        lax.psum(key_sum.astype(jnp.bfloat16), "dp").astype(jnp.float32),
        lax.psum(value_sum.astype(jnp.bfloat16), "dp").astype(jnp.float32),
        lax.psum(output_sum.astype(jnp.bfloat16), "dp").astype(jnp.float32),
        lax.psum(gate_sum.astype(jnp.bfloat16), "dp").astype(jnp.float32),
        lax.psum(upward_sum.astype(jnp.bfloat16), "dp").astype(jnp.float32),
        lax.psum(down_sum.astype(jnp.bfloat16), "dp").astype(jnp.float32),
    )
    back_out, back_grad = (
        lax.all_to_all(
            out_rows.astype(jnp.bfloat16)[arrival_slot],
            "dp",
            split_axis=0,
            concat_axis=0,
            tiled=True,
        ),
        lax.all_to_all(
            input_grad.astype(jnp.bfloat16)[arrival_slot],
            "dp",
            split_axis=0,
            concat_axis=0,
            tiled=True,
        ),
    )
    return (
        back_out[send_at],
        back_grad[send_at],
        gain_one_sum,
        gain_two_sum,
        weight_sums[0],
        weight_sums[1],
        weight_sums[2],
        weight_sums[3],
        weight_sums[4],
        weight_sums[5],
        weight_sums[6],
    )


MESH = pl.DeviceIdType.MESH
LANES = 128
F32 = jnp.float32
BF16 = jnp.bfloat16
VMEM_LIMIT = 56 * 1024 * 1024


def plane():
    me = lax.axis_index("dp")
    side = me + 1 - 2 * lax.rem(me, 2)
    over_x = me + 2 - 4 * lax.rem(lax.div(me, 2), 2)
    over_y = me + 4 - 8 * lax.rem(lax.div(me, 4), 2)
    corner = over_x + 4 - 8 * lax.rem(lax.div(over_x, 4), 2)
    return (me, side, over_x, over_y, corner)


def to_dp(source, target, send_sem, recv_sem, index):
    return pltpu.make_async_remote_copy(
        src_ref=source,
        dst_ref=target,
        send_sem=send_sem,
        recv_sem=recv_sem,
        device_id={"dp": index},
        device_id_type=MESH,
    )


def to_mp(source, target, send_sem, recv_sem, index):
    return pltpu.make_async_remote_copy(
        src_ref=source,
        dst_ref=target,
        send_sem=send_sem,
        recv_sem=recv_sem,
        device_id={"mp": index},
        device_id_type=MESH,
    )


def greet_plane():
    _, side, over_x, over_y, _ = plane()
    barrier = pltpu.get_barrier_semaphore()
    for other in (side, over_x, over_y):
        pl.semaphore_signal(barrier, inc=1, device_id={"dp": other}, device_id_type=MESH)
    return barrier


def owner_at(turn):
    me, side, over_x, over_y, _ = plane()
    block = turn // 2
    near = ((block + 1) // 2) % 2
    far = block // 3
    second = turn % 2
    other = (1 - near) * second + (block // 2) * near
    owner = me + (near * (1 - second) + far) * (over_x - me)
    return owner + (near * second + far) * (over_y - me) + other * (side - me)


ARRIVALS = (
    (1, (4,)),
    (2, (0, 1, 2)),
    (3, (3,)),
    (4, (6, 9)),
    (5, (8, 10)),
    (6, (5, 7)),
    (7, (11, 12)),
)


class Gather:
    AFTER = {0: (5, 6), 1: (7, 8), 2: (9,), 3: (10,), 5: (11,), 7: (12,)}

    def __init__(self, own, out, send, recv, local=None):
        me, side, over_x, over_y, corner = plane()
        half = out.shape[1] // 2
        low, high = pl.ds(0, half), pl.ds(half, half)
        self.keep = None if own is None else pltpu.make_async_copy(own, out.at[me], local)
        own = out.at[me] if own is None else own

        def hop(number, source, target, index):
            return to_dp(source, target, send.at[number], recv.at[number], index)

        def onward(number, owner, part, index):
            place = out.at[owner, part]
            return hop(number, place, place, index)

        self.copies = [
            hop(0, own.at[low], out.at[me, low], over_x),
            hop(1, own.at[high], out.at[me, high], over_y),
            hop(2, own.at[high], out.at[me, high], over_x),
            hop(3, own.at[low], out.at[me, low], over_y),
            hop(4, own, out.at[me], side),
            onward(5, over_x, low, over_y),
            onward(6, over_x, low, side),
            onward(7, over_y, high, over_x),
            onward(8, over_y, high, side),
            onward(9, over_x, high, side),
            onward(10, over_y, low, side),
            onward(11, corner, low, side),
            onward(12, corner, high, side),
        ]

    def start(self):
        for number in range(5):
            self.copies[number].start()
        if self.keep is not None:
            self.keep.start()

    def arrive(self, *numbers):
        for number in numbers:
            self.copies[number].wait_recv()
            for later in self.AFTER.get(number, ()):
                self.copies[later].start()

    def pass_on(self):
        self.arrive(0, 1, 2, 3)

    def sent(self):
        for copy in self.copies:
            copy.wait_send()
        if self.keep is not None:
            self.keep.wait()

    def finish(self):
        self.arrive(5, 7, 4, 6, 8, 9, 10, 11, 12)
        self.sent()


def greet_all(barrier):
    me, z = lax.axis_index("dp"), lax.axis_index("mp")
    for step in range(1, 8):
        pl.semaphore_signal(
            barrier, inc=1, device_id={"dp": lax.rem(me + step, 8)}, device_id_type=MESH
        )
    core = lax.rem(me, 2)
    for step in range(1, 4):
        for other in (me, me + 1 - 2 * core):
            pl.semaphore_signal(
                barrier,
                inc=1,
                device_id={"dp": other, "mp": lax.rem(z + step, 4)},
                device_id_type=MESH,
            )
    pl.semaphore_wait(barrier, 13)


def swap_all(source, target, send, recv):
    me = lax.axis_index("dp")
    return [
        to_dp(source, target.at[me], send.at[step - 1], recv.at[step - 1], lax.rem(me + step, 8))
        for step in range(1, 8)
    ]


class Spread:
    def __init__(self, share, w_qkv, w_out, send, recv, local):
        me, z = lax.axis_index("dp"), lax.axis_index("mp")
        core = lax.rem(me, 2)
        self.place = z + core * (3 - 2 * z)
        self.send, self.recv, self.local = send, recv, local
        self.shares = [share.at[0], share.at[1], share.at[2], share.at[3]]
        self.slots = (core, 1 - core)
        self.core = core
        self.w_qkv, self.w_out = w_qkv, w_out

    def target(self, which, piece):
        slot = self.slots[which]
        block = slot if piece == 3 else 2 * piece + slot
        rows = pl.ds(pl.multiple_of(block * LANES, LANES), HEAD_DIM)
        return (self.w_out if piece == 3 else self.w_qkv).at[rows]

    def hop(self, which, piece, number, place, own):
        source = self.shares[piece] if own else self.target(which, piece)
        z = place + self.core * (3 - 2 * place)
        return to_mp(
            source,
            self.target(which, piece),
            self.send.at[number * 4 + piece],
            self.recv.at[which * 4 + piece],
            z,
        )

    def keep(self, which, piece):
        return pltpu.make_async_copy(
            self.shares[piece], self.target(which, piece), self.local.at[piece]
        )

    def start(self):
        @pl.when(self.place == 0)
        def _():
            for piece in range(4):
                self.hop(0, piece, 0, 1, True).start()
                self.keep(0, piece).start()

        @pl.when(self.place == 1)
        def _():
            for piece in range(4):
                self.hop(1, piece, 0, 0, True).start()
                self.hop(1, piece, 1, 2, True).start()
                self.keep(1, piece).start()

    def pass_on(self):
        @pl.when(self.place == 1)
        def _():
            for piece in range(4):
                self.hop(0, piece, 2, 2, False).wait_recv()
                self.hop(0, piece, 2, 2, False).start()

        @pl.when(self.place == 2)
        def _():
            for piece in range(4):
                for which in (1, 0):
                    self.hop(which, piece, which, 3, False).wait_recv()
                    self.hop(which, piece, which, 3, False).start()

    def finish(self):
        @pl.when(self.place == 0)
        def _():
            for piece in range(4):
                self.hop(1, piece, 0, 1, False).wait_recv()
                self.hop(0, piece, 0, 1, True).wait_send()
                self.keep(0, piece).wait()

        @pl.when(self.place == 1)
        def _():
            for piece in range(4):
                self.hop(1, piece, 0, 0, True).wait_send()
                self.hop(1, piece, 1, 2, True).wait_send()
                self.hop(0, piece, 2, 2, False).wait_send()
                self.keep(1, piece).wait()

        @pl.when(self.place == 2)
        def _():
            for piece in range(4):
                for which in (1, 0):
                    self.hop(which, piece, which, 3, False).wait_send()

        @pl.when(self.place == 3)
        def _():
            for piece in range(4):
                for which in (1, 0):
                    self.hop(which, piece, which, 3, False).wait_recv()


def first_kernel(
    hidden, query, keys, values, project, gate, upward, down, notes,
    hidden_all, w_qkv, w_out, notes_all, both_own, down_own,
    share, none, send_a, recv_a, send_w, recv_w, send_n, recv_n, local,
):
    me = lax.axis_index("dp")
    head = pl.ds(pl.multiple_of(lax.div(me, 2) * HEAD_DIM, 16), HEAD_DIM)
    loads = [
        pltpu.make_async_copy(source.at[head], share.at[piece], local.at[piece])
        for piece, source in enumerate((query, keys, values, project))
    ]
    units = pl.ds(pl.multiple_of(me * LANES, LANES), LANES)
    loads += [
        pltpu.make_async_copy(gate.at[:, units], both_own.at[:, pl.ds(0, LANES)], local.at[14]),
        pltpu.make_async_copy(upward.at[:, units], both_own.at[:, pl.ds(LANES, LANES)], local.at[15]),
        pltpu.make_async_copy(down.at[units], down_own, local.at[16]),
    ]
    for copy in loads:
        copy.start()
    none[...] = jnp.zeros_like(none)
    greet_all(pltpu.get_barrier_semaphore())
    gather = Gather(hidden, hidden_all, send_a, recv_a, local.at[4])
    gather.start()
    swaps = swap_all(notes, notes_all, send_n, recv_n)
    for copy in swaps:
        copy.start()
    keep = pltpu.make_async_copy(notes, notes_all.at[me], local.at[5])
    keep.start()
    pads = [
        pltpu.make_async_copy(
            none, weight.at[pl.ds(block * LANES + HEAD_DIM, LANES - HEAD_DIM)], local.at[6 + number]
        )
        for number, (weight, block) in enumerate(
            [(w_qkv, block) for block in range(6)] + [(w_out, block) for block in range(2)]
        )
    ]
    for copy in pads:
        copy.start()
    for copy in loads[:4]:
        copy.wait()
    spread = Spread(share, w_qkv, w_out, send_w, recv_w, local)
    spread.start()
    spread.pass_on()
    gather.pass_on()
    gather.finish()
    spread.finish()
    for copy in swaps:
        copy.wait()
    for copy in pads + loads[4:]:
        copy.wait()
    keep.wait()


def anywhere():
    return pl.BlockSpec(memory_space=pl.ANY)


def on_chip():
    return pl.BlockSpec(memory_space=pltpu.VMEM)


def in_scalar():
    return pl.BlockSpec(memory_space=pltpu.SMEM)


def remote_params(number, limit=VMEM_LIMIT):
    return pltpu.CompilerParams(
        collective_id=number, has_side_effects=True, vmem_limit_bytes=limit
    )


def gather_first(hidden, query, keys, values, project, gate, upward, down, notes):
    rows, width = hidden.shape
    groups = lax.axis_size("dp")
    dma = pltpu.SemaphoreType.DMA
    return pl.pallas_call(
        first_kernel,
        out_shape=(
            jax.ShapeDtypeStruct((groups, rows, width), BF16),
            jax.ShapeDtypeStruct((6 * LANES, width), BF16),
            jax.ShapeDtypeStruct((2 * LANES, width), BF16),
            jax.ShapeDtypeStruct((groups,) + notes.shape, notes.dtype),
            jax.ShapeDtypeStruct((width, 2 * LANES), BF16),
            jax.ShapeDtypeStruct((LANES, width), BF16),
        ),
        in_specs=[on_chip()] + [anywhere()] * 7 + [on_chip()],
        out_specs=(anywhere(),) * 4 + (on_chip(),) * 2,
        scratch_shapes=[
            pltpu.VMEM((4, HEAD_DIM, width), BF16),
            pltpu.VMEM((LANES - HEAD_DIM, width), BF16),
            dma((13,)), dma((13,)), dma((12,)), dma((8,)), dma((7,)), dma((7,)), dma((17,)),
        ],
        compiler_params=remote_params(1),
        cost_estimate=pl.CostEstimate(flops=0, bytes_accessed=200_000_000, transcendentals=0),
        name="gather_first",
    )(hidden, query, keys, values, project, gate, upward, down, notes)


def one_hot(slots, k, size):
    row = slots[pl.ds(k, 1), :]
    place = lax.broadcasted_iota(jnp.int32, (size, size), 0)
    return (place == row).astype(BF16)


def block_mask(lengths, flags, k, block, z, rows):
    position = rows * z + block * 128 + lax.broadcasted_iota(jnp.int32, (128, 1), 0)
    first_end = lengths[k, 0]
    second_end = first_end + lengths[k, 1]
    begin = jnp.where(position >= first_end, first_end, 0)
    begin = jnp.where(position >= second_end, second_end, begin)
    column = lax.broadcasted_iota(jnp.int32, (128, 192), 1)
    distance = 64 + lax.broadcasted_iota(jnp.int32, (128, 192), 0) - column
    key_position = rows * z + block * 128 - 64 + column
    live = flags[pl.ds(k, 1), block * 128 : block * 128 + 192]
    allowed = (distance >= 0) & (distance < WINDOW) & (key_position >= begin)
    return allowed & ((live == 1) | (distance == 0))


NT = (((1,), (1,)), ((), ()))
TN = (((0,), (0,)), ((), ()))


def forward_kernel(
    lengths, hidden_all, w_qkv, slots, flags, cotangent, mixed, kept, cotangent_all,
    qkv, shard, shard_sem, send, recv, send_g, recv_g, local, *, scale, groups, rows
):
    z = lax.axis_index("mp")
    members = lax.axis_size("mp")
    barrier = greet_plane()

    @pl.when(z > 0)
    def _():
        pl.semaphore_signal(barrier, inc=1, device_id={"mp": z - 1}, device_id_type=MESH)

    @pl.when(z < members - 1)
    def _():
        pl.semaphore_wait(barrier, 4)

    @pl.when(z == members - 1)
    def _():
        pl.semaphore_wait(barrier, 3)

    gather = Gather(cotangent, cotangent_all, send_g, recv_g, local)
    gather.start()

    def load(g):
        slot = lax.rem(g, 2)
        return pltpu.make_async_copy(hidden_all.at[g], shard.at[slot], shard_sem.at[slot])

    load(0).start()

    def multiply(g, carry):
        @pl.when(g < groups - 1)
        def _():
            load(g + 1).start()

        load(g).wait()
        product = lax.dot_general(
            shard[lax.rem(g, 2)], w_qkv[...], NT, preferred_element_type=F32
        ).astype(BF16)
        qkv[g] = product.reshape(groups, rows // groups, 768)
        return carry

    lax.fori_loop(0, groups, multiply, 0)

    def halo(k, other):
        return to_mp(
            kept.at[k, pl.ds(rows, 64), pl.ds(256, 512)],
            kept.at[k, pl.ds(0, 64), pl.ds(256, 512)],
            send.at[k],
            recv.at[k],
            other,
        )

    def order(k, carry):
        hot = one_hot(slots, k, rows)
        given = qkv[:, pl.ds(k, 1)].reshape(rows, 768)
        kept[k, pl.ds(64, rows), :] = jnp.dot(hot, given, preferred_element_type=F32).astype(BF16)
        kept[k, pl.ds(0, 64), pl.ds(0, 256)] = jnp.zeros((64, 256), BF16)

        @pl.when(z < members - 1)
        def _():
            halo(k, z + 1).start()

        @pl.when(z == 0)
        def _():
            kept[k, pl.ds(0, 64), pl.ds(256, 512)] = jnp.zeros((64, 512), BF16)

        return carry

    lax.fori_loop(0, groups, order, 0)

    def attend(k, carry):
        @pl.when(z > 0)
        def _():
            halo(k, z).wait_recv()

        hot = one_hot(slots, k, rows)
        found = []
        for block in range(rows // 128):
            allowed = block_mask(lengths, flags, k, block, z, rows)
            heads = []
            for head in range(2):
                query = kept[k, pl.ds(64 + block * 128, 128), pl.ds(head * 128, 128)]
                keys = kept[k, pl.ds(block * 128, 192), pl.ds(256 + head * 128, 128)]
                values = kept[k, pl.ds(block * 128, 192), pl.ds(512 + head * 128, 128)]
                scores = lax.dot_general(query, keys, NT, preferred_element_type=F32) * scale
                scores = jnp.where(allowed, scores, -MASKED)
                weights = jnp.exp(scores - jnp.max(scores, axis=-1, keepdims=True))
                total = jnp.sum(weights, axis=-1, keepdims=True)
                chances = (weights / total).astype(BF16)
                heads.append(jnp.dot(chances, values, preferred_element_type=F32).astype(BF16))
            found.append(jnp.concatenate(heads, axis=1))
        ordered = jnp.concatenate(found, axis=0)
        back = lax.dot_general(hot, ordered, TN, preferred_element_type=F32).astype(BF16)
        mixed[:, pl.ds(k, 1)] = back.reshape(groups, 1, rows // groups, 256)
        return carry

    lax.fori_loop(0, groups // 4, attend, 0)
    gather.pass_on()
    lax.fori_loop(groups // 4, groups, attend, 0)
    gather.finish()

    @pl.when(z < members - 1)
    def _():
        def done(k, carry):
            halo(k, z + 1).wait_send()
            return carry

        lax.fori_loop(0, groups, done, 0)


def attend_ahead(lengths, hidden_all, w_qkv, slots, flags, cotangent, scale):
    groups, rows, width = hidden_all.shape
    dma = pltpu.SemaphoreType.DMA
    return pl.pallas_call(
        functools.partial(forward_kernel, scale=scale, groups=groups, rows=rows),
        out_shape=(
            jax.ShapeDtypeStruct((groups, groups, rows // groups, 256), BF16),
            jax.ShapeDtypeStruct((groups, rows + 64, 768), BF16),
            jax.ShapeDtypeStruct((groups,) + cotangent.shape, BF16),
        ),
        in_specs=[in_scalar(), anywhere()] + [on_chip()] * 4,
        out_specs=(on_chip(), on_chip(), anywhere()),
        scratch_shapes=[
            pltpu.VMEM((groups, groups, rows // groups, 768), BF16),
            pltpu.VMEM((2, rows, width), BF16),
            dma((2,)),
            dma((groups,)),
            dma((groups,)),
            dma((13,)),
            dma((13,)),
            dma(()),
        ],
        compiler_params=remote_params(2),
        cost_estimate=pl.CostEstimate(flops=0, bytes_accessed=200_000_000, transcendentals=0),
        name="attend_ahead",
    )(lengths, hidden_all, w_qkv, slots, flags, cotangent)


CHUNK = 32


def each_chunk(rows, body, chunk=CHUNK):
    def step(i, carry):
        body(pl.ds(pl.multiple_of(i * chunk, chunk), chunk))
        return carry

    lax.fori_loop(0, rows // chunk, step, 0)


class Reduce:
    COUNT = 10

    def __init__(self, left, right, across, part, from_side, from_corner, from_near, send, recv):
        self.left, self.right, self.across, self.part = left, right, across, part
        self.from_side, self.from_corner, self.from_near = from_side, from_corner, from_near
        self.send, self.recv = send, recv
        self.rows = part.shape[1]

    def product(self, owner, slot):
        rows, width = self.rows, self.part.shape[2]
        picked = pl.ds(pl.multiple_of(owner * rows, rows), rows)

        def tile(t, carry):
            columns = pl.ds(pl.multiple_of(t * 256, 256), 256)
            if self.across:
                value = lax.dot_general(
                    self.left[picked, :], self.right[columns, :], NT, preferred_element_type=F32
                )
            else:
                value = jnp.dot(
                    self.left[picked, :], self.right[:, columns], preferred_element_type=F32
                )
            self.part[slot, :, columns] = value.astype(BF16)
            return carry

        lax.fori_loop(0, width // 256, tile, 0)

    def prepare(self):
        _, side, over_x, over_y, corner = plane()
        part, near = self.part, self.from_near
        half = self.rows // 2
        low, high = pl.ds(0, half), pl.ds(half, half)

        def hop(number, source, target, index):
            return to_dp(source, target, self.send.at[number], self.recv.at[number], index)

        self.shares = [hop(i, part.at[4 + i], self.from_side.at[i], side) for i in range(4)]
        self.corners = [
            hop(4, part.at[0, low], self.from_corner.at[0], over_x),
            hop(5, part.at[0, high], self.from_corner.at[1], over_y),
        ]
        self.nears = [
            hop(6, part.at[1, low], near.at[0, low], over_x),
            hop(7, part.at[1, high], near.at[0, high], over_x),
            hop(8, part.at[2, high], near.at[1, high], over_y),
            hop(9, part.at[2, low], near.at[1, low], over_y),
        ]

    def add_side(self, slot):
        self.shares[slot].wait_recv()

        def body(span):
            self.part[slot, span, :] = (
                self.part[slot, span, :].astype(F32) + self.from_side[slot, span, :].astype(F32)
            ).astype(BF16)

        each_chunk(self.rows, body)

    def add_corner(self, slot, offset, which):
        self.corners[which].wait_recv()

        def body(span):
            target = pl.ds(pl.multiple_of(offset + span.start, CHUNK), CHUNK)
            self.part[slot, target, :] = (
                self.part[slot, target, :].astype(F32)
                + self.from_corner[which, span, :].astype(F32)
            ).astype(BF16)

        each_chunk(self.rows // 2, body)

    def products(self):
        self.prepare()
        me, _, over_x, over_y, corner = plane()
        turn = 1 - 2 * lax.rem(me, 2)
        for slot, owner in enumerate((corner, over_x, over_y, me)):
            self.product(owner + turn, 4 + slot)
            self.shares[slot].start()
        for slot, owner in enumerate((corner, over_x, over_y, me)):
            self.product(owner, slot)

    def launch(self):
        self.add_side(0)
        self.corners[0].start()
        self.corners[1].start()
        self.add_side(1)
        self.nears[0].start()
        self.add_side(2)
        self.nears[2].start()

    def begin(self):
        self.prepare()
        me, _, over_x, over_y, corner = plane()
        turn = 1 - 2 * lax.rem(me, 2)
        self.product(corner + turn, 4)
        self.shares[0].start()
        self.product(corner, 0)
        self.product(over_x + turn, 5)
        self.shares[1].start()
        self.add_side(0)
        self.corners[0].start()
        self.corners[1].start()
        self.product(over_x, 1)
        self.product(over_y + turn, 6)
        self.shares[2].start()
        self.add_side(1)
        self.nears[0].start()
        self.product(over_y, 2)
        self.product(me + turn, 7)
        self.shares[3].start()
        self.add_side(2)
        self.nears[2].start()
        self.product(me, 3)

    def middle(self):
        self.add_corner(2, 0, 0)
        self.nears[3].start()
        self.add_corner(1, self.rows // 2, 1)
        self.nears[1].start()

    def end(self):
        self.shares[3].wait_recv()
        for copy in self.nears:
            copy.wait_recv()

    def run(self):
        self.begin()
        self.middle()
        self.end()

    def rows_of(self, span):
        return (
            self.part[3, span, :].astype(F32)
            + self.from_side[3, span, :].astype(F32)
            + self.from_near[0, span, :].astype(F32)
            + self.from_near[1, span, :].astype(F32)
        )

    def finish(self):
        for copy in self.shares + self.corners + self.nears:
            copy.wait_send()


def reduce_scratch(rows, width):
    dma = pltpu.SemaphoreType.DMA
    return [
        pltpu.VMEM((8, rows, width), BF16),
        pltpu.VMEM((4, rows, width), BF16),
        pltpu.VMEM((2, rows // 2, width), BF16),
        pltpu.VMEM((2, rows, width), BF16),
        dma((10,)),
        dma((10,)),
    ]


def gather_scratch(rows, width):
    dma = pltpu.SemaphoreType.DMA
    return [pltpu.VMEM((rows, width), BF16), dma((13,)), dma((13,)), dma(())]


def mean_rows(values):
    return jnp.mean(values, axis=-1, keepdims=True)


class Heads:
    def __init__(self, source, arrive, send, recv, views):
        me, z = lax.axis_index("dp"), lax.axis_index("mp")
        self.me, self.z = me, z
        self.core = lax.rem(me, 2)
        self.source, self.arrive, self.send, self.recv, self.views = source, arrive, send, recv, views
        self.owner = lax.div(z, 2)

    def copy(self, slot, half, number):
        target_z = 2 * self.core + slot
        index = (slot * 2 + half) * self.views + number
        return to_at(
            self.view(slot, half, number),
            self.arrive.at[self.z, number],
            self.send.at[index],
            self.recv.at[self.z * self.views + number],
            self.me - self.core + half,
            target_z,
        )

    def view(self, slot, half, number):
        rows = pl.ds(pl.multiple_of((2 * number + slot) * LANES, LANES), HEAD_DIM)
        columns = self.source.shape[1] // 2
        return self.source.at[rows, pl.ds(pl.multiple_of(half * columns, LANES), columns)]

    def each(self, action):
        for slot in range(2):
            for half in range(2):
                mine = (2 * self.core + slot == self.z) & (self.core == half)

                @pl.when(jnp.logical_not(mine))
                def _():
                    for number in range(self.views):
                        action(self.copy(slot, half, number))

    def start(self):
        self.each(lambda copy: copy.start())

    def finish_send(self):
        self.each(lambda copy: copy.wait_send())

    def total(self, out):
        me, z = self.me, self.z
        for number in range(self.views):
            for other in range(4):
                waiting = to_at(
                    self.view(0, 0, number),
                    self.arrive.at[other, number],
                    self.send.at[0],
                    self.recv.at[other * self.views + number],
                    me,
                    other,
                )

                @pl.when((z != other) | (self.core != self.owner))
                def _():
                    waiting.wait_recv()

                @pl.when((z == other) & (self.core == self.owner))
                def _():
                    self.arrive[other, number] = self.view(lax.rem(z, 2), self.core, number)[...]

            count = self.arrive.shape[2]

            def body(span):
                found = self.arrive[0, number, span, :].astype(F32)
                for other in range(1, 4):
                    found = found + self.arrive[other, number, span, :].astype(F32)
                out[number, span, :] = found.astype(BF16)

            each_chunk(count, body, 16)


def to_at(source, target, send_sem, recv_sem, dp, mp):
    return pltpu.make_async_remote_copy(
        src_ref=source,
        dst_ref=target,
        send_sem=send_sem,
        recv_sem=recv_sem,
        device_id={"dp": dp, "mp": mp},
        device_id_type=MESH,
    )


class Units:
    def __init__(self, both_sum, down_sum, both_in, down_in, both_stage, down_stage, send, recv, local):
        self.z = lax.axis_index("mp")
        self.sums = (both_sum, down_sum)
        self.inputs = (both_in, down_in)
        self.stages = (both_stage, down_stage)
        self.send, self.recv, self.local = send, recv, local
        z = self.z
        self.outer = (z == 0) | (z == 3)
        self.far = 3 - z
        self.near = 1 + lax.div(z, 3)
        self.second = 3 - self.near
        self.edge = 3 * (z - 1)

    def part(self, kind, z):
        if kind == 0:
            return self.sums[0].at[z]
        return self.sums[1].at[pl.ds(pl.multiple_of(z * LANES, LANES), LANES)]

    def straight(self, kind, number, target):
        return to_mp(
            self.part(kind, target),
            self.inputs[kind].at[self.z],
            self.send.at[number * 2 + kind],
            self.recv.at[self.z * 2 + kind],
            target,
        )

    def staged(self, kind):
        return to_mp(
            self.part(kind, self.far),
            self.stages[kind].at[0],
            self.send.at[4 + kind],
            self.recv.at[8 + kind],
            self.near,
        )

    def summed(self, kind):
        return to_mp(
            self.stages[kind].at[1],
            self.inputs[kind].at[self.z],
            self.send.at[4 + kind],
            self.recv.at[self.z * 2 + kind],
            3 - self.edge,
        )

    def mine(self, kind):
        return pltpu.make_async_copy(
            self.part(kind, 3 - self.edge), self.stages[kind].at[1], self.local.at[kind]
        )

    def start(self):
        @pl.when(self.outer)
        def _():
            for kind in range(2):
                self.staged(kind).start()
            for kind in range(2):
                self.straight(kind, 0, self.near).start()
                self.straight(kind, 1, self.second).start()

        @pl.when(jnp.logical_not(self.outer))
        def _():
            for kind in range(2):
                self.mine(kind).start()
                self.straight(kind, 0, 3 - self.z).start()
                self.straight(kind, 1, self.edge).start()

    def add(self):
        @pl.when(jnp.logical_not(self.outer))
        def _():
            for kind in range(2):
                stage = self.stages[kind]
                self.mine(kind).wait()
                to_mp(
                    self.part(kind, 0),
                    stage.at[0],
                    self.send.at[4 + kind],
                    self.recv.at[8 + kind],
                    self.edge,
                ).wait_recv()

                def body(span):
                    stage[1, span, :] = (
                        stage[0, span, :].astype(F32) + stage[1, span, :].astype(F32)
                    ).astype(BF16)

                each_chunk(stage.shape[1], body)
                self.summed(kind).start()

    def arrived(self, kind, source):
        to_mp(
            self.part(kind, 0),
            self.inputs[kind].at[source],
            self.send.at[kind],
            self.recv.at[source * 2 + kind],
            source,
        ).wait_recv()

    def finish(self):
        @pl.when(self.outer)
        def _():
            for kind in range(2):
                self.arrived(kind, 1)
                self.arrived(kind, 2)
                self.straight(kind, 0, self.near).wait_send()
                self.straight(kind, 1, self.second).wait_send()
                self.staged(kind).wait_send()

        @pl.when(jnp.logical_not(self.outer))
        def _():
            for kind in range(2):
                self.arrived(kind, 0)
                self.arrived(kind, 3)
                self.arrived(kind, 3 - self.z)
                self.straight(kind, 0, 3 - self.z).wait_send()
                self.straight(kind, 1, self.edge).wait_send()
                self.summed(kind).wait_send()


def backward_kernel(
    lengths, kept, branch, mixed, w_out, slots, flags, activated, w_down, middle, both_sum, down_sum,
    out, result, proj_part, branch_all, both_in, down_in,
    totals, query_part, key_value, ending, leaving, arriving, send, recv,
    part, from_side, from_corner, from_near, send_r, recv_r, arrive, send_h, recv_h,
    mixed_grad, proj_sum, shard, branch_tile, load_sem, send_g, recv_g,
    both_stage, down_stage, send_u, recv_u, local,
    *, scale, groups, rows,
):
    z = lax.axis_index("mp")
    members = lax.axis_size("mp")
    count, width = groups * rows, middle.shape[1]
    greet_all(pltpu.get_barrier_semaphore())
    units = Units(
        both_sum, down_sum, both_in, down_in, both_stage, down_stage, send_u, recv_u, local
    )
    gather = Gather(branch, branch_all, send_g, recv_g, local.at[2])
    gather.start()
    units.start()
    reduce = Reduce(activated, w_down, False, part, from_side, from_corner, from_near, send_r, recv_r)
    reduce.products()

    def spread_back(turn, carry):
        for number, numbers in ARRIVALS:
            pl.when(turn == number)(functools.partial(gather.arrive, *numbers))

        @pl.when(turn == 0)
        def _():
            gather.keep.wait()

        owner = owner_at(turn)
        load = pltpu.make_async_copy(branch_all.at[owner], shard, load_sem.at[0])
        load.start()
        load.wait()
        mixed_grad[owner] = (
            lax.dot_general(shard[...], w_out[...], NT, preferred_element_type=F32)
            .astype(BF16)
            .reshape(groups, rows // groups, 256)
        )
        return carry

    lax.fori_loop(0, 8, spread_back, 0)
    reduce.launch()
    units.add()

    def load_tile(t):
        columns = pl.ds(pl.multiple_of(t * 256, 256), 256)
        return pltpu.make_async_copy(
            branch_all.at[:, :, columns], branch_tile.at[t % 2], load_sem.at[1 + t % 2]
        )

    load_tile(0).start()

    def project_tile(t, carry):
        columns = pl.ds(pl.multiple_of(t * 256, 256), 256)

        @pl.when(t < width // 256 - 1)
        def _():
            load_tile(t + 1).start()

        load_tile(t).wait()
        proj_sum[:, columns] = lax.dot_general(
            mixed[...], branch_tile[t % 2].reshape(count, 256), TN, preferred_element_type=F32
        ).astype(BF16)
        return carry

    lax.fori_loop(0, width // 256, project_tile, 0)
    heads = Heads(proj_sum, arrive, send_h, recv_h, 1)
    heads.start()

    def halo(k, other):
        return to_mp(leaving.at[k], arriving.at[k], send.at[k], recv.at[k], other)

    def attend(k, carry):
        hot = one_hot(slots, k, rows)
        given = mixed_grad[:, pl.ds(k, 1)].reshape(rows, 256)
        grad_ordered = jnp.dot(hot, given, preferred_element_type=F32).astype(BF16)
        totals[...] = jnp.zeros_like(totals)
        for block in range(rows // 128):
            allowed = block_mask(lengths, flags, k, block, z, rows)
            for head in range(2):
                query = kept[k, pl.ds(64 + block * 128, 128), pl.ds(head * 128, 128)]
                keys = kept[k, pl.ds(block * 128, 192), pl.ds(256 + head * 128, 128)]
                values = kept[k, pl.ds(block * 128, 192), pl.ds(512 + head * 128, 128)]
                grad = grad_ordered[block * 128 : block * 128 + 128, head * 128 : head * 128 + 128]
                scores = lax.dot_general(query, keys, NT, preferred_element_type=F32) * scale
                scores = jnp.where(allowed, scores, -MASKED)
                weights = jnp.exp(scores - jnp.max(scores, axis=-1, keepdims=True))
                again = weights / jnp.sum(weights, axis=-1, keepdims=True)
                chance_grad = lax.dot_general(grad, values, NT, preferred_element_type=F32)
                row_dot = jnp.sum(again * chance_grad, axis=-1, keepdims=True)
                score_grad = (again * (chance_grad - row_dot)).astype(BF16)
                query_part[k, pl.ds(block * 128, 128), pl.ds(head * 128, 128)] = (
                    jnp.dot(score_grad, keys, preferred_element_type=F32) * scale
                ).astype(BF16)
                totals[pl.ds(block * 128, 192), pl.ds(head * 128, 128)] += (
                    lax.dot_general(score_grad, query, TN, preferred_element_type=F32) * scale
                )
                totals[pl.ds(block * 128, 192), pl.ds(256 + head * 128, 128)] += lax.dot_general(
                    again.astype(BF16), grad, TN, preferred_element_type=F32
                )
        key_value[k] = totals[pl.ds(64, rows), :].astype(BF16)
        ending[k] = totals[pl.ds(rows, 64), :]

        @pl.when(z > 0)
        def _():
            leaving[k] = totals[pl.ds(0, 64), :].astype(BF16)
            halo(k, z - 1).start()

        return carry

    lax.fori_loop(0, 3, attend, 0)
    reduce.middle()
    lax.fori_loop(3, groups, attend, 0)

    def restore(k, carry):
        @pl.when(z < members - 1)
        def _():
            halo(k, z).wait_recv()
            key_value[k, pl.ds(rows - 64, 64), :] = (
                ending[k] + arriving[k].astype(F32)
            ).astype(BF16)

        hot = one_hot(slots, k, rows)
        ordered = jnp.concatenate([query_part[k], key_value[k]], axis=1)
        back = lax.dot_general(hot, ordered, TN, preferred_element_type=F32).astype(BF16)
        out[:, pl.ds(k, 1)] = back.reshape(groups, 1, rows // groups, 768)
        return carry

    lax.fori_loop(0, groups, restore, 0)
    reduce.end()

    def body(span):
        result[span, :] = (middle[span, :] + reduce.rows_of(span)).astype(BF16)

    each_chunk(rows, body)
    heads.total(proj_part)
    heads.finish_send()
    units.finish()
    for copy in gather.copies:
        copy.wait_send()
    reduce.finish()

    @pl.when(z > 0)
    def _():
        def done(k, carry):
            halo(k, z - 1).wait_send()
            return carry

        lax.fori_loop(0, groups, done, 0)


def attend_back(
    lengths, kept, branch, mixed, w_out, slots, flags, activated, w_down, middle,
    both_sum, down_sum, scale,
):
    groups = kept.shape[0]
    rows, width = middle.shape
    members = both_sum.shape[0]
    dma = pltpu.SemaphoreType.DMA
    shape = jax.ShapeDtypeStruct
    return pl.pallas_call(
        functools.partial(backward_kernel, scale=scale, groups=groups, rows=rows),
        out_shape=(
            shape((groups, groups, rows // groups, 768), BF16),
            shape((rows, width), BF16),
            shape((1, HEAD_DIM, width // 2), BF16),
            shape((groups, rows, width), BF16),
            shape((members, width, 256), BF16),
            shape((members, LANES, width), BF16),
        ),
        in_specs=[in_scalar()] + [on_chip()] * 9 + [anywhere()] * 2,
        out_specs=(on_chip(),) * 3 + (anywhere(),) * 3,
        scratch_shapes=[
            pltpu.VMEM((rows + 64, 512), F32),
            pltpu.VMEM((groups, rows, 256), BF16),
            pltpu.VMEM((groups, rows, 512), BF16),
            pltpu.VMEM((groups, 64, 512), F32),
            pltpu.VMEM((groups, 64, 512), BF16),
            pltpu.VMEM((groups, 64, 512), BF16),
            dma((groups,)),
            dma((groups,)),
        ]
        + reduce_scratch(rows, width)
        + [
            pltpu.VMEM((4, 1, HEAD_DIM, width // 2), BF16),
            dma((4,)),
            dma((4,)),
            pltpu.VMEM((groups, groups, rows // groups, 256), BF16),
            pltpu.VMEM((2 * LANES, width), BF16),
            pltpu.VMEM((rows, width), BF16),
            pltpu.VMEM((2, groups, rows, 256), BF16),
            dma((3,)),
            dma((13,)),
            dma((13,)),
            pltpu.VMEM((2, width, 256), BF16),
            pltpu.VMEM((2, LANES, width), BF16),
            dma((6,)),
            dma((10,)),
            dma((3,)),
        ],
        compiler_params=remote_params(3, 63 * 1024 * 1024),
        cost_estimate=pl.CostEstimate(flops=0, bytes_accessed=300_000_000, transcendentals=0),
        name="attend_back",
    )(
        lengths, kept, branch, mixed, w_out, slots, flags, activated, w_down, middle,
        both_sum, down_sum,
    )


def middle_kernel(
    mixed, w_out, tokens, gain, middle, hidden,
    part, from_side, from_corner, from_near, send, recv,
):
    pl.semaphore_wait(greet_plane(), 3)
    reduce = Reduce(mixed, w_out, False, part, from_side, from_corner, from_near, send, recv)
    reduce.run()

    def body(span):
        values = tokens[span, :].astype(F32) + reduce.rows_of(span)
        middle[span, :] = values
        inverse = lax.rsqrt(mean_rows(values * values) + EPSILON)
        hidden[span, :] = (values * inverse * gain[...]).astype(BF16)

    each_chunk(hidden.shape[0], body)
    reduce.finish()


def project_middle(mixed, w_out, tokens, gain):
    rows, width = tokens.shape
    return pl.pallas_call(
        middle_kernel,
        out_shape=(
            jax.ShapeDtypeStruct((rows, width), F32),
            jax.ShapeDtypeStruct((rows, width), BF16),
        ),
        in_specs=[on_chip()] * 4,
        out_specs=(on_chip(), on_chip()),
        scratch_shapes=reduce_scratch(rows, width),
        compiler_params=remote_params(4),
        cost_estimate=pl.CostEstimate(flops=0, bytes_accessed=150_000_000, transcendentals=0),
        name="project_middle",
    )(mixed, w_out, tokens, gain)


def norm_back_rows(gradient, values, gain, sums, span):
    inverse = lax.rsqrt(mean_rows(values * values) + EPSILON)
    normed = values * inverse
    product = gradient * normed
    folded = product[0:8]
    for step in range(1, CHUNK // 8):
        folded = folded + product[step * 8 : step * 8 + 8]
    sums[...] += folded
    scaled = gradient * gain
    return inverse * (scaled - normed * mean_rows(scaled * normed))


def feed_kernel(
    hidden_own, cotangent_all, middle, cotangent, gain, w_both, w_down,
    middle_grad, branch, sums, activated, both_sum, down_sum,
    hidden_all, both_grad, part, from_side, from_corner, from_near, send_r, recv_r,
    send_a, recv_a, cot_half, cot_tile, stage_both, stage_down, load_sem, local,
):
    groups, rows, width = hidden_all.shape
    members = w_both.shape[0]
    half_rows = rows // 2
    me, side, over_x, over_y, _ = plane()
    own = pltpu.make_async_copy(hidden_own, hidden_all.at[me], local.at[0])
    own.start()
    start_middle = pltpu.make_async_copy(middle, middle_grad, local.at[1])
    start_middle.start()

    def place_of(step):
        block = step // 4
        near = ((block + 1) // 2) % 2
        far = block // 3
        mixed_order = near * (1 - block // 2)
        second = mixed_order * (step % 2) + (1 - mixed_order) * ((step // 2) % 2)
        half = mixed_order * ((step % 2 + (step // 2) % 2) % 2) + (1 - mixed_order) * (step % 2)
        other = (1 - near) * second + (block // 2) * near
        in_x = near * (1 - second) + far
        in_y = near * second + far
        owner = me + in_x * (over_x - me) + in_y * (over_y - me) + other * (side - me)
        slot = 4 * other + 3 * (1 - near) * (1 - far) + near * (1 + second)
        return owner, half, slot

    def load_cotangent(step):
        owner, half, _ = place_of(step)
        span = pl.ds(pl.multiple_of(half * half_rows, half_rows), half_rows)
        return pltpu.make_async_copy(
            cotangent_all.at[owner, span], cot_half.at[step % 2], load_sem.at[step % 2]
        )

    load_cotangent(0).start()
    pl.semaphore_wait(greet_plane(), 3)
    own.wait()
    gather = Gather(None, hidden_all, send_a, recv_a)
    gather.start()
    reduce = Reduce(None, None, False, part, from_side, from_corner, from_near, send_r, recv_r)
    reduce.prepare()

    def before(step, *numbers):
        return (step, lambda: gather.arrive(*numbers))

    def nears():
        reduce.add_side(1)
        reduce.nears[0].start()
        reduce.add_side(2)
        reduce.nears[2].start()

    early = [
        before(2, 4),
        before(4, 0),
        before(5, 1),
        before(6, 2),
        before(7, 3),
        before(8, 6, 9),
        before(10, 8, 10),
        before(12, 5, 7),
        (13, nears),
        before(14, 11, 12),
    ]
    late = [(3, 3), (9, 1), (11, 2), (15, 0)]

    def unit(step, carry):
        for number, action in early:
            pl.when(step == number)(action)

        @pl.when(step < 15)
        def _():
            load_cotangent(step + 1).start()

        load_cotangent(step).wait()
        owner, half, slot = place_of(step)
        span = pl.ds(pl.multiple_of(half * half_rows, half_rows), half_rows)
        mine = hidden_all[owner, span, :]
        grads = cot_half[step % 2]
        for z in range(members):
            raw = jnp.dot(mine, w_both[z], preferred_element_type=F32)
            units = pl.ds(z * 128, 128)
            if z % 2 == 0:
                pair = lax.dot_general(
                    grads, w_down[pl.ds(z * 128, 256), :], NT, preferred_element_type=F32
                )
            active_grad = pair[:, 128 * (z % 2) : 128 * (z % 2) + 128]
            gate, upward = raw[:, :128], raw[:, 128:]
            sigmoid = jax.nn.sigmoid(gate)
            activated[owner, span, units] = (gate * sigmoid * upward).astype(BF16)
            both_grad[owner, span, pl.ds(z * 256, 128)] = (
                active_grad * upward * sigmoid * (1.0 + gate * (1.0 - sigmoid))
            ).astype(BF16)
            both_grad[owner, span, pl.ds(z * 256 + 128, 128)] = (
                active_grad * gate * sigmoid
            ).astype(BF16)

        def tile(t, inner):
            columns = pl.ds(pl.multiple_of(t * 256, 256), 256)
            value = sum(
                lax.dot_general(
                    both_grad[owner, span, pl.ds(z * 256, 256)],
                    w_both[z, columns, :],
                    NT,
                    preferred_element_type=F32,
                )
                for z in range(members)
            )
            part[slot, span, columns] = value.astype(BF16)
            return inner

        lax.fori_loop(0, width // 256, tile, 0)
        for number, share in late:
            pl.when(step == number)(reduce.shares[share].start)
        return carry

    lax.fori_loop(0, 16, unit, 0)

    def load_tile(t):
        columns = pl.ds(pl.multiple_of(t * 256, 256), 256)
        return pltpu.make_async_copy(
            cotangent_all.at[:, :, columns], cot_tile.at[t % 2], load_sem.at[2 + t % 2]
        )

    def store_both(t):
        columns = pl.ds(pl.multiple_of(t * 256, 256), 256)
        return pltpu.make_async_copy(
            stage_both.at[t % 2], both_sum.at[:, columns], load_sem.at[4 + t % 2]
        )

    def store_down(t):
        columns = pl.ds(pl.multiple_of(t * 256, 256), 256)
        return pltpu.make_async_copy(
            stage_down.at[t % 2], down_sum.at[:, columns], load_sem.at[6 + t % 2]
        )

    tiles = width // 256
    count = groups * rows

    def weight_tile(t, carry):
        columns = pl.ds(pl.multiple_of(t * 256, 256), 256)

        @pl.when(t < tiles - 1)
        def _():
            load_tile(t + 1).start()

        load_tile(t).wait()

        @pl.when(t >= 2)
        def _():
            store_both(t - 2).wait()
            store_down(t - 2).wait()

        value = lax.dot_general(
            hidden_all[:, :, columns].reshape(count, 256),
            both_grad[...].reshape(count, members * 256),
            TN,
            preferred_element_type=F32,
        )
        for z in range(members):
            stage_both[t % 2, z] = value[:, z * 256 : z * 256 + 256].astype(BF16)
        stage_down[t % 2] = lax.dot_general(
            activated[...].reshape(count, members * 128),
            cot_tile[t % 2].reshape(count, 256),
            TN,
            preferred_element_type=F32,
        ).astype(BF16)
        store_both(t).start()
        store_down(t).start()
        return carry

    load_tile(0).start()
    reduce.add_side(0)
    reduce.corners[0].start()
    reduce.corners[1].start()
    lax.fori_loop(0, 4, weight_tile, 0)
    reduce.middle()
    lax.fori_loop(4, tiles, weight_tile, 0)
    reduce.end()
    start_middle.wait()
    sums[...] = jnp.zeros_like(sums)

    def body(span):
        change = norm_back_rows(reduce.rows_of(span), middle_grad[span, :], gain[...], sums, span)
        total = cotangent[span, :].astype(F32) + change
        middle_grad[span, :] = total
        branch[span, :] = total.astype(BF16)

    each_chunk(rows, body)
    gather.sent()
    reduce.finish()
    for t in (tiles - 2, tiles - 1):
        store_both(t).wait()
        store_down(t).wait()


def feed(hidden_own, cotangent_all, middle, cotangent, gain, w_both, w_down):
    groups, rows, width = cotangent_all.shape
    members = w_both.shape[0]
    dma = pltpu.SemaphoreType.DMA
    units = members * 128
    return pl.pallas_call(
        feed_kernel,
        out_shape=(
            jax.ShapeDtypeStruct((rows, width), F32),
            jax.ShapeDtypeStruct((rows, width), BF16),
            jax.ShapeDtypeStruct((8, width), F32),
            jax.ShapeDtypeStruct((groups, rows, units), BF16),
            jax.ShapeDtypeStruct((members, width, 256), BF16),
            jax.ShapeDtypeStruct((units, width), BF16),
        ),
        in_specs=[anywhere()] * 3 + [on_chip()] * 4,
        out_specs=(on_chip(),) * 4 + (anywhere(),) * 2,
        scratch_shapes=[
            pltpu.VMEM((groups, rows, width), BF16),
            pltpu.VMEM((groups, rows, 2 * units), BF16),
        ]
        + reduce_scratch(rows, width)
        + [
            dma((13,)),
            dma((13,)),
            pltpu.VMEM((2, rows // 2, width), BF16),
            pltpu.VMEM((2, groups, rows, 256), BF16),
            pltpu.VMEM((2, members, 256, 256), BF16),
            pltpu.VMEM((2, units, 256), BF16),
            dma((8,)),
            dma((2,)),
        ],
        compiler_params=remote_params(5, 62 * 1024 * 1024),
        cost_estimate=pl.CostEstimate(flops=0, bytes_accessed=400_000_000, transcendentals=0),
        name="feed",
    )(hidden_own, cotangent_all, middle, cotangent, gain, w_both, w_down)


def input_kernel(
    qkv_grad, w_qkv, hidden_all, tokens, middle_grad, gain, sums_two, proj_part,
    both_sum, down_sum, both_in, down_in,
    result, heads_part, gains, both_all, down_all,
    part, from_side, from_corner, from_near, send, recv, sums,
    arrive, send_h, recv_h, own, plane_sums, column_sums, send_s, recv_s,
    qkv_sum, hidden_tile, tile_sem, send_b, recv_b, send_d, recv_d, both_found, down_found, local,
):
    me, z = lax.axis_index("dp"), lax.axis_index("mp")
    count = qkv_grad.shape[0]
    tiles = tokens.shape[1] // 256

    def load(t):
        columns = pl.ds(pl.multiple_of(t * 256, 256), 256)
        return pltpu.make_async_copy(
            hidden_all.at[:, :, columns], hidden_tile.at[t % 2], tile_sem.at[t % 2]
        )

    load(0).start()

    def weight_tile(t, carry):
        columns = pl.ds(pl.multiple_of(t * 256, 256), 256)

        @pl.when(t < tiles - 1)
        def _():
            load(t + 1).start()

        load(t).wait()
        qkv_sum[:, columns] = lax.dot_general(
            qkv_grad[...], hidden_tile[t % 2].reshape(count, 256), TN, preferred_element_type=F32
        ).astype(BF16)
        return carry

    outer = (z == 0) | (z == 3)
    inner = 3 - z
    rows_down = pl.ds(pl.multiple_of(z * LANES, LANES), LANES)
    sources = [(outer, 1), (outer, 2), (z == 1, 0), (z == 1, 2), (z == 1, 3)]
    sources += [(z == 2, 0), (z == 2, 1), (z == 2, 3)]
    places = [1, 2, 1, 2, 3, 1, 2, 3]

    def found(source, place):
        return (
            pltpu.make_async_copy(both_in.at[source], both_found.at[place], local.at[2 * place]),
            pltpu.make_async_copy(down_in.at[source], down_found.at[place], local.at[2 * place + 1]),
        )

    own_parts = (
        pltpu.make_async_copy(both_sum.at[z], both_found.at[0], local.at[0]),
        pltpu.make_async_copy(down_sum.at[rows_down], down_found.at[0], local.at[1]),
    )
    for copy in own_parts:
        copy.start()
    for (here, source), place in zip(sources, places):
        @pl.when(here)
        def _():
            for copy in found(source, place):
                copy.start()

    @pl.when(outer)
    def _():
        both_found[3] = jnp.zeros_like(both_found[3])
        down_found[3] = jnp.zeros_like(down_found[3])

    greet_all(pltpu.get_barrier_semaphore())
    reduce = Reduce(qkv_grad, w_qkv, False, part, from_side, from_corner, from_near, send, recv)
    reduce.begin()
    lax.fori_loop(0, tiles, weight_tile, 0)
    heads = Heads(qkv_sum, arrive, send_h, recv_h, 3)
    heads.start()
    heads_part[3] = proj_part[0]
    reduce.middle()
    for copy in own_parts:
        copy.wait()
    for (here, source), place in zip(sources, places):
        @pl.when(here)
        def _():
            for copy in found(source, place):
                copy.wait()

    for buffer in (both_found, down_found):
        def add(span):
            value = buffer[0, span, :].astype(F32) + buffer[1, span, :].astype(F32)
            value = value + buffer[2, span, :].astype(F32) + buffer[3, span, :].astype(F32)
            buffer[0, span, :] = value.astype(BF16)

        each_chunk(buffer.shape[1], add)
    both = Gather(both_found.at[0], both_all, send_b, recv_b, local.at[8])
    down = Gather(down_found.at[0], down_all, send_d, recv_d, local.at[9])
    both.start()
    down.start()
    reduce.end()
    sums[...] = jnp.zeros_like(sums)

    def body(span):
        values = tokens[span, :].astype(F32)
        change = norm_back_rows(reduce.rows_of(span), values, gain[...], sums, span)
        result[span, :] = (middle_grad[span, :] + change).astype(BF16)

    each_chunk(result.shape[0], body)
    own[...] = jnp.concatenate(
        [
            jnp.sum(sums[...], axis=0, keepdims=True),
            jnp.sum(sums_two[...], axis=0, keepdims=True),
        ],
        axis=0,
    )
    swaps = swap_all(own, plane_sums, send_s, recv_s)
    for copy in swaps:
        copy.start()
    plane_sums[me] = own[...]
    both.pass_on()
    down.pass_on()
    for copy in swaps:
        copy.wait()
    found = plane_sums[0]
    for other in range(1, 8):
        found = found + plane_sums[other]
    column_sums[z] = found
    passes = [
        to_mp(
            column_sums.at[z],
            column_sums.at[z],
            send_s.at[6 + step],
            recv_s.at[6 + step],
            lax.rem(z + step, 4),
        )
        for step in range(1, 4)
    ]
    for copy in passes:
        copy.start()
    heads.total(heads_part)
    for copy in passes:
        copy.wait()
    gains[...] = (column_sums[0] + column_sums[1]) + (column_sums[2] + column_sums[3])
    both.finish()
    down.finish()
    heads.finish_send()
    reduce.finish()


def project_input(
    qkv_grad, w_qkv, hidden_all, tokens, middle_grad, gain, sums_two, proj_part,
    both_sum, down_sum, both_in, down_in,
):
    rows, width = tokens.shape
    groups = hidden_all.shape[0]
    dma = pltpu.SemaphoreType.DMA
    return pl.pallas_call(
        input_kernel,
        out_shape=(
            jax.ShapeDtypeStruct((rows, width), BF16),
            jax.ShapeDtypeStruct((4, HEAD_DIM, width // 2), BF16),
            jax.ShapeDtypeStruct((2, width), F32),
            jax.ShapeDtypeStruct((groups, width, 256), BF16),
            jax.ShapeDtypeStruct((groups, LANES, width), BF16),
        ),
        in_specs=[on_chip()] * 2 + [anywhere()] + [on_chip()] * 5 + [anywhere()] * 4,
        out_specs=(on_chip(),) * 3 + (anywhere(),) * 2,
        scratch_shapes=reduce_scratch(rows, width)
        + [
            pltpu.VMEM((8, width), F32),
            pltpu.VMEM((4, 3, HEAD_DIM, width // 2), BF16),
            dma((12,)),
            dma((12,)),
            pltpu.VMEM((2, width), F32),
            pltpu.VMEM((8, 2, width), F32),
            pltpu.VMEM((4, 2, width), F32),
            dma((10,)),
            dma((10,)),
            pltpu.VMEM((6 * LANES, width), BF16),
            pltpu.VMEM((2, groups, rows, 256), BF16),
            dma((2,)),
            dma((13,)),
            dma((13,)),
            dma((13,)),
            dma((13,)),
            pltpu.VMEM((4, width, 256), BF16),
            pltpu.VMEM((4, LANES, width), BF16),
            dma((10,)),
        ],
        compiler_params=remote_params(6, 62 * 1024 * 1024),
        cost_estimate=pl.CostEstimate(flops=0, bytes_accessed=250_000_000, transcendentals=0),
        name="project_input",
    )(
        qkv_grad, w_qkv, hidden_all, tokens, middle_grad, gain, sums_two, proj_part,
        both_sum, down_sum, both_in, down_in,
    )


def units_kernel(both, gate, upward):
    for d in range(both.shape[0]):
        gate[:, d * 128 : d * 128 + 128] = both[d, :, :128].astype(F32)
        upward[:, d * 128 : d * 128 + 128] = both[d, :, 128:].astype(F32)


def assemble_units(both):
    groups, width, wide = both.shape
    tile = 256
    shape = jax.ShapeDtypeStruct((width, groups * wide // 2), F32)
    spec = pl.BlockSpec((tile, groups * wide // 2), lambda i: (i, 0))
    return pl.pallas_call(
        units_kernel,
        grid=(width // tile,),
        out_shape=(shape, shape),
        in_specs=[pl.BlockSpec((groups, tile, wide), lambda i: (0, i, 0))],
        out_specs=(spec, spec),
        cost_estimate=pl.CostEstimate(flops=0, bytes_accessed=22_000_000, transcendentals=0),
        name="assemble_units",
    )(both)


def heads_kernel(whole, *outs):
    columns = whole.shape[4]
    for kind, out in enumerate(outs):
        for half in range(whole.shape[1]):
            out[:, half * columns : half * columns + columns] = whole[0, half, kind].astype(F32)


def assemble_heads(whole):
    chips, halves, kinds, rows, columns = whole.shape
    shape = jax.ShapeDtypeStruct((chips * rows, halves * columns), F32)
    spec = pl.BlockSpec((rows, halves * columns), lambda c: (c, 0))
    return pl.pallas_call(
        heads_kernel,
        grid=(chips,),
        out_shape=(shape,) * kinds,
        in_specs=[pl.BlockSpec((1, halves, kinds, rows, columns), lambda c: (c, 0, 0, 0, 0))],
        out_specs=(spec,) * kinds,
        cost_estimate=pl.CostEstimate(flops=0, bytes_accessed=20_000_000, transcendentals=0),
        name="assemble_heads",
    )(whole)


def swapped(
    tokens, cotangent, route, lengths, key_mask, norm1_gain, norm2_gain,
    w_query, w_key, w_value, w_out, w_gate, w_up, w_down,
):
    groups = lax.axis_size("dp")
    members = lax.axis_size("mp")
    me = lax.axis_index("dp")
    z = lax.axis_index("mp")
    rows, width = tokens.shape
    bucket = rows // groups
    units = w_down.shape[0] // groups

    target = route // TOK_DEV
    earlier = jnp.arange(rows, dtype=jnp.int32)
    same = (target[:, None] == target[None, :]) & (earlier[None, :] < earlier[:, None])
    send_at = target * bucket + jnp.sum(same.astype(jnp.int32), axis=1)
    sorting = send_at[None, :] == earlier[:, None]
    slots_own = jnp.sum(jnp.where(sorting, (route % rows)[None, :], 0), axis=1)
    sort_hot = sorting.astype(BF16)
    tokens_b = jnp.dot(sort_hot, tokens, preferred_element_type=F32).astype(BF16)
    cotangent_b = jnp.dot(sort_hot, cotangent, preferred_element_type=F32).astype(BF16)

    mask_window = lax.dynamic_slice_in_dim(
        jnp.concatenate([jnp.zeros((WINDOW,), jnp.int32), key_mask]), z * rows, rows + WINDOW
    )
    notes = jnp.concatenate([slots_own, mask_window, lengths[0]])
    notes = jnp.pad(notes, (0, 8 * LANES - notes.shape[0])).reshape(8, LANES)

    normed, _ = norm_rows(tokens_b.astype(F32))
    hidden_own = (normed * norm1_gain).astype(BF16)
    hidden_one, w_qkv, w_proj, notes_all, both_own, down_own = gather_first(
        hidden_own, w_query.T, w_key.T, w_value.T, w_out, w_gate, w_up, w_down, notes
    )
    notes_all = notes_all.reshape(groups, 8 * LANES)
    slots = (
        notes_all[:, :rows].reshape(groups, groups, bucket).transpose(1, 0, 2).reshape(groups, rows)
    )
    flags = notes_all[:, rows : 2 * rows + WINDOW]
    lengths_all = notes_all[:, 2 * rows + WINDOW : 2 * rows + WINDOW + 3]

    w_both = lax.all_gather(both_own, "mp")
    down_all = lax.all_gather(down_own, "mp", axis=0, tiled=True)

    count = groups * rows
    scale = HEAD_DIM ** (-0.5)
    mixed, kept, cotangent_all = attend_ahead(
        lengths_all, hidden_one, w_qkv, slots, flags, cotangent_b, scale
    )
    mixed = mixed.reshape(count, 2 * LANES)
    middle, hidden_two = project_middle(mixed, w_proj, tokens_b, norm2_gain[None])
    middle_grad, branch, sums_two, activated, both_sum, down_sum = feed(
        hidden_two, cotangent_all, middle, cotangent_b, norm2_gain[None], w_both, down_all
    )
    qkv_grad, output_rows, proj_part, _, both_in, down_in = attend_back(
        lengths_all,
        kept,
        branch,
        mixed,
        w_proj,
        slots,
        flags,
        activated.reshape(count, units * members),
        down_all,
        middle,
        both_sum,
        down_sum,
        scale,
    )
    qkv_grad = qkv_grad.reshape(count, 6 * LANES)
    input_rows, heads_part, gain_sums, both_whole, down_whole = project_input(
        qkv_grad,
        w_qkv,
        hidden_one,
        tokens_b,
        middle_grad,
        norm1_gain[None],
        sums_two,
        proj_part,
        both_sum,
        down_sum,
        both_in,
        down_in,
    )
    heads_whole = lax.all_gather(heads_part.reshape(4 * HEAD_DIM, width // 2), "dp")
    gate_grad, up_grad = assemble_units(both_whole)
    down_grad = down_whole.astype(F32).reshape(groups * units, width)
    query_grad, key_grad, value_grad, proj_grad = assemble_heads(
        heads_whole.reshape(groups // 2, 2, 4, HEAD_DIM, width // 2)
    )

    unsort = (((0,), (0,)), ((), ()))
    return (
        lax.dot_general(sort_hot, output_rows, unsort, preferred_element_type=F32).astype(BF16),
        lax.dot_general(sort_hot, input_rows, unsort, preferred_element_type=F32).astype(BF16),
        gain_sums[0],
        gain_sums[1],
        query_grad.T,
        key_grad.T,
        value_grad.T,
        proj_grad,
        gate_grad,
        up_grad,
        down_grad,
    )


def solution(mesh):
    in_specs = (
        P(("dp", "mp"), None),
        P(("dp", "mp"), None),
        P(("dp", "mp")),
        P("dp", None),
        P("dp"),
        P(),
        P(),
        P(None, "mp"),
        P(None, "mp"),
        P(None, "mp"),
        P("mp", None),
        P(None, "mp"),
        P(None, "mp"),
        P("mp", None),
    )
    out_specs = (
        P(("dp", "mp"), None),
        P(("dp", "mp"), None),
        P(),
        P(),
        P(None, "mp"),
        P(None, "mp"),
        P(None, "mp"),
        P("mp", None),
        P(None, "mp"),
        P(None, "mp"),
        P("mp", None),
    )
    body = swapped if (mesh.shape["dp"], mesh.shape["mp"]) == (8, 4) else local
    return jax.shard_map(body, mesh=mesh, in_specs=in_specs, out_specs=out_specs, check_vma=False)
```

```python
import functools

import jax
import jax.numpy as jnp
from jax import lax
from jax.experimental import pallas as pl
from jax.experimental.pallas import tpu as pltpu
from jax.sharding import PartitionSpec as P

HEAD_DIM = 112
WINDOW = 64
TOK_DEV = 1536


EPSILON = 1e-05
MASKED = 1e30


def norm_rows(values):
    inverse = lax.rsqrt(jnp.mean(values * values, axis=-1, keepdims=True) + EPSILON)
    return (values * inverse, inverse)


def norm_back(gradient, normed, inverse, norm_gain):
    scaled = gradient * norm_gain
    result = inverse * (scaled - normed * jnp.mean(scaled * normed, axis=-1, keepdims=True))
    return (result, jnp.sum(gradient * normed, axis=0))


def padded(values, filler):
    front = jnp.full((WINDOW,) + values.shape[1:], filler, values.dtype)
    return jnp.concatenate([front, values], axis=0)


def block_scores(query_block, key_block, query_seg, key_seg, key_flag, first_row, score_scale):
    query_pos = first_row + jnp.arange(query_block.shape[0], dtype=jnp.int32)
    key_pos = first_row - WINDOW + jnp.arange(key_block.shape[0], dtype=jnp.int32)
    distance = query_pos[:, None] - key_pos[None, :]
    allowed = (distance >= 0) & (distance < WINDOW) & (query_seg[:, None] == key_seg[None, :])
    allowed = allowed & ((key_flag[None, :] == 1) | (distance == 0))
    raw_scores = (
        jnp.einsum("qhd,khd->hqk", query_block, key_block, preferred_element_type=jnp.float32)
        * score_scale
    )
    return jnp.where(allowed[None], raw_scores, -MASKED)


def block_inputs(query, key_pad, value_pad, segment, seg_pad, live_pad, first_row, block_rows):
    key_span = block_rows + WINDOW
    return (
        lax.dynamic_slice_in_dim(query, first_row, block_rows, 0),
        lax.dynamic_slice_in_dim(key_pad, first_row, key_span, 0),
        lax.dynamic_slice_in_dim(value_pad, first_row, key_span, 0),
        lax.dynamic_slice_in_dim(segment, first_row, block_rows, 0),
        lax.dynamic_slice_in_dim(seg_pad, first_row, key_span, 0),
        lax.dynamic_slice_in_dim(live_pad, first_row, key_span, 0),
    )


def attend_forward(query, key_all, value_all, segment, key_live):
    token_count, head_count, head_width = query.shape
    block_rows = min(512, token_count)
    score_scale = head_width ** (-0.5)
    key_pad = padded(key_all, 0.0)
    value_pad = padded(value_all, 0.0)
    seg_pad = padded(segment, -1)
    live_pad = padded(key_live, 0)

    def one_block(running, block_index):
        first_row = block_index * block_rows
        query_block, key_block, value_block, query_seg, key_seg, key_flag = block_inputs(
            query, key_pad, value_pad, segment, seg_pad, live_pad, first_row, block_rows
        )
        scores = block_scores(
            query_block, key_block, query_seg, key_seg, key_flag, first_row, score_scale
        )
        row_max = jnp.max(scores, axis=-1, keepdims=True)
        weights = jnp.exp(scores - row_max)
        denominator = jnp.sum(weights, axis=-1, keepdims=True)
        chances = (weights / denominator).astype(jnp.bfloat16)
        mixed = jnp.einsum("hqk,khd->qhd", chances, value_block, preferred_element_type=jnp.float32)
        return (
            running,
            (mixed.astype(jnp.bfloat16), row_max[..., 0] + jnp.log(denominator[..., 0])),
        )

    _, (mixed, logsum) = lax.scan(
        one_block, jnp.zeros((), jnp.int32), jnp.arange(token_count // block_rows, dtype=jnp.int32)
    )
    return (mixed.reshape(token_count, head_count * head_width), logsum)


def attend_backward(query, key_all, value_all, segment, key_live, logsum, mixed_grad):
    token_count, head_count, head_width = query.shape
    block_rows = min(512, token_count)
    key_span = block_rows + WINDOW
    score_scale = head_width ** (-0.5)
    key_pad = padded(key_all, 0.0)
    value_pad = padded(value_all, 0.0)
    seg_pad = padded(segment, -1)
    live_pad = padded(key_live, 0)

    def one_block(running, inputs):
        key_grad, value_grad = running
        block_index, block_logsum = inputs
        first_row = block_index * block_rows
        query_block, key_block, value_block, query_seg, key_seg, key_flag = block_inputs(
            query, key_pad, value_pad, segment, seg_pad, live_pad, first_row, block_rows
        )
        grad_block = lax.dynamic_slice_in_dim(mixed_grad, first_row, block_rows, 0)
        scores = block_scores(
            query_block, key_block, query_seg, key_seg, key_flag, first_row, score_scale
        )
        chances = jnp.exp(scores - block_logsum[..., None])
        chance_grad = jnp.einsum(
            "qhd,khd->hqk", grad_block, value_block, preferred_element_type=jnp.float32
        )
        row_dot = jnp.sum(chances * chance_grad, axis=-1, keepdims=True)
        score_grad = (chances * (chance_grad - row_dot)).astype(jnp.bfloat16)
        query_grad = (
            jnp.einsum("hqk,khd->qhd", score_grad, key_block, preferred_element_type=jnp.float32)
            * score_scale
        )
        key_part = (
            jnp.einsum("hqk,qhd->khd", score_grad, query_block, preferred_element_type=jnp.float32)
            * score_scale
        )
        value_part = jnp.einsum(
            "hqk,qhd->khd",
            chances.astype(jnp.bfloat16),
            grad_block,
            preferred_element_type=jnp.float32,
        )
        key_grad = lax.dynamic_update_slice_in_dim(
            key_grad,
            lax.dynamic_slice_in_dim(key_grad, first_row, key_span, 0) + key_part,
            first_row,
            0,
        )
        value_grad = lax.dynamic_update_slice_in_dim(
            value_grad,
            lax.dynamic_slice_in_dim(value_grad, first_row, key_span, 0) + value_part,
            first_row,
            0,
        )
        return ((key_grad, value_grad), query_grad)

    empty_grad = jnp.zeros((token_count + WINDOW, head_count, head_width), jnp.float32)
    (key_grad, value_grad), query_grad = lax.scan(
        one_block,
        (empty_grad, empty_grad),
        (jnp.arange(token_count // block_rows, dtype=jnp.int32), logsum),
    )
    flat_width = head_count * head_width
    return (
        query_grad.reshape(token_count, flat_width).astype(jnp.bfloat16),
        key_grad[WINDOW:].reshape(token_count, flat_width).astype(jnp.bfloat16),
        value_grad[WINDOW:].reshape(token_count, flat_width).astype(jnp.bfloat16),
    )


def local(
    tokens,
    cotangent,
    route,
    lengths,
    key_mask,
    norm1_gain,
    norm2_gain,
    w_query,
    w_key,
    w_value,
    w_out,
    w_gate,
    w_up,
    w_down,
):
    groups = lax.axis_size("dp")
    members = lax.axis_size("mp")
    member = lax.axis_index("mp")
    local_rows = tokens.shape[0]
    group_rows = local_rows * members
    bucket = local_rows // groups
    target = route // TOK_DEV
    chosen = (target[:, None] == jnp.arange(groups, dtype=jnp.int32)[None, :]).astype(jnp.int32)
    ranking = jnp.sum((jnp.cumsum(chosen, axis=0) - chosen) * chosen, axis=1)
    send_at = target * bucket + ranking
    arrival, arrival_grad, arrival_slot = (
        lax.all_to_all(
            jnp.zeros_like(tokens).at[send_at].set(tokens),
            "dp",
            split_axis=0,
            concat_axis=0,
            tiled=True,
        ),
        lax.all_to_all(
            jnp.zeros_like(cotangent).at[send_at].set(cotangent),
            "dp",
            split_axis=0,
            concat_axis=0,
            tiled=True,
        ),
        lax.all_to_all(
            jnp.zeros_like(route).at[send_at].set(route % local_rows),
            "dp",
            split_axis=0,
            concat_axis=0,
            tiled=True,
        ),
    )
    token_rows = jnp.zeros_like(arrival).at[arrival_slot].set(arrival)
    grad_rows = jnp.zeros_like(arrival_grad).at[arrival_slot].set(arrival_grad)
    seq_ends = jnp.cumsum(lengths[0])
    positions = jnp.arange(group_rows, dtype=jnp.int32)
    segment = jnp.sum((positions[:, None] >= seq_ends[None, :]).astype(jnp.int32), axis=1)
    input_rows = token_rows.astype(jnp.float32)
    normed_one, inverse_one = norm_rows(input_rows)
    leading_all, grad_all = (
        lax.all_gather(token_rows, "mp", axis=0, tiled=True),
        lax.all_gather(grad_rows, "mp", axis=0, tiled=True),
    )
    input_all = leading_all.astype(jnp.float32)
    normed_all, _ = norm_rows(input_all)
    hidden_one = (normed_all * norm1_gain).astype(jnp.bfloat16)
    head_count = w_query.shape[1] // HEAD_DIM
    query = jnp.dot(hidden_one, w_query, preferred_element_type=jnp.float32).astype(jnp.bfloat16)
    keys = jnp.dot(hidden_one, w_key, preferred_element_type=jnp.float32).astype(jnp.bfloat16)
    values = jnp.dot(hidden_one, w_value, preferred_element_type=jnp.float32).astype(jnp.bfloat16)
    query_heads = query.reshape(group_rows, head_count, HEAD_DIM)
    key_heads = keys.reshape(group_rows, head_count, HEAD_DIM)
    value_heads = values.reshape(group_rows, head_count, HEAD_DIM)
    mixed_flat, logsum = attend_forward(query_heads, key_heads, value_heads, segment, key_mask)
    attention_all = lax.psum(jnp.dot(mixed_flat, w_out, preferred_element_type=jnp.float32), "mp")
    middle_all = input_all + attention_all
    middle_rows = lax.dynamic_slice_in_dim(middle_all, member * local_rows, local_rows, 0)
    normed_mid, _ = norm_rows(middle_all)
    hidden_two = (normed_mid * norm2_gain).astype(jnp.bfloat16)
    normed_two, inverse_two = norm_rows(middle_rows)
    gate_value = jnp.dot(hidden_two, w_gate, preferred_element_type=jnp.float32)
    upward = jnp.dot(hidden_two, w_up, preferred_element_type=jnp.float32)
    sigmoid = jax.nn.sigmoid(gate_value)
    activated = (gate_value * sigmoid * upward).astype(jnp.bfloat16)
    out_rows = middle_rows + lax.psum_scatter(
        jnp.dot(activated, w_down, preferred_element_type=jnp.float32).astype(jnp.bfloat16),
        "mp",
        scatter_dimension=0,
        tiled=True,
    ).astype(jnp.float32)
    activated_grad = jnp.einsum("td,fd->tf", grad_all, w_down, preferred_element_type=jnp.float32)
    gate_grad = (activated_grad * upward * sigmoid * (1.0 + gate_value * (1.0 - sigmoid))).astype(
        jnp.bfloat16
    )
    upward_grad = (activated_grad * gate_value * sigmoid).astype(jnp.bfloat16)
    down_sum = jnp.einsum("tf,td->fd", activated, grad_all, preferred_element_type=jnp.float32)
    gate_sum = jnp.einsum("td,tf->df", hidden_two, gate_grad, preferred_element_type=jnp.float32)
    upward_sum = jnp.einsum(
        "td,tf->df", hidden_two, upward_grad, preferred_element_type=jnp.float32
    )
    hidden_two_grad = lax.psum_scatter(
        jnp.einsum("tf,df->td", gate_grad, w_gate, preferred_element_type=jnp.float32)
        + jnp.einsum("tf,df->td", upward_grad, w_up, preferred_element_type=jnp.float32),
        "mp",
        scatter_dimension=0,
        tiled=True,
    )
    norm_part_two, gain_two_grad = norm_back(hidden_two_grad, normed_two, inverse_two, norm2_gain)
    middle_grad = grad_rows.astype(jnp.float32) + norm_part_two
    branch_all = lax.all_gather(middle_grad.astype(jnp.bfloat16), "mp", axis=0, tiled=True)
    output_sum = jnp.einsum("tc,td->cd", mixed_flat, branch_all, preferred_element_type=jnp.float32)
    mixed_grad = jnp.einsum(
        "td,cd->tc", branch_all, w_out, preferred_element_type=jnp.float32
    ).astype(jnp.bfloat16)
    query_grad, key_grad, value_grad = attend_backward(
        query_heads,
        key_heads,
        value_heads,
        segment,
        key_mask,
        logsum,
        mixed_grad.reshape(group_rows, head_count, HEAD_DIM),
    )
    query_sum = jnp.einsum("td,tc->dc", hidden_one, query_grad, preferred_element_type=jnp.float32)
    key_sum = jnp.einsum("td,tc->dc", hidden_one, key_grad, preferred_element_type=jnp.float32)
    value_sum = jnp.einsum("td,tc->dc", hidden_one, value_grad, preferred_element_type=jnp.float32)
    hidden_one_grad = lax.psum_scatter(
        (
            jnp.einsum("tc,dc->td", query_grad, w_query, preferred_element_type=jnp.float32)
            + jnp.einsum("tc,dc->td", key_grad, w_key, preferred_element_type=jnp.float32)
            + jnp.einsum("tc,dc->td", value_grad, w_value, preferred_element_type=jnp.float32)
        ).astype(jnp.bfloat16),
        "mp",
        scatter_dimension=0,
        tiled=True,
    ).astype(jnp.float32)
    norm_part_one, gain_one_grad = norm_back(hidden_one_grad, normed_one, inverse_one, norm1_gain)
    input_grad = middle_grad + norm_part_one
    gain_one_sum, gain_two_sum = lax.psum((gain_one_grad, gain_two_grad), ("dp", "mp"))
    weight_sums = (
        lax.psum(query_sum.astype(jnp.bfloat16), "dp").astype(jnp.float32),
        lax.psum(key_sum.astype(jnp.bfloat16), "dp").astype(jnp.float32),
        lax.psum(value_sum.astype(jnp.bfloat16), "dp").astype(jnp.float32),
        lax.psum(output_sum.astype(jnp.bfloat16), "dp").astype(jnp.float32),
        lax.psum(gate_sum.astype(jnp.bfloat16), "dp").astype(jnp.float32),
        lax.psum(upward_sum.astype(jnp.bfloat16), "dp").astype(jnp.float32),
        lax.psum(down_sum.astype(jnp.bfloat16), "dp").astype(jnp.float32),
    )
    back_out, back_grad = (
        lax.all_to_all(
            out_rows.astype(jnp.bfloat16)[arrival_slot],
            "dp",
            split_axis=0,
            concat_axis=0,
            tiled=True,
        ),
        lax.all_to_all(
            input_grad.astype(jnp.bfloat16)[arrival_slot],
            "dp",
            split_axis=0,
            concat_axis=0,
            tiled=True,
        ),
    )
    return (
        back_out[send_at],
        back_grad[send_at],
        gain_one_sum,
        gain_two_sum,
        weight_sums[0],
        weight_sums[1],
        weight_sums[2],
        weight_sums[3],
        weight_sums[4],
        weight_sums[5],
        weight_sums[6],
    )


MESH = pl.DeviceIdType.MESH
LANES = 128
F32 = jnp.float32
BF16 = jnp.bfloat16
VMEM_LIMIT = 56 * 1024 * 1024


def plane():
    me = lax.axis_index("dp")
    side = me + 1 - 2 * lax.rem(me, 2)
    over_x = me + 2 - 4 * lax.rem(lax.div(me, 2), 2)
    over_y = me + 4 - 8 * lax.rem(lax.div(me, 4), 2)
    corner = over_x + 4 - 8 * lax.rem(lax.div(over_x, 4), 2)
    return (me, side, over_x, over_y, corner)


def to_dp(source, target, send_sem, recv_sem, index):
    return pltpu.make_async_remote_copy(
        src_ref=source,
        dst_ref=target,
        send_sem=send_sem,
        recv_sem=recv_sem,
        device_id={"dp": index},
        device_id_type=MESH,
    )


def to_mp(source, target, send_sem, recv_sem, index):
    return pltpu.make_async_remote_copy(
        src_ref=source,
        dst_ref=target,
        send_sem=send_sem,
        recv_sem=recv_sem,
        device_id={"mp": index},
        device_id_type=MESH,
    )


def greet_plane():
    _, side, over_x, over_y, _ = plane()
    barrier = pltpu.get_barrier_semaphore()
    for other in (side, over_x, over_y):
        pl.semaphore_signal(barrier, inc=1, device_id={"dp": other}, device_id_type=MESH)
    return barrier


def owner_at(turn):
    me, side, over_x, over_y, _ = plane()
    block = turn // 2
    near = ((block + 1) // 2) % 2
    far = block // 3
    second = turn % 2
    other = (1 - near) * second + (block // 2) * near
    owner = me + (near * (1 - second) + far) * (over_x - me)
    return owner + (near * second + far) * (over_y - me) + other * (side - me)


ARRIVALS = (
    (1, (4,)),
    (2, (0, 1, 2)),
    (3, (3,)),
    (4, (6, 9)),
    (5, (8, 10)),
    (6, (5, 7)),
    (7, (11, 12)),
)


class Gather:
    AFTER = {0: (5, 6), 1: (7, 8), 2: (9,), 3: (10,), 5: (11,), 7: (12,)}

    def __init__(self, own, out, send, recv, local=None):
        me, side, over_x, over_y, corner = plane()
        half = out.shape[1] // 2
        low, high = pl.ds(0, half), pl.ds(half, half)
        self.keep = None if own is None else pltpu.make_async_copy(own, out.at[me], local)
        own = out.at[me] if own is None else own

        def hop(number, source, target, index):
            return to_dp(source, target, send.at[number], recv.at[number], index)

        def onward(number, owner, part, index):
            place = out.at[owner, part]
            return hop(number, place, place, index)

        self.copies = [
            hop(0, own.at[low], out.at[me, low], over_x),
            hop(1, own.at[high], out.at[me, high], over_y),
            hop(2, own.at[high], out.at[me, high], over_x),
            hop(3, own.at[low], out.at[me, low], over_y),
            hop(4, own, out.at[me], side),
            onward(5, over_x, low, over_y),
            onward(6, over_x, low, side),
            onward(7, over_y, high, over_x),
            onward(8, over_y, high, side),
            onward(9, over_x, high, side),
            onward(10, over_y, low, side),
            onward(11, corner, low, side),
            onward(12, corner, high, side),
        ]

    def start(self):
        for number in range(5):
            self.copies[number].start()
        if self.keep is not None:
            self.keep.start()

    def arrive(self, *numbers):
        for number in numbers:
            self.copies[number].wait_recv()
            for later in self.AFTER.get(number, ()):
                self.copies[later].start()

    def pass_on(self):
        self.arrive(0, 1, 2, 3)

    def sent(self):
        for copy in self.copies:
            copy.wait_send()
        if self.keep is not None:
            self.keep.wait()

    def finish(self):
        self.arrive(5, 7, 4, 6, 8, 9, 10, 11, 12)
        self.sent()


def greet_all(barrier):
    me, z = lax.axis_index("dp"), lax.axis_index("mp")
    for step in range(1, 8):
        pl.semaphore_signal(
            barrier, inc=1, device_id={"dp": lax.rem(me + step, 8)}, device_id_type=MESH
        )
    core = lax.rem(me, 2)
    for step in range(1, 4):
        for other in (me, me + 1 - 2 * core):
            pl.semaphore_signal(
                barrier,
                inc=1,
                device_id={"dp": other, "mp": lax.rem(z + step, 4)},
                device_id_type=MESH,
            )
    pl.semaphore_wait(barrier, 13)


def swap_all(source, target, send, recv):
    me = lax.axis_index("dp")
    return [
        to_dp(source, target.at[me], send.at[step - 1], recv.at[step - 1], lax.rem(me + step, 8))
        for step in range(1, 8)
    ]


class Spread:
    def __init__(self, share, w_qkv, w_out, send, recv, local):
        me, z = lax.axis_index("dp"), lax.axis_index("mp")
        core = lax.rem(me, 2)
        self.place = z + core * (3 - 2 * z)
        self.send, self.recv, self.local = send, recv, local
        self.shares = [share.at[0], share.at[1], share.at[2], share.at[3]]
        self.slots = (core, 1 - core)
        self.core = core
        self.w_qkv, self.w_out = w_qkv, w_out

    def target(self, which, piece):
        slot = self.slots[which]
        block = slot if piece == 3 else 2 * piece + slot
        rows = pl.ds(pl.multiple_of(block * LANES, LANES), HEAD_DIM)
        return (self.w_out if piece == 3 else self.w_qkv).at[rows]

    def hop(self, which, piece, number, place, own):
        source = self.shares[piece] if own else self.target(which, piece)
        z = place + self.core * (3 - 2 * place)
        return to_mp(
            source,
            self.target(which, piece),
            self.send.at[number * 4 + piece],
            self.recv.at[which * 4 + piece],
            z,
        )

    def keep(self, which, piece):
        return pltpu.make_async_copy(
            self.shares[piece], self.target(which, piece), self.local.at[piece]
        )

    def start(self):
        @pl.when(self.place == 0)
        def _():
            for piece in range(4):
                self.hop(0, piece, 0, 1, True).start()
                self.keep(0, piece).start()

        @pl.when(self.place == 1)
        def _():
            for piece in range(4):
                self.hop(1, piece, 0, 0, True).start()
                self.hop(1, piece, 1, 2, True).start()
                self.keep(1, piece).start()

    def pass_on(self):
        @pl.when(self.place == 1)
        def _():
            for piece in range(4):
                self.hop(0, piece, 2, 2, False).wait_recv()
                self.hop(0, piece, 2, 2, False).start()

        @pl.when(self.place == 2)
        def _():
            for piece in range(4):
                for which in (1, 0):
                    self.hop(which, piece, which, 3, False).wait_recv()
                    self.hop(which, piece, which, 3, False).start()

    def finish(self):
        @pl.when(self.place == 0)
        def _():
            for piece in range(4):
                self.hop(1, piece, 0, 1, False).wait_recv()
                self.hop(0, piece, 0, 1, True).wait_send()
                self.keep(0, piece).wait()

        @pl.when(self.place == 1)
        def _():
            for piece in range(4):
                self.hop(1, piece, 0, 0, True).wait_send()
                self.hop(1, piece, 1, 2, True).wait_send()
                self.hop(0, piece, 2, 2, False).wait_send()
                self.keep(1, piece).wait()

        @pl.when(self.place == 2)
        def _():
            for piece in range(4):
                for which in (1, 0):
                    self.hop(which, piece, which, 3, False).wait_send()

        @pl.when(self.place == 3)
        def _():
            for piece in range(4):
                for which in (1, 0):
                    self.hop(which, piece, which, 3, False).wait_recv()


def first_kernel(
    hidden, query, keys, values, project, gate, upward, down, notes,
    hidden_all, w_qkv, w_out, notes_all, both_own, down_own,
    share, none, send_a, recv_a, send_w, recv_w, send_n, recv_n, local,
):
    me = lax.axis_index("dp")
    head = pl.ds(pl.multiple_of(lax.div(me, 2) * HEAD_DIM, 16), HEAD_DIM)
    loads = [
        pltpu.make_async_copy(source.at[head], share.at[piece], local.at[piece])
        for piece, source in enumerate((query, keys, values, project))
    ]
    units = pl.ds(pl.multiple_of(me * LANES, LANES), LANES)
    loads += [
        pltpu.make_async_copy(gate.at[:, units], both_own.at[:, pl.ds(0, LANES)], local.at[14]),
        pltpu.make_async_copy(upward.at[:, units], both_own.at[:, pl.ds(LANES, LANES)], local.at[15]),
        pltpu.make_async_copy(down.at[units], down_own, local.at[16]),
    ]
    for copy in loads:
        copy.start()
    none[...] = jnp.zeros_like(none)
    greet_all(pltpu.get_barrier_semaphore())
    gather = Gather(hidden, hidden_all, send_a, recv_a, local.at[4])
    gather.start()
    swaps = swap_all(notes, notes_all, send_n, recv_n)
    for copy in swaps:
        copy.start()
    keep = pltpu.make_async_copy(notes, notes_all.at[me], local.at[5])
    keep.start()
    pads = [
        pltpu.make_async_copy(
            none, weight.at[pl.ds(block * LANES + HEAD_DIM, LANES - HEAD_DIM)], local.at[6 + number]
        )
        for number, (weight, block) in enumerate(
            [(w_qkv, block) for block in range(6)] + [(w_out, block) for block in range(2)]
        )
    ]
    for copy in pads:
        copy.start()
    for copy in loads[:4]:
        copy.wait()
    spread = Spread(share, w_qkv, w_out, send_w, recv_w, local)
    spread.start()
    spread.pass_on()
    gather.pass_on()
    gather.finish()
    spread.finish()
    for copy in swaps:
        copy.wait()
    for copy in pads + loads[4:]:
        copy.wait()
    keep.wait()


def anywhere():
    return pl.BlockSpec(memory_space=pl.ANY)


def on_chip():
    return pl.BlockSpec(memory_space=pltpu.VMEM)


def in_scalar():
    return pl.BlockSpec(memory_space=pltpu.SMEM)


def remote_params(number, limit=VMEM_LIMIT):
    return pltpu.CompilerParams(
        collective_id=number, has_side_effects=True, vmem_limit_bytes=limit
    )


def gather_first(hidden, query, keys, values, project, gate, upward, down, notes):
    rows, width = hidden.shape
    groups = lax.axis_size("dp")
    dma = pltpu.SemaphoreType.DMA
    return pl.pallas_call(
        first_kernel,
        out_shape=(
            jax.ShapeDtypeStruct((groups, rows, width), BF16),
            jax.ShapeDtypeStruct((6 * LANES, width), BF16),
            jax.ShapeDtypeStruct((2 * LANES, width), BF16),
            jax.ShapeDtypeStruct((groups,) + notes.shape, notes.dtype),
            jax.ShapeDtypeStruct((width, 2 * LANES), BF16),
            jax.ShapeDtypeStruct((LANES, width), BF16),
        ),
        in_specs=[on_chip()] + [anywhere()] * 7 + [on_chip()],
        out_specs=(anywhere(),) * 4 + (on_chip(),) * 2,
        scratch_shapes=[
            pltpu.VMEM((4, HEAD_DIM, width), BF16),
            pltpu.VMEM((LANES - HEAD_DIM, width), BF16),
            dma((13,)), dma((13,)), dma((12,)), dma((8,)), dma((7,)), dma((7,)), dma((17,)),
        ],
        compiler_params=remote_params(1),
        cost_estimate=pl.CostEstimate(flops=0, bytes_accessed=200_000_000, transcendentals=0),
        name="gather_first",
    )(hidden, query, keys, values, project, gate, upward, down, notes)


def one_hot(slots, k, size):
    row = slots[pl.ds(k, 1), :]
    place = lax.broadcasted_iota(jnp.int32, (size, size), 0)
    return (place == row).astype(BF16)


def block_mask(lengths, flags, k, block, z, rows):
    position = rows * z + block * 128 + lax.broadcasted_iota(jnp.int32, (128, 1), 0)
    first_end = lengths[k, 0]
    second_end = first_end + lengths[k, 1]
    begin = jnp.where(position >= first_end, first_end, 0)
    begin = jnp.where(position >= second_end, second_end, begin)
    column = lax.broadcasted_iota(jnp.int32, (128, 192), 1)
    distance = 64 + lax.broadcasted_iota(jnp.int32, (128, 192), 0) - column
    key_position = rows * z + block * 128 - 64 + column
    live = flags[pl.ds(k, 1), block * 128 : block * 128 + 192]
    allowed = (distance >= 0) & (distance < WINDOW) & (key_position >= begin)
    return allowed & ((live == 1) | (distance == 0))


NT = (((1,), (1,)), ((), ()))
TN = (((0,), (0,)), ((), ()))


def forward_kernel(
    lengths, hidden_all, w_qkv, slots, flags, cotangent, mixed, kept, cotangent_all,
    qkv, shard, shard_sem, send, recv, send_g, recv_g, local, *, scale, groups, rows
):
    z = lax.axis_index("mp")
    members = lax.axis_size("mp")
    barrier = greet_plane()

    @pl.when(z > 0)
    def _():
        pl.semaphore_signal(barrier, inc=1, device_id={"mp": z - 1}, device_id_type=MESH)

    @pl.when(z < members - 1)
    def _():
        pl.semaphore_wait(barrier, 4)

    @pl.when(z == members - 1)
    def _():
        pl.semaphore_wait(barrier, 3)

    gather = Gather(cotangent, cotangent_all, send_g, recv_g, local)
    gather.start()

    def load(g):
        slot = lax.rem(g, 2)
        return pltpu.make_async_copy(hidden_all.at[g], shard.at[slot], shard_sem.at[slot])

    load(0).start()

    def multiply(g, carry):
        @pl.when(g < groups - 1)
        def _():
            load(g + 1).start()

        load(g).wait()
        product = lax.dot_general(
            shard[lax.rem(g, 2)], w_qkv[...], NT, preferred_element_type=F32
        ).astype(BF16)
        qkv[g] = product.reshape(groups, rows // groups, 768)
        return carry

    lax.fori_loop(0, groups, multiply, 0)

    def halo(k, other):
        return to_mp(
            kept.at[k, pl.ds(rows, 64), pl.ds(256, 512)],
            kept.at[k, pl.ds(0, 64), pl.ds(256, 512)],
            send.at[k],
            recv.at[k],
            other,
        )

    def order(k, carry):
        hot = one_hot(slots, k, rows)
        given = qkv[:, pl.ds(k, 1)].reshape(rows, 768)
        kept[k, pl.ds(64, rows), :] = jnp.dot(hot, given, preferred_element_type=F32).astype(BF16)
        kept[k, pl.ds(0, 64), pl.ds(0, 256)] = jnp.zeros((64, 256), BF16)

        @pl.when(z < members - 1)
        def _():
            halo(k, z + 1).start()

        @pl.when(z == 0)
        def _():
            kept[k, pl.ds(0, 64), pl.ds(256, 512)] = jnp.zeros((64, 512), BF16)

        return carry

    lax.fori_loop(0, groups, order, 0)

    def attend(k, carry):
        @pl.when(z > 0)
        def _():
            halo(k, z).wait_recv()

        hot = one_hot(slots, k, rows)
        found = []
        for block in range(rows // 128):
            allowed = block_mask(lengths, flags, k, block, z, rows)
            heads = []
            for head in range(2):
                query = kept[k, pl.ds(64 + block * 128, 128), pl.ds(head * 128, 128)]
                keys = kept[k, pl.ds(block * 128, 192), pl.ds(256 + head * 128, 128)]
                values = kept[k, pl.ds(block * 128, 192), pl.ds(512 + head * 128, 128)]
                scores = lax.dot_general(query, keys, NT, preferred_element_type=F32) * scale
                scores = jnp.where(allowed, scores, -MASKED)
                weights = jnp.exp(scores - jnp.max(scores, axis=-1, keepdims=True))
                total = jnp.sum(weights, axis=-1, keepdims=True)
                chances = (weights / total).astype(BF16)
                heads.append(jnp.dot(chances, values, preferred_element_type=F32).astype(BF16))
            found.append(jnp.concatenate(heads, axis=1))
        ordered = jnp.concatenate(found, axis=0)
        back = lax.dot_general(hot, ordered, TN, preferred_element_type=F32).astype(BF16)
        mixed[:, pl.ds(k, 1)] = back.reshape(groups, 1, rows // groups, 256)
        return carry

    lax.fori_loop(0, groups // 4, attend, 0)
    gather.pass_on()
    lax.fori_loop(groups // 4, groups, attend, 0)
    gather.finish()

    @pl.when(z < members - 1)
    def _():
        def done(k, carry):
            halo(k, z + 1).wait_send()
            return carry

        lax.fori_loop(0, groups, done, 0)


def attend_ahead(lengths, hidden_all, w_qkv, slots, flags, cotangent, scale):
    groups, rows, width = hidden_all.shape
    dma = pltpu.SemaphoreType.DMA
    return pl.pallas_call(
        functools.partial(forward_kernel, scale=scale, groups=groups, rows=rows),
        out_shape=(
            jax.ShapeDtypeStruct((groups, groups, rows // groups, 256), BF16),
            jax.ShapeDtypeStruct((groups, rows + 64, 768), BF16),
            jax.ShapeDtypeStruct((groups,) + cotangent.shape, BF16),
        ),
        in_specs=[in_scalar(), anywhere()] + [on_chip()] * 4,
        out_specs=(on_chip(), on_chip(), anywhere()),
        scratch_shapes=[
            pltpu.VMEM((groups, groups, rows // groups, 768), BF16),
            pltpu.VMEM((2, rows, width), BF16),
            dma((2,)),
            dma((groups,)),
            dma((groups,)),
            dma((13,)),
            dma((13,)),
            dma(()),
        ],
        compiler_params=remote_params(2),
        cost_estimate=pl.CostEstimate(flops=0, bytes_accessed=200_000_000, transcendentals=0),
        name="attend_ahead",
    )(lengths, hidden_all, w_qkv, slots, flags, cotangent)


CHUNK = 32


def each_chunk(rows, body, chunk=CHUNK):
    def step(i, carry):
        body(pl.ds(pl.multiple_of(i * chunk, chunk), chunk))
        return carry

    lax.fori_loop(0, rows // chunk, step, 0)


class Reduce:
    COUNT = 10

    def __init__(self, left, right, across, part, from_side, from_corner, from_near, send, recv):
        self.left, self.right, self.across, self.part = left, right, across, part
        self.from_side, self.from_corner, self.from_near = from_side, from_corner, from_near
        self.send, self.recv = send, recv
        self.rows = part.shape[1]

    def product(self, owner, slot):
        rows, width = self.rows, self.part.shape[2]
        picked = pl.ds(pl.multiple_of(owner * rows, rows), rows)

        def tile(t, carry):
            columns = pl.ds(pl.multiple_of(t * 256, 256), 256)
            if self.across:
                value = lax.dot_general(
                    self.left[picked, :], self.right[columns, :], NT, preferred_element_type=F32
                )
            else:
                value = jnp.dot(
                    self.left[picked, :], self.right[:, columns], preferred_element_type=F32
                )
            self.part[slot, :, columns] = value.astype(BF16)
            return carry

        lax.fori_loop(0, width // 256, tile, 0)

    def prepare(self):
        _, side, over_x, over_y, corner = plane()
        part, near = self.part, self.from_near
        half = self.rows // 2
        low, high = pl.ds(0, half), pl.ds(half, half)

        def hop(number, source, target, index):
            return to_dp(source, target, self.send.at[number], self.recv.at[number], index)

        self.shares = [hop(i, part.at[4 + i], self.from_side.at[i], side) for i in range(4)]
        self.corners = [
            hop(4, part.at[0, low], self.from_corner.at[0], over_x),
            hop(5, part.at[0, high], self.from_corner.at[1], over_y),
        ]
        self.nears = [
            hop(6, part.at[1, low], near.at[0, low], over_x),
            hop(7, part.at[1, high], near.at[0, high], over_x),
            hop(8, part.at[2, high], near.at[1, high], over_y),
            hop(9, part.at[2, low], near.at[1, low], over_y),
        ]

    def add_side(self, slot):
        self.shares[slot].wait_recv()

        def body(span):
            self.part[slot, span, :] = (
                self.part[slot, span, :].astype(F32) + self.from_side[slot, span, :].astype(F32)
            ).astype(BF16)

        each_chunk(self.rows, body)

    def add_corner(self, slot, offset, which):
        self.corners[which].wait_recv()

        def body(span):
            target = pl.ds(pl.multiple_of(offset + span.start, CHUNK), CHUNK)
            self.part[slot, target, :] = (
                self.part[slot, target, :].astype(F32)
                + self.from_corner[which, span, :].astype(F32)
            ).astype(BF16)

        each_chunk(self.rows // 2, body)

    def products(self):
        self.prepare()
        me, _, over_x, over_y, corner = plane()
        turn = 1 - 2 * lax.rem(me, 2)
        for slot, owner in enumerate((corner, over_x, over_y, me)):
            self.product(owner + turn, 4 + slot)
            self.shares[slot].start()
        for slot, owner in enumerate((corner, over_x, over_y, me)):
            self.product(owner, slot)

    def launch(self):
        self.add_side(0)
        self.corners[0].start()
        self.corners[1].start()
        self.add_side(1)
        self.nears[0].start()
        self.add_side(2)
        self.nears[2].start()

    def begin(self):
        self.prepare()
        me, _, over_x, over_y, corner = plane()
        turn = 1 - 2 * lax.rem(me, 2)
        self.product(corner + turn, 4)
        self.shares[0].start()
        self.product(corner, 0)
        self.product(over_x + turn, 5)
        self.shares[1].start()
        self.add_side(0)
        self.corners[0].start()
        self.corners[1].start()
        self.product(over_x, 1)
        self.product(over_y + turn, 6)
        self.shares[2].start()
        self.add_side(1)
        self.nears[0].start()
        self.product(over_y, 2)
        self.product(me + turn, 7)
        self.shares[3].start()
        self.add_side(2)
        self.nears[2].start()
        self.product(me, 3)

    def middle(self):
        self.add_corner(2, 0, 0)
        self.nears[3].start()
        self.add_corner(1, self.rows // 2, 1)
        self.nears[1].start()

    def end(self):
        self.shares[3].wait_recv()
        for copy in self.nears:
            copy.wait_recv()

    def run(self):
        self.begin()
        self.middle()
        self.end()

    def rows_of(self, span):
        return (
            self.part[3, span, :].astype(F32)
            + self.from_side[3, span, :].astype(F32)
            + self.from_near[0, span, :].astype(F32)
            + self.from_near[1, span, :].astype(F32)
        )

    def finish(self):
        for copy in self.shares + self.corners + self.nears:
            copy.wait_send()


def reduce_scratch(rows, width):
    dma = pltpu.SemaphoreType.DMA
    return [
        pltpu.VMEM((8, rows, width), BF16),
        pltpu.VMEM((4, rows, width), BF16),
        pltpu.VMEM((2, rows // 2, width), BF16),
        pltpu.VMEM((2, rows, width), BF16),
        dma((10,)),
        dma((10,)),
    ]


def gather_scratch(rows, width):
    dma = pltpu.SemaphoreType.DMA
    return [pltpu.VMEM((rows, width), BF16), dma((13,)), dma((13,)), dma(())]


def mean_rows(values):
    return jnp.mean(values, axis=-1, keepdims=True)


class Heads:
    def __init__(self, source, stage, arrive, send, recv_stage, recv):
        me, z = lax.axis_index("dp"), lax.axis_index("mp")
        self.me, self.z = me, z
        self.core = lax.rem(me, 2)
        self.source, self.stage, self.arrive = source, stage, arrive
        self.send, self.recv_stage, self.recv = send, recv_stage, recv
        self.place = z + self.core * (3 - 2 * z)
        self.columns = source.shape[1] // 2

    def z_of(self, place):
        return place + self.core * (3 - 2 * place)

    def slot_of(self, place):
        return self.core if place == 0 else 1 - self.core

    def rows_of(self, place, kind):
        block = 2 * kind + self.slot_of(place)
        return self.source.at[pl.ds(pl.multiple_of(block * LANES, LANES), HEAD_DIM)]

    def half_of(self, ref, half):
        return ref.at[:, pl.ds(pl.multiple_of(half * self.columns, LANES), self.columns)]

    def to_stage(self, place, kind):
        return to_at(
            self.rows_of(place, kind),
            self.stage.at[place, kind],
            self.send.at[place * 4 + kind],
            self.recv_stage.at[place * 4 + kind],
            self.me,
            self.z_of(2),
        )

    def to_owner(self, place, kind, half, way, ref, number):
        return to_at(
            self.half_of(ref, half),
            self.arrive.at[way, kind],
            self.send.at[number],
            self.recv.at[way * 4 + kind],
            self.me - self.core + half,
            self.z_of(place),
        )

    def sums(self, kind):
        return [
            self.to_owner(
                place, kind, half, 2, self.stage.at[place, kind], place * 8 + kind * 2 + half
            )
            for place in (0, 1)
            for half in (0, 1)
        ]

    def cross(self, own, kind):
        other = 1 - own
        copies = [
            self.to_owner(other, kind, half, 0, self.rows_of(other, kind), kind * 2 + half)
            for half in (0, 1)
        ]
        copies.append(
            to_at(
                self.half_of(self.rows_of(own, kind), 1 - self.core),
                self.arrive.at[1, kind],
                self.send.at[8 + kind],
                self.recv.at[4 + kind],
                self.me + 1 - 2 * self.core,
                self.z,
            )
        )
        return copies

    def start(self, kinds):
        @pl.when(self.place == 3)
        def _():
            for kind in kinds:
                self.to_stage(0, kind).start()
                self.to_stage(1, kind).start()

        for own in (0, 1):
            @pl.when(self.place == own)
            def _():
                for kind in kinds:
                    for copy in self.cross(own, kind):
                        copy.start()

    def add(self, kinds):
        @pl.when(self.place == 2)
        def _():
            for kind in kinds:
                for place in (0, 1):
                    self.to_stage(place, kind).wait_recv()
                    mine = self.rows_of(place, kind)

                    def body(span):
                        self.stage[place, kind, span, :] = (
                            self.stage[place, kind, span, :].astype(F32)
                            + mine[span, :].astype(F32)
                        ).astype(BF16)

                    each_chunk(HEAD_DIM, body, 16)
                for copy in self.sums(kind):
                    copy.start()

    def total(self, out):
        owner = lax.div(self.z, 2) == self.core
        for kind in range(4):
            for own in (0, 1):
                @pl.when(self.place == own)
                def _():
                    self.arrive[1, kind] = self.half_of(self.rows_of(own, kind), self.core)[...]

            for way in range(3):
                waiting = to_at(
                    self.half_of(self.rows_of(0, kind), 0),
                    self.arrive.at[way, kind],
                    self.send.at[0],
                    self.recv.at[way * 4 + kind],
                    self.me,
                    lax.rem(self.z + 1, 4),
                )
                if way == 1:
                    pl.when(jnp.logical_not(owner))(waiting.wait_recv)
                else:
                    waiting.wait_recv()

            def body(span):
                found = self.arrive[0, kind, span, :].astype(F32)
                found = found + self.arrive[1, kind, span, :].astype(F32)
                found = found + self.arrive[2, kind, span, :].astype(F32)
                target = pl.ds(pl.multiple_of(kind * HEAD_DIM + span.start, 16), 16)
                out[target, :] = found.astype(BF16)

            each_chunk(HEAD_DIM, body, 16)

    def finish_send(self):
        for kind in range(4):
            @pl.when(self.place == 3)
            def _():
                self.to_stage(0, kind).wait_send()
                self.to_stage(1, kind).wait_send()

            @pl.when(self.place == 2)
            def _():
                for copy in self.sums(kind):
                    copy.wait_send()

            for own in (0, 1):
                @pl.when(self.place == own)
                def _():
                    for copy in self.cross(own, kind):
                        copy.wait_send()


def to_at(source, target, send_sem, recv_sem, dp, mp):
    return pltpu.make_async_remote_copy(
        src_ref=source,
        dst_ref=target,
        send_sem=send_sem,
        recv_sem=recv_sem,
        device_id={"dp": dp, "mp": mp},
        device_id_type=MESH,
    )


class Units:
    def __init__(self, both_sum, both_in, both_stage, send, recv, local):
        self.z = lax.axis_index("mp")
        self.sums = (both_sum,)
        self.inputs = (both_in,)
        self.stages = (both_stage,)
        self.send, self.recv, self.local = send, recv, local
        z = self.z
        self.outer = (z == 0) | (z == 3)
        self.far = 3 - z
        self.near = 1 + lax.div(z, 3)
        self.second = 3 - self.near
        self.edge = 3 * (z - 1)

    def part(self, kind, z):
        return self.sums[kind].at[z]

    def straight(self, kind, number, target):
        return to_mp(
            self.part(kind, target),
            self.inputs[kind].at[self.z],
            self.send.at[number * 2 + kind],
            self.recv.at[self.z * 2 + kind],
            target,
        )

    def staged(self, kind):
        return to_mp(
            self.part(kind, self.far),
            self.stages[kind].at[0],
            self.send.at[4 + kind],
            self.recv.at[8 + kind],
            self.near,
        )

    def summed(self, kind):
        return to_mp(
            self.stages[kind].at[1],
            self.inputs[kind].at[self.z],
            self.send.at[4 + kind],
            self.recv.at[self.z * 2 + kind],
            3 - self.edge,
        )

    def mine(self, kind):
        return pltpu.make_async_copy(
            self.part(kind, 3 - self.edge), self.stages[kind].at[1], self.local.at[kind]
        )

    def start(self):
        @pl.when(self.outer)
        def _():
            for kind in range(1):
                self.staged(kind).start()
            for kind in range(1):
                self.straight(kind, 0, self.near).start()
                self.straight(kind, 1, self.second).start()

        @pl.when(jnp.logical_not(self.outer))
        def _():
            for kind in range(1):
                self.mine(kind).start()
                self.straight(kind, 0, 3 - self.z).start()
                self.straight(kind, 1, self.edge).start()

    def add(self):
        @pl.when(jnp.logical_not(self.outer))
        def _():
            for kind in range(1):
                stage = self.stages[kind]
                self.mine(kind).wait()
                to_mp(
                    self.part(kind, 0),
                    stage.at[0],
                    self.send.at[4 + kind],
                    self.recv.at[8 + kind],
                    self.edge,
                ).wait_recv()

                def body(span):
                    stage[1, span, :] = (
                        stage[0, span, :].astype(F32) + stage[1, span, :].astype(F32)
                    ).astype(BF16)

                each_chunk(stage.shape[1], body)
                self.summed(kind).start()

    def arrived(self, kind, source):
        to_mp(
            self.part(kind, 0),
            self.inputs[kind].at[source],
            self.send.at[kind],
            self.recv.at[source * 2 + kind],
            source,
        ).wait_recv()

    def finish(self):
        @pl.when(self.outer)
        def _():
            for kind in range(1):
                self.arrived(kind, 1)
                self.arrived(kind, 2)
                self.straight(kind, 0, self.near).wait_send()
                self.straight(kind, 1, self.second).wait_send()
                self.staged(kind).wait_send()

        @pl.when(jnp.logical_not(self.outer))
        def _():
            for kind in range(1):
                self.arrived(kind, 0)
                self.arrived(kind, 3)
                self.arrived(kind, 3 - self.z)
                self.straight(kind, 0, 3 - self.z).wait_send()
                self.straight(kind, 1, self.edge).wait_send()
                self.summed(kind).wait_send()


def backward_kernel(
    lengths, kept, branch, w_out, slots, flags, activated, w_down, middle, both_sum, down_in,
    out, result, branch_all, both_in, down_all,
    totals, query_part, key_value, ending, leaving, arriving, send, recv,
    part, from_side, from_corner, from_near, send_r, recv_r,
    mixed_grad, shard, load_sem, send_g, recv_g,
    both_stage, send_u, recv_u, local, down_found, send_d, recv_d,
    *, scale, groups, rows,
):
    z = lax.axis_index("mp")
    members = lax.axis_size("mp")
    load_down = pltpu.make_async_copy(down_in, down_found, load_sem.at[2])
    load_down.start()
    greet_all(pltpu.get_barrier_semaphore())
    units = Units(both_sum, both_in, both_stage, send_u, recv_u, local)
    gather = Gather(branch, branch_all, send_g, recv_g, local.at[2])
    gather.start()
    units.start()
    reduce = Reduce(activated, w_down, False, part, from_side, from_corner, from_near, send_r, recv_r)
    reduce.products()
    load_down.wait()

    def add_down(span):
        value = down_found[0, span, :].astype(F32) + down_found[1, span, :].astype(F32)
        value = value + down_found[2, span, :].astype(F32) + down_found[3, span, :].astype(F32)
        down_found[0, span, :] = value.astype(BF16)

    each_chunk(down_found.shape[1], add_down)
    down = Gather(down_found.at[0], down_all, send_d, recv_d, local.at[1])

    def load_shard(turn):
        slot = turn % 2
        return pltpu.make_async_copy(branch_all.at[owner_at(turn)], shard.at[slot], load_sem.at[slot])

    def spread_back(turn, carry):
        for number, numbers in ARRIVALS:
            pl.when(turn == number)(functools.partial(gather.arrive, *numbers))

        @pl.when(turn == 0)
        def _():
            gather.keep.wait()

        load_shard(turn).start()
        load_shard(turn).wait()
        mixed_grad[owner_at(turn)] = (
            lax.dot_general(shard[turn % 2], w_out[...], NT, preferred_element_type=F32)
            .astype(BF16)
            .reshape(groups, rows // groups, 256)
        )
        return carry

    lax.fori_loop(0, 8, spread_back, 0)
    reduce.launch()
    down.start()
    units.add()


    def halo(k, other):
        return to_mp(leaving.at[k], arriving.at[k], send.at[k], recv.at[k], other)

    def attend(k, carry):
        hot = one_hot(slots, k, rows)
        given = mixed_grad[:, pl.ds(k, 1)].reshape(rows, 256)
        grad_ordered = jnp.dot(hot, given, preferred_element_type=F32).astype(BF16)
        totals[...] = jnp.zeros_like(totals)
        for block in range(rows // 128):
            allowed = block_mask(lengths, flags, k, block, z, rows)
            for head in range(2):
                query = kept[k, pl.ds(64 + block * 128, 128), pl.ds(head * 128, 128)]
                keys = kept[k, pl.ds(block * 128, 192), pl.ds(256 + head * 128, 128)]
                values = kept[k, pl.ds(block * 128, 192), pl.ds(512 + head * 128, 128)]
                grad = grad_ordered[block * 128 : block * 128 + 128, head * 128 : head * 128 + 128]
                scores = lax.dot_general(query, keys, NT, preferred_element_type=F32) * scale
                scores = jnp.where(allowed, scores, -MASKED)
                weights = jnp.exp(scores - jnp.max(scores, axis=-1, keepdims=True))
                again = weights / jnp.sum(weights, axis=-1, keepdims=True)
                chance_grad = lax.dot_general(grad, values, NT, preferred_element_type=F32)
                row_dot = jnp.sum(again * chance_grad, axis=-1, keepdims=True)
                score_grad = (again * (chance_grad - row_dot)).astype(BF16)
                query_part[k, pl.ds(block * 128, 128), pl.ds(head * 128, 128)] = (
                    jnp.dot(score_grad, keys, preferred_element_type=F32) * scale
                ).astype(BF16)
                totals[pl.ds(block * 128, 192), pl.ds(head * 128, 128)] += (
                    lax.dot_general(score_grad, query, TN, preferred_element_type=F32) * scale
                )
                totals[pl.ds(block * 128, 192), pl.ds(256 + head * 128, 128)] += lax.dot_general(
                    again.astype(BF16), grad, TN, preferred_element_type=F32
                )
        key_value[k] = totals[pl.ds(64, rows), :].astype(BF16)
        ending[k] = totals[pl.ds(rows, 64), :]

        @pl.when(z > 0)
        def _():
            leaving[k] = totals[pl.ds(0, 64), :].astype(BF16)
            halo(k, z - 1).start()

        return carry

    lax.fori_loop(0, 3, attend, 0)
    reduce.middle()
    lax.fori_loop(3, 7, attend, 0)
    down.pass_on()
    lax.fori_loop(7, groups, attend, 0)

    def restore(k, carry):
        @pl.when(z < members - 1)
        def _():
            halo(k, z).wait_recv()
            key_value[k, pl.ds(rows - 64, 64), :] = (
                ending[k] + arriving[k].astype(F32)
            ).astype(BF16)

        hot = one_hot(slots, k, rows)
        ordered = jnp.concatenate([query_part[k], key_value[k]], axis=1)
        back = lax.dot_general(hot, ordered, TN, preferred_element_type=F32).astype(BF16)
        out[:, pl.ds(k, 1)] = back.reshape(groups, 1, rows // groups, 768)
        return carry

    lax.fori_loop(0, groups, restore, 0)
    reduce.end()

    def body(span):
        result[span, :] = (middle[span, :] + reduce.rows_of(span)).astype(BF16)

    each_chunk(rows, body)
    down.finish()
    units.finish()
    for copy in gather.copies:
        copy.wait_send()
    reduce.finish()

    @pl.when(z > 0)
    def _():
        def done(k, carry):
            halo(k, z - 1).wait_send()
            return carry

        lax.fori_loop(0, groups, done, 0)


def attend_back(
    lengths, kept, branch, w_out, slots, flags, activated, w_down, middle, both_sum, down_in, scale
):
    groups = kept.shape[0]
    rows, width = middle.shape
    members = both_sum.shape[0]
    dma = pltpu.SemaphoreType.DMA
    shape = jax.ShapeDtypeStruct
    return pl.pallas_call(
        functools.partial(backward_kernel, scale=scale, groups=groups, rows=rows),
        out_shape=(
            shape((groups, groups, rows // groups, 768), BF16),
            shape((rows, width), BF16),
            shape((groups, rows, width), BF16),
            shape((members, width, 256), BF16),
            shape((groups, LANES, width), BF16),
        ),
        in_specs=[in_scalar()] + [on_chip()] * 8 + [anywhere()] * 2,
        out_specs=(on_chip(),) * 2 + (anywhere(),) * 3,
        scratch_shapes=[
            pltpu.VMEM((rows + 64, 512), F32),
            pltpu.VMEM((groups, rows, 256), BF16),
            pltpu.VMEM((groups, rows, 512), BF16),
            pltpu.VMEM((groups, 64, 512), F32),
            pltpu.VMEM((groups, 64, 512), BF16),
            pltpu.VMEM((groups, 64, 512), BF16),
            dma((groups,)),
            dma((groups,)),
        ]
        + reduce_scratch(rows, width)
        + [
            pltpu.VMEM((groups, groups, rows // groups, 256), BF16),
            pltpu.VMEM((2, rows, width), BF16),
            dma((3,)),
            dma((13,)),
            dma((13,)),
            pltpu.VMEM((2, width, 256), BF16),
            dma((6,)),
            dma((10,)),
            dma((3,)),
            pltpu.VMEM((members, LANES, width), BF16),
            dma((13,)),
            dma((13,)),
        ],
        compiler_params=remote_params(3, 63 * 1024 * 1024),
        cost_estimate=pl.CostEstimate(flops=0, bytes_accessed=300_000_000, transcendentals=0),
        name="attend_back",
    )(lengths, kept, branch, w_out, slots, flags, activated, w_down, middle, both_sum, down_in)


def middle_kernel(
    mixed, w_out, tokens, gain, middle, hidden,
    part, from_side, from_corner, from_near, send, recv,
):
    pl.semaphore_wait(greet_plane(), 3)
    reduce = Reduce(mixed, w_out, False, part, from_side, from_corner, from_near, send, recv)
    reduce.run()

    def body(span):
        values = tokens[span, :].astype(F32) + reduce.rows_of(span)
        middle[span, :] = values
        inverse = lax.rsqrt(mean_rows(values * values) + EPSILON)
        hidden[span, :] = (values * inverse * gain[...]).astype(BF16)

    each_chunk(hidden.shape[0], body)
    reduce.finish()


def project_middle(mixed, w_out, tokens, gain):
    rows, width = tokens.shape
    return pl.pallas_call(
        middle_kernel,
        out_shape=(
            jax.ShapeDtypeStruct((rows, width), F32),
            jax.ShapeDtypeStruct((rows, width), BF16),
        ),
        in_specs=[on_chip()] * 4,
        out_specs=(on_chip(), on_chip()),
        scratch_shapes=reduce_scratch(rows, width),
        compiler_params=remote_params(4),
        cost_estimate=pl.CostEstimate(flops=0, bytes_accessed=150_000_000, transcendentals=0),
        name="project_middle",
    )(mixed, w_out, tokens, gain)


def norm_back_rows(gradient, values, gain, sums, span):
    inverse = lax.rsqrt(mean_rows(values * values) + EPSILON)
    normed = values * inverse
    product = gradient * normed
    folded = product[0:8]
    for step in range(1, CHUNK // 8):
        folded = folded + product[step * 8 : step * 8 + 8]
    sums[...] += folded
    scaled = gradient * gain
    return inverse * (scaled - normed * mean_rows(scaled * normed))


def feed_kernel(
    hidden_own, cotangent_all, middle, cotangent, gain, w_both, w_down,
    middle_grad, branch, sums, activated, both_sum, down_in,
    hidden_all, both_grad, part, from_side, from_corner, from_near, send_r, recv_r,
    send_a, recv_a, cot_half, cot_tile, stage_both, down_sum, load_sem, local, send_z, recv_z,
):
    groups, rows, width = hidden_all.shape
    members = w_both.shape[0]
    half_rows = rows // 2
    me, side, over_x, over_y, _ = plane()
    own = pltpu.make_async_copy(hidden_own, hidden_all.at[me], local.at[0])
    own.start()
    start_middle = pltpu.make_async_copy(middle, middle_grad, local.at[1])
    start_middle.start()

    def place_of(step):
        block = step // 4
        near = ((block + 1) // 2) % 2
        far = block // 3
        mixed_order = near * (1 - block // 2)
        second = mixed_order * (step % 2) + (1 - mixed_order) * ((step // 2) % 2)
        half = mixed_order * ((step % 2 + (step // 2) % 2) % 2) + (1 - mixed_order) * (step % 2)
        other = (1 - near) * second + (block // 2) * near
        in_x = near * (1 - second) + far
        in_y = near * second + far
        owner = me + in_x * (over_x - me) + in_y * (over_y - me) + other * (side - me)
        slot = 4 * other + 3 * (1 - near) * (1 - far) + near * (1 + second)
        return owner, half, slot

    def load_cotangent(step):
        owner, half, _ = place_of(step)
        span = pl.ds(pl.multiple_of(half * half_rows, half_rows), half_rows)
        return pltpu.make_async_copy(
            cotangent_all.at[owner, span], cot_half.at[step % 2], load_sem.at[step % 2]
        )

    load_cotangent(0).start()
    greet_all(pltpu.get_barrier_semaphore())
    own.wait()
    gather = Gather(None, hidden_all, send_a, recv_a)
    gather.start()
    reduce = Reduce(None, None, False, part, from_side, from_corner, from_near, send_r, recv_r)
    reduce.prepare()

    def before(step, *numbers):
        return (step, lambda: gather.arrive(*numbers))

    def nears():
        reduce.add_side(1)
        reduce.nears[0].start()
        reduce.add_side(2)
        reduce.nears[2].start()

    early = [
        before(2, 4),
        before(4, 0),
        before(5, 1),
        before(6, 2),
        before(7, 3),
        before(8, 6, 9),
        before(10, 8, 10),
        before(12, 5, 7),
        (13, nears),
        before(14, 11, 12),
    ]
    late = [(3, 3), (9, 1), (11, 2), (15, 0)]

    def unit(step, carry):
        for number, action in early:
            pl.when(step == number)(action)

        @pl.when(step < 15)
        def _():
            load_cotangent(step + 1).start()

        load_cotangent(step).wait()
        owner, half, slot = place_of(step)
        span = pl.ds(pl.multiple_of(half * half_rows, half_rows), half_rows)
        mine = hidden_all[owner, span, :]
        grads = cot_half[step % 2]
        for z in range(members):
            raw = jnp.dot(mine, w_both[z], preferred_element_type=F32)
            units = pl.ds(z * 128, 128)
            if z % 2 == 0:
                pair = lax.dot_general(
                    grads, w_down[pl.ds(z * 128, 256), :], NT, preferred_element_type=F32
                )
            active_grad = pair[:, 128 * (z % 2) : 128 * (z % 2) + 128]
            gate, upward = raw[:, :128], raw[:, 128:]
            sigmoid = jax.nn.sigmoid(gate)
            activated[owner, span, units] = (gate * sigmoid * upward).astype(BF16)
            both_grad[owner, span, pl.ds(z * 256, 128)] = (
                active_grad * upward * sigmoid * (1.0 + gate * (1.0 - sigmoid))
            ).astype(BF16)
            both_grad[owner, span, pl.ds(z * 256 + 128, 128)] = (
                active_grad * gate * sigmoid
            ).astype(BF16)

        def tile(t, inner):
            columns = pl.ds(pl.multiple_of(t * 256, 256), 256)
            value = sum(
                lax.dot_general(
                    both_grad[owner, span, pl.ds(z * 256, 256)],
                    w_both[z, columns, :],
                    NT,
                    preferred_element_type=F32,
                )
                for z in range(members)
            )
            part[slot, span, columns] = value.astype(BF16)
            return inner

        lax.fori_loop(0, width // 256, tile, 0)
        for number, share in late:
            pl.when(step == number)(reduce.shares[share].start)
        return carry

    lax.fori_loop(0, 16, unit, 0)

    def load_tile(t):
        columns = pl.ds(pl.multiple_of(t * 256, 256), 256)
        return pltpu.make_async_copy(
            cotangent_all.at[:, :, columns], cot_tile.at[t % 2], load_sem.at[2 + t % 2]
        )

    def store_both(t):
        columns = pl.ds(pl.multiple_of(t * 256, 256), 256)
        return pltpu.make_async_copy(
            stage_both.at[t % 2], both_sum.at[:, columns], load_sem.at[4 + t % 2]
        )

    tiles = width // 256
    count = groups * rows

    def down_tile(t, carry):
        columns = pl.ds(pl.multiple_of(t * 256, 256), 256)

        @pl.when(t < tiles - 1)
        def _():
            load_tile(t + 1).start()

        load_tile(t).wait()
        down_sum[:, columns] = lax.dot_general(
            activated[...].reshape(count, members * 128),
            cot_tile[t % 2].reshape(count, 256),
            TN,
            preferred_element_type=F32,
        ).astype(BF16)
        return carry

    z = lax.axis_index("mp")

    def down_rows(owner):
        return down_sum.at[pl.ds(pl.multiple_of(owner * LANES, LANES), LANES)]

    keep_down = pltpu.make_async_copy(down_rows(z), down_in.at[z], local.at[2])
    pass_down = [
        to_mp(
            down_rows(lax.rem(z + step, members)),
            down_in.at[z],
            send_z.at[step - 1],
            recv_z.at[step - 1],
            lax.rem(z + step, members),
        )
        for step in range(1, members)
    ]

    def weight_tile(t, carry):
        columns = pl.ds(pl.multiple_of(t * 256, 256), 256)

        @pl.when(t >= 2)
        def _():
            store_both(t - 2).wait()

        value = lax.dot_general(
            hidden_all[:, :, columns].reshape(count, 256),
            both_grad[...].reshape(count, members * 256),
            TN,
            preferred_element_type=F32,
        )
        for z in range(members):
            stage_both[t % 2, z] = value[:, z * 256 : z * 256 + 256].astype(BF16)
        store_both(t).start()
        return carry

    load_tile(0).start()
    reduce.add_side(0)
    reduce.corners[0].start()
    reduce.corners[1].start()
    lax.fori_loop(0, tiles, down_tile, 0)
    keep_down.start()
    for copy in pass_down:
        copy.start()
    lax.fori_loop(0, 2, weight_tile, 0)
    reduce.middle()
    lax.fori_loop(2, tiles, weight_tile, 0)
    reduce.end()
    start_middle.wait()
    sums[...] = jnp.zeros_like(sums)

    def body(span):
        change = norm_back_rows(reduce.rows_of(span), middle_grad[span, :], gain[...], sums, span)
        total = cotangent[span, :].astype(F32) + change
        middle_grad[span, :] = total
        branch[span, :] = total.astype(BF16)

    each_chunk(rows, body)
    gather.sent()
    reduce.finish()
    for t in (tiles - 2, tiles - 1):
        store_both(t).wait()
    keep_down.wait()
    for copy in pass_down:
        copy.wait()


def feed(hidden_own, cotangent_all, middle, cotangent, gain, w_both, w_down):
    groups, rows, width = cotangent_all.shape
    members = w_both.shape[0]
    dma = pltpu.SemaphoreType.DMA
    units = members * 128
    return pl.pallas_call(
        feed_kernel,
        out_shape=(
            jax.ShapeDtypeStruct((rows, width), F32),
            jax.ShapeDtypeStruct((rows, width), BF16),
            jax.ShapeDtypeStruct((8, width), F32),
            jax.ShapeDtypeStruct((groups, rows, units), BF16),
            jax.ShapeDtypeStruct((members, width, 256), BF16),
            jax.ShapeDtypeStruct((members, LANES, width), BF16),
        ),
        in_specs=[anywhere()] * 3 + [on_chip()] * 4,
        out_specs=(on_chip(),) * 4 + (anywhere(),) * 2,
        scratch_shapes=[
            pltpu.VMEM((groups, rows, width), BF16),
            pltpu.VMEM((groups, rows, 2 * units), BF16),
        ]
        + reduce_scratch(rows, width)
        + [
            dma((13,)),
            dma((13,)),
            pltpu.VMEM((2, rows // 2, width), BF16),
            pltpu.VMEM((2, groups, rows, 256), BF16),
            pltpu.VMEM((2, members, 256, 256), BF16),
            pltpu.VMEM((units, width), BF16),
            dma((6,)),
            dma((3,)),
            dma((3,)),
            dma((3,)),
        ],
        compiler_params=remote_params(5, 62 * 1024 * 1024),
        cost_estimate=pl.CostEstimate(flops=0, bytes_accessed=400_000_000, transcendentals=0),
        name="feed",
    )(hidden_own, cotangent_all, middle, cotangent, gain, w_both, w_down)


def input_kernel(
    qkv_grad, w_qkv, hidden_all, branch_all, mixed, tokens, middle_grad, gain, sums_two,
    both_sum, both_in,
    result, gains, both_all, heads_all,
    part, from_side, from_corner, from_near, send, recv, sums,
    stage, arrive, send_h, recv_s, recv_h, own, plane_sums, column_sums, send_p, recv_p,
    weight_sum, row_tile, tile_sem, send_b, recv_b, send_t, recv_t, both_found, heads_own, local,
):
    me, z = lax.axis_index("dp"), lax.axis_index("mp")
    count = qkv_grad.shape[0]
    tiles = tokens.shape[1] // 256
    outer = (z == 0) | (z == 3)

    def columns_of(t):
        return pl.ds(pl.multiple_of(lax.rem(t, tiles) * 256, 256), 256)

    def load(t, source):
        return pltpu.make_async_copy(
            source.at[:, :, columns_of(t)], row_tile.at[t % 2], tile_sem.at[t % 2]
        )

    own_part = pltpu.make_async_copy(both_sum.at[z], both_found.at[0], local.at[0])
    own_part.start()
    ways = [(outer, 1, 1), (outer, 2, 2)]
    ways += [(z == 1, 0, 1), (z == 1, 2, 2), (z == 1, 3, 3)]
    ways += [(z == 2, 0, 1), (z == 2, 1, 2), (z == 2, 3, 3)]

    def came(source, place):
        return pltpu.make_async_copy(both_in.at[source], both_found.at[place], local.at[place])

    for here, source, place in ways:
        pl.when(here)(came(source, place).start)

    @pl.when(outer)
    def _():
        both_found[3] = jnp.zeros_like(both_found[3])

    load(0, branch_all).start()
    greet_all(pltpu.get_barrier_semaphore())
    own_part.wait()
    for here, source, place in ways:
        pl.when(here)(came(source, place).wait)

    def add(span):
        value = both_found[0, span, :].astype(F32) + both_found[1, span, :].astype(F32)
        value = value + both_found[2, span, :].astype(F32) + both_found[3, span, :].astype(F32)
        both_found[0, span, :] = value.astype(BF16)

    each_chunk(both_found.shape[1], add)
    both = Gather(both_found.at[0], both_all, send_b, recv_b, local.at[4])
    both.start()

    def weight_tile(t, carry):
        @pl.when(t < tiles - 1)
        def _():
            load(t + 1, branch_all).start()

        @pl.when((t >= tiles - 1) & (t < 2 * tiles - 1))
        def _():
            load(t + 1, hidden_all).start()

        load(t, hidden_all).wait()

        @pl.when(t < tiles)
        def _():
            weight_sum[pl.ds(768, 256), columns_of(t)] = lax.dot_general(
                mixed[...], row_tile[t % 2].reshape(count, 256), TN, preferred_element_type=F32
            ).astype(BF16)

        @pl.when(t >= tiles)
        def _():
            weight_sum[pl.ds(0, 768), columns_of(t)] = lax.dot_general(
                qkv_grad[...], row_tile[t % 2].reshape(count, 256), TN, preferred_element_type=F32
            ).astype(BF16)

        return carry

    heads = Heads(weight_sum, stage, arrive, send_h, recv_s, recv_h)
    lax.fori_loop(0, tiles, weight_tile, 0)
    heads.start((3,))
    lax.fori_loop(tiles, 2 * tiles, weight_tile, 0)
    heads.start((0, 1, 2))
    reduce = Reduce(qkv_grad, w_qkv, False, part, from_side, from_corner, from_near, send, recv)
    reduce.begin()
    both.pass_on()
    heads.add((3, 0))
    reduce.middle()
    heads.add((1, 2))
    reduce.end()
    sums[...] = jnp.zeros_like(sums)

    def body(span):
        values = tokens[span, :].astype(F32)
        change = norm_back_rows(reduce.rows_of(span), values, gain[...], sums, span)
        result[span, :] = (middle_grad[span, :] + change).astype(BF16)

    each_chunk(result.shape[0], body)
    own[...] = jnp.concatenate(
        [
            jnp.sum(sums[...], axis=0, keepdims=True),
            jnp.sum(sums_two[...], axis=0, keepdims=True),
        ],
        axis=0,
    )
    swaps = swap_all(own, plane_sums, send_p, recv_p)
    for copy in swaps:
        copy.start()
    plane_sums[me] = own[...]
    heads.total(heads_own)
    gather = Gather(heads_own, heads_all, send_t, recv_t, local.at[5])
    gather.start()
    for copy in swaps:
        copy.wait()
    found = plane_sums[0]
    for other in range(1, 8):
        found = found + plane_sums[other]
    column_sums[z] = found
    passes = [
        to_mp(
            column_sums.at[z],
            column_sums.at[z],
            send_p.at[6 + step],
            recv_p.at[6 + step],
            lax.rem(z + step, 4),
        )
        for step in range(1, 4)
    ]
    for copy in passes:
        copy.start()
    both.finish()
    for copy in passes:
        copy.wait()
    gains[...] = (column_sums[0] + column_sums[1]) + (column_sums[2] + column_sums[3])
    gather.pass_on()
    heads.finish_send()
    reduce.finish()
    gather.finish()


def project_input(
    qkv_grad, w_qkv, hidden_all, branch_all, mixed, tokens, middle_grad, gain, sums_two,
    both_sum, both_in,
):
    rows, width = tokens.shape
    groups = hidden_all.shape[0]
    dma = pltpu.SemaphoreType.DMA
    shape = jax.ShapeDtypeStruct
    return pl.pallas_call(
        input_kernel,
        out_shape=(
            shape((rows, width), BF16),
            shape((2, width), F32),
            shape((groups, width, 256), BF16),
            shape((groups, 4 * HEAD_DIM, width // 2), BF16),
        ),
        in_specs=[on_chip()] * 2 + [anywhere()] * 2 + [on_chip()] * 5 + [anywhere()] * 2,
        out_specs=(on_chip(),) * 2 + (anywhere(),) * 2,
        scratch_shapes=reduce_scratch(rows, width)
        + [
            pltpu.VMEM((8, width), F32),
            pltpu.VMEM((2, 4, HEAD_DIM, width), BF16),
            pltpu.VMEM((3, 4, HEAD_DIM, width // 2), BF16),
            dma((16,)),
            dma((8,)),
            dma((12,)),
            pltpu.VMEM((2, width), F32),
            pltpu.VMEM((8, 2, width), F32),
            pltpu.VMEM((4, 2, width), F32),
            dma((10,)),
            dma((10,)),
            pltpu.VMEM((8 * LANES, width), BF16),
            pltpu.VMEM((2, groups, rows, 256), BF16),
            dma((2,)),
            dma((13,)),
            dma((13,)),
            dma((13,)),
            dma((13,)),
            pltpu.VMEM((4, width, 256), BF16),
            pltpu.VMEM((4 * HEAD_DIM, width // 2), BF16),
            dma((6,)),
        ],
        compiler_params=remote_params(6, 63 * 1024 * 1024),
        cost_estimate=pl.CostEstimate(flops=0, bytes_accessed=250_000_000, transcendentals=0),
        name="project_input",
    )(
        qkv_grad, w_qkv, hidden_all, branch_all, mixed, tokens, middle_grad, gain, sums_two,
        both_sum, both_in,
    )


def units_kernel(both, gate, upward):
    for d in range(both.shape[0]):
        gate[:, d * 128 : d * 128 + 128] = both[d, :, :128].astype(F32)
        upward[:, d * 128 : d * 128 + 128] = both[d, :, 128:].astype(F32)


def assemble_units(both):
    groups, width, wide = both.shape
    tile = 256
    shape = jax.ShapeDtypeStruct((width, groups * wide // 2), F32)
    spec = pl.BlockSpec((tile, groups * wide // 2), lambda i: (i, 0))
    return pl.pallas_call(
        units_kernel,
        grid=(width // tile,),
        out_shape=(shape, shape),
        in_specs=[pl.BlockSpec((groups, tile, wide), lambda i: (0, i, 0))],
        out_specs=(spec, spec),
        cost_estimate=pl.CostEstimate(flops=0, bytes_accessed=22_000_000, transcendentals=0),
        name="assemble_units",
    )(both)


def heads_kernel(whole, *outs):
    columns = whole.shape[4]
    for kind, out in enumerate(outs):
        for half in range(whole.shape[1]):
            out[:, half * columns : half * columns + columns] = whole[0, half, kind].astype(F32)


def assemble_heads(whole):
    chips, halves, kinds, rows, columns = whole.shape
    shape = jax.ShapeDtypeStruct((chips * rows, halves * columns), F32)
    spec = pl.BlockSpec((rows, halves * columns), lambda c: (c, 0))
    return pl.pallas_call(
        heads_kernel,
        grid=(chips,),
        out_shape=(shape,) * kinds,
        in_specs=[pl.BlockSpec((1, halves, kinds, rows, columns), lambda c: (c, 0, 0, 0, 0))],
        out_specs=(spec,) * kinds,
        cost_estimate=pl.CostEstimate(flops=0, bytes_accessed=20_000_000, transcendentals=0),
        name="assemble_heads",
    )(whole)


def swapped(
    tokens, cotangent, route, lengths, key_mask, norm1_gain, norm2_gain,
    w_query, w_key, w_value, w_out, w_gate, w_up, w_down,
):
    groups = lax.axis_size("dp")
    members = lax.axis_size("mp")
    me = lax.axis_index("dp")
    z = lax.axis_index("mp")
    rows, width = tokens.shape
    bucket = rows // groups
    units = w_down.shape[0] // groups

    target = route // TOK_DEV
    earlier = jnp.arange(rows, dtype=jnp.int32)
    same = (target[:, None] == target[None, :]) & (earlier[None, :] < earlier[:, None])
    send_at = target * bucket + jnp.sum(same.astype(jnp.int32), axis=1)
    sorting = send_at[None, :] == earlier[:, None]
    slots_own = jnp.sum(jnp.where(sorting, (route % rows)[None, :], 0), axis=1)
    sort_hot = sorting.astype(BF16)
    tokens_b = jnp.dot(sort_hot, tokens, preferred_element_type=F32).astype(BF16)
    cotangent_b = jnp.dot(sort_hot, cotangent, preferred_element_type=F32).astype(BF16)

    mask_window = lax.dynamic_slice_in_dim(
        jnp.concatenate([jnp.zeros((WINDOW,), jnp.int32), key_mask]), z * rows, rows + WINDOW
    )
    notes = jnp.concatenate([slots_own, mask_window, lengths[0]])
    notes = jnp.pad(notes, (0, 8 * LANES - notes.shape[0])).reshape(8, LANES)

    normed, _ = norm_rows(tokens_b.astype(F32))
    hidden_own = (normed * norm1_gain).astype(BF16)
    hidden_one, w_qkv, w_proj, notes_all, both_own, down_own = gather_first(
        hidden_own, w_query.T, w_key.T, w_value.T, w_out, w_gate, w_up, w_down, notes
    )
    notes_all = notes_all.reshape(groups, 8 * LANES)
    slots = (
        notes_all[:, :rows].reshape(groups, groups, bucket).transpose(1, 0, 2).reshape(groups, rows)
    )
    flags = notes_all[:, rows : 2 * rows + WINDOW]
    lengths_all = notes_all[:, 2 * rows + WINDOW : 2 * rows + WINDOW + 3]

    w_both = lax.all_gather(both_own, "mp")
    down_all = lax.all_gather(down_own, "mp", axis=0, tiled=True)

    count = groups * rows
    scale = HEAD_DIM ** (-0.5)
    mixed, kept, cotangent_all = attend_ahead(
        lengths_all, hidden_one, w_qkv, slots, flags, cotangent_b, scale
    )
    mixed = mixed.reshape(count, 2 * LANES)
    middle, hidden_two = project_middle(mixed, w_proj, tokens_b, norm2_gain[None])
    middle_grad, branch, sums_two, activated, both_sum, down_in = feed(
        hidden_two, cotangent_all, middle, cotangent_b, norm2_gain[None], w_both, down_all
    )
    qkv_grad, output_rows, branch_all, both_in, down_whole = attend_back(
        lengths_all,
        kept,
        branch,
        w_proj,
        slots,
        flags,
        activated.reshape(count, units * members),
        down_all,
        middle,
        both_sum,
        down_in,
        scale,
    )
    qkv_grad = qkv_grad.reshape(count, 6 * LANES)
    input_rows, gain_sums, both_whole, heads_whole = project_input(
        qkv_grad,
        w_qkv,
        hidden_one,
        branch_all,
        mixed,
        tokens_b,
        middle_grad,
        norm1_gain[None],
        sums_two,
        both_sum,
        both_in,
    )
    gate_grad, up_grad = assemble_units(both_whole)
    down_grad = down_whole.astype(F32).reshape(groups * units, width)
    query_grad, key_grad, value_grad, proj_grad = assemble_heads(
        heads_whole.reshape(groups // 2, 2, 4, HEAD_DIM, width // 2)
    )

    unsort = (((0,), (0,)), ((), ()))
    return (
        lax.dot_general(sort_hot, output_rows, unsort, preferred_element_type=F32).astype(BF16),
        lax.dot_general(sort_hot, input_rows, unsort, preferred_element_type=F32).astype(BF16),
        gain_sums[0],
        gain_sums[1],
        query_grad.T,
        key_grad.T,
        value_grad.T,
        proj_grad,
        gate_grad,
        up_grad,
        down_grad,
    )


def solution(mesh):
    in_specs = (
        P(("dp", "mp"), None),
        P(("dp", "mp"), None),
        P(("dp", "mp")),
        P("dp", None),
        P("dp"),
        P(),
        P(),
        P(None, "mp"),
        P(None, "mp"),
        P(None, "mp"),
        P("mp", None),
        P(None, "mp"),
        P(None, "mp"),
        P("mp", None),
    )
    out_specs = (
        P(("dp", "mp"), None),
        P(("dp", "mp"), None),
        P(),
        P(),
        P(None, "mp"),
        P(None, "mp"),
        P(None, "mp"),
        P("mp", None),
        P(None, "mp"),
        P(None, "mp"),
        P("mp", None),
    )
    body = swapped if (mesh.shape["dp"], mesh.shape["mp"]) == (8, 4) else local
    return jax.shard_map(body, mesh=mesh, in_specs=in_specs, out_specs=out_specs, check_vma=False)
```

```python
import functools

import jax
import jax.numpy as jnp
from jax import lax
from jax.experimental import pallas as pl
from jax.experimental.pallas import tpu as pltpu
from jax.sharding import PartitionSpec as P

HEAD_DIM = 112
WINDOW = 64
TOK_DEV = 1536


EPSILON = 1e-05
MASKED = 1e30


def norm_rows(values):
    inverse = lax.rsqrt(jnp.mean(values * values, axis=-1, keepdims=True) + EPSILON)
    return (values * inverse, inverse)


def norm_back(gradient, normed, inverse, norm_gain):
    scaled = gradient * norm_gain
    result = inverse * (scaled - normed * jnp.mean(scaled * normed, axis=-1, keepdims=True))
    return (result, jnp.sum(gradient * normed, axis=0))


def padded(values, filler):
    front = jnp.full((WINDOW,) + values.shape[1:], filler, values.dtype)
    return jnp.concatenate([front, values], axis=0)


def block_scores(query_block, key_block, query_seg, key_seg, key_flag, first_row, score_scale):
    query_pos = first_row + jnp.arange(query_block.shape[0], dtype=jnp.int32)
    key_pos = first_row - WINDOW + jnp.arange(key_block.shape[0], dtype=jnp.int32)
    distance = query_pos[:, None] - key_pos[None, :]
    allowed = (distance >= 0) & (distance < WINDOW) & (query_seg[:, None] == key_seg[None, :])
    allowed = allowed & ((key_flag[None, :] == 1) | (distance == 0))
    raw_scores = (
        jnp.einsum("qhd,khd->hqk", query_block, key_block, preferred_element_type=jnp.float32)
        * score_scale
    )
    return jnp.where(allowed[None], raw_scores, -MASKED)


def block_inputs(query, key_pad, value_pad, segment, seg_pad, live_pad, first_row, block_rows):
    key_span = block_rows + WINDOW
    return (
        lax.dynamic_slice_in_dim(query, first_row, block_rows, 0),
        lax.dynamic_slice_in_dim(key_pad, first_row, key_span, 0),
        lax.dynamic_slice_in_dim(value_pad, first_row, key_span, 0),
        lax.dynamic_slice_in_dim(segment, first_row, block_rows, 0),
        lax.dynamic_slice_in_dim(seg_pad, first_row, key_span, 0),
        lax.dynamic_slice_in_dim(live_pad, first_row, key_span, 0),
    )


def attend_forward(query, key_all, value_all, segment, key_live):
    token_count, head_count, head_width = query.shape
    block_rows = min(512, token_count)
    score_scale = head_width ** (-0.5)
    key_pad = padded(key_all, 0.0)
    value_pad = padded(value_all, 0.0)
    seg_pad = padded(segment, -1)
    live_pad = padded(key_live, 0)

    def one_block(running, block_index):
        first_row = block_index * block_rows
        query_block, key_block, value_block, query_seg, key_seg, key_flag = block_inputs(
            query, key_pad, value_pad, segment, seg_pad, live_pad, first_row, block_rows
        )
        scores = block_scores(
            query_block, key_block, query_seg, key_seg, key_flag, first_row, score_scale
        )
        row_max = jnp.max(scores, axis=-1, keepdims=True)
        weights = jnp.exp(scores - row_max)
        denominator = jnp.sum(weights, axis=-1, keepdims=True)
        chances = (weights / denominator).astype(jnp.bfloat16)
        mixed = jnp.einsum("hqk,khd->qhd", chances, value_block, preferred_element_type=jnp.float32)
        return (
            running,
            (mixed.astype(jnp.bfloat16), row_max[..., 0] + jnp.log(denominator[..., 0])),
        )

    _, (mixed, logsum) = lax.scan(
        one_block, jnp.zeros((), jnp.int32), jnp.arange(token_count // block_rows, dtype=jnp.int32)
    )
    return (mixed.reshape(token_count, head_count * head_width), logsum)


def attend_backward(query, key_all, value_all, segment, key_live, logsum, mixed_grad):
    token_count, head_count, head_width = query.shape
    block_rows = min(512, token_count)
    key_span = block_rows + WINDOW
    score_scale = head_width ** (-0.5)
    key_pad = padded(key_all, 0.0)
    value_pad = padded(value_all, 0.0)
    seg_pad = padded(segment, -1)
    live_pad = padded(key_live, 0)

    def one_block(running, inputs):
        key_grad, value_grad = running
        block_index, block_logsum = inputs
        first_row = block_index * block_rows
        query_block, key_block, value_block, query_seg, key_seg, key_flag = block_inputs(
            query, key_pad, value_pad, segment, seg_pad, live_pad, first_row, block_rows
        )
        grad_block = lax.dynamic_slice_in_dim(mixed_grad, first_row, block_rows, 0)
        scores = block_scores(
            query_block, key_block, query_seg, key_seg, key_flag, first_row, score_scale
        )
        chances = jnp.exp(scores - block_logsum[..., None])
        chance_grad = jnp.einsum(
            "qhd,khd->hqk", grad_block, value_block, preferred_element_type=jnp.float32
        )
        row_dot = jnp.sum(chances * chance_grad, axis=-1, keepdims=True)
        score_grad = (chances * (chance_grad - row_dot)).astype(jnp.bfloat16)
        query_grad = (
            jnp.einsum("hqk,khd->qhd", score_grad, key_block, preferred_element_type=jnp.float32)
            * score_scale
        )
        key_part = (
            jnp.einsum("hqk,qhd->khd", score_grad, query_block, preferred_element_type=jnp.float32)
            * score_scale
        )
        value_part = jnp.einsum(
            "hqk,qhd->khd",
            chances.astype(jnp.bfloat16),
            grad_block,
            preferred_element_type=jnp.float32,
        )
        key_grad = lax.dynamic_update_slice_in_dim(
            key_grad,
            lax.dynamic_slice_in_dim(key_grad, first_row, key_span, 0) + key_part,
            first_row,
            0,
        )
        value_grad = lax.dynamic_update_slice_in_dim(
            value_grad,
            lax.dynamic_slice_in_dim(value_grad, first_row, key_span, 0) + value_part,
            first_row,
            0,
        )
        return ((key_grad, value_grad), query_grad)

    empty_grad = jnp.zeros((token_count + WINDOW, head_count, head_width), jnp.float32)
    (key_grad, value_grad), query_grad = lax.scan(
        one_block,
        (empty_grad, empty_grad),
        (jnp.arange(token_count // block_rows, dtype=jnp.int32), logsum),
    )
    flat_width = head_count * head_width
    return (
        query_grad.reshape(token_count, flat_width).astype(jnp.bfloat16),
        key_grad[WINDOW:].reshape(token_count, flat_width).astype(jnp.bfloat16),
        value_grad[WINDOW:].reshape(token_count, flat_width).astype(jnp.bfloat16),
    )


def local(
    tokens,
    cotangent,
    route,
    lengths,
    key_mask,
    norm1_gain,
    norm2_gain,
    w_query,
    w_key,
    w_value,
    w_out,
    w_gate,
    w_up,
    w_down,
):
    groups = lax.axis_size("dp")
    members = lax.axis_size("mp")
    member = lax.axis_index("mp")
    local_rows = tokens.shape[0]
    group_rows = local_rows * members
    bucket = local_rows // groups
    target = route // TOK_DEV
    chosen = (target[:, None] == jnp.arange(groups, dtype=jnp.int32)[None, :]).astype(jnp.int32)
    ranking = jnp.sum((jnp.cumsum(chosen, axis=0) - chosen) * chosen, axis=1)
    send_at = target * bucket + ranking
    arrival, arrival_grad, arrival_slot = (
        lax.all_to_all(
            jnp.zeros_like(tokens).at[send_at].set(tokens),
            "dp",
            split_axis=0,
            concat_axis=0,
            tiled=True,
        ),
        lax.all_to_all(
            jnp.zeros_like(cotangent).at[send_at].set(cotangent),
            "dp",
            split_axis=0,
            concat_axis=0,
            tiled=True,
        ),
        lax.all_to_all(
            jnp.zeros_like(route).at[send_at].set(route % local_rows),
            "dp",
            split_axis=0,
            concat_axis=0,
            tiled=True,
        ),
    )
    token_rows = jnp.zeros_like(arrival).at[arrival_slot].set(arrival)
    grad_rows = jnp.zeros_like(arrival_grad).at[arrival_slot].set(arrival_grad)
    seq_ends = jnp.cumsum(lengths[0])
    positions = jnp.arange(group_rows, dtype=jnp.int32)
    segment = jnp.sum((positions[:, None] >= seq_ends[None, :]).astype(jnp.int32), axis=1)
    input_rows = token_rows.astype(jnp.float32)
    normed_one, inverse_one = norm_rows(input_rows)
    leading_all, grad_all = (
        lax.all_gather(token_rows, "mp", axis=0, tiled=True),
        lax.all_gather(grad_rows, "mp", axis=0, tiled=True),
    )
    input_all = leading_all.astype(jnp.float32)
    normed_all, _ = norm_rows(input_all)
    hidden_one = (normed_all * norm1_gain).astype(jnp.bfloat16)
    head_count = w_query.shape[1] // HEAD_DIM
    query = jnp.dot(hidden_one, w_query, preferred_element_type=jnp.float32).astype(jnp.bfloat16)
    keys = jnp.dot(hidden_one, w_key, preferred_element_type=jnp.float32).astype(jnp.bfloat16)
    values = jnp.dot(hidden_one, w_value, preferred_element_type=jnp.float32).astype(jnp.bfloat16)
    query_heads = query.reshape(group_rows, head_count, HEAD_DIM)
    key_heads = keys.reshape(group_rows, head_count, HEAD_DIM)
    value_heads = values.reshape(group_rows, head_count, HEAD_DIM)
    mixed_flat, logsum = attend_forward(query_heads, key_heads, value_heads, segment, key_mask)
    attention_all = lax.psum(jnp.dot(mixed_flat, w_out, preferred_element_type=jnp.float32), "mp")
    middle_all = input_all + attention_all
    middle_rows = lax.dynamic_slice_in_dim(middle_all, member * local_rows, local_rows, 0)
    normed_mid, _ = norm_rows(middle_all)
    hidden_two = (normed_mid * norm2_gain).astype(jnp.bfloat16)
    normed_two, inverse_two = norm_rows(middle_rows)
    gate_value = jnp.dot(hidden_two, w_gate, preferred_element_type=jnp.float32)
    upward = jnp.dot(hidden_two, w_up, preferred_element_type=jnp.float32)
    sigmoid = jax.nn.sigmoid(gate_value)
    activated = (gate_value * sigmoid * upward).astype(jnp.bfloat16)
    out_rows = middle_rows + lax.psum_scatter(
        jnp.dot(activated, w_down, preferred_element_type=jnp.float32).astype(jnp.bfloat16),
        "mp",
        scatter_dimension=0,
        tiled=True,
    ).astype(jnp.float32)
    activated_grad = jnp.einsum("td,fd->tf", grad_all, w_down, preferred_element_type=jnp.float32)
    gate_grad = (activated_grad * upward * sigmoid * (1.0 + gate_value * (1.0 - sigmoid))).astype(
        jnp.bfloat16
    )
    upward_grad = (activated_grad * gate_value * sigmoid).astype(jnp.bfloat16)
    down_sum = jnp.einsum("tf,td->fd", activated, grad_all, preferred_element_type=jnp.float32)
    gate_sum = jnp.einsum("td,tf->df", hidden_two, gate_grad, preferred_element_type=jnp.float32)
    upward_sum = jnp.einsum(
        "td,tf->df", hidden_two, upward_grad, preferred_element_type=jnp.float32
    )
    hidden_two_grad = lax.psum_scatter(
        jnp.einsum("tf,df->td", gate_grad, w_gate, preferred_element_type=jnp.float32)
        + jnp.einsum("tf,df->td", upward_grad, w_up, preferred_element_type=jnp.float32),
        "mp",
        scatter_dimension=0,
        tiled=True,
    )
    norm_part_two, gain_two_grad = norm_back(hidden_two_grad, normed_two, inverse_two, norm2_gain)
    middle_grad = grad_rows.astype(jnp.float32) + norm_part_two
    branch_all = lax.all_gather(middle_grad.astype(jnp.bfloat16), "mp", axis=0, tiled=True)
    output_sum = jnp.einsum("tc,td->cd", mixed_flat, branch_all, preferred_element_type=jnp.float32)
    mixed_grad = jnp.einsum(
        "td,cd->tc", branch_all, w_out, preferred_element_type=jnp.float32
    ).astype(jnp.bfloat16)
    query_grad, key_grad, value_grad = attend_backward(
        query_heads,
        key_heads,
        value_heads,
        segment,
        key_mask,
        logsum,
        mixed_grad.reshape(group_rows, head_count, HEAD_DIM),
    )
    query_sum = jnp.einsum("td,tc->dc", hidden_one, query_grad, preferred_element_type=jnp.float32)
    key_sum = jnp.einsum("td,tc->dc", hidden_one, key_grad, preferred_element_type=jnp.float32)
    value_sum = jnp.einsum("td,tc->dc", hidden_one, value_grad, preferred_element_type=jnp.float32)
    hidden_one_grad = lax.psum_scatter(
        (
            jnp.einsum("tc,dc->td", query_grad, w_query, preferred_element_type=jnp.float32)
            + jnp.einsum("tc,dc->td", key_grad, w_key, preferred_element_type=jnp.float32)
            + jnp.einsum("tc,dc->td", value_grad, w_value, preferred_element_type=jnp.float32)
        ).astype(jnp.bfloat16),
        "mp",
        scatter_dimension=0,
        tiled=True,
    ).astype(jnp.float32)
    norm_part_one, gain_one_grad = norm_back(hidden_one_grad, normed_one, inverse_one, norm1_gain)
    input_grad = middle_grad + norm_part_one
    gain_one_sum, gain_two_sum = lax.psum((gain_one_grad, gain_two_grad), ("dp", "mp"))
    weight_sums = (
        lax.psum(query_sum.astype(jnp.bfloat16), "dp").astype(jnp.float32),
        lax.psum(key_sum.astype(jnp.bfloat16), "dp").astype(jnp.float32),
        lax.psum(value_sum.astype(jnp.bfloat16), "dp").astype(jnp.float32),
        lax.psum(output_sum.astype(jnp.bfloat16), "dp").astype(jnp.float32),
        lax.psum(gate_sum.astype(jnp.bfloat16), "dp").astype(jnp.float32),
        lax.psum(upward_sum.astype(jnp.bfloat16), "dp").astype(jnp.float32),
        lax.psum(down_sum.astype(jnp.bfloat16), "dp").astype(jnp.float32),
    )
    back_out, back_grad = (
        lax.all_to_all(
            out_rows.astype(jnp.bfloat16)[arrival_slot],
            "dp",
            split_axis=0,
            concat_axis=0,
            tiled=True,
        ),
        lax.all_to_all(
            input_grad.astype(jnp.bfloat16)[arrival_slot],
            "dp",
            split_axis=0,
            concat_axis=0,
            tiled=True,
        ),
    )
    return (
        back_out[send_at],
        back_grad[send_at],
        gain_one_sum,
        gain_two_sum,
        weight_sums[0],
        weight_sums[1],
        weight_sums[2],
        weight_sums[3],
        weight_sums[4],
        weight_sums[5],
        weight_sums[6],
    )


MESH = pl.DeviceIdType.MESH
LANES = 128
F32 = jnp.float32
BF16 = jnp.bfloat16
VMEM_LIMIT = 56 * 1024 * 1024


def plane():
    me = lax.axis_index("dp")
    side = me + 1 - 2 * lax.rem(me, 2)
    over_x = me + 2 - 4 * lax.rem(lax.div(me, 2), 2)
    over_y = me + 4 - 8 * lax.rem(lax.div(me, 4), 2)
    corner = over_x + 4 - 8 * lax.rem(lax.div(over_x, 4), 2)
    return (me, side, over_x, over_y, corner)


def to_dp(source, target, send_sem, recv_sem, index):
    return pltpu.make_async_remote_copy(
        src_ref=source,
        dst_ref=target,
        send_sem=send_sem,
        recv_sem=recv_sem,
        device_id={"dp": index},
        device_id_type=MESH,
    )


def to_mp(source, target, send_sem, recv_sem, index):
    return pltpu.make_async_remote_copy(
        src_ref=source,
        dst_ref=target,
        send_sem=send_sem,
        recv_sem=recv_sem,
        device_id={"mp": index},
        device_id_type=MESH,
    )


def greet_plane():
    _, side, over_x, over_y, _ = plane()
    barrier = pltpu.get_barrier_semaphore()
    for other in (side, over_x, over_y):
        pl.semaphore_signal(barrier, inc=1, device_id={"dp": other}, device_id_type=MESH)
    return barrier


def owner_at(turn):
    me, side, over_x, over_y, _ = plane()
    block = turn // 2
    near = ((block + 1) // 2) % 2
    far = block // 3
    second = turn % 2
    other = (1 - near) * second + (block // 2) * near
    owner = me + (near * (1 - second) + far) * (over_x - me)
    return owner + (near * second + far) * (over_y - me) + other * (side - me)


ARRIVALS = (
    (1, (4,)),
    (2, (0, 1, 2)),
    (3, (3,)),
    (4, (6, 9)),
    (5, (8, 10)),
    (6, (5, 7)),
    (7, (11, 12)),
)


class Gather:
    AFTER = {0: (5, 6), 1: (7, 8), 2: (9,), 3: (10,), 5: (11,), 7: (12,)}

    def __init__(self, own, out, send, recv, local=None):
        me, side, over_x, over_y, corner = plane()
        half = out.shape[1] // 2
        low, high = pl.ds(0, half), pl.ds(half, half)
        self.keep = None if own is None else pltpu.make_async_copy(own, out.at[me], local)
        own = out.at[me] if own is None else own

        def hop(number, source, target, index):
            return to_dp(source, target, send.at[number], recv.at[number], index)

        def onward(number, owner, part, index):
            place = out.at[owner, part]
            return hop(number, place, place, index)

        self.copies = [
            hop(0, own.at[low], out.at[me, low], over_x),
            hop(1, own.at[high], out.at[me, high], over_y),
            hop(2, own.at[high], out.at[me, high], over_x),
            hop(3, own.at[low], out.at[me, low], over_y),
            hop(4, own, out.at[me], side),
            onward(5, over_x, low, over_y),
            onward(6, over_x, low, side),
            onward(7, over_y, high, over_x),
            onward(8, over_y, high, side),
            onward(9, over_x, high, side),
            onward(10, over_y, low, side),
            onward(11, corner, low, side),
            onward(12, corner, high, side),
        ]

    def start(self):
        for number in range(5):
            self.copies[number].start()
        if self.keep is not None:
            self.keep.start()

    def arrive(self, *numbers):
        for number in numbers:
            self.copies[number].wait_recv()
            for later in self.AFTER.get(number, ()):
                self.copies[later].start()

    def pass_on(self):
        self.arrive(0, 1, 2, 3)

    def sent(self):
        for copy in self.copies:
            copy.wait_send()
        if self.keep is not None:
            self.keep.wait()

    def finish(self):
        self.arrive(5, 7, 4, 6, 8, 9, 10, 11, 12)
        self.sent()


def greet_all(barrier):
    me, z = lax.axis_index("dp"), lax.axis_index("mp")
    for step in range(1, 8):
        pl.semaphore_signal(
            barrier, inc=1, device_id={"dp": lax.rem(me + step, 8)}, device_id_type=MESH
        )
    core = lax.rem(me, 2)
    for step in range(1, 4):
        for other in (me, me + 1 - 2 * core):
            pl.semaphore_signal(
                barrier,
                inc=1,
                device_id={"dp": other, "mp": lax.rem(z + step, 4)},
                device_id_type=MESH,
            )
    pl.semaphore_wait(barrier, 13)


def swap_all(source, target, send, recv):
    me = lax.axis_index("dp")
    return [
        to_dp(source, target.at[me], send.at[step - 1], recv.at[step - 1], lax.rem(me + step, 8))
        for step in range(1, 8)
    ]


class Spread:
    def __init__(self, share, w_qkv, w_out, send, recv, local):
        me, z = lax.axis_index("dp"), lax.axis_index("mp")
        core = lax.rem(me, 2)
        self.place = z + core * (3 - 2 * z)
        self.send, self.recv, self.local = send, recv, local
        self.shares = [share.at[0], share.at[1], share.at[2], share.at[3]]
        self.slots = (core, 1 - core)
        self.core = core
        self.w_qkv, self.w_out = w_qkv, w_out

    def target(self, which, piece):
        slot = self.slots[which]
        block = slot if piece == 3 else 2 * piece + slot
        rows = pl.ds(pl.multiple_of(block * LANES, LANES), HEAD_DIM)
        return (self.w_out if piece == 3 else self.w_qkv).at[rows]

    def hop(self, which, piece, number, place, own):
        source = self.shares[piece] if own else self.target(which, piece)
        z = place + self.core * (3 - 2 * place)
        return to_mp(
            source,
            self.target(which, piece),
            self.send.at[number * 4 + piece],
            self.recv.at[which * 4 + piece],
            z,
        )

    def keep(self, which, piece):
        return pltpu.make_async_copy(
            self.shares[piece], self.target(which, piece), self.local.at[piece]
        )

    def start(self):
        @pl.when(self.place == 0)
        def _():
            for piece in range(4):
                self.hop(0, piece, 0, 1, True).start()
                self.keep(0, piece).start()

        @pl.when(self.place == 1)
        def _():
            for piece in range(4):
                self.hop(1, piece, 0, 0, True).start()
                self.hop(1, piece, 1, 2, True).start()
                self.keep(1, piece).start()

    def pass_on(self, pieces):
        @pl.when(self.place == 1)
        def _():
            for piece in pieces:
                self.hop(0, piece, 2, 2, False).wait_recv()
                self.hop(0, piece, 2, 2, False).start()

        @pl.when(self.place == 2)
        def _():
            for piece in pieces:
                for which in (1, 0):
                    self.hop(which, piece, which, 3, False).wait_recv()
                    self.hop(which, piece, which, 3, False).start()

    def finish(self):
        @pl.when(self.place == 0)
        def _():
            for piece in range(4):
                self.hop(1, piece, 0, 1, False).wait_recv()
                self.hop(0, piece, 0, 1, True).wait_send()
                self.keep(0, piece).wait()

        @pl.when(self.place == 1)
        def _():
            for piece in range(4):
                self.hop(1, piece, 0, 0, True).wait_send()
                self.hop(1, piece, 1, 2, True).wait_send()
                self.hop(0, piece, 2, 2, False).wait_send()
                self.keep(1, piece).wait()

        @pl.when(self.place == 2)
        def _():
            for piece in range(4):
                for which in (1, 0):
                    self.hop(which, piece, which, 3, False).wait_send()

        @pl.when(self.place == 3)
        def _():
            for piece in range(4):
                for which in (1, 0):
                    self.hop(which, piece, which, 3, False).wait_recv()


class Chain:
    def __init__(self, own, out, send, recv, local):
        self.z = lax.axis_index("mp")
        self.own, self.out, self.send, self.recv = own, out, send, recv
        self.keep = pltpu.make_async_copy(own, out.at[self.z], local)

    def hop(self, way, distance):
        z = self.z
        source = z - way * distance
        return to_mp(
            self.own if distance == 0 else self.out.at[source],
            self.out.at[source],
            self.send.at[3 * (way > 0) + distance],
            self.recv.at[3 * (way > 0) + distance],
            z + way,
        )

    def ways(self, distance):
        z = self.z
        return (
            (1, z >= distance, (z >= distance) & (z < 3)),
            (-1, z <= 3 - distance, (z <= 3 - distance) & (z > 0)),
        )

    def step(self, distance):
        if distance == 0:
            self.keep.start()
        for way, there, onward in self.ways(distance):
            if distance > 0:
                pl.when(there)(self.hop(way, distance - 1).wait_recv)
            if distance < 3:
                pl.when(onward)(self.hop(way, distance).start)

    def finish(self):
        self.step(3)
        for distance in range(3):
            for way, _, onward in self.ways(distance):
                pl.when(onward)(self.hop(way, distance).wait_send)
        self.keep.wait()


def anywhere():
    return pl.BlockSpec(memory_space=pl.ANY)


def on_chip():
    return pl.BlockSpec(memory_space=pltpu.VMEM)


def remote_params(number, limit=VMEM_LIMIT):
    return pltpu.CompilerParams(
        collective_id=number, has_side_effects=True, vmem_limit_bytes=limit
    )


def hot_of(notes, k, size):
    own = notes[:, 0:48, :].reshape(size, LANES)
    lane = lax.broadcasted_iota(jnp.int32, (size, LANES), 1)
    slot = jnp.sum(jnp.where(lane == k, own, 0.0), axis=1, keepdims=True)
    return (lax.broadcasted_iota(jnp.int32, (size, size), 1).astype(F32) == slot).astype(BF16)


def block_mask(notes, k, block, z, rows):
    position = rows * z + block * 128 + lax.broadcasted_iota(jnp.int32, (128, 1), 0)
    position = position.astype(F32)
    first_end = notes[k, 52:53, 0:1]
    second_end = first_end + notes[k, 52:53, 1:2]
    begin = jnp.where(position >= first_end, first_end, 0.0)
    begin = jnp.where(position >= second_end, second_end, begin)
    column = lax.broadcasted_iota(jnp.int32, (128, 192), 1)
    distance = 64 + lax.broadcasted_iota(jnp.int32, (128, 192), 0) - column
    key_position = (rows * z + block * 128 - 64 + column).astype(F32)
    live = jnp.concatenate(
        [notes[k, 48 + block : 49 + block, :], notes[k, 49 + block : 50 + block, 0:64]], axis=1
    )
    allowed = (distance >= 0) & (distance < WINDOW) & (key_position >= begin)
    return allowed & ((live == 1.0) | (distance == 0))


NT = (((1,), (1,)), ((), ()))
TN = (((0,), (0,)), ((), ()))


def forward_kernel(
    tokens, cotangent, order_row, gain, notes, query, keys, values, project, gate, upward,
    hidden_out, w_qkv, w_out, notes_all, w_both, mixed, kept, tokens_b, cotangent_b, cotangent_all,
    hidden_all, qkv, share, both_own,
    send, recv, send_a, recv_a, send_g, recv_g, send_w, recv_w, send_n, recv_n, send_c, recv_c,
    local, out_sem, *, scale,
):
    groups, rows, width = hidden_all.shape
    me, z = lax.axis_index("dp"), lax.axis_index("mp")
    members = lax.axis_size("mp")
    head = pl.ds(pl.multiple_of(lax.div(me, 2) * HEAD_DIM, 16), HEAD_DIM)
    units = pl.ds(pl.multiple_of(me * LANES, LANES), LANES)
    loads = [
        pltpu.make_async_copy(source.at[head], share.at[piece], local.at[piece])
        for piece, source in enumerate((query, keys, values, project))
    ]
    loads += [
        pltpu.make_async_copy(gate.at[:, units], both_own.at[:, pl.ds(0, LANES)], local.at[4]),
        pltpu.make_async_copy(upward.at[:, units], both_own.at[:, pl.ds(LANES, LANES)], local.at[5]),
    ]
    for copy in loads:
        copy.start()
    none = jnp.zeros((LANES - HEAD_DIM, width), BF16)
    for block in range(6):
        w_qkv[block * LANES + HEAD_DIM : block * LANES + LANES, :] = none
    for block in range(2):
        w_out[block * LANES + HEAD_DIM : block * LANES + LANES, :] = none

    place = lax.broadcasted_iota(jnp.int32, (rows, rows), 0).astype(F32)
    sort = (place == order_row[...]).astype(BF16)
    tokens_b[...] = jnp.dot(sort, tokens[...], preferred_element_type=F32).astype(BF16)

    def normalise(span):
        value = tokens_b[span, :].astype(F32)
        inverse = lax.rsqrt(mean_rows(value * value) + EPSILON)
        hidden_all[me, span, :] = (value * inverse * gain[...]).astype(BF16)

    each_chunk(rows, normalise)
    notes_all[me] = notes[...]
    greet_all(pltpu.get_barrier_semaphore())
    gather = Gather(None, hidden_all, send_a, recv_a)
    gather.start()
    swaps = swap_all(notes, notes_all, send_n, recv_n)
    for copy in swaps:
        copy.start()
    for copy in loads[:4]:
        copy.wait()
    spread = Spread(share, w_qkv, w_out, send_w, recv_w, local)
    spread.start()
    cotangent_b[...] = jnp.dot(sort, cotangent[...], preferred_element_type=F32).astype(BF16)
    for copy in loads[4:]:
        copy.wait()
    chain = Chain(both_own, w_both, send_c, recv_c, local.at[4])
    second = Gather(cotangent_b, cotangent_all, send_g, recv_g, local.at[5])
    spread.pass_on((0, 1))
    gather.arrive(0, 1)
    spread.pass_on((2, 3))
    gather.arrive(2, 3)
    second.start()
    chain.step(0)
    spread.finish()
    for copy in swaps:
        copy.wait()

    def keep(turn):
        owner = owner_at(turn)
        return pltpu.make_async_copy(hidden_all.at[owner], hidden_out.at[owner], out_sem.at[turn])

    def multiply(turn, carry):
        for number, numbers in ARRIVALS:
            left = tuple(n for n in numbers if n > 3)
            if left:
                pl.when(turn == number)(functools.partial(gather.arrive, *left))
        owner = owner_at(turn)
        keep(turn).start()
        product = lax.dot_general(
            hidden_all[owner], w_qkv[...], NT, preferred_element_type=F32
        ).astype(BF16)
        qkv[owner] = product.reshape(groups, rows // groups, 768)
        return carry

    lax.fori_loop(0, groups, multiply, 0)

    def halo(k, other):
        return to_mp(
            kept.at[k, pl.ds(rows, 64), pl.ds(256, 512)],
            kept.at[k, pl.ds(0, 64), pl.ds(256, 512)],
            send.at[k],
            recv.at[k],
            other,
        )

    def order(k, carry):
        hot = hot_of(notes_all, k, rows)
        given = qkv[:, pl.ds(k, 1)].reshape(rows, 768)
        kept[k, pl.ds(64, rows), :] = lax.dot_general(
            hot, given, TN, preferred_element_type=F32
        ).astype(BF16)
        kept[k, pl.ds(0, 64), pl.ds(0, 256)] = jnp.zeros((64, 256), BF16)

        @pl.when(z < members - 1)
        def _():
            halo(k, z + 1).start()

        @pl.when(z == 0)
        def _():
            kept[k, pl.ds(0, 64), pl.ds(256, 512)] = jnp.zeros((64, 512), BF16)

        return carry

    lax.fori_loop(0, groups, order, 0)

    def attend(k, carry):
        @pl.when(z > 0)
        def _():
            halo(k, z).wait_recv()

        hot = hot_of(notes_all, k, rows)
        found = []
        for block in range(rows // 128):
            allowed = block_mask(notes_all, k, block, z, rows)
            heads = []
            for head in range(2):
                query = kept[k, pl.ds(64 + block * 128, 128), pl.ds(head * 128, 128)]
                keys = kept[k, pl.ds(block * 128, 192), pl.ds(256 + head * 128, 128)]
                values = kept[k, pl.ds(block * 128, 192), pl.ds(512 + head * 128, 128)]
                scores = lax.dot_general(query, keys, NT, preferred_element_type=F32) * scale
                scores = jnp.where(allowed, scores, -MASKED)
                weights = jnp.exp(scores - jnp.max(scores, axis=-1, keepdims=True))
                total = jnp.sum(weights, axis=-1, keepdims=True)
                chances = (weights / total).astype(BF16)
                heads.append(jnp.dot(chances, values, preferred_element_type=F32).astype(BF16))
            found.append(jnp.concatenate(heads, axis=1))
        ordered = jnp.concatenate(found, axis=0)
        back = jnp.dot(hot, ordered, preferred_element_type=F32).astype(BF16)
        mixed[:, pl.ds(k, 1)] = back.reshape(groups, 1, rows // groups, 256)
        return carry

    chain.step(1)
    lax.fori_loop(0, groups // 2, attend, 0)
    second.pass_on()
    chain.step(2)
    lax.fori_loop(groups // 2, groups, attend, 0)
    second.finish()
    chain.finish()
    gather.sent()

    def kept_out(turn, carry):
        keep(turn).wait()
        return carry

    lax.fori_loop(0, groups, kept_out, 0)

    @pl.when(z < members - 1)
    def _():
        def done(k, carry):
            halo(k, z + 1).wait_send()
            return carry

        lax.fori_loop(0, groups, done, 0)


def attend_ahead(
    tokens, cotangent, order_row, gain, notes, query, keys, values, project, gate, upward, scale
):
    rows, width = tokens.shape
    groups, members = lax.axis_size("dp"), lax.axis_size("mp")
    dma = pltpu.SemaphoreType.DMA
    shape = jax.ShapeDtypeStruct
    return pl.pallas_call(
        functools.partial(forward_kernel, scale=scale),
        out_shape=(
            shape((groups, rows, width), BF16),
            shape((6 * LANES, width), BF16),
            shape((2 * LANES, width), BF16),
            shape((groups,) + notes.shape, F32),
            shape((members, width, 2 * LANES), BF16),
            shape((groups, groups, rows // groups, 256), BF16),
            shape((groups, rows + 64, 768), BF16),
            shape((rows, width), BF16),
            shape((rows, width), BF16),
            shape((groups, rows, width), BF16),
        ),
        in_specs=[on_chip()] * 5 + [anywhere()] * 6,
        out_specs=(anywhere(),)
        + (on_chip(),) * 3
        + (anywhere(),)
        + (on_chip(),) * 4
        + (anywhere(),),
        scratch_shapes=[
            pltpu.VMEM((groups, rows, width), BF16),
            pltpu.VMEM((groups, groups, rows // groups, 768), BF16),
            pltpu.VMEM((4, HEAD_DIM, width), BF16),
            pltpu.VMEM((width, 2 * LANES), BF16),
            dma((groups,)),
            dma((groups,)),
            dma((13,)),
            dma((13,)),
            dma((13,)),
            dma((13,)),
            dma((12,)),
            dma((8,)),
            dma((7,)),
            dma((7,)),
            dma((6,)),
            dma((6,)),
            dma((6,)),
            dma((groups,)),
        ],
        compiler_params=remote_params(2, 60 * 1024 * 1024),
        cost_estimate=pl.CostEstimate(flops=0, bytes_accessed=300_000_000, transcendentals=0),
        name="attend_ahead",
    )(tokens, cotangent, order_row, gain, notes, query, keys, values, project, gate, upward)


CHUNK = 32


def each_chunk(rows, body, chunk=CHUNK):
    def step(i, carry):
        body(pl.ds(pl.multiple_of(i * chunk, chunk), chunk))
        return carry

    lax.fori_loop(0, rows // chunk, step, 0)


class Reduce:
    COUNT = 10

    def __init__(self, left, right, across, part, from_side, from_corner, from_near, send, recv):
        self.left, self.right, self.across, self.part = left, right, across, part
        self.from_side, self.from_corner, self.from_near = from_side, from_corner, from_near
        self.send, self.recv = send, recv
        self.rows = part.shape[1]

    def product(self, owner, slot):
        rows, width = self.rows, self.part.shape[2]
        picked = pl.ds(pl.multiple_of(owner * rows, rows), rows)

        def tile(t, carry):
            columns = pl.ds(pl.multiple_of(t * 256, 256), 256)
            if self.across:
                value = lax.dot_general(
                    self.left[picked, :], self.right[columns, :], NT, preferred_element_type=F32
                )
            else:
                value = jnp.dot(
                    self.left[picked, :], self.right[:, columns], preferred_element_type=F32
                )
            self.part[slot, :, columns] = value.astype(BF16)
            return carry

        lax.fori_loop(0, width // 256, tile, 0)

    def prepare(self):
        _, side, over_x, over_y, corner = plane()
        part, near = self.part, self.from_near
        half = self.rows // 2
        low, high = pl.ds(0, half), pl.ds(half, half)

        def hop(number, source, target, index):
            return to_dp(source, target, self.send.at[number], self.recv.at[number], index)

        self.shares = [hop(i, part.at[4 + i], self.from_side.at[i], side) for i in range(4)]
        self.corners = [
            hop(4, part.at[0, low], self.from_corner.at[0], over_x),
            hop(5, part.at[0, high], self.from_corner.at[1], over_y),
        ]
        self.nears = [
            hop(6, part.at[1, low], near.at[0, low], over_x),
            hop(7, part.at[1, high], near.at[0, high], over_x),
            hop(8, part.at[2, high], near.at[1, high], over_y),
            hop(9, part.at[2, low], near.at[1, low], over_y),
        ]

    def add_side(self, slot):
        self.shares[slot].wait_recv()

        def body(span):
            self.part[slot, span, :] = (
                self.part[slot, span, :].astype(F32) + self.from_side[slot, span, :].astype(F32)
            ).astype(BF16)

        each_chunk(self.rows, body)

    def add_corner(self, slot, offset, which):
        self.corners[which].wait_recv()

        def body(span):
            target = pl.ds(pl.multiple_of(offset + span.start, CHUNK), CHUNK)
            self.part[slot, target, :] = (
                self.part[slot, target, :].astype(F32)
                + self.from_corner[which, span, :].astype(F32)
            ).astype(BF16)

        each_chunk(self.rows // 2, body)

    def products(self):
        self.prepare()
        me, _, over_x, over_y, corner = plane()
        turn = 1 - 2 * lax.rem(me, 2)
        for slot, owner in enumerate((corner, over_x, over_y, me)):
            self.product(owner + turn, 4 + slot)
            self.shares[slot].start()
        for slot, owner in enumerate((corner, over_x, over_y, me)):
            self.product(owner, slot)

    def launch(self):
        self.add_side(0)
        self.corners[0].start()
        self.corners[1].start()
        self.add_side(1)
        self.nears[0].start()
        self.add_side(2)
        self.nears[2].start()

    def begin(self):
        self.prepare()
        me, _, over_x, over_y, corner = plane()
        turn = 1 - 2 * lax.rem(me, 2)
        self.product(corner + turn, 4)
        self.shares[0].start()
        self.product(corner, 0)
        self.product(over_x + turn, 5)
        self.shares[1].start()
        self.add_side(0)
        self.corners[0].start()
        self.corners[1].start()
        self.product(over_x, 1)
        self.product(over_y + turn, 6)
        self.shares[2].start()
        self.add_side(1)
        self.nears[0].start()
        self.product(over_y, 2)
        self.product(me + turn, 7)
        self.shares[3].start()
        self.add_side(2)
        self.nears[2].start()
        self.product(me, 3)

    def middle(self):
        self.add_corner(2, 0, 0)
        self.nears[3].start()
        self.add_corner(1, self.rows // 2, 1)
        self.nears[1].start()

    def end(self):
        self.shares[3].wait_recv()
        for copy in self.nears:
            copy.wait_recv()

    def run(self):
        self.begin()
        self.middle()
        self.end()

    def rows_of(self, span):
        return (
            self.part[3, span, :].astype(F32)
            + self.from_side[3, span, :].astype(F32)
            + self.from_near[0, span, :].astype(F32)
            + self.from_near[1, span, :].astype(F32)
        )

    def finish(self):
        for copy in self.shares + self.corners + self.nears:
            copy.wait_send()


def reduce_scratch(rows, width):
    dma = pltpu.SemaphoreType.DMA
    return [
        pltpu.VMEM((8, rows, width), BF16),
        pltpu.VMEM((4, rows, width), BF16),
        pltpu.VMEM((2, rows // 2, width), BF16),
        pltpu.VMEM((2, rows, width), BF16),
        dma((10,)),
        dma((10,)),
    ]


def gather_scratch(rows, width):
    dma = pltpu.SemaphoreType.DMA
    return [pltpu.VMEM((rows, width), BF16), dma((13,)), dma((13,)), dma(())]


def mean_rows(values):
    return jnp.mean(values, axis=-1, keepdims=True)


class Heads:
    def __init__(self, source, stage, arrive, send, recv_stage, recv):
        me, z = lax.axis_index("dp"), lax.axis_index("mp")
        self.me, self.z = me, z
        self.core = lax.rem(me, 2)
        self.source, self.stage, self.arrive = source, stage, arrive
        self.send, self.recv_stage, self.recv = send, recv_stage, recv
        self.place = z + self.core * (3 - 2 * z)
        self.columns = source.shape[1] // 2

    def z_of(self, place):
        return place + self.core * (3 - 2 * place)

    def slot_of(self, place):
        return self.core if place == 0 else 1 - self.core

    def rows_of(self, place, kind):
        block = 2 * kind + self.slot_of(place)
        return self.source.at[pl.ds(pl.multiple_of(block * LANES, LANES), HEAD_DIM)]

    def half_of(self, ref, half):
        return ref.at[:, pl.ds(pl.multiple_of(half * self.columns, LANES), self.columns)]

    def to_stage(self, place, kind):
        return to_at(
            self.rows_of(place, kind),
            self.stage.at[place, kind],
            self.send.at[place * 4 + kind],
            self.recv_stage.at[place * 4 + kind],
            self.me,
            self.z_of(2),
        )

    def to_owner(self, place, kind, half, way, ref, number):
        return to_at(
            self.half_of(ref, half),
            self.arrive.at[way, kind],
            self.send.at[number],
            self.recv.at[way * 4 + kind],
            self.me - self.core + half,
            self.z_of(place),
        )

    def sums(self, kind):
        return [
            self.to_owner(
                place, kind, half, 2, self.stage.at[place, kind], place * 8 + kind * 2 + half
            )
            for place in (0, 1)
            for half in (0, 1)
        ]

    def cross(self, own, kind):
        other = 1 - own
        copies = [
            self.to_owner(other, kind, half, 0, self.rows_of(other, kind), kind * 2 + half)
            for half in (0, 1)
        ]
        copies.append(
            to_at(
                self.half_of(self.rows_of(own, kind), 1 - self.core),
                self.arrive.at[1, kind],
                self.send.at[8 + kind],
                self.recv.at[4 + kind],
                self.me + 1 - 2 * self.core,
                self.z,
            )
        )
        return copies

    def start(self, kinds):
        @pl.when(self.place == 3)
        def _():
            for kind in kinds:
                self.to_stage(0, kind).start()
                self.to_stage(1, kind).start()

        for own in (0, 1):
            @pl.when(self.place == own)
            def _():
                for kind in kinds:
                    for copy in self.cross(own, kind):
                        copy.start()

    def add(self, kinds):
        @pl.when(self.place == 2)
        def _():
            for kind in kinds:
                for place in (0, 1):
                    self.to_stage(place, kind).wait_recv()
                    mine = self.rows_of(place, kind)

                    def body(span):
                        self.stage[place, kind, span, :] = (
                            self.stage[place, kind, span, :].astype(F32)
                            + mine[span, :].astype(F32)
                        ).astype(BF16)

                    each_chunk(HEAD_DIM, body, 16)
                for copy in self.sums(kind):
                    copy.start()

    def total(self, out):
        owner = lax.div(self.z, 2) == self.core
        for kind in range(4):
            for own in (0, 1):
                @pl.when(self.place == own)
                def _():
                    self.arrive[1, kind] = self.half_of(self.rows_of(own, kind), self.core)[...]

            for way in range(3):
                waiting = to_at(
                    self.half_of(self.rows_of(0, kind), 0),
                    self.arrive.at[way, kind],
                    self.send.at[0],
                    self.recv.at[way * 4 + kind],
                    self.me,
                    lax.rem(self.z + 1, 4),
                )
                if way == 1:
                    pl.when(jnp.logical_not(owner))(waiting.wait_recv)
                else:
                    waiting.wait_recv()

            def body(span):
                found = self.arrive[0, kind, span, :].astype(F32)
                found = found + self.arrive[1, kind, span, :].astype(F32)
                found = found + self.arrive[2, kind, span, :].astype(F32)
                target = pl.ds(pl.multiple_of(kind * HEAD_DIM + span.start, 16), 16)
                out[target, :] = found.astype(BF16)

            each_chunk(HEAD_DIM, body, 16)

    def finish_send(self):
        for kind in range(4):
            @pl.when(self.place == 3)
            def _():
                self.to_stage(0, kind).wait_send()
                self.to_stage(1, kind).wait_send()

            @pl.when(self.place == 2)
            def _():
                for copy in self.sums(kind):
                    copy.wait_send()

            for own in (0, 1):
                @pl.when(self.place == own)
                def _():
                    for copy in self.cross(own, kind):
                        copy.wait_send()


def to_at(source, target, send_sem, recv_sem, dp, mp):
    return pltpu.make_async_remote_copy(
        src_ref=source,
        dst_ref=target,
        send_sem=send_sem,
        recv_sem=recv_sem,
        device_id={"dp": dp, "mp": mp},
        device_id_type=MESH,
    )


class Units:
    def __init__(self, both_sum, both_in, both_stage, send, recv, local):
        self.z = lax.axis_index("mp")
        self.sums = (both_sum,)
        self.inputs = (both_in,)
        self.stages = (both_stage,)
        self.send, self.recv, self.local = send, recv, local
        z = self.z
        self.outer = (z == 0) | (z == 3)
        self.far = 3 - z
        self.near = 1 + lax.div(z, 3)
        self.second = 3 - self.near
        self.edge = 3 * (z - 1)

    def part(self, kind, z):
        return self.sums[kind].at[z]

    def straight(self, kind, number, target):
        return to_mp(
            self.part(kind, target),
            self.inputs[kind].at[self.z],
            self.send.at[number * 2 + kind],
            self.recv.at[self.z * 2 + kind],
            target,
        )

    def staged(self, kind):
        return to_mp(
            self.part(kind, self.far),
            self.stages[kind].at[0],
            self.send.at[4 + kind],
            self.recv.at[8 + kind],
            self.near,
        )

    def summed(self, kind):
        return to_mp(
            self.stages[kind].at[1],
            self.inputs[kind].at[self.z],
            self.send.at[4 + kind],
            self.recv.at[self.z * 2 + kind],
            3 - self.edge,
        )

    def mine(self, kind):
        return pltpu.make_async_copy(
            self.part(kind, 3 - self.edge), self.stages[kind].at[1], self.local.at[kind]
        )

    def start(self):
        @pl.when(self.outer)
        def _():
            for kind in range(1):
                self.staged(kind).start()
            for kind in range(1):
                self.straight(kind, 0, self.near).start()
                self.straight(kind, 1, self.second).start()

        @pl.when(jnp.logical_not(self.outer))
        def _():
            for kind in range(1):
                self.mine(kind).start()
                self.straight(kind, 0, 3 - self.z).start()
                self.straight(kind, 1, self.edge).start()

    def add(self):
        @pl.when(jnp.logical_not(self.outer))
        def _():
            for kind in range(1):
                stage = self.stages[kind]
                self.mine(kind).wait()
                to_mp(
                    self.part(kind, 0),
                    stage.at[0],
                    self.send.at[4 + kind],
                    self.recv.at[8 + kind],
                    self.edge,
                ).wait_recv()

                def body(span):
                    stage[1, span, :] = (
                        stage[0, span, :].astype(F32) + stage[1, span, :].astype(F32)
                    ).astype(BF16)

                each_chunk(stage.shape[1], body)
                self.summed(kind).start()

    def arrived(self, kind, source):
        to_mp(
            self.part(kind, 0),
            self.inputs[kind].at[source],
            self.send.at[kind],
            self.recv.at[source * 2 + kind],
            source,
        ).wait_recv()

    def finish(self):
        @pl.when(self.outer)
        def _():
            for kind in range(1):
                self.arrived(kind, 1)
                self.arrived(kind, 2)
                self.straight(kind, 0, self.near).wait_send()
                self.straight(kind, 1, self.second).wait_send()
                self.staged(kind).wait_send()

        @pl.when(jnp.logical_not(self.outer))
        def _():
            for kind in range(1):
                self.arrived(kind, 0)
                self.arrived(kind, 3)
                self.arrived(kind, 3 - self.z)
                self.straight(kind, 0, 3 - self.z).wait_send()
                self.straight(kind, 1, self.edge).wait_send()
                self.summed(kind).wait_send()


def backward_kernel(
    kept, branch, w_out, notes_all, activated, w_down, middle, both_sum, down_in,
    out, result, branch_all, both_in, down_all,
    totals, query_part, key_value, ending, leaving, arriving, send, recv,
    part, from_side, from_corner, from_near, send_r, recv_r,
    mixed_grad, shard, load_sem, send_g, recv_g,
    both_stage, send_u, recv_u, local, down_found, send_d, recv_d,
    *, scale, groups, rows,
):
    z = lax.axis_index("mp")
    members = lax.axis_size("mp")
    load_down = pltpu.make_async_copy(down_in, down_found, load_sem.at[2])
    load_down.start()
    greet_all(pltpu.get_barrier_semaphore())
    units = Units(both_sum, both_in, both_stage, send_u, recv_u, local)
    gather = Gather(branch, branch_all, send_g, recv_g, local.at[2])
    gather.start()
    units.start()
    reduce = Reduce(activated, w_down, False, part, from_side, from_corner, from_near, send_r, recv_r)
    reduce.products()
    load_down.wait()

    def add_down(span):
        value = down_found[0, span, :].astype(F32) + down_found[1, span, :].astype(F32)
        value = value + down_found[2, span, :].astype(F32) + down_found[3, span, :].astype(F32)
        down_found[0, span, :] = value.astype(BF16)

    each_chunk(down_found.shape[1], add_down)
    down = Gather(down_found.at[0], down_all, send_d, recv_d, local.at[1])

    def load_shard(turn):
        slot = turn % 2
        return pltpu.make_async_copy(branch_all.at[owner_at(turn)], shard.at[slot], load_sem.at[slot])

    def spread_back(turn, carry):
        for number, numbers in ARRIVALS:
            pl.when(turn == number)(functools.partial(gather.arrive, *numbers))

        @pl.when(turn == 0)
        def _():
            gather.keep.wait()

        load_shard(turn).start()
        load_shard(turn).wait()
        mixed_grad[owner_at(turn)] = (
            lax.dot_general(shard[turn % 2], w_out[...], NT, preferred_element_type=F32)
            .astype(BF16)
            .reshape(groups, rows // groups, 256)
        )
        return carry

    lax.fori_loop(0, 8, spread_back, 0)
    reduce.launch()
    down.start()
    units.add()


    def halo(k, other):
        return to_mp(leaving.at[k], arriving.at[k], send.at[k], recv.at[k], other)

    def attend(k, carry):
        hot = hot_of(notes_all, k, rows)
        given = mixed_grad[:, pl.ds(k, 1)].reshape(rows, 256)
        grad_ordered = lax.dot_general(hot, given, TN, preferred_element_type=F32).astype(BF16)
        totals[...] = jnp.zeros_like(totals)
        for block in range(rows // 128):
            allowed = block_mask(notes_all, k, block, z, rows)
            for head in range(2):
                query = kept[k, pl.ds(64 + block * 128, 128), pl.ds(head * 128, 128)]
                keys = kept[k, pl.ds(block * 128, 192), pl.ds(256 + head * 128, 128)]
                values = kept[k, pl.ds(block * 128, 192), pl.ds(512 + head * 128, 128)]
                grad = grad_ordered[block * 128 : block * 128 + 128, head * 128 : head * 128 + 128]
                scores = lax.dot_general(query, keys, NT, preferred_element_type=F32) * scale
                scores = jnp.where(allowed, scores, -MASKED)
                weights = jnp.exp(scores - jnp.max(scores, axis=-1, keepdims=True))
                again = weights / jnp.sum(weights, axis=-1, keepdims=True)
                chance_grad = lax.dot_general(grad, values, NT, preferred_element_type=F32)
                row_dot = jnp.sum(again * chance_grad, axis=-1, keepdims=True)
                score_grad = (again * (chance_grad - row_dot)).astype(BF16)
                query_part[k, pl.ds(block * 128, 128), pl.ds(head * 128, 128)] = (
                    jnp.dot(score_grad, keys, preferred_element_type=F32) * scale
                ).astype(BF16)
                totals[pl.ds(block * 128, 192), pl.ds(head * 128, 128)] += (
                    lax.dot_general(score_grad, query, TN, preferred_element_type=F32) * scale
                )
                totals[pl.ds(block * 128, 192), pl.ds(256 + head * 128, 128)] += lax.dot_general(
                    again.astype(BF16), grad, TN, preferred_element_type=F32
                )
        key_value[k] = totals[pl.ds(64, rows), :].astype(BF16)
        ending[k] = totals[pl.ds(rows, 64), :]

        @pl.when(z > 0)
        def _():
            leaving[k] = totals[pl.ds(0, 64), :].astype(BF16)
            halo(k, z - 1).start()

        return carry

    lax.fori_loop(0, 3, attend, 0)
    reduce.middle()
    lax.fori_loop(3, 7, attend, 0)
    down.pass_on()
    lax.fori_loop(7, groups, attend, 0)

    def restore(k, carry):
        @pl.when(z < members - 1)
        def _():
            halo(k, z).wait_recv()
            key_value[k, pl.ds(rows - 64, 64), :] = (
                ending[k] + arriving[k].astype(F32)
            ).astype(BF16)

        hot = hot_of(notes_all, k, rows)
        ordered = jnp.concatenate([query_part[k], key_value[k]], axis=1)
        back = jnp.dot(hot, ordered, preferred_element_type=F32).astype(BF16)
        out[:, pl.ds(k, 1)] = back.reshape(groups, 1, rows // groups, 768)
        return carry

    lax.fori_loop(0, groups, restore, 0)
    reduce.end()

    def body(span):
        result[span, :] = (middle[span, :] + reduce.rows_of(span)).astype(BF16)

    each_chunk(rows, body)
    down.finish()
    units.finish()
    for copy in gather.copies:
        copy.wait_send()
    reduce.finish()

    @pl.when(z > 0)
    def _():
        def done(k, carry):
            halo(k, z - 1).wait_send()
            return carry

        lax.fori_loop(0, groups, done, 0)


def attend_back(
    kept, branch, w_out, notes_all, activated, w_down, middle, both_sum, down_in, scale
):
    groups = kept.shape[0]
    rows, width = middle.shape
    members = both_sum.shape[0]
    dma = pltpu.SemaphoreType.DMA
    shape = jax.ShapeDtypeStruct
    return pl.pallas_call(
        functools.partial(backward_kernel, scale=scale, groups=groups, rows=rows),
        out_shape=(
            shape((groups, groups, rows // groups, 768), BF16),
            shape((rows, width), BF16),
            shape((groups, rows, width), BF16),
            shape((members, width, 256), BF16),
            shape((groups, LANES, width), BF16),
        ),
        in_specs=[on_chip()] * 7 + [anywhere()] * 2,
        out_specs=(on_chip(),) * 2 + (anywhere(),) * 3,
        scratch_shapes=[
            pltpu.VMEM((rows + 64, 512), F32),
            pltpu.VMEM((groups, rows, 256), BF16),
            pltpu.VMEM((groups, rows, 512), BF16),
            pltpu.VMEM((groups, 64, 512), F32),
            pltpu.VMEM((groups, 64, 512), BF16),
            pltpu.VMEM((groups, 64, 512), BF16),
            dma((groups,)),
            dma((groups,)),
        ]
        + reduce_scratch(rows, width)
        + [
            pltpu.VMEM((groups, groups, rows // groups, 256), BF16),
            pltpu.VMEM((2, rows, width), BF16),
            dma((3,)),
            dma((13,)),
            dma((13,)),
            pltpu.VMEM((2, width, 256), BF16),
            dma((6,)),
            dma((10,)),
            dma((3,)),
            pltpu.VMEM((members, LANES, width), BF16),
            dma((13,)),
            dma((13,)),
        ],
        compiler_params=remote_params(3, 63 * 1024 * 1024),
        cost_estimate=pl.CostEstimate(flops=0, bytes_accessed=300_000_000, transcendentals=0),
        name="attend_back",
    )(kept, branch, w_out, notes_all, activated, w_down, middle, both_sum, down_in)


def middle_kernel(
    mixed, w_out, tokens, gain, w_down, middle, hidden, down_all,
    part, from_side, from_corner, from_near, send, recv, down_own, send_c, recv_c, local,
):
    units = pl.ds(pl.multiple_of(lax.axis_index("dp") * LANES, LANES), LANES)
    load = pltpu.make_async_copy(w_down.at[units], down_own, local.at[0])
    load.start()
    greet_all(pltpu.get_barrier_semaphore())
    load.wait()
    chain = Chain(down_own, down_all, send_c, recv_c, local.at[1])
    chain.step(0)
    reduce = Reduce(mixed, w_out, False, part, from_side, from_corner, from_near, send, recv)
    reduce.begin()
    chain.step(1)
    reduce.middle()
    chain.step(2)
    reduce.end()

    def body(span):
        values = tokens[span, :].astype(F32) + reduce.rows_of(span)
        middle[span, :] = values
        inverse = lax.rsqrt(mean_rows(values * values) + EPSILON)
        hidden[span, :] = (values * inverse * gain[...]).astype(BF16)

    each_chunk(hidden.shape[0], body)
    chain.finish()
    reduce.finish()


def project_middle(mixed, w_out, tokens, gain, w_down):
    rows, width = tokens.shape
    dma = pltpu.SemaphoreType.DMA
    members = lax.axis_size("mp")
    return pl.pallas_call(
        middle_kernel,
        out_shape=(
            jax.ShapeDtypeStruct((rows, width), F32),
            jax.ShapeDtypeStruct((rows, width), BF16),
            jax.ShapeDtypeStruct((members, LANES, width), BF16),
        ),
        in_specs=[on_chip()] * 4 + [anywhere()],
        out_specs=(on_chip(), on_chip(), anywhere()),
        scratch_shapes=reduce_scratch(rows, width)
        + [pltpu.VMEM((LANES, width), BF16), dma((6,)), dma((6,)), dma((2,))],
        compiler_params=remote_params(4),
        cost_estimate=pl.CostEstimate(flops=0, bytes_accessed=150_000_000, transcendentals=0),
        name="project_middle",
    )(mixed, w_out, tokens, gain, w_down)


def norm_back_rows(gradient, values, gain, sums, span):
    inverse = lax.rsqrt(mean_rows(values * values) + EPSILON)
    normed = values * inverse
    product = gradient * normed
    folded = product[0:8]
    for step in range(1, CHUNK // 8):
        folded = folded + product[step * 8 : step * 8 + 8]
    sums[...] += folded
    scaled = gradient * gain
    return inverse * (scaled - normed * mean_rows(scaled * normed))


def feed_kernel(
    hidden_own, cotangent_all, middle, cotangent, gain, w_both, w_down,
    middle_grad, branch, sums, activated, both_sum, down_in,
    hidden_all, both_grad, part, from_side, from_corner, from_near, send_r, recv_r,
    send_a, recv_a, cot_half, cot_tile, stage_both, down_sum, load_sem, local, send_z, recv_z,
):
    groups, rows, width = hidden_all.shape
    members = w_both.shape[0]
    half_rows = rows // 2
    me, side, over_x, over_y, _ = plane()
    own = pltpu.make_async_copy(hidden_own, hidden_all.at[me], local.at[0])
    own.start()
    start_middle = pltpu.make_async_copy(middle, middle_grad, local.at[1])
    start_middle.start()

    def place_of(step):
        block = step // 4
        near = ((block + 1) // 2) % 2
        far = block // 3
        mixed_order = near * (1 - block // 2)
        second = mixed_order * (step % 2) + (1 - mixed_order) * ((step // 2) % 2)
        half = mixed_order * ((step % 2 + (step // 2) % 2) % 2) + (1 - mixed_order) * (step % 2)
        other = (1 - near) * second + (block // 2) * near
        in_x = near * (1 - second) + far
        in_y = near * second + far
        owner = me + in_x * (over_x - me) + in_y * (over_y - me) + other * (side - me)
        slot = 4 * other + 3 * (1 - near) * (1 - far) + near * (1 + second)
        return owner, half, slot

    def load_cotangent(step):
        owner, half, _ = place_of(step)
        span = pl.ds(pl.multiple_of(half * half_rows, half_rows), half_rows)
        return pltpu.make_async_copy(
            cotangent_all.at[owner, span], cot_half.at[step % 2], load_sem.at[step % 2]
        )

    load_cotangent(0).start()
    greet_all(pltpu.get_barrier_semaphore())
    own.wait()
    gather = Gather(None, hidden_all, send_a, recv_a)
    gather.start()
    reduce = Reduce(None, None, False, part, from_side, from_corner, from_near, send_r, recv_r)
    reduce.prepare()

    def before(step, *numbers):
        return (step, lambda: gather.arrive(*numbers))

    def nears():
        reduce.add_side(1)
        reduce.nears[0].start()
        reduce.add_side(2)
        reduce.nears[2].start()

    early = [
        before(2, 4),
        before(4, 0),
        before(5, 1),
        before(6, 2),
        before(7, 3),
        before(8, 6, 9),
        before(10, 8, 10),
        before(12, 5, 7),
        (13, nears),
        before(14, 11, 12),
    ]
    late = [(3, 3), (9, 1), (11, 2), (15, 0)]

    def unit(step, carry):
        for number, action in early:
            pl.when(step == number)(action)

        @pl.when(step < 15)
        def _():
            load_cotangent(step + 1).start()

        load_cotangent(step).wait()
        owner, half, slot = place_of(step)
        span = pl.ds(pl.multiple_of(half * half_rows, half_rows), half_rows)
        mine = hidden_all[owner, span, :]
        grads = cot_half[step % 2]
        for z in range(members):
            raw = jnp.dot(mine, w_both[z], preferred_element_type=F32)
            units = pl.ds(z * 128, 128)
            if z % 2 == 0:
                pair = lax.dot_general(
                    grads, w_down[pl.ds(z * 128, 256), :], NT, preferred_element_type=F32
                )
            active_grad = pair[:, 128 * (z % 2) : 128 * (z % 2) + 128]
            gate, upward = raw[:, :128], raw[:, 128:]
            sigmoid = jax.nn.sigmoid(gate)
            activated[owner, span, units] = (gate * sigmoid * upward).astype(BF16)
            both_grad[owner, span, pl.ds(z * 256, 128)] = (
                active_grad * upward * sigmoid * (1.0 + gate * (1.0 - sigmoid))
            ).astype(BF16)
            both_grad[owner, span, pl.ds(z * 256 + 128, 128)] = (
                active_grad * gate * sigmoid
            ).astype(BF16)

        def tile(t, inner):
            columns = pl.ds(pl.multiple_of(t * 256, 256), 256)
            value = sum(
                lax.dot_general(
                    both_grad[owner, span, pl.ds(z * 256, 256)],
                    w_both[z, columns, :],
                    NT,
                    preferred_element_type=F32,
                )
                for z in range(members)
            )
            part[slot, span, columns] = value.astype(BF16)
            return inner

        lax.fori_loop(0, width // 256, tile, 0)
        for number, share in late:
            pl.when(step == number)(reduce.shares[share].start)
        return carry

    lax.fori_loop(0, 16, unit, 0)

    def load_tile(t):
        columns = pl.ds(pl.multiple_of(t * 256, 256), 256)
        return pltpu.make_async_copy(
            cotangent_all.at[:, :, columns], cot_tile.at[t % 2], load_sem.at[2 + t % 2]
        )

    def store_both(t):
        columns = pl.ds(pl.multiple_of(t * 256, 256), 256)
        return pltpu.make_async_copy(
            stage_both.at[t % 2], both_sum.at[:, columns], load_sem.at[4 + t % 2]
        )

    tiles = width // 256
    count = groups * rows

    def down_tile(t, carry):
        columns = pl.ds(pl.multiple_of(t * 256, 256), 256)

        @pl.when(t < tiles - 1)
        def _():
            load_tile(t + 1).start()

        load_tile(t).wait()
        down_sum[:, columns] = lax.dot_general(
            activated[...].reshape(count, members * 128),
            cot_tile[t % 2].reshape(count, 256),
            TN,
            preferred_element_type=F32,
        ).astype(BF16)
        return carry

    z = lax.axis_index("mp")

    def down_rows(owner):
        return down_sum.at[pl.ds(pl.multiple_of(owner * LANES, LANES), LANES)]

    keep_down = pltpu.make_async_copy(down_rows(z), down_in.at[z], local.at[2])
    pass_down = [
        to_mp(
            down_rows(lax.rem(z + step, members)),
            down_in.at[z],
            send_z.at[step - 1],
            recv_z.at[step - 1],
            lax.rem(z + step, members),
        )
        for step in range(1, members)
    ]

    def weight_tile(t, carry):
        columns = pl.ds(pl.multiple_of(t * 256, 256), 256)

        @pl.when(t >= 2)
        def _():
            store_both(t - 2).wait()

        value = lax.dot_general(
            hidden_all[:, :, columns].reshape(count, 256),
            both_grad[...].reshape(count, members * 256),
            TN,
            preferred_element_type=F32,
        )
        for z in range(members):
            stage_both[t % 2, z] = value[:, z * 256 : z * 256 + 256].astype(BF16)
        store_both(t).start()
        return carry

    load_tile(0).start()
    reduce.add_side(0)
    reduce.corners[0].start()
    reduce.corners[1].start()
    lax.fori_loop(0, tiles, down_tile, 0)
    keep_down.start()
    for copy in pass_down:
        copy.start()
    lax.fori_loop(0, 2, weight_tile, 0)
    reduce.middle()
    lax.fori_loop(2, tiles, weight_tile, 0)
    reduce.end()
    start_middle.wait()
    sums[...] = jnp.zeros_like(sums)

    def body(span):
        change = norm_back_rows(reduce.rows_of(span), middle_grad[span, :], gain[...], sums, span)
        total = cotangent[span, :].astype(F32) + change
        middle_grad[span, :] = total
        branch[span, :] = total.astype(BF16)

    each_chunk(rows, body)
    gather.sent()
    reduce.finish()
    for t in (tiles - 2, tiles - 1):
        store_both(t).wait()
    keep_down.wait()
    for copy in pass_down:
        copy.wait()


def feed(hidden_own, cotangent_all, middle, cotangent, gain, w_both, w_down):
    groups, rows, width = cotangent_all.shape
    members = w_both.shape[0]
    dma = pltpu.SemaphoreType.DMA
    units = members * 128
    return pl.pallas_call(
        feed_kernel,
        out_shape=(
            jax.ShapeDtypeStruct((rows, width), F32),
            jax.ShapeDtypeStruct((rows, width), BF16),
            jax.ShapeDtypeStruct((8, width), F32),
            jax.ShapeDtypeStruct((groups, rows, units), BF16),
            jax.ShapeDtypeStruct((members, width, 256), BF16),
            jax.ShapeDtypeStruct((members, LANES, width), BF16),
        ),
        in_specs=[anywhere()] * 3 + [on_chip()] * 4,
        out_specs=(on_chip(),) * 4 + (anywhere(),) * 2,
        scratch_shapes=[
            pltpu.VMEM((groups, rows, width), BF16),
            pltpu.VMEM((groups, rows, 2 * units), BF16),
        ]
        + reduce_scratch(rows, width)
        + [
            dma((13,)),
            dma((13,)),
            pltpu.VMEM((2, rows // 2, width), BF16),
            pltpu.VMEM((2, groups, rows, 256), BF16),
            pltpu.VMEM((2, members, 256, 256), BF16),
            pltpu.VMEM((units, width), BF16),
            dma((6,)),
            dma((3,)),
            dma((3,)),
            dma((3,)),
        ],
        compiler_params=remote_params(5, 62 * 1024 * 1024),
        cost_estimate=pl.CostEstimate(flops=0, bytes_accessed=400_000_000, transcendentals=0),
        name="feed",
    )(hidden_own, cotangent_all, middle, cotangent, gain, w_both, w_down)


def input_kernel(
    qkv_grad, w_qkv, hidden_all, branch_all, mixed, tokens, middle_grad, gain, sums_two,
    both_sum, both_in,
    result, gains, both_all, heads_all,
    part, from_side, from_corner, from_near, send, recv, sums,
    stage, arrive, send_h, recv_s, recv_h, own, plane_sums, column_sums, send_p, recv_p,
    weight_sum, row_tile, tile_sem, send_b, recv_b, send_t, recv_t, both_found, heads_own, local,
):
    me, z = lax.axis_index("dp"), lax.axis_index("mp")
    count = qkv_grad.shape[0]
    tiles = tokens.shape[1] // 256
    outer = (z == 0) | (z == 3)

    def columns_of(t):
        return pl.ds(pl.multiple_of(lax.rem(t, tiles) * 256, 256), 256)

    def load(t, source):
        return pltpu.make_async_copy(
            source.at[:, :, columns_of(t)], row_tile.at[t % 2], tile_sem.at[t % 2]
        )

    own_part = pltpu.make_async_copy(both_sum.at[z], both_found.at[0], local.at[0])
    own_part.start()
    ways = [(outer, 1, 1), (outer, 2, 2)]
    ways += [(z == 1, 0, 1), (z == 1, 2, 2), (z == 1, 3, 3)]
    ways += [(z == 2, 0, 1), (z == 2, 1, 2), (z == 2, 3, 3)]

    def came(source, place):
        return pltpu.make_async_copy(both_in.at[source], both_found.at[place], local.at[place])

    for here, source, place in ways:
        pl.when(here)(came(source, place).start)

    @pl.when(outer)
    def _():
        both_found[3] = jnp.zeros_like(both_found[3])

    load(0, branch_all).start()
    greet_all(pltpu.get_barrier_semaphore())
    own_part.wait()
    for here, source, place in ways:
        pl.when(here)(came(source, place).wait)

    def add(span):
        value = both_found[0, span, :].astype(F32) + both_found[1, span, :].astype(F32)
        value = value + both_found[2, span, :].astype(F32) + both_found[3, span, :].astype(F32)
        both_found[0, span, :] = value.astype(BF16)

    each_chunk(both_found.shape[1], add)
    both = Gather(both_found.at[0], both_all, send_b, recv_b, local.at[4])
    both.start()

    def weight_tile(t, carry):
        @pl.when(t < tiles - 1)
        def _():
            load(t + 1, branch_all).start()

        @pl.when((t >= tiles - 1) & (t < 2 * tiles - 1))
        def _():
            load(t + 1, hidden_all).start()

        load(t, hidden_all).wait()

        @pl.when(t < tiles)
        def _():
            weight_sum[pl.ds(768, 256), columns_of(t)] = lax.dot_general(
                mixed[...], row_tile[t % 2].reshape(count, 256), TN, preferred_element_type=F32
            ).astype(BF16)

        @pl.when(t >= tiles)
        def _():
            weight_sum[pl.ds(0, 768), columns_of(t)] = lax.dot_general(
                qkv_grad[...], row_tile[t % 2].reshape(count, 256), TN, preferred_element_type=F32
            ).astype(BF16)

        return carry

    heads = Heads(weight_sum, stage, arrive, send_h, recv_s, recv_h)
    lax.fori_loop(0, tiles, weight_tile, 0)
    heads.start((3,))
    lax.fori_loop(tiles, 2 * tiles, weight_tile, 0)
    heads.start((0, 1, 2))
    reduce = Reduce(qkv_grad, w_qkv, False, part, from_side, from_corner, from_near, send, recv)
    reduce.begin()
    both.pass_on()
    heads.add((3, 0))
    reduce.middle()
    heads.add((1, 2))
    reduce.end()
    sums[...] = jnp.zeros_like(sums)

    def body(span):
        values = tokens[span, :].astype(F32)
        change = norm_back_rows(reduce.rows_of(span), values, gain[...], sums, span)
        result[span, :] = (middle_grad[span, :] + change).astype(BF16)

    each_chunk(result.shape[0], body)
    own[...] = jnp.concatenate(
        [
            jnp.sum(sums[...], axis=0, keepdims=True),
            jnp.sum(sums_two[...], axis=0, keepdims=True),
        ],
        axis=0,
    )
    swaps = swap_all(own, plane_sums, send_p, recv_p)
    for copy in swaps:
        copy.start()
    plane_sums[me] = own[...]
    heads.total(heads_own)
    gather = Gather(heads_own, heads_all, send_t, recv_t, local.at[5])
    gather.start()
    for copy in swaps:
        copy.wait()
    found = plane_sums[0]
    for other in range(1, 8):
        found = found + plane_sums[other]
    column_sums[z] = found
    passes = [
        to_mp(
            column_sums.at[z],
            column_sums.at[z],
            send_p.at[6 + step],
            recv_p.at[6 + step],
            lax.rem(z + step, 4),
        )
        for step in range(1, 4)
    ]
    for copy in passes:
        copy.start()
    both.finish()
    for copy in passes:
        copy.wait()
    gains[...] = (column_sums[0] + column_sums[1]) + (column_sums[2] + column_sums[3])
    gather.pass_on()
    heads.finish_send()
    reduce.finish()
    gather.finish()


def project_input(
    qkv_grad, w_qkv, hidden_all, branch_all, mixed, tokens, middle_grad, gain, sums_two,
    both_sum, both_in,
):
    rows, width = tokens.shape
    groups = hidden_all.shape[0]
    dma = pltpu.SemaphoreType.DMA
    shape = jax.ShapeDtypeStruct
    return pl.pallas_call(
        input_kernel,
        out_shape=(
            shape((rows, width), BF16),
            shape((2, width), F32),
            shape((groups, width, 256), BF16),
            shape((groups, 4 * HEAD_DIM, width // 2), BF16),
        ),
        in_specs=[on_chip()] * 2 + [anywhere()] * 2 + [on_chip()] * 5 + [anywhere()] * 2,
        out_specs=(on_chip(),) * 2 + (anywhere(),) * 2,
        scratch_shapes=reduce_scratch(rows, width)
        + [
            pltpu.VMEM((8, width), F32),
            pltpu.VMEM((2, 4, HEAD_DIM, width), BF16),
            pltpu.VMEM((3, 4, HEAD_DIM, width // 2), BF16),
            dma((16,)),
            dma((8,)),
            dma((12,)),
            pltpu.VMEM((2, width), F32),
            pltpu.VMEM((8, 2, width), F32),
            pltpu.VMEM((4, 2, width), F32),
            dma((10,)),
            dma((10,)),
            pltpu.VMEM((8 * LANES, width), BF16),
            pltpu.VMEM((2, groups, rows, 256), BF16),
            dma((2,)),
            dma((13,)),
            dma((13,)),
            dma((13,)),
            dma((13,)),
            pltpu.VMEM((4, width, 256), BF16),
            pltpu.VMEM((4 * HEAD_DIM, width // 2), BF16),
            dma((6,)),
        ],
        compiler_params=remote_params(6, 63 * 1024 * 1024),
        cost_estimate=pl.CostEstimate(flops=0, bytes_accessed=250_000_000, transcendentals=0),
        name="project_input",
    )(
        qkv_grad, w_qkv, hidden_all, branch_all, mixed, tokens, middle_grad, gain, sums_two,
        both_sum, both_in,
    )


def units_kernel(both, gate, upward):
    for d in range(both.shape[0]):
        gate[:, d * 128 : d * 128 + 128] = both[d, :, :128].astype(F32)
        upward[:, d * 128 : d * 128 + 128] = both[d, :, 128:].astype(F32)


def assemble_units(both):
    groups, width, wide = both.shape
    tile = 256
    shape = jax.ShapeDtypeStruct((width, groups * wide // 2), F32)
    spec = pl.BlockSpec((tile, groups * wide // 2), lambda i: (i, 0))
    return pl.pallas_call(
        units_kernel,
        grid=(width // tile,),
        out_shape=(shape, shape),
        in_specs=[pl.BlockSpec((groups, tile, wide), lambda i: (0, i, 0))],
        out_specs=(spec, spec),
        cost_estimate=pl.CostEstimate(flops=0, bytes_accessed=22_000_000, transcendentals=0),
        name="assemble_units",
    )(both)


def heads_kernel(whole, *outs):
    columns = whole.shape[4]
    for kind, out in enumerate(outs):
        for half in range(whole.shape[1]):
            out[:, half * columns : half * columns + columns] = whole[0, half, kind].astype(F32)


def assemble_heads(whole):
    chips, halves, kinds, rows, columns = whole.shape
    shape = jax.ShapeDtypeStruct((chips * rows, halves * columns), F32)
    spec = pl.BlockSpec((rows, halves * columns), lambda c: (c, 0))
    return pl.pallas_call(
        heads_kernel,
        grid=(chips,),
        out_shape=(shape,) * kinds,
        in_specs=[pl.BlockSpec((1, halves, kinds, rows, columns), lambda c: (c, 0, 0, 0, 0))],
        out_specs=(spec,) * kinds,
        cost_estimate=pl.CostEstimate(flops=0, bytes_accessed=20_000_000, transcendentals=0),
        name="assemble_heads",
    )(whole)


def swapped(
    tokens, cotangent, route, lengths, key_mask, norm1_gain, norm2_gain,
    w_query, w_key, w_value, w_out, w_gate, w_up, w_down,
):
    groups = lax.axis_size("dp")
    members = lax.axis_size("mp")
    me = lax.axis_index("dp")
    z = lax.axis_index("mp")
    rows, width = tokens.shape
    bucket = rows // groups
    units = w_down.shape[0] // groups

    target = route // TOK_DEV
    earlier = jnp.arange(rows, dtype=jnp.int32)
    same = (target[:, None] == target[None, :]) & (earlier[None, :] < earlier[:, None])
    send_at = target * bucket + jnp.sum(same.astype(jnp.int32), axis=1)
    sorting = send_at[None, :] == earlier[:, None]
    slots_own = jnp.sum(jnp.where(sorting, (route % rows)[None, :], 0), axis=1)
    sort_hot = sorting.astype(BF16)

    mask_window = lax.dynamic_slice_in_dim(
        jnp.concatenate([jnp.zeros((WINDOW,), jnp.int32), key_mask]), z * rows, rows + WINDOW
    )
    slot_rows = jnp.pad(slots_own.reshape(groups, bucket).T, ((0, 0), (0, LANES - groups)))
    mask_rows = jnp.pad(mask_window, (0, 4 * LANES - rows - WINDOW)).reshape(4, LANES)
    length_rows = jnp.pad(lengths, ((0, 3), (0, LANES - lengths.shape[1])))
    notes = jnp.concatenate([slot_rows, mask_rows, length_rows], axis=0).astype(F32)

    count = groups * rows
    scale = HEAD_DIM ** (-0.5)
    (
        hidden_one,
        w_qkv,
        w_proj,
        notes_all,
        w_both,
        mixed,
        kept,
        tokens_b,
        cotangent_b,
        cotangent_all,
    ) = attend_ahead(
        tokens,
        cotangent,
        send_at.astype(F32)[None],
        norm1_gain[None],
        notes,
        w_query.T,
        w_key.T,
        w_value.T,
        w_out,
        w_gate,
        w_up,
        scale,
    )
    mixed = mixed.reshape(count, 2 * LANES)
    middle, hidden_two, down_all = project_middle(mixed, w_proj, tokens_b, norm2_gain[None], w_down)
    down_all = down_all.reshape(members * units, width)
    middle_grad, branch, sums_two, activated, both_sum, down_in = feed(
        hidden_two, cotangent_all, middle, cotangent_b, norm2_gain[None], w_both, down_all
    )
    qkv_grad, output_rows, branch_all, both_in, down_whole = attend_back(
        kept,
        branch,
        w_proj,
        notes_all,
        activated.reshape(count, units * members),
        down_all,
        middle,
        both_sum,
        down_in,
        scale,
    )
    qkv_grad = qkv_grad.reshape(count, 6 * LANES)
    input_rows, gain_sums, both_whole, heads_whole = project_input(
        qkv_grad,
        w_qkv,
        hidden_one,
        branch_all,
        mixed,
        tokens_b,
        middle_grad,
        norm1_gain[None],
        sums_two,
        both_sum,
        both_in,
    )
    gate_grad, up_grad = assemble_units(both_whole)
    down_grad = down_whole.astype(F32).reshape(groups * units, width)
    query_grad, key_grad, value_grad, proj_grad = assemble_heads(
        heads_whole.reshape(groups // 2, 2, 4, HEAD_DIM, width // 2)
    )

    unsort = (((0,), (0,)), ((), ()))
    return (
        lax.dot_general(sort_hot, output_rows, unsort, preferred_element_type=F32).astype(BF16),
        lax.dot_general(sort_hot, input_rows, unsort, preferred_element_type=F32).astype(BF16),
        gain_sums[0],
        gain_sums[1],
        query_grad.T,
        key_grad.T,
        value_grad.T,
        proj_grad,
        gate_grad,
        up_grad,
        down_grad,
    )


def solution(mesh):
    in_specs = (
        P(("dp", "mp"), None),
        P(("dp", "mp"), None),
        P(("dp", "mp")),
        P("dp", None),
        P("dp"),
        P(),
        P(),
        P(None, "mp"),
        P(None, "mp"),
        P(None, "mp"),
        P("mp", None),
        P(None, "mp"),
        P(None, "mp"),
        P("mp", None),
    )
    out_specs = (
        P(("dp", "mp"), None),
        P(("dp", "mp"), None),
        P(),
        P(),
        P(None, "mp"),
        P(None, "mp"),
        P(None, "mp"),
        P("mp", None),
        P(None, "mp"),
        P(None, "mp"),
        P("mp", None),
    )
    body = swapped if (mesh.shape["dp"], mesh.shape["mp"]) == (8, 4) else local
    return jax.shard_map(body, mesh=mesh, in_specs=in_specs, out_specs=out_specs, check_vma=False)
```

```python
import functools

import jax
import jax.numpy as jnp
from jax import lax
from jax.experimental import pallas as pl
from jax.experimental.pallas import tpu as pltpu
from jax.sharding import PartitionSpec as P

HEAD_DIM = 112
WINDOW = 64
TOK_DEV = 1536


EPSILON = 1e-05
MASKED = 1e30


def norm_rows(values):
    inverse = lax.rsqrt(jnp.mean(values * values, axis=-1, keepdims=True) + EPSILON)
    return (values * inverse, inverse)


def norm_back(gradient, normed, inverse, norm_gain):
    scaled = gradient * norm_gain
    result = inverse * (scaled - normed * jnp.mean(scaled * normed, axis=-1, keepdims=True))
    return (result, jnp.sum(gradient * normed, axis=0))


def padded(values, filler):
    front = jnp.full((WINDOW,) + values.shape[1:], filler, values.dtype)
    return jnp.concatenate([front, values], axis=0)


def block_scores(query_block, key_block, query_seg, key_seg, key_flag, first_row, score_scale):
    query_pos = first_row + jnp.arange(query_block.shape[0], dtype=jnp.int32)
    key_pos = first_row - WINDOW + jnp.arange(key_block.shape[0], dtype=jnp.int32)
    distance = query_pos[:, None] - key_pos[None, :]
    allowed = (distance >= 0) & (distance < WINDOW) & (query_seg[:, None] == key_seg[None, :])
    allowed = allowed & ((key_flag[None, :] == 1) | (distance == 0))
    raw_scores = (
        jnp.einsum("qhd,khd->hqk", query_block, key_block, preferred_element_type=jnp.float32)
        * score_scale
    )
    return jnp.where(allowed[None], raw_scores, -MASKED)


def block_inputs(query, key_pad, value_pad, segment, seg_pad, live_pad, first_row, block_rows):
    key_span = block_rows + WINDOW
    return (
        lax.dynamic_slice_in_dim(query, first_row, block_rows, 0),
        lax.dynamic_slice_in_dim(key_pad, first_row, key_span, 0),
        lax.dynamic_slice_in_dim(value_pad, first_row, key_span, 0),
        lax.dynamic_slice_in_dim(segment, first_row, block_rows, 0),
        lax.dynamic_slice_in_dim(seg_pad, first_row, key_span, 0),
        lax.dynamic_slice_in_dim(live_pad, first_row, key_span, 0),
    )


def attend_forward(query, key_all, value_all, segment, key_live):
    token_count, head_count, head_width = query.shape
    block_rows = min(512, token_count)
    score_scale = head_width ** (-0.5)
    key_pad = padded(key_all, 0.0)
    value_pad = padded(value_all, 0.0)
    seg_pad = padded(segment, -1)
    live_pad = padded(key_live, 0)

    def one_block(running, block_index):
        first_row = block_index * block_rows
        query_block, key_block, value_block, query_seg, key_seg, key_flag = block_inputs(
            query, key_pad, value_pad, segment, seg_pad, live_pad, first_row, block_rows
        )
        scores = block_scores(
            query_block, key_block, query_seg, key_seg, key_flag, first_row, score_scale
        )
        row_max = jnp.max(scores, axis=-1, keepdims=True)
        weights = jnp.exp(scores - row_max)
        denominator = jnp.sum(weights, axis=-1, keepdims=True)
        chances = (weights / denominator).astype(jnp.bfloat16)
        mixed = jnp.einsum("hqk,khd->qhd", chances, value_block, preferred_element_type=jnp.float32)
        return (
            running,
            (mixed.astype(jnp.bfloat16), row_max[..., 0] + jnp.log(denominator[..., 0])),
        )

    _, (mixed, logsum) = lax.scan(
        one_block, jnp.zeros((), jnp.int32), jnp.arange(token_count // block_rows, dtype=jnp.int32)
    )
    return (mixed.reshape(token_count, head_count * head_width), logsum)


def attend_backward(query, key_all, value_all, segment, key_live, logsum, mixed_grad):
    token_count, head_count, head_width = query.shape
    block_rows = min(512, token_count)
    key_span = block_rows + WINDOW
    score_scale = head_width ** (-0.5)
    key_pad = padded(key_all, 0.0)
    value_pad = padded(value_all, 0.0)
    seg_pad = padded(segment, -1)
    live_pad = padded(key_live, 0)

    def one_block(running, inputs):
        key_grad, value_grad = running
        block_index, block_logsum = inputs
        first_row = block_index * block_rows
        query_block, key_block, value_block, query_seg, key_seg, key_flag = block_inputs(
            query, key_pad, value_pad, segment, seg_pad, live_pad, first_row, block_rows
        )
        grad_block = lax.dynamic_slice_in_dim(mixed_grad, first_row, block_rows, 0)
        scores = block_scores(
            query_block, key_block, query_seg, key_seg, key_flag, first_row, score_scale
        )
        chances = jnp.exp(scores - block_logsum[..., None])
        chance_grad = jnp.einsum(
            "qhd,khd->hqk", grad_block, value_block, preferred_element_type=jnp.float32
        )
        row_dot = jnp.sum(chances * chance_grad, axis=-1, keepdims=True)
        score_grad = (chances * (chance_grad - row_dot)).astype(jnp.bfloat16)
        query_grad = (
            jnp.einsum("hqk,khd->qhd", score_grad, key_block, preferred_element_type=jnp.float32)
            * score_scale
        )
        key_part = (
            jnp.einsum("hqk,qhd->khd", score_grad, query_block, preferred_element_type=jnp.float32)
            * score_scale
        )
        value_part = jnp.einsum(
            "hqk,qhd->khd",
            chances.astype(jnp.bfloat16),
            grad_block,
            preferred_element_type=jnp.float32,
        )
        key_grad = lax.dynamic_update_slice_in_dim(
            key_grad,
            lax.dynamic_slice_in_dim(key_grad, first_row, key_span, 0) + key_part,
            first_row,
            0,
        )
        value_grad = lax.dynamic_update_slice_in_dim(
            value_grad,
            lax.dynamic_slice_in_dim(value_grad, first_row, key_span, 0) + value_part,
            first_row,
            0,
        )
        return ((key_grad, value_grad), query_grad)

    empty_grad = jnp.zeros((token_count + WINDOW, head_count, head_width), jnp.float32)
    (key_grad, value_grad), query_grad = lax.scan(
        one_block,
        (empty_grad, empty_grad),
        (jnp.arange(token_count // block_rows, dtype=jnp.int32), logsum),
    )
    flat_width = head_count * head_width
    return (
        query_grad.reshape(token_count, flat_width).astype(jnp.bfloat16),
        key_grad[WINDOW:].reshape(token_count, flat_width).astype(jnp.bfloat16),
        value_grad[WINDOW:].reshape(token_count, flat_width).astype(jnp.bfloat16),
    )


def local(
    tokens,
    cotangent,
    route,
    lengths,
    key_mask,
    norm1_gain,
    norm2_gain,
    w_query,
    w_key,
    w_value,
    w_out,
    w_gate,
    w_up,
    w_down,
):
    groups = lax.axis_size("dp")
    members = lax.axis_size("mp")
    member = lax.axis_index("mp")
    local_rows = tokens.shape[0]
    group_rows = local_rows * members
    bucket = local_rows // groups
    target = route // TOK_DEV
    chosen = (target[:, None] == jnp.arange(groups, dtype=jnp.int32)[None, :]).astype(jnp.int32)
    ranking = jnp.sum((jnp.cumsum(chosen, axis=0) - chosen) * chosen, axis=1)
    send_at = target * bucket + ranking
    arrival, arrival_grad, arrival_slot = (
        lax.all_to_all(
            jnp.zeros_like(tokens).at[send_at].set(tokens),
            "dp",
            split_axis=0,
            concat_axis=0,
            tiled=True,
        ),
        lax.all_to_all(
            jnp.zeros_like(cotangent).at[send_at].set(cotangent),
            "dp",
            split_axis=0,
            concat_axis=0,
            tiled=True,
        ),
        lax.all_to_all(
            jnp.zeros_like(route).at[send_at].set(route % local_rows),
            "dp",
            split_axis=0,
            concat_axis=0,
            tiled=True,
        ),
    )
    token_rows = jnp.zeros_like(arrival).at[arrival_slot].set(arrival)
    grad_rows = jnp.zeros_like(arrival_grad).at[arrival_slot].set(arrival_grad)
    seq_ends = jnp.cumsum(lengths[0])
    positions = jnp.arange(group_rows, dtype=jnp.int32)
    segment = jnp.sum((positions[:, None] >= seq_ends[None, :]).astype(jnp.int32), axis=1)
    input_rows = token_rows.astype(jnp.float32)
    normed_one, inverse_one = norm_rows(input_rows)
    leading_all, grad_all = (
        lax.all_gather(token_rows, "mp", axis=0, tiled=True),
        lax.all_gather(grad_rows, "mp", axis=0, tiled=True),
    )
    input_all = leading_all.astype(jnp.float32)
    normed_all, _ = norm_rows(input_all)
    hidden_one = (normed_all * norm1_gain).astype(jnp.bfloat16)
    head_count = w_query.shape[1] // HEAD_DIM
    query = jnp.dot(hidden_one, w_query, preferred_element_type=jnp.float32).astype(jnp.bfloat16)
    keys = jnp.dot(hidden_one, w_key, preferred_element_type=jnp.float32).astype(jnp.bfloat16)
    values = jnp.dot(hidden_one, w_value, preferred_element_type=jnp.float32).astype(jnp.bfloat16)
    query_heads = query.reshape(group_rows, head_count, HEAD_DIM)
    key_heads = keys.reshape(group_rows, head_count, HEAD_DIM)
    value_heads = values.reshape(group_rows, head_count, HEAD_DIM)
    mixed_flat, logsum = attend_forward(query_heads, key_heads, value_heads, segment, key_mask)
    attention_all = lax.psum(jnp.dot(mixed_flat, w_out, preferred_element_type=jnp.float32), "mp")
    middle_all = input_all + attention_all
    middle_rows = lax.dynamic_slice_in_dim(middle_all, member * local_rows, local_rows, 0)
    normed_mid, _ = norm_rows(middle_all)
    hidden_two = (normed_mid * norm2_gain).astype(jnp.bfloat16)
    normed_two, inverse_two = norm_rows(middle_rows)
    gate_value = jnp.dot(hidden_two, w_gate, preferred_element_type=jnp.float32)
    upward = jnp.dot(hidden_two, w_up, preferred_element_type=jnp.float32)
    sigmoid = jax.nn.sigmoid(gate_value)
    activated = (gate_value * sigmoid * upward).astype(jnp.bfloat16)
    out_rows = middle_rows + lax.psum_scatter(
        jnp.dot(activated, w_down, preferred_element_type=jnp.float32).astype(jnp.bfloat16),
        "mp",
        scatter_dimension=0,
        tiled=True,
    ).astype(jnp.float32)
    activated_grad = jnp.einsum("td,fd->tf", grad_all, w_down, preferred_element_type=jnp.float32)
    gate_grad = (activated_grad * upward * sigmoid * (1.0 + gate_value * (1.0 - sigmoid))).astype(
        jnp.bfloat16
    )
    upward_grad = (activated_grad * gate_value * sigmoid).astype(jnp.bfloat16)
    down_sum = jnp.einsum("tf,td->fd", activated, grad_all, preferred_element_type=jnp.float32)
    gate_sum = jnp.einsum("td,tf->df", hidden_two, gate_grad, preferred_element_type=jnp.float32)
    upward_sum = jnp.einsum(
        "td,tf->df", hidden_two, upward_grad, preferred_element_type=jnp.float32
    )
    hidden_two_grad = lax.psum_scatter(
        jnp.einsum("tf,df->td", gate_grad, w_gate, preferred_element_type=jnp.float32)
        + jnp.einsum("tf,df->td", upward_grad, w_up, preferred_element_type=jnp.float32),
        "mp",
        scatter_dimension=0,
        tiled=True,
    )
    norm_part_two, gain_two_grad = norm_back(hidden_two_grad, normed_two, inverse_two, norm2_gain)
    middle_grad = grad_rows.astype(jnp.float32) + norm_part_two
    branch_all = lax.all_gather(middle_grad.astype(jnp.bfloat16), "mp", axis=0, tiled=True)
    output_sum = jnp.einsum("tc,td->cd", mixed_flat, branch_all, preferred_element_type=jnp.float32)
    mixed_grad = jnp.einsum(
        "td,cd->tc", branch_all, w_out, preferred_element_type=jnp.float32
    ).astype(jnp.bfloat16)
    query_grad, key_grad, value_grad = attend_backward(
        query_heads,
        key_heads,
        value_heads,
        segment,
        key_mask,
        logsum,
        mixed_grad.reshape(group_rows, head_count, HEAD_DIM),
    )
    query_sum = jnp.einsum("td,tc->dc", hidden_one, query_grad, preferred_element_type=jnp.float32)
    key_sum = jnp.einsum("td,tc->dc", hidden_one, key_grad, preferred_element_type=jnp.float32)
    value_sum = jnp.einsum("td,tc->dc", hidden_one, value_grad, preferred_element_type=jnp.float32)
    hidden_one_grad = lax.psum_scatter(
        (
            jnp.einsum("tc,dc->td", query_grad, w_query, preferred_element_type=jnp.float32)
            + jnp.einsum("tc,dc->td", key_grad, w_key, preferred_element_type=jnp.float32)
            + jnp.einsum("tc,dc->td", value_grad, w_value, preferred_element_type=jnp.float32)
        ).astype(jnp.bfloat16),
        "mp",
        scatter_dimension=0,
        tiled=True,
    ).astype(jnp.float32)
    norm_part_one, gain_one_grad = norm_back(hidden_one_grad, normed_one, inverse_one, norm1_gain)
    input_grad = middle_grad + norm_part_one
    gain_one_sum, gain_two_sum = lax.psum((gain_one_grad, gain_two_grad), ("dp", "mp"))
    weight_sums = (
        lax.psum(query_sum.astype(jnp.bfloat16), "dp").astype(jnp.float32),
        lax.psum(key_sum.astype(jnp.bfloat16), "dp").astype(jnp.float32),
        lax.psum(value_sum.astype(jnp.bfloat16), "dp").astype(jnp.float32),
        lax.psum(output_sum.astype(jnp.bfloat16), "dp").astype(jnp.float32),
        lax.psum(gate_sum.astype(jnp.bfloat16), "dp").astype(jnp.float32),
        lax.psum(upward_sum.astype(jnp.bfloat16), "dp").astype(jnp.float32),
        lax.psum(down_sum.astype(jnp.bfloat16), "dp").astype(jnp.float32),
    )
    back_out, back_grad = (
        lax.all_to_all(
            out_rows.astype(jnp.bfloat16)[arrival_slot],
            "dp",
            split_axis=0,
            concat_axis=0,
            tiled=True,
        ),
        lax.all_to_all(
            input_grad.astype(jnp.bfloat16)[arrival_slot],
            "dp",
            split_axis=0,
            concat_axis=0,
            tiled=True,
        ),
    )
    return (
        back_out[send_at],
        back_grad[send_at],
        gain_one_sum,
        gain_two_sum,
        weight_sums[0],
        weight_sums[1],
        weight_sums[2],
        weight_sums[3],
        weight_sums[4],
        weight_sums[5],
        weight_sums[6],
    )


MESH = pl.DeviceIdType.MESH
LANES = 128
F32 = jnp.float32
BF16 = jnp.bfloat16
VMEM_LIMIT = 56 * 1024 * 1024


def plane():
    me = lax.axis_index("dp")
    side = me + 1 - 2 * lax.rem(me, 2)
    over_x = me + 2 - 4 * lax.rem(lax.div(me, 2), 2)
    over_y = me + 4 - 8 * lax.rem(lax.div(me, 4), 2)
    corner = over_x + 4 - 8 * lax.rem(lax.div(over_x, 4), 2)
    return (me, side, over_x, over_y, corner)


def to_dp(source, target, send_sem, recv_sem, index):
    return pltpu.make_async_remote_copy(
        src_ref=source,
        dst_ref=target,
        send_sem=send_sem,
        recv_sem=recv_sem,
        device_id={"dp": index},
        device_id_type=MESH,
    )


def to_mp(source, target, send_sem, recv_sem, index):
    return pltpu.make_async_remote_copy(
        src_ref=source,
        dst_ref=target,
        send_sem=send_sem,
        recv_sem=recv_sem,
        device_id={"mp": index},
        device_id_type=MESH,
    )


def greet_plane():
    _, side, over_x, over_y, _ = plane()
    barrier = pltpu.get_barrier_semaphore()
    for other in (side, over_x, over_y):
        pl.semaphore_signal(barrier, inc=1, device_id={"dp": other}, device_id_type=MESH)
    return barrier


def owner_at(turn):
    me, side, over_x, over_y, _ = plane()
    block = turn // 2
    near = ((block + 1) // 2) % 2
    far = block // 3
    second = turn % 2
    other = (1 - near) * second + (block // 2) * near
    owner = me + (near * (1 - second) + far) * (over_x - me)
    return owner + (near * second + far) * (over_y - me) + other * (side - me)


ARRIVALS = (
    (1, (4,)),
    (2, (0, 1, 2)),
    (3, (3,)),
    (4, (6, 9)),
    (5, (8, 10)),
    (6, (5, 7)),
    (7, (11, 12)),
)


class Gather:
    AFTER = {0: (5, 6), 1: (7, 8), 2: (9,), 3: (10,), 5: (11,), 7: (12,)}

    def __init__(self, own, out, send, recv, local=None):
        me, side, over_x, over_y, corner = plane()
        half = out.shape[1] // 2
        low, high = pl.ds(0, half), pl.ds(half, half)
        self.keep = None if own is None else pltpu.make_async_copy(own, out.at[me], local)
        own = out.at[me] if own is None else own

        def hop(number, source, target, index):
            return to_dp(source, target, send.at[number], recv.at[number], index)

        def onward(number, owner, part, index):
            place = out.at[owner, part]
            return hop(number, place, place, index)

        self.copies = [
            hop(0, own.at[low], out.at[me, low], over_x),
            hop(1, own.at[high], out.at[me, high], over_y),
            hop(2, own.at[high], out.at[me, high], over_x),
            hop(3, own.at[low], out.at[me, low], over_y),
            hop(4, own, out.at[me], side),
            onward(5, over_x, low, over_y),
            onward(6, over_x, low, side),
            onward(7, over_y, high, over_x),
            onward(8, over_y, high, side),
            onward(9, over_x, high, side),
            onward(10, over_y, low, side),
            onward(11, corner, low, side),
            onward(12, corner, high, side),
        ]

    def start(self):
        for number in range(5):
            self.copies[number].start()
        if self.keep is not None:
            self.keep.start()

    def arrive(self, *numbers):
        for number in numbers:
            self.copies[number].wait_recv()
            for later in self.AFTER.get(number, ()):
                self.copies[later].start()

    def pass_on(self):
        self.arrive(0, 1, 2, 3)

    def sent(self):
        for copy in self.copies:
            copy.wait_send()
        if self.keep is not None:
            self.keep.wait()

    def finish(self):
        self.arrive(5, 7, 4, 6, 8, 9, 10, 11, 12)
        self.sent()


def greet_all(barrier):
    me, z = lax.axis_index("dp"), lax.axis_index("mp")
    for step in range(1, 8):
        pl.semaphore_signal(
            barrier, inc=1, device_id={"dp": lax.rem(me + step, 8)}, device_id_type=MESH
        )
    core = lax.rem(me, 2)
    for step in range(1, 4):
        for other in (me, me + 1 - 2 * core):
            pl.semaphore_signal(
                barrier,
                inc=1,
                device_id={"dp": other, "mp": lax.rem(z + step, 4)},
                device_id_type=MESH,
            )
    pl.semaphore_wait(barrier, 13)


def swap_all(source, target, send, recv):
    me = lax.axis_index("dp")
    return [
        to_dp(source, target.at[me], send.at[step - 1], recv.at[step - 1], lax.rem(me + step, 8))
        for step in range(1, 8)
    ]


class Spread:
    def __init__(self, share, w_qkv, w_out, send, recv, local):
        me, z = lax.axis_index("dp"), lax.axis_index("mp")
        core = lax.rem(me, 2)
        self.place = z + core * (3 - 2 * z)
        self.send, self.recv, self.local = send, recv, local
        self.shares = [share.at[0], share.at[1], share.at[2], share.at[3]]
        self.slots = (core, 1 - core)
        self.core = core
        self.w_qkv, self.w_out = w_qkv, w_out

    def target(self, which, piece):
        slot = self.slots[which]
        block = slot if piece == 3 else 2 * piece + slot
        rows = pl.ds(pl.multiple_of(block * LANES, LANES), HEAD_DIM)
        return (self.w_out if piece == 3 else self.w_qkv).at[rows]

    def hop(self, which, piece, number, place, own):
        source = self.shares[piece] if own else self.target(which, piece)
        z = place + self.core * (3 - 2 * place)
        return to_mp(
            source,
            self.target(which, piece),
            self.send.at[number * 4 + piece],
            self.recv.at[which * 4 + piece],
            z,
        )

    def keep(self, which, piece):
        return pltpu.make_async_copy(
            self.shares[piece], self.target(which, piece), self.local.at[piece]
        )

    def start(self, pieces):
        @pl.when(self.place == 0)
        def _():
            for piece in pieces:
                self.hop(0, piece, 0, 1, True).start()
                self.keep(0, piece).start()

        @pl.when(self.place == 1)
        def _():
            for piece in pieces:
                self.hop(1, piece, 0, 0, True).start()
                self.hop(1, piece, 1, 2, True).start()
                self.keep(1, piece).start()

    def pass_on(self, pieces):
        @pl.when(self.place == 1)
        def _():
            for piece in pieces:
                self.hop(0, piece, 2, 2, False).wait_recv()
                self.hop(0, piece, 2, 2, False).start()

        @pl.when(self.place == 2)
        def _():
            for which in (1, 0):
                for piece in pieces:
                    self.hop(which, piece, which, 3, False).wait_recv()
                    self.hop(which, piece, which, 3, False).start()

    def finish(self, pieces):
        @pl.when(self.place == 0)
        def _():
            for piece in pieces:
                self.hop(1, piece, 0, 1, False).wait_recv()
                self.hop(0, piece, 0, 1, True).wait_send()
                self.keep(0, piece).wait()

        @pl.when(self.place == 1)
        def _():
            for piece in pieces:
                self.hop(1, piece, 0, 0, True).wait_send()
                self.hop(1, piece, 1, 2, True).wait_send()
                self.hop(0, piece, 2, 2, False).wait_send()
                self.keep(1, piece).wait()

        @pl.when(self.place == 2)
        def _():
            for piece in pieces:
                for which in (1, 0):
                    self.hop(which, piece, which, 3, False).wait_send()

        @pl.when(self.place == 3)
        def _():
            for piece in pieces:
                for which in (1, 0):
                    self.hop(which, piece, which, 3, False).wait_recv()


class Column:
    def __init__(self, own, out, send, recv, local):
        z = lax.axis_index("mp")
        self.z, self.own, self.out, self.send, self.recv = z, own, out, send, recv
        self.outer = (z == 0) | (z == 3)
        near = 1 + lax.div(z, 3)
        self.from_outer = (near, 3 - near)
        self.edge = 3 * (z - 1)
        self.from_inner = (3 - z, 3 - self.edge, self.edge)
        self.keep = pltpu.make_async_copy(own, out.at[z], local)

    def straight(self, number, target):
        return to_mp(
            self.own, self.out.at[self.z], self.send.at[number], self.recv.at[self.z], target
        )

    def onward(self):
        far = 3 - self.edge
        return to_mp(
            self.out.at[far], self.out.at[far], self.send.at[3], self.recv.at[far], self.edge
        )

    def came(self, source):
        return to_mp(
            self.own, self.out.at[source], self.send.at[0], self.recv.at[source], source
        ).wait_recv

    def start(self):
        self.keep.start()

        @pl.when(self.outer)
        def _():
            for number, target in enumerate(self.from_outer):
                self.straight(number, target).start()

        @pl.when(jnp.logical_not(self.outer))
        def _():
            for number, target in enumerate(self.from_inner):
                self.straight(number, target).start()

    def pass_on(self):
        @pl.when(jnp.logical_not(self.outer))
        def _():
            self.came(3 - self.edge)()
            self.onward().start()

    def finish(self):
        @pl.when(self.outer)
        def _():
            for source in (1, 2):
                self.came(source)()
            self.came(3 - self.z)()
            for number, target in enumerate(self.from_outer):
                self.straight(number, target).wait_send()

        @pl.when(jnp.logical_not(self.outer))
        def _():
            self.came(3 - self.z)()
            self.came(self.edge)()
            for number, target in enumerate(self.from_inner):
                self.straight(number, target).wait_send()
            self.onward().wait_send()

        self.keep.wait()


def anywhere():
    return pl.BlockSpec(memory_space=pl.ANY)


def on_chip():
    return pl.BlockSpec(memory_space=pltpu.VMEM)


def remote_params(number, limit=VMEM_LIMIT):
    return pltpu.CompilerParams(
        collective_id=number, has_side_effects=True, vmem_limit_bytes=limit
    )


def hot_of(notes, k, size):
    own = notes[:, 0:48, :].reshape(size, LANES)
    lane = lax.broadcasted_iota(jnp.int32, (size, LANES), 1)
    slot = jnp.sum(jnp.where(lane == k, own, 0.0), axis=1, keepdims=True)
    return (lax.broadcasted_iota(jnp.int32, (size, size), 1).astype(F32) == slot).astype(BF16)


def block_mask(notes, k, block, z, rows):
    position = rows * z + block * 128 + lax.broadcasted_iota(jnp.int32, (128, 1), 0)
    position = position.astype(F32)
    first_end = notes[k, 52:53, 0:1]
    second_end = first_end + notes[k, 52:53, 1:2]
    begin = jnp.where(position >= first_end, first_end, 0.0)
    begin = jnp.where(position >= second_end, second_end, begin)
    column = lax.broadcasted_iota(jnp.int32, (128, 192), 1)
    distance = 64 + lax.broadcasted_iota(jnp.int32, (128, 192), 0) - column
    key_position = (rows * z + block * 128 - 64 + column).astype(F32)
    live = jnp.concatenate(
        [notes[k, 48 + block : 49 + block, :], notes[k, 49 + block : 50 + block, 0:64]], axis=1
    )
    allowed = (distance >= 0) & (distance < WINDOW) & (key_position >= begin)
    return allowed & ((live == 1.0) | (distance == 0))


NT = (((1,), (1,)), ((), ()))
TN = (((0,), (0,)), ((), ()))


def forward_kernel(
    tokens, cotangent, order_row, gain, notes, query, keys, values, project, gate, upward,
    hidden_out, w_qkv, w_out, notes_all, w_both, mixed, kept, tokens_b, cotangent_b, cotangent_all,
    hidden_all, qkv, share, both_own,
    send, recv, send_a, recv_a, send_g, recv_g, send_w, recv_w, send_n, recv_n, send_c, recv_c,
    local, out_sem, *, scale,
):
    groups, rows, width = hidden_all.shape
    me, z = lax.axis_index("dp"), lax.axis_index("mp")
    members = lax.axis_size("mp")
    head = pl.ds(pl.multiple_of(lax.div(me, 2) * HEAD_DIM, 16), HEAD_DIM)
    units = pl.ds(pl.multiple_of(me * LANES, LANES), LANES)
    loads = [
        pltpu.make_async_copy(source.at[head], share.at[piece], local.at[piece])
        for piece, source in enumerate((query, keys, values, project))
    ]
    loads += [
        pltpu.make_async_copy(gate.at[:, units], both_own.at[:, pl.ds(0, LANES)], local.at[4]),
        pltpu.make_async_copy(upward.at[:, units], both_own.at[:, pl.ds(LANES, LANES)], local.at[5]),
    ]
    for copy in loads:
        copy.start()
    none = jnp.zeros((LANES - HEAD_DIM, width), BF16)
    for block in range(6):
        w_qkv[block * LANES + HEAD_DIM : block * LANES + LANES, :] = none
    for block in range(2):
        w_out[block * LANES + HEAD_DIM : block * LANES + LANES, :] = none

    place = lax.broadcasted_iota(jnp.int32, (rows, rows), 0).astype(F32)
    sort = (place == order_row[...]).astype(BF16)
    tokens_b[...] = jnp.dot(sort, tokens[...], preferred_element_type=F32).astype(BF16)

    def normalise(span):
        value = tokens_b[span, :].astype(F32)
        inverse = lax.rsqrt(mean_rows(value * value) + EPSILON)
        hidden_all[me, span, :] = (value * inverse * gain[...]).astype(BF16)

    each_chunk(rows, normalise)
    notes_all[me] = notes[...]
    greet_all(pltpu.get_barrier_semaphore())
    gather = Gather(None, hidden_all, send_a, recv_a)
    gather.start()
    swaps = swap_all(notes, notes_all, send_n, recv_n)
    for copy in swaps:
        copy.start()
    for copy in loads[:4]:
        copy.wait()
    spread = Spread(share, w_qkv, w_out, send_w, recv_w, local)
    spread.start((0, 1, 2))
    cotangent_b[...] = jnp.dot(sort, cotangent[...], preferred_element_type=F32).astype(BF16)
    for copy in loads[4:]:
        copy.wait()
    column = Column(both_own, w_both, send_c, recv_c, local.at[4])
    second = Gather(cotangent_b, cotangent_all, send_g, recv_g, local.at[5])
    gather.arrive(0, 1)
    second.start()
    spread.pass_on((0, 1, 2))
    column.start()
    gather.arrive(2, 3)
    spread.finish((0, 1, 2))
    spread.start((3,))
    for copy in swaps:
        copy.wait()

    def keep(turn):
        owner = owner_at(turn)
        return pltpu.make_async_copy(hidden_all.at[owner], hidden_out.at[owner], out_sem.at[turn])

    def multiply(turn, carry):
        for number, numbers in ARRIVALS:
            left = tuple(n for n in numbers if n > 3)
            if left:
                pl.when(turn == number)(functools.partial(gather.arrive, *left))
        owner = owner_at(turn)
        keep(turn).start()
        product = lax.dot_general(
            hidden_all[owner], w_qkv[...], NT, preferred_element_type=F32
        ).astype(BF16)
        qkv[owner] = product.reshape(groups, rows // groups, 768)
        return carry

    lax.fori_loop(0, groups, multiply, 0)

    def halo(k, other):
        return to_mp(
            kept.at[k, pl.ds(rows, 64), pl.ds(256, 512)],
            kept.at[k, pl.ds(0, 64), pl.ds(256, 512)],
            send.at[k],
            recv.at[k],
            other,
        )

    def order(k, carry):
        hot = hot_of(notes_all, k, rows)
        given = qkv[:, pl.ds(k, 1)].reshape(rows, 768)
        kept[k, pl.ds(64, rows), :] = lax.dot_general(
            hot, given, TN, preferred_element_type=F32
        ).astype(BF16)
        kept[k, pl.ds(0, 64), pl.ds(0, 256)] = jnp.zeros((64, 256), BF16)

        @pl.when(z < members - 1)
        def _():
            halo(k, z + 1).start()

        @pl.when(z == 0)
        def _():
            kept[k, pl.ds(0, 64), pl.ds(256, 512)] = jnp.zeros((64, 512), BF16)

        return carry

    lax.fori_loop(0, groups, order, 0)

    def attend(k, carry):
        @pl.when(z > 0)
        def _():
            halo(k, z).wait_recv()

        hot = hot_of(notes_all, k, rows)
        found = []
        for block in range(rows // 128):
            allowed = block_mask(notes_all, k, block, z, rows)
            heads = []
            for head in range(2):
                query = kept[k, pl.ds(64 + block * 128, 128), pl.ds(head * 128, 128)]
                keys = kept[k, pl.ds(block * 128, 192), pl.ds(256 + head * 128, 128)]
                values = kept[k, pl.ds(block * 128, 192), pl.ds(512 + head * 128, 128)]
                scores = lax.dot_general(query, keys, NT, preferred_element_type=F32) * scale
                scores = jnp.where(allowed, scores, -MASKED)
                weights = jnp.exp(scores - jnp.max(scores, axis=-1, keepdims=True))
                total = jnp.sum(weights, axis=-1, keepdims=True)
                chances = (weights / total).astype(BF16)
                heads.append(jnp.dot(chances, values, preferred_element_type=F32).astype(BF16))
            found.append(jnp.concatenate(heads, axis=1))
        ordered = jnp.concatenate(found, axis=0)
        back = jnp.dot(hot, ordered, preferred_element_type=F32).astype(BF16)
        mixed[:, pl.ds(k, 1)] = back.reshape(groups, 1, rows // groups, 256)
        return carry

    spread.pass_on((3,))
    lax.fori_loop(0, groups // 2, attend, 0)
    second.pass_on()
    column.pass_on()
    lax.fori_loop(groups // 2, groups, attend, 0)
    spread.finish((3,))
    second.finish()
    column.finish()
    gather.sent()

    def kept_out(turn, carry):
        keep(turn).wait()
        return carry

    lax.fori_loop(0, groups, kept_out, 0)

    @pl.when(z < members - 1)
    def _():
        def done(k, carry):
            halo(k, z + 1).wait_send()
            return carry

        lax.fori_loop(0, groups, done, 0)


def attend_ahead(
    tokens, cotangent, order_row, gain, notes, query, keys, values, project, gate, upward, scale
):
    rows, width = tokens.shape
    groups, members = lax.axis_size("dp"), lax.axis_size("mp")
    dma = pltpu.SemaphoreType.DMA
    shape = jax.ShapeDtypeStruct
    return pl.pallas_call(
        functools.partial(forward_kernel, scale=scale),
        out_shape=(
            shape((groups, rows, width), BF16),
            shape((6 * LANES, width), BF16),
            shape((2 * LANES, width), BF16),
            shape((groups,) + notes.shape, F32),
            shape((members, width, 2 * LANES), BF16),
            shape((groups, groups, rows // groups, 256), BF16),
            shape((groups, rows + 64, 768), BF16),
            shape((rows, width), BF16),
            shape((rows, width), BF16),
            shape((groups, rows, width), BF16),
        ),
        in_specs=[on_chip()] * 5 + [anywhere()] * 6,
        out_specs=(anywhere(),)
        + (on_chip(),) * 3
        + (anywhere(),)
        + (on_chip(),) * 4
        + (anywhere(),),
        scratch_shapes=[
            pltpu.VMEM((groups, rows, width), BF16),
            pltpu.VMEM((groups, groups, rows // groups, 768), BF16),
            pltpu.VMEM((4, HEAD_DIM, width), BF16),
            pltpu.VMEM((width, 2 * LANES), BF16),
            dma((groups,)),
            dma((groups,)),
            dma((13,)),
            dma((13,)),
            dma((13,)),
            dma((13,)),
            dma((12,)),
            dma((8,)),
            dma((7,)),
            dma((7,)),
            dma((4,)),
            dma((4,)),
            dma((6,)),
            dma((groups,)),
        ],
        compiler_params=remote_params(2, 60 * 1024 * 1024),
        cost_estimate=pl.CostEstimate(flops=0, bytes_accessed=300_000_000, transcendentals=0),
        name="attend_ahead",
    )(tokens, cotangent, order_row, gain, notes, query, keys, values, project, gate, upward)


CHUNK = 32


def each_chunk(rows, body, chunk=CHUNK):
    def step(i, carry):
        body(pl.ds(pl.multiple_of(i * chunk, chunk), chunk))
        return carry

    lax.fori_loop(0, rows // chunk, step, 0)


class Reduce:
    COUNT = 10

    def __init__(self, left, right, across, part, from_side, from_corner, from_near, send, recv):
        self.left, self.right, self.across, self.part = left, right, across, part
        self.from_side, self.from_corner, self.from_near = from_side, from_corner, from_near
        self.send, self.recv = send, recv
        self.rows = part.shape[1]

    def product(self, owner, slot):
        rows, width = self.rows, self.part.shape[2]
        picked = pl.ds(pl.multiple_of(owner * rows, rows), rows)

        def tile(t, carry):
            columns = pl.ds(pl.multiple_of(t * 256, 256), 256)
            if self.across:
                value = lax.dot_general(
                    self.left[picked, :], self.right[columns, :], NT, preferred_element_type=F32
                )
            else:
                value = jnp.dot(
                    self.left[picked, :], self.right[:, columns], preferred_element_type=F32
                )
            self.part[slot, :, columns] = value.astype(BF16)
            return carry

        lax.fori_loop(0, width // 256, tile, 0)

    def prepare(self):
        _, side, over_x, over_y, corner = plane()
        part, near = self.part, self.from_near
        half = self.rows // 2
        low, high = pl.ds(0, half), pl.ds(half, half)

        def hop(number, source, target, index):
            return to_dp(source, target, self.send.at[number], self.recv.at[number], index)

        self.shares = [hop(i, part.at[4 + i], self.from_side.at[i], side) for i in range(4)]
        self.corners = [
            hop(4, part.at[0, low], self.from_corner.at[0], over_x),
            hop(5, part.at[0, high], self.from_corner.at[1], over_y),
        ]
        self.nears = [
            hop(6, part.at[1, low], near.at[0, low], over_x),
            hop(7, part.at[1, high], near.at[0, high], over_x),
            hop(8, part.at[2, high], near.at[1, high], over_y),
            hop(9, part.at[2, low], near.at[1, low], over_y),
        ]

    def add_side(self, slot):
        self.shares[slot].wait_recv()

        def body(span):
            self.part[slot, span, :] = (
                self.part[slot, span, :].astype(F32) + self.from_side[slot, span, :].astype(F32)
            ).astype(BF16)

        each_chunk(self.rows, body)

    def add_corner(self, slot, offset, which):
        self.corners[which].wait_recv()

        def body(span):
            target = pl.ds(pl.multiple_of(offset + span.start, CHUNK), CHUNK)
            self.part[slot, target, :] = (
                self.part[slot, target, :].astype(F32)
                + self.from_corner[which, span, :].astype(F32)
            ).astype(BF16)

        each_chunk(self.rows // 2, body)

    def products(self):
        self.prepare()
        me, _, over_x, over_y, corner = plane()
        turn = 1 - 2 * lax.rem(me, 2)
        for slot, owner in enumerate((corner, over_x, over_y, me)):
            self.product(owner + turn, 4 + slot)
            self.shares[slot].start()
        for slot, owner in enumerate((corner, over_x, over_y, me)):
            self.product(owner, slot)

    def launch(self):
        self.add_side(0)
        self.corners[0].start()
        self.corners[1].start()
        self.add_side(1)
        self.nears[0].start()
        self.add_side(2)
        self.nears[2].start()

    def begin(self):
        self.prepare()
        me, _, over_x, over_y, corner = plane()
        turn = 1 - 2 * lax.rem(me, 2)
        self.product(corner + turn, 4)
        self.shares[0].start()
        self.product(corner, 0)
        self.product(over_x + turn, 5)
        self.shares[1].start()
        self.add_side(0)
        self.corners[0].start()
        self.corners[1].start()
        self.product(over_x, 1)
        self.product(over_y + turn, 6)
        self.shares[2].start()
        self.add_side(1)
        self.nears[0].start()
        self.product(over_y, 2)
        self.product(me + turn, 7)
        self.shares[3].start()
        self.add_side(2)
        self.nears[2].start()
        self.product(me, 3)

    def middle(self):
        self.add_corner(2, 0, 0)
        self.nears[3].start()
        self.add_corner(1, self.rows // 2, 1)
        self.nears[1].start()

    def end(self):
        self.shares[3].wait_recv()
        for copy in self.nears:
            copy.wait_recv()

    def run(self):
        self.begin()
        self.middle()
        self.end()

    def rows_of(self, span):
        return (
            self.part[3, span, :].astype(F32)
            + self.from_side[3, span, :].astype(F32)
            + self.from_near[0, span, :].astype(F32)
            + self.from_near[1, span, :].astype(F32)
        )

    def finish(self):
        for copy in self.shares + self.corners + self.nears:
            copy.wait_send()


def reduce_scratch(rows, width):
    dma = pltpu.SemaphoreType.DMA
    return [
        pltpu.VMEM((8, rows, width), BF16),
        pltpu.VMEM((4, rows, width), BF16),
        pltpu.VMEM((2, rows // 2, width), BF16),
        pltpu.VMEM((2, rows, width), BF16),
        dma((10,)),
        dma((10,)),
    ]


def gather_scratch(rows, width):
    dma = pltpu.SemaphoreType.DMA
    return [pltpu.VMEM((rows, width), BF16), dma((13,)), dma((13,)), dma(())]


def mean_rows(values):
    return jnp.mean(values, axis=-1, keepdims=True)


class Heads:
    def __init__(self, source, stage, arrive, send, recv_stage, recv):
        me, z = lax.axis_index("dp"), lax.axis_index("mp")
        self.me, self.z = me, z
        self.core = lax.rem(me, 2)
        self.source, self.stage, self.arrive = source, stage, arrive
        self.send, self.recv_stage, self.recv = send, recv_stage, recv
        self.place = z + self.core * (3 - 2 * z)
        self.columns = source.shape[1] // 2

    def z_of(self, place):
        return place + self.core * (3 - 2 * place)

    def slot_of(self, place):
        return self.core if place == 0 else 1 - self.core

    def rows_of(self, place, kind):
        block = 2 * kind + self.slot_of(place)
        return self.source.at[pl.ds(pl.multiple_of(block * LANES, LANES), HEAD_DIM)]

    def half_of(self, ref, half):
        return ref.at[:, pl.ds(pl.multiple_of(half * self.columns, LANES), self.columns)]

    def to_stage(self, place, kind):
        return to_at(
            self.rows_of(place, kind),
            self.stage.at[place, kind],
            self.send.at[place * 4 + kind],
            self.recv_stage.at[place * 4 + kind],
            self.me,
            self.z_of(2),
        )

    def to_owner(self, place, kind, half, way, ref, number):
        return to_at(
            self.half_of(ref, half),
            self.arrive.at[way, kind],
            self.send.at[number],
            self.recv.at[way * 4 + kind],
            self.me - self.core + half,
            self.z_of(place),
        )

    def sums(self, kind):
        return [
            self.to_owner(
                place, kind, half, 2, self.stage.at[place, kind], place * 8 + kind * 2 + half
            )
            for place in (0, 1)
            for half in (0, 1)
        ]

    def cross(self, own, kind):
        other = 1 - own
        copies = [
            self.to_owner(other, kind, half, 0, self.rows_of(other, kind), kind * 2 + half)
            for half in (0, 1)
        ]
        copies.append(
            to_at(
                self.half_of(self.rows_of(own, kind), 1 - self.core),
                self.arrive.at[1, kind],
                self.send.at[8 + kind],
                self.recv.at[4 + kind],
                self.me + 1 - 2 * self.core,
                self.z,
            )
        )
        return copies

    def start(self, kinds):
        @pl.when(self.place == 3)
        def _():
            for kind in kinds:
                self.to_stage(0, kind).start()
                self.to_stage(1, kind).start()

        for own in (0, 1):
            @pl.when(self.place == own)
            def _():
                for kind in kinds:
                    for copy in self.cross(own, kind):
                        copy.start()

    def add(self, kinds):
        @pl.when(self.place == 2)
        def _():
            for kind in kinds:
                for place in (0, 1):
                    self.to_stage(place, kind).wait_recv()
                    mine = self.rows_of(place, kind)

                    def body(span):
                        self.stage[place, kind, span, :] = (
                            self.stage[place, kind, span, :].astype(F32)
                            + mine[span, :].astype(F32)
                        ).astype(BF16)

                    each_chunk(HEAD_DIM, body, 16)
                for copy in self.sums(kind):
                    copy.start()

    def total(self, out):
        owner = lax.div(self.z, 2) == self.core
        for kind in range(4):
            for own in (0, 1):
                @pl.when(self.place == own)
                def _():
                    self.arrive[1, kind] = self.half_of(self.rows_of(own, kind), self.core)[...]

            for way in range(3):
                waiting = to_at(
                    self.half_of(self.rows_of(0, kind), 0),
                    self.arrive.at[way, kind],
                    self.send.at[0],
                    self.recv.at[way * 4 + kind],
                    self.me,
                    lax.rem(self.z + 1, 4),
                )
                if way == 1:
                    pl.when(jnp.logical_not(owner))(waiting.wait_recv)
                else:
                    waiting.wait_recv()

            def body(span):
                found = self.arrive[0, kind, span, :].astype(F32)
                found = found + self.arrive[1, kind, span, :].astype(F32)
                found = found + self.arrive[2, kind, span, :].astype(F32)
                target = pl.ds(pl.multiple_of(kind * HEAD_DIM + span.start, 16), 16)
                out[target, :] = found.astype(BF16)

            each_chunk(HEAD_DIM, body, 16)

    def finish_send(self):
        for kind in range(4):
            @pl.when(self.place == 3)
            def _():
                self.to_stage(0, kind).wait_send()
                self.to_stage(1, kind).wait_send()

            @pl.when(self.place == 2)
            def _():
                for copy in self.sums(kind):
                    copy.wait_send()

            for own in (0, 1):
                @pl.when(self.place == own)
                def _():
                    for copy in self.cross(own, kind):
                        copy.wait_send()


def to_at(source, target, send_sem, recv_sem, dp, mp):
    return pltpu.make_async_remote_copy(
        src_ref=source,
        dst_ref=target,
        send_sem=send_sem,
        recv_sem=recv_sem,
        device_id={"dp": dp, "mp": mp},
        device_id_type=MESH,
    )


class Units:
    def __init__(self, both_sum, both_in, both_stage, send, recv, local):
        self.z = lax.axis_index("mp")
        self.sums = (both_sum,)
        self.inputs = (both_in,)
        self.stages = (both_stage,)
        self.send, self.recv, self.local = send, recv, local
        z = self.z
        self.outer = (z == 0) | (z == 3)
        self.far = 3 - z
        self.near = 1 + lax.div(z, 3)
        self.second = 3 - self.near
        self.edge = 3 * (z - 1)

    def part(self, kind, z):
        return self.sums[kind].at[z]

    def straight(self, kind, number, target):
        return to_mp(
            self.part(kind, target),
            self.inputs[kind].at[self.z],
            self.send.at[number * 2 + kind],
            self.recv.at[self.z * 2 + kind],
            target,
        )

    def staged(self, kind):
        return to_mp(
            self.part(kind, self.far),
            self.stages[kind].at[0],
            self.send.at[4 + kind],
            self.recv.at[8 + kind],
            self.near,
        )

    def summed(self, kind):
        return to_mp(
            self.stages[kind].at[1],
            self.inputs[kind].at[self.z],
            self.send.at[4 + kind],
            self.recv.at[self.z * 2 + kind],
            3 - self.edge,
        )

    def mine(self, kind):
        return pltpu.make_async_copy(
            self.part(kind, 3 - self.edge), self.stages[kind].at[1], self.local.at[kind]
        )

    def start(self):
        @pl.when(self.outer)
        def _():
            for kind in range(1):
                self.staged(kind).start()
            for kind in range(1):
                self.straight(kind, 0, self.near).start()
                self.straight(kind, 1, self.second).start()

        @pl.when(jnp.logical_not(self.outer))
        def _():
            for kind in range(1):
                self.mine(kind).start()
                self.straight(kind, 0, 3 - self.z).start()
                self.straight(kind, 1, self.edge).start()

    def add(self):
        @pl.when(jnp.logical_not(self.outer))
        def _():
            for kind in range(1):
                stage = self.stages[kind]
                self.mine(kind).wait()
                to_mp(
                    self.part(kind, 0),
                    stage.at[0],
                    self.send.at[4 + kind],
                    self.recv.at[8 + kind],
                    self.edge,
                ).wait_recv()

                def body(span):
                    stage[1, span, :] = (
                        stage[0, span, :].astype(F32) + stage[1, span, :].astype(F32)
                    ).astype(BF16)

                each_chunk(stage.shape[1], body)
                self.summed(kind).start()

    def arrived(self, kind, source):
        to_mp(
            self.part(kind, 0),
            self.inputs[kind].at[source],
            self.send.at[kind],
            self.recv.at[source * 2 + kind],
            source,
        ).wait_recv()

    def finish(self):
        @pl.when(self.outer)
        def _():
            for kind in range(1):
                self.arrived(kind, 1)
                self.arrived(kind, 2)
                self.straight(kind, 0, self.near).wait_send()
                self.straight(kind, 1, self.second).wait_send()
                self.staged(kind).wait_send()

        @pl.when(jnp.logical_not(self.outer))
        def _():
            for kind in range(1):
                self.arrived(kind, 0)
                self.arrived(kind, 3)
                self.arrived(kind, 3 - self.z)
                self.straight(kind, 0, 3 - self.z).wait_send()
                self.straight(kind, 1, self.edge).wait_send()
                self.summed(kind).wait_send()


def backward_kernel(
    kept, branch, w_out, notes_all, activated, w_down, middle, both_sum, down_in,
    out, result, branch_all, both_in, down_all,
    totals, query_part, key_value, ending, leaving, arriving, send, recv,
    part, from_side, from_corner, from_near, send_r, recv_r,
    mixed_grad, shard, load_sem, send_g, recv_g,
    both_stage, send_u, recv_u, local, down_found, send_d, recv_d,
    *, scale, groups, rows,
):
    z = lax.axis_index("mp")
    members = lax.axis_size("mp")
    load_down = pltpu.make_async_copy(down_in, down_found, load_sem.at[2])
    load_down.start()
    greet_all(pltpu.get_barrier_semaphore())
    units = Units(both_sum, both_in, both_stage, send_u, recv_u, local)
    gather = Gather(branch, branch_all, send_g, recv_g, local.at[2])
    gather.start()
    units.start()
    reduce = Reduce(activated, w_down, False, part, from_side, from_corner, from_near, send_r, recv_r)
    reduce.products()
    load_down.wait()

    def add_down(span):
        value = down_found[0, span, :].astype(F32) + down_found[1, span, :].astype(F32)
        value = value + down_found[2, span, :].astype(F32) + down_found[3, span, :].astype(F32)
        down_found[0, span, :] = value.astype(BF16)

    each_chunk(down_found.shape[1], add_down)
    down = Gather(down_found.at[0], down_all, send_d, recv_d, local.at[1])

    def load_shard(turn):
        slot = turn % 2
        return pltpu.make_async_copy(branch_all.at[owner_at(turn)], shard.at[slot], load_sem.at[slot])

    def spread_back(turn, carry):
        for number, numbers in ARRIVALS:
            pl.when(turn == number)(functools.partial(gather.arrive, *numbers))

        @pl.when(turn == 0)
        def _():
            gather.keep.wait()

        load_shard(turn).start()
        load_shard(turn).wait()
        mixed_grad[owner_at(turn)] = (
            lax.dot_general(shard[turn % 2], w_out[...], NT, preferred_element_type=F32)
            .astype(BF16)
            .reshape(groups, rows // groups, 256)
        )
        return carry

    lax.fori_loop(0, 8, spread_back, 0)
    reduce.launch()
    down.start()
    units.add()


    def halo(k, other):
        return to_mp(leaving.at[k], arriving.at[k], send.at[k], recv.at[k], other)

    def attend(k, carry):
        hot = hot_of(notes_all, k, rows)
        given = mixed_grad[:, pl.ds(k, 1)].reshape(rows, 256)
        grad_ordered = lax.dot_general(hot, given, TN, preferred_element_type=F32).astype(BF16)
        totals[...] = jnp.zeros_like(totals)
        for block in range(rows // 128):
            allowed = block_mask(notes_all, k, block, z, rows)
            for head in range(2):
                query = kept[k, pl.ds(64 + block * 128, 128), pl.ds(head * 128, 128)]
                keys = kept[k, pl.ds(block * 128, 192), pl.ds(256 + head * 128, 128)]
                values = kept[k, pl.ds(block * 128, 192), pl.ds(512 + head * 128, 128)]
                grad = grad_ordered[block * 128 : block * 128 + 128, head * 128 : head * 128 + 128]
                scores = lax.dot_general(query, keys, NT, preferred_element_type=F32) * scale
                scores = jnp.where(allowed, scores, -MASKED)
                weights = jnp.exp(scores - jnp.max(scores, axis=-1, keepdims=True))
                again = weights / jnp.sum(weights, axis=-1, keepdims=True)
                chance_grad = lax.dot_general(grad, values, NT, preferred_element_type=F32)
                row_dot = jnp.sum(again * chance_grad, axis=-1, keepdims=True)
                score_grad = (again * (chance_grad - row_dot)).astype(BF16)
                query_part[k, pl.ds(block * 128, 128), pl.ds(head * 128, 128)] = (
                    jnp.dot(score_grad, keys, preferred_element_type=F32) * scale
                ).astype(BF16)
                totals[pl.ds(block * 128, 192), pl.ds(head * 128, 128)] += (
                    lax.dot_general(score_grad, query, TN, preferred_element_type=F32) * scale
                )
                totals[pl.ds(block * 128, 192), pl.ds(256 + head * 128, 128)] += lax.dot_general(
                    again.astype(BF16), grad, TN, preferred_element_type=F32
                )
        key_value[k] = totals[pl.ds(64, rows), :].astype(BF16)
        ending[k] = totals[pl.ds(rows, 64), :]

        @pl.when(z > 0)
        def _():
            leaving[k] = totals[pl.ds(0, 64), :].astype(BF16)
            halo(k, z - 1).start()

        return carry

    lax.fori_loop(0, 3, attend, 0)
    reduce.middle()
    lax.fori_loop(3, 7, attend, 0)
    down.pass_on()
    lax.fori_loop(7, groups, attend, 0)

    def restore(k, carry):
        @pl.when(z < members - 1)
        def _():
            halo(k, z).wait_recv()
            key_value[k, pl.ds(rows - 64, 64), :] = (
                ending[k] + arriving[k].astype(F32)
            ).astype(BF16)

        hot = hot_of(notes_all, k, rows)
        ordered = jnp.concatenate([query_part[k], key_value[k]], axis=1)
        back = jnp.dot(hot, ordered, preferred_element_type=F32).astype(BF16)
        out[:, pl.ds(k, 1)] = back.reshape(groups, 1, rows // groups, 768)
        return carry

    lax.fori_loop(0, groups, restore, 0)
    reduce.end()

    def body(span):
        result[span, :] = (middle[span, :] + reduce.rows_of(span)).astype(BF16)

    each_chunk(rows, body)
    down.finish()
    units.finish()
    for copy in gather.copies:
        copy.wait_send()
    reduce.finish()

    @pl.when(z > 0)
    def _():
        def done(k, carry):
            halo(k, z - 1).wait_send()
            return carry

        lax.fori_loop(0, groups, done, 0)


def attend_back(
    kept, branch, w_out, notes_all, activated, w_down, middle, both_sum, down_in, scale
):
    groups = kept.shape[0]
    rows, width = middle.shape
    members = both_sum.shape[0]
    dma = pltpu.SemaphoreType.DMA
    shape = jax.ShapeDtypeStruct
    return pl.pallas_call(
        functools.partial(backward_kernel, scale=scale, groups=groups, rows=rows),
        out_shape=(
            shape((groups, groups, rows // groups, 768), BF16),
            shape((rows, width), BF16),
            shape((groups, rows, width), BF16),
            shape((members, width, 256), BF16),
            shape((groups, LANES, width), BF16),
        ),
        in_specs=[on_chip()] * 7 + [anywhere()] * 2,
        out_specs=(on_chip(),) * 2 + (anywhere(),) * 3,
        scratch_shapes=[
            pltpu.VMEM((rows + 64, 512), F32),
            pltpu.VMEM((groups, rows, 256), BF16),
            pltpu.VMEM((groups, rows, 512), BF16),
            pltpu.VMEM((groups, 64, 512), F32),
            pltpu.VMEM((groups, 64, 512), BF16),
            pltpu.VMEM((groups, 64, 512), BF16),
            dma((groups,)),
            dma((groups,)),
        ]
        + reduce_scratch(rows, width)
        + [
            pltpu.VMEM((groups, groups, rows // groups, 256), BF16),
            pltpu.VMEM((2, rows, width), BF16),
            dma((3,)),
            dma((13,)),
            dma((13,)),
            pltpu.VMEM((2, width, 256), BF16),
            dma((6,)),
            dma((10,)),
            dma((3,)),
            pltpu.VMEM((members, LANES, width), BF16),
            dma((13,)),
            dma((13,)),
        ],
        compiler_params=remote_params(3, 63 * 1024 * 1024),
        cost_estimate=pl.CostEstimate(flops=0, bytes_accessed=300_000_000, transcendentals=0),
        name="attend_back",
    )(kept, branch, w_out, notes_all, activated, w_down, middle, both_sum, down_in)


def middle_kernel(
    mixed, w_out, tokens, gain, w_down, middle, hidden, down_all,
    part, from_side, from_corner, from_near, send, recv, down_own, send_c, recv_c, local,
):
    units = pl.ds(pl.multiple_of(lax.axis_index("dp") * LANES, LANES), LANES)
    load = pltpu.make_async_copy(w_down.at[units], down_own, local.at[0])
    load.start()
    greet_all(pltpu.get_barrier_semaphore())
    load.wait()
    column = Column(down_own, down_all, send_c, recv_c, local.at[1])
    column.start()
    reduce = Reduce(mixed, w_out, False, part, from_side, from_corner, from_near, send, recv)
    reduce.begin()
    reduce.middle()
    column.pass_on()
    reduce.end()

    def body(span):
        values = tokens[span, :].astype(F32) + reduce.rows_of(span)
        middle[span, :] = values
        inverse = lax.rsqrt(mean_rows(values * values) + EPSILON)
        hidden[span, :] = (values * inverse * gain[...]).astype(BF16)

    each_chunk(hidden.shape[0], body)
    column.finish()
    reduce.finish()


def project_middle(mixed, w_out, tokens, gain, w_down):
    rows, width = tokens.shape
    dma = pltpu.SemaphoreType.DMA
    members = lax.axis_size("mp")
    return pl.pallas_call(
        middle_kernel,
        out_shape=(
            jax.ShapeDtypeStruct((rows, width), F32),
            jax.ShapeDtypeStruct((rows, width), BF16),
            jax.ShapeDtypeStruct((members, LANES, width), BF16),
        ),
        in_specs=[on_chip()] * 4 + [anywhere()],
        out_specs=(on_chip(), on_chip(), anywhere()),
        scratch_shapes=reduce_scratch(rows, width)
        + [pltpu.VMEM((LANES, width), BF16), dma((4,)), dma((4,)), dma((2,))],
        compiler_params=remote_params(4),
        cost_estimate=pl.CostEstimate(flops=0, bytes_accessed=150_000_000, transcendentals=0),
        name="project_middle",
    )(mixed, w_out, tokens, gain, w_down)


def norm_back_rows(gradient, values, gain, sums, span):
    inverse = lax.rsqrt(mean_rows(values * values) + EPSILON)
    normed = values * inverse
    product = gradient * normed
    folded = product[0:8]
    for step in range(1, CHUNK // 8):
        folded = folded + product[step * 8 : step * 8 + 8]
    sums[...] += folded
    scaled = gradient * gain
    return inverse * (scaled - normed * mean_rows(scaled * normed))


def feed_kernel(
    hidden_own, cotangent_all, middle, w_parts, cotangent, gain, w_down,
    middle_grad, branch, sums, activated, both_sum, down_in,
    hidden_all, both_grad, part, from_side, from_corner, from_near, send_r, recv_r,
    send_a, recv_a, cot_shard, cot_tile, stage_both, down_sum, w_both, load_sem, local, send_z, recv_z,
):
    groups, rows, width = hidden_all.shape
    members = w_parts.shape[0]
    me = lax.axis_index("dp")
    own = pltpu.make_async_copy(hidden_own, hidden_all.at[me], local.at[0])
    own.start()
    start_middle = pltpu.make_async_copy(middle, middle_grad, local.at[1])
    loads = [
        pltpu.make_async_copy(w_parts.at[z], w_both.at[:, pl.ds(z * 256, 256)], load_sem.at[6 + z])
        for z in range(members)
    ]

    def slot_of(turn):
        block = turn // 2
        near = ((block + 1) // 2) % 2
        far = block // 3
        second = turn % 2
        other = (1 - near) * second + (block // 2) * near
        return 4 * other + 3 * (1 - near) * (1 - far) + near * (1 + second)

    def load_cotangent(turn):
        return pltpu.make_async_copy(
            cotangent_all.at[owner_at(turn)], cot_shard.at[turn % 2], load_sem.at[turn % 2]
        )

    for copy in loads:
        copy.start()
    load_cotangent(0).start()
    greet_all(pltpu.get_barrier_semaphore())
    own.wait()
    gather = Gather(None, hidden_all, send_a, recv_a)
    gather.start()
    reduce = Reduce(None, None, False, part, from_side, from_corner, from_near, send_r, recv_r)
    reduce.prepare()

    def nears():
        reduce.add_side(1)
        reduce.nears[0].start()
        reduce.add_side(2)
        reduce.nears[2].start()

    early = [(turn, functools.partial(gather.arrive, *numbers)) for turn, numbers in ARRIVALS]
    early += [(6, nears)]
    late = [(1, 3), (4, 1), (5, 2), (7, 0)]
    start_middle.start()
    for copy in loads:
        copy.wait()

    def unit(turn, carry):
        for number, action in early:
            pl.when(turn == number)(action)

        @pl.when(turn < 7)
        def _():
            load_cotangent(turn + 1).start()

        load_cotangent(turn).wait()
        owner, slot = owner_at(turn), slot_of(turn)
        mine = hidden_all[owner]
        grads = cot_shard[turn % 2]
        for z in range(members):
            raw = jnp.dot(mine, w_both[:, z * 256 : z * 256 + 256], preferred_element_type=F32)
            units = pl.ds(z * 128, 128)
            if z % 2 == 0:
                pair = lax.dot_general(
                    grads, w_down[pl.ds(z * 128, 256), :], NT, preferred_element_type=F32
                )
            active_grad = pair[:, 128 * (z % 2) : 128 * (z % 2) + 128]
            gate, upward = raw[:, :128], raw[:, 128:]
            sigmoid = jax.nn.sigmoid(gate)
            activated[owner, :, units] = (gate * sigmoid * upward).astype(BF16)
            both_grad[owner, :, pl.ds(z * 256, 128)] = (
                active_grad * upward * sigmoid * (1.0 + gate * (1.0 - sigmoid))
            ).astype(BF16)
            both_grad[owner, :, pl.ds(z * 256 + 128, 128)] = (
                active_grad * gate * sigmoid
            ).astype(BF16)

        def tile(t, inner):
            columns = pl.ds(pl.multiple_of(t * 256, 256), 256)
            part[slot, :, columns] = lax.dot_general(
                both_grad[owner], w_both[columns, :], NT, preferred_element_type=F32
            ).astype(BF16)
            return inner

        lax.fori_loop(0, width // 256, tile, 0)
        for number, share in late:
            pl.when(turn == number)(reduce.shares[share].start)
        return carry

    lax.fori_loop(0, 8, unit, 0)

    def load_tile(t):
        columns = pl.ds(pl.multiple_of(t * 256, 256), 256)
        return pltpu.make_async_copy(
            cotangent_all.at[:, :, columns], cot_tile.at[t % 2], load_sem.at[2 + t % 2]
        )

    def store_both(t):
        columns = pl.ds(pl.multiple_of(t * 256, 256), 256)
        return pltpu.make_async_copy(
            stage_both.at[t % 2], both_sum.at[:, columns], load_sem.at[4 + t % 2]
        )

    tiles = width // 256
    count = groups * rows

    def down_tile(t, carry):
        columns = pl.ds(pl.multiple_of(t * 256, 256), 256)

        @pl.when(t < tiles - 1)
        def _():
            load_tile(t + 1).start()

        load_tile(t).wait()
        down_sum[:, columns] = lax.dot_general(
            activated[...].reshape(count, members * 128),
            cot_tile[t % 2].reshape(count, 256),
            TN,
            preferred_element_type=F32,
        ).astype(BF16)
        return carry

    z = lax.axis_index("mp")

    def down_rows(owner):
        return down_sum.at[pl.ds(pl.multiple_of(owner * LANES, LANES), LANES)]

    keep_down = pltpu.make_async_copy(down_rows(z), down_in.at[z], local.at[2])
    pass_down = [
        to_mp(
            down_rows(lax.rem(z + step, members)),
            down_in.at[z],
            send_z.at[step - 1],
            recv_z.at[step - 1],
            lax.rem(z + step, members),
        )
        for step in range(1, members)
    ]

    def weight_tile(t, carry):
        columns = pl.ds(pl.multiple_of(t * 256, 256), 256)

        @pl.when(t >= 2)
        def _():
            store_both(t - 2).wait()

        value = lax.dot_general(
            hidden_all[:, :, columns].reshape(count, 256),
            both_grad[...].reshape(count, members * 256),
            TN,
            preferred_element_type=F32,
        )
        for z in range(members):
            stage_both[t % 2, z] = value[:, z * 256 : z * 256 + 256].astype(BF16)
        store_both(t).start()
        return carry

    load_tile(0).start()
    reduce.add_side(0)
    reduce.corners[0].start()
    reduce.corners[1].start()
    lax.fori_loop(0, tiles, down_tile, 0)
    keep_down.start()
    for copy in pass_down:
        copy.start()
    lax.fori_loop(0, 2, weight_tile, 0)
    reduce.middle()
    lax.fori_loop(2, tiles, weight_tile, 0)
    reduce.end()
    start_middle.wait()
    sums[...] = jnp.zeros_like(sums)

    def body(span):
        change = norm_back_rows(reduce.rows_of(span), middle_grad[span, :], gain[...], sums, span)
        total = cotangent[span, :].astype(F32) + change
        middle_grad[span, :] = total
        branch[span, :] = total.astype(BF16)

    each_chunk(rows, body)
    gather.sent()
    reduce.finish()
    for t in (tiles - 2, tiles - 1):
        store_both(t).wait()
    keep_down.wait()
    for copy in pass_down:
        copy.wait()


def feed(hidden_own, cotangent_all, middle, w_both, cotangent, gain, w_down):
    groups, rows, width = cotangent_all.shape
    members = w_both.shape[0]
    dma = pltpu.SemaphoreType.DMA
    units = members * 128
    return pl.pallas_call(
        feed_kernel,
        out_shape=(
            jax.ShapeDtypeStruct((rows, width), F32),
            jax.ShapeDtypeStruct((rows, width), BF16),
            jax.ShapeDtypeStruct((8, width), F32),
            jax.ShapeDtypeStruct((groups, rows, units), BF16),
            jax.ShapeDtypeStruct((members, width, 256), BF16),
            jax.ShapeDtypeStruct((members, LANES, width), BF16),
        ),
        in_specs=[anywhere()] * 4 + [on_chip()] * 3,
        out_specs=(on_chip(),) * 4 + (anywhere(),) * 2,
        scratch_shapes=[
            pltpu.VMEM((groups, rows, width), BF16),
            pltpu.VMEM((groups, rows, 2 * units), BF16),
        ]
        + reduce_scratch(rows, width)
        + [
            dma((13,)),
            dma((13,)),
            pltpu.VMEM((2, rows, width), BF16),
            pltpu.VMEM((2, groups, rows, 256), BF16),
            pltpu.VMEM((2, members, 256, 256), BF16),
            pltpu.VMEM((units, width), BF16),
            pltpu.VMEM((width, 2 * units), BF16),
            dma((6 + members,)),
            dma((3,)),
            dma((3,)),
            dma((3,)),
        ],
        compiler_params=remote_params(5, 63 * 1024 * 1024),
        cost_estimate=pl.CostEstimate(flops=0, bytes_accessed=400_000_000, transcendentals=0),
        name="feed",
    )(hidden_own, cotangent_all, middle, w_both, cotangent, gain, w_down)


def input_kernel(
    qkv_grad, w_qkv, hidden_all, branch_all, mixed, tokens, middle_grad, gain, sums_two,
    both_sum, both_in,
    result, gains, both_all, heads_all,
    part, from_side, from_corner, from_near, send, recv, sums,
    stage, arrive, send_h, recv_s, recv_h, own, plane_sums, column_sums, send_p, recv_p,
    weight_sum, row_tile, tile_sem, send_b, recv_b, send_t, recv_t, both_found, heads_own, local,
):
    me, z = lax.axis_index("dp"), lax.axis_index("mp")
    count = qkv_grad.shape[0]
    tiles = tokens.shape[1] // 256
    outer = (z == 0) | (z == 3)

    def columns_of(t):
        return pl.ds(pl.multiple_of(lax.rem(t, tiles) * 256, 256), 256)

    def load(t, source):
        return pltpu.make_async_copy(
            source.at[:, :, columns_of(t)], row_tile.at[t % 2], tile_sem.at[t % 2]
        )

    own_part = pltpu.make_async_copy(both_sum.at[z], both_found.at[0], local.at[0])
    own_part.start()
    ways = [(outer, 1, 1), (outer, 2, 2)]
    ways += [(z == 1, 0, 1), (z == 1, 2, 2), (z == 1, 3, 3)]
    ways += [(z == 2, 0, 1), (z == 2, 1, 2), (z == 2, 3, 3)]

    def came(source, place):
        return pltpu.make_async_copy(both_in.at[source], both_found.at[place], local.at[place])

    for here, source, place in ways:
        pl.when(here)(came(source, place).start)

    @pl.when(outer)
    def _():
        both_found[3] = jnp.zeros_like(both_found[3])

    load(0, branch_all).start()
    greet_all(pltpu.get_barrier_semaphore())
    own_part.wait()
    for here, source, place in ways:
        pl.when(here)(came(source, place).wait)

    def add(span):
        value = both_found[0, span, :].astype(F32) + both_found[1, span, :].astype(F32)
        value = value + both_found[2, span, :].astype(F32) + both_found[3, span, :].astype(F32)
        both_found[0, span, :] = value.astype(BF16)

    each_chunk(both_found.shape[1], add)
    both = Gather(both_found.at[0], both_all, send_b, recv_b, local.at[4])

    def weight_tile(t, carry):
        @pl.when(t < tiles - 1)
        def _():
            load(t + 1, branch_all).start()

        @pl.when((t >= tiles - 1) & (t < 2 * tiles - 1))
        def _():
            load(t + 1, hidden_all).start()

        load(t, hidden_all).wait()

        @pl.when(t < tiles)
        def _():
            weight_sum[pl.ds(768, 256), columns_of(t)] = lax.dot_general(
                mixed[...], row_tile[t % 2].reshape(count, 256), TN, preferred_element_type=F32
            ).astype(BF16)

        @pl.when(t >= tiles)
        def _():
            weight_sum[pl.ds(0, 768), columns_of(t)] = lax.dot_general(
                qkv_grad[...], row_tile[t % 2].reshape(count, 256), TN, preferred_element_type=F32
            ).astype(BF16)

        return carry

    heads = Heads(weight_sum, stage, arrive, send_h, recv_s, recv_h)
    reduce = Reduce(qkv_grad, w_qkv, False, part, from_side, from_corner, from_near, send, recv)
    reduce.begin()
    lax.fori_loop(0, tiles, weight_tile, 0)
    heads.start((3,))
    reduce.middle()
    both.start()
    lax.fori_loop(tiles, 2 * tiles, weight_tile, 0)
    heads.start((0, 1, 2))
    heads.add((3,))
    reduce.end()
    sums[...] = jnp.zeros_like(sums)

    def body(span):
        values = tokens[span, :].astype(F32)
        change = norm_back_rows(reduce.rows_of(span), values, gain[...], sums, span)
        result[span, :] = (middle_grad[span, :] + change).astype(BF16)

    each_chunk(result.shape[0], body)
    own[...] = jnp.concatenate(
        [
            jnp.sum(sums[...], axis=0, keepdims=True),
            jnp.sum(sums_two[...], axis=0, keepdims=True),
        ],
        axis=0,
    )
    swaps = swap_all(own, plane_sums, send_p, recv_p)
    for copy in swaps:
        copy.start()
    plane_sums[me] = own[...]
    heads.add((0, 1, 2))
    both.pass_on()
    heads.total(heads_own)
    gather = Gather(heads_own, heads_all, send_t, recv_t, local.at[5])
    gather.start()
    for copy in swaps:
        copy.wait()
    found = plane_sums[0]
    for other in range(1, 8):
        found = found + plane_sums[other]
    column_sums[z] = found
    passes = [
        to_mp(
            column_sums.at[z],
            column_sums.at[z],
            send_p.at[6 + step],
            recv_p.at[6 + step],
            lax.rem(z + step, 4),
        )
        for step in range(1, 4)
    ]
    for copy in passes:
        copy.start()
    both.finish()
    for copy in passes:
        copy.wait()
    gains[...] = (column_sums[0] + column_sums[1]) + (column_sums[2] + column_sums[3])
    gather.pass_on()
    heads.finish_send()
    reduce.finish()
    gather.finish()


def project_input(
    qkv_grad, w_qkv, hidden_all, branch_all, mixed, tokens, middle_grad, gain, sums_two,
    both_sum, both_in,
):
    rows, width = tokens.shape
    groups = hidden_all.shape[0]
    dma = pltpu.SemaphoreType.DMA
    shape = jax.ShapeDtypeStruct
    return pl.pallas_call(
        input_kernel,
        out_shape=(
            shape((rows, width), BF16),
            shape((2, width), F32),
            shape((groups, width, 256), BF16),
            shape((groups, 4 * HEAD_DIM, width // 2), BF16),
        ),
        in_specs=[on_chip()] * 2 + [anywhere()] * 2 + [on_chip()] * 5 + [anywhere()] * 2,
        out_specs=(on_chip(),) * 2 + (anywhere(),) * 2,
        scratch_shapes=reduce_scratch(rows, width)
        + [
            pltpu.VMEM((8, width), F32),
            pltpu.VMEM((2, 4, HEAD_DIM, width), BF16),
            pltpu.VMEM((3, 4, HEAD_DIM, width // 2), BF16),
            dma((16,)),
            dma((8,)),
            dma((12,)),
            pltpu.VMEM((2, width), F32),
            pltpu.VMEM((8, 2, width), F32),
            pltpu.VMEM((4, 2, width), F32),
            dma((10,)),
            dma((10,)),
            pltpu.VMEM((8 * LANES, width), BF16),
            pltpu.VMEM((2, groups, rows, 256), BF16),
            dma((2,)),
            dma((13,)),
            dma((13,)),
            dma((13,)),
            dma((13,)),
            pltpu.VMEM((4, width, 256), BF16),
            pltpu.VMEM((4 * HEAD_DIM, width // 2), BF16),
            dma((6,)),
        ],
        compiler_params=remote_params(6, 63 * 1024 * 1024),
        cost_estimate=pl.CostEstimate(flops=0, bytes_accessed=250_000_000, transcendentals=0),
        name="project_input",
    )(
        qkv_grad, w_qkv, hidden_all, branch_all, mixed, tokens, middle_grad, gain, sums_two,
        both_sum, both_in,
    )


def assemble_kernel(
    both, down, heads, order_column, output_b, input_b,
    output, inputs, query, keys, values, project, gate, upward, down_out,
):
    for d in range(both.shape[0]):
        gate[:, d * 128 : d * 128 + 128] = both[d, :, :128].astype(F32)
        upward[:, d * 128 : d * 128 + 128] = both[d, :, 128:].astype(F32)
    down_out[...] = down[0].astype(F32)
    for kind, out in enumerate((query, keys, values, project)):
        out[...] = heads[0, kind].astype(F32)
    place = lax.broadcasted_iota(jnp.int32, (order_column.shape[0], output_b.shape[0]), 1)
    unsort = (place.astype(F32) == order_column[...]).astype(BF16)
    output[...] = jnp.dot(unsort, output_b[...], preferred_element_type=F32).astype(BF16)
    inputs[...] = jnp.dot(unsort, input_b[...], preferred_element_type=F32).astype(BF16)


def assemble(both, down, heads, order_column, output_b, input_b):
    groups, width, wide = both.shape
    rows = output_b.shape[0]
    units = down.shape[1]
    chips = groups // 2
    columns = heads.shape[3]
    row_tile, tile = rows // groups, width // groups
    shape = jax.ShapeDtypeStruct
    head = shape((chips * HEAD_DIM, 2 * columns), F32)
    head_spec = pl.BlockSpec((HEAD_DIM, columns), lambda i: (i // 2, i % 2))
    wide_spec = pl.BlockSpec((tile, groups * units), lambda i: (i, 0))
    row_spec = pl.BlockSpec((row_tile, width), lambda i: (i, 0))
    whole_spec = pl.BlockSpec((rows, width), lambda i: (0, 0))
    return pl.pallas_call(
        assemble_kernel,
        grid=(groups,),
        out_shape=(
            shape((rows, width), BF16),
            shape((rows, width), BF16),
            head,
            head,
            head,
            head,
            shape((width, groups * units), F32),
            shape((width, groups * units), F32),
            shape((groups * units, width), F32),
        ),
        in_specs=[
            pl.BlockSpec((groups, tile, wide), lambda i: (0, i, 0)),
            pl.BlockSpec((1, units, width), lambda i: (i, 0, 0)),
            pl.BlockSpec((1, 4, HEAD_DIM, columns), lambda i: (i, 0, 0, 0)),
            pl.BlockSpec((row_tile, 1), lambda i: (i, 0)),
            whole_spec,
            whole_spec,
        ],
        out_specs=(
            row_spec, row_spec, head_spec, head_spec, head_spec, head_spec, wide_spec, wide_spec,
            pl.BlockSpec((units, width), lambda i: (i, 0)),
        ),
        compiler_params=pltpu.CompilerParams(vmem_limit_bytes=VMEM_LIMIT),
        cost_estimate=pl.CostEstimate(flops=0, bytes_accessed=58_000_000, transcendentals=0),
        name="assemble",
    )(both, down, heads, order_column, output_b, input_b)


def swapped(
    tokens, cotangent, route, lengths, key_mask, norm1_gain, norm2_gain,
    w_query, w_key, w_value, w_out, w_gate, w_up, w_down,
):
    groups = lax.axis_size("dp")
    members = lax.axis_size("mp")
    me = lax.axis_index("dp")
    z = lax.axis_index("mp")
    rows, width = tokens.shape
    bucket = rows // groups
    units = w_down.shape[0] // groups

    target = route // TOK_DEV
    earlier = jnp.arange(rows, dtype=jnp.int32)
    same = (target[:, None] == target[None, :]) & (earlier[None, :] < earlier[:, None])
    send_at = target * bucket + jnp.sum(same.astype(jnp.int32), axis=1)
    sorting = send_at[None, :] == earlier[:, None]
    slots_own = jnp.sum(jnp.where(sorting, (route % rows)[None, :], 0), axis=1)

    mask_window = lax.dynamic_slice_in_dim(
        jnp.concatenate([jnp.zeros((WINDOW,), jnp.int32), key_mask]), z * rows, rows + WINDOW
    )
    slot_rows = jnp.pad(slots_own.reshape(groups, bucket).T, ((0, 0), (0, LANES - groups)))
    mask_rows = jnp.pad(mask_window, (0, 4 * LANES - rows - WINDOW)).reshape(4, LANES)
    length_rows = jnp.pad(lengths, ((0, 3), (0, LANES - lengths.shape[1])))
    notes = jnp.concatenate([slot_rows, mask_rows, length_rows], axis=0).astype(F32)

    count = groups * rows
    scale = HEAD_DIM ** (-0.5)
    (
        hidden_one,
        w_qkv,
        w_proj,
        notes_all,
        w_both,
        mixed,
        kept,
        tokens_b,
        cotangent_b,
        cotangent_all,
    ) = attend_ahead(
        tokens,
        cotangent,
        send_at.astype(F32)[None],
        norm1_gain[None],
        notes,
        w_query.T,
        w_key.T,
        w_value.T,
        w_out,
        w_gate,
        w_up,
        scale,
    )
    mixed = mixed.reshape(count, 2 * LANES)
    middle, hidden_two, down_all = project_middle(mixed, w_proj, tokens_b, norm2_gain[None], w_down)
    down_all = down_all.reshape(members * units, width)
    middle_grad, branch, sums_two, activated, both_sum, down_in = feed(
        hidden_two, cotangent_all, middle, w_both, cotangent_b, norm2_gain[None], down_all
    )
    qkv_grad, output_rows, branch_all, both_in, down_whole = attend_back(
        kept,
        branch,
        w_proj,
        notes_all,
        activated.reshape(count, units * members),
        down_all,
        middle,
        both_sum,
        down_in,
        scale,
    )
    qkv_grad = qkv_grad.reshape(count, 6 * LANES)
    input_rows, gain_sums, both_whole, heads_whole = project_input(
        qkv_grad,
        w_qkv,
        hidden_one,
        branch_all,
        mixed,
        tokens_b,
        middle_grad,
        norm1_gain[None],
        sums_two,
        both_sum,
        both_in,
    )
    (
        output,
        input_grad,
        query_grad,
        key_grad,
        value_grad,
        proj_grad,
        gate_grad,
        up_grad,
        down_grad,
    ) = assemble(
        both_whole,
        down_whole,
        heads_whole.reshape(groups, 4, HEAD_DIM, width // 2),
        send_at.astype(F32)[:, None],
        output_rows,
        input_rows,
    )
    return (
        output,
        input_grad,
        gain_sums[0],
        gain_sums[1],
        query_grad.T,
        key_grad.T,
        value_grad.T,
        proj_grad,
        gate_grad,
        up_grad,
        down_grad,
    )


def solution(mesh):
    in_specs = (
        P(("dp", "mp"), None),
        P(("dp", "mp"), None),
        P(("dp", "mp")),
        P("dp", None),
        P("dp"),
        P(),
        P(),
        P(None, "mp"),
        P(None, "mp"),
        P(None, "mp"),
        P("mp", None),
        P(None, "mp"),
        P(None, "mp"),
        P("mp", None),
    )
    out_specs = (
        P(("dp", "mp"), None),
        P(("dp", "mp"), None),
        P(),
        P(),
        P(None, "mp"),
        P(None, "mp"),
        P(None, "mp"),
        P("mp", None),
        P(None, "mp"),
        P(None, "mp"),
        P("mp", None),
    )
    body = swapped if (mesh.shape["dp"], mesh.shape["mp"]) == (8, 4) else local
    return jax.shard_map(body, mesh=mesh, in_specs=in_specs, out_specs=out_specs, check_vma=False)
```

```python
import functools

import jax
import jax.numpy as jnp
from jax import lax
from jax.experimental import pallas as pl
from jax.experimental.pallas import tpu as pltpu
from jax.sharding import PartitionSpec as P

HEAD_DIM = 112
WINDOW = 64
TOK_DEV = 1536


EPSILON = 1e-05
MASKED = 1e30


def norm_rows(values):
    inverse = lax.rsqrt(jnp.mean(values * values, axis=-1, keepdims=True) + EPSILON)
    return (values * inverse, inverse)


def norm_back(gradient, normed, inverse, norm_gain):
    scaled = gradient * norm_gain
    result = inverse * (scaled - normed * jnp.mean(scaled * normed, axis=-1, keepdims=True))
    return (result, jnp.sum(gradient * normed, axis=0))


def padded(values, filler):
    front = jnp.full((WINDOW,) + values.shape[1:], filler, values.dtype)
    return jnp.concatenate([front, values], axis=0)


def block_scores(query_block, key_block, query_seg, key_seg, key_flag, first_row, score_scale):
    query_pos = first_row + jnp.arange(query_block.shape[0], dtype=jnp.int32)
    key_pos = first_row - WINDOW + jnp.arange(key_block.shape[0], dtype=jnp.int32)
    distance = query_pos[:, None] - key_pos[None, :]
    allowed = (distance >= 0) & (distance < WINDOW) & (query_seg[:, None] == key_seg[None, :])
    allowed = allowed & ((key_flag[None, :] == 1) | (distance == 0))
    raw_scores = (
        jnp.einsum("qhd,khd->hqk", query_block, key_block, preferred_element_type=jnp.float32)
        * score_scale
    )
    return jnp.where(allowed[None], raw_scores, -MASKED)


def block_inputs(query, key_pad, value_pad, segment, seg_pad, live_pad, first_row, block_rows):
    key_span = block_rows + WINDOW
    return (
        lax.dynamic_slice_in_dim(query, first_row, block_rows, 0),
        lax.dynamic_slice_in_dim(key_pad, first_row, key_span, 0),
        lax.dynamic_slice_in_dim(value_pad, first_row, key_span, 0),
        lax.dynamic_slice_in_dim(segment, first_row, block_rows, 0),
        lax.dynamic_slice_in_dim(seg_pad, first_row, key_span, 0),
        lax.dynamic_slice_in_dim(live_pad, first_row, key_span, 0),
    )


def attend_forward(query, key_all, value_all, segment, key_live):
    token_count, head_count, head_width = query.shape
    block_rows = min(512, token_count)
    score_scale = head_width ** (-0.5)
    key_pad = padded(key_all, 0.0)
    value_pad = padded(value_all, 0.0)
    seg_pad = padded(segment, -1)
    live_pad = padded(key_live, 0)

    def one_block(running, block_index):
        first_row = block_index * block_rows
        query_block, key_block, value_block, query_seg, key_seg, key_flag = block_inputs(
            query, key_pad, value_pad, segment, seg_pad, live_pad, first_row, block_rows
        )
        scores = block_scores(
            query_block, key_block, query_seg, key_seg, key_flag, first_row, score_scale
        )
        row_max = jnp.max(scores, axis=-1, keepdims=True)
        weights = jnp.exp(scores - row_max)
        denominator = jnp.sum(weights, axis=-1, keepdims=True)
        chances = (weights / denominator).astype(jnp.bfloat16)
        mixed = jnp.einsum("hqk,khd->qhd", chances, value_block, preferred_element_type=jnp.float32)
        return (
            running,
            (mixed.astype(jnp.bfloat16), row_max[..., 0] + jnp.log(denominator[..., 0])),
        )

    _, (mixed, logsum) = lax.scan(
        one_block, jnp.zeros((), jnp.int32), jnp.arange(token_count // block_rows, dtype=jnp.int32)
    )
    return (mixed.reshape(token_count, head_count * head_width), logsum)


def attend_backward(query, key_all, value_all, segment, key_live, logsum, mixed_grad):
    token_count, head_count, head_width = query.shape
    block_rows = min(512, token_count)
    key_span = block_rows + WINDOW
    score_scale = head_width ** (-0.5)
    key_pad = padded(key_all, 0.0)
    value_pad = padded(value_all, 0.0)
    seg_pad = padded(segment, -1)
    live_pad = padded(key_live, 0)

    def one_block(running, inputs):
        key_grad, value_grad = running
        block_index, block_logsum = inputs
        first_row = block_index * block_rows
        query_block, key_block, value_block, query_seg, key_seg, key_flag = block_inputs(
            query, key_pad, value_pad, segment, seg_pad, live_pad, first_row, block_rows
        )
        grad_block = lax.dynamic_slice_in_dim(mixed_grad, first_row, block_rows, 0)
        scores = block_scores(
            query_block, key_block, query_seg, key_seg, key_flag, first_row, score_scale
        )
        chances = jnp.exp(scores - block_logsum[..., None])
        chance_grad = jnp.einsum(
            "qhd,khd->hqk", grad_block, value_block, preferred_element_type=jnp.float32
        )
        row_dot = jnp.sum(chances * chance_grad, axis=-1, keepdims=True)
        score_grad = (chances * (chance_grad - row_dot)).astype(jnp.bfloat16)
        query_grad = (
            jnp.einsum("hqk,khd->qhd", score_grad, key_block, preferred_element_type=jnp.float32)
            * score_scale
        )
        key_part = (
            jnp.einsum("hqk,qhd->khd", score_grad, query_block, preferred_element_type=jnp.float32)
            * score_scale
        )
        value_part = jnp.einsum(
            "hqk,qhd->khd",
            chances.astype(jnp.bfloat16),
            grad_block,
            preferred_element_type=jnp.float32,
        )
        key_grad = lax.dynamic_update_slice_in_dim(
            key_grad,
            lax.dynamic_slice_in_dim(key_grad, first_row, key_span, 0) + key_part,
            first_row,
            0,
        )
        value_grad = lax.dynamic_update_slice_in_dim(
            value_grad,
            lax.dynamic_slice_in_dim(value_grad, first_row, key_span, 0) + value_part,
            first_row,
            0,
        )
        return ((key_grad, value_grad), query_grad)

    empty_grad = jnp.zeros((token_count + WINDOW, head_count, head_width), jnp.float32)
    (key_grad, value_grad), query_grad = lax.scan(
        one_block,
        (empty_grad, empty_grad),
        (jnp.arange(token_count // block_rows, dtype=jnp.int32), logsum),
    )
    flat_width = head_count * head_width
    return (
        query_grad.reshape(token_count, flat_width).astype(jnp.bfloat16),
        key_grad[WINDOW:].reshape(token_count, flat_width).astype(jnp.bfloat16),
        value_grad[WINDOW:].reshape(token_count, flat_width).astype(jnp.bfloat16),
    )


def local(
    tokens,
    cotangent,
    route,
    lengths,
    key_mask,
    norm1_gain,
    norm2_gain,
    w_query,
    w_key,
    w_value,
    w_out,
    w_gate,
    w_up,
    w_down,
):
    groups = lax.axis_size("dp")
    members = lax.axis_size("mp")
    member = lax.axis_index("mp")
    local_rows = tokens.shape[0]
    group_rows = local_rows * members
    bucket = local_rows // groups
    target = route // TOK_DEV
    chosen = (target[:, None] == jnp.arange(groups, dtype=jnp.int32)[None, :]).astype(jnp.int32)
    ranking = jnp.sum((jnp.cumsum(chosen, axis=0) - chosen) * chosen, axis=1)
    send_at = target * bucket + ranking
    arrival, arrival_grad, arrival_slot = (
        lax.all_to_all(
            jnp.zeros_like(tokens).at[send_at].set(tokens),
            "dp",
            split_axis=0,
            concat_axis=0,
            tiled=True,
        ),
        lax.all_to_all(
            jnp.zeros_like(cotangent).at[send_at].set(cotangent),
            "dp",
            split_axis=0,
            concat_axis=0,
            tiled=True,
        ),
        lax.all_to_all(
            jnp.zeros_like(route).at[send_at].set(route % local_rows),
            "dp",
            split_axis=0,
            concat_axis=0,
            tiled=True,
        ),
    )
    token_rows = jnp.zeros_like(arrival).at[arrival_slot].set(arrival)
    grad_rows = jnp.zeros_like(arrival_grad).at[arrival_slot].set(arrival_grad)
    seq_ends = jnp.cumsum(lengths[0])
    positions = jnp.arange(group_rows, dtype=jnp.int32)
    segment = jnp.sum((positions[:, None] >= seq_ends[None, :]).astype(jnp.int32), axis=1)
    input_rows = token_rows.astype(jnp.float32)
    normed_one, inverse_one = norm_rows(input_rows)
    leading_all, grad_all = (
        lax.all_gather(token_rows, "mp", axis=0, tiled=True),
        lax.all_gather(grad_rows, "mp", axis=0, tiled=True),
    )
    input_all = leading_all.astype(jnp.float32)
    normed_all, _ = norm_rows(input_all)
    hidden_one = (normed_all * norm1_gain).astype(jnp.bfloat16)
    head_count = w_query.shape[1] // HEAD_DIM
    query = jnp.dot(hidden_one, w_query, preferred_element_type=jnp.float32).astype(jnp.bfloat16)
    keys = jnp.dot(hidden_one, w_key, preferred_element_type=jnp.float32).astype(jnp.bfloat16)
    values = jnp.dot(hidden_one, w_value, preferred_element_type=jnp.float32).astype(jnp.bfloat16)
    query_heads = query.reshape(group_rows, head_count, HEAD_DIM)
    key_heads = keys.reshape(group_rows, head_count, HEAD_DIM)
    value_heads = values.reshape(group_rows, head_count, HEAD_DIM)
    mixed_flat, logsum = attend_forward(query_heads, key_heads, value_heads, segment, key_mask)
    attention_all = lax.psum(jnp.dot(mixed_flat, w_out, preferred_element_type=jnp.float32), "mp")
    middle_all = input_all + attention_all
    middle_rows = lax.dynamic_slice_in_dim(middle_all, member * local_rows, local_rows, 0)
    normed_mid, _ = norm_rows(middle_all)
    hidden_two = (normed_mid * norm2_gain).astype(jnp.bfloat16)
    normed_two, inverse_two = norm_rows(middle_rows)
    gate_value = jnp.dot(hidden_two, w_gate, preferred_element_type=jnp.float32)
    upward = jnp.dot(hidden_two, w_up, preferred_element_type=jnp.float32)
    sigmoid = jax.nn.sigmoid(gate_value)
    activated = (gate_value * sigmoid * upward).astype(jnp.bfloat16)
    out_rows = middle_rows + lax.psum_scatter(
        jnp.dot(activated, w_down, preferred_element_type=jnp.float32).astype(jnp.bfloat16),
        "mp",
        scatter_dimension=0,
        tiled=True,
    ).astype(jnp.float32)
    activated_grad = jnp.einsum("td,fd->tf", grad_all, w_down, preferred_element_type=jnp.float32)
    gate_grad = (activated_grad * upward * sigmoid * (1.0 + gate_value * (1.0 - sigmoid))).astype(
        jnp.bfloat16
    )
    upward_grad = (activated_grad * gate_value * sigmoid).astype(jnp.bfloat16)
    down_sum = jnp.einsum("tf,td->fd", activated, grad_all, preferred_element_type=jnp.float32)
    gate_sum = jnp.einsum("td,tf->df", hidden_two, gate_grad, preferred_element_type=jnp.float32)
    upward_sum = jnp.einsum(
        "td,tf->df", hidden_two, upward_grad, preferred_element_type=jnp.float32
    )
    hidden_two_grad = lax.psum_scatter(
        jnp.einsum("tf,df->td", gate_grad, w_gate, preferred_element_type=jnp.float32)
        + jnp.einsum("tf,df->td", upward_grad, w_up, preferred_element_type=jnp.float32),
        "mp",
        scatter_dimension=0,
        tiled=True,
    )
    norm_part_two, gain_two_grad = norm_back(hidden_two_grad, normed_two, inverse_two, norm2_gain)
    middle_grad = grad_rows.astype(jnp.float32) + norm_part_two
    branch_all = lax.all_gather(middle_grad.astype(jnp.bfloat16), "mp", axis=0, tiled=True)
    output_sum = jnp.einsum("tc,td->cd", mixed_flat, branch_all, preferred_element_type=jnp.float32)
    mixed_grad = jnp.einsum(
        "td,cd->tc", branch_all, w_out, preferred_element_type=jnp.float32
    ).astype(jnp.bfloat16)
    query_grad, key_grad, value_grad = attend_backward(
        query_heads,
        key_heads,
        value_heads,
        segment,
        key_mask,
        logsum,
        mixed_grad.reshape(group_rows, head_count, HEAD_DIM),
    )
    query_sum = jnp.einsum("td,tc->dc", hidden_one, query_grad, preferred_element_type=jnp.float32)
    key_sum = jnp.einsum("td,tc->dc", hidden_one, key_grad, preferred_element_type=jnp.float32)
    value_sum = jnp.einsum("td,tc->dc", hidden_one, value_grad, preferred_element_type=jnp.float32)
    hidden_one_grad = lax.psum_scatter(
        (
            jnp.einsum("tc,dc->td", query_grad, w_query, preferred_element_type=jnp.float32)
            + jnp.einsum("tc,dc->td", key_grad, w_key, preferred_element_type=jnp.float32)
            + jnp.einsum("tc,dc->td", value_grad, w_value, preferred_element_type=jnp.float32)
        ).astype(jnp.bfloat16),
        "mp",
        scatter_dimension=0,
        tiled=True,
    ).astype(jnp.float32)
    norm_part_one, gain_one_grad = norm_back(hidden_one_grad, normed_one, inverse_one, norm1_gain)
    input_grad = middle_grad + norm_part_one
    gain_one_sum, gain_two_sum = lax.psum((gain_one_grad, gain_two_grad), ("dp", "mp"))
    weight_sums = (
        lax.psum(query_sum.astype(jnp.bfloat16), "dp").astype(jnp.float32),
        lax.psum(key_sum.astype(jnp.bfloat16), "dp").astype(jnp.float32),
        lax.psum(value_sum.astype(jnp.bfloat16), "dp").astype(jnp.float32),
        lax.psum(output_sum.astype(jnp.bfloat16), "dp").astype(jnp.float32),
        lax.psum(gate_sum.astype(jnp.bfloat16), "dp").astype(jnp.float32),
        lax.psum(upward_sum.astype(jnp.bfloat16), "dp").astype(jnp.float32),
        lax.psum(down_sum.astype(jnp.bfloat16), "dp").astype(jnp.float32),
    )
    back_out, back_grad = (
        lax.all_to_all(
            out_rows.astype(jnp.bfloat16)[arrival_slot],
            "dp",
            split_axis=0,
            concat_axis=0,
            tiled=True,
        ),
        lax.all_to_all(
            input_grad.astype(jnp.bfloat16)[arrival_slot],
            "dp",
            split_axis=0,
            concat_axis=0,
            tiled=True,
        ),
    )
    return (
        back_out[send_at],
        back_grad[send_at],
        gain_one_sum,
        gain_two_sum,
        weight_sums[0],
        weight_sums[1],
        weight_sums[2],
        weight_sums[3],
        weight_sums[4],
        weight_sums[5],
        weight_sums[6],
    )


MESH = pl.DeviceIdType.MESH
LANES = 128
F32 = jnp.float32
BF16 = jnp.bfloat16
VMEM_LIMIT = 56 * 1024 * 1024


def plane():
    me = lax.axis_index("dp")
    side = me + 1 - 2 * lax.rem(me, 2)
    over_x = me + 2 - 4 * lax.rem(lax.div(me, 2), 2)
    over_y = me + 4 - 8 * lax.rem(lax.div(me, 4), 2)
    corner = over_x + 4 - 8 * lax.rem(lax.div(over_x, 4), 2)
    return (me, side, over_x, over_y, corner)


def to_dp(source, target, send_sem, recv_sem, index):
    return pltpu.make_async_remote_copy(
        src_ref=source,
        dst_ref=target,
        send_sem=send_sem,
        recv_sem=recv_sem,
        device_id={"dp": index},
        device_id_type=MESH,
    )


def to_mp(source, target, send_sem, recv_sem, index):
    return pltpu.make_async_remote_copy(
        src_ref=source,
        dst_ref=target,
        send_sem=send_sem,
        recv_sem=recv_sem,
        device_id={"mp": index},
        device_id_type=MESH,
    )


def owner_at(turn):
    me, side, over_x, over_y, _ = plane()
    block = turn // 2
    near = ((block + 1) // 2) % 2
    far = block // 3
    second = turn % 2
    other = (1 - near) * second + (block // 2) * near
    owner = me + (near * (1 - second) + far) * (over_x - me)
    return owner + (near * second + far) * (over_y - me) + other * (side - me)


ARRIVALS = (
    (1, (4,)),
    (2, (0, 1, 2)),
    (3, (3,)),
    (4, (6, 9)),
    (5, (8, 10)),
    (6, (5, 7)),
    (7, (11, 12)),
)


class Gather:
    AFTER = {0: (5, 6), 1: (7, 8), 2: (9,), 3: (10,), 5: (11,), 7: (12,)}

    def __init__(self, own, out, send, recv, local=None):
        me, side, over_x, over_y, corner = plane()
        half = out.shape[1] // 2
        low, high = pl.ds(0, half), pl.ds(half, half)
        self.keep = None if own is None else pltpu.make_async_copy(own, out.at[me], local)
        own = out.at[me] if own is None else own

        def hop(number, source, target, index):
            return to_dp(source, target, send.at[number], recv.at[number], index)

        def onward(number, owner, part, index):
            place = out.at[owner, part]
            return hop(number, place, place, index)

        self.copies = [
            hop(0, own.at[low], out.at[me, low], over_x),
            hop(1, own.at[high], out.at[me, high], over_y),
            hop(2, own.at[high], out.at[me, high], over_x),
            hop(3, own.at[low], out.at[me, low], over_y),
            hop(4, own, out.at[me], side),
            onward(5, over_x, low, over_y),
            onward(6, over_x, low, side),
            onward(7, over_y, high, over_x),
            onward(8, over_y, high, side),
            onward(9, over_x, high, side),
            onward(10, over_y, low, side),
            onward(11, corner, low, side),
            onward(12, corner, high, side),
        ]

    def start(self):
        for number in range(5):
            self.copies[number].start()
        if self.keep is not None:
            self.keep.start()

    def arrive(self, *numbers):
        for number in numbers:
            self.copies[number].wait_recv()
            for later in self.AFTER.get(number, ()):
                self.copies[later].start()

    def pass_on(self):
        self.arrive(0, 1, 2, 3)

    def sent(self):
        for copy in self.copies:
            copy.wait_send()
        if self.keep is not None:
            self.keep.wait()

    def finish(self):
        self.arrive(5, 7, 4, 6, 8, 9, 10, 11, 12)
        self.sent()


def greet_all():
    barrier = pltpu.get_barrier_semaphore()
    me, z = lax.axis_index("dp"), lax.axis_index("mp")
    for step in range(1, 8):
        pl.semaphore_signal(
            barrier, inc=1, device_id={"dp": lax.rem(me + step, 8)}, device_id_type=MESH
        )
    core = lax.rem(me, 2)
    for step in range(1, 4):
        for other in (me, me + 1 - 2 * core):
            pl.semaphore_signal(
                barrier,
                inc=1,
                device_id={"dp": other, "mp": lax.rem(z + step, 4)},
                device_id_type=MESH,
            )
    return barrier


def start_all(copies):
    for copy in copies:
        copy.start()
    return copies


def wait_all(copies):
    for copy in copies:
        copy.wait()


def swap_all(source, target, send, recv):
    me = lax.axis_index("dp")
    return [
        to_dp(source, target.at[me], send.at[step - 1], recv.at[step - 1], lax.rem(me + step, 8))
        for step in range(1, 8)
    ]


class Spread:
    def __init__(self, share, w_qkv, w_out, send, recv, local):
        me, z = lax.axis_index("dp"), lax.axis_index("mp")
        core = lax.rem(me, 2)
        self.place = z + core * (3 - 2 * z)
        self.send, self.recv, self.local = send, recv, local
        self.shares = [share.at[0], share.at[1], share.at[2], share.at[3]]
        self.slots = (core, 1 - core)
        self.core = core
        self.w_qkv, self.w_out = w_qkv, w_out

    def target(self, which, piece):
        slot = self.slots[which]
        block = slot if piece == 3 else 2 * piece + slot
        rows = pl.ds(pl.multiple_of(block * LANES, LANES), HEAD_DIM)
        return (self.w_out if piece == 3 else self.w_qkv).at[rows]

    def hop(self, which, piece, number, place, own):
        source = self.shares[piece] if own else self.target(which, piece)
        z = place + self.core * (3 - 2 * place)
        return to_mp(
            source,
            self.target(which, piece),
            self.send.at[number * 4 + piece],
            self.recv.at[which * 4 + piece],
            z,
        )

    def keep(self, which, piece):
        return pltpu.make_async_copy(
            self.shares[piece], self.target(which, piece), self.local.at[piece]
        )

    def start(self, pieces):
        @pl.when(self.place == 0)
        def _():
            for piece in pieces:
                self.hop(0, piece, 0, 1, True).start()
                self.keep(0, piece).start()

        @pl.when(self.place == 1)
        def _():
            for piece in pieces:
                self.hop(1, piece, 0, 0, True).start()
                self.hop(1, piece, 1, 2, True).start()
                self.keep(1, piece).start()

    def pass_on(self, pieces):
        @pl.when(self.place == 1)
        def _():
            for piece in pieces:
                self.hop(0, piece, 2, 2, False).wait_recv()
                self.hop(0, piece, 2, 2, False).start()

        @pl.when(self.place == 2)
        def _():
            for which in (1, 0):
                for piece in pieces:
                    self.hop(which, piece, which, 3, False).wait_recv()
                    self.hop(which, piece, which, 3, False).start()

    def finish(self, pieces):
        @pl.when(self.place == 0)
        def _():
            for piece in pieces:
                self.hop(1, piece, 0, 1, False).wait_recv()
                self.hop(0, piece, 0, 1, True).wait_send()
                self.keep(0, piece).wait()

        @pl.when(self.place == 1)
        def _():
            for piece in pieces:
                self.hop(1, piece, 0, 0, True).wait_send()
                self.hop(1, piece, 1, 2, True).wait_send()
                self.hop(0, piece, 2, 2, False).wait_send()
                self.keep(1, piece).wait()

        @pl.when(self.place == 2)
        def _():
            for piece in pieces:
                for which in (1, 0):
                    self.hop(which, piece, which, 3, False).wait_send()

        @pl.when(self.place == 3)
        def _():
            for piece in pieces:
                for which in (1, 0):
                    self.hop(which, piece, which, 3, False).wait_recv()


class Column:
    def __init__(self, own, out, send, recv, local):
        z = lax.axis_index("mp")
        self.z, self.own, self.out, self.send, self.recv = z, own, out, send, recv
        self.outer = (z == 0) | (z == 3)
        near = 1 + lax.div(z, 3)
        self.from_outer = (near, 3 - near)
        self.edge = 3 * (z - 1)
        self.from_inner = (3 - z, 3 - self.edge, self.edge)
        self.keep = pltpu.make_async_copy(own, out.at[z], local)

    def straight(self, number, target):
        return to_mp(
            self.own, self.out.at[self.z], self.send.at[number], self.recv.at[self.z], target
        )

    def onward(self):
        far = 3 - self.edge
        return to_mp(
            self.out.at[far], self.out.at[far], self.send.at[3], self.recv.at[far], self.edge
        )

    def came(self, source):
        return to_mp(
            self.own, self.out.at[source], self.send.at[0], self.recv.at[source], source
        ).wait_recv

    def start(self):
        self.keep.start()

        @pl.when(self.outer)
        def _():
            for number, target in enumerate(self.from_outer):
                self.straight(number, target).start()

        @pl.when(jnp.logical_not(self.outer))
        def _():
            for number, target in enumerate(self.from_inner):
                self.straight(number, target).start()

    def pass_on(self):
        @pl.when(jnp.logical_not(self.outer))
        def _():
            self.came(3 - self.edge)()
            self.onward().start()

    def finish(self):
        @pl.when(self.outer)
        def _():
            for source in (1, 2):
                self.came(source)()
            self.came(3 - self.z)()
            for number, target in enumerate(self.from_outer):
                self.straight(number, target).wait_send()

        @pl.when(jnp.logical_not(self.outer))
        def _():
            self.came(3 - self.z)()
            self.came(self.edge)()
            for number, target in enumerate(self.from_inner):
                self.straight(number, target).wait_send()
            self.onward().wait_send()

        self.keep.wait()


def anywhere():
    return pl.BlockSpec(memory_space=pl.ANY)


def on_chip():
    return pl.BlockSpec(memory_space=pltpu.VMEM)


def remote_params(number, limit=VMEM_LIMIT):
    return pltpu.CompilerParams(
        collective_id=number, has_side_effects=True, vmem_limit_bytes=limit
    )


def hot_of(notes, k, size):
    own = notes[:, 0:48, :].reshape(size, LANES)
    lane = lax.broadcasted_iota(jnp.int32, (size, LANES), 1)
    slot = jnp.sum(jnp.where(lane == k, own, 0.0), axis=1, keepdims=True)
    return (lax.broadcasted_iota(jnp.int32, (size, size), 1).astype(F32) == slot).astype(BF16)


def block_mask(notes, k, block, z, rows):
    position = rows * z + block * 128 + lax.broadcasted_iota(jnp.int32, (128, 1), 0)
    position = position.astype(F32)
    first_end = notes[k, 52:53, 0:1]
    second_end = first_end + notes[k, 52:53, 1:2]
    begin = jnp.where(position >= first_end, first_end, 0.0)
    begin = jnp.where(position >= second_end, second_end, begin)
    column = lax.broadcasted_iota(jnp.int32, (128, 192), 1)
    distance = 64 + lax.broadcasted_iota(jnp.int32, (128, 192), 0) - column
    key_position = (rows * z + block * 128 - 64 + column).astype(F32)
    live = jnp.concatenate(
        [notes[k, 48 + block : 49 + block, :], notes[k, 49 + block : 50 + block, 0:64]], axis=1
    )
    allowed = (distance >= 0) & (distance < WINDOW) & (key_position >= begin)
    return allowed & ((live == 1.0) | (distance == 0))


NT = (((1,), (1,)), ((), ()))
TN = (((0,), (0,)), ((), ()))


def forward_kernel(
    tokens, cotangent, order_row, gain, notes, query, keys, values, project, gate,
    hidden_out, w_qkv_out, w_out, notes_all, gate_all, mixed_out, kept_out, tokens_out, cotangent_out,
    cotangent_all,
    hidden_all, qkv, share, gate_own, w_qkv, mixed, kept, tokens_b, cotangent_b,
    send, recv, send_a, recv_a, send_g, recv_g, send_w, recv_w, send_n, recv_n, send_c, recv_c,
    local, out_sem, store_sem, *, scale,
):
    groups, rows, width = hidden_all.shape
    me, z = lax.axis_index("dp"), lax.axis_index("mp")
    members = lax.axis_size("mp")
    barrier = greet_all()
    head = pl.ds(pl.multiple_of(lax.div(me, 2) * HEAD_DIM, 16), HEAD_DIM)
    units = pl.ds(pl.multiple_of(me * LANES, LANES), LANES)
    loads = [
        pltpu.make_async_copy(source.at[head], share.at[piece], local.at[piece])
        for piece, source in enumerate((query, keys, values, project))
    ]
    loads.append(pltpu.make_async_copy(gate.at[:, units], gate_own, local.at[4]))
    for copy in loads:
        copy.start()
    none = jnp.zeros((LANES - HEAD_DIM, width), BF16)
    for block in range(6):
        w_qkv[block * LANES + HEAD_DIM : block * LANES + LANES, :] = none
    for block in range(2):
        w_out[block * LANES + HEAD_DIM : block * LANES + LANES, :] = none

    place = lax.broadcasted_iota(jnp.int32, (rows, rows), 0).astype(F32)
    sort = (place == order_row[...]).astype(BF16)
    tokens_b[...] = jnp.dot(sort, tokens[...], preferred_element_type=F32).astype(BF16)

    def normalise(span):
        value = tokens_b[span, :].astype(F32)
        inverse = lax.rsqrt(mean_rows(value * value) + EPSILON)
        hidden_all[me, span, :] = (value * inverse * gain[...]).astype(BF16)

    each_chunk(rows, normalise)
    notes_all[me] = notes[...]
    stores = start_all([pltpu.make_async_copy(tokens_b, tokens_out, store_sem.at[0])])
    pl.semaphore_wait(barrier, 13)
    gather = Gather(None, hidden_all, send_a, recv_a)
    gather.start()
    swaps = swap_all(notes, notes_all, send_n, recv_n)
    for copy in swaps:
        copy.start()
    for copy in loads[:4]:
        copy.wait()
    spread = Spread(share, w_qkv, w_out, send_w, recv_w, local)
    spread.start((0, 1, 2))
    cotangent_b[...] = jnp.dot(sort, cotangent[...], preferred_element_type=F32).astype(BF16)
    stores += start_all([pltpu.make_async_copy(cotangent_b, cotangent_out, store_sem.at[1])])
    wait_all(loads[4:])
    column = Column(gate_own, gate_all, send_c, recv_c, local.at[4])
    second = Gather(cotangent_b, cotangent_all, send_g, recv_g, local.at[5])
    spread.pass_on((0, 1, 2))
    gather.arrive(0, 1)
    second.start()
    column.start()
    gather.arrive(2, 3)
    spread.finish((0, 1, 2))
    spread.start((3,))
    stores += start_all([pltpu.make_async_copy(w_qkv, w_qkv_out, store_sem.at[2])])
    for copy in swaps:
        copy.wait()

    def keep(turn):
        owner = owner_at(turn)
        return pltpu.make_async_copy(hidden_all.at[owner], hidden_out.at[owner], out_sem.at[turn])

    def multiply(turn, carry):
        for number, numbers in ARRIVALS:
            left = tuple(n for n in numbers if n > 3)
            if left:
                pl.when(turn == number)(functools.partial(gather.arrive, *left))
        owner = owner_at(turn)
        keep(turn).start()
        product = lax.dot_general(
            hidden_all[owner], w_qkv[...], NT, preferred_element_type=F32
        ).astype(BF16)
        qkv[owner] = product.reshape(groups, rows // groups, 768)
        return carry

    lax.fori_loop(0, groups, multiply, 0)

    def halo(k, other):
        return to_mp(
            kept.at[k, pl.ds(rows, 64), pl.ds(256, 512)],
            kept.at[k, pl.ds(0, 64), pl.ds(256, 512)],
            send.at[k],
            recv.at[k],
            other,
        )

    def store_kept(k):
        return pltpu.make_async_copy(kept.at[k], kept_out.at[k], store_sem.at[3 + k])

    def store_mixed(k):
        span = pl.ds(k, 1)
        return pltpu.make_async_copy(
            mixed.at[:, span], mixed_out.at[:, span], store_sem.at[3 + groups + k]
        )

    def order(k, carry):
        hot = hot_of(notes_all, k, rows)
        given = qkv[:, pl.ds(k, 1)].reshape(rows, 768)
        kept[k, pl.ds(64, rows), :] = lax.dot_general(
            hot, given, TN, preferred_element_type=F32
        ).astype(BF16)
        kept[k, pl.ds(0, 64), pl.ds(0, 256)] = jnp.zeros((64, 256), BF16)

        @pl.when(z < members - 1)
        def _():
            halo(k, z + 1).start()

        @pl.when(z == 0)
        def _():
            kept[k, pl.ds(0, 64), pl.ds(256, 512)] = jnp.zeros((64, 512), BF16)

        return carry

    lax.fori_loop(0, groups, order, 0)

    def attend(k, carry):
        @pl.when(z > 0)
        def _():
            halo(k, z).wait_recv()

        store_kept(k).start()
        hot = hot_of(notes_all, k, rows)
        found = []
        for block in range(rows // 128):
            allowed = block_mask(notes_all, k, block, z, rows)
            heads = []
            for head in range(2):
                query = kept[k, pl.ds(64 + block * 128, 128), pl.ds(head * 128, 128)]
                keys = kept[k, pl.ds(block * 128, 192), pl.ds(256 + head * 128, 128)]
                values = kept[k, pl.ds(block * 128, 192), pl.ds(512 + head * 128, 128)]
                scores = lax.dot_general(query, keys, NT, preferred_element_type=F32) * scale
                scores = jnp.where(allowed, scores, -MASKED)
                weights = jnp.exp(scores - jnp.max(scores, axis=-1, keepdims=True))
                total = jnp.sum(weights, axis=-1, keepdims=True)
                chances = (weights / total).astype(BF16)
                heads.append(jnp.dot(chances, values, preferred_element_type=F32).astype(BF16))
            found.append(jnp.concatenate(heads, axis=1))
        ordered = jnp.concatenate(found, axis=0)
        back = jnp.dot(hot, ordered, preferred_element_type=F32).astype(BF16)
        mixed[:, pl.ds(k, 1)] = back.reshape(groups, 1, rows // groups, 256)
        store_mixed(k).start()
        return carry

    spread.pass_on((3,))
    lax.fori_loop(0, groups // 2, attend, 0)
    second.pass_on()
    column.pass_on()
    lax.fori_loop(groups // 2, groups, attend, 0)
    spread.finish((3,))
    second.finish()
    column.finish()
    gather.sent()

    wait_all(stores)

    def stored(turn, carry):
        keep(turn).wait()
        store_kept(turn).wait()
        store_mixed(turn).wait()
        return carry

    lax.fori_loop(0, groups, stored, 0)

    @pl.when(z < members - 1)
    def _():
        def done(k, carry):
            halo(k, z + 1).wait_send()
            return carry

        lax.fori_loop(0, groups, done, 0)


def attend_ahead(
    tokens, cotangent, order_row, gain, notes, query, keys, values, project, gate, scale
):
    rows, width = tokens.shape
    groups, members = lax.axis_size("dp"), lax.axis_size("mp")
    dma = pltpu.SemaphoreType.DMA
    shape = jax.ShapeDtypeStruct
    return pl.pallas_call(
        functools.partial(forward_kernel, scale=scale),
        out_shape=(
            shape((groups, rows, width), BF16),
            shape((6 * LANES, width), BF16),
            shape((2 * LANES, width), BF16),
            shape((groups,) + notes.shape, F32),
            shape((members, width, LANES), BF16),
            shape((groups, groups, rows // groups, 256), BF16),
            shape((groups, rows + 64, 768), BF16),
            shape((rows, width), BF16),
            shape((rows, width), BF16),
            shape((groups, rows, width), BF16),
        ),
        in_specs=[on_chip()] * 5 + [anywhere()] * 5,
        out_specs=(
            anywhere(), anywhere(), on_chip(), on_chip(), anywhere(),
            anywhere(), anywhere(), anywhere(), anywhere(), anywhere(),
        ),
        scratch_shapes=[
            pltpu.VMEM((groups, rows, width), BF16),
            pltpu.VMEM((groups, groups, rows // groups, 768), BF16),
            pltpu.VMEM((4, HEAD_DIM, width), BF16),
            pltpu.VMEM((width, LANES), BF16),
            pltpu.VMEM((6 * LANES, width), BF16),
            pltpu.VMEM((groups, groups, rows // groups, 256), BF16),
            pltpu.VMEM((groups, rows + 64, 768), BF16),
            pltpu.VMEM((rows, width), BF16),
            pltpu.VMEM((rows, width), BF16),
            dma((groups,)),
            dma((groups,)),
            dma((13,)),
            dma((13,)),
            dma((13,)),
            dma((13,)),
            dma((12,)),
            dma((8,)),
            dma((7,)),
            dma((7,)),
            dma((4,)),
            dma((4,)),
            dma((6,)),
            dma((groups,)),
            dma((3 + 2 * groups,)),
        ],
        compiler_params=remote_params(2, 60 * 1024 * 1024),
        cost_estimate=pl.CostEstimate(flops=0, bytes_accessed=300_000_000, transcendentals=0),
        name="attend_ahead",
    )(tokens, cotangent, order_row, gain, notes, query, keys, values, project, gate)


CHUNK = 32


def each_chunk(rows, body, chunk=CHUNK):
    def step(i, carry):
        body(pl.ds(pl.multiple_of(i * chunk, chunk), chunk))
        return carry

    lax.fori_loop(0, rows // chunk, step, 0)


class Reduce:
    COUNT = 10

    def __init__(self, left, right, across, part, from_side, from_corner, from_near, send, recv):
        self.left, self.right, self.across, self.part = left, right, across, part
        self.from_side, self.from_corner, self.from_near = from_side, from_corner, from_near
        self.send, self.recv = send, recv
        self.rows = part.shape[1]

    def product(self, owner, slot):
        rows, width = self.rows, self.part.shape[2]
        picked = pl.ds(pl.multiple_of(owner * rows, rows), rows)

        def tile(t, carry):
            columns = pl.ds(pl.multiple_of(t * 256, 256), 256)
            if self.across:
                value = lax.dot_general(
                    self.left[picked, :], self.right[columns, :], NT, preferred_element_type=F32
                )
            else:
                value = jnp.dot(
                    self.left[picked, :], self.right[:, columns], preferred_element_type=F32
                )
            self.part[slot, :, columns] = value.astype(BF16)
            return carry

        lax.fori_loop(0, width // 256, tile, 0)

    def prepare(self):
        _, side, over_x, over_y, corner = plane()
        part, near = self.part, self.from_near
        half = self.rows // 2
        low, high = pl.ds(0, half), pl.ds(half, half)

        def hop(number, source, target, index):
            return to_dp(source, target, self.send.at[number], self.recv.at[number], index)

        self.shares = [hop(i, part.at[4 + i], self.from_side.at[i], side) for i in range(4)]
        self.corners = [
            hop(4, part.at[0, low], self.from_corner.at[0], over_x),
            hop(5, part.at[0, high], self.from_corner.at[1], over_y),
        ]
        self.nears = [
            hop(6, part.at[1, low], near.at[0, low], over_x),
            hop(7, part.at[1, high], near.at[0, high], over_x),
            hop(8, part.at[2, high], near.at[1, high], over_y),
            hop(9, part.at[2, low], near.at[1, low], over_y),
        ]

    def add_side(self, slot):
        self.shares[slot].wait_recv()

        def body(span):
            self.part[slot, span, :] = (
                self.part[slot, span, :].astype(F32) + self.from_side[slot, span, :].astype(F32)
            ).astype(BF16)

        each_chunk(self.rows, body)

    def add_corner(self, slot, offset, which):
        self.corners[which].wait_recv()

        def body(span):
            target = pl.ds(pl.multiple_of(offset + span.start, CHUNK), CHUNK)
            self.part[slot, target, :] = (
                self.part[slot, target, :].astype(F32)
                + self.from_corner[which, span, :].astype(F32)
            ).astype(BF16)

        each_chunk(self.rows // 2, body)

    def products(self):
        self.prepare()
        me, _, over_x, over_y, corner = plane()
        turn = 1 - 2 * lax.rem(me, 2)
        for slot, owner in enumerate((corner, over_x, over_y, me)):
            self.product(owner + turn, 4 + slot)
            self.shares[slot].start()
        for slot, owner in enumerate((corner, over_x, over_y, me)):
            self.product(owner, slot)

    def launch(self):
        self.add_side(0)
        self.corners[0].start()
        self.corners[1].start()
        self.add_side(1)
        self.nears[0].start()
        self.add_side(2)
        self.nears[2].start()

    def begin(self):
        self.prepare()
        me, _, over_x, over_y, corner = plane()
        turn = 1 - 2 * lax.rem(me, 2)
        self.product(corner + turn, 4)
        self.shares[0].start()
        self.product(corner, 0)
        self.product(over_x + turn, 5)
        self.shares[1].start()
        self.add_side(0)
        self.corners[0].start()
        self.corners[1].start()
        self.product(over_x, 1)
        self.product(over_y + turn, 6)
        self.shares[2].start()
        self.add_side(1)
        self.nears[0].start()
        self.product(over_y, 2)
        self.product(me + turn, 7)
        self.shares[3].start()
        self.add_side(2)
        self.nears[2].start()
        self.product(me, 3)

    def middle(self):
        self.add_corner(2, 0, 0)
        self.nears[3].start()
        self.add_corner(1, self.rows // 2, 1)
        self.nears[1].start()

    def end(self):
        self.shares[3].wait_recv()
        for copy in self.nears:
            copy.wait_recv()

    def run(self):
        self.begin()
        self.middle()
        self.end()

    def rows_of(self, span):
        return (
            self.part[3, span, :].astype(F32)
            + self.from_side[3, span, :].astype(F32)
            + self.from_near[0, span, :].astype(F32)
            + self.from_near[1, span, :].astype(F32)
        )

    def finish(self):
        for copy in self.shares + self.corners + self.nears:
            copy.wait_send()


def reduce_scratch(rows, width):
    dma = pltpu.SemaphoreType.DMA
    return [
        pltpu.VMEM((8, rows, width), BF16),
        pltpu.VMEM((4, rows, width), BF16),
        pltpu.VMEM((2, rows // 2, width), BF16),
        pltpu.VMEM((2, rows, width), BF16),
        dma((10,)),
        dma((10,)),
    ]


def gather_scratch(rows, width):
    dma = pltpu.SemaphoreType.DMA
    return [pltpu.VMEM((rows, width), BF16), dma((13,)), dma((13,)), dma(())]


def mean_rows(values):
    return jnp.mean(values, axis=-1, keepdims=True)


class Heads:
    def __init__(self, source, stage, arrive, send, recv_stage, recv):
        me, z = lax.axis_index("dp"), lax.axis_index("mp")
        self.me, self.z = me, z
        self.core = lax.rem(me, 2)
        self.source, self.stage, self.arrive = source, stage, arrive
        self.send, self.recv_stage, self.recv = send, recv_stage, recv
        self.place = z + self.core * (3 - 2 * z)
        self.columns = source.shape[1] // 2

    def z_of(self, place):
        return place + self.core * (3 - 2 * place)

    def slot_of(self, place):
        return self.core if place == 0 else 1 - self.core

    def rows_of(self, place, kind):
        block = 2 * kind + self.slot_of(place)
        return self.source.at[pl.ds(pl.multiple_of(block * LANES, LANES), HEAD_DIM)]

    def half_of(self, ref, half):
        return ref.at[:, pl.ds(pl.multiple_of(half * self.columns, LANES), self.columns)]

    def to_stage(self, place, kind):
        return to_at(
            self.rows_of(place, kind),
            self.stage.at[place, kind],
            self.send.at[place * 4 + kind],
            self.recv_stage.at[place * 4 + kind],
            self.me,
            self.z_of(2),
        )

    def to_owner(self, place, kind, half, way, ref, number):
        return to_at(
            self.half_of(ref, half),
            self.arrive.at[way, kind],
            self.send.at[number],
            self.recv.at[way * 4 + kind],
            self.me - self.core + half,
            self.z_of(place),
        )

    def sums(self, kind):
        return [
            self.to_owner(
                place, kind, half, 2, self.stage.at[place, kind], place * 8 + kind * 2 + half
            )
            for place in (0, 1)
            for half in (0, 1)
        ]

    def cross(self, own, kind):
        other = 1 - own
        copies = [
            self.to_owner(other, kind, half, 0, self.rows_of(other, kind), kind * 2 + half)
            for half in (0, 1)
        ]
        copies.append(
            to_at(
                self.half_of(self.rows_of(own, kind), 1 - self.core),
                self.arrive.at[1, kind],
                self.send.at[8 + kind],
                self.recv.at[4 + kind],
                self.me + 1 - 2 * self.core,
                self.z,
            )
        )
        return copies

    def start(self, kinds):
        @pl.when(self.place == 3)
        def _():
            for kind in kinds:
                self.to_stage(0, kind).start()
                self.to_stage(1, kind).start()

        for own in (0, 1):
            @pl.when(self.place == own)
            def _():
                for kind in kinds:
                    for copy in self.cross(own, kind):
                        copy.start()

    def add(self, kinds):
        @pl.when(self.place == 2)
        def _():
            for kind in kinds:
                for place in (0, 1):
                    self.to_stage(place, kind).wait_recv()
                    mine = self.rows_of(place, kind)

                    def body(span):
                        self.stage[place, kind, span, :] = (
                            self.stage[place, kind, span, :].astype(F32)
                            + mine[span, :].astype(F32)
                        ).astype(BF16)

                    each_chunk(HEAD_DIM, body, 16)
                for copy in self.sums(kind):
                    copy.start()

    def total(self, out):
        owner = lax.div(self.z, 2) == self.core
        for kind in range(4):
            for own in (0, 1):
                @pl.when(self.place == own)
                def _():
                    self.arrive[1, kind] = self.half_of(self.rows_of(own, kind), self.core)[...]

            for way in range(3):
                waiting = to_at(
                    self.half_of(self.rows_of(0, kind), 0),
                    self.arrive.at[way, kind],
                    self.send.at[0],
                    self.recv.at[way * 4 + kind],
                    self.me,
                    lax.rem(self.z + 1, 4),
                )
                if way == 1:
                    pl.when(jnp.logical_not(owner))(waiting.wait_recv)
                else:
                    waiting.wait_recv()

            def body(span):
                found = self.arrive[0, kind, span, :].astype(F32)
                found = found + self.arrive[1, kind, span, :].astype(F32)
                found = found + self.arrive[2, kind, span, :].astype(F32)
                target = pl.ds(pl.multiple_of(kind * HEAD_DIM + span.start, 16), 16)
                out[target, :] = found.astype(BF16)

            each_chunk(HEAD_DIM, body, 16)

    def finish_send(self):
        for kind in range(4):
            @pl.when(self.place == 3)
            def _():
                self.to_stage(0, kind).wait_send()
                self.to_stage(1, kind).wait_send()

            @pl.when(self.place == 2)
            def _():
                for copy in self.sums(kind):
                    copy.wait_send()

            for own in (0, 1):
                @pl.when(self.place == own)
                def _():
                    for copy in self.cross(own, kind):
                        copy.wait_send()


def to_at(source, target, send_sem, recv_sem, dp, mp):
    return pltpu.make_async_remote_copy(
        src_ref=source,
        dst_ref=target,
        send_sem=send_sem,
        recv_sem=recv_sem,
        device_id={"dp": dp, "mp": mp},
        device_id_type=MESH,
    )


class Units:
    def __init__(self, both_sum, both_in, both_stage, send, recv, local):
        self.z = lax.axis_index("mp")
        self.sums = (both_sum,)
        self.inputs = (both_in,)
        self.stages = (both_stage,)
        self.send, self.recv, self.local = send, recv, local
        z = self.z
        self.outer = (z == 0) | (z == 3)
        self.far = 3 - z
        self.near = 1 + lax.div(z, 3)
        self.second = 3 - self.near
        self.edge = 3 * (z - 1)

    def part(self, kind, z):
        return self.sums[kind].at[z]

    def straight(self, kind, number, target):
        return to_mp(
            self.part(kind, target),
            self.inputs[kind].at[self.z],
            self.send.at[number * 2 + kind],
            self.recv.at[self.z * 2 + kind],
            target,
        )

    def staged(self, kind):
        return to_mp(
            self.part(kind, self.far),
            self.stages[kind].at[0],
            self.send.at[4 + kind],
            self.recv.at[8 + kind],
            self.near,
        )

    def summed(self, kind):
        return to_mp(
            self.stages[kind].at[1],
            self.inputs[kind].at[self.z],
            self.send.at[4 + kind],
            self.recv.at[self.z * 2 + kind],
            3 - self.edge,
        )

    def mine(self, kind):
        return pltpu.make_async_copy(
            self.part(kind, 3 - self.edge), self.stages[kind].at[1], self.local.at[kind]
        )

    def start(self):
        @pl.when(self.outer)
        def _():
            for kind in range(1):
                self.staged(kind).start()
            for kind in range(1):
                self.straight(kind, 0, self.near).start()
                self.straight(kind, 1, self.second).start()

        @pl.when(jnp.logical_not(self.outer))
        def _():
            for kind in range(1):
                self.mine(kind).start()
                self.straight(kind, 0, 3 - self.z).start()
                self.straight(kind, 1, self.edge).start()

    def add(self):
        @pl.when(jnp.logical_not(self.outer))
        def _():
            for kind in range(1):
                stage = self.stages[kind]
                self.mine(kind).wait()
                to_mp(
                    self.part(kind, 0),
                    stage.at[0],
                    self.send.at[4 + kind],
                    self.recv.at[8 + kind],
                    self.edge,
                ).wait_recv()

                def body(span):
                    stage[1, span, :] = (
                        stage[0, span, :].astype(F32) + stage[1, span, :].astype(F32)
                    ).astype(BF16)

                each_chunk(stage.shape[1], body)
                self.summed(kind).start()

    def arrived(self, kind, source):
        to_mp(
            self.part(kind, 0),
            self.inputs[kind].at[source],
            self.send.at[kind],
            self.recv.at[source * 2 + kind],
            source,
        ).wait_recv()

    def finish(self):
        @pl.when(self.outer)
        def _():
            for kind in range(1):
                self.arrived(kind, 1)
                self.arrived(kind, 2)
                self.straight(kind, 0, self.near).wait_send()
                self.straight(kind, 1, self.second).wait_send()
                self.staged(kind).wait_send()

        @pl.when(jnp.logical_not(self.outer))
        def _():
            for kind in range(1):
                self.arrived(kind, 0)
                self.arrived(kind, 3)
                self.arrived(kind, 3 - self.z)
                self.straight(kind, 0, 3 - self.z).wait_send()
                self.straight(kind, 1, self.edge).wait_send()
                self.summed(kind).wait_send()


def backward_kernel(
    branch, notes_all, kept_in, w_out_in, activated_in, w_down_in, middle_in, both_sum, down_in,
    out, result, branch_all, both_in, down_all,
    totals, query_part, key_value, ending, leaving, arriving, send, recv,
    part, from_side, from_corner, from_near, send_r, recv_r,
    mixed_grad, shard, load_sem, send_g, recv_g,
    both_stage, send_u, recv_u, local, down_found, send_d, recv_d,
    kept, w_out, activated, w_down, middle, fetch_sem,
    *, scale, groups, rows,
):
    z = lax.axis_index("mp")
    members = lax.axis_size("mp")
    barrier = greet_all()
    pairs = ((w_down_in, w_down), (activated_in, activated), (w_out_in, w_out))
    pairs += ((kept_in, kept), (middle_in, middle))
    fetches = [
        pltpu.make_async_copy(source, target, fetch_sem.at[number])
        for number, (source, target) in enumerate(pairs)
    ]
    load_down = pltpu.make_async_copy(down_in, down_found, load_sem.at[2])
    pl.semaphore_wait(barrier, 13)
    units = Units(both_sum, both_in, both_stage, send_u, recv_u, local)
    gather = Gather(branch, branch_all, send_g, recv_g, local.at[2])
    gather.start()
    units.start()
    start_all(fetches)
    load_down.start()
    wait_all(fetches[:2])
    reduce = Reduce(activated, w_down, False, part, from_side, from_corner, from_near, send_r, recv_r)
    reduce.products()
    load_down.wait()

    def add_down(span):
        value = down_found[0, span, :].astype(F32) + down_found[1, span, :].astype(F32)
        value = value + down_found[2, span, :].astype(F32) + down_found[3, span, :].astype(F32)
        down_found[0, span, :] = value.astype(BF16)

    each_chunk(down_found.shape[1], add_down)
    down = Gather(down_found.at[0], down_all, send_d, recv_d, local.at[1])

    def load_shard(turn):
        slot = turn % 2
        return pltpu.make_async_copy(branch_all.at[owner_at(turn)], shard.at[slot], load_sem.at[slot])

    def spread_back(turn, carry):
        for number, numbers in ARRIVALS:
            pl.when(turn == number)(functools.partial(gather.arrive, *numbers))

        @pl.when(turn == 0)
        def _():
            gather.keep.wait()

        load_shard(turn).start()
        load_shard(turn).wait()
        mixed_grad[owner_at(turn)] = (
            lax.dot_general(shard[turn % 2], w_out[...], NT, preferred_element_type=F32)
            .astype(BF16)
            .reshape(groups, rows // groups, 256)
        )
        return carry

    fetches[2].wait()
    lax.fori_loop(0, 8, spread_back, 0)
    reduce.launch()
    down.start()
    units.add()


    def halo(k, other):
        return to_mp(leaving.at[k], arriving.at[k], send.at[k], recv.at[k], other)

    def attend(k, carry):
        hot = hot_of(notes_all, k, rows)
        given = mixed_grad[:, pl.ds(k, 1)].reshape(rows, 256)
        grad_ordered = lax.dot_general(hot, given, TN, preferred_element_type=F32).astype(BF16)
        totals[...] = jnp.zeros_like(totals)
        for block in range(rows // 128):
            allowed = block_mask(notes_all, k, block, z, rows)
            for head in range(2):
                query = kept[k, pl.ds(64 + block * 128, 128), pl.ds(head * 128, 128)]
                keys = kept[k, pl.ds(block * 128, 192), pl.ds(256 + head * 128, 128)]
                values = kept[k, pl.ds(block * 128, 192), pl.ds(512 + head * 128, 128)]
                grad = grad_ordered[block * 128 : block * 128 + 128, head * 128 : head * 128 + 128]
                scores = lax.dot_general(query, keys, NT, preferred_element_type=F32) * scale
                scores = jnp.where(allowed, scores, -MASKED)
                weights = jnp.exp(scores - jnp.max(scores, axis=-1, keepdims=True))
                again = weights / jnp.sum(weights, axis=-1, keepdims=True)
                chance_grad = lax.dot_general(grad, values, NT, preferred_element_type=F32)
                row_dot = jnp.sum(again * chance_grad, axis=-1, keepdims=True)
                score_grad = (again * (chance_grad - row_dot)).astype(BF16)
                query_part[k, pl.ds(block * 128, 128), pl.ds(head * 128, 128)] = (
                    jnp.dot(score_grad, keys, preferred_element_type=F32) * scale
                ).astype(BF16)
                totals[pl.ds(block * 128, 192), pl.ds(head * 128, 128)] += (
                    lax.dot_general(score_grad, query, TN, preferred_element_type=F32) * scale
                )
                totals[pl.ds(block * 128, 192), pl.ds(256 + head * 128, 128)] += lax.dot_general(
                    again.astype(BF16), grad, TN, preferred_element_type=F32
                )
        key_value[k] = totals[pl.ds(64, rows), :].astype(BF16)
        ending[k] = totals[pl.ds(rows, 64), :]

        @pl.when(z > 0)
        def _():
            leaving[k] = totals[pl.ds(0, 64), :].astype(BF16)
            halo(k, z - 1).start()

        return carry

    wait_all(fetches[3:])
    lax.fori_loop(0, 3, attend, 0)
    reduce.middle()
    lax.fori_loop(3, 7, attend, 0)
    down.pass_on()
    lax.fori_loop(7, groups, attend, 0)

    def restore(k, carry):
        @pl.when(z < members - 1)
        def _():
            halo(k, z).wait_recv()
            key_value[k, pl.ds(rows - 64, 64), :] = (
                ending[k] + arriving[k].astype(F32)
            ).astype(BF16)

        hot = hot_of(notes_all, k, rows)
        ordered = jnp.concatenate([query_part[k], key_value[k]], axis=1)
        back = jnp.dot(hot, ordered, preferred_element_type=F32).astype(BF16)
        out[:, pl.ds(k, 1)] = back.reshape(groups, 1, rows // groups, 768)
        return carry

    lax.fori_loop(0, groups, restore, 0)
    reduce.end()

    def body(span):
        result[span, :] = (middle[span, :] + reduce.rows_of(span)).astype(BF16)

    each_chunk(rows, body)
    down.finish()
    units.finish()
    for copy in gather.copies:
        copy.wait_send()
    reduce.finish()

    @pl.when(z > 0)
    def _():
        def done(k, carry):
            halo(k, z - 1).wait_send()
            return carry

        lax.fori_loop(0, groups, done, 0)


def attend_back(
    branch, notes_all, kept, w_out, activated, w_down, middle, both_sum, down_in, scale
):
    groups = kept.shape[0]
    rows, width = middle.shape
    members = both_sum.shape[0]
    dma = pltpu.SemaphoreType.DMA
    shape = jax.ShapeDtypeStruct
    return pl.pallas_call(
        functools.partial(backward_kernel, scale=scale, groups=groups, rows=rows),
        out_shape=(
            shape((groups, groups, rows // groups, 768), BF16),
            shape((rows, width), BF16),
            shape((groups, rows, width), BF16),
            shape((members, width, 256), BF16),
            shape((groups, LANES, width), BF16),
        ),
        in_specs=[on_chip()] * 2 + [anywhere()] * 7,
        out_specs=(on_chip(),) * 2 + (anywhere(),) * 3,
        scratch_shapes=[
            pltpu.VMEM((rows + 64, 512), F32),
            pltpu.VMEM((groups, rows, 256), BF16),
            pltpu.VMEM((groups, rows, 512), BF16),
            pltpu.VMEM((groups, 64, 512), F32),
            pltpu.VMEM((groups, 64, 512), BF16),
            pltpu.VMEM((groups, 64, 512), BF16),
            dma((groups,)),
            dma((groups,)),
        ]
        + reduce_scratch(rows, width)
        + [
            pltpu.VMEM((groups, groups, rows // groups, 256), BF16),
            pltpu.VMEM((2, rows, width), BF16),
            dma((3,)),
            dma((13,)),
            dma((13,)),
            pltpu.VMEM((2, width, 256), BF16),
            dma((6,)),
            dma((10,)),
            dma((3,)),
            pltpu.VMEM((members, LANES, width), BF16),
            dma((13,)),
            dma((13,)),
            pltpu.VMEM(kept.shape, BF16),
            pltpu.VMEM(w_out.shape, BF16),
            pltpu.VMEM(activated.shape, BF16),
            pltpu.VMEM(w_down.shape, BF16),
            pltpu.VMEM((rows, width), F32),
            dma((5,)),
        ],
        compiler_params=remote_params(3, 63 * 1024 * 1024),
        cost_estimate=pl.CostEstimate(flops=0, bytes_accessed=300_000_000, transcendentals=0),
        name="attend_back",
    )(branch, notes_all, kept, w_out, activated, w_down, middle, both_sum, down_in)


def middle_kernel(
    mixed, w_out, tokens, gain, w_up, w_down, middle, hidden, up_all, down_all,
    part, from_side, from_corner, from_near, send, recv, up_own, down_own,
    send_u, recv_u, send_d, recv_d, local,
):
    barrier = greet_all()
    units = pl.ds(pl.multiple_of(lax.axis_index("dp") * LANES, LANES), LANES)
    loads = [
        pltpu.make_async_copy(w_up.at[:, units], up_own, local.at[0]),
        pltpu.make_async_copy(w_down.at[units], down_own, local.at[1]),
    ]
    for copy in loads:
        copy.start()
    pl.semaphore_wait(barrier, 13)
    for copy in loads:
        copy.wait()
    columns = [
        Column(up_own, up_all, send_u, recv_u, local.at[0]),
        Column(down_own, down_all, send_d, recv_d, local.at[1]),
    ]
    for column in columns:
        column.start()
    reduce = Reduce(mixed, w_out, False, part, from_side, from_corner, from_near, send, recv)
    reduce.begin()
    reduce.middle()
    for column in columns:
        column.pass_on()
    reduce.end()

    def body(span):
        values = tokens[span, :].astype(F32) + reduce.rows_of(span)
        middle[span, :] = values
        inverse = lax.rsqrt(mean_rows(values * values) + EPSILON)
        hidden[span, :] = (values * inverse * gain[...]).astype(BF16)

    each_chunk(hidden.shape[0], body)
    for column in columns:
        column.finish()
    reduce.finish()


def project_middle(mixed, w_out, tokens, gain, w_up, w_down):
    rows, width = tokens.shape
    dma = pltpu.SemaphoreType.DMA
    members = lax.axis_size("mp")
    return pl.pallas_call(
        middle_kernel,
        out_shape=(
            jax.ShapeDtypeStruct((rows, width), F32),
            jax.ShapeDtypeStruct((rows, width), BF16),
            jax.ShapeDtypeStruct((members, width, LANES), BF16),
            jax.ShapeDtypeStruct((members, LANES, width), BF16),
        ),
        in_specs=[on_chip()] * 4 + [anywhere()] * 2,
        out_specs=(on_chip(), on_chip(), anywhere(), anywhere()),
        scratch_shapes=reduce_scratch(rows, width)
        + [
            pltpu.VMEM((width, LANES), BF16),
            pltpu.VMEM((LANES, width), BF16),
            dma((4,)),
            dma((4,)),
            dma((4,)),
            dma((4,)),
            dma((2,)),
        ],
        compiler_params=remote_params(4),
        cost_estimate=pl.CostEstimate(flops=0, bytes_accessed=150_000_000, transcendentals=0),
        name="project_middle",
    )(mixed, w_out, tokens, gain, w_up, w_down)


def norm_back_rows(gradient, values, gain, sums, span):
    inverse = lax.rsqrt(mean_rows(values * values) + EPSILON)
    normed = values * inverse
    product = gradient * normed
    folded = product[0:8]
    for step in range(1, CHUNK // 8):
        folded = folded + product[step * 8 : step * 8 + 8]
    sums[...] += folded
    scaled = gradient * gain
    return inverse * (scaled - normed * mean_rows(scaled * normed))


def feed_kernel(
    hidden_own, cotangent_all, middle, gate_all, up_all, cotangent_own, down_all, gain,
    middle_grad, branch, sums, activated_out, both_sum, down_in,
    hidden_all, both_grad, part, from_side, from_corner, from_near, send_r, recv_r,
    send_a, recv_a, cot_shard, cot_tile, stage_both, down_sum, w_both, w_down, cotangent, activated,
    load_sem, local, send_z, recv_z,
):
    groups, rows, width = hidden_all.shape
    members = gate_all.shape[0]
    me = lax.axis_index("dp")
    barrier = greet_all()
    own = pltpu.make_async_copy(hidden_own, hidden_all.at[me], local.at[0])
    own.start()
    start_middle = pltpu.make_async_copy(middle, middle_grad, local.at[1])
    loads = [
        pltpu.make_async_copy(
            source.at[z], w_both.at[:, pl.ds(z * 256 + offset, 128)], load_sem.at[6 + 2 * z + number]
        )
        for z in range(members)
        for number, (source, offset) in enumerate(((gate_all, 0), (up_all, 128)))
    ]

    def slot_of(turn):
        block = turn // 2
        near = ((block + 1) // 2) % 2
        far = block // 3
        second = turn % 2
        other = (1 - near) * second + (block // 2) * near
        return 4 * other + 3 * (1 - near) * (1 - far) + near * (1 + second)

    def load_cotangent(turn):
        return pltpu.make_async_copy(
            cotangent_all.at[owner_at(turn)], cot_shard.at[turn % 2], load_sem.at[turn % 2]
        )

    loads.append(pltpu.make_async_copy(down_all, w_down, local.at[2]))
    load_own = pltpu.make_async_copy(cotangent_own, cotangent, local.at[3])
    start_all(loads)
    load_cotangent(0).start()
    own.wait()
    pl.semaphore_wait(barrier, 13)
    gather = Gather(None, hidden_all, send_a, recv_a)
    gather.start()
    reduce = Reduce(None, None, False, part, from_side, from_corner, from_near, send_r, recv_r)
    reduce.prepare()

    def nears():
        reduce.add_side(1)
        reduce.nears[0].start()
        reduce.add_side(2)
        reduce.nears[2].start()

    early = [(turn, functools.partial(gather.arrive, *numbers)) for turn, numbers in ARRIVALS]
    early += [(6, nears)]
    late = [(1, 3), (4, 1), (5, 2), (7, 0)]
    start_middle.start()
    load_own.start()
    wait_all(loads)

    def unit(turn, carry):
        for number, action in early:
            pl.when(turn == number)(action)

        @pl.when(turn < 7)
        def _():
            load_cotangent(turn + 1).start()

        load_cotangent(turn).wait()
        owner, slot = owner_at(turn), slot_of(turn)
        mine = hidden_all[owner]
        grads = cot_shard[turn % 2]
        for z in range(members):
            raw = jnp.dot(mine, w_both[:, z * 256 : z * 256 + 256], preferred_element_type=F32)
            units = pl.ds(z * 128, 128)
            if z % 2 == 0:
                pair = lax.dot_general(
                    grads, w_down[pl.ds(z * 128, 256), :], NT, preferred_element_type=F32
                )
            active_grad = pair[:, 128 * (z % 2) : 128 * (z % 2) + 128]
            gate, upward = raw[:, :128], raw[:, 128:]
            sigmoid = jax.nn.sigmoid(gate)
            activated[owner, :, units] = (gate * sigmoid * upward).astype(BF16)
            both_grad[owner, :, pl.ds(z * 256, 128)] = (
                active_grad * upward * sigmoid * (1.0 + gate * (1.0 - sigmoid))
            ).astype(BF16)
            both_grad[owner, :, pl.ds(z * 256 + 128, 128)] = (
                active_grad * gate * sigmoid
            ).astype(BF16)

        def tile(t, inner):
            columns = pl.ds(pl.multiple_of(t * 256, 256), 256)
            part[slot, :, columns] = lax.dot_general(
                both_grad[owner], w_both[columns, :], NT, preferred_element_type=F32
            ).astype(BF16)
            return inner

        lax.fori_loop(0, width // 256, tile, 0)
        for number, share in late:
            pl.when(turn == number)(reduce.shares[share].start)
        return carry

    lax.fori_loop(0, 8, unit, 0)
    store_activated = pltpu.make_async_copy(activated, activated_out, local.at[4])
    store_activated.start()

    def load_tile(t):
        columns = pl.ds(pl.multiple_of(t * 256, 256), 256)
        return pltpu.make_async_copy(
            cotangent_all.at[:, :, columns], cot_tile.at[t % 2], load_sem.at[2 + t % 2]
        )

    def store_both(t):
        columns = pl.ds(pl.multiple_of(t * 256, 256), 256)
        return pltpu.make_async_copy(
            stage_both.at[t % 2], both_sum.at[:, columns], load_sem.at[4 + t % 2]
        )

    tiles = width // 256
    count = groups * rows

    def down_tile(t, carry):
        columns = pl.ds(pl.multiple_of(t * 256, 256), 256)

        @pl.when(t < tiles - 1)
        def _():
            load_tile(t + 1).start()

        load_tile(t).wait()
        down_sum[:, columns] = lax.dot_general(
            activated[...].reshape(count, members * 128),
            cot_tile[t % 2].reshape(count, 256),
            TN,
            preferred_element_type=F32,
        ).astype(BF16)
        return carry

    z = lax.axis_index("mp")

    def down_rows(owner):
        return down_sum.at[pl.ds(pl.multiple_of(owner * LANES, LANES), LANES)]

    keep_down = pltpu.make_async_copy(down_rows(z), down_in.at[z], local.at[5])
    pass_down = [
        to_mp(
            down_rows(lax.rem(z + step, members)),
            down_in.at[z],
            send_z.at[step - 1],
            recv_z.at[step - 1],
            lax.rem(z + step, members),
        )
        for step in range(1, members)
    ]

    def weight_tile(t, carry):
        columns = pl.ds(pl.multiple_of(t * 256, 256), 256)

        @pl.when(t >= 2)
        def _():
            store_both(t - 2).wait()

        value = lax.dot_general(
            hidden_all[:, :, columns].reshape(count, 256),
            both_grad[...].reshape(count, members * 256),
            TN,
            preferred_element_type=F32,
        )
        for z in range(members):
            stage_both[t % 2, z] = value[:, z * 256 : z * 256 + 256].astype(BF16)
        store_both(t).start()
        return carry

    load_tile(0).start()
    reduce.add_side(0)
    reduce.corners[0].start()
    reduce.corners[1].start()
    lax.fori_loop(0, tiles, down_tile, 0)
    keep_down.start()
    for copy in pass_down:
        copy.start()
    lax.fori_loop(0, 2, weight_tile, 0)
    reduce.middle()
    lax.fori_loop(2, tiles, weight_tile, 0)
    reduce.end()
    start_middle.wait()
    load_own.wait()
    sums[...] = jnp.zeros_like(sums)

    def body(span):
        change = norm_back_rows(reduce.rows_of(span), middle_grad[span, :], gain[...], sums, span)
        total = cotangent[span, :].astype(F32) + change
        middle_grad[span, :] = total
        branch[span, :] = total.astype(BF16)

    each_chunk(rows, body)
    gather.sent()
    reduce.finish()
    for t in (tiles - 2, tiles - 1):
        store_both(t).wait()
    keep_down.wait()
    store_activated.wait()
    for copy in pass_down:
        copy.wait()


def feed(hidden_own, cotangent_all, middle, gate_all, up_all, cotangent, down_all, gain):
    groups, rows, width = cotangent_all.shape
    members = gate_all.shape[0]
    dma = pltpu.SemaphoreType.DMA
    units = members * 128
    return pl.pallas_call(
        feed_kernel,
        out_shape=(
            jax.ShapeDtypeStruct((rows, width), F32),
            jax.ShapeDtypeStruct((rows, width), BF16),
            jax.ShapeDtypeStruct((8, width), F32),
            jax.ShapeDtypeStruct((groups, rows, units), BF16),
            jax.ShapeDtypeStruct((members, width, 256), BF16),
            jax.ShapeDtypeStruct((members, LANES, width), BF16),
        ),
        in_specs=[anywhere()] * 7 + [on_chip()],
        out_specs=(on_chip(),) * 3 + (anywhere(),) * 3,
        scratch_shapes=[
            pltpu.VMEM((groups, rows, width), BF16),
            pltpu.VMEM((groups, rows, 2 * units), BF16),
        ]
        + reduce_scratch(rows, width)
        + [
            dma((13,)),
            dma((13,)),
            pltpu.VMEM((2, rows, width), BF16),
            pltpu.VMEM((2, groups, rows, 256), BF16),
            pltpu.VMEM((2, members, 256, 256), BF16),
            pltpu.VMEM((units, width), BF16),
            pltpu.VMEM((width, 2 * units), BF16),
            pltpu.VMEM((units, width), BF16),
            pltpu.VMEM((rows, width), BF16),
            pltpu.VMEM((groups, rows, units), BF16),
            dma((6 + 2 * members,)),
            dma((6,)),
            dma((3,)),
            dma((3,)),
        ],
        compiler_params=remote_params(5, 63 * 1024 * 1024),
        cost_estimate=pl.CostEstimate(flops=0, bytes_accessed=400_000_000, transcendentals=0),
        name="feed",
    )(hidden_own, cotangent_all, middle, gate_all, up_all, cotangent, down_all, gain)


def input_kernel(
    qkv_grad, w_qkv, hidden_all, branch_all, mixed_in, tokens_in, middle_in, gain, sums_two,
    both_sum, both_in,
    result, gains, both_all, heads_all,
    part, from_side, from_corner, from_near, send, recv, sums,
    stage, arrive, send_h, recv_s, recv_h, own, plane_sums, column_sums, send_p, recv_p,
    weight_sum, row_tile, tile_sem, send_b, recv_b, send_t, recv_t, both_found, heads_own, local,
    mixed, tokens, middle_grad, fetch_sem,
):
    me, z = lax.axis_index("dp"), lax.axis_index("mp")
    barrier = greet_all()
    count = qkv_grad.shape[0]
    tiles = tokens.shape[1] // 256
    outer = (z == 0) | (z == 3)

    def columns_of(t):
        return pl.ds(pl.multiple_of(lax.rem(t, tiles) * 256, 256), 256)

    def load(t, source):
        return pltpu.make_async_copy(
            source.at[:, :, columns_of(t)], row_tile.at[t % 2], tile_sem.at[t % 2]
        )

    own_part = pltpu.make_async_copy(both_sum.at[z], both_found.at[0], local.at[0])
    own_part.start()
    ways = [(outer, 1, 1), (outer, 2, 2)]
    ways += [(z == 1, 0, 1), (z == 1, 2, 2), (z == 1, 3, 3)]
    ways += [(z == 2, 0, 1), (z == 2, 1, 2), (z == 2, 3, 3)]

    def came(source, place):
        return pltpu.make_async_copy(both_in.at[source], both_found.at[place], local.at[place])

    for here, source, place in ways:
        pl.when(here)(came(source, place).start)

    @pl.when(outer)
    def _():
        both_found[3] = jnp.zeros_like(both_found[3])

    load(0, hidden_all).start()
    fetches = start_all(
        [
            pltpu.make_async_copy(source, target, fetch_sem.at[number])
            for number, (source, target) in enumerate(
                ((mixed_in, mixed), (tokens_in, tokens), (middle_in, middle_grad))
            )
        ]
    )
    pl.semaphore_wait(barrier, 13)
    both = Gather(both_found.at[0], both_all, send_b, recv_b, local.at[4])

    def weight_tile(t, carry):
        @pl.when(t < tiles - 1)
        def _():
            load(t + 1, hidden_all).start()

        @pl.when((t >= tiles - 1) & (t < 2 * tiles - 1))
        def _():
            load(t + 1, branch_all).start()

        load(t, hidden_all).wait()

        @pl.when(t < tiles)
        def _():
            weight_sum[pl.ds(0, 768), columns_of(t)] = lax.dot_general(
                qkv_grad[...], row_tile[t % 2].reshape(count, 256), TN, preferred_element_type=F32
            ).astype(BF16)

        @pl.when(t >= tiles)
        def _():
            weight_sum[pl.ds(768, 256), columns_of(t)] = lax.dot_general(
                mixed[...], row_tile[t % 2].reshape(count, 256), TN, preferred_element_type=F32
            ).astype(BF16)

        return carry

    heads = Heads(weight_sum, stage, arrive, send_h, recv_s, recv_h)
    reduce = Reduce(qkv_grad, w_qkv, False, part, from_side, from_corner, from_near, send, recv)
    reduce.begin()
    lax.fori_loop(0, tiles, weight_tile, 0)
    heads.start((0, 1, 2))
    reduce.middle()
    own_part.wait()
    for here, source, place in ways:
        pl.when(here)(came(source, place).wait)

    def add(span):
        value = both_found[0, span, :].astype(F32) + both_found[1, span, :].astype(F32)
        value = value + both_found[2, span, :].astype(F32) + both_found[3, span, :].astype(F32)
        both_found[0, span, :] = value.astype(BF16)

    each_chunk(both_found.shape[1], add)
    both.start()
    wait_all(fetches)
    lax.fori_loop(tiles, 2 * tiles, weight_tile, 0)
    heads.start((3,))
    heads.add((0, 1, 2, 3))
    reduce.end()
    sums[...] = jnp.zeros_like(sums)

    def body(span):
        values = tokens[span, :].astype(F32)
        change = norm_back_rows(reduce.rows_of(span), values, gain[...], sums, span)
        result[span, :] = (middle_grad[span, :] + change).astype(BF16)

    each_chunk(result.shape[0], body)
    own[...] = jnp.concatenate(
        [
            jnp.sum(sums[...], axis=0, keepdims=True),
            jnp.sum(sums_two[...], axis=0, keepdims=True),
        ],
        axis=0,
    )
    swaps = swap_all(own, plane_sums, send_p, recv_p)
    for copy in swaps:
        copy.start()
    plane_sums[me] = own[...]
    both.pass_on()
    heads.total(heads_own)
    gather = Gather(heads_own, heads_all, send_t, recv_t, local.at[5])
    gather.start()
    for copy in swaps:
        copy.wait()
    found = plane_sums[0]
    for other in range(1, 8):
        found = found + plane_sums[other]
    column_sums[z] = found
    passes = [
        to_mp(
            column_sums.at[z],
            column_sums.at[z],
            send_p.at[6 + step],
            recv_p.at[6 + step],
            lax.rem(z + step, 4),
        )
        for step in range(1, 4)
    ]
    for copy in passes:
        copy.start()
    both.finish()
    for copy in passes:
        copy.wait()
    gains[...] = (column_sums[0] + column_sums[1]) + (column_sums[2] + column_sums[3])
    gather.pass_on()
    heads.finish_send()
    reduce.finish()
    gather.finish()


def project_input(
    qkv_grad, w_qkv, hidden_all, branch_all, mixed, tokens, middle_grad, gain, sums_two,
    both_sum, both_in,
):
    rows, width = tokens.shape
    groups = hidden_all.shape[0]
    dma = pltpu.SemaphoreType.DMA
    shape = jax.ShapeDtypeStruct
    return pl.pallas_call(
        input_kernel,
        out_shape=(
            shape((rows, width), BF16),
            shape((2, width), F32),
            shape((groups, width, 256), BF16),
            shape((groups, 4 * HEAD_DIM, width // 2), BF16),
        ),
        in_specs=[on_chip()] * 2 + [anywhere()] * 5 + [on_chip()] * 2 + [anywhere()] * 2,
        out_specs=(on_chip(),) * 2 + (anywhere(),) * 2,
        scratch_shapes=reduce_scratch(rows, width)
        + [
            pltpu.VMEM((8, width), F32),
            pltpu.VMEM((2, 4, HEAD_DIM, width), BF16),
            pltpu.VMEM((3, 4, HEAD_DIM, width // 2), BF16),
            dma((16,)),
            dma((8,)),
            dma((12,)),
            pltpu.VMEM((2, width), F32),
            pltpu.VMEM((8, 2, width), F32),
            pltpu.VMEM((4, 2, width), F32),
            dma((10,)),
            dma((10,)),
            pltpu.VMEM((8 * LANES, width), BF16),
            pltpu.VMEM((2, groups, rows, 256), BF16),
            dma((2,)),
            dma((13,)),
            dma((13,)),
            dma((13,)),
            dma((13,)),
            pltpu.VMEM((4, width, 256), BF16),
            pltpu.VMEM((4 * HEAD_DIM, width // 2), BF16),
            dma((6,)),
            pltpu.VMEM(mixed.shape, BF16),
            pltpu.VMEM((rows, width), BF16),
            pltpu.VMEM((rows, width), F32),
            dma((3,)),
        ],
        compiler_params=remote_params(6, 63 * 1024 * 1024),
        cost_estimate=pl.CostEstimate(flops=0, bytes_accessed=250_000_000, transcendentals=0),
        name="project_input",
    )(
        qkv_grad, w_qkv, hidden_all, branch_all, mixed, tokens, middle_grad, gain, sums_two,
        both_sum, both_in,
    )


def assemble_kernel(
    both, down, heads, order_column, output_b, input_b,
    output, inputs, query, keys, values, project, gate, upward, down_out,
):
    for d in range(both.shape[0]):
        gate[:, d * 128 : d * 128 + 128] = both[d, :, :128].astype(F32)
        upward[:, d * 128 : d * 128 + 128] = both[d, :, 128:].astype(F32)
    down_out[...] = down[0].astype(F32)
    for kind, out in enumerate((query, keys, values, project)):
        out[...] = heads[0, kind].astype(F32)
    place = lax.broadcasted_iota(jnp.int32, (order_column.shape[0], output_b.shape[0]), 1)
    unsort = (place.astype(F32) == order_column[...]).astype(BF16)
    output[...] = jnp.dot(unsort, output_b[...], preferred_element_type=F32).astype(BF16)
    inputs[...] = jnp.dot(unsort, input_b[...], preferred_element_type=F32).astype(BF16)


def assemble(both, down, heads, order_column, output_b, input_b):
    groups, width, wide = both.shape
    rows = output_b.shape[0]
    units = down.shape[1]
    chips = groups // 2
    columns = heads.shape[3]
    row_tile, tile = rows // groups, width // groups
    shape = jax.ShapeDtypeStruct
    head = shape((chips * HEAD_DIM, 2 * columns), F32)
    head_spec = pl.BlockSpec((HEAD_DIM, columns), lambda i: (i // 2, i % 2))
    wide_spec = pl.BlockSpec((tile, groups * units), lambda i: (i, 0))
    row_spec = pl.BlockSpec((row_tile, width), lambda i: (i, 0))
    whole_spec = pl.BlockSpec((rows, width), lambda i: (0, 0))
    return pl.pallas_call(
        assemble_kernel,
        grid=(groups,),
        out_shape=(
            shape((rows, width), BF16),
            shape((rows, width), BF16),
            head,
            head,
            head,
            head,
            shape((width, groups * units), F32),
            shape((width, groups * units), F32),
            shape((groups * units, width), F32),
        ),
        in_specs=[
            pl.BlockSpec((groups, tile, wide), lambda i: (0, i, 0)),
            pl.BlockSpec((1, units, width), lambda i: (i, 0, 0)),
            pl.BlockSpec((1, 4, HEAD_DIM, columns), lambda i: (i, 0, 0, 0)),
            pl.BlockSpec((row_tile, 1), lambda i: (i, 0)),
            whole_spec,
            whole_spec,
        ],
        out_specs=(
            row_spec, row_spec, head_spec, head_spec, head_spec, head_spec, wide_spec, wide_spec,
            pl.BlockSpec((units, width), lambda i: (i, 0)),
        ),
        compiler_params=pltpu.CompilerParams(vmem_limit_bytes=VMEM_LIMIT),
        cost_estimate=pl.CostEstimate(flops=0, bytes_accessed=58_000_000, transcendentals=0),
        name="assemble",
    )(both, down, heads, order_column, output_b, input_b)


def swapped(
    tokens, cotangent, route, lengths, key_mask, norm1_gain, norm2_gain,
    w_query, w_key, w_value, w_out, w_gate, w_up, w_down,
):
    groups = lax.axis_size("dp")
    members = lax.axis_size("mp")
    me = lax.axis_index("dp")
    z = lax.axis_index("mp")
    rows, width = tokens.shape
    bucket = rows // groups
    units = w_down.shape[0] // groups

    target = route // TOK_DEV
    earlier = jnp.arange(rows, dtype=jnp.int32)
    same = (target[:, None] == target[None, :]) & (earlier[None, :] < earlier[:, None])
    send_at = target * bucket + jnp.sum(same.astype(jnp.int32), axis=1)
    sorting = send_at[None, :] == earlier[:, None]
    slots_own = jnp.sum(jnp.where(sorting, (route % rows)[None, :], 0), axis=1)

    mask_window = lax.dynamic_slice_in_dim(
        jnp.concatenate([jnp.zeros((WINDOW,), jnp.int32), key_mask]), z * rows, rows + WINDOW
    )
    slot_rows = jnp.pad(slots_own.reshape(groups, bucket).T, ((0, 0), (0, LANES - groups)))
    mask_rows = jnp.pad(mask_window, (0, 4 * LANES - rows - WINDOW)).reshape(4, LANES)
    length_rows = jnp.pad(lengths, ((0, 3), (0, LANES - lengths.shape[1])))
    notes = jnp.concatenate([slot_rows, mask_rows, length_rows], axis=0).astype(F32)

    count = groups * rows
    scale = HEAD_DIM ** (-0.5)
    (
        hidden_one,
        w_qkv,
        w_proj,
        notes_all,
        gate_all,
        mixed,
        kept,
        tokens_b,
        cotangent_b,
        cotangent_all,
    ) = attend_ahead(
        tokens,
        cotangent,
        send_at.astype(F32)[None],
        norm1_gain[None],
        notes,
        w_query.T,
        w_key.T,
        w_value.T,
        w_out,
        w_gate,
        scale,
    )
    mixed = mixed.reshape(count, 2 * LANES)
    middle, hidden_two, up_all, down_all = project_middle(
        mixed, w_proj, tokens_b, norm2_gain[None], w_up, w_down
    )
    down_all = down_all.reshape(members * units, width)
    middle_grad, branch, sums_two, activated, both_sum, down_in = feed(
        hidden_two, cotangent_all, middle, gate_all, up_all, cotangent_b, down_all, norm2_gain[None]
    )
    qkv_grad, output_rows, branch_all, both_in, down_whole = attend_back(
        branch,
        notes_all,
        kept,
        w_proj,
        activated.reshape(count, units * members),
        down_all,
        middle,
        both_sum,
        down_in,
        scale,
    )
    qkv_grad = qkv_grad.reshape(count, 6 * LANES)
    input_rows, gain_sums, both_whole, heads_whole = project_input(
        qkv_grad,
        w_qkv,
        hidden_one,
        branch_all,
        mixed,
        tokens_b,
        middle_grad,
        norm1_gain[None],
        sums_two,
        both_sum,
        both_in,
    )
    (
        output,
        input_grad,
        query_grad,
        key_grad,
        value_grad,
        proj_grad,
        gate_grad,
        up_grad,
        down_grad,
    ) = assemble(
        both_whole,
        down_whole,
        heads_whole.reshape(groups, 4, HEAD_DIM, width // 2),
        send_at.astype(F32)[:, None],
        output_rows,
        input_rows,
    )
    return (
        output,
        input_grad,
        gain_sums[0],
        gain_sums[1],
        query_grad.T,
        key_grad.T,
        value_grad.T,
        proj_grad,
        gate_grad,
        up_grad,
        down_grad,
    )


def solution(mesh):
    in_specs = (
        P(("dp", "mp"), None),
        P(("dp", "mp"), None),
        P(("dp", "mp")),
        P("dp", None),
        P("dp"),
        P(),
        P(),
        P(None, "mp"),
        P(None, "mp"),
        P(None, "mp"),
        P("mp", None),
        P(None, "mp"),
        P(None, "mp"),
        P("mp", None),
    )
    out_specs = (
        P(("dp", "mp"), None),
        P(("dp", "mp"), None),
        P(),
        P(),
        P(None, "mp"),
        P(None, "mp"),
        P(None, "mp"),
        P("mp", None),
        P(None, "mp"),
        P(None, "mp"),
        P("mp", None),
    )
    body = swapped if (mesh.shape["dp"], mesh.shape["mp"]) == (8, 4) else local
    return jax.shard_map(body, mesh=mesh, in_specs=in_specs, out_specs=out_specs, check_vma=False)
```

```python
import functools

import jax
import jax.numpy as jnp
from jax import lax
from jax.experimental import pallas as pl
from jax.experimental.pallas import tpu as pltpu
from jax.sharding import PartitionSpec as P

HEAD_DIM = 112
WINDOW = 64
TOK_DEV = 1536


EPSILON = 1e-05
MASKED = 1e30


def norm_rows(values):
    inverse = lax.rsqrt(jnp.mean(values * values, axis=-1, keepdims=True) + EPSILON)
    return (values * inverse, inverse)


def norm_back(gradient, normed, inverse, norm_gain):
    scaled = gradient * norm_gain
    result = inverse * (scaled - normed * jnp.mean(scaled * normed, axis=-1, keepdims=True))
    return (result, jnp.sum(gradient * normed, axis=0))


def padded(values, filler):
    front = jnp.full((WINDOW,) + values.shape[1:], filler, values.dtype)
    return jnp.concatenate([front, values], axis=0)


def block_scores(query_block, key_block, query_seg, key_seg, key_flag, first_row, score_scale):
    query_pos = first_row + jnp.arange(query_block.shape[0], dtype=jnp.int32)
    key_pos = first_row - WINDOW + jnp.arange(key_block.shape[0], dtype=jnp.int32)
    distance = query_pos[:, None] - key_pos[None, :]
    allowed = (distance >= 0) & (distance < WINDOW) & (query_seg[:, None] == key_seg[None, :])
    allowed = allowed & ((key_flag[None, :] == 1) | (distance == 0))
    raw_scores = (
        jnp.einsum("qhd,khd->hqk", query_block, key_block, preferred_element_type=jnp.float32)
        * score_scale
    )
    return jnp.where(allowed[None], raw_scores, -MASKED)


def block_inputs(query, key_pad, value_pad, segment, seg_pad, live_pad, first_row, block_rows):
    key_span = block_rows + WINDOW
    return (
        lax.dynamic_slice_in_dim(query, first_row, block_rows, 0),
        lax.dynamic_slice_in_dim(key_pad, first_row, key_span, 0),
        lax.dynamic_slice_in_dim(value_pad, first_row, key_span, 0),
        lax.dynamic_slice_in_dim(segment, first_row, block_rows, 0),
        lax.dynamic_slice_in_dim(seg_pad, first_row, key_span, 0),
        lax.dynamic_slice_in_dim(live_pad, first_row, key_span, 0),
    )


def attend_forward(query, key_all, value_all, segment, key_live):
    token_count, head_count, head_width = query.shape
    block_rows = min(512, token_count)
    score_scale = head_width ** (-0.5)
    key_pad = padded(key_all, 0.0)
    value_pad = padded(value_all, 0.0)
    seg_pad = padded(segment, -1)
    live_pad = padded(key_live, 0)

    def one_block(running, block_index):
        first_row = block_index * block_rows
        query_block, key_block, value_block, query_seg, key_seg, key_flag = block_inputs(
            query, key_pad, value_pad, segment, seg_pad, live_pad, first_row, block_rows
        )
        scores = block_scores(
            query_block, key_block, query_seg, key_seg, key_flag, first_row, score_scale
        )
        row_max = jnp.max(scores, axis=-1, keepdims=True)
        weights = jnp.exp(scores - row_max)
        denominator = jnp.sum(weights, axis=-1, keepdims=True)
        chances = (weights / denominator).astype(jnp.bfloat16)
        mixed = jnp.einsum("hqk,khd->qhd", chances, value_block, preferred_element_type=jnp.float32)
        return (
            running,
            (mixed.astype(jnp.bfloat16), row_max[..., 0] + jnp.log(denominator[..., 0])),
        )

    _, (mixed, logsum) = lax.scan(
        one_block, jnp.zeros((), jnp.int32), jnp.arange(token_count // block_rows, dtype=jnp.int32)
    )
    return (mixed.reshape(token_count, head_count * head_width), logsum)


def attend_backward(query, key_all, value_all, segment, key_live, logsum, mixed_grad):
    token_count, head_count, head_width = query.shape
    block_rows = min(512, token_count)
    key_span = block_rows + WINDOW
    score_scale = head_width ** (-0.5)
    key_pad = padded(key_all, 0.0)
    value_pad = padded(value_all, 0.0)
    seg_pad = padded(segment, -1)
    live_pad = padded(key_live, 0)

    def one_block(running, inputs):
        key_grad, value_grad = running
        block_index, block_logsum = inputs
        first_row = block_index * block_rows
        query_block, key_block, value_block, query_seg, key_seg, key_flag = block_inputs(
            query, key_pad, value_pad, segment, seg_pad, live_pad, first_row, block_rows
        )
        grad_block = lax.dynamic_slice_in_dim(mixed_grad, first_row, block_rows, 0)
        scores = block_scores(
            query_block, key_block, query_seg, key_seg, key_flag, first_row, score_scale
        )
        chances = jnp.exp(scores - block_logsum[..., None])
        chance_grad = jnp.einsum(
            "qhd,khd->hqk", grad_block, value_block, preferred_element_type=jnp.float32
        )
        row_dot = jnp.sum(chances * chance_grad, axis=-1, keepdims=True)
        score_grad = (chances * (chance_grad - row_dot)).astype(jnp.bfloat16)
        query_grad = (
            jnp.einsum("hqk,khd->qhd", score_grad, key_block, preferred_element_type=jnp.float32)
            * score_scale
        )
        key_part = (
            jnp.einsum("hqk,qhd->khd", score_grad, query_block, preferred_element_type=jnp.float32)
            * score_scale
        )
        value_part = jnp.einsum(
            "hqk,qhd->khd",
            chances.astype(jnp.bfloat16),
            grad_block,
            preferred_element_type=jnp.float32,
        )
        key_grad = lax.dynamic_update_slice_in_dim(
            key_grad,
            lax.dynamic_slice_in_dim(key_grad, first_row, key_span, 0) + key_part,
            first_row,
            0,
        )
        value_grad = lax.dynamic_update_slice_in_dim(
            value_grad,
            lax.dynamic_slice_in_dim(value_grad, first_row, key_span, 0) + value_part,
            first_row,
            0,
        )
        return ((key_grad, value_grad), query_grad)

    empty_grad = jnp.zeros((token_count + WINDOW, head_count, head_width), jnp.float32)
    (key_grad, value_grad), query_grad = lax.scan(
        one_block,
        (empty_grad, empty_grad),
        (jnp.arange(token_count // block_rows, dtype=jnp.int32), logsum),
    )
    flat_width = head_count * head_width
    return (
        query_grad.reshape(token_count, flat_width).astype(jnp.bfloat16),
        key_grad[WINDOW:].reshape(token_count, flat_width).astype(jnp.bfloat16),
        value_grad[WINDOW:].reshape(token_count, flat_width).astype(jnp.bfloat16),
    )


def local(
    tokens,
    cotangent,
    route,
    lengths,
    key_mask,
    norm1_gain,
    norm2_gain,
    w_query,
    w_key,
    w_value,
    w_out,
    w_gate,
    w_up,
    w_down,
):
    groups = lax.axis_size("dp")
    members = lax.axis_size("mp")
    member = lax.axis_index("mp")
    local_rows = tokens.shape[0]
    group_rows = local_rows * members
    bucket = local_rows // groups
    target = route // TOK_DEV
    chosen = (target[:, None] == jnp.arange(groups, dtype=jnp.int32)[None, :]).astype(jnp.int32)
    ranking = jnp.sum((jnp.cumsum(chosen, axis=0) - chosen) * chosen, axis=1)
    send_at = target * bucket + ranking
    arrival, arrival_grad, arrival_slot = (
        lax.all_to_all(
            jnp.zeros_like(tokens).at[send_at].set(tokens),
            "dp",
            split_axis=0,
            concat_axis=0,
            tiled=True,
        ),
        lax.all_to_all(
            jnp.zeros_like(cotangent).at[send_at].set(cotangent),
            "dp",
            split_axis=0,
            concat_axis=0,
            tiled=True,
        ),
        lax.all_to_all(
            jnp.zeros_like(route).at[send_at].set(route % local_rows),
            "dp",
            split_axis=0,
            concat_axis=0,
            tiled=True,
        ),
    )
    token_rows = jnp.zeros_like(arrival).at[arrival_slot].set(arrival)
    grad_rows = jnp.zeros_like(arrival_grad).at[arrival_slot].set(arrival_grad)
    seq_ends = jnp.cumsum(lengths[0])
    positions = jnp.arange(group_rows, dtype=jnp.int32)
    segment = jnp.sum((positions[:, None] >= seq_ends[None, :]).astype(jnp.int32), axis=1)
    input_rows = token_rows.astype(jnp.float32)
    normed_one, inverse_one = norm_rows(input_rows)
    leading_all, grad_all = (
        lax.all_gather(token_rows, "mp", axis=0, tiled=True),
        lax.all_gather(grad_rows, "mp", axis=0, tiled=True),
    )
    input_all = leading_all.astype(jnp.float32)
    normed_all, _ = norm_rows(input_all)
    hidden_one = (normed_all * norm1_gain).astype(jnp.bfloat16)
    head_count = w_query.shape[1] // HEAD_DIM
    query = jnp.dot(hidden_one, w_query, preferred_element_type=jnp.float32).astype(jnp.bfloat16)
    keys = jnp.dot(hidden_one, w_key, preferred_element_type=jnp.float32).astype(jnp.bfloat16)
    values = jnp.dot(hidden_one, w_value, preferred_element_type=jnp.float32).astype(jnp.bfloat16)
    query_heads = query.reshape(group_rows, head_count, HEAD_DIM)
    key_heads = keys.reshape(group_rows, head_count, HEAD_DIM)
    value_heads = values.reshape(group_rows, head_count, HEAD_DIM)
    mixed_flat, logsum = attend_forward(query_heads, key_heads, value_heads, segment, key_mask)
    attention_all = lax.psum(jnp.dot(mixed_flat, w_out, preferred_element_type=jnp.float32), "mp")
    middle_all = input_all + attention_all
    middle_rows = lax.dynamic_slice_in_dim(middle_all, member * local_rows, local_rows, 0)
    normed_mid, _ = norm_rows(middle_all)
    hidden_two = (normed_mid * norm2_gain).astype(jnp.bfloat16)
    normed_two, inverse_two = norm_rows(middle_rows)
    gate_value = jnp.dot(hidden_two, w_gate, preferred_element_type=jnp.float32)
    upward = jnp.dot(hidden_two, w_up, preferred_element_type=jnp.float32)
    sigmoid = jax.nn.sigmoid(gate_value)
    activated = (gate_value * sigmoid * upward).astype(jnp.bfloat16)
    out_rows = middle_rows + lax.psum_scatter(
        jnp.dot(activated, w_down, preferred_element_type=jnp.float32).astype(jnp.bfloat16),
        "mp",
        scatter_dimension=0,
        tiled=True,
    ).astype(jnp.float32)
    activated_grad = jnp.einsum("td,fd->tf", grad_all, w_down, preferred_element_type=jnp.float32)
    gate_grad = (activated_grad * upward * sigmoid * (1.0 + gate_value * (1.0 - sigmoid))).astype(
        jnp.bfloat16
    )
    upward_grad = (activated_grad * gate_value * sigmoid).astype(jnp.bfloat16)
    down_sum = jnp.einsum("tf,td->fd", activated, grad_all, preferred_element_type=jnp.float32)
    gate_sum = jnp.einsum("td,tf->df", hidden_two, gate_grad, preferred_element_type=jnp.float32)
    upward_sum = jnp.einsum(
        "td,tf->df", hidden_two, upward_grad, preferred_element_type=jnp.float32
    )
    hidden_two_grad = lax.psum_scatter(
        jnp.einsum("tf,df->td", gate_grad, w_gate, preferred_element_type=jnp.float32)
        + jnp.einsum("tf,df->td", upward_grad, w_up, preferred_element_type=jnp.float32),
        "mp",
        scatter_dimension=0,
        tiled=True,
    )
    norm_part_two, gain_two_grad = norm_back(hidden_two_grad, normed_two, inverse_two, norm2_gain)
    middle_grad = grad_rows.astype(jnp.float32) + norm_part_two
    branch_all = lax.all_gather(middle_grad.astype(jnp.bfloat16), "mp", axis=0, tiled=True)
    output_sum = jnp.einsum("tc,td->cd", mixed_flat, branch_all, preferred_element_type=jnp.float32)
    mixed_grad = jnp.einsum(
        "td,cd->tc", branch_all, w_out, preferred_element_type=jnp.float32
    ).astype(jnp.bfloat16)
    query_grad, key_grad, value_grad = attend_backward(
        query_heads,
        key_heads,
        value_heads,
        segment,
        key_mask,
        logsum,
        mixed_grad.reshape(group_rows, head_count, HEAD_DIM),
    )
    query_sum = jnp.einsum("td,tc->dc", hidden_one, query_grad, preferred_element_type=jnp.float32)
    key_sum = jnp.einsum("td,tc->dc", hidden_one, key_grad, preferred_element_type=jnp.float32)
    value_sum = jnp.einsum("td,tc->dc", hidden_one, value_grad, preferred_element_type=jnp.float32)
    hidden_one_grad = lax.psum_scatter(
        (
            jnp.einsum("tc,dc->td", query_grad, w_query, preferred_element_type=jnp.float32)
            + jnp.einsum("tc,dc->td", key_grad, w_key, preferred_element_type=jnp.float32)
            + jnp.einsum("tc,dc->td", value_grad, w_value, preferred_element_type=jnp.float32)
        ).astype(jnp.bfloat16),
        "mp",
        scatter_dimension=0,
        tiled=True,
    ).astype(jnp.float32)
    norm_part_one, gain_one_grad = norm_back(hidden_one_grad, normed_one, inverse_one, norm1_gain)
    input_grad = middle_grad + norm_part_one
    gain_one_sum, gain_two_sum = lax.psum((gain_one_grad, gain_two_grad), ("dp", "mp"))
    weight_sums = (
        lax.psum(query_sum.astype(jnp.bfloat16), "dp").astype(jnp.float32),
        lax.psum(key_sum.astype(jnp.bfloat16), "dp").astype(jnp.float32),
        lax.psum(value_sum.astype(jnp.bfloat16), "dp").astype(jnp.float32),
        lax.psum(output_sum.astype(jnp.bfloat16), "dp").astype(jnp.float32),
        lax.psum(gate_sum.astype(jnp.bfloat16), "dp").astype(jnp.float32),
        lax.psum(upward_sum.astype(jnp.bfloat16), "dp").astype(jnp.float32),
        lax.psum(down_sum.astype(jnp.bfloat16), "dp").astype(jnp.float32),
    )
    back_out, back_grad = (
        lax.all_to_all(
            out_rows.astype(jnp.bfloat16)[arrival_slot],
            "dp",
            split_axis=0,
            concat_axis=0,
            tiled=True,
        ),
        lax.all_to_all(
            input_grad.astype(jnp.bfloat16)[arrival_slot],
            "dp",
            split_axis=0,
            concat_axis=0,
            tiled=True,
        ),
    )
    return (
        back_out[send_at],
        back_grad[send_at],
        gain_one_sum,
        gain_two_sum,
        weight_sums[0],
        weight_sums[1],
        weight_sums[2],
        weight_sums[3],
        weight_sums[4],
        weight_sums[5],
        weight_sums[6],
    )


MESH = pl.DeviceIdType.MESH
LANES = 128
F32 = jnp.float32
BF16 = jnp.bfloat16
VMEM_LIMIT = 56 * 1024 * 1024


def plane():
    me = lax.axis_index("dp")
    side = me + 1 - 2 * lax.rem(me, 2)
    over_x = me + 2 - 4 * lax.rem(lax.div(me, 2), 2)
    over_y = me + 4 - 8 * lax.rem(lax.div(me, 4), 2)
    corner = over_x + 4 - 8 * lax.rem(lax.div(over_x, 4), 2)
    return (me, side, over_x, over_y, corner)


def to_dp(source, target, send_sem, recv_sem, index):
    return pltpu.make_async_remote_copy(
        src_ref=source,
        dst_ref=target,
        send_sem=send_sem,
        recv_sem=recv_sem,
        device_id={"dp": index},
        device_id_type=MESH,
    )


def to_mp(source, target, send_sem, recv_sem, index):
    return pltpu.make_async_remote_copy(
        src_ref=source,
        dst_ref=target,
        send_sem=send_sem,
        recv_sem=recv_sem,
        device_id={"mp": index},
        device_id_type=MESH,
    )


def owner_at(turn):
    me, side, over_x, over_y, _ = plane()
    block = turn // 2
    near = ((block + 1) // 2) % 2
    far = block // 3
    second = turn % 2
    other = (1 - near) * second + (block // 2) * near
    owner = me + (near * (1 - second) + far) * (over_x - me)
    return owner + (near * second + far) * (over_y - me) + other * (side - me)


ARRIVALS = (
    (1, (4,)),
    (2, (0, 1, 2)),
    (3, (3,)),
    (4, (6, 9)),
    (5, (8, 10)),
    (6, (5, 7)),
    (7, (11, 12)),
)


class Gather:
    AFTER = {0: (5, 6), 1: (7, 8), 2: (9,), 3: (10,), 5: (11,), 7: (12,)}

    def __init__(self, own, out, send, recv, local=None):
        me, side, over_x, over_y, corner = plane()
        half = out.shape[1] // 2
        low, high = pl.ds(0, half), pl.ds(half, half)
        self.keep = None if own is None else pltpu.make_async_copy(own, out.at[me], local)
        own = out.at[me] if own is None else own

        def hop(number, source, target, index):
            return to_dp(source, target, send.at[number], recv.at[number], index)

        def onward(number, owner, part, index):
            place = out.at[owner, part]
            return hop(number, place, place, index)

        self.copies = [
            hop(0, own.at[low], out.at[me, low], over_x),
            hop(1, own.at[high], out.at[me, high], over_y),
            hop(2, own.at[high], out.at[me, high], over_x),
            hop(3, own.at[low], out.at[me, low], over_y),
            hop(4, own, out.at[me], side),
            onward(5, over_x, low, over_y),
            onward(6, over_x, low, side),
            onward(7, over_y, high, over_x),
            onward(8, over_y, high, side),
            onward(9, over_x, high, side),
            onward(10, over_y, low, side),
            onward(11, corner, low, side),
            onward(12, corner, high, side),
        ]

    def start(self):
        for number in range(5):
            self.copies[number].start()
        if self.keep is not None:
            self.keep.start()

    def arrive(self, *numbers):
        for number in numbers:
            self.copies[number].wait_recv()
            for later in self.AFTER.get(number, ()):
                self.copies[later].start()

    def pass_on(self):
        self.arrive(0, 1, 2, 3)

    def sent(self):
        for copy in self.copies:
            copy.wait_send()
        if self.keep is not None:
            self.keep.wait()

    def finish(self):
        self.arrive(5, 7, 4, 6, 8, 9, 10, 11, 12)
        self.sent()


def greet_all():
    barrier = pltpu.get_barrier_semaphore()
    me, z = lax.axis_index("dp"), lax.axis_index("mp")
    for step in range(1, 8):
        pl.semaphore_signal(
            barrier, inc=1, device_id={"dp": lax.rem(me + step, 8)}, device_id_type=MESH
        )
    core = lax.rem(me, 2)
    for step in range(1, 4):
        for other in (me, me + 1 - 2 * core):
            pl.semaphore_signal(
                barrier,
                inc=1,
                device_id={"dp": other, "mp": lax.rem(z + step, 4)},
                device_id_type=MESH,
            )
    return barrier


def start_all(copies):
    for copy in copies:
        copy.start()
    return copies


def wait_all(copies):
    for copy in copies:
        copy.wait()


def swap_all(source, target, send, recv):
    me = lax.axis_index("dp")
    return [
        to_dp(source, target.at[me], send.at[step - 1], recv.at[step - 1], lax.rem(me + step, 8))
        for step in range(1, 8)
    ]


class Spread:
    def __init__(self, share, w_qkv, w_out, send, recv, local):
        me, z = lax.axis_index("dp"), lax.axis_index("mp")
        core = lax.rem(me, 2)
        self.place = z + core * (3 - 2 * z)
        self.send, self.recv, self.local = send, recv, local
        self.shares = [share.at[0], share.at[1], share.at[2], share.at[3]]
        self.slots = (core, 1 - core)
        self.core = core
        self.w_qkv, self.w_out = w_qkv, w_out

    def target(self, which, piece):
        slot = self.slots[which]
        block = slot if piece == 3 else 2 * piece + slot
        rows = pl.ds(pl.multiple_of(block * LANES, LANES), HEAD_DIM)
        return (self.w_out if piece == 3 else self.w_qkv).at[rows]

    def hop(self, which, piece, number, place, own):
        source = self.shares[piece] if own else self.target(which, piece)
        z = place + self.core * (3 - 2 * place)
        return to_mp(
            source,
            self.target(which, piece),
            self.send.at[number * 4 + piece],
            self.recv.at[which * 4 + piece],
            z,
        )

    def keep(self, which, piece):
        return pltpu.make_async_copy(
            self.shares[piece], self.target(which, piece), self.local.at[piece]
        )

    def start(self, pieces):
        @pl.when(self.place == 0)
        def _():
            for piece in pieces:
                self.hop(0, piece, 0, 1, True).start()
                self.keep(0, piece).start()

        @pl.when(self.place == 1)
        def _():
            for piece in pieces:
                self.hop(1, piece, 0, 0, True).start()
                self.hop(1, piece, 1, 2, True).start()
                self.keep(1, piece).start()

    def pass_on(self, pieces):
        @pl.when(self.place == 1)
        def _():
            for piece in pieces:
                self.hop(0, piece, 2, 2, False).wait_recv()
                self.hop(0, piece, 2, 2, False).start()

        @pl.when(self.place == 2)
        def _():
            for which in (1, 0):
                for piece in pieces:
                    self.hop(which, piece, which, 3, False).wait_recv()
                    self.hop(which, piece, which, 3, False).start()

    def finish(self, pieces):
        @pl.when(self.place == 0)
        def _():
            for piece in pieces:
                self.hop(1, piece, 0, 1, False).wait_recv()
                self.hop(0, piece, 0, 1, True).wait_send()
                self.keep(0, piece).wait()

        @pl.when(self.place == 1)
        def _():
            for piece in pieces:
                self.hop(1, piece, 0, 0, True).wait_send()
                self.hop(1, piece, 1, 2, True).wait_send()
                self.hop(0, piece, 2, 2, False).wait_send()
                self.keep(1, piece).wait()

        @pl.when(self.place == 2)
        def _():
            for piece in pieces:
                for which in (1, 0):
                    self.hop(which, piece, which, 3, False).wait_send()

        @pl.when(self.place == 3)
        def _():
            for piece in pieces:
                for which in (1, 0):
                    self.hop(which, piece, which, 3, False).wait_recv()


class Column:
    def __init__(self, own, out, send, recv, local):
        z = lax.axis_index("mp")
        self.z, self.own, self.out, self.send, self.recv = z, own, out, send, recv
        self.outer = (z == 0) | (z == 3)
        near = 1 + lax.div(z, 3)
        self.from_outer = (near, 3 - near)
        self.edge = 3 * (z - 1)
        self.from_inner = (3 - z, 3 - self.edge, self.edge)
        self.keep = pltpu.make_async_copy(own, out.at[z], local)

    def straight(self, number, target):
        return to_mp(
            self.own, self.out.at[self.z], self.send.at[number], self.recv.at[self.z], target
        )

    def onward(self):
        far = 3 - self.edge
        return to_mp(
            self.out.at[far], self.out.at[far], self.send.at[3], self.recv.at[far], self.edge
        )

    def came(self, source):
        return to_mp(
            self.own, self.out.at[source], self.send.at[0], self.recv.at[source], source
        ).wait_recv

    def start(self):
        self.keep.start()

        @pl.when(self.outer)
        def _():
            for number, target in enumerate(self.from_outer):
                self.straight(number, target).start()

        @pl.when(jnp.logical_not(self.outer))
        def _():
            for number, target in enumerate(self.from_inner):
                self.straight(number, target).start()

    def pass_on(self):
        @pl.when(jnp.logical_not(self.outer))
        def _():
            self.came(3 - self.edge)()
            self.onward().start()

    def finish(self):
        @pl.when(self.outer)
        def _():
            for source in (1, 2):
                self.came(source)()
            self.came(3 - self.z)()
            for number, target in enumerate(self.from_outer):
                self.straight(number, target).wait_send()

        @pl.when(jnp.logical_not(self.outer))
        def _():
            self.came(3 - self.z)()
            self.came(self.edge)()
            for number, target in enumerate(self.from_inner):
                self.straight(number, target).wait_send()
            self.onward().wait_send()

        self.keep.wait()


def anywhere():
    return pl.BlockSpec(memory_space=pl.ANY)


def on_chip():
    return pl.BlockSpec(memory_space=pltpu.VMEM)


def remote_params(number, limit=VMEM_LIMIT):
    return pltpu.CompilerParams(
        collective_id=number, has_side_effects=True, vmem_limit_bytes=limit
    )


def hot_of(notes, k, size):
    own = notes[:, 0:48, :].reshape(size, LANES)
    lane = lax.broadcasted_iota(jnp.int32, (size, LANES), 1)
    slot = jnp.sum(jnp.where(lane == k, own, 0.0), axis=1, keepdims=True)
    return (lax.broadcasted_iota(jnp.int32, (size, size), 1).astype(F32) == slot).astype(BF16)


def block_mask(notes, k, block, z, rows):
    position = rows * z + block * 128 + lax.broadcasted_iota(jnp.int32, (128, 1), 0)
    position = position.astype(F32)
    first_end = notes[k, 52:53, 0:1]
    second_end = first_end + notes[k, 52:53, 1:2]
    begin = jnp.where(position >= first_end, first_end, 0.0)
    begin = jnp.where(position >= second_end, second_end, begin)
    column = lax.broadcasted_iota(jnp.int32, (128, 192), 1)
    distance = 64 + lax.broadcasted_iota(jnp.int32, (128, 192), 0) - column
    key_position = (rows * z + block * 128 - 64 + column).astype(F32)
    live = jnp.concatenate(
        [notes[k, 48 + block : 49 + block, :], notes[k, 49 + block : 50 + block, 0:64]], axis=1
    )
    allowed = (distance >= 0) & (distance < WINDOW) & (key_position >= begin)
    return allowed & ((live == 1.0) | (distance == 0))


NT = (((1,), (1,)), ((), ()))
TN = (((0,), (0,)), ((), ()))


def forward_kernel(
    tokens, cotangent, order_row, gain, notes, query, keys, values, project, gate, down,
    hidden_out, w_qkv_out, w_out, notes_all, gate_all, mixed_out, kept_out, tokens_out, cotangent_out,
    cotangent_all, low_all,
    hidden_all, qkv, share, gate_own, low_own, send_l, recv_l, w_qkv, mixed, kept, tokens_b, cotangent_b,
    send, recv, send_a, recv_a, send_g, recv_g, send_w, recv_w, send_n, recv_n, send_c, recv_c,
    local, out_sem, store_sem, *, scale,
):
    groups, rows, width = hidden_all.shape
    me, z = lax.axis_index("dp"), lax.axis_index("mp")
    members = lax.axis_size("mp")
    barrier = greet_all()
    head = pl.ds(pl.multiple_of(lax.div(me, 2) * HEAD_DIM, 16), HEAD_DIM)
    units = pl.ds(pl.multiple_of(me * LANES, LANES), LANES)
    loads = [
        pltpu.make_async_copy(source.at[head], share.at[piece], local.at[piece])
        for piece, source in enumerate((query, keys, values, project))
    ]
    half_units = pl.ds(pl.multiple_of(me * LANES, LANES // 2), LANES // 2)
    loads.append(pltpu.make_async_copy(gate.at[:, units], gate_own, local.at[4]))
    loads.append(pltpu.make_async_copy(down.at[half_units], low_own, local.at[6]))
    for copy in loads:
        copy.start()
    none = jnp.zeros((LANES - HEAD_DIM, width), BF16)
    for block in range(6):
        w_qkv[block * LANES + HEAD_DIM : block * LANES + LANES, :] = none
    for block in range(2):
        w_out[block * LANES + HEAD_DIM : block * LANES + LANES, :] = none

    place = lax.broadcasted_iota(jnp.int32, (rows, rows), 0).astype(F32)
    sort = (place == order_row[...]).astype(BF16)
    tokens_b[...] = jnp.dot(sort, tokens[...], preferred_element_type=F32).astype(BF16)

    def normalise(span):
        value = tokens_b[span, :].astype(F32)
        inverse = lax.rsqrt(mean_rows(value * value) + EPSILON)
        hidden_all[me, span, :] = (value * inverse * gain[...]).astype(BF16)

    each_chunk(rows, normalise)
    notes_all[me] = notes[...]
    stores = start_all([pltpu.make_async_copy(tokens_b, tokens_out, store_sem.at[0])])
    pl.semaphore_wait(barrier, 13)
    gather = Gather(None, hidden_all, send_a, recv_a)
    gather.start()
    swaps = swap_all(notes, notes_all, send_n, recv_n)
    for copy in swaps:
        copy.start()
    for copy in loads[:4]:
        copy.wait()
    spread = Spread(share, w_qkv, w_out, send_w, recv_w, local)
    spread.start((0, 1, 2))
    cotangent_b[...] = jnp.dot(sort, cotangent[...], preferred_element_type=F32).astype(BF16)
    stores += start_all([pltpu.make_async_copy(cotangent_b, cotangent_out, store_sem.at[1])])
    wait_all(loads[4:])
    column = Column(gate_own, gate_all, send_c, recv_c, local.at[4])
    second = Gather(cotangent_b, cotangent_all, send_g, recv_g, local.at[5])
    low = Column(low_own, low_all, send_l, recv_l, local.at[6])
    spread.pass_on((0, 1, 2))
    gather.arrive(0, 1)
    second.start()
    column.start()
    gather.arrive(2, 3)
    spread.finish((0, 1, 2))
    spread.start((3,))
    stores += start_all([pltpu.make_async_copy(w_qkv, w_qkv_out, store_sem.at[2])])
    for copy in swaps:
        copy.wait()

    def keep(turn):
        owner = owner_at(turn)
        return pltpu.make_async_copy(hidden_all.at[owner], hidden_out.at[owner], out_sem.at[turn])

    def multiply(turn, carry):
        for number, numbers in ARRIVALS:
            left = tuple(n for n in numbers if n > 3)
            if left:
                pl.when(turn == number)(functools.partial(gather.arrive, *left))
        owner = owner_at(turn)
        keep(turn).start()
        product = lax.dot_general(
            hidden_all[owner], w_qkv[...], NT, preferred_element_type=F32
        ).astype(BF16)
        qkv[owner] = product.reshape(groups, rows // groups, 768)
        return carry

    lax.fori_loop(0, groups, multiply, 0)

    def halo(k, other):
        return to_mp(
            kept.at[k, pl.ds(rows, 64), pl.ds(256, 512)],
            kept.at[k, pl.ds(0, 64), pl.ds(256, 512)],
            send.at[k],
            recv.at[k],
            other,
        )

    def store_kept(k):
        return pltpu.make_async_copy(kept.at[k], kept_out.at[k], store_sem.at[3 + k])

    def store_mixed(k):
        span = pl.ds(k, 1)
        return pltpu.make_async_copy(
            mixed.at[:, span], mixed_out.at[:, span], store_sem.at[3 + groups + k]
        )

    def order(k, carry):
        hot = hot_of(notes_all, k, rows)
        given = qkv[:, pl.ds(k, 1)].reshape(rows, 768)
        kept[k, pl.ds(64, rows), :] = lax.dot_general(
            hot, given, TN, preferred_element_type=F32
        ).astype(BF16)
        kept[k, pl.ds(0, 64), pl.ds(0, 256)] = jnp.zeros((64, 256), BF16)

        @pl.when(z < members - 1)
        def _():
            halo(k, z + 1).start()

        @pl.when(z == 0)
        def _():
            kept[k, pl.ds(0, 64), pl.ds(256, 512)] = jnp.zeros((64, 512), BF16)

        return carry

    lax.fori_loop(0, groups, order, 0)

    def attend(k, carry):
        @pl.when(z > 0)
        def _():
            halo(k, z).wait_recv()

        store_kept(k).start()
        hot = hot_of(notes_all, k, rows)
        found = []
        for block in range(rows // 128):
            allowed = block_mask(notes_all, k, block, z, rows)
            heads = []
            for head in range(2):
                query = kept[k, pl.ds(64 + block * 128, 128), pl.ds(head * 128, 128)]
                keys = kept[k, pl.ds(block * 128, 192), pl.ds(256 + head * 128, 128)]
                values = kept[k, pl.ds(block * 128, 192), pl.ds(512 + head * 128, 128)]
                scores = lax.dot_general(query, keys, NT, preferred_element_type=F32) * scale
                scores = jnp.where(allowed, scores, -MASKED)
                weights = jnp.exp(scores - jnp.max(scores, axis=-1, keepdims=True))
                total = jnp.sum(weights, axis=-1, keepdims=True)
                chances = (weights / total).astype(BF16)
                heads.append(jnp.dot(chances, values, preferred_element_type=F32).astype(BF16))
            found.append(jnp.concatenate(heads, axis=1))
        ordered = jnp.concatenate(found, axis=0)
        back = jnp.dot(hot, ordered, preferred_element_type=F32).astype(BF16)
        mixed[:, pl.ds(k, 1)] = back.reshape(groups, 1, rows // groups, 256)
        store_mixed(k).start()
        return carry

    spread.pass_on((3,))
    low.start()
    lax.fori_loop(0, groups // 2, attend, 0)
    second.pass_on()
    column.pass_on()
    lax.fori_loop(groups // 2, groups - 1, attend, 0)
    low.pass_on()
    lax.fori_loop(groups - 1, groups, attend, 0)
    spread.finish((3,))
    second.finish()
    column.finish()
    low.finish()
    gather.sent()

    wait_all(stores)

    def stored(turn, carry):
        keep(turn).wait()
        store_kept(turn).wait()
        store_mixed(turn).wait()
        return carry

    lax.fori_loop(0, groups, stored, 0)

    @pl.when(z < members - 1)
    def _():
        def done(k, carry):
            halo(k, z + 1).wait_send()
            return carry

        lax.fori_loop(0, groups, done, 0)


def attend_ahead(
    tokens, cotangent, order_row, gain, notes, query, keys, values, project, gate, down, scale
):
    rows, width = tokens.shape
    groups, members = lax.axis_size("dp"), lax.axis_size("mp")
    dma = pltpu.SemaphoreType.DMA
    shape = jax.ShapeDtypeStruct
    return pl.pallas_call(
        functools.partial(forward_kernel, scale=scale),
        out_shape=(
            shape((groups, rows, width), BF16),
            shape((6 * LANES, width), BF16),
            shape((2 * LANES, width), BF16),
            shape((groups,) + notes.shape, F32),
            shape((members, width, LANES), BF16),
            shape((groups, groups, rows // groups, 256), BF16),
            shape((groups, rows + 64, 768), BF16),
            shape((rows, width), BF16),
            shape((rows, width), BF16),
            shape((groups, rows, width), BF16),
            shape((members, LANES // 2, width), BF16),
        ),
        in_specs=[on_chip()] * 5 + [anywhere()] * 6,
        out_specs=(
            anywhere(), anywhere(), on_chip(), on_chip(), anywhere(),
            anywhere(), anywhere(), anywhere(), anywhere(), anywhere(), anywhere(),
        ),
        scratch_shapes=[
            pltpu.VMEM((groups, rows, width), BF16),
            pltpu.VMEM((groups, groups, rows // groups, 768), BF16),
            pltpu.VMEM((4, HEAD_DIM, width), BF16),
            pltpu.VMEM((width, LANES), BF16),
            pltpu.VMEM((LANES // 2, width), BF16),
            dma((4,)),
            dma((4,)),
            pltpu.VMEM((6 * LANES, width), BF16),
            pltpu.VMEM((groups, groups, rows // groups, 256), BF16),
            pltpu.VMEM((groups, rows + 64, 768), BF16),
            pltpu.VMEM((rows, width), BF16),
            pltpu.VMEM((rows, width), BF16),
            dma((groups,)),
            dma((groups,)),
            dma((13,)),
            dma((13,)),
            dma((13,)),
            dma((13,)),
            dma((12,)),
            dma((8,)),
            dma((7,)),
            dma((7,)),
            dma((4,)),
            dma((4,)),
            dma((7,)),
            dma((groups,)),
            dma((3 + 2 * groups,)),
        ],
        compiler_params=remote_params(2, 60 * 1024 * 1024),
        cost_estimate=pl.CostEstimate(flops=0, bytes_accessed=300_000_000, transcendentals=0),
        name="attend_ahead",
    )(tokens, cotangent, order_row, gain, notes, query, keys, values, project, gate, down)


CHUNK = 32


def each_chunk(rows, body, chunk=CHUNK):
    def step(i, carry):
        body(pl.ds(pl.multiple_of(i * chunk, chunk), chunk))
        return carry

    lax.fori_loop(0, rows // chunk, step, 0)


class Units:
    def __init__(self, part, came_in, stage, send, recv, local):
        self.z = lax.axis_index("mp")
        self.part_of = part
        self.inputs = (came_in,)
        self.stages = (stage,)
        self.send, self.recv, self.local = send, recv, local
        z = self.z
        self.outer = (z == 0) | (z == 3)
        self.far = 3 - z
        self.near = 1 + lax.div(z, 3)
        self.second = 3 - self.near
        self.edge = 3 * (z - 1)

    def part(self, kind, z):
        return self.part_of(z)

    def straight(self, kind, number, target):
        return to_mp(
            self.part(kind, target),
            self.inputs[kind].at[self.z],
            self.send.at[number * 2 + kind],
            self.recv.at[self.z * 2 + kind],
            target,
        )

    def staged(self, kind):
        return to_mp(
            self.part(kind, self.far),
            self.stages[kind].at[0],
            self.send.at[4 + kind],
            self.recv.at[8 + kind],
            self.near,
        )

    def summed(self, kind):
        return to_mp(
            self.stages[kind].at[1],
            self.inputs[kind].at[self.z],
            self.send.at[4 + kind],
            self.recv.at[self.z * 2 + kind],
            3 - self.edge,
        )

    def mine(self, kind):
        return pltpu.make_async_copy(
            self.part(kind, 3 - self.edge), self.stages[kind].at[1], self.local.at[kind]
        )

    def start(self):
        @pl.when(self.outer)
        def _():
            for kind in range(1):
                self.staged(kind).start()
            for kind in range(1):
                self.straight(kind, 0, self.near).start()
                self.straight(kind, 1, self.second).start()

        @pl.when(jnp.logical_not(self.outer))
        def _():
            for kind in range(1):
                self.mine(kind).start()
                self.straight(kind, 0, 3 - self.z).start()
                self.straight(kind, 1, self.edge).start()

    def add(self):
        @pl.when(jnp.logical_not(self.outer))
        def _():
            for kind in range(1):
                stage = self.stages[kind]
                self.mine(kind).wait()
                to_mp(
                    self.part(kind, 0),
                    stage.at[0],
                    self.send.at[4 + kind],
                    self.recv.at[8 + kind],
                    self.edge,
                ).wait_recv()

                def body(span):
                    stage[1, span, :] = (
                        stage[0, span, :].astype(F32) + stage[1, span, :].astype(F32)
                    ).astype(BF16)

                each_chunk(stage.shape[1], body)
                self.summed(kind).start()

    def arrived(self, kind, source):
        to_mp(
            self.part(kind, 0),
            self.inputs[kind].at[source],
            self.send.at[kind],
            self.recv.at[source * 2 + kind],
            source,
        ).wait_recv()

    def finish(self):
        @pl.when(self.outer)
        def _():
            for kind in range(1):
                self.arrived(kind, 1)
                self.arrived(kind, 2)
                self.straight(kind, 0, self.near).wait_send()
                self.straight(kind, 1, self.second).wait_send()
                self.staged(kind).wait_send()

        @pl.when(jnp.logical_not(self.outer))
        def _():
            for kind in range(1):
                self.arrived(kind, 0)
                self.arrived(kind, 3)
                self.arrived(kind, 3 - self.z)
                self.straight(kind, 0, 3 - self.z).wait_send()
                self.straight(kind, 1, self.edge).wait_send()
                self.summed(kind).wait_send()


class Reduce:
    COUNT = 10

    def __init__(self, left, right, across, part, from_side, from_corner, from_near, send, recv):
        self.left, self.right, self.across, self.part = left, right, across, part
        self.from_side, self.from_corner, self.from_near = from_side, from_corner, from_near
        self.send, self.recv = send, recv
        self.rows = part.shape[1]

    def product(self, owner, slot):
        rows, width = self.rows, self.part.shape[2]
        picked = pl.ds(pl.multiple_of(owner * rows, rows), rows)

        def tile(t, carry):
            columns = pl.ds(pl.multiple_of(t * 256, 256), 256)
            if self.across:
                value = lax.dot_general(
                    self.left[picked, :], self.right[columns, :], NT, preferred_element_type=F32
                )
            else:
                value = jnp.dot(
                    self.left[picked, :], self.right[:, columns], preferred_element_type=F32
                )
            self.part[slot, :, columns] = value.astype(BF16)
            return carry

        lax.fori_loop(0, width // 256, tile, 0)

    def prepare(self):
        _, side, over_x, over_y, corner = plane()
        part, near = self.part, self.from_near
        half = self.rows // 2
        low, high = pl.ds(0, half), pl.ds(half, half)

        def hop(number, source, target, index):
            return to_dp(source, target, self.send.at[number], self.recv.at[number], index)

        self.shares = [hop(i, part.at[4 + i], self.from_side.at[i], side) for i in range(4)]
        self.corners = [
            hop(4, part.at[0, low], self.from_corner.at[0], over_x),
            hop(5, part.at[0, high], self.from_corner.at[1], over_y),
        ]
        self.nears = [
            hop(6, part.at[1, low], near.at[0, low], over_x),
            hop(7, part.at[1, high], near.at[0, high], over_x),
            hop(8, part.at[2, high], near.at[1, high], over_y),
            hop(9, part.at[2, low], near.at[1, low], over_y),
        ]

    def add_side(self, slot):
        self.shares[slot].wait_recv()

        def body(span):
            self.part[slot, span, :] = (
                self.part[slot, span, :].astype(F32) + self.from_side[slot, span, :].astype(F32)
            ).astype(BF16)

        each_chunk(self.rows, body)

    def add_corner(self, slot, offset, which):
        self.corners[which].wait_recv()

        def body(span):
            target = pl.ds(pl.multiple_of(offset + span.start, CHUNK), CHUNK)
            self.part[slot, target, :] = (
                self.part[slot, target, :].astype(F32)
                + self.from_corner[which, span, :].astype(F32)
            ).astype(BF16)

        each_chunk(self.rows // 2, body)

    def products(self):
        self.prepare()
        me, _, over_x, over_y, corner = plane()
        turn = 1 - 2 * lax.rem(me, 2)
        for slot, owner in enumerate((corner, over_x, over_y, me)):
            self.product(owner + turn, 4 + slot)
            self.shares[slot].start()
        for slot, owner in enumerate((corner, over_x, over_y, me)):
            self.product(owner, slot)

    def launch(self):
        self.add_side(0)
        self.corners[0].start()
        self.corners[1].start()
        self.add_side(1)
        self.nears[0].start()
        self.add_side(2)
        self.nears[2].start()

    def begin(self):
        self.prepare()
        me, _, over_x, over_y, corner = plane()
        turn = 1 - 2 * lax.rem(me, 2)
        self.product(corner + turn, 4)
        self.shares[0].start()
        self.product(corner, 0)
        self.product(over_x + turn, 5)
        self.shares[1].start()
        self.add_side(0)
        self.corners[0].start()
        self.corners[1].start()
        self.product(over_x, 1)
        self.product(over_y + turn, 6)
        self.shares[2].start()
        self.add_side(1)
        self.nears[0].start()
        self.product(over_y, 2)
        self.product(me + turn, 7)
        self.shares[3].start()
        self.add_side(2)
        self.nears[2].start()
        self.product(me, 3)

    def middle(self):
        self.add_corner(2, 0, 0)
        self.nears[3].start()
        self.add_corner(1, self.rows // 2, 1)
        self.nears[1].start()

    def end(self):
        self.shares[3].wait_recv()
        for copy in self.nears:
            copy.wait_recv()

    def run(self):
        self.begin()
        self.middle()
        self.end()

    def rows_of(self, span):
        return (
            self.part[3, span, :].astype(F32)
            + self.from_side[3, span, :].astype(F32)
            + self.from_near[0, span, :].astype(F32)
            + self.from_near[1, span, :].astype(F32)
        )

    def finish(self):
        for copy in self.shares + self.corners + self.nears:
            copy.wait_send()


def reduce_scratch(rows, width):
    dma = pltpu.SemaphoreType.DMA
    return [
        pltpu.VMEM((8, rows, width), BF16),
        pltpu.VMEM((4, rows, width), BF16),
        pltpu.VMEM((2, rows // 2, width), BF16),
        pltpu.VMEM((2, rows, width), BF16),
        dma((10,)),
        dma((10,)),
    ]


def gather_scratch(rows, width):
    dma = pltpu.SemaphoreType.DMA
    return [pltpu.VMEM((rows, width), BF16), dma((13,)), dma((13,)), dma(())]


def mean_rows(values):
    return jnp.mean(values, axis=-1, keepdims=True)


class Heads:
    def __init__(self, source, stage, arrive, send, recv_stage, recv):
        me, z = lax.axis_index("dp"), lax.axis_index("mp")
        self.me, self.z = me, z
        self.core = lax.rem(me, 2)
        self.source, self.stage, self.arrive = source, stage, arrive
        self.send, self.recv_stage, self.recv = send, recv_stage, recv
        self.place = z + self.core * (3 - 2 * z)
        self.columns = source.shape[1] // 2

    def z_of(self, place):
        return place + self.core * (3 - 2 * place)

    def slot_of(self, place):
        return self.core if place == 0 else 1 - self.core

    def rows_of(self, place, kind):
        block = 2 * kind + self.slot_of(place)
        return self.source.at[pl.ds(pl.multiple_of(block * LANES, LANES), HEAD_DIM)]

    def half_of(self, ref, half):
        return ref.at[:, pl.ds(pl.multiple_of(half * self.columns, LANES), self.columns)]

    def to_stage(self, place, kind):
        return to_at(
            self.rows_of(place, kind),
            self.stage.at[place, kind],
            self.send.at[place * 4 + kind],
            self.recv_stage.at[place * 4 + kind],
            self.me,
            self.z_of(2),
        )

    def to_owner(self, place, kind, half, way, ref, number):
        return to_at(
            self.half_of(ref, half),
            self.arrive.at[way, kind],
            self.send.at[number],
            self.recv.at[way * 4 + kind],
            self.me - self.core + half,
            self.z_of(place),
        )

    def sums(self, kind):
        return [
            self.to_owner(
                place, kind, half, 2, self.stage.at[place, kind], place * 8 + kind * 2 + half
            )
            for place in (0, 1)
            for half in (0, 1)
        ]

    def cross(self, own, kind):
        other = 1 - own
        copies = [
            self.to_owner(other, kind, half, 0, self.rows_of(other, kind), kind * 2 + half)
            for half in (0, 1)
        ]
        copies.append(
            to_at(
                self.half_of(self.rows_of(own, kind), 1 - self.core),
                self.arrive.at[1, kind],
                self.send.at[8 + kind],
                self.recv.at[4 + kind],
                self.me + 1 - 2 * self.core,
                self.z,
            )
        )
        return copies

    def start(self, kinds):
        @pl.when(self.place == 3)
        def _():
            for kind in kinds:
                self.to_stage(0, kind).start()
                self.to_stage(1, kind).start()

        for own in (0, 1):
            @pl.when(self.place == own)
            def _():
                for kind in kinds:
                    for copy in self.cross(own, kind):
                        copy.start()

    def add(self, kinds):
        @pl.when(self.place == 2)
        def _():
            for kind in kinds:
                for place in (0, 1):
                    self.to_stage(place, kind).wait_recv()
                    mine = self.rows_of(place, kind)

                    def body(span):
                        self.stage[place, kind, span, :] = (
                            self.stage[place, kind, span, :].astype(F32)
                            + mine[span, :].astype(F32)
                        ).astype(BF16)

                    each_chunk(HEAD_DIM, body, 16)
                for copy in self.sums(kind):
                    copy.start()

    def total(self, out):
        owner = lax.div(self.z, 2) == self.core
        for kind in range(4):
            for own in (0, 1):
                @pl.when(self.place == own)
                def _():
                    self.arrive[1, kind] = self.half_of(self.rows_of(own, kind), self.core)[...]

            for way in range(3):
                waiting = to_at(
                    self.half_of(self.rows_of(0, kind), 0),
                    self.arrive.at[way, kind],
                    self.send.at[0],
                    self.recv.at[way * 4 + kind],
                    self.me,
                    lax.rem(self.z + 1, 4),
                )
                if way == 1:
                    pl.when(jnp.logical_not(owner))(waiting.wait_recv)
                else:
                    waiting.wait_recv()

            def body(span):
                found = self.arrive[0, kind, span, :].astype(F32)
                found = found + self.arrive[1, kind, span, :].astype(F32)
                found = found + self.arrive[2, kind, span, :].astype(F32)
                target = pl.ds(pl.multiple_of(kind * HEAD_DIM + span.start, 16), 16)
                out[target, :] = found.astype(BF16)

            each_chunk(HEAD_DIM, body, 16)

    def finish_send(self):
        for kind in range(4):
            @pl.when(self.place == 3)
            def _():
                self.to_stage(0, kind).wait_send()
                self.to_stage(1, kind).wait_send()

            @pl.when(self.place == 2)
            def _():
                for copy in self.sums(kind):
                    copy.wait_send()

            for own in (0, 1):
                @pl.when(self.place == own)
                def _():
                    for copy in self.cross(own, kind):
                        copy.wait_send()


def to_at(source, target, send_sem, recv_sem, dp, mp):
    return pltpu.make_async_remote_copy(
        src_ref=source,
        dst_ref=target,
        send_sem=send_sem,
        recv_sem=recv_sem,
        device_id={"dp": dp, "mp": mp},
        device_id_type=MESH,
    )


def backward_kernel(
    branch, notes_all, kept_in, w_out_in, activated_in, low_all, high_all, middle_in, both_sum, down_in,
    out, result, branch_all, both_in, down_all,
    totals, query_part, key_value, ending, leaving, arriving, send, recv,
    part, from_side, from_corner, from_near, send_r, recv_r,
    mixed_grad, shard, load_sem, send_g, recv_g,
    both_stage, send_u, recv_u, local, down_found, send_d, recv_d,
    kept, w_out, activated, w_down, middle, fetch_sem,
    *, scale, groups, rows,
):
    z = lax.axis_index("mp")
    members = lax.axis_size("mp")
    barrier = greet_all()
    pairs = ((activated_in, activated), (w_out_in, w_out), (kept_in, kept), (middle_in, middle))
    fetches = [
        pltpu.make_async_copy(source, target, fetch_sem.at[number])
        for number, (source, target) in enumerate(pairs)
    ]
    load_down = pltpu.make_async_copy(down_in, down_found, load_sem.at[2])
    pl.semaphore_wait(barrier, 13)
    units = Units(lambda owner: both_sum.at[owner], both_in, both_stage, send_u, recv_u, local)
    gather = Gather(branch, branch_all, send_g, recv_g, local.at[2])
    gather.start()
    units.start()
    halves = start_all(load_halves(low_all, high_all, w_down, fetch_sem, 4))
    start_all(fetches)
    load_down.start()
    wait_all(halves + fetches[:1])
    reduce = Reduce(activated, w_down, False, part, from_side, from_corner, from_near, send_r, recv_r)
    reduce.products()
    load_down.wait()

    @pl.when((z == 0) | (z == members - 1))
    def _():
        down_found[members - 1 - z] = jnp.zeros_like(down_found[0])

    def add_down(span):
        value = down_found[0, span, :].astype(F32) + down_found[1, span, :].astype(F32)
        value = value + down_found[2, span, :].astype(F32) + down_found[3, span, :].astype(F32)
        down_found[0, span, :] = value.astype(BF16)

    each_chunk(down_found.shape[1], add_down)
    down = Gather(down_found.at[0], down_all, send_d, recv_d, local.at[1])

    def load_shard(turn):
        slot = turn % 2
        return pltpu.make_async_copy(branch_all.at[owner_at(turn)], shard.at[slot], load_sem.at[slot])

    def spread_back(turn, carry):
        for number, numbers in ARRIVALS:
            pl.when(turn == number)(functools.partial(gather.arrive, *numbers))

        @pl.when(turn == 0)
        def _():
            gather.keep.wait()

        load_shard(turn).start()
        load_shard(turn).wait()
        mixed_grad[owner_at(turn)] = (
            lax.dot_general(shard[turn % 2], w_out[...], NT, preferred_element_type=F32)
            .astype(BF16)
            .reshape(groups, rows // groups, 256)
        )
        return carry

    fetches[1].wait()
    lax.fori_loop(0, 8, spread_back, 0)
    reduce.launch()
    units.add()


    def halo(k, other):
        return to_mp(leaving.at[k], arriving.at[k], send.at[k], recv.at[k], other)

    def attend(k, carry):
        hot = hot_of(notes_all, k, rows)
        given = mixed_grad[:, pl.ds(k, 1)].reshape(rows, 256)
        grad_ordered = lax.dot_general(hot, given, TN, preferred_element_type=F32).astype(BF16)
        totals[...] = jnp.zeros_like(totals)
        for block in range(rows // 128):
            allowed = block_mask(notes_all, k, block, z, rows)
            for head in range(2):
                query = kept[k, pl.ds(64 + block * 128, 128), pl.ds(head * 128, 128)]
                keys = kept[k, pl.ds(block * 128, 192), pl.ds(256 + head * 128, 128)]
                values = kept[k, pl.ds(block * 128, 192), pl.ds(512 + head * 128, 128)]
                grad = grad_ordered[block * 128 : block * 128 + 128, head * 128 : head * 128 + 128]
                scores = lax.dot_general(query, keys, NT, preferred_element_type=F32) * scale
                scores = jnp.where(allowed, scores, -MASKED)
                weights = jnp.exp(scores - jnp.max(scores, axis=-1, keepdims=True))
                again = weights / jnp.sum(weights, axis=-1, keepdims=True)
                chance_grad = lax.dot_general(grad, values, NT, preferred_element_type=F32)
                row_dot = jnp.sum(again * chance_grad, axis=-1, keepdims=True)
                score_grad = (again * (chance_grad - row_dot)).astype(BF16)
                query_part[k, pl.ds(block * 128, 128), pl.ds(head * 128, 128)] = (
                    jnp.dot(score_grad, keys, preferred_element_type=F32) * scale
                ).astype(BF16)
                totals[pl.ds(block * 128, 192), pl.ds(head * 128, 128)] += (
                    lax.dot_general(score_grad, query, TN, preferred_element_type=F32) * scale
                )
                totals[pl.ds(block * 128, 192), pl.ds(256 + head * 128, 128)] += lax.dot_general(
                    again.astype(BF16), grad, TN, preferred_element_type=F32
                )
        key_value[k] = totals[pl.ds(64, rows), :].astype(BF16)
        ending[k] = totals[pl.ds(rows, 64), :]

        @pl.when(z > 0)
        def _():
            leaving[k] = totals[pl.ds(0, 64), :].astype(BF16)
            halo(k, z - 1).start()

        return carry

    wait_all(fetches[2:])
    lax.fori_loop(0, 3, attend, 0)
    reduce.middle()
    down.start()
    lax.fori_loop(3, 7, attend, 0)
    down.pass_on()
    lax.fori_loop(7, groups, attend, 0)

    def restore(k, carry):
        @pl.when(z < members - 1)
        def _():
            halo(k, z).wait_recv()
            key_value[k, pl.ds(rows - 64, 64), :] = (
                ending[k] + arriving[k].astype(F32)
            ).astype(BF16)

        hot = hot_of(notes_all, k, rows)
        ordered = jnp.concatenate([query_part[k], key_value[k]], axis=1)
        back = jnp.dot(hot, ordered, preferred_element_type=F32).astype(BF16)
        out[:, pl.ds(k, 1)] = back.reshape(groups, 1, rows // groups, 768)
        return carry

    lax.fori_loop(0, groups, restore, 0)
    reduce.end()

    def body(span):
        result[span, :] = (middle[span, :] + reduce.rows_of(span)).astype(BF16)

    each_chunk(rows, body)
    down.finish()
    units.finish()
    for copy in gather.copies:
        copy.wait_send()
    reduce.finish()

    @pl.when(z > 0)
    def _():
        def done(k, carry):
            halo(k, z - 1).wait_send()
            return carry

        lax.fori_loop(0, groups, done, 0)


def attend_back(
    branch, notes_all, kept, w_out, activated, low_all, high_all, middle, both_sum, down_in, scale
):
    groups = kept.shape[0]
    rows, width = middle.shape
    members = both_sum.shape[0]
    dma = pltpu.SemaphoreType.DMA
    shape = jax.ShapeDtypeStruct
    return pl.pallas_call(
        functools.partial(backward_kernel, scale=scale, groups=groups, rows=rows),
        out_shape=(
            shape((groups, groups, rows // groups, 768), BF16),
            shape((rows, width), BF16),
            shape((groups, rows, width), BF16),
            shape((members, width, 256), BF16),
            shape((groups, LANES, width), BF16),
        ),
        in_specs=[on_chip()] * 2 + [anywhere()] * 8,
        out_specs=(on_chip(),) * 2 + (anywhere(),) * 3,
        scratch_shapes=[
            pltpu.VMEM((rows + 64, 512), F32),
            pltpu.VMEM((groups, rows, 256), BF16),
            pltpu.VMEM((groups, rows, 512), BF16),
            pltpu.VMEM((groups, 64, 512), F32),
            pltpu.VMEM((groups, 64, 512), BF16),
            pltpu.VMEM((groups, 64, 512), BF16),
            dma((groups,)),
            dma((groups,)),
        ]
        + reduce_scratch(rows, width)
        + [
            pltpu.VMEM((groups, groups, rows // groups, 256), BF16),
            pltpu.VMEM((2, rows, width), BF16),
            dma((3,)),
            dma((13,)),
            dma((13,)),
            pltpu.VMEM((2, width, 256), BF16),
            dma((6,)),
            dma((10,)),
            dma((3,)),
            pltpu.VMEM((members, LANES, width), BF16),
            dma((13,)),
            dma((13,)),
            pltpu.VMEM(kept.shape, BF16),
            pltpu.VMEM(w_out.shape, BF16),
            pltpu.VMEM(activated.shape, BF16),
            pltpu.VMEM((members * LANES, width), BF16),
            pltpu.VMEM((rows, width), F32),
            dma((4 + 2 * members,)),
        ],
        compiler_params=remote_params(3, 63 * 1024 * 1024),
        cost_estimate=pl.CostEstimate(flops=0, bytes_accessed=300_000_000, transcendentals=0),
        name="attend_back",
    )(branch, notes_all, kept, w_out, activated, low_all, high_all, middle, both_sum, down_in)


def middle_kernel(
    mixed, w_out, tokens, gain, w_up, w_down, middle, hidden, up_all, down_all,
    part, from_side, from_corner, from_near, send, recv, up_own, down_own,
    send_u, recv_u, send_d, recv_d, local,
):
    barrier = greet_all()
    units = pl.ds(pl.multiple_of(lax.axis_index("dp") * LANES, LANES), LANES)
    high_units = pl.ds(
        pl.multiple_of(lax.axis_index("dp") * LANES + LANES // 2, LANES // 2), LANES // 2
    )
    loads = [
        pltpu.make_async_copy(w_up.at[:, units], up_own, local.at[0]),
        pltpu.make_async_copy(w_down.at[high_units], down_own, local.at[1]),
    ]
    for copy in loads:
        copy.start()
    pl.semaphore_wait(barrier, 13)
    for copy in loads:
        copy.wait()
    columns = [
        Column(up_own, up_all, send_u, recv_u, local.at[0]),
        Column(down_own, down_all, send_d, recv_d, local.at[1]),
    ]
    for column in columns:
        column.start()
    reduce = Reduce(mixed, w_out, False, part, from_side, from_corner, from_near, send, recv)
    reduce.begin()
    reduce.middle()
    for column in columns:
        column.pass_on()
    reduce.end()

    def body(span):
        values = tokens[span, :].astype(F32) + reduce.rows_of(span)
        middle[span, :] = values
        inverse = lax.rsqrt(mean_rows(values * values) + EPSILON)
        hidden[span, :] = (values * inverse * gain[...]).astype(BF16)

    each_chunk(hidden.shape[0], body)
    for column in columns:
        column.finish()
    reduce.finish()


def project_middle(mixed, w_out, tokens, gain, w_up, w_down):
    rows, width = tokens.shape
    dma = pltpu.SemaphoreType.DMA
    members = lax.axis_size("mp")
    return pl.pallas_call(
        middle_kernel,
        out_shape=(
            jax.ShapeDtypeStruct((rows, width), F32),
            jax.ShapeDtypeStruct((rows, width), BF16),
            jax.ShapeDtypeStruct((members, width, LANES), BF16),
            jax.ShapeDtypeStruct((members, LANES // 2, width), BF16),
        ),
        in_specs=[on_chip()] * 4 + [anywhere()] * 2,
        out_specs=(on_chip(), on_chip(), anywhere(), anywhere()),
        scratch_shapes=reduce_scratch(rows, width)
        + [
            pltpu.VMEM((width, LANES), BF16),
            pltpu.VMEM((LANES // 2, width), BF16),
            dma((4,)),
            dma((4,)),
            dma((4,)),
            dma((4,)),
            dma((2,)),
        ],
        compiler_params=remote_params(4),
        cost_estimate=pl.CostEstimate(flops=0, bytes_accessed=150_000_000, transcendentals=0),
        name="project_middle",
    )(mixed, w_out, tokens, gain, w_up, w_down)


def norm_back_rows(gradient, values, gain, sums, span):
    inverse = lax.rsqrt(mean_rows(values * values) + EPSILON)
    normed = values * inverse
    product = gradient * normed
    folded = product[0:8]
    for step in range(1, CHUNK // 8):
        folded = folded + product[step * 8 : step * 8 + 8]
    sums[...] += folded
    scaled = gradient * gain
    return inverse * (scaled - normed * mean_rows(scaled * normed))


def load_halves(low_all, high_all, weight, sems, first):
    half = low_all.shape[1]
    return [
        pltpu.make_async_copy(
            source.at[z], weight.at[pl.ds((2 * z + number) * half, half)], sems.at[first + 2 * z + number]
        )
        for z in range(low_all.shape[0])
        for number, source in enumerate((low_all, high_all))
    ]


def feed_kernel(
    hidden_own, cotangent_all, middle, gate_all, up_all, cotangent_own, low_all, high_all, gain,
    middle_grad, branch, sums, activated_out, both_sum, down_in,
    hidden_all, both_grad, part, from_side, from_corner, from_near, send_r, recv_r,
    send_a, recv_a, cot_shard, cot_tile, stage_both, down_sum, w_both, w_down, cotangent, activated,
    load_sem, local, send_z, recv_z, stage_down,
):
    groups, rows, width = hidden_all.shape
    members = gate_all.shape[0]
    me = lax.axis_index("dp")
    barrier = greet_all()
    own = pltpu.make_async_copy(hidden_own, hidden_all.at[me], local.at[0])
    own.start()
    start_middle = pltpu.make_async_copy(middle, middle_grad, local.at[1])
    loads = [
        pltpu.make_async_copy(
            source.at[z], w_both.at[:, pl.ds(z * 256 + offset, 128)], load_sem.at[6 + 2 * z + number]
        )
        for z in range(members)
        for number, (source, offset) in enumerate(((gate_all, 0), (up_all, 128)))
    ]

    def slot_of(turn):
        block = turn // 2
        near = ((block + 1) // 2) % 2
        far = block // 3
        second = turn % 2
        other = (1 - near) * second + (block // 2) * near
        return 4 * other + 3 * (1 - near) * (1 - far) + near * (1 + second)

    def load_cotangent(turn):
        return pltpu.make_async_copy(
            cotangent_all.at[owner_at(turn)], cot_shard.at[turn % 2], load_sem.at[turn % 2]
        )

    loads += load_halves(low_all, high_all, w_down, load_sem, 6 + 2 * members)
    load_own = pltpu.make_async_copy(cotangent_own, cotangent, local.at[3])
    start_all(loads)
    load_cotangent(0).start()
    own.wait()
    pl.semaphore_wait(barrier, 13)
    gather = Gather(None, hidden_all, send_a, recv_a)
    gather.start()
    reduce = Reduce(None, None, False, part, from_side, from_corner, from_near, send_r, recv_r)
    reduce.prepare()

    def nears():
        reduce.add_side(1)
        reduce.nears[0].start()
        reduce.add_side(2)
        reduce.nears[2].start()

    early = [(turn, functools.partial(gather.arrive, *numbers)) for turn, numbers in ARRIVALS]
    early += [(6, nears)]
    late = [(1, 3), (4, 1), (5, 2), (7, 0)]
    start_middle.start()
    load_own.start()
    wait_all(loads)

    def unit(turn, carry):
        for number, action in early:
            pl.when(turn == number)(action)

        @pl.when(turn < 7)
        def _():
            load_cotangent(turn + 1).start()

        load_cotangent(turn).wait()
        owner, slot = owner_at(turn), slot_of(turn)
        mine = hidden_all[owner]
        grads = cot_shard[turn % 2]
        for z in range(members):
            raw = jnp.dot(mine, w_both[:, z * 256 : z * 256 + 256], preferred_element_type=F32)
            units = pl.ds(z * 128, 128)
            if z % 2 == 0:
                pair = lax.dot_general(
                    grads, w_down[pl.ds(z * 128, 256), :], NT, preferred_element_type=F32
                )
            active_grad = pair[:, 128 * (z % 2) : 128 * (z % 2) + 128]
            gate, upward = raw[:, :128], raw[:, 128:]
            sigmoid = jax.nn.sigmoid(gate)
            activated[owner, :, units] = (gate * sigmoid * upward).astype(BF16)
            both_grad[owner, :, pl.ds(z * 256, 128)] = (
                active_grad * upward * sigmoid * (1.0 + gate * (1.0 - sigmoid))
            ).astype(BF16)
            both_grad[owner, :, pl.ds(z * 256 + 128, 128)] = (
                active_grad * gate * sigmoid
            ).astype(BF16)

        def tile(t, inner):
            columns = pl.ds(pl.multiple_of(t * 256, 256), 256)
            part[slot, :, columns] = lax.dot_general(
                both_grad[owner], w_both[columns, :], NT, preferred_element_type=F32
            ).astype(BF16)
            return inner

        lax.fori_loop(0, width // 256, tile, 0)
        for number, share in late:
            pl.when(turn == number)(reduce.shares[share].start)
        return carry

    lax.fori_loop(0, 8, unit, 0)
    store_activated = pltpu.make_async_copy(activated, activated_out, local.at[4])
    store_activated.start()

    def load_tile(t):
        columns = pl.ds(pl.multiple_of(t * 256, 256), 256)
        return pltpu.make_async_copy(
            cotangent_all.at[:, :, columns], cot_tile.at[t % 2], load_sem.at[2 + t % 2]
        )

    def store_both(t):
        columns = pl.ds(pl.multiple_of(t * 256, 256), 256)
        return pltpu.make_async_copy(
            stage_both.at[t % 2], both_sum.at[:, columns], load_sem.at[4 + t % 2]
        )

    tiles = width // 256
    count = groups * rows

    def down_tile(t, carry):
        columns = pl.ds(pl.multiple_of(t * 256, 256), 256)

        @pl.when(t < tiles - 1)
        def _():
            load_tile(t + 1).start()

        load_tile(t).wait()
        down_sum[:, columns] = lax.dot_general(
            activated[...].reshape(count, members * 128),
            cot_tile[t % 2].reshape(count, 256),
            TN,
            preferred_element_type=F32,
        ).astype(BF16)
        return carry

    z = lax.axis_index("mp")

    def down_rows(owner):
        return down_sum.at[pl.ds(pl.multiple_of(owner * LANES, LANES), LANES)]

    keep_down = pltpu.make_async_copy(down_rows(z), down_in.at[z], local.at[5])
    passing = Units(down_rows, down_in, stage_down, send_z, recv_z, local.at[pl.ds(6, 1)])

    def weight_tile(t, carry):
        columns = pl.ds(pl.multiple_of(t * 256, 256), 256)

        @pl.when(t >= 2)
        def _():
            store_both(t - 2).wait()

        value = lax.dot_general(
            hidden_all[:, :, columns].reshape(count, 256),
            both_grad[...].reshape(count, members * 256),
            TN,
            preferred_element_type=F32,
        )
        for z in range(members):
            stage_both[t % 2, z] = value[:, z * 256 : z * 256 + 256].astype(BF16)
        store_both(t).start()
        return carry

    load_tile(0).start()
    reduce.add_side(0)
    reduce.corners[0].start()
    reduce.corners[1].start()
    lax.fori_loop(0, tiles, down_tile, 0)
    keep_down.start()
    passing.start()
    lax.fori_loop(0, 2, weight_tile, 0)
    reduce.middle()
    passing.add()
    lax.fori_loop(2, tiles, weight_tile, 0)
    reduce.end()
    start_middle.wait()
    load_own.wait()
    sums[...] = jnp.zeros_like(sums)

    def body(span):
        change = norm_back_rows(reduce.rows_of(span), middle_grad[span, :], gain[...], sums, span)
        total = cotangent[span, :].astype(F32) + change
        middle_grad[span, :] = total
        branch[span, :] = total.astype(BF16)

    each_chunk(rows, body)
    gather.sent()
    reduce.finish()
    for t in (tiles - 2, tiles - 1):
        store_both(t).wait()
    keep_down.wait()
    store_activated.wait()
    passing.finish()


def feed(hidden_own, cotangent_all, middle, gate_all, up_all, cotangent, low_all, high_all, gain):
    groups, rows, width = cotangent_all.shape
    members = gate_all.shape[0]
    dma = pltpu.SemaphoreType.DMA
    units = members * 128
    return pl.pallas_call(
        feed_kernel,
        out_shape=(
            jax.ShapeDtypeStruct((rows, width), F32),
            jax.ShapeDtypeStruct((rows, width), BF16),
            jax.ShapeDtypeStruct((8, width), F32),
            jax.ShapeDtypeStruct((groups, rows, units), BF16),
            jax.ShapeDtypeStruct((members, width, 256), BF16),
            jax.ShapeDtypeStruct((members, LANES, width), BF16),
        ),
        in_specs=[anywhere()] * 8 + [on_chip()],
        out_specs=(on_chip(),) * 3 + (anywhere(),) * 3,
        scratch_shapes=[
            pltpu.VMEM((groups, rows, width), BF16),
            pltpu.VMEM((groups, rows, 2 * units), BF16),
        ]
        + reduce_scratch(rows, width)
        + [
            dma((13,)),
            dma((13,)),
            pltpu.VMEM((2, rows, width), BF16),
            pltpu.VMEM((2, groups, rows, 256), BF16),
            pltpu.VMEM((2, members, 256, 256), BF16),
            pltpu.VMEM((units, width), BF16),
            pltpu.VMEM((width, 2 * units), BF16),
            pltpu.VMEM((units, width), BF16),
            pltpu.VMEM((rows, width), BF16),
            pltpu.VMEM((groups, rows, units), BF16),
            dma((6 + 4 * members,)),
            dma((7,)),
            dma((6,)),
            dma((10,)),
            pltpu.VMEM((2, LANES, width), BF16),
        ],
        compiler_params=remote_params(5, 63 * 1024 * 1024),
        cost_estimate=pl.CostEstimate(flops=0, bytes_accessed=400_000_000, transcendentals=0),
        name="feed",
    )(hidden_own, cotangent_all, middle, gate_all, up_all, cotangent, low_all, high_all, gain)


def input_kernel(
    qkv_grad, w_qkv, hidden_all, branch_all, mixed_in, tokens_in, middle_in, gain, sums_two,
    both_sum, both_in,
    result, gains, both_all, heads_all,
    part, from_side, from_corner, from_near, send, recv, sums,
    stage, arrive, send_h, recv_s, recv_h, own, plane_sums, column_sums, send_p, recv_p,
    weight_sum, row_tile, tile_sem, send_b, recv_b, send_t, recv_t, both_found, heads_own, local,
    mixed, tokens, middle_grad, fetch_sem,
):
    me, z = lax.axis_index("dp"), lax.axis_index("mp")
    barrier = greet_all()
    count = qkv_grad.shape[0]
    tiles = tokens.shape[1] // 256
    outer = (z == 0) | (z == 3)

    def columns_of(t):
        return pl.ds(pl.multiple_of(lax.rem(t, tiles) * 256, 256), 256)

    def load(t, source):
        return pltpu.make_async_copy(
            source.at[:, :, columns_of(t)], row_tile.at[t % 2], tile_sem.at[t % 2]
        )

    own_part = pltpu.make_async_copy(both_sum.at[z], both_found.at[0], local.at[0])
    own_part.start()
    ways = [(outer, 1, 1), (outer, 2, 2)]
    ways += [(z == 1, 0, 1), (z == 1, 2, 2), (z == 1, 3, 3)]
    ways += [(z == 2, 0, 1), (z == 2, 1, 2), (z == 2, 3, 3)]

    def came(source, place):
        return pltpu.make_async_copy(both_in.at[source], both_found.at[place], local.at[place])

    for here, source, place in ways:
        pl.when(here)(came(source, place).start)

    @pl.when(outer)
    def _():
        both_found[3] = jnp.zeros_like(both_found[3])

    load(0, hidden_all).start()
    fetches = start_all(
        [
            pltpu.make_async_copy(source, target, fetch_sem.at[number])
            for number, (source, target) in enumerate(
                ((mixed_in, mixed), (tokens_in, tokens), (middle_in, middle_grad))
            )
        ]
    )
    pl.semaphore_wait(barrier, 13)
    both = Gather(both_found.at[0], both_all, send_b, recv_b, local.at[4])

    def weight_tile(t, carry):
        @pl.when(t < tiles - 1)
        def _():
            load(t + 1, hidden_all).start()

        @pl.when((t >= tiles - 1) & (t < 2 * tiles - 1))
        def _():
            load(t + 1, branch_all).start()

        load(t, hidden_all).wait()

        @pl.when(t < tiles)
        def _():
            weight_sum[pl.ds(0, 768), columns_of(t)] = lax.dot_general(
                qkv_grad[...], row_tile[t % 2].reshape(count, 256), TN, preferred_element_type=F32
            ).astype(BF16)

        @pl.when(t >= tiles)
        def _():
            weight_sum[pl.ds(768, 256), columns_of(t)] = lax.dot_general(
                mixed[...], row_tile[t % 2].reshape(count, 256), TN, preferred_element_type=F32
            ).astype(BF16)

        return carry

    heads = Heads(weight_sum, stage, arrive, send_h, recv_s, recv_h)
    reduce = Reduce(qkv_grad, w_qkv, False, part, from_side, from_corner, from_near, send, recv)
    own_part.wait()
    for here, source, place in ways:
        pl.when(here)(came(source, place).wait)

    def add(span):
        value = both_found[0, span, :].astype(F32) + both_found[1, span, :].astype(F32)
        value = value + both_found[2, span, :].astype(F32) + both_found[3, span, :].astype(F32)
        both_found[0, span, :] = value.astype(BF16)

    each_chunk(both_found.shape[1], add)
    both.start()
    lax.fori_loop(0, tiles, weight_tile, 0)
    heads.start((0, 1, 2))
    wait_all(fetches)
    lax.fori_loop(tiles, 2 * tiles, weight_tile, 0)
    heads.start((3,))
    both.pass_on()
    reduce.begin()
    heads.add((0, 1))
    reduce.middle()
    heads.add((2, 3))
    reduce.end()
    sums[...] = jnp.zeros_like(sums)

    def body(span):
        values = tokens[span, :].astype(F32)
        change = norm_back_rows(reduce.rows_of(span), values, gain[...], sums, span)
        result[span, :] = (middle_grad[span, :] + change).astype(BF16)

    each_chunk(result.shape[0], body)
    own[...] = jnp.concatenate(
        [
            jnp.sum(sums[...], axis=0, keepdims=True),
            jnp.sum(sums_two[...], axis=0, keepdims=True),
        ],
        axis=0,
    )
    swaps = swap_all(own, plane_sums, send_p, recv_p)
    for copy in swaps:
        copy.start()
    plane_sums[me] = own[...]
    heads.total(heads_own)
    gather = Gather(heads_own, heads_all, send_t, recv_t, local.at[5])
    gather.start()
    for copy in swaps:
        copy.wait()
    found = plane_sums[0]
    for other in range(1, 8):
        found = found + plane_sums[other]
    column_sums[z] = found
    passes = [
        to_mp(
            column_sums.at[z],
            column_sums.at[z],
            send_p.at[6 + step],
            recv_p.at[6 + step],
            lax.rem(z + step, 4),
        )
        for step in range(1, 4)
    ]
    for copy in passes:
        copy.start()
    both.finish()
    for copy in passes:
        copy.wait()
    gains[...] = (column_sums[0] + column_sums[1]) + (column_sums[2] + column_sums[3])
    gather.pass_on()
    heads.finish_send()
    reduce.finish()
    gather.finish()


def project_input(
    qkv_grad, w_qkv, hidden_all, branch_all, mixed, tokens, middle_grad, gain, sums_two,
    both_sum, both_in,
):
    rows, width = tokens.shape
    groups = hidden_all.shape[0]
    dma = pltpu.SemaphoreType.DMA
    shape = jax.ShapeDtypeStruct
    return pl.pallas_call(
        input_kernel,
        out_shape=(
            shape((rows, width), BF16),
            shape((2, width), F32),
            shape((groups, width, 256), BF16),
            shape((groups, 4 * HEAD_DIM, width // 2), BF16),
        ),
        in_specs=[on_chip()] * 2 + [anywhere()] * 5 + [on_chip()] * 2 + [anywhere()] * 2,
        out_specs=(on_chip(),) * 2 + (anywhere(),) * 2,
        scratch_shapes=reduce_scratch(rows, width)
        + [
            pltpu.VMEM((8, width), F32),
            pltpu.VMEM((2, 4, HEAD_DIM, width), BF16),
            pltpu.VMEM((3, 4, HEAD_DIM, width // 2), BF16),
            dma((16,)),
            dma((8,)),
            dma((12,)),
            pltpu.VMEM((2, width), F32),
            pltpu.VMEM((8, 2, width), F32),
            pltpu.VMEM((4, 2, width), F32),
            dma((10,)),
            dma((10,)),
            pltpu.VMEM((8 * LANES, width), BF16),
            pltpu.VMEM((2, groups, rows, 256), BF16),
            dma((2,)),
            dma((13,)),
            dma((13,)),
            dma((13,)),
            dma((13,)),
            pltpu.VMEM((4, width, 256), BF16),
            pltpu.VMEM((4 * HEAD_DIM, width // 2), BF16),
            dma((6,)),
            pltpu.VMEM(mixed.shape, BF16),
            pltpu.VMEM((rows, width), BF16),
            pltpu.VMEM((rows, width), F32),
            dma((3,)),
        ],
        compiler_params=remote_params(6, 63 * 1024 * 1024),
        cost_estimate=pl.CostEstimate(flops=0, bytes_accessed=250_000_000, transcendentals=0),
        name="project_input",
    )(
        qkv_grad, w_qkv, hidden_all, branch_all, mixed, tokens, middle_grad, gain, sums_two,
        both_sum, both_in,
    )


def assemble_kernel(
    both, down, heads, order_column, output_b, input_b,
    output, inputs, query, keys, values, project, gate, upward, down_out,
):
    for d in range(both.shape[0]):
        gate[:, d * 128 : d * 128 + 128] = both[d, :, :128].astype(F32)
        upward[:, d * 128 : d * 128 + 128] = both[d, :, 128:].astype(F32)
    down_out[...] = down[0].astype(F32)
    for kind, out in enumerate((query, keys, values, project)):
        out[...] = heads[0, kind].astype(F32)
    place = lax.broadcasted_iota(jnp.int32, (order_column.shape[0], output_b.shape[0]), 1)
    unsort = (place.astype(F32) == order_column[...]).astype(BF16)
    output[...] = jnp.dot(unsort, output_b[...], preferred_element_type=F32).astype(BF16)
    inputs[...] = jnp.dot(unsort, input_b[...], preferred_element_type=F32).astype(BF16)


def assemble(both, down, heads, order_column, output_b, input_b):
    groups, width, wide = both.shape
    rows = output_b.shape[0]
    units = down.shape[1]
    chips = groups // 2
    columns = heads.shape[3]
    row_tile, tile = rows // groups, width // groups
    shape = jax.ShapeDtypeStruct
    head = shape((chips * HEAD_DIM, 2 * columns), F32)
    head_spec = pl.BlockSpec((HEAD_DIM, columns), lambda i: (i // 2, i % 2))
    wide_spec = pl.BlockSpec((tile, groups * units), lambda i: (i, 0))
    row_spec = pl.BlockSpec((row_tile, width), lambda i: (i, 0))
    whole_spec = pl.BlockSpec((rows, width), lambda i: (0, 0))
    return pl.pallas_call(
        assemble_kernel,
        grid=(groups,),
        out_shape=(
            shape((rows, width), BF16),
            shape((rows, width), BF16),
            head,
            head,
            head,
            head,
            shape((width, groups * units), F32),
            shape((width, groups * units), F32),
            shape((groups * units, width), F32),
        ),
        in_specs=[
            pl.BlockSpec((groups, tile, wide), lambda i: (0, i, 0)),
            pl.BlockSpec((1, units, width), lambda i: (i, 0, 0)),
            pl.BlockSpec((1, 4, HEAD_DIM, columns), lambda i: (i, 0, 0, 0)),
            pl.BlockSpec((row_tile, 1), lambda i: (i, 0)),
            whole_spec,
            whole_spec,
        ],
        out_specs=(
            row_spec, row_spec, head_spec, head_spec, head_spec, head_spec, wide_spec, wide_spec,
            pl.BlockSpec((units, width), lambda i: (i, 0)),
        ),
        compiler_params=pltpu.CompilerParams(vmem_limit_bytes=VMEM_LIMIT),
        cost_estimate=pl.CostEstimate(flops=0, bytes_accessed=58_000_000, transcendentals=0),
        name="assemble",
    )(both, down, heads, order_column, output_b, input_b)


def swapped(
    tokens, cotangent, route, lengths, key_mask, norm1_gain, norm2_gain,
    w_query, w_key, w_value, w_out, w_gate, w_up, w_down,
):
    groups = lax.axis_size("dp")
    members = lax.axis_size("mp")
    me = lax.axis_index("dp")
    z = lax.axis_index("mp")
    rows, width = tokens.shape
    bucket = rows // groups
    units = w_down.shape[0] // groups

    target = route // TOK_DEV
    earlier = jnp.arange(rows, dtype=jnp.int32)
    same = (target[:, None] == target[None, :]) & (earlier[None, :] < earlier[:, None])
    send_at = target * bucket + jnp.sum(same.astype(jnp.int32), axis=1)
    sorting = send_at[None, :] == earlier[:, None]
    slots_own = jnp.sum(jnp.where(sorting, (route % rows)[None, :], 0), axis=1)

    mask_window = lax.dynamic_slice_in_dim(
        jnp.concatenate([jnp.zeros((WINDOW,), jnp.int32), key_mask]), z * rows, rows + WINDOW
    )
    slot_rows = jnp.pad(slots_own.reshape(groups, bucket).T, ((0, 0), (0, LANES - groups)))
    mask_rows = jnp.pad(mask_window, (0, 4 * LANES - rows - WINDOW)).reshape(4, LANES)
    length_rows = jnp.pad(lengths, ((0, 3), (0, LANES - lengths.shape[1])))
    notes = jnp.concatenate([slot_rows, mask_rows, length_rows], axis=0).astype(F32)

    count = groups * rows
    scale = HEAD_DIM ** (-0.5)
    (
        hidden_one,
        w_qkv,
        w_proj,
        notes_all,
        gate_all,
        mixed,
        kept,
        tokens_b,
        cotangent_b,
        cotangent_all,
        low_all,
    ) = attend_ahead(
        tokens,
        cotangent,
        send_at.astype(F32)[None],
        norm1_gain[None],
        notes,
        w_query.T,
        w_key.T,
        w_value.T,
        w_out,
        w_gate,
        w_down,
        scale,
    )
    mixed = mixed.reshape(count, 2 * LANES)
    middle, hidden_two, up_all, high_all = project_middle(
        mixed, w_proj, tokens_b, norm2_gain[None], w_up, w_down
    )
    middle_grad, branch, sums_two, activated, both_sum, down_in = feed(
        hidden_two,
        cotangent_all,
        middle,
        gate_all,
        up_all,
        cotangent_b,
        low_all,
        high_all,
        norm2_gain[None],
    )
    qkv_grad, output_rows, branch_all, both_in, down_whole = attend_back(
        branch,
        notes_all,
        kept,
        w_proj,
        activated.reshape(count, units * members),
        low_all,
        high_all,
        middle,
        both_sum,
        down_in,
        scale,
    )
    qkv_grad = qkv_grad.reshape(count, 6 * LANES)
    input_rows, gain_sums, both_whole, heads_whole = project_input(
        qkv_grad,
        w_qkv,
        hidden_one,
        branch_all,
        mixed,
        tokens_b,
        middle_grad,
        norm1_gain[None],
        sums_two,
        both_sum,
        both_in,
    )
    (
        output,
        input_grad,
        query_grad,
        key_grad,
        value_grad,
        proj_grad,
        gate_grad,
        up_grad,
        down_grad,
    ) = assemble(
        both_whole,
        down_whole,
        heads_whole.reshape(groups, 4, HEAD_DIM, width // 2),
        send_at.astype(F32)[:, None],
        output_rows,
        input_rows,
    )
    return (
        output,
        input_grad,
        gain_sums[0],
        gain_sums[1],
        query_grad.T,
        key_grad.T,
        value_grad.T,
        proj_grad,
        gate_grad,
        up_grad,
        down_grad,
    )


def solution(mesh):
    in_specs = (
        P(("dp", "mp"), None),
        P(("dp", "mp"), None),
        P(("dp", "mp")),
        P("dp", None),
        P("dp"),
        P(),
        P(),
        P(None, "mp"),
        P(None, "mp"),
        P(None, "mp"),
        P("mp", None),
        P(None, "mp"),
        P(None, "mp"),
        P("mp", None),
    )
    out_specs = (
        P(("dp", "mp"), None),
        P(("dp", "mp"), None),
        P(),
        P(),
        P(None, "mp"),
        P(None, "mp"),
        P(None, "mp"),
        P("mp", None),
        P(None, "mp"),
        P(None, "mp"),
        P("mp", None),
    )
    body = swapped if (mesh.shape["dp"], mesh.shape["mp"]) == (8, 4) else local
    return jax.shard_map(body, mesh=mesh, in_specs=in_specs, out_specs=out_specs, check_vma=False)
```

```python
import functools

import jax
import jax.numpy as jnp
from jax import lax
from jax.experimental import pallas as pl
from jax.experimental.pallas import tpu as pltpu
from jax.sharding import PartitionSpec as P

HEAD_DIM = 112
WINDOW = 64
TOK_DEV = 1536


EPSILON = 1e-05
MASKED = 1e30


def norm_rows(values):
    inverse = lax.rsqrt(jnp.mean(values * values, axis=-1, keepdims=True) + EPSILON)
    return (values * inverse, inverse)


def norm_back(gradient, normed, inverse, norm_gain):
    scaled = gradient * norm_gain
    result = inverse * (scaled - normed * jnp.mean(scaled * normed, axis=-1, keepdims=True))
    return (result, jnp.sum(gradient * normed, axis=0))


def padded(values, filler):
    front = jnp.full((WINDOW,) + values.shape[1:], filler, values.dtype)
    return jnp.concatenate([front, values], axis=0)


def block_scores(query_block, key_block, query_seg, key_seg, key_flag, first_row, score_scale):
    query_pos = first_row + jnp.arange(query_block.shape[0], dtype=jnp.int32)
    key_pos = first_row - WINDOW + jnp.arange(key_block.shape[0], dtype=jnp.int32)
    distance = query_pos[:, None] - key_pos[None, :]
    allowed = (distance >= 0) & (distance < WINDOW) & (query_seg[:, None] == key_seg[None, :])
    allowed = allowed & ((key_flag[None, :] == 1) | (distance == 0))
    raw_scores = (
        jnp.einsum("qhd,khd->hqk", query_block, key_block, preferred_element_type=jnp.float32)
        * score_scale
    )
    return jnp.where(allowed[None], raw_scores, -MASKED)


def block_inputs(query, key_pad, value_pad, segment, seg_pad, live_pad, first_row, block_rows):
    key_span = block_rows + WINDOW
    return (
        lax.dynamic_slice_in_dim(query, first_row, block_rows, 0),
        lax.dynamic_slice_in_dim(key_pad, first_row, key_span, 0),
        lax.dynamic_slice_in_dim(value_pad, first_row, key_span, 0),
        lax.dynamic_slice_in_dim(segment, first_row, block_rows, 0),
        lax.dynamic_slice_in_dim(seg_pad, first_row, key_span, 0),
        lax.dynamic_slice_in_dim(live_pad, first_row, key_span, 0),
    )


def attend_forward(query, key_all, value_all, segment, key_live):
    token_count, head_count, head_width = query.shape
    block_rows = min(512, token_count)
    score_scale = head_width ** (-0.5)
    key_pad = padded(key_all, 0.0)
    value_pad = padded(value_all, 0.0)
    seg_pad = padded(segment, -1)
    live_pad = padded(key_live, 0)

    def one_block(running, block_index):
        first_row = block_index * block_rows
        query_block, key_block, value_block, query_seg, key_seg, key_flag = block_inputs(
            query, key_pad, value_pad, segment, seg_pad, live_pad, first_row, block_rows
        )
        scores = block_scores(
            query_block, key_block, query_seg, key_seg, key_flag, first_row, score_scale
        )
        row_max = jnp.max(scores, axis=-1, keepdims=True)
        weights = jnp.exp(scores - row_max)
        denominator = jnp.sum(weights, axis=-1, keepdims=True)
        chances = (weights / denominator).astype(jnp.bfloat16)
        mixed = jnp.einsum("hqk,khd->qhd", chances, value_block, preferred_element_type=jnp.float32)
        return (
            running,
            (mixed.astype(jnp.bfloat16), row_max[..., 0] + jnp.log(denominator[..., 0])),
        )

    _, (mixed, logsum) = lax.scan(
        one_block, jnp.zeros((), jnp.int32), jnp.arange(token_count // block_rows, dtype=jnp.int32)
    )
    return (mixed.reshape(token_count, head_count * head_width), logsum)


def attend_backward(query, key_all, value_all, segment, key_live, logsum, mixed_grad):
    token_count, head_count, head_width = query.shape
    block_rows = min(512, token_count)
    key_span = block_rows + WINDOW
    score_scale = head_width ** (-0.5)
    key_pad = padded(key_all, 0.0)
    value_pad = padded(value_all, 0.0)
    seg_pad = padded(segment, -1)
    live_pad = padded(key_live, 0)

    def one_block(running, inputs):
        key_grad, value_grad = running
        block_index, block_logsum = inputs
        first_row = block_index * block_rows
        query_block, key_block, value_block, query_seg, key_seg, key_flag = block_inputs(
            query, key_pad, value_pad, segment, seg_pad, live_pad, first_row, block_rows
        )
        grad_block = lax.dynamic_slice_in_dim(mixed_grad, first_row, block_rows, 0)
        scores = block_scores(
            query_block, key_block, query_seg, key_seg, key_flag, first_row, score_scale
        )
        chances = jnp.exp(scores - block_logsum[..., None])
        chance_grad = jnp.einsum(
            "qhd,khd->hqk", grad_block, value_block, preferred_element_type=jnp.float32
        )
        row_dot = jnp.sum(chances * chance_grad, axis=-1, keepdims=True)
        score_grad = (chances * (chance_grad - row_dot)).astype(jnp.bfloat16)
        query_grad = (
            jnp.einsum("hqk,khd->qhd", score_grad, key_block, preferred_element_type=jnp.float32)
            * score_scale
        )
        key_part = (
            jnp.einsum("hqk,qhd->khd", score_grad, query_block, preferred_element_type=jnp.float32)
            * score_scale
        )
        value_part = jnp.einsum(
            "hqk,qhd->khd",
            chances.astype(jnp.bfloat16),
            grad_block,
            preferred_element_type=jnp.float32,
        )
        key_grad = lax.dynamic_update_slice_in_dim(
            key_grad,
            lax.dynamic_slice_in_dim(key_grad, first_row, key_span, 0) + key_part,
            first_row,
            0,
        )
        value_grad = lax.dynamic_update_slice_in_dim(
            value_grad,
            lax.dynamic_slice_in_dim(value_grad, first_row, key_span, 0) + value_part,
            first_row,
            0,
        )
        return ((key_grad, value_grad), query_grad)

    empty_grad = jnp.zeros((token_count + WINDOW, head_count, head_width), jnp.float32)
    (key_grad, value_grad), query_grad = lax.scan(
        one_block,
        (empty_grad, empty_grad),
        (jnp.arange(token_count // block_rows, dtype=jnp.int32), logsum),
    )
    flat_width = head_count * head_width
    return (
        query_grad.reshape(token_count, flat_width).astype(jnp.bfloat16),
        key_grad[WINDOW:].reshape(token_count, flat_width).astype(jnp.bfloat16),
        value_grad[WINDOW:].reshape(token_count, flat_width).astype(jnp.bfloat16),
    )


def local(
    tokens,
    cotangent,
    route,
    lengths,
    key_mask,
    norm1_gain,
    norm2_gain,
    w_query,
    w_key,
    w_value,
    w_out,
    w_gate,
    w_up,
    w_down,
):
    groups = lax.axis_size("dp")
    members = lax.axis_size("mp")
    member = lax.axis_index("mp")
    local_rows = tokens.shape[0]
    group_rows = local_rows * members
    bucket = local_rows // groups
    target = route // TOK_DEV
    chosen = (target[:, None] == jnp.arange(groups, dtype=jnp.int32)[None, :]).astype(jnp.int32)
    ranking = jnp.sum((jnp.cumsum(chosen, axis=0) - chosen) * chosen, axis=1)
    send_at = target * bucket + ranking
    arrival, arrival_grad, arrival_slot = (
        lax.all_to_all(
            jnp.zeros_like(tokens).at[send_at].set(tokens),
            "dp",
            split_axis=0,
            concat_axis=0,
            tiled=True,
        ),
        lax.all_to_all(
            jnp.zeros_like(cotangent).at[send_at].set(cotangent),
            "dp",
            split_axis=0,
            concat_axis=0,
            tiled=True,
        ),
        lax.all_to_all(
            jnp.zeros_like(route).at[send_at].set(route % local_rows),
            "dp",
            split_axis=0,
            concat_axis=0,
            tiled=True,
        ),
    )
    token_rows = jnp.zeros_like(arrival).at[arrival_slot].set(arrival)
    grad_rows = jnp.zeros_like(arrival_grad).at[arrival_slot].set(arrival_grad)
    seq_ends = jnp.cumsum(lengths[0])
    positions = jnp.arange(group_rows, dtype=jnp.int32)
    segment = jnp.sum((positions[:, None] >= seq_ends[None, :]).astype(jnp.int32), axis=1)
    input_rows = token_rows.astype(jnp.float32)
    normed_one, inverse_one = norm_rows(input_rows)
    leading_all, grad_all = (
        lax.all_gather(token_rows, "mp", axis=0, tiled=True),
        lax.all_gather(grad_rows, "mp", axis=0, tiled=True),
    )
    input_all = leading_all.astype(jnp.float32)
    normed_all, _ = norm_rows(input_all)
    hidden_one = (normed_all * norm1_gain).astype(jnp.bfloat16)
    head_count = w_query.shape[1] // HEAD_DIM
    query = jnp.dot(hidden_one, w_query, preferred_element_type=jnp.float32).astype(jnp.bfloat16)
    keys = jnp.dot(hidden_one, w_key, preferred_element_type=jnp.float32).astype(jnp.bfloat16)
    values = jnp.dot(hidden_one, w_value, preferred_element_type=jnp.float32).astype(jnp.bfloat16)
    query_heads = query.reshape(group_rows, head_count, HEAD_DIM)
    key_heads = keys.reshape(group_rows, head_count, HEAD_DIM)
    value_heads = values.reshape(group_rows, head_count, HEAD_DIM)
    mixed_flat, logsum = attend_forward(query_heads, key_heads, value_heads, segment, key_mask)
    attention_all = lax.psum(jnp.dot(mixed_flat, w_out, preferred_element_type=jnp.float32), "mp")
    middle_all = input_all + attention_all
    middle_rows = lax.dynamic_slice_in_dim(middle_all, member * local_rows, local_rows, 0)
    normed_mid, _ = norm_rows(middle_all)
    hidden_two = (normed_mid * norm2_gain).astype(jnp.bfloat16)
    normed_two, inverse_two = norm_rows(middle_rows)
    gate_value = jnp.dot(hidden_two, w_gate, preferred_element_type=jnp.float32)
    upward = jnp.dot(hidden_two, w_up, preferred_element_type=jnp.float32)
    sigmoid = jax.nn.sigmoid(gate_value)
    activated = (gate_value * sigmoid * upward).astype(jnp.bfloat16)
    out_rows = middle_rows + lax.psum_scatter(
        jnp.dot(activated, w_down, preferred_element_type=jnp.float32).astype(jnp.bfloat16),
        "mp",
        scatter_dimension=0,
        tiled=True,
    ).astype(jnp.float32)
    activated_grad = jnp.einsum("td,fd->tf", grad_all, w_down, preferred_element_type=jnp.float32)
    gate_grad = (activated_grad * upward * sigmoid * (1.0 + gate_value * (1.0 - sigmoid))).astype(
        jnp.bfloat16
    )
    upward_grad = (activated_grad * gate_value * sigmoid).astype(jnp.bfloat16)
    down_sum = jnp.einsum("tf,td->fd", activated, grad_all, preferred_element_type=jnp.float32)
    gate_sum = jnp.einsum("td,tf->df", hidden_two, gate_grad, preferred_element_type=jnp.float32)
    upward_sum = jnp.einsum(
        "td,tf->df", hidden_two, upward_grad, preferred_element_type=jnp.float32
    )
    hidden_two_grad = lax.psum_scatter(
        jnp.einsum("tf,df->td", gate_grad, w_gate, preferred_element_type=jnp.float32)
        + jnp.einsum("tf,df->td", upward_grad, w_up, preferred_element_type=jnp.float32),
        "mp",
        scatter_dimension=0,
        tiled=True,
    )
    norm_part_two, gain_two_grad = norm_back(hidden_two_grad, normed_two, inverse_two, norm2_gain)
    middle_grad = grad_rows.astype(jnp.float32) + norm_part_two
    branch_all = lax.all_gather(middle_grad.astype(jnp.bfloat16), "mp", axis=0, tiled=True)
    output_sum = jnp.einsum("tc,td->cd", mixed_flat, branch_all, preferred_element_type=jnp.float32)
    mixed_grad = jnp.einsum(
        "td,cd->tc", branch_all, w_out, preferred_element_type=jnp.float32
    ).astype(jnp.bfloat16)
    query_grad, key_grad, value_grad = attend_backward(
        query_heads,
        key_heads,
        value_heads,
        segment,
        key_mask,
        logsum,
        mixed_grad.reshape(group_rows, head_count, HEAD_DIM),
    )
    query_sum = jnp.einsum("td,tc->dc", hidden_one, query_grad, preferred_element_type=jnp.float32)
    key_sum = jnp.einsum("td,tc->dc", hidden_one, key_grad, preferred_element_type=jnp.float32)
    value_sum = jnp.einsum("td,tc->dc", hidden_one, value_grad, preferred_element_type=jnp.float32)
    hidden_one_grad = lax.psum_scatter(
        (
            jnp.einsum("tc,dc->td", query_grad, w_query, preferred_element_type=jnp.float32)
            + jnp.einsum("tc,dc->td", key_grad, w_key, preferred_element_type=jnp.float32)
            + jnp.einsum("tc,dc->td", value_grad, w_value, preferred_element_type=jnp.float32)
        ).astype(jnp.bfloat16),
        "mp",
        scatter_dimension=0,
        tiled=True,
    ).astype(jnp.float32)
    norm_part_one, gain_one_grad = norm_back(hidden_one_grad, normed_one, inverse_one, norm1_gain)
    input_grad = middle_grad + norm_part_one
    gain_one_sum, gain_two_sum = lax.psum((gain_one_grad, gain_two_grad), ("dp", "mp"))
    weight_sums = (
        lax.psum(query_sum.astype(jnp.bfloat16), "dp").astype(jnp.float32),
        lax.psum(key_sum.astype(jnp.bfloat16), "dp").astype(jnp.float32),
        lax.psum(value_sum.astype(jnp.bfloat16), "dp").astype(jnp.float32),
        lax.psum(output_sum.astype(jnp.bfloat16), "dp").astype(jnp.float32),
        lax.psum(gate_sum.astype(jnp.bfloat16), "dp").astype(jnp.float32),
        lax.psum(upward_sum.astype(jnp.bfloat16), "dp").astype(jnp.float32),
        lax.psum(down_sum.astype(jnp.bfloat16), "dp").astype(jnp.float32),
    )
    back_out, back_grad = (
        lax.all_to_all(
            out_rows.astype(jnp.bfloat16)[arrival_slot],
            "dp",
            split_axis=0,
            concat_axis=0,
            tiled=True,
        ),
        lax.all_to_all(
            input_grad.astype(jnp.bfloat16)[arrival_slot],
            "dp",
            split_axis=0,
            concat_axis=0,
            tiled=True,
        ),
    )
    return (
        back_out[send_at],
        back_grad[send_at],
        gain_one_sum,
        gain_two_sum,
        weight_sums[0],
        weight_sums[1],
        weight_sums[2],
        weight_sums[3],
        weight_sums[4],
        weight_sums[5],
        weight_sums[6],
    )


MESH = pl.DeviceIdType.MESH
LANES = 128
F32 = jnp.float32
BF16 = jnp.bfloat16
VMEM_LIMIT = 56 * 1024 * 1024


def plane():
    me = lax.axis_index("dp")
    side = me + 1 - 2 * lax.rem(me, 2)
    over_x = me + 2 - 4 * lax.rem(lax.div(me, 2), 2)
    over_y = me + 4 - 8 * lax.rem(lax.div(me, 4), 2)
    corner = over_x + 4 - 8 * lax.rem(lax.div(over_x, 4), 2)
    return (me, side, over_x, over_y, corner)


def to_dp(source, target, send_sem, recv_sem, index):
    return pltpu.make_async_remote_copy(
        src_ref=source,
        dst_ref=target,
        send_sem=send_sem,
        recv_sem=recv_sem,
        device_id={"dp": index},
        device_id_type=MESH,
    )


def to_mp(source, target, send_sem, recv_sem, index):
    return pltpu.make_async_remote_copy(
        src_ref=source,
        dst_ref=target,
        send_sem=send_sem,
        recv_sem=recv_sem,
        device_id={"mp": index},
        device_id_type=MESH,
    )


def owner_at(turn):
    me, side, over_x, over_y, _ = plane()
    block = turn // 2
    near = ((block + 1) // 2) % 2
    far = block // 3
    second = turn % 2
    other = (1 - near) * second + (block // 2) * near
    owner = me + (near * (1 - second) + far) * (over_x - me)
    return owner + (near * second + far) * (over_y - me) + other * (side - me)


ARRIVALS = (
    (1, (4,)),
    (2, (0, 1, 2)),
    (3, (3,)),
    (4, (6, 9)),
    (5, (8, 10)),
    (6, (5, 7)),
    (7, (11, 12)),
)


class Gather:
    AFTER = {0: (5, 6), 1: (7, 8), 2: (9,), 3: (10,), 5: (11,), 7: (12,)}

    def __init__(self, own, out, send, recv, local=None):
        me, side, over_x, over_y, corner = plane()
        half = out.shape[1] // 2
        low, high = pl.ds(0, half), pl.ds(half, half)
        self.keep = None if own is None else pltpu.make_async_copy(own, out.at[me], local)
        own = out.at[me] if own is None else own

        def hop(number, source, target, index):
            return to_dp(source, target, send.at[number], recv.at[number], index)

        def onward(number, owner, part, index):
            place = out.at[owner, part]
            return hop(number, place, place, index)

        self.copies = [
            hop(0, own.at[low], out.at[me, low], over_x),
            hop(1, own.at[high], out.at[me, high], over_y),
            hop(2, own.at[high], out.at[me, high], over_x),
            hop(3, own.at[low], out.at[me, low], over_y),
            hop(4, own, out.at[me], side),
            onward(5, over_x, low, over_y),
            onward(6, over_x, low, side),
            onward(7, over_y, high, over_x),
            onward(8, over_y, high, side),
            onward(9, over_x, high, side),
            onward(10, over_y, low, side),
            onward(11, corner, low, side),
            onward(12, corner, high, side),
        ]

    def start(self):
        for number in range(5):
            self.copies[number].start()
        if self.keep is not None:
            self.keep.start()

    def arrive(self, *numbers):
        for number in numbers:
            self.copies[number].wait_recv()
            for later in self.AFTER.get(number, ()):
                self.copies[later].start()

    def pass_on(self):
        self.arrive(0, 1, 2, 3)

    def sent(self):
        for copy in self.copies:
            copy.wait_send()
        if self.keep is not None:
            self.keep.wait()

    def finish(self):
        self.arrive(5, 7, 4, 6, 8, 9, 10, 11, 12)
        self.sent()


def greet_all():
    barrier = pltpu.get_barrier_semaphore()
    me, z = lax.axis_index("dp"), lax.axis_index("mp")
    for step in range(1, 8):
        pl.semaphore_signal(
            barrier, inc=1, device_id={"dp": lax.rem(me + step, 8)}, device_id_type=MESH
        )
    core = lax.rem(me, 2)
    for step in range(1, 4):
        for other in (me, me + 1 - 2 * core):
            pl.semaphore_signal(
                barrier,
                inc=1,
                device_id={"dp": other, "mp": lax.rem(z + step, 4)},
                device_id_type=MESH,
            )
    return barrier


def start_all(copies):
    for copy in copies:
        copy.start()
    return copies


def wait_all(copies):
    for copy in copies:
        copy.wait()


def swap_all(source, target, send, recv):
    me = lax.axis_index("dp")
    return [
        to_dp(source, target.at[me], send.at[step - 1], recv.at[step - 1], lax.rem(me + step, 8))
        for step in range(1, 8)
    ]


class Spread:
    def __init__(self, share, w_qkv, w_out, send, recv, local):
        me, z = lax.axis_index("dp"), lax.axis_index("mp")
        core = lax.rem(me, 2)
        self.place = z + core * (3 - 2 * z)
        self.send, self.recv, self.local = send, recv, local
        self.shares = [share.at[0], share.at[1], share.at[2], share.at[3]]
        self.slots = (core, 1 - core)
        self.core = core
        self.w_qkv, self.w_out = w_qkv, w_out

    def target(self, which, piece):
        slot = self.slots[which]
        block = slot if piece == 3 else 2 * piece + slot
        rows = pl.ds(pl.multiple_of(block * LANES, LANES), HEAD_DIM)
        return (self.w_out if piece == 3 else self.w_qkv).at[rows]

    def hop(self, which, piece, number, place, own):
        source = self.shares[piece] if own else self.target(which, piece)
        z = place + self.core * (3 - 2 * place)
        return to_mp(
            source,
            self.target(which, piece),
            self.send.at[number * 4 + piece],
            self.recv.at[which * 4 + piece],
            z,
        )

    def keep(self, which, piece):
        return pltpu.make_async_copy(
            self.shares[piece], self.target(which, piece), self.local.at[piece]
        )

    def start(self, pieces):
        @pl.when(self.place == 0)
        def _():
            for piece in pieces:
                self.hop(0, piece, 0, 1, True).start()
                self.keep(0, piece).start()

        @pl.when(self.place == 1)
        def _():
            for piece in pieces:
                self.hop(1, piece, 0, 0, True).start()
                self.hop(1, piece, 1, 2, True).start()
                self.keep(1, piece).start()

    def pass_on(self, pieces):
        @pl.when(self.place == 1)
        def _():
            for piece in pieces:
                self.hop(0, piece, 2, 2, False).wait_recv()
                self.hop(0, piece, 2, 2, False).start()

        @pl.when(self.place == 2)
        def _():
            for which in (1, 0):
                for piece in pieces:
                    self.hop(which, piece, which, 3, False).wait_recv()
                    self.hop(which, piece, which, 3, False).start()

    def finish(self, pieces):
        @pl.when(self.place == 0)
        def _():
            for piece in pieces:
                self.hop(1, piece, 0, 1, False).wait_recv()
                self.hop(0, piece, 0, 1, True).wait_send()
                self.keep(0, piece).wait()

        @pl.when(self.place == 1)
        def _():
            for piece in pieces:
                self.hop(1, piece, 0, 0, True).wait_send()
                self.hop(1, piece, 1, 2, True).wait_send()
                self.hop(0, piece, 2, 2, False).wait_send()
                self.keep(1, piece).wait()

        @pl.when(self.place == 2)
        def _():
            for piece in pieces:
                for which in (1, 0):
                    self.hop(which, piece, which, 3, False).wait_send()

        @pl.when(self.place == 3)
        def _():
            for piece in pieces:
                for which in (1, 0):
                    self.hop(which, piece, which, 3, False).wait_recv()


class Column:
    def __init__(self, own, out, send, recv, local):
        z = lax.axis_index("mp")
        self.z, self.own, self.out, self.send, self.recv = z, own, out, send, recv
        self.outer = (z == 0) | (z == 3)
        near = 1 + lax.div(z, 3)
        self.from_outer = (near, 3 - near)
        self.edge = 3 * (z - 1)
        self.from_inner = (3 - z, 3 - self.edge, self.edge)
        self.keep = pltpu.make_async_copy(own, out.at[z], local)

    def straight(self, number, target):
        return to_mp(
            self.own, self.out.at[self.z], self.send.at[number], self.recv.at[self.z], target
        )

    def onward(self):
        far = 3 - self.edge
        return to_mp(
            self.out.at[far], self.out.at[far], self.send.at[3], self.recv.at[far], self.edge
        )

    def came(self, source):
        return to_mp(
            self.own, self.out.at[source], self.send.at[0], self.recv.at[source], source
        ).wait_recv

    def start(self):
        self.keep.start()

        @pl.when(self.outer)
        def _():
            for number, target in enumerate(self.from_outer):
                self.straight(number, target).start()

        @pl.when(jnp.logical_not(self.outer))
        def _():
            for number, target in enumerate(self.from_inner):
                self.straight(number, target).start()

    def pass_on(self):
        @pl.when(jnp.logical_not(self.outer))
        def _():
            self.came(3 - self.edge)()
            self.onward().start()

    def finish(self):
        @pl.when(self.outer)
        def _():
            for source in (1, 2):
                self.came(source)()
            self.came(3 - self.z)()
            for number, target in enumerate(self.from_outer):
                self.straight(number, target).wait_send()

        @pl.when(jnp.logical_not(self.outer))
        def _():
            self.came(3 - self.z)()
            self.came(self.edge)()
            for number, target in enumerate(self.from_inner):
                self.straight(number, target).wait_send()
            self.onward().wait_send()

        self.keep.wait()


def anywhere():
    return pl.BlockSpec(memory_space=pl.ANY)


def on_chip():
    return pl.BlockSpec(memory_space=pltpu.VMEM)


def remote_params(number, limit=VMEM_LIMIT):
    return pltpu.CompilerParams(
        collective_id=number, has_side_effects=True, vmem_limit_bytes=limit
    )


def hot_of(notes, k, size):
    own = notes[:, 0:48, :].reshape(size, LANES)
    lane = lax.broadcasted_iota(jnp.int32, (size, LANES), 1)
    slot = jnp.sum(jnp.where(lane == k, own, 0.0), axis=1, keepdims=True)
    return (lax.broadcasted_iota(jnp.int32, (size, size), 1).astype(F32) == slot).astype(BF16)


def block_mask(notes, k, block, z, rows):
    position = rows * z + block * 128 + lax.broadcasted_iota(jnp.int32, (128, 1), 0)
    position = position.astype(F32)
    first_end = notes[k, 52:53, 0:1]
    second_end = first_end + notes[k, 52:53, 1:2]
    begin = jnp.where(position >= first_end, first_end, 0.0)
    begin = jnp.where(position >= second_end, second_end, begin)
    column = lax.broadcasted_iota(jnp.int32, (128, 192), 1)
    distance = 64 + lax.broadcasted_iota(jnp.int32, (128, 192), 0) - column
    key_position = (rows * z + block * 128 - 64 + column).astype(F32)
    live = jnp.concatenate(
        [notes[k, 48 + block : 49 + block, :], notes[k, 49 + block : 50 + block, 0:64]], axis=1
    )
    allowed = (distance >= 0) & (distance < WINDOW) & (key_position >= begin)
    return allowed & ((live == 1.0) | (distance == 0))


NT = (((1,), (1,)), ((), ()))
TN = (((0,), (0,)), ((), ()))


def forward_kernel(
    tokens, cotangent, order_row, gain, notes, query, keys, values, project, gate,
    hidden_out, w_qkv_out, w_out, notes_all, gate_all, mixed_out, kept_out, tokens_out, cotangent_out,
    cotangent_all,
    hidden_all, qkv, share, gate_own, w_qkv, mixed, kept, tokens_b, cotangent_b,
    send, recv, send_a, recv_a, send_g, recv_g, send_w, recv_w, send_n, recv_n, send_c, recv_c,
    local, out_sem, store_sem, *, scale,
):
    groups, rows, width = hidden_all.shape
    me, z = lax.axis_index("dp"), lax.axis_index("mp")
    members = lax.axis_size("mp")
    barrier = greet_all()
    head = pl.ds(pl.multiple_of(lax.div(me, 2) * HEAD_DIM, 16), HEAD_DIM)
    units = pl.ds(pl.multiple_of(me * LANES, LANES), LANES)
    loads = [
        pltpu.make_async_copy(source.at[head], share.at[piece], local.at[piece])
        for piece, source in enumerate((query, keys, values, project))
    ]
    loads.append(pltpu.make_async_copy(gate.at[:, units], gate_own, local.at[4]))
    for copy in loads:
        copy.start()
    none = jnp.zeros((LANES - HEAD_DIM, width), BF16)
    for block in range(6):
        w_qkv[block * LANES + HEAD_DIM : block * LANES + LANES, :] = none
    for block in range(2):
        w_out[block * LANES + HEAD_DIM : block * LANES + LANES, :] = none

    place = lax.broadcasted_iota(jnp.int32, (rows, rows), 0).astype(F32)
    sort = (place == order_row[...]).astype(BF16)
    tokens_b[...] = jnp.dot(sort, tokens[...], preferred_element_type=F32).astype(BF16)

    def normalise(span):
        value = tokens_b[span, :].astype(F32)
        inverse = lax.rsqrt(mean_rows(value * value) + EPSILON)
        hidden_all[me, span, :] = (value * inverse * gain[...]).astype(BF16)

    each_chunk(rows, normalise)
    notes_all[me] = notes[...]
    stores = start_all([pltpu.make_async_copy(tokens_b, tokens_out, store_sem.at[0])])
    pl.semaphore_wait(barrier, 13)
    gather = Gather(None, hidden_all, send_a, recv_a)
    gather.start()
    swaps = swap_all(notes, notes_all, send_n, recv_n)
    for copy in swaps:
        copy.start()
    for copy in loads[:4]:
        copy.wait()
    spread = Spread(share, w_qkv, w_out, send_w, recv_w, local)
    spread.start((0, 1, 2))
    cotangent_b[...] = jnp.dot(sort, cotangent[...], preferred_element_type=F32).astype(BF16)
    stores += start_all([pltpu.make_async_copy(cotangent_b, cotangent_out, store_sem.at[1])])
    wait_all(loads[4:])
    column = Column(gate_own, gate_all, send_c, recv_c, local.at[4])
    second = Gather(cotangent_b, cotangent_all, send_g, recv_g, local.at[5])
    spread.pass_on((0, 1, 2))
    gather.arrive(0, 1)
    second.start()
    column.start()
    gather.arrive(2, 3)
    spread.finish((0, 1, 2))
    spread.start((3,))
    stores += start_all([pltpu.make_async_copy(w_qkv, w_qkv_out, store_sem.at[2])])
    for copy in swaps:
        copy.wait()

    def keep(turn):
        owner = owner_at(turn)
        return pltpu.make_async_copy(hidden_all.at[owner], hidden_out.at[owner], out_sem.at[turn])

    def multiply(turn, carry):
        for number, numbers in ARRIVALS:
            left = tuple(n for n in numbers if n > 3)
            if left:
                pl.when(turn == number)(functools.partial(gather.arrive, *left))
        owner = owner_at(turn)
        keep(turn).start()
        product = lax.dot_general(
            hidden_all[owner], w_qkv[...], NT, preferred_element_type=F32
        ).astype(BF16)
        qkv[owner] = product.reshape(groups, rows // groups, 768)
        return carry

    lax.fori_loop(0, groups, multiply, 0)

    def halo(k, other):
        return to_mp(
            kept.at[k, pl.ds(rows, 64), pl.ds(256, 512)],
            kept.at[k, pl.ds(0, 64), pl.ds(256, 512)],
            send.at[k],
            recv.at[k],
            other,
        )

    def store_kept(k):
        return pltpu.make_async_copy(kept.at[k], kept_out.at[k], store_sem.at[3 + k])

    def store_mixed(k):
        span = pl.ds(k, 1)
        return pltpu.make_async_copy(
            mixed.at[:, span], mixed_out.at[:, span], store_sem.at[3 + groups + k]
        )

    def order(k, carry):
        hot = hot_of(notes_all, k, rows)
        given = qkv[:, pl.ds(k, 1)].reshape(rows, 768)
        kept[k, pl.ds(64, rows), :] = lax.dot_general(
            hot, given, TN, preferred_element_type=F32
        ).astype(BF16)
        kept[k, pl.ds(0, 64), pl.ds(0, 256)] = jnp.zeros((64, 256), BF16)

        @pl.when(z < members - 1)
        def _():
            halo(k, z + 1).start()

        @pl.when(z == 0)
        def _():
            kept[k, pl.ds(0, 64), pl.ds(256, 512)] = jnp.zeros((64, 512), BF16)

        return carry

    lax.fori_loop(0, groups, order, 0)

    def attend(k, carry):
        @pl.when(z > 0)
        def _():
            halo(k, z).wait_recv()

        store_kept(k).start()
        hot = hot_of(notes_all, k, rows)
        found = []
        for block in range(rows // 128):
            allowed = block_mask(notes_all, k, block, z, rows)
            heads = []
            for head in range(2):
                query = kept[k, pl.ds(64 + block * 128, 128), pl.ds(head * 128, 128)]
                keys = kept[k, pl.ds(block * 128, 192), pl.ds(256 + head * 128, 128)]
                values = kept[k, pl.ds(block * 128, 192), pl.ds(512 + head * 128, 128)]
                scores = lax.dot_general(query, keys, NT, preferred_element_type=F32) * scale
                scores = jnp.where(allowed, scores, -MASKED)
                weights = jnp.exp(scores - jnp.max(scores, axis=-1, keepdims=True))
                total = jnp.sum(weights, axis=-1, keepdims=True)
                chances = (weights / total).astype(BF16)
                heads.append(jnp.dot(chances, values, preferred_element_type=F32).astype(BF16))
            found.append(jnp.concatenate(heads, axis=1))
        ordered = jnp.concatenate(found, axis=0)
        back = jnp.dot(hot, ordered, preferred_element_type=F32).astype(BF16)
        mixed[:, pl.ds(k, 1)] = back.reshape(groups, 1, rows // groups, 256)
        store_mixed(k).start()
        return carry

    spread.pass_on((3,))
    lax.fori_loop(0, groups // 2, attend, 0)
    second.pass_on()
    column.pass_on()
    lax.fori_loop(groups // 2, groups, attend, 0)
    spread.finish((3,))
    second.finish()
    column.finish()
    gather.sent()

    wait_all(stores)

    def stored(turn, carry):
        keep(turn).wait()
        store_kept(turn).wait()
        store_mixed(turn).wait()
        return carry

    lax.fori_loop(0, groups, stored, 0)

    @pl.when(z < members - 1)
    def _():
        def done(k, carry):
            halo(k, z + 1).wait_send()
            return carry

        lax.fori_loop(0, groups, done, 0)


def attend_ahead(
    tokens, cotangent, order_row, gain, notes, query, keys, values, project, gate, scale
):
    rows, width = tokens.shape
    groups, members = lax.axis_size("dp"), lax.axis_size("mp")
    dma = pltpu.SemaphoreType.DMA
    shape = jax.ShapeDtypeStruct
    return pl.pallas_call(
        functools.partial(forward_kernel, scale=scale),
        out_shape=(
            shape((groups, rows, width), BF16),
            shape((6 * LANES, width), BF16),
            shape((2 * LANES, width), BF16),
            shape((groups,) + notes.shape, F32),
            shape((members, width, LANES), BF16),
            shape((groups, groups, rows // groups, 256), BF16),
            shape((groups, rows + 64, 768), BF16),
            shape((rows, width), BF16),
            shape((rows, width), BF16),
            shape((groups, rows, width), BF16),
        ),
        in_specs=[on_chip()] * 5 + [anywhere()] * 5,
        out_specs=(
            anywhere(), anywhere(), on_chip(), on_chip(), anywhere(),
            anywhere(), anywhere(), anywhere(), anywhere(), anywhere(),
        ),
        scratch_shapes=[
            pltpu.VMEM((groups, rows, width), BF16),
            pltpu.VMEM((groups, groups, rows // groups, 768), BF16),
            pltpu.VMEM((4, HEAD_DIM, width), BF16),
            pltpu.VMEM((width, LANES), BF16),
            pltpu.VMEM((6 * LANES, width), BF16),
            pltpu.VMEM((groups, groups, rows // groups, 256), BF16),
            pltpu.VMEM((groups, rows + 64, 768), BF16),
            pltpu.VMEM((rows, width), BF16),
            pltpu.VMEM((rows, width), BF16),
            dma((groups,)),
            dma((groups,)),
            dma((13,)),
            dma((13,)),
            dma((13,)),
            dma((13,)),
            dma((12,)),
            dma((8,)),
            dma((7,)),
            dma((7,)),
            dma((4,)),
            dma((4,)),
            dma((6,)),
            dma((groups,)),
            dma((3 + 2 * groups,)),
        ],
        compiler_params=remote_params(2, 60 * 1024 * 1024),
        cost_estimate=pl.CostEstimate(flops=0, bytes_accessed=300_000_000, transcendentals=0),
        name="attend_ahead",
    )(tokens, cotangent, order_row, gain, notes, query, keys, values, project, gate)


CHUNK = 32


def each_chunk(rows, body, chunk=CHUNK):
    def step(i, carry):
        body(pl.ds(pl.multiple_of(i * chunk, chunk), chunk))
        return carry

    lax.fori_loop(0, rows // chunk, step, 0)


class Units:
    def __init__(self, part, came_in, stage, send, recv, local):
        self.z = lax.axis_index("mp")
        self.part_of = part
        self.inputs = (came_in,)
        self.stages = (stage,)
        self.send, self.recv, self.local = send, recv, local
        z = self.z
        self.outer = (z == 0) | (z == 3)
        self.far = 3 - z
        self.near = 1 + lax.div(z, 3)
        self.second = 3 - self.near
        self.edge = 3 * (z - 1)

    def part(self, kind, z):
        return self.part_of(z)

    def straight(self, kind, number, target):
        return to_mp(
            self.part(kind, target),
            self.inputs[kind].at[self.z],
            self.send.at[number * 2 + kind],
            self.recv.at[self.z * 2 + kind],
            target,
        )

    def staged(self, kind):
        return to_mp(
            self.part(kind, self.far),
            self.stages[kind].at[0],
            self.send.at[4 + kind],
            self.recv.at[8 + kind],
            self.near,
        )

    def summed(self, kind):
        return to_mp(
            self.stages[kind].at[1],
            self.inputs[kind].at[self.z],
            self.send.at[4 + kind],
            self.recv.at[self.z * 2 + kind],
            3 - self.edge,
        )

    def mine(self, kind):
        return pltpu.make_async_copy(
            self.part(kind, 3 - self.edge), self.stages[kind].at[1], self.local.at[kind]
        )

    def start(self):
        @pl.when(self.outer)
        def _():
            for kind in range(1):
                self.staged(kind).start()
            for kind in range(1):
                self.straight(kind, 0, self.near).start()
                self.straight(kind, 1, self.second).start()

        @pl.when(jnp.logical_not(self.outer))
        def _():
            for kind in range(1):
                self.mine(kind).start()
                self.straight(kind, 0, 3 - self.z).start()
                self.straight(kind, 1, self.edge).start()

    def add(self):
        @pl.when(jnp.logical_not(self.outer))
        def _():
            for kind in range(1):
                stage = self.stages[kind]
                self.mine(kind).wait()
                to_mp(
                    self.part(kind, 0),
                    stage.at[0],
                    self.send.at[4 + kind],
                    self.recv.at[8 + kind],
                    self.edge,
                ).wait_recv()

                def body(span):
                    stage[1, span, :] = (
                        stage[0, span, :].astype(F32) + stage[1, span, :].astype(F32)
                    ).astype(BF16)

                each_chunk(stage.shape[1], body)
                self.summed(kind).start()

    def arrived(self, kind, source):
        to_mp(
            self.part(kind, 0),
            self.inputs[kind].at[source],
            self.send.at[kind],
            self.recv.at[source * 2 + kind],
            source,
        ).wait_recv()

    def finish(self):
        @pl.when(self.outer)
        def _():
            for kind in range(1):
                self.arrived(kind, 1)
                self.arrived(kind, 2)
                self.straight(kind, 0, self.near).wait_send()
                self.straight(kind, 1, self.second).wait_send()
                self.staged(kind).wait_send()

        @pl.when(jnp.logical_not(self.outer))
        def _():
            for kind in range(1):
                self.arrived(kind, 0)
                self.arrived(kind, 3)
                self.arrived(kind, 3 - self.z)
                self.straight(kind, 0, 3 - self.z).wait_send()
                self.straight(kind, 1, self.edge).wait_send()
                self.summed(kind).wait_send()


class Reduce:
    COUNT = 10

    def __init__(self, left, right, across, part, from_side, from_corner, from_near, send, recv):
        self.left, self.right, self.across, self.part = left, right, across, part
        self.from_side, self.from_corner, self.from_near = from_side, from_corner, from_near
        self.send, self.recv = send, recv
        self.rows = part.shape[1]

    def product(self, owner, slot):
        rows, width = self.rows, self.part.shape[2]
        picked = pl.ds(pl.multiple_of(owner * rows, rows), rows)

        def tile(t, carry):
            columns = pl.ds(pl.multiple_of(t * 256, 256), 256)
            if callable(self.left):
                value = jnp.dot(
                    self.left(owner), self.right[:, columns], preferred_element_type=F32
                )
            elif self.across:
                value = lax.dot_general(
                    self.left[picked, :], self.right[columns, :], NT, preferred_element_type=F32
                )
            else:
                value = jnp.dot(
                    self.left[picked, :], self.right[:, columns], preferred_element_type=F32
                )
            self.part[slot, :, columns] = value.astype(BF16)
            return carry

        lax.fori_loop(0, width // 256, tile, 0)

    def prepare(self):
        _, side, over_x, over_y, corner = plane()
        part, near = self.part, self.from_near
        half = self.rows // 2
        low, high = pl.ds(0, half), pl.ds(half, half)

        def hop(number, source, target, index):
            return to_dp(source, target, self.send.at[number], self.recv.at[number], index)

        self.shares = [hop(i, part.at[4 + i], self.from_side.at[i], side) for i in range(4)]
        self.corners = [
            hop(4, part.at[0, low], self.from_corner.at[0], over_x),
            hop(5, part.at[0, high], self.from_corner.at[1], over_y),
        ]
        self.nears = [
            hop(6, part.at[1, low], near.at[0, low], over_x),
            hop(7, part.at[1, high], near.at[0, high], over_x),
            hop(8, part.at[2, high], near.at[1, high], over_y),
            hop(9, part.at[2, low], near.at[1, low], over_y),
        ]

    def add_side(self, slot):
        self.shares[slot].wait_recv()

        def body(span):
            self.part[slot, span, :] = (
                self.part[slot, span, :].astype(F32) + self.from_side[slot, span, :].astype(F32)
            ).astype(BF16)

        each_chunk(self.rows, body)

    def add_corner(self, slot, offset, which):
        self.corners[which].wait_recv()

        def body(span):
            target = pl.ds(pl.multiple_of(offset + span.start, CHUNK), CHUNK)
            self.part[slot, target, :] = (
                self.part[slot, target, :].astype(F32)
                + self.from_corner[which, span, :].astype(F32)
            ).astype(BF16)

        each_chunk(self.rows // 2, body)

    def products(self):
        self.prepare()
        me, _, over_x, over_y, corner = plane()
        turn = 1 - 2 * lax.rem(me, 2)
        for slot, owner in enumerate((corner, over_x, over_y, me)):
            self.product(owner + turn, 4 + slot)
            self.shares[slot].start()
        for slot, owner in enumerate((corner, over_x, over_y, me)):
            self.product(owner, slot)

    def launch(self):
        self.add_side(0)
        self.corners[0].start()
        self.corners[1].start()
        self.add_side(1)
        self.nears[0].start()
        self.add_side(2)
        self.nears[2].start()

    def begin(self):
        self.prepare()
        me, _, over_x, over_y, corner = plane()
        turn = 1 - 2 * lax.rem(me, 2)
        self.product(corner + turn, 4)
        self.shares[0].start()
        self.product(corner, 0)
        self.product(over_x + turn, 5)
        self.shares[1].start()
        self.add_side(0)
        self.corners[0].start()
        self.corners[1].start()
        self.product(over_x, 1)
        self.product(over_y + turn, 6)
        self.shares[2].start()
        self.add_side(1)
        self.nears[0].start()
        self.product(over_y, 2)
        self.product(me + turn, 7)
        self.shares[3].start()
        self.add_side(2)
        self.nears[2].start()
        self.product(me, 3)

    def middle(self):
        self.add_corner(2, 0, 0)
        self.nears[3].start()
        self.add_corner(1, self.rows // 2, 1)
        self.nears[1].start()

    def end(self):
        self.shares[3].wait_recv()
        for copy in self.nears:
            copy.wait_recv()

    def run(self):
        self.begin()
        self.middle()
        self.end()

    def rows_of(self, span):
        return (
            self.part[3, span, :].astype(F32)
            + self.from_side[3, span, :].astype(F32)
            + self.from_near[0, span, :].astype(F32)
            + self.from_near[1, span, :].astype(F32)
        )

    def finish(self):
        for copy in self.shares + self.corners + self.nears:
            copy.wait_send()


def reduce_scratch(rows, width):
    dma = pltpu.SemaphoreType.DMA
    return [
        pltpu.VMEM((8, rows, width), BF16),
        pltpu.VMEM((4, rows, width), BF16),
        pltpu.VMEM((2, rows // 2, width), BF16),
        pltpu.VMEM((2, rows, width), BF16),
        dma((10,)),
        dma((10,)),
    ]


def gather_scratch(rows, width):
    dma = pltpu.SemaphoreType.DMA
    return [pltpu.VMEM((rows, width), BF16), dma((13,)), dma((13,)), dma(())]


def mean_rows(values):
    return jnp.mean(values, axis=-1, keepdims=True)


class Heads:
    def __init__(self, source, stage, arrive, send, recv_stage, recv):
        me, z = lax.axis_index("dp"), lax.axis_index("mp")
        self.me, self.z = me, z
        self.core = lax.rem(me, 2)
        self.source, self.stage, self.arrive = source, stage, arrive
        self.send, self.recv_stage, self.recv = send, recv_stage, recv
        self.place = z + self.core * (3 - 2 * z)
        self.columns = source.shape[1] // 2

    def z_of(self, place):
        return place + self.core * (3 - 2 * place)

    def slot_of(self, place):
        return self.core if place == 0 else 1 - self.core

    def rows_of(self, place, kind):
        block = 2 * kind + self.slot_of(place)
        return self.source.at[pl.ds(pl.multiple_of(block * LANES, LANES), HEAD_DIM)]

    def half_of(self, ref, half):
        return ref.at[:, pl.ds(pl.multiple_of(half * self.columns, LANES), self.columns)]

    def to_stage(self, place, kind):
        return to_at(
            self.rows_of(place, kind),
            self.stage.at[place, kind],
            self.send.at[place * 4 + kind],
            self.recv_stage.at[place * 4 + kind],
            self.me,
            self.z_of(2),
        )

    def to_owner(self, place, kind, half, way, ref, number):
        return to_at(
            self.half_of(ref, half),
            self.arrive.at[way, kind],
            self.send.at[number],
            self.recv.at[way * 4 + kind],
            self.me - self.core + half,
            self.z_of(place),
        )

    def sums(self, kind):
        return [
            self.to_owner(
                place, kind, half, 2, self.stage.at[place, kind], place * 8 + kind * 2 + half
            )
            for place in (0, 1)
            for half in (0, 1)
        ]

    def cross(self, own, kind):
        other = 1 - own
        copies = [
            self.to_owner(other, kind, half, 0, self.rows_of(other, kind), kind * 2 + half)
            for half in (0, 1)
        ]
        copies.append(
            to_at(
                self.half_of(self.rows_of(own, kind), 1 - self.core),
                self.arrive.at[1, kind],
                self.send.at[8 + kind],
                self.recv.at[4 + kind],
                self.me + 1 - 2 * self.core,
                self.z,
            )
        )
        return copies

    def start(self, kinds):
        @pl.when(self.place == 3)
        def _():
            for kind in kinds:
                self.to_stage(0, kind).start()
                self.to_stage(1, kind).start()

        for own in (0, 1):
            @pl.when(self.place == own)
            def _():
                for kind in kinds:
                    for copy in self.cross(own, kind):
                        copy.start()

    def add(self, kinds):
        @pl.when(self.place == 2)
        def _():
            for kind in kinds:
                for place in (0, 1):
                    self.to_stage(place, kind).wait_recv()
                    mine = self.rows_of(place, kind)

                    def body(span):
                        self.stage[place, kind, span, :] = (
                            self.stage[place, kind, span, :].astype(F32)
                            + mine[span, :].astype(F32)
                        ).astype(BF16)

                    each_chunk(HEAD_DIM, body, 16)
                for copy in self.sums(kind):
                    copy.start()

    def total(self, out):
        owner = lax.div(self.z, 2) == self.core
        for kind in range(4):
            for own in (0, 1):
                @pl.when(self.place == own)
                def _():
                    self.arrive[1, kind] = self.half_of(self.rows_of(own, kind), self.core)[...]

            for way in range(3):
                waiting = to_at(
                    self.half_of(self.rows_of(0, kind), 0),
                    self.arrive.at[way, kind],
                    self.send.at[0],
                    self.recv.at[way * 4 + kind],
                    self.me,
                    lax.rem(self.z + 1, 4),
                )
                if way == 1:
                    pl.when(jnp.logical_not(owner))(waiting.wait_recv)
                else:
                    waiting.wait_recv()

            def body(span):
                found = self.arrive[0, kind, span, :].astype(F32)
                found = found + self.arrive[1, kind, span, :].astype(F32)
                found = found + self.arrive[2, kind, span, :].astype(F32)
                target = pl.ds(pl.multiple_of(kind * HEAD_DIM + span.start, 16), 16)
                out[target, :] = found.astype(BF16)

            each_chunk(HEAD_DIM, body, 16)

    def finish_send(self):
        for kind in range(4):
            @pl.when(self.place == 3)
            def _():
                self.to_stage(0, kind).wait_send()
                self.to_stage(1, kind).wait_send()

            @pl.when(self.place == 2)
            def _():
                for copy in self.sums(kind):
                    copy.wait_send()

            for own in (0, 1):
                @pl.when(self.place == own)
                def _():
                    for copy in self.cross(own, kind):
                        copy.wait_send()


def to_at(source, target, send_sem, recv_sem, dp, mp):
    return pltpu.make_async_remote_copy(
        src_ref=source,
        dst_ref=target,
        send_sem=send_sem,
        recv_sem=recv_sem,
        device_id={"dp": dp, "mp": mp},
        device_id_type=MESH,
    )


def backward_kernel(
    branch, notes_all, kept_in, w_out_in, activated_in, w_down_in, middle_in, both_sum, down_in,
    out, result, branch_all, both_in, down_all,
    totals, query_part, key_value, ending, leaving, arriving, send, recv,
    part, from_side, from_corner, from_near, send_r, recv_r,
    mixed_grad, shard, load_sem, send_g, recv_g,
    both_stage, send_u, recv_u, local, down_found, send_d, recv_d,
    kept, w_out, activated, w_down, middle, fetch_sem,
    *, scale, groups, rows,
):
    z = lax.axis_index("mp")
    members = lax.axis_size("mp")
    barrier = greet_all()
    pairs = ((activated_in, activated), (w_out_in, w_out), (kept_in, kept), (middle_in, middle))
    pairs += ((w_down_in, w_down),)
    fetches = [
        pltpu.make_async_copy(source, target, fetch_sem.at[number])
        for number, (source, target) in enumerate(pairs)
    ]
    load_down = pltpu.make_async_copy(down_in, down_found, load_sem.at[2])
    pl.semaphore_wait(barrier, 13)
    units = Units(lambda owner: both_sum.at[owner], both_in, both_stage, send_u, recv_u, local)
    gather = Gather(branch, branch_all, send_g, recv_g, local.at[2])
    gather.start()
    units.start()
    start_all(fetches)
    load_down.start()
    wait_all((fetches[0], fetches[4]))
    reduce = Reduce(activated, w_down, False, part, from_side, from_corner, from_near, send_r, recv_r)
    reduce.products()
    load_down.wait()

    @pl.when((z == 0) | (z == members - 1))
    def _():
        down_found[members - 1 - z] = jnp.zeros_like(down_found[0])

    def add_down(span):
        value = down_found[0, span, :].astype(F32) + down_found[1, span, :].astype(F32)
        value = value + down_found[2, span, :].astype(F32) + down_found[3, span, :].astype(F32)
        down_found[0, span, :] = value.astype(BF16)

    each_chunk(down_found.shape[1], add_down)
    down = Gather(down_found.at[0], down_all, send_d, recv_d, local.at[1])

    def load_shard(turn):
        slot = turn % 2
        return pltpu.make_async_copy(branch_all.at[owner_at(turn)], shard.at[slot], load_sem.at[slot])

    def spread_back(turn, carry):
        for number, numbers in ARRIVALS:
            pl.when(turn == number)(functools.partial(gather.arrive, *numbers))

        @pl.when(turn == 0)
        def _():
            gather.keep.wait()

        load_shard(turn).start()
        load_shard(turn).wait()
        mixed_grad[owner_at(turn)] = (
            lax.dot_general(shard[turn % 2], w_out[...], NT, preferred_element_type=F32)
            .astype(BF16)
            .reshape(groups, rows // groups, 256)
        )
        return carry

    fetches[1].wait()
    lax.fori_loop(0, 4, spread_back, 0)
    reduce.launch()
    lax.fori_loop(4, 8, spread_back, 0)
    units.add()


    def halo(k, other):
        return to_mp(leaving.at[k], arriving.at[k], send.at[k], recv.at[k], other)

    def attend(k, carry):
        hot = hot_of(notes_all, k, rows)
        given = mixed_grad[:, pl.ds(k, 1)].reshape(rows, 256)
        grad_ordered = lax.dot_general(hot, given, TN, preferred_element_type=F32).astype(BF16)
        totals[...] = jnp.zeros_like(totals)
        for block in range(rows // 128):
            allowed = block_mask(notes_all, k, block, z, rows)
            for head in range(2):
                query = kept[k, pl.ds(64 + block * 128, 128), pl.ds(head * 128, 128)]
                keys = kept[k, pl.ds(block * 128, 192), pl.ds(256 + head * 128, 128)]
                values = kept[k, pl.ds(block * 128, 192), pl.ds(512 + head * 128, 128)]
                grad = grad_ordered[block * 128 : block * 128 + 128, head * 128 : head * 128 + 128]
                scores = lax.dot_general(query, keys, NT, preferred_element_type=F32) * scale
                scores = jnp.where(allowed, scores, -MASKED)
                weights = jnp.exp(scores - jnp.max(scores, axis=-1, keepdims=True))
                again = weights / jnp.sum(weights, axis=-1, keepdims=True)
                chance_grad = lax.dot_general(grad, values, NT, preferred_element_type=F32)
                row_dot = jnp.sum(again * chance_grad, axis=-1, keepdims=True)
                score_grad = (again * (chance_grad - row_dot)).astype(BF16)
                query_part[k, pl.ds(block * 128, 128), pl.ds(head * 128, 128)] = (
                    jnp.dot(score_grad, keys, preferred_element_type=F32) * scale
                ).astype(BF16)
                totals[pl.ds(block * 128, 192), pl.ds(head * 128, 128)] += (
                    lax.dot_general(score_grad, query, TN, preferred_element_type=F32) * scale
                )
                totals[pl.ds(block * 128, 192), pl.ds(256 + head * 128, 128)] += lax.dot_general(
                    again.astype(BF16), grad, TN, preferred_element_type=F32
                )
        key_value[k] = totals[pl.ds(64, rows), :].astype(BF16)
        ending[k] = totals[pl.ds(rows, 64), :]

        @pl.when(z > 0)
        def _():
            leaving[k] = totals[pl.ds(0, 64), :].astype(BF16)
            halo(k, z - 1).start()

        return carry

    wait_all(fetches[2:4])
    lax.fori_loop(0, 3, attend, 0)
    reduce.middle()
    down.start()
    lax.fori_loop(3, 7, attend, 0)
    down.pass_on()
    lax.fori_loop(7, groups, attend, 0)

    def restore(k, carry):
        @pl.when(z < members - 1)
        def _():
            halo(k, z).wait_recv()
            key_value[k, pl.ds(rows - 64, 64), :] = (
                ending[k] + arriving[k].astype(F32)
            ).astype(BF16)

        hot = hot_of(notes_all, k, rows)
        ordered = jnp.concatenate([query_part[k], key_value[k]], axis=1)
        back = jnp.dot(hot, ordered, preferred_element_type=F32).astype(BF16)
        out[:, pl.ds(k, 1)] = back.reshape(groups, 1, rows // groups, 768)
        return carry

    lax.fori_loop(0, groups, restore, 0)
    reduce.end()

    def body(span):
        result[span, :] = (middle[span, :] + reduce.rows_of(span)).astype(BF16)

    each_chunk(rows, body)
    down.finish()
    units.finish()
    for copy in gather.copies:
        copy.wait_send()
    reduce.finish()

    @pl.when(z > 0)
    def _():
        def done(k, carry):
            halo(k, z - 1).wait_send()
            return carry

        lax.fori_loop(0, groups, done, 0)


def attend_back(
    branch, notes_all, kept, w_out, activated, w_down, middle, both_sum, down_in, scale
):
    groups = kept.shape[0]
    rows, width = middle.shape
    members = both_sum.shape[0]
    dma = pltpu.SemaphoreType.DMA
    shape = jax.ShapeDtypeStruct
    return pl.pallas_call(
        functools.partial(backward_kernel, scale=scale, groups=groups, rows=rows),
        out_shape=(
            shape((groups, groups, rows // groups, 768), BF16),
            shape((rows, width), BF16),
            shape((groups, rows, width), BF16),
            shape((members, width, 256), BF16),
            shape((groups, LANES, width), BF16),
        ),
        in_specs=[on_chip()] * 2 + [anywhere()] * 7,
        out_specs=(on_chip(),) * 2 + (anywhere(),) * 3,
        scratch_shapes=[
            pltpu.VMEM((rows + 64, 512), F32),
            pltpu.VMEM((groups, rows, 256), BF16),
            pltpu.VMEM((groups, rows, 512), BF16),
            pltpu.VMEM((groups, 64, 512), F32),
            pltpu.VMEM((groups, 64, 512), BF16),
            pltpu.VMEM((groups, 64, 512), BF16),
            dma((groups,)),
            dma((groups,)),
        ]
        + reduce_scratch(rows, width)
        + [
            pltpu.VMEM((groups, groups, rows // groups, 256), BF16),
            pltpu.VMEM((2, rows, width), BF16),
            dma((3,)),
            dma((13,)),
            dma((13,)),
            pltpu.VMEM((2, width, 256), BF16),
            dma((6,)),
            dma((10,)),
            dma((3,)),
            pltpu.VMEM((members, LANES, width), BF16),
            dma((13,)),
            dma((13,)),
            pltpu.VMEM(kept.shape, BF16),
            pltpu.VMEM(w_out.shape, BF16),
            pltpu.VMEM(activated.shape, BF16),
            pltpu.VMEM((members * LANES, width), BF16),
            pltpu.VMEM((rows, width), F32),
            dma((5,)),
        ],
        compiler_params=remote_params(3, 63 * 1024 * 1024),
        cost_estimate=pl.CostEstimate(flops=0, bytes_accessed=300_000_000, transcendentals=0),
        name="attend_back",
    )(branch, notes_all, kept, w_out, activated, w_down, middle, both_sum, down_in)


def norm_back_rows(gradient, values, gain, sums, span):
    inverse = lax.rsqrt(mean_rows(values * values) + EPSILON)
    normed = values * inverse
    product = gradient * normed
    folded = product[0:8]
    for step in range(1, CHUNK // 8):
        folded = folded + product[step * 8 : step * 8 + 8]
    sums[...] += folded
    scaled = gradient * gain
    return inverse * (scaled - normed * mean_rows(scaled * normed))


def feed_kernel(
    mixed, w_out, tokens, cotangent_all, gate_all, w_up, down_weight, cotangent_own, gain,
    middle, middle_grad, branch, sums, activated_out, both_sum, down_in, up_all, down_all,
    hidden_all, both_grad, part, from_side, from_corner, from_near, send_r, recv_r,
    send_m, recv_m, send_a, recv_a, cot_shard, cot_tile, stage_both, down_sum, w_both, w_down,
    cotangent, activated, load_sem, local, send_z, recv_z, stage_down,
    up_own, down_own, send_u, recv_u, send_d, recv_d, first_sem,
):
    groups, rows, width = hidden_all.shape
    members = gate_all.shape[0]
    me = lax.axis_index("dp")
    barrier = greet_all()
    units_own = pl.ds(pl.multiple_of(me * LANES, LANES), LANES)
    first = start_all(
        [
            pltpu.make_async_copy(source, target, first_sem.at[number])
            for number, (source, target) in enumerate(
                (
                    (mixed, activated.at[:, :, pl.ds(0, 256)]),
                    (w_out, down_sum.at[pl.ds(0, 256)]),
                    (w_up.at[:, units_own], up_own),
                    (down_weight.at[units_own], down_own),
                    (tokens, cotangent),
                )
            )
        ]
    )
    gates = start_all(
        [
            pltpu.make_async_copy(
                gate_all.at[z], w_both.at[:, pl.ds(z * 256, 128)], load_sem.at[6 + z]
            )
            for z in range(members)
        ]
    )

    def slot_of(turn):
        block = turn // 2
        near = ((block + 1) // 2) % 2
        far = block // 3
        second = turn % 2
        other = (1 - near) * second + (block // 2) * near
        return 4 * other + 3 * (1 - near) * (1 - far) + near * (1 + second)

    def load_cotangent(turn):
        return pltpu.make_async_copy(
            cotangent_all.at[owner_at(turn)], cot_shard.at[turn % 2], load_sem.at[turn % 2]
        )

    load_cotangent(0).start()
    wait_all(first)
    pl.semaphore_wait(barrier, 13)
    columns_up = Column(up_own, up_all, send_u, recv_u, local.at[0])
    columns_down = Column(down_own, down_all, send_d, recv_d, local.at[2])
    columns_up.start()
    columns_down.start()
    project = Reduce(
        lambda owner: activated[owner, :, 0:256], down_sum.at[pl.ds(0, 256)], False,
        part, from_side, from_corner, from_near, send_m, recv_m,
    )
    project.begin()
    project.middle()
    columns_up.pass_on()
    columns_down.pass_on()
    project.end()

    def normalise(span):
        values = cotangent[span, :].astype(F32) + project.rows_of(span)
        middle_grad[span, :] = values
        inverse = lax.rsqrt(mean_rows(values * values) + EPSILON)
        hidden_all[me, span, :] = (values * inverse * gain[...]).astype(BF16)

    each_chunk(rows, normalise)
    project.finish()
    gather = Gather(None, hidden_all, send_a, recv_a)
    gather.start()
    store_middle = pltpu.make_async_copy(middle_grad, middle, local.at[1])
    load_own = pltpu.make_async_copy(cotangent_own, cotangent, local.at[3])
    store_middle.start()
    load_own.start()
    columns_up.finish()
    columns_down.finish()
    ups = start_all(
        [
            pltpu.make_async_copy(
                up_all.at[z], w_both.at[:, pl.ds(z * 256 + 128, 128)], load_sem.at[10 + z]
            )
            for z in range(members)
        ]
    )
    ups += start_all(
        [
            pltpu.make_async_copy(
                down_all.at[z], w_down.at[pl.ds(z * LANES, LANES)], load_sem.at[14 + z]
            )
            for z in range(members)
        ]
    )
    reduce = Reduce(None, None, False, part, from_side, from_corner, from_near, send_r, recv_r)
    reduce.prepare()

    def nears():
        reduce.add_side(1)
        reduce.nears[0].start()
        reduce.add_side(2)
        reduce.nears[2].start()

    early = [(turn, functools.partial(gather.arrive, *numbers)) for turn, numbers in ARRIVALS]
    early += [(6, nears)]
    late = [(1, 3), (4, 1), (5, 2), (7, 0)]
    wait_all(gates + ups)

    def unit(turn, carry):
        for number, action in early:
            pl.when(turn == number)(action)

        @pl.when(turn < 7)
        def _():
            load_cotangent(turn + 1).start()

        load_cotangent(turn).wait()
        owner, slot = owner_at(turn), slot_of(turn)
        mine = hidden_all[owner]
        grads = cot_shard[turn % 2]
        for z in range(members):
            raw = jnp.dot(mine, w_both[:, z * 256 : z * 256 + 256], preferred_element_type=F32)
            units = pl.ds(z * 128, 128)
            if z % 2 == 0:
                pair = lax.dot_general(
                    grads, w_down[pl.ds(z * 128, 256), :], NT, preferred_element_type=F32
                )
            active_grad = pair[:, 128 * (z % 2) : 128 * (z % 2) + 128]
            gate, upward = raw[:, :128], raw[:, 128:]
            sigmoid = jax.nn.sigmoid(gate)
            activated[owner, :, units] = (gate * sigmoid * upward).astype(BF16)
            both_grad[owner, :, pl.ds(z * 256, 128)] = (
                active_grad * upward * sigmoid * (1.0 + gate * (1.0 - sigmoid))
            ).astype(BF16)
            both_grad[owner, :, pl.ds(z * 256 + 128, 128)] = (
                active_grad * gate * sigmoid
            ).astype(BF16)

        def tile(t, inner):
            columns = pl.ds(pl.multiple_of(t * 256, 256), 256)
            part[slot, :, columns] = lax.dot_general(
                both_grad[owner], w_both[columns, :], NT, preferred_element_type=F32
            ).astype(BF16)
            return inner

        lax.fori_loop(0, width // 256, tile, 0)
        for number, share in late:
            pl.when(turn == number)(reduce.shares[share].start)
        return carry

    lax.fori_loop(0, 8, unit, 0)
    store_activated = pltpu.make_async_copy(activated, activated_out, local.at[4])
    store_activated.start()

    def load_tile(t):
        columns = pl.ds(pl.multiple_of(t * 256, 256), 256)
        return pltpu.make_async_copy(
            cotangent_all.at[:, :, columns], cot_tile.at[t % 2], load_sem.at[2 + t % 2]
        )

    def store_both(t):
        columns = pl.ds(pl.multiple_of(t * 256, 256), 256)
        return pltpu.make_async_copy(
            stage_both.at[t % 2], both_sum.at[:, columns], load_sem.at[4 + t % 2]
        )

    tiles = width // 256
    count = groups * rows

    def down_tile(t, carry):
        columns = pl.ds(pl.multiple_of(t * 256, 256), 256)

        @pl.when(t < tiles - 1)
        def _():
            load_tile(t + 1).start()

        load_tile(t).wait()
        down_sum[:, columns] = lax.dot_general(
            activated[...].reshape(count, members * 128),
            cot_tile[t % 2].reshape(count, 256),
            TN,
            preferred_element_type=F32,
        ).astype(BF16)
        return carry

    z = lax.axis_index("mp")

    def down_rows(owner):
        return down_sum.at[pl.ds(pl.multiple_of(owner * LANES, LANES), LANES)]

    keep_down = pltpu.make_async_copy(down_rows(z), down_in.at[z], local.at[5])
    passing = Units(down_rows, down_in, stage_down, send_z, recv_z, local.at[pl.ds(6, 1)])

    def weight_tile(t, carry):
        columns = pl.ds(pl.multiple_of(t * 256, 256), 256)

        @pl.when(t >= 2)
        def _():
            store_both(t - 2).wait()

        value = lax.dot_general(
            hidden_all[:, :, columns].reshape(count, 256),
            both_grad[...].reshape(count, members * 256),
            TN,
            preferred_element_type=F32,
        )
        for z in range(members):
            stage_both[t % 2, z] = value[:, z * 256 : z * 256 + 256].astype(BF16)
        store_both(t).start()
        return carry

    load_tile(0).start()
    reduce.add_side(0)
    reduce.corners[0].start()
    reduce.corners[1].start()
    lax.fori_loop(0, tiles, down_tile, 0)
    keep_down.start()
    passing.start()
    lax.fori_loop(0, 2, weight_tile, 0)
    reduce.middle()
    passing.add()
    lax.fori_loop(2, tiles, weight_tile, 0)
    reduce.end()
    store_middle.wait()
    load_own.wait()
    sums[...] = jnp.zeros_like(sums)

    def body(span):
        change = norm_back_rows(reduce.rows_of(span), middle_grad[span, :], gain[...], sums, span)
        total = cotangent[span, :].astype(F32) + change
        middle_grad[span, :] = total
        branch[span, :] = total.astype(BF16)

    each_chunk(rows, body)
    gather.sent()
    reduce.finish()
    for t in (tiles - 2, tiles - 1):
        store_both(t).wait()
    keep_down.wait()
    store_activated.wait()
    passing.finish()


def feed(mixed, w_out, tokens, cotangent_all, gate_all, w_up, w_down, cotangent, gain):
    groups, rows, width = cotangent_all.shape
    members = gate_all.shape[0]
    dma = pltpu.SemaphoreType.DMA
    units = members * 128
    return pl.pallas_call(
        feed_kernel,
        out_shape=(
            jax.ShapeDtypeStruct((rows, width), F32),
            jax.ShapeDtypeStruct((rows, width), F32),
            jax.ShapeDtypeStruct((rows, width), BF16),
            jax.ShapeDtypeStruct((8, width), F32),
            jax.ShapeDtypeStruct((groups, rows, units), BF16),
            jax.ShapeDtypeStruct((members, width, 256), BF16),
            jax.ShapeDtypeStruct((members, LANES, width), BF16),
            jax.ShapeDtypeStruct((members, width, LANES), BF16),
            jax.ShapeDtypeStruct((members, LANES, width), BF16),
        ),
        in_specs=[anywhere()] * 8 + [on_chip()],
        out_specs=(anywhere(),) + (on_chip(),) * 3 + (anywhere(),) * 5,
        scratch_shapes=[
            pltpu.VMEM((groups, rows, width), BF16),
            pltpu.VMEM((groups, rows, 2 * units), BF16),
        ]
        + reduce_scratch(rows, width)
        + [
            dma((10,)),
            dma((10,)),
            dma((13,)),
            dma((13,)),
            pltpu.VMEM((2, rows, width), BF16),
            pltpu.VMEM((2, groups, rows, 256), BF16),
            pltpu.VMEM((2, members, 256, 256), BF16),
            pltpu.VMEM((units, width), BF16),
            pltpu.VMEM((width, 2 * units), BF16),
            pltpu.VMEM((units, width), BF16),
            pltpu.VMEM((rows, width), BF16),
            pltpu.VMEM((groups, rows, units), BF16),
            dma((6 + 4 * members,)),
            dma((7,)),
            dma((6,)),
            dma((10,)),
            pltpu.VMEM((2, LANES, width), BF16),
            pltpu.VMEM((width, LANES), BF16),
            pltpu.VMEM((LANES, width), BF16),
            dma((4,)),
            dma((4,)),
            dma((4,)),
            dma((4,)),
            dma((5,)),
        ],
        compiler_params=remote_params(5, 63 * 1024 * 1024),
        cost_estimate=pl.CostEstimate(flops=0, bytes_accessed=400_000_000, transcendentals=0),
        name="feed",
    )(mixed, w_out, tokens, cotangent_all, gate_all, w_up, w_down, cotangent, gain)


def input_kernel(
    qkv_grad, w_qkv, hidden_all, branch_all, mixed_in, tokens_in, middle_in, gain, sums_two,
    both_sum, both_in,
    result, gains, both_all, heads_all,
    part, from_side, from_corner, from_near, send, recv, sums,
    stage, arrive, send_h, recv_s, recv_h, own, plane_sums, column_sums, send_p, recv_p,
    weight_sum, row_tile, tile_sem, send_b, recv_b, send_t, recv_t, both_found, heads_own, local,
    mixed, tokens, middle_grad, fetch_sem,
):
    me, z = lax.axis_index("dp"), lax.axis_index("mp")
    barrier = greet_all()
    count = qkv_grad.shape[0]
    tiles = tokens.shape[1] // 256
    outer = (z == 0) | (z == 3)

    def columns_of(t):
        return pl.ds(pl.multiple_of(lax.rem(t, tiles) * 256, 256), 256)

    def load(t, source):
        return pltpu.make_async_copy(
            source.at[:, :, columns_of(t)], row_tile.at[t % 2], tile_sem.at[t % 2]
        )

    own_part = pltpu.make_async_copy(both_sum.at[z], both_found.at[0], local.at[0])
    own_part.start()
    ways = [(outer, 1, 1), (outer, 2, 2)]
    ways += [(z == 1, 0, 1), (z == 1, 2, 2), (z == 1, 3, 3)]
    ways += [(z == 2, 0, 1), (z == 2, 1, 2), (z == 2, 3, 3)]

    def came(source, place):
        return pltpu.make_async_copy(both_in.at[source], both_found.at[place], local.at[place])

    for here, source, place in ways:
        pl.when(here)(came(source, place).start)

    @pl.when(outer)
    def _():
        both_found[3] = jnp.zeros_like(both_found[3])

    load(0, hidden_all).start()
    fetches = start_all(
        [
            pltpu.make_async_copy(source, target, fetch_sem.at[number])
            for number, (source, target) in enumerate(
                ((mixed_in, mixed), (tokens_in, tokens), (middle_in, middle_grad))
            )
        ]
    )
    pl.semaphore_wait(barrier, 13)
    both = Gather(both_found.at[0], both_all, send_b, recv_b, local.at[4])

    def weight_tile(t, carry):
        @pl.when(t < tiles - 1)
        def _():
            load(t + 1, hidden_all).start()

        @pl.when((t >= tiles - 1) & (t < 2 * tiles - 1))
        def _():
            load(t + 1, branch_all).start()

        load(t, hidden_all).wait()

        @pl.when(t < tiles)
        def _():
            weight_sum[pl.ds(0, 768), columns_of(t)] = lax.dot_general(
                qkv_grad[...], row_tile[t % 2].reshape(count, 256), TN, preferred_element_type=F32
            ).astype(BF16)

        @pl.when(t >= tiles)
        def _():
            weight_sum[pl.ds(768, 256), columns_of(t)] = lax.dot_general(
                mixed[...], row_tile[t % 2].reshape(count, 256), TN, preferred_element_type=F32
            ).astype(BF16)

        return carry

    heads = Heads(weight_sum, stage, arrive, send_h, recv_s, recv_h)
    reduce = Reduce(qkv_grad, w_qkv, False, part, from_side, from_corner, from_near, send, recv)
    own_part.wait()
    for here, source, place in ways:
        pl.when(here)(came(source, place).wait)

    def add(span):
        value = both_found[0, span, :].astype(F32) + both_found[1, span, :].astype(F32)
        value = value + both_found[2, span, :].astype(F32) + both_found[3, span, :].astype(F32)
        both_found[0, span, :] = value.astype(BF16)

    each_chunk(both_found.shape[1], add)
    both.start()
    lax.fori_loop(0, tiles, weight_tile, 0)
    heads.start((0, 1, 2))
    wait_all(fetches)
    lax.fori_loop(tiles, 2 * tiles, weight_tile, 0)
    heads.start((3,))
    both.pass_on()
    reduce.begin()
    heads.add((0, 1))
    reduce.middle()
    heads.add((2, 3))
    reduce.end()
    sums[...] = jnp.zeros_like(sums)

    def body(span):
        values = tokens[span, :].astype(F32)
        change = norm_back_rows(reduce.rows_of(span), values, gain[...], sums, span)
        result[span, :] = (middle_grad[span, :] + change).astype(BF16)

    each_chunk(result.shape[0], body)
    own[...] = jnp.concatenate(
        [
            jnp.sum(sums[...], axis=0, keepdims=True),
            jnp.sum(sums_two[...], axis=0, keepdims=True),
        ],
        axis=0,
    )
    swaps = swap_all(own, plane_sums, send_p, recv_p)
    for copy in swaps:
        copy.start()
    plane_sums[me] = own[...]
    heads.total(heads_own)
    gather = Gather(heads_own, heads_all, send_t, recv_t, local.at[5])
    gather.start()
    for copy in swaps:
        copy.wait()
    found = plane_sums[0]
    for other in range(1, 8):
        found = found + plane_sums[other]
    column_sums[z] = found
    passes = [
        to_mp(
            column_sums.at[z],
            column_sums.at[z],
            send_p.at[6 + step],
            recv_p.at[6 + step],
            lax.rem(z + step, 4),
        )
        for step in range(1, 4)
    ]
    for copy in passes:
        copy.start()
    both.finish()
    for copy in passes:
        copy.wait()
    gains[...] = (column_sums[0] + column_sums[1]) + (column_sums[2] + column_sums[3])
    gather.pass_on()
    heads.finish_send()
    reduce.finish()
    gather.finish()


def project_input(
    qkv_grad, w_qkv, hidden_all, branch_all, mixed, tokens, middle_grad, gain, sums_two,
    both_sum, both_in,
):
    rows, width = tokens.shape
    groups = hidden_all.shape[0]
    dma = pltpu.SemaphoreType.DMA
    shape = jax.ShapeDtypeStruct
    return pl.pallas_call(
        input_kernel,
        out_shape=(
            shape((rows, width), BF16),
            shape((2, width), F32),
            shape((groups, width, 256), BF16),
            shape((groups, 4 * HEAD_DIM, width // 2), BF16),
        ),
        in_specs=[on_chip()] * 2 + [anywhere()] * 5 + [on_chip()] * 2 + [anywhere()] * 2,
        out_specs=(on_chip(),) * 2 + (anywhere(),) * 2,
        scratch_shapes=reduce_scratch(rows, width)
        + [
            pltpu.VMEM((8, width), F32),
            pltpu.VMEM((2, 4, HEAD_DIM, width), BF16),
            pltpu.VMEM((3, 4, HEAD_DIM, width // 2), BF16),
            dma((16,)),
            dma((8,)),
            dma((12,)),
            pltpu.VMEM((2, width), F32),
            pltpu.VMEM((8, 2, width), F32),
            pltpu.VMEM((4, 2, width), F32),
            dma((10,)),
            dma((10,)),
            pltpu.VMEM((8 * LANES, width), BF16),
            pltpu.VMEM((2, groups, rows, 256), BF16),
            dma((2,)),
            dma((13,)),
            dma((13,)),
            dma((13,)),
            dma((13,)),
            pltpu.VMEM((4, width, 256), BF16),
            pltpu.VMEM((4 * HEAD_DIM, width // 2), BF16),
            dma((6,)),
            pltpu.VMEM(mixed.shape, BF16),
            pltpu.VMEM((rows, width), BF16),
            pltpu.VMEM((rows, width), F32),
            dma((3,)),
        ],
        compiler_params=remote_params(6, 63 * 1024 * 1024),
        cost_estimate=pl.CostEstimate(flops=0, bytes_accessed=250_000_000, transcendentals=0),
        name="project_input",
    )(
        qkv_grad, w_qkv, hidden_all, branch_all, mixed, tokens, middle_grad, gain, sums_two,
        both_sum, both_in,
    )


def assemble_kernel(
    both, down, heads, order_column, output_b, input_b,
    output, inputs, query, keys, values, project, gate, upward, down_out,
):
    for d in range(both.shape[0]):
        gate[:, d * 128 : d * 128 + 128] = both[d, :, :128].astype(F32)
        upward[:, d * 128 : d * 128 + 128] = both[d, :, 128:].astype(F32)
    down_out[...] = down[0].astype(F32)
    for kind, out in enumerate((query, keys, values, project)):
        out[...] = heads[0, kind].astype(F32)
    place = lax.broadcasted_iota(jnp.int32, (order_column.shape[0], output_b.shape[0]), 1)
    unsort = (place.astype(F32) == order_column[...]).astype(BF16)
    output[...] = jnp.dot(unsort, output_b[...], preferred_element_type=F32).astype(BF16)
    inputs[...] = jnp.dot(unsort, input_b[...], preferred_element_type=F32).astype(BF16)


def assemble(both, down, heads, order_column, output_b, input_b):
    groups, width, wide = both.shape
    rows = output_b.shape[0]
    units = down.shape[1]
    chips = groups // 2
    columns = heads.shape[3]
    row_tile, tile = rows // groups, width // groups
    shape = jax.ShapeDtypeStruct
    head = shape((chips * HEAD_DIM, 2 * columns), F32)
    head_spec = pl.BlockSpec((HEAD_DIM, columns), lambda i: (i // 2, i % 2))
    wide_spec = pl.BlockSpec((tile, groups * units), lambda i: (i, 0))
    row_spec = pl.BlockSpec((row_tile, width), lambda i: (i, 0))
    whole_spec = pl.BlockSpec((rows, width), lambda i: (0, 0))
    return pl.pallas_call(
        assemble_kernel,
        grid=(groups,),
        out_shape=(
            shape((rows, width), BF16),
            shape((rows, width), BF16),
            head,
            head,
            head,
            head,
            shape((width, groups * units), F32),
            shape((width, groups * units), F32),
            shape((groups * units, width), F32),
        ),
        in_specs=[
            pl.BlockSpec((groups, tile, wide), lambda i: (0, i, 0)),
            pl.BlockSpec((1, units, width), lambda i: (i, 0, 0)),
            pl.BlockSpec((1, 4, HEAD_DIM, columns), lambda i: (i, 0, 0, 0)),
            pl.BlockSpec((row_tile, 1), lambda i: (i, 0)),
            whole_spec,
            whole_spec,
        ],
        out_specs=(
            row_spec, row_spec, head_spec, head_spec, head_spec, head_spec, wide_spec, wide_spec,
            pl.BlockSpec((units, width), lambda i: (i, 0)),
        ),
        compiler_params=pltpu.CompilerParams(vmem_limit_bytes=VMEM_LIMIT),
        cost_estimate=pl.CostEstimate(flops=0, bytes_accessed=58_000_000, transcendentals=0),
        name="assemble",
    )(both, down, heads, order_column, output_b, input_b)


def swapped(
    tokens, cotangent, route, lengths, key_mask, norm1_gain, norm2_gain,
    w_query, w_key, w_value, w_out, w_gate, w_up, w_down,
):
    groups = lax.axis_size("dp")
    members = lax.axis_size("mp")
    me = lax.axis_index("dp")
    z = lax.axis_index("mp")
    rows, width = tokens.shape
    bucket = rows // groups
    units = w_down.shape[0] // groups

    target = route // TOK_DEV
    earlier = jnp.arange(rows, dtype=jnp.int32)
    same = (target[:, None] == target[None, :]) & (earlier[None, :] < earlier[:, None])
    send_at = target * bucket + jnp.sum(same.astype(jnp.int32), axis=1)
    sorting = send_at[None, :] == earlier[:, None]
    slots_own = jnp.sum(jnp.where(sorting, (route % rows)[None, :], 0), axis=1)

    mask_window = lax.dynamic_slice_in_dim(
        jnp.concatenate([jnp.zeros((WINDOW,), jnp.int32), key_mask]), z * rows, rows + WINDOW
    )
    slot_rows = jnp.pad(slots_own.reshape(groups, bucket).T, ((0, 0), (0, LANES - groups)))
    mask_rows = jnp.pad(mask_window, (0, 4 * LANES - rows - WINDOW)).reshape(4, LANES)
    length_rows = jnp.pad(lengths, ((0, 3), (0, LANES - lengths.shape[1])))
    notes = jnp.concatenate([slot_rows, mask_rows, length_rows], axis=0).astype(F32)

    count = groups * rows
    scale = HEAD_DIM ** (-0.5)
    (
        hidden_one,
        w_qkv,
        w_proj,
        notes_all,
        gate_all,
        mixed,
        kept,
        tokens_b,
        cotangent_b,
        cotangent_all,
    ) = attend_ahead(
        tokens,
        cotangent,
        send_at.astype(F32)[None],
        norm1_gain[None],
        notes,
        w_query.T,
        w_key.T,
        w_value.T,
        w_out,
        w_gate,
        scale,
    )
    mixed = mixed.reshape(count, 2 * LANES)
    middle, middle_grad, branch, sums_two, activated, both_sum, down_in, _, down_all = feed(
        mixed.reshape(groups, rows, 2 * LANES),
        w_proj,
        tokens_b,
        cotangent_all,
        gate_all,
        w_up,
        w_down,
        cotangent_b,
        norm2_gain[None],
    )
    qkv_grad, output_rows, branch_all, both_in, down_whole = attend_back(
        branch,
        notes_all,
        kept,
        w_proj,
        activated.reshape(count, units * members),
        down_all.reshape(members * units, width),
        middle,
        both_sum,
        down_in,
        scale,
    )
    qkv_grad = qkv_grad.reshape(count, 6 * LANES)
    input_rows, gain_sums, both_whole, heads_whole = project_input(
        qkv_grad,
        w_qkv,
        hidden_one,
        branch_all,
        mixed,
        tokens_b,
        middle_grad,
        norm1_gain[None],
        sums_two,
        both_sum,
        both_in,
    )
    (
        output,
        input_grad,
        query_grad,
        key_grad,
        value_grad,
        proj_grad,
        gate_grad,
        up_grad,
        down_grad,
    ) = assemble(
        both_whole,
        down_whole,
        heads_whole.reshape(groups, 4, HEAD_DIM, width // 2),
        send_at.astype(F32)[:, None],
        output_rows,
        input_rows,
    )
    return (
        output,
        input_grad,
        gain_sums[0],
        gain_sums[1],
        query_grad.T,
        key_grad.T,
        value_grad.T,
        proj_grad,
        gate_grad,
        up_grad,
        down_grad,
    )


def solution(mesh):
    in_specs = (
        P(("dp", "mp"), None),
        P(("dp", "mp"), None),
        P(("dp", "mp")),
        P("dp", None),
        P("dp"),
        P(),
        P(),
        P(None, "mp"),
        P(None, "mp"),
        P(None, "mp"),
        P("mp", None),
        P(None, "mp"),
        P(None, "mp"),
        P("mp", None),
    )
    out_specs = (
        P(("dp", "mp"), None),
        P(("dp", "mp"), None),
        P(),
        P(),
        P(None, "mp"),
        P(None, "mp"),
        P(None, "mp"),
        P("mp", None),
        P(None, "mp"),
        P(None, "mp"),
        P("mp", None),
    )
    body = swapped if (mesh.shape["dp"], mesh.shape["mp"]) == (8, 4) else local
    return jax.shard_map(body, mesh=mesh, in_specs=in_specs, out_specs=out_specs, check_vma=False)
```

```python
import functools

import jax
import jax.numpy as jnp
from jax import lax
from jax.experimental import pallas as pl
from jax.experimental.pallas import tpu as pltpu
from jax.sharding import PartitionSpec as P

HEAD_DIM = 112
WINDOW = 64
TOK_DEV = 1536


EPSILON = 1e-05
MASKED = 1e30


def norm_rows(values):
    inverse = lax.rsqrt(jnp.mean(values * values, axis=-1, keepdims=True) + EPSILON)
    return (values * inverse, inverse)


def norm_back(gradient, normed, inverse, norm_gain):
    scaled = gradient * norm_gain
    result = inverse * (scaled - normed * jnp.mean(scaled * normed, axis=-1, keepdims=True))
    return (result, jnp.sum(gradient * normed, axis=0))


def padded(values, filler):
    front = jnp.full((WINDOW,) + values.shape[1:], filler, values.dtype)
    return jnp.concatenate([front, values], axis=0)


def block_scores(query_block, key_block, query_seg, key_seg, key_flag, first_row, score_scale):
    query_pos = first_row + jnp.arange(query_block.shape[0], dtype=jnp.int32)
    key_pos = first_row - WINDOW + jnp.arange(key_block.shape[0], dtype=jnp.int32)
    distance = query_pos[:, None] - key_pos[None, :]
    allowed = (distance >= 0) & (distance < WINDOW) & (query_seg[:, None] == key_seg[None, :])
    allowed = allowed & ((key_flag[None, :] == 1) | (distance == 0))
    raw_scores = (
        jnp.einsum("qhd,khd->hqk", query_block, key_block, preferred_element_type=jnp.float32)
        * score_scale
    )
    return jnp.where(allowed[None], raw_scores, -MASKED)


def block_inputs(query, key_pad, value_pad, segment, seg_pad, live_pad, first_row, block_rows):
    key_span = block_rows + WINDOW
    return (
        lax.dynamic_slice_in_dim(query, first_row, block_rows, 0),
        lax.dynamic_slice_in_dim(key_pad, first_row, key_span, 0),
        lax.dynamic_slice_in_dim(value_pad, first_row, key_span, 0),
        lax.dynamic_slice_in_dim(segment, first_row, block_rows, 0),
        lax.dynamic_slice_in_dim(seg_pad, first_row, key_span, 0),
        lax.dynamic_slice_in_dim(live_pad, first_row, key_span, 0),
    )


def attend_forward(query, key_all, value_all, segment, key_live):
    token_count, head_count, head_width = query.shape
    block_rows = min(512, token_count)
    score_scale = head_width ** (-0.5)
    key_pad = padded(key_all, 0.0)
    value_pad = padded(value_all, 0.0)
    seg_pad = padded(segment, -1)
    live_pad = padded(key_live, 0)

    def one_block(running, block_index):
        first_row = block_index * block_rows
        query_block, key_block, value_block, query_seg, key_seg, key_flag = block_inputs(
            query, key_pad, value_pad, segment, seg_pad, live_pad, first_row, block_rows
        )
        scores = block_scores(
            query_block, key_block, query_seg, key_seg, key_flag, first_row, score_scale
        )
        row_max = jnp.max(scores, axis=-1, keepdims=True)
        weights = jnp.exp(scores - row_max)
        denominator = jnp.sum(weights, axis=-1, keepdims=True)
        chances = (weights / denominator).astype(jnp.bfloat16)
        mixed = jnp.einsum("hqk,khd->qhd", chances, value_block, preferred_element_type=jnp.float32)
        return (
            running,
            (mixed.astype(jnp.bfloat16), row_max[..., 0] + jnp.log(denominator[..., 0])),
        )

    _, (mixed, logsum) = lax.scan(
        one_block, jnp.zeros((), jnp.int32), jnp.arange(token_count // block_rows, dtype=jnp.int32)
    )
    return (mixed.reshape(token_count, head_count * head_width), logsum)


def attend_backward(query, key_all, value_all, segment, key_live, logsum, mixed_grad):
    token_count, head_count, head_width = query.shape
    block_rows = min(512, token_count)
    key_span = block_rows + WINDOW
    score_scale = head_width ** (-0.5)
    key_pad = padded(key_all, 0.0)
    value_pad = padded(value_all, 0.0)
    seg_pad = padded(segment, -1)
    live_pad = padded(key_live, 0)

    def one_block(running, inputs):
        key_grad, value_grad = running
        block_index, block_logsum = inputs
        first_row = block_index * block_rows
        query_block, key_block, value_block, query_seg, key_seg, key_flag = block_inputs(
            query, key_pad, value_pad, segment, seg_pad, live_pad, first_row, block_rows
        )
        grad_block = lax.dynamic_slice_in_dim(mixed_grad, first_row, block_rows, 0)
        scores = block_scores(
            query_block, key_block, query_seg, key_seg, key_flag, first_row, score_scale
        )
        chances = jnp.exp(scores - block_logsum[..., None])
        chance_grad = jnp.einsum(
            "qhd,khd->hqk", grad_block, value_block, preferred_element_type=jnp.float32
        )
        row_dot = jnp.sum(chances * chance_grad, axis=-1, keepdims=True)
        score_grad = (chances * (chance_grad - row_dot)).astype(jnp.bfloat16)
        query_grad = (
            jnp.einsum("hqk,khd->qhd", score_grad, key_block, preferred_element_type=jnp.float32)
            * score_scale
        )
        key_part = (
            jnp.einsum("hqk,qhd->khd", score_grad, query_block, preferred_element_type=jnp.float32)
            * score_scale
        )
        value_part = jnp.einsum(
            "hqk,qhd->khd",
            chances.astype(jnp.bfloat16),
            grad_block,
            preferred_element_type=jnp.float32,
        )
        key_grad = lax.dynamic_update_slice_in_dim(
            key_grad,
            lax.dynamic_slice_in_dim(key_grad, first_row, key_span, 0) + key_part,
            first_row,
            0,
        )
        value_grad = lax.dynamic_update_slice_in_dim(
            value_grad,
            lax.dynamic_slice_in_dim(value_grad, first_row, key_span, 0) + value_part,
            first_row,
            0,
        )
        return ((key_grad, value_grad), query_grad)

    empty_grad = jnp.zeros((token_count + WINDOW, head_count, head_width), jnp.float32)
    (key_grad, value_grad), query_grad = lax.scan(
        one_block,
        (empty_grad, empty_grad),
        (jnp.arange(token_count // block_rows, dtype=jnp.int32), logsum),
    )
    flat_width = head_count * head_width
    return (
        query_grad.reshape(token_count, flat_width).astype(jnp.bfloat16),
        key_grad[WINDOW:].reshape(token_count, flat_width).astype(jnp.bfloat16),
        value_grad[WINDOW:].reshape(token_count, flat_width).astype(jnp.bfloat16),
    )


def local(
    tokens,
    cotangent,
    route,
    lengths,
    key_mask,
    norm1_gain,
    norm2_gain,
    w_query,
    w_key,
    w_value,
    w_out,
    w_gate,
    w_up,
    w_down,
):
    groups = lax.axis_size("dp")
    members = lax.axis_size("mp")
    member = lax.axis_index("mp")
    local_rows = tokens.shape[0]
    group_rows = local_rows * members
    bucket = local_rows // groups
    target = route // TOK_DEV
    chosen = (target[:, None] == jnp.arange(groups, dtype=jnp.int32)[None, :]).astype(jnp.int32)
    ranking = jnp.sum((jnp.cumsum(chosen, axis=0) - chosen) * chosen, axis=1)
    send_at = target * bucket + ranking
    arrival, arrival_grad, arrival_slot = (
        lax.all_to_all(
            jnp.zeros_like(tokens).at[send_at].set(tokens),
            "dp",
            split_axis=0,
            concat_axis=0,
            tiled=True,
        ),
        lax.all_to_all(
            jnp.zeros_like(cotangent).at[send_at].set(cotangent),
            "dp",
            split_axis=0,
            concat_axis=0,
            tiled=True,
        ),
        lax.all_to_all(
            jnp.zeros_like(route).at[send_at].set(route % local_rows),
            "dp",
            split_axis=0,
            concat_axis=0,
            tiled=True,
        ),
    )
    token_rows = jnp.zeros_like(arrival).at[arrival_slot].set(arrival)
    grad_rows = jnp.zeros_like(arrival_grad).at[arrival_slot].set(arrival_grad)
    seq_ends = jnp.cumsum(lengths[0])
    positions = jnp.arange(group_rows, dtype=jnp.int32)
    segment = jnp.sum((positions[:, None] >= seq_ends[None, :]).astype(jnp.int32), axis=1)
    input_rows = token_rows.astype(jnp.float32)
    normed_one, inverse_one = norm_rows(input_rows)
    leading_all, grad_all = (
        lax.all_gather(token_rows, "mp", axis=0, tiled=True),
        lax.all_gather(grad_rows, "mp", axis=0, tiled=True),
    )
    input_all = leading_all.astype(jnp.float32)
    normed_all, _ = norm_rows(input_all)
    hidden_one = (normed_all * norm1_gain).astype(jnp.bfloat16)
    head_count = w_query.shape[1] // HEAD_DIM
    query = jnp.dot(hidden_one, w_query, preferred_element_type=jnp.float32).astype(jnp.bfloat16)
    keys = jnp.dot(hidden_one, w_key, preferred_element_type=jnp.float32).astype(jnp.bfloat16)
    values = jnp.dot(hidden_one, w_value, preferred_element_type=jnp.float32).astype(jnp.bfloat16)
    query_heads = query.reshape(group_rows, head_count, HEAD_DIM)
    key_heads = keys.reshape(group_rows, head_count, HEAD_DIM)
    value_heads = values.reshape(group_rows, head_count, HEAD_DIM)
    mixed_flat, logsum = attend_forward(query_heads, key_heads, value_heads, segment, key_mask)
    attention_all = lax.psum(jnp.dot(mixed_flat, w_out, preferred_element_type=jnp.float32), "mp")
    middle_all = input_all + attention_all
    middle_rows = lax.dynamic_slice_in_dim(middle_all, member * local_rows, local_rows, 0)
    normed_mid, _ = norm_rows(middle_all)
    hidden_two = (normed_mid * norm2_gain).astype(jnp.bfloat16)
    normed_two, inverse_two = norm_rows(middle_rows)
    gate_value = jnp.dot(hidden_two, w_gate, preferred_element_type=jnp.float32)
    upward = jnp.dot(hidden_two, w_up, preferred_element_type=jnp.float32)
    sigmoid = jax.nn.sigmoid(gate_value)
    activated = (gate_value * sigmoid * upward).astype(jnp.bfloat16)
    out_rows = middle_rows + lax.psum_scatter(
        jnp.dot(activated, w_down, preferred_element_type=jnp.float32).astype(jnp.bfloat16),
        "mp",
        scatter_dimension=0,
        tiled=True,
    ).astype(jnp.float32)
    activated_grad = jnp.einsum("td,fd->tf", grad_all, w_down, preferred_element_type=jnp.float32)
    gate_grad = (activated_grad * upward * sigmoid * (1.0 + gate_value * (1.0 - sigmoid))).astype(
        jnp.bfloat16
    )
    upward_grad = (activated_grad * gate_value * sigmoid).astype(jnp.bfloat16)
    down_sum = jnp.einsum("tf,td->fd", activated, grad_all, preferred_element_type=jnp.float32)
    gate_sum = jnp.einsum("td,tf->df", hidden_two, gate_grad, preferred_element_type=jnp.float32)
    upward_sum = jnp.einsum(
        "td,tf->df", hidden_two, upward_grad, preferred_element_type=jnp.float32
    )
    hidden_two_grad = lax.psum_scatter(
        jnp.einsum("tf,df->td", gate_grad, w_gate, preferred_element_type=jnp.float32)
        + jnp.einsum("tf,df->td", upward_grad, w_up, preferred_element_type=jnp.float32),
        "mp",
        scatter_dimension=0,
        tiled=True,
    )
    norm_part_two, gain_two_grad = norm_back(hidden_two_grad, normed_two, inverse_two, norm2_gain)
    middle_grad = grad_rows.astype(jnp.float32) + norm_part_two
    branch_all = lax.all_gather(middle_grad.astype(jnp.bfloat16), "mp", axis=0, tiled=True)
    output_sum = jnp.einsum("tc,td->cd", mixed_flat, branch_all, preferred_element_type=jnp.float32)
    mixed_grad = jnp.einsum(
        "td,cd->tc", branch_all, w_out, preferred_element_type=jnp.float32
    ).astype(jnp.bfloat16)
    query_grad, key_grad, value_grad = attend_backward(
        query_heads,
        key_heads,
        value_heads,
        segment,
        key_mask,
        logsum,
        mixed_grad.reshape(group_rows, head_count, HEAD_DIM),
    )
    query_sum = jnp.einsum("td,tc->dc", hidden_one, query_grad, preferred_element_type=jnp.float32)
    key_sum = jnp.einsum("td,tc->dc", hidden_one, key_grad, preferred_element_type=jnp.float32)
    value_sum = jnp.einsum("td,tc->dc", hidden_one, value_grad, preferred_element_type=jnp.float32)
    hidden_one_grad = lax.psum_scatter(
        (
            jnp.einsum("tc,dc->td", query_grad, w_query, preferred_element_type=jnp.float32)
            + jnp.einsum("tc,dc->td", key_grad, w_key, preferred_element_type=jnp.float32)
            + jnp.einsum("tc,dc->td", value_grad, w_value, preferred_element_type=jnp.float32)
        ).astype(jnp.bfloat16),
        "mp",
        scatter_dimension=0,
        tiled=True,
    ).astype(jnp.float32)
    norm_part_one, gain_one_grad = norm_back(hidden_one_grad, normed_one, inverse_one, norm1_gain)
    input_grad = middle_grad + norm_part_one
    gain_one_sum, gain_two_sum = lax.psum((gain_one_grad, gain_two_grad), ("dp", "mp"))
    weight_sums = (
        lax.psum(query_sum.astype(jnp.bfloat16), "dp").astype(jnp.float32),
        lax.psum(key_sum.astype(jnp.bfloat16), "dp").astype(jnp.float32),
        lax.psum(value_sum.astype(jnp.bfloat16), "dp").astype(jnp.float32),
        lax.psum(output_sum.astype(jnp.bfloat16), "dp").astype(jnp.float32),
        lax.psum(gate_sum.astype(jnp.bfloat16), "dp").astype(jnp.float32),
        lax.psum(upward_sum.astype(jnp.bfloat16), "dp").astype(jnp.float32),
        lax.psum(down_sum.astype(jnp.bfloat16), "dp").astype(jnp.float32),
    )
    back_out, back_grad = (
        lax.all_to_all(
            out_rows.astype(jnp.bfloat16)[arrival_slot],
            "dp",
            split_axis=0,
            concat_axis=0,
            tiled=True,
        ),
        lax.all_to_all(
            input_grad.astype(jnp.bfloat16)[arrival_slot],
            "dp",
            split_axis=0,
            concat_axis=0,
            tiled=True,
        ),
    )
    return (
        back_out[send_at],
        back_grad[send_at],
        gain_one_sum,
        gain_two_sum,
        weight_sums[0],
        weight_sums[1],
        weight_sums[2],
        weight_sums[3],
        weight_sums[4],
        weight_sums[5],
        weight_sums[6],
    )


MESH = pl.DeviceIdType.MESH
LANES = 128
F32 = jnp.float32
BF16 = jnp.bfloat16
VMEM_LIMIT = 56 * 1024 * 1024


def plane():
    me = lax.axis_index("dp")
    side = me + 1 - 2 * lax.rem(me, 2)
    over_x = me + 2 - 4 * lax.rem(lax.div(me, 2), 2)
    over_y = me + 4 - 8 * lax.rem(lax.div(me, 4), 2)
    corner = over_x + 4 - 8 * lax.rem(lax.div(over_x, 4), 2)
    return (me, side, over_x, over_y, corner)


def to_dp(source, target, send_sem, recv_sem, index):
    return pltpu.make_async_remote_copy(
        src_ref=source,
        dst_ref=target,
        send_sem=send_sem,
        recv_sem=recv_sem,
        device_id={"dp": index},
        device_id_type=MESH,
    )


def to_mp(source, target, send_sem, recv_sem, index):
    return pltpu.make_async_remote_copy(
        src_ref=source,
        dst_ref=target,
        send_sem=send_sem,
        recv_sem=recv_sem,
        device_id={"mp": index},
        device_id_type=MESH,
    )


def owner_at(turn):
    me, side, over_x, over_y, _ = plane()
    block = turn // 2
    near = ((block + 1) // 2) % 2
    far = block // 3
    second = turn % 2
    other = (1 - near) * second + (block // 2) * near
    owner = me + (near * (1 - second) + far) * (over_x - me)
    return owner + (near * second + far) * (over_y - me) + other * (side - me)


ARRIVALS = (
    (1, (4,)),
    (2, (0, 1, 2)),
    (3, (3,)),
    (4, (6, 9)),
    (5, (8, 10)),
    (6, (5, 7)),
    (7, (11, 12)),
)


class Gather:
    AFTER = {0: (5, 6), 1: (7, 8), 2: (9,), 3: (10,), 5: (11,), 7: (12,)}

    def __init__(self, own, out, send, recv, local=None):
        me, side, over_x, over_y, corner = plane()
        half = out.shape[1] // 2
        low, high = pl.ds(0, half), pl.ds(half, half)
        self.keep = None if own is None else pltpu.make_async_copy(own, out.at[me], local)
        own = out.at[me] if own is None else own

        def hop(number, source, target, index):
            return to_dp(source, target, send.at[number], recv.at[number], index)

        def onward(number, owner, part, index):
            place = out.at[owner, part]
            return hop(number, place, place, index)

        self.copies = [
            hop(0, own.at[low], out.at[me, low], over_x),
            hop(1, own.at[high], out.at[me, high], over_y),
            hop(2, own.at[high], out.at[me, high], over_x),
            hop(3, own.at[low], out.at[me, low], over_y),
            hop(4, own, out.at[me], side),
            onward(5, over_x, low, over_y),
            onward(6, over_x, low, side),
            onward(7, over_y, high, over_x),
            onward(8, over_y, high, side),
            onward(9, over_x, high, side),
            onward(10, over_y, low, side),
            onward(11, corner, low, side),
            onward(12, corner, high, side),
        ]

    def start(self):
        for number in range(5):
            self.copies[number].start()
        if self.keep is not None:
            self.keep.start()

    def arrive(self, *numbers):
        for number in numbers:
            self.copies[number].wait_recv()
            for later in self.AFTER.get(number, ()):
                self.copies[later].start()

    def pass_on(self):
        self.arrive(0, 1, 2, 3)

    def sent(self):
        for copy in self.copies:
            copy.wait_send()
        if self.keep is not None:
            self.keep.wait()

    def finish(self):
        self.arrive(5, 7, 4, 6, 8, 9, 10, 11, 12)
        self.sent()


def greet_all():
    barrier = pltpu.get_barrier_semaphore()
    me, z = lax.axis_index("dp"), lax.axis_index("mp")
    for step in range(1, 8):
        pl.semaphore_signal(
            barrier, inc=1, device_id={"dp": lax.rem(me + step, 8)}, device_id_type=MESH
        )
    core = lax.rem(me, 2)
    for step in range(1, 4):
        for other in (me, me + 1 - 2 * core):
            pl.semaphore_signal(
                barrier,
                inc=1,
                device_id={"dp": other, "mp": lax.rem(z + step, 4)},
                device_id_type=MESH,
            )
    return barrier


def start_all(copies):
    for copy in copies:
        copy.start()
    return copies


def wait_all(copies):
    for copy in copies:
        copy.wait()


def swap_all(source, target, send, recv):
    me = lax.axis_index("dp")
    return [
        to_dp(source, target.at[me], send.at[step - 1], recv.at[step - 1], lax.rem(me + step, 8))
        for step in range(1, 8)
    ]


class Spread:
    def __init__(self, share, w_qkv, w_out, send, recv, local):
        me, z = lax.axis_index("dp"), lax.axis_index("mp")
        core = lax.rem(me, 2)
        self.place = z + core * (3 - 2 * z)
        self.send, self.recv, self.local = send, recv, local
        self.shares = [share.at[0], share.at[1], share.at[2], share.at[3]]
        self.slots = (core, 1 - core)
        self.core = core
        self.w_qkv, self.w_out = w_qkv, w_out

    def target(self, which, piece):
        slot = self.slots[which]
        block = slot if piece == 3 else 2 * piece + slot
        rows = pl.ds(pl.multiple_of(block * LANES, LANES), HEAD_DIM)
        return (self.w_out if piece == 3 else self.w_qkv).at[rows]

    def hop(self, which, piece, number, place, own):
        source = self.shares[piece] if own else self.target(which, piece)
        z = place + self.core * (3 - 2 * place)
        return to_mp(
            source,
            self.target(which, piece),
            self.send.at[number * 4 + piece],
            self.recv.at[which * 4 + piece],
            z,
        )

    def keep(self, which, piece):
        return pltpu.make_async_copy(
            self.shares[piece], self.target(which, piece), self.local.at[piece]
        )

    def start(self, pieces):
        @pl.when(self.place == 0)
        def _():
            for piece in pieces:
                self.hop(0, piece, 0, 1, True).start()
                self.keep(0, piece).start()

        @pl.when(self.place == 1)
        def _():
            for piece in pieces:
                self.hop(1, piece, 0, 0, True).start()
                self.hop(1, piece, 1, 2, True).start()
                self.keep(1, piece).start()

    def pass_on(self, pieces):
        @pl.when(self.place == 1)
        def _():
            for piece in pieces:
                self.hop(0, piece, 2, 2, False).wait_recv()
                self.hop(0, piece, 2, 2, False).start()

        @pl.when(self.place == 2)
        def _():
            for which in (1, 0):
                for piece in pieces:
                    self.hop(which, piece, which, 3, False).wait_recv()
                    self.hop(which, piece, which, 3, False).start()

    def finish(self, pieces):
        @pl.when(self.place == 0)
        def _():
            for piece in pieces:
                self.hop(1, piece, 0, 1, False).wait_recv()
                self.hop(0, piece, 0, 1, True).wait_send()
                self.keep(0, piece).wait()

        @pl.when(self.place == 1)
        def _():
            for piece in pieces:
                self.hop(1, piece, 0, 0, True).wait_send()
                self.hop(1, piece, 1, 2, True).wait_send()
                self.hop(0, piece, 2, 2, False).wait_send()
                self.keep(1, piece).wait()

        @pl.when(self.place == 2)
        def _():
            for piece in pieces:
                for which in (1, 0):
                    self.hop(which, piece, which, 3, False).wait_send()

        @pl.when(self.place == 3)
        def _():
            for piece in pieces:
                for which in (1, 0):
                    self.hop(which, piece, which, 3, False).wait_recv()


class Column:
    def __init__(self, own, out, send, recv, local):
        z = lax.axis_index("mp")
        self.z, self.own, self.out, self.send, self.recv = z, own, out, send, recv
        self.outer = (z == 0) | (z == 3)
        near = 1 + lax.div(z, 3)
        self.from_outer = (near, 3 - near)
        self.edge = 3 * (z - 1)
        self.from_inner = (3 - z, 3 - self.edge, self.edge)
        self.keep = pltpu.make_async_copy(own, out.at[z], local)

    def straight(self, number, target):
        return to_mp(
            self.own, self.out.at[self.z], self.send.at[number], self.recv.at[self.z], target
        )

    def onward(self):
        far = 3 - self.edge
        return to_mp(
            self.out.at[far], self.out.at[far], self.send.at[3], self.recv.at[far], self.edge
        )

    def came(self, source):
        return to_mp(
            self.own, self.out.at[source], self.send.at[0], self.recv.at[source], source
        ).wait_recv

    def start(self):
        self.keep.start()

        @pl.when(self.outer)
        def _():
            for number, target in enumerate(self.from_outer):
                self.straight(number, target).start()

        @pl.when(jnp.logical_not(self.outer))
        def _():
            for number, target in enumerate(self.from_inner):
                self.straight(number, target).start()

    def pass_on(self):
        @pl.when(jnp.logical_not(self.outer))
        def _():
            self.came(3 - self.edge)()
            self.onward().start()

    def finish(self):
        @pl.when(self.outer)
        def _():
            for source in (1, 2):
                self.came(source)()
            self.came(3 - self.z)()
            for number, target in enumerate(self.from_outer):
                self.straight(number, target).wait_send()

        @pl.when(jnp.logical_not(self.outer))
        def _():
            self.came(3 - self.z)()
            self.came(self.edge)()
            for number, target in enumerate(self.from_inner):
                self.straight(number, target).wait_send()
            self.onward().wait_send()

        self.keep.wait()


def anywhere():
    return pl.BlockSpec(memory_space=pl.ANY)


def on_chip():
    return pl.BlockSpec(memory_space=pltpu.VMEM)


def remote_params(number, limit=VMEM_LIMIT):
    return pltpu.CompilerParams(
        collective_id=number, has_side_effects=True, vmem_limit_bytes=limit
    )


def hot_of(notes, k, size):
    own = notes[:, 0:48, :].reshape(size, LANES)
    lane = lax.broadcasted_iota(jnp.int32, (size, LANES), 1)
    slot = jnp.sum(jnp.where(lane == k, own, 0.0), axis=1, keepdims=True)
    return (lax.broadcasted_iota(jnp.int32, (size, size), 1).astype(F32) == slot).astype(BF16)


def block_mask(notes, k, block, z, rows):
    position = rows * z + block * 128 + lax.broadcasted_iota(jnp.int32, (128, 1), 0)
    position = position.astype(F32)
    first_end = notes[k, 52:53, 0:1]
    second_end = first_end + notes[k, 52:53, 1:2]
    begin = jnp.where(position >= first_end, first_end, 0.0)
    begin = jnp.where(position >= second_end, second_end, begin)
    column = lax.broadcasted_iota(jnp.int32, (128, 192), 1)
    distance = 64 + lax.broadcasted_iota(jnp.int32, (128, 192), 0) - column
    key_position = (rows * z + block * 128 - 64 + column).astype(F32)
    live = jnp.concatenate(
        [notes[k, 48 + block : 49 + block, :], notes[k, 49 + block : 50 + block, 0:64]], axis=1
    )
    allowed = (distance >= 0) & (distance < WINDOW) & (key_position >= begin)
    return allowed & ((live == 1.0) | (distance == 0))


NT = (((1,), (1,)), ((), ()))
TN = (((0,), (0,)), ((), ()))


def forward_kernel(
    tokens, cotangent, order_row, gain, notes, query, keys, values, project, gate,
    hidden_out, w_qkv_out, w_out, notes_all, gate_all, mixed_out, kept_out, tokens_out, cotangent_out,
    cotangent_all,
    hidden_all, qkv, share, gate_own, w_qkv, mixed, kept, tokens_b, cotangent_b,
    send, recv, send_a, recv_a, send_g, recv_g, send_w, recv_w, send_n, recv_n, send_c, recv_c,
    local, out_sem, store_sem, *, scale,
):
    groups, rows, width = hidden_all.shape
    me, z = lax.axis_index("dp"), lax.axis_index("mp")
    members = lax.axis_size("mp")
    barrier = greet_all()
    head = pl.ds(pl.multiple_of(lax.div(me, 2) * HEAD_DIM, 16), HEAD_DIM)
    units = pl.ds(pl.multiple_of(me * LANES, LANES), LANES)
    loads = [
        pltpu.make_async_copy(source.at[head], share.at[piece], local.at[piece])
        for piece, source in enumerate((query, keys, values, project))
    ]
    loads.append(pltpu.make_async_copy(gate.at[:, units], gate_own, local.at[4]))
    for copy in loads:
        copy.start()
    none = jnp.zeros((LANES - HEAD_DIM, width), BF16)
    for block in range(6):
        w_qkv[block * LANES + HEAD_DIM : block * LANES + LANES, :] = none
    for block in range(2):
        w_out[block * LANES + HEAD_DIM : block * LANES + LANES, :] = none

    place = lax.broadcasted_iota(jnp.int32, (rows, rows), 0).astype(F32)
    sort = (place == order_row[...]).astype(BF16)
    tokens_b[...] = jnp.dot(sort, tokens[...], preferred_element_type=F32).astype(BF16)

    def normalise(span):
        value = tokens_b[span, :].astype(F32)
        inverse = lax.rsqrt(mean_rows(value * value) + EPSILON)
        hidden_all[me, span, :] = (value * inverse * gain[...]).astype(BF16)

    each_chunk(rows, normalise)
    notes_all[me] = notes[...]
    stores = start_all([pltpu.make_async_copy(tokens_b, tokens_out, store_sem.at[0])])
    pl.semaphore_wait(barrier, 13)
    gather = Gather(None, hidden_all, send_a, recv_a)
    gather.start()
    swaps = swap_all(notes, notes_all, send_n, recv_n)
    for copy in swaps:
        copy.start()
    for copy in loads[:4]:
        copy.wait()
    spread = Spread(share, w_qkv, w_out, send_w, recv_w, local)
    spread.start((0, 1, 2))
    cotangent_b[...] = jnp.dot(sort, cotangent[...], preferred_element_type=F32).astype(BF16)
    stores += start_all([pltpu.make_async_copy(cotangent_b, cotangent_out, store_sem.at[1])])
    wait_all(loads[4:])
    column = Column(gate_own, gate_all, send_c, recv_c, local.at[4])
    second = Gather(cotangent_b, cotangent_all, send_g, recv_g, local.at[5])
    spread.pass_on((0, 1, 2))
    gather.arrive(0, 1)
    second.start()
    column.start()
    gather.arrive(2, 3)
    spread.finish((0, 1, 2))
    spread.start((3,))
    stores += start_all([pltpu.make_async_copy(w_qkv, w_qkv_out, store_sem.at[2])])
    for copy in swaps:
        copy.wait()

    def keep(turn):
        owner = owner_at(turn)
        return pltpu.make_async_copy(hidden_all.at[owner], hidden_out.at[owner], out_sem.at[turn])

    def multiply(turn, carry):
        for number, numbers in ARRIVALS:
            left = tuple(n for n in numbers if n > 3)
            if left:
                pl.when(turn == number)(functools.partial(gather.arrive, *left))
        owner = owner_at(turn)
        keep(turn).start()
        product = lax.dot_general(
            hidden_all[owner], w_qkv[...], NT, preferred_element_type=F32
        ).astype(BF16)
        qkv[owner] = product.reshape(groups, rows // groups, 768)
        return carry

    lax.fori_loop(0, groups, multiply, 0)

    def halo(k, other):
        return to_mp(
            kept.at[k, pl.ds(rows, 64), pl.ds(256, 512)],
            kept.at[k, pl.ds(0, 64), pl.ds(256, 512)],
            send.at[k],
            recv.at[k],
            other,
        )

    def store_kept(k):
        return pltpu.make_async_copy(kept.at[k], kept_out.at[k], store_sem.at[3 + k])

    def store_mixed(k):
        span = pl.ds(k, 1)
        return pltpu.make_async_copy(
            mixed.at[:, span], mixed_out.at[:, span], store_sem.at[3 + groups + k]
        )

    def order(k, carry):
        hot = hot_of(notes_all, k, rows)
        given = qkv[:, pl.ds(k, 1)].reshape(rows, 768)
        kept[k, pl.ds(64, rows), :] = lax.dot_general(
            hot, given, TN, preferred_element_type=F32
        ).astype(BF16)
        kept[k, pl.ds(0, 64), pl.ds(0, 256)] = jnp.zeros((64, 256), BF16)

        @pl.when(z < members - 1)
        def _():
            halo(k, z + 1).start()

        @pl.when(z == 0)
        def _():
            kept[k, pl.ds(0, 64), pl.ds(256, 512)] = jnp.zeros((64, 512), BF16)

        return carry

    lax.fori_loop(0, groups, order, 0)

    def attend(k, carry):
        @pl.when(z > 0)
        def _():
            halo(k, z).wait_recv()

        store_kept(k).start()
        hot = hot_of(notes_all, k, rows)
        pairs = [(block, head) for block in range(rows // 128) for head in range(2)]
        masks = [block_mask(notes_all, k, block, z, rows) for block in range(rows // 128)]
        scores = []
        for block, head in pairs:
            query = kept[k, pl.ds(64 + block * 128, 128), pl.ds(head * 128, 128)]
            keys = kept[k, pl.ds(block * 128, 192), pl.ds(256 + head * 128, 128)]
            value = lax.dot_general(query, keys, NT, preferred_element_type=F32) * scale
            scores.append(jnp.where(masks[block], value, -MASKED))
        chances = []
        for value in scores:
            weights = jnp.exp(value - jnp.max(value, axis=-1, keepdims=True))
            total = jnp.sum(weights, axis=-1, keepdims=True)
            chances.append((weights / total).astype(BF16))
        parts = []
        for (block, head), chance in zip(pairs, chances):
            values = kept[k, pl.ds(block * 128, 192), pl.ds(512 + head * 128, 128)]
            parts.append(jnp.dot(chance, values, preferred_element_type=F32).astype(BF16))
        found = [
            jnp.concatenate(parts[2 * block : 2 * block + 2], axis=1)
            for block in range(rows // 128)
        ]
        ordered = jnp.concatenate(found, axis=0)
        back = jnp.dot(hot, ordered, preferred_element_type=F32).astype(BF16)
        mixed[:, pl.ds(k, 1)] = back.reshape(groups, 1, rows // groups, 256)
        store_mixed(k).start()
        return carry

    spread.pass_on((3,))
    lax.fori_loop(0, groups // 2, attend, 0)
    second.pass_on()
    column.pass_on()
    lax.fori_loop(groups // 2, groups, attend, 0)
    spread.finish((3,))
    second.finish()
    column.finish()
    gather.sent()

    wait_all(stores)

    def stored(turn, carry):
        keep(turn).wait()
        store_kept(turn).wait()
        store_mixed(turn).wait()
        return carry

    lax.fori_loop(0, groups, stored, 0)

    @pl.when(z < members - 1)
    def _():
        def done(k, carry):
            halo(k, z + 1).wait_send()
            return carry

        lax.fori_loop(0, groups, done, 0)


def attend_ahead(
    tokens, cotangent, order_row, gain, notes, query, keys, values, project, gate, scale
):
    rows, width = tokens.shape
    groups, members = lax.axis_size("dp"), lax.axis_size("mp")
    dma = pltpu.SemaphoreType.DMA
    shape = jax.ShapeDtypeStruct
    return pl.pallas_call(
        functools.partial(forward_kernel, scale=scale),
        out_shape=(
            shape((groups, rows, width), BF16),
            shape((6 * LANES, width), BF16),
            shape((2 * LANES, width), BF16),
            shape((groups,) + notes.shape, F32),
            shape((members, width, LANES), BF16),
            shape((groups, groups, rows // groups, 256), BF16),
            shape((groups, rows + 64, 768), BF16),
            shape((rows, width), BF16),
            shape((rows, width), BF16),
            shape((groups, rows, width), BF16),
        ),
        in_specs=[on_chip()] * 5 + [anywhere()] * 5,
        out_specs=(
            anywhere(), anywhere(), on_chip(), on_chip(), anywhere(),
            anywhere(), anywhere(), anywhere(), anywhere(), anywhere(),
        ),
        scratch_shapes=[
            pltpu.VMEM((groups, rows, width), BF16),
            pltpu.VMEM((groups, groups, rows // groups, 768), BF16),
            pltpu.VMEM((4, HEAD_DIM, width), BF16),
            pltpu.VMEM((width, LANES), BF16),
            pltpu.VMEM((6 * LANES, width), BF16),
            pltpu.VMEM((groups, groups, rows // groups, 256), BF16),
            pltpu.VMEM((groups, rows + 64, 768), BF16),
            pltpu.VMEM((rows, width), BF16),
            pltpu.VMEM((rows, width), BF16),
            dma((groups,)),
            dma((groups,)),
            dma((13,)),
            dma((13,)),
            dma((13,)),
            dma((13,)),
            dma((12,)),
            dma((8,)),
            dma((7,)),
            dma((7,)),
            dma((4,)),
            dma((4,)),
            dma((6,)),
            dma((groups,)),
            dma((3 + 2 * groups,)),
        ],
        compiler_params=remote_params(2, 60 * 1024 * 1024),
        cost_estimate=pl.CostEstimate(flops=0, bytes_accessed=300_000_000, transcendentals=0),
        name="attend_ahead",
    )(tokens, cotangent, order_row, gain, notes, query, keys, values, project, gate)


CHUNK = 32


def each_chunk(rows, body, chunk=CHUNK):
    def step(i, carry):
        body(pl.ds(pl.multiple_of(i * chunk, chunk), chunk))
        return carry

    lax.fori_loop(0, rows // chunk, step, 0)


class Units:
    def __init__(self, part, came_in, stage, send, recv, local):
        self.z = lax.axis_index("mp")
        self.part_of = part
        self.inputs = (came_in,)
        self.stages = (stage,)
        self.send, self.recv, self.local = send, recv, local
        z = self.z
        self.outer = (z == 0) | (z == 3)
        self.far = 3 - z
        self.near = 1 + lax.div(z, 3)
        self.second = 3 - self.near
        self.edge = 3 * (z - 1)

    def part(self, kind, z):
        return self.part_of(z)

    def straight(self, kind, number, target):
        return to_mp(
            self.part(kind, target),
            self.inputs[kind].at[self.z],
            self.send.at[number * 2 + kind],
            self.recv.at[self.z * 2 + kind],
            target,
        )

    def staged(self, kind):
        return to_mp(
            self.part(kind, self.far),
            self.stages[kind].at[0],
            self.send.at[4 + kind],
            self.recv.at[8 + kind],
            self.near,
        )

    def summed(self, kind):
        return to_mp(
            self.stages[kind].at[1],
            self.inputs[kind].at[self.z],
            self.send.at[4 + kind],
            self.recv.at[self.z * 2 + kind],
            3 - self.edge,
        )

    def mine(self, kind):
        return pltpu.make_async_copy(
            self.part(kind, 3 - self.edge), self.stages[kind].at[1], self.local.at[kind]
        )

    def start(self):
        @pl.when(self.outer)
        def _():
            for kind in range(1):
                self.staged(kind).start()
            for kind in range(1):
                self.straight(kind, 0, self.near).start()
                self.straight(kind, 1, self.second).start()

        @pl.when(jnp.logical_not(self.outer))
        def _():
            for kind in range(1):
                self.mine(kind).start()
                self.straight(kind, 0, 3 - self.z).start()
                self.straight(kind, 1, self.edge).start()

    def add(self):
        @pl.when(jnp.logical_not(self.outer))
        def _():
            for kind in range(1):
                stage = self.stages[kind]
                self.mine(kind).wait()
                to_mp(
                    self.part(kind, 0),
                    stage.at[0],
                    self.send.at[4 + kind],
                    self.recv.at[8 + kind],
                    self.edge,
                ).wait_recv()

                def body(span):
                    stage[1, span, :] = (
                        stage[0, span, :].astype(F32) + stage[1, span, :].astype(F32)
                    ).astype(BF16)

                each_chunk(stage.shape[1], body)
                self.summed(kind).start()

    def arrived(self, kind, source):
        to_mp(
            self.part(kind, 0),
            self.inputs[kind].at[source],
            self.send.at[kind],
            self.recv.at[source * 2 + kind],
            source,
        ).wait_recv()

    def finish(self):
        @pl.when(self.outer)
        def _():
            for kind in range(1):
                self.arrived(kind, 1)
                self.arrived(kind, 2)
                self.straight(kind, 0, self.near).wait_send()
                self.straight(kind, 1, self.second).wait_send()
                self.staged(kind).wait_send()

        @pl.when(jnp.logical_not(self.outer))
        def _():
            for kind in range(1):
                self.arrived(kind, 0)
                self.arrived(kind, 3)
                self.arrived(kind, 3 - self.z)
                self.straight(kind, 0, 3 - self.z).wait_send()
                self.straight(kind, 1, self.edge).wait_send()
                self.summed(kind).wait_send()


class Reduce:
    COUNT = 10

    def __init__(self, left, right, across, part, from_side, from_corner, from_near, send, recv):
        self.left, self.right, self.across, self.part = left, right, across, part
        self.from_side, self.from_corner, self.from_near = from_side, from_corner, from_near
        self.send, self.recv = send, recv
        self.rows = part.shape[1]

    def product(self, owner, slot):
        rows, width = self.rows, self.part.shape[2]
        picked = pl.ds(pl.multiple_of(owner * rows, rows), rows)

        def tile(t, carry):
            columns = pl.ds(pl.multiple_of(t * 256, 256), 256)
            if callable(self.left):
                value = jnp.dot(
                    self.left(owner), self.right[:, columns], preferred_element_type=F32
                )
            elif self.across:
                value = lax.dot_general(
                    self.left[picked, :], self.right[columns, :], NT, preferred_element_type=F32
                )
            else:
                value = jnp.dot(
                    self.left[picked, :], self.right[:, columns], preferred_element_type=F32
                )
            self.part[slot, :, columns] = value.astype(BF16)
            return carry

        lax.fori_loop(0, width // 256, tile, 0)

    def prepare(self):
        _, side, over_x, over_y, corner = plane()
        part, near = self.part, self.from_near
        half = self.rows // 2
        low, high = pl.ds(0, half), pl.ds(half, half)

        def hop(number, source, target, index):
            return to_dp(source, target, self.send.at[number], self.recv.at[number], index)

        self.shares = [hop(i, part.at[4 + i], self.from_side.at[i], side) for i in range(4)]
        self.corners = [
            hop(4, part.at[0, low], self.from_corner.at[0], over_x),
            hop(5, part.at[0, high], self.from_corner.at[1], over_y),
        ]
        self.nears = [
            hop(6, part.at[1, low], near.at[0, low], over_x),
            hop(7, part.at[1, high], near.at[0, high], over_x),
            hop(8, part.at[2, high], near.at[1, high], over_y),
            hop(9, part.at[2, low], near.at[1, low], over_y),
        ]

    def add_side(self, slot):
        self.shares[slot].wait_recv()

        def body(span):
            self.part[slot, span, :] = (
                self.part[slot, span, :].astype(F32) + self.from_side[slot, span, :].astype(F32)
            ).astype(BF16)

        each_chunk(self.rows, body)

    def add_corner(self, slot, offset, which):
        self.corners[which].wait_recv()

        def body(span):
            target = pl.ds(pl.multiple_of(offset + span.start, CHUNK), CHUNK)
            self.part[slot, target, :] = (
                self.part[slot, target, :].astype(F32)
                + self.from_corner[which, span, :].astype(F32)
            ).astype(BF16)

        each_chunk(self.rows // 2, body)

    def products(self):
        self.prepare()
        me, _, over_x, over_y, corner = plane()
        turn = 1 - 2 * lax.rem(me, 2)
        for slot, owner in enumerate((corner, over_x, over_y, me)):
            self.product(owner + turn, 4 + slot)
            self.shares[slot].start()
        for slot, owner in enumerate((corner, over_x, over_y, me)):
            self.product(owner, slot)

    def launch(self):
        self.add_side(0)
        self.corners[0].start()
        self.corners[1].start()
        self.add_side(1)
        self.nears[0].start()
        self.add_side(2)
        self.nears[2].start()

    def begin(self):
        self.prepare()
        me, _, over_x, over_y, corner = plane()
        turn = 1 - 2 * lax.rem(me, 2)
        self.product(corner + turn, 4)
        self.shares[0].start()
        self.product(corner, 0)
        self.product(over_x + turn, 5)
        self.shares[1].start()
        self.add_side(0)
        self.corners[0].start()
        self.corners[1].start()
        self.product(over_x, 1)
        self.product(over_y + turn, 6)
        self.shares[2].start()
        self.add_side(1)
        self.nears[0].start()
        self.product(over_y, 2)
        self.product(me + turn, 7)
        self.shares[3].start()
        self.add_side(2)
        self.nears[2].start()
        self.product(me, 3)

    def middle(self):
        self.add_corner(2, 0, 0)
        self.nears[3].start()
        self.add_corner(1, self.rows // 2, 1)
        self.nears[1].start()

    def end(self):
        self.shares[3].wait_recv()
        for copy in self.nears:
            copy.wait_recv()

    def run(self):
        self.begin()
        self.middle()
        self.end()

    def rows_of(self, span):
        return (
            self.part[3, span, :].astype(F32)
            + self.from_side[3, span, :].astype(F32)
            + self.from_near[0, span, :].astype(F32)
            + self.from_near[1, span, :].astype(F32)
        )

    def finish(self):
        for copy in self.shares + self.corners + self.nears:
            copy.wait_send()


def reduce_scratch(rows, width):
    dma = pltpu.SemaphoreType.DMA
    return [
        pltpu.VMEM((8, rows, width), BF16),
        pltpu.VMEM((4, rows, width), BF16),
        pltpu.VMEM((2, rows // 2, width), BF16),
        pltpu.VMEM((2, rows, width), BF16),
        dma((10,)),
        dma((10,)),
    ]


def gather_scratch(rows, width):
    dma = pltpu.SemaphoreType.DMA
    return [pltpu.VMEM((rows, width), BF16), dma((13,)), dma((13,)), dma(())]


def mean_rows(values):
    return jnp.mean(values, axis=-1, keepdims=True)


class Heads:
    def __init__(self, source, stage, arrive, send, recv_stage, recv):
        me, z = lax.axis_index("dp"), lax.axis_index("mp")
        self.me, self.z = me, z
        self.core = lax.rem(me, 2)
        self.source, self.stage, self.arrive = source, stage, arrive
        self.send, self.recv_stage, self.recv = send, recv_stage, recv
        self.place = z + self.core * (3 - 2 * z)
        self.columns = source.shape[1] // 2

    def z_of(self, place):
        return place + self.core * (3 - 2 * place)

    def slot_of(self, place):
        return self.core if place == 0 else 1 - self.core

    def rows_of(self, place, kind):
        block = 2 * kind + self.slot_of(place)
        return self.source.at[pl.ds(pl.multiple_of(block * LANES, LANES), HEAD_DIM)]

    def half_of(self, ref, half):
        return ref.at[:, pl.ds(pl.multiple_of(half * self.columns, LANES), self.columns)]

    def to_stage(self, place, kind):
        return to_at(
            self.rows_of(place, kind),
            self.stage.at[place, kind],
            self.send.at[place * 4 + kind],
            self.recv_stage.at[place * 4 + kind],
            self.me,
            self.z_of(2),
        )

    def to_owner(self, place, kind, half, way, ref, number):
        return to_at(
            self.half_of(ref, half),
            self.arrive.at[way, kind],
            self.send.at[number],
            self.recv.at[way * 4 + kind],
            self.me - self.core + half,
            self.z_of(place),
        )

    def sums(self, kind):
        return [
            self.to_owner(
                place, kind, half, 2, self.stage.at[place, kind], place * 8 + kind * 2 + half
            )
            for place in (0, 1)
            for half in (0, 1)
        ]

    def cross(self, own, kind):
        other = 1 - own
        copies = [
            self.to_owner(other, kind, half, 0, self.rows_of(other, kind), kind * 2 + half)
            for half in (0, 1)
        ]
        copies.append(
            to_at(
                self.half_of(self.rows_of(own, kind), 1 - self.core),
                self.arrive.at[1, kind],
                self.send.at[8 + kind],
                self.recv.at[4 + kind],
                self.me + 1 - 2 * self.core,
                self.z,
            )
        )
        return copies

    def start(self, kinds):
        @pl.when(self.place == 3)
        def _():
            for kind in kinds:
                self.to_stage(0, kind).start()
                self.to_stage(1, kind).start()

        for own in (0, 1):
            @pl.when(self.place == own)
            def _():
                for kind in kinds:
                    for copy in self.cross(own, kind):
                        copy.start()

    def add(self, kinds):
        @pl.when(self.place == 2)
        def _():
            for kind in kinds:
                for place in (0, 1):
                    self.to_stage(place, kind).wait_recv()
                    mine = self.rows_of(place, kind)

                    def body(span):
                        self.stage[place, kind, span, :] = (
                            self.stage[place, kind, span, :].astype(F32)
                            + mine[span, :].astype(F32)
                        ).astype(BF16)

                    each_chunk(HEAD_DIM, body, 16)
                for copy in self.sums(kind):
                    copy.start()

    def total(self, out):
        owner = lax.div(self.z, 2) == self.core
        for kind in range(4):
            for own in (0, 1):
                @pl.when(self.place == own)
                def _():
                    self.arrive[1, kind] = self.half_of(self.rows_of(own, kind), self.core)[...]

            for way in range(3):
                waiting = to_at(
                    self.half_of(self.rows_of(0, kind), 0),
                    self.arrive.at[way, kind],
                    self.send.at[0],
                    self.recv.at[way * 4 + kind],
                    self.me,
                    lax.rem(self.z + 1, 4),
                )
                if way == 1:
                    pl.when(jnp.logical_not(owner))(waiting.wait_recv)
                else:
                    waiting.wait_recv()

            def body(span):
                found = self.arrive[0, kind, span, :].astype(F32)
                found = found + self.arrive[1, kind, span, :].astype(F32)
                found = found + self.arrive[2, kind, span, :].astype(F32)
                target = pl.ds(pl.multiple_of(kind * HEAD_DIM + span.start, 16), 16)
                out[target, :] = found.astype(BF16)

            each_chunk(HEAD_DIM, body, 16)

    def finish_send(self):
        for kind in range(4):
            @pl.when(self.place == 3)
            def _():
                self.to_stage(0, kind).wait_send()
                self.to_stage(1, kind).wait_send()

            @pl.when(self.place == 2)
            def _():
                for copy in self.sums(kind):
                    copy.wait_send()

            for own in (0, 1):
                @pl.when(self.place == own)
                def _():
                    for copy in self.cross(own, kind):
                        copy.wait_send()


def to_at(source, target, send_sem, recv_sem, dp, mp):
    return pltpu.make_async_remote_copy(
        src_ref=source,
        dst_ref=target,
        send_sem=send_sem,
        recv_sem=recv_sem,
        device_id={"dp": dp, "mp": mp},
        device_id_type=MESH,
    )


def backward_kernel(
    branch, notes_all, kept_in, w_out_in, activated_in, w_down_in, middle_in, both_sum, down_sum,
    out, result, branch_all, both_in, down_all,
    totals, query_part, key_value, ending, leaving, arriving, send, recv,
    part, from_side, from_corner, from_near, send_r, recv_r,
    mixed_grad, shard, load_sem, send_g, recv_g,
    both_stage, send_u, recv_u, local, down_found, send_d, recv_d,
    kept, w_out, activated, w_down, middle, fetch_sem, down_stage, send_v, recv_v, local_v,
    *, scale, groups, rows,
):
    z = lax.axis_index("mp")
    members = lax.axis_size("mp")
    barrier = greet_all()
    pairs = ((activated_in, activated), (w_out_in, w_out), (kept_in, kept), (middle_in, middle))
    pairs += ((w_down_in, w_down),)
    fetches = [
        pltpu.make_async_copy(source, target, fetch_sem.at[number])
        for number, (source, target) in enumerate(pairs)
    ]

    def down_rows(owner):
        return down_sum.at[pl.ds(pl.multiple_of(owner * LANES, LANES), LANES)]

    down_units = Units(down_rows, down_found, down_stage, send_v, recv_v, local_v)
    load_down = pltpu.make_async_copy(down_rows(z), down_found.at[z], load_sem.at[2])
    pl.semaphore_wait(barrier, 13)
    units = Units(lambda owner: both_sum.at[owner], both_in, both_stage, send_u, recv_u, local)
    gather = Gather(branch, branch_all, send_g, recv_g, local.at[2])
    gather.start()
    down_units.start()
    units.start()
    start_all(fetches)
    load_down.start()
    wait_all((fetches[0], fetches[4]))
    reduce = Reduce(activated, w_down, False, part, from_side, from_corner, from_near, send_r, recv_r)
    reduce.products()
    down_units.add()
    down = Gather(down_found.at[0], down_all, send_d, recv_d, local.at[1])

    def load_shard(turn):
        slot = turn % 2
        return pltpu.make_async_copy(branch_all.at[owner_at(turn)], shard.at[slot], load_sem.at[slot])

    def spread_back(turn, carry):
        for number, numbers in ARRIVALS:
            pl.when(turn == number)(functools.partial(gather.arrive, *numbers))

        @pl.when(turn == 0)
        def _():
            gather.keep.wait()

        load_shard(turn).start()
        load_shard(turn).wait()
        mixed_grad[owner_at(turn)] = (
            lax.dot_general(shard[turn % 2], w_out[...], NT, preferred_element_type=F32)
            .astype(BF16)
            .reshape(groups, rows // groups, 256)
        )
        return carry

    fetches[1].wait()
    lax.fori_loop(0, 4, spread_back, 0)
    reduce.launch()
    lax.fori_loop(4, 8, spread_back, 0)
    units.add()


    def halo(k, other):
        return to_mp(leaving.at[k], arriving.at[k], send.at[k], recv.at[k], other)

    def attend(k, carry):
        hot = hot_of(notes_all, k, rows)
        given = mixed_grad[:, pl.ds(k, 1)].reshape(rows, 256)
        grad_ordered = lax.dot_general(hot, given, TN, preferred_element_type=F32).astype(BF16)
        totals[...] = jnp.zeros_like(totals)
        pairs = [(block, head) for block in range(rows // 128) for head in range(2)]
        masks = [block_mask(notes_all, k, block, z, rows) for block in range(rows // 128)]

        def query_of(block, head):
            return kept[k, pl.ds(64 + block * 128, 128), pl.ds(head * 128, 128)]

        def keys_of(block, head):
            return kept[k, pl.ds(block * 128, 192), pl.ds(256 + head * 128, 128)]

        def grad_of(block, head):
            return grad_ordered[block * 128 : block * 128 + 128, head * 128 : head * 128 + 128]

        scores, chance_grads = [], []
        for block, head in pairs:
            value = lax.dot_general(
                query_of(block, head), keys_of(block, head), NT, preferred_element_type=F32
            )
            scores.append(jnp.where(masks[block], value * scale, -MASKED))
            values = kept[k, pl.ds(block * 128, 192), pl.ds(512 + head * 128, 128)]
            chance_grads.append(
                lax.dot_general(grad_of(block, head), values, NT, preferred_element_type=F32)
            )
        agains, score_grads = [], []
        for value, chance_grad in zip(scores, chance_grads):
            weights = jnp.exp(value - jnp.max(value, axis=-1, keepdims=True))
            again = weights / jnp.sum(weights, axis=-1, keepdims=True)
            row_dot = jnp.sum(again * chance_grad, axis=-1, keepdims=True)
            agains.append(again.astype(BF16))
            score_grads.append((again * (chance_grad - row_dot)).astype(BF16))
        for (block, head), again, score_grad in zip(pairs, agains, score_grads):
            query_part[k, pl.ds(block * 128, 128), pl.ds(head * 128, 128)] = (
                jnp.dot(score_grad, keys_of(block, head), preferred_element_type=F32) * scale
            ).astype(BF16)
            totals[pl.ds(block * 128, 192), pl.ds(head * 128, 128)] += (
                lax.dot_general(score_grad, query_of(block, head), TN, preferred_element_type=F32)
                * scale
            )
            totals[pl.ds(block * 128, 192), pl.ds(256 + head * 128, 128)] += lax.dot_general(
                again, grad_of(block, head), TN, preferred_element_type=F32
            )
        key_value[k] = totals[pl.ds(64, rows), :].astype(BF16)
        ending[k] = totals[pl.ds(rows, 64), :]

        @pl.when(z > 0)
        def _():
            leaving[k] = totals[pl.ds(0, 64), :].astype(BF16)
            halo(k, z - 1).start()

        return carry

    wait_all(fetches[2:4])
    lax.fori_loop(0, 3, attend, 0)
    reduce.middle()
    load_down.wait()
    down_units.finish()

    @pl.when((z == 0) | (z == members - 1))
    def _():
        down_found[members - 1 - z] = jnp.zeros_like(down_found[0])

    def add_down(span):
        value = down_found[0, span, :].astype(F32) + down_found[1, span, :].astype(F32)
        value = value + down_found[2, span, :].astype(F32) + down_found[3, span, :].astype(F32)
        down_found[0, span, :] = value.astype(BF16)

    each_chunk(down_found.shape[1], add_down)
    down.start()
    lax.fori_loop(3, 7, attend, 0)
    down.pass_on()
    lax.fori_loop(7, groups, attend, 0)

    def restore(k, carry):
        @pl.when(z < members - 1)
        def _():
            halo(k, z).wait_recv()
            key_value[k, pl.ds(rows - 64, 64), :] = (
                ending[k] + arriving[k].astype(F32)
            ).astype(BF16)

        hot = hot_of(notes_all, k, rows)
        ordered = jnp.concatenate([query_part[k], key_value[k]], axis=1)
        back = jnp.dot(hot, ordered, preferred_element_type=F32).astype(BF16)
        out[:, pl.ds(k, 1)] = back.reshape(groups, 1, rows // groups, 768)
        return carry

    lax.fori_loop(0, groups, restore, 0)
    reduce.end()

    def body(span):
        result[span, :] = (middle[span, :] + reduce.rows_of(span)).astype(BF16)

    each_chunk(rows, body)
    down.finish()
    units.finish()
    for copy in gather.copies:
        copy.wait_send()
    reduce.finish()

    @pl.when(z > 0)
    def _():
        def done(k, carry):
            halo(k, z - 1).wait_send()
            return carry

        lax.fori_loop(0, groups, done, 0)


def attend_back(
    branch, notes_all, kept, w_out, activated, w_down, middle, both_sum, down_sum, scale
):
    groups = kept.shape[0]
    rows, width = middle.shape
    members = both_sum.shape[0]
    dma = pltpu.SemaphoreType.DMA
    shape = jax.ShapeDtypeStruct
    return pl.pallas_call(
        functools.partial(backward_kernel, scale=scale, groups=groups, rows=rows),
        out_shape=(
            shape((groups, groups, rows // groups, 768), BF16),
            shape((rows, width), BF16),
            shape((groups, rows, width), BF16),
            shape((members, width, 256), BF16),
            shape((groups, LANES, width), BF16),
        ),
        in_specs=[on_chip()] * 2 + [anywhere()] * 7,
        out_specs=(on_chip(),) * 2 + (anywhere(),) * 3,
        scratch_shapes=[
            pltpu.VMEM((rows + 64, 512), F32),
            pltpu.VMEM((groups, rows, 256), BF16),
            pltpu.VMEM((groups, rows, 512), BF16),
            pltpu.VMEM((groups, 64, 512), F32),
            pltpu.VMEM((groups, 64, 512), BF16),
            pltpu.VMEM((groups, 64, 512), BF16),
            dma((groups,)),
            dma((groups,)),
        ]
        + reduce_scratch(rows, width)
        + [
            pltpu.VMEM((groups, groups, rows // groups, 256), BF16),
            pltpu.VMEM((2, rows, width), BF16),
            dma((3,)),
            dma((13,)),
            dma((13,)),
            pltpu.VMEM((2, width, 256), BF16),
            dma((6,)),
            dma((10,)),
            dma((3,)),
            pltpu.VMEM((members, LANES, width), BF16),
            dma((13,)),
            dma((13,)),
            pltpu.VMEM(kept.shape, BF16),
            pltpu.VMEM(w_out.shape, BF16),
            pltpu.VMEM(activated.shape, BF16),
            pltpu.VMEM((members * LANES, width), BF16),
            pltpu.VMEM((rows, width), F32),
            dma((5,)),
            pltpu.VMEM((2, LANES, width), BF16),
            dma((6,)),
            dma((10,)),
            dma((1,)),
        ],
        compiler_params=remote_params(3, 63 * 1024 * 1024),
        cost_estimate=pl.CostEstimate(flops=0, bytes_accessed=300_000_000, transcendentals=0),
        name="attend_back",
    )(branch, notes_all, kept, w_out, activated, w_down, middle, both_sum, down_sum)


def norm_back_rows(gradient, values, gain, sums, span):
    inverse = lax.rsqrt(mean_rows(values * values) + EPSILON)
    normed = values * inverse
    product = gradient * normed
    folded = product[0:8]
    for step in range(1, CHUNK // 8):
        folded = folded + product[step * 8 : step * 8 + 8]
    sums[...] += folded
    scaled = gradient * gain
    return inverse * (scaled - normed * mean_rows(scaled * normed))


def feed_kernel(
    mixed, w_out, tokens, cotangent_all, gate_all, w_up, down_weight, cotangent_own, gain,
    middle, middle_grad, branch, sums, activated_out, both_sum, down_out, up_all, down_all,
    hidden_all, both_grad, part, from_side, from_corner, from_near, send_r, recv_r,
    send_m, recv_m, send_a, recv_a, cot_shard, cot_tile, stage_both, down_sum, w_both, w_down,
    cotangent, activated, load_sem, local,
    up_own, down_own, send_u, recv_u, send_d, recv_d, first_sem,
):
    groups, rows, width = hidden_all.shape
    members = gate_all.shape[0]
    me = lax.axis_index("dp")
    barrier = greet_all()
    units_own = pl.ds(pl.multiple_of(me * LANES, LANES), LANES)
    first = start_all(
        [
            pltpu.make_async_copy(source, target, first_sem.at[number])
            for number, (source, target) in enumerate(
                (
                    (mixed, activated.at[:, :, pl.ds(0, 256)]),
                    (w_out, down_sum.at[pl.ds(0, 256)]),
                    (w_up.at[:, units_own], up_own),
                    (down_weight.at[units_own], down_own),
                    (tokens, cotangent),
                )
            )
        ]
    )
    gates = start_all(
        [
            pltpu.make_async_copy(
                gate_all.at[z], w_both.at[:, pl.ds(z * 256, 128)], load_sem.at[6 + z]
            )
            for z in range(members)
        ]
    )

    def slot_of(turn):
        block = turn // 2
        near = ((block + 1) // 2) % 2
        far = block // 3
        second = turn % 2
        other = (1 - near) * second + (block // 2) * near
        return 4 * other + 3 * (1 - near) * (1 - far) + near * (1 + second)

    def load_cotangent(turn):
        return pltpu.make_async_copy(
            cotangent_all.at[owner_at(turn)], cot_shard.at[turn % 2], load_sem.at[turn % 2]
        )

    load_cotangent(0).start()
    wait_all(first)
    pl.semaphore_wait(barrier, 13)
    columns_up = Column(up_own, up_all, send_u, recv_u, local.at[0])
    columns_down = Column(down_own, down_all, send_d, recv_d, local.at[2])
    columns_up.start()
    columns_down.start()
    project = Reduce(
        lambda owner: activated[owner, :, 0:256], down_sum.at[pl.ds(0, 256)], False,
        part, from_side, from_corner, from_near, send_m, recv_m,
    )
    project.begin()
    project.middle()
    columns_up.pass_on()
    columns_down.pass_on()
    project.end()

    def normalise(span):
        values = cotangent[span, :].astype(F32) + project.rows_of(span)
        middle_grad[span, :] = values
        inverse = lax.rsqrt(mean_rows(values * values) + EPSILON)
        hidden_all[me, span, :] = (values * inverse * gain[...]).astype(BF16)

    each_chunk(rows, normalise)
    project.finish()
    gather = Gather(None, hidden_all, send_a, recv_a)
    gather.start()
    store_middle = pltpu.make_async_copy(middle_grad, middle, local.at[1])
    load_own = pltpu.make_async_copy(cotangent_own, cotangent, local.at[3])
    store_middle.start()
    load_own.start()
    columns_up.finish()
    columns_down.finish()
    ups = start_all(
        [
            pltpu.make_async_copy(
                up_all.at[z], w_both.at[:, pl.ds(z * 256 + 128, 128)], load_sem.at[10 + z]
            )
            for z in range(members)
        ]
    )
    ups += start_all(
        [
            pltpu.make_async_copy(
                down_all.at[z], w_down.at[pl.ds(z * LANES, LANES)], load_sem.at[14 + z]
            )
            for z in range(members)
        ]
    )
    reduce = Reduce(None, None, False, part, from_side, from_corner, from_near, send_r, recv_r)
    reduce.prepare()

    def nears():
        reduce.add_side(1)
        reduce.nears[0].start()
        reduce.add_side(2)
        reduce.nears[2].start()

    early = [(turn, functools.partial(gather.arrive, *numbers)) for turn, numbers in ARRIVALS]
    early += [(6, nears)]
    late = [(1, 3), (4, 1), (5, 2), (7, 0)]
    wait_all(gates + ups)

    def unit(turn, carry):
        for number, action in early:
            pl.when(turn == number)(action)

        @pl.when(turn < 7)
        def _():
            load_cotangent(turn + 1).start()

        load_cotangent(turn).wait()
        owner, slot = owner_at(turn), slot_of(turn)
        mine = hidden_all[owner]
        grads = cot_shard[turn % 2]
        for z in range(members):
            raw = jnp.dot(mine, w_both[:, z * 256 : z * 256 + 256], preferred_element_type=F32)
            units = pl.ds(z * 128, 128)
            if z % 2 == 0:
                pair = lax.dot_general(
                    grads, w_down[pl.ds(z * 128, 256), :], NT, preferred_element_type=F32
                )
            active_grad = pair[:, 128 * (z % 2) : 128 * (z % 2) + 128]
            gate, upward = raw[:, :128], raw[:, 128:]
            sigmoid = jax.nn.sigmoid(gate)
            activated[owner, :, units] = (gate * sigmoid * upward).astype(BF16)
            both_grad[owner, :, pl.ds(z * 256, 128)] = (
                active_grad * upward * sigmoid * (1.0 + gate * (1.0 - sigmoid))
            ).astype(BF16)
            both_grad[owner, :, pl.ds(z * 256 + 128, 128)] = (
                active_grad * gate * sigmoid
            ).astype(BF16)

        def tile(t, inner):
            columns = pl.ds(pl.multiple_of(t * 256, 256), 256)
            part[slot, :, columns] = lax.dot_general(
                both_grad[owner], w_both[columns, :], NT, preferred_element_type=F32
            ).astype(BF16)
            return inner

        lax.fori_loop(0, width // 256, tile, 0)
        for number, share in late:
            pl.when(turn == number)(reduce.shares[share].start)
        return carry

    lax.fori_loop(0, 8, unit, 0)
    store_activated = pltpu.make_async_copy(activated, activated_out, local.at[4])
    store_activated.start()

    def load_tile(t):
        columns = pl.ds(pl.multiple_of(t * 256, 256), 256)
        return pltpu.make_async_copy(
            cotangent_all.at[:, :, columns], cot_tile.at[t % 2], load_sem.at[2 + t % 2]
        )

    def store_both(t):
        columns = pl.ds(pl.multiple_of(t * 256, 256), 256)
        return pltpu.make_async_copy(
            stage_both.at[t % 2], both_sum.at[:, columns], load_sem.at[4 + t % 2]
        )

    tiles = width // 256
    count = groups * rows

    def down_tile(t, carry):
        columns = pl.ds(pl.multiple_of(t * 256, 256), 256)

        @pl.when(t < tiles - 1)
        def _():
            load_tile(t + 1).start()

        load_tile(t).wait()
        down_sum[:, columns] = lax.dot_general(
            activated[...].reshape(count, members * 128),
            cot_tile[t % 2].reshape(count, 256),
            TN,
            preferred_element_type=F32,
        ).astype(BF16)
        return carry

    store_down = pltpu.make_async_copy(down_sum, down_out, local.at[5])

    def weight_tile(t, carry):
        columns = pl.ds(pl.multiple_of(t * 256, 256), 256)

        @pl.when(t >= 2)
        def _():
            store_both(t - 2).wait()

        value = lax.dot_general(
            hidden_all[:, :, columns].reshape(count, 256),
            both_grad[...].reshape(count, members * 256),
            TN,
            preferred_element_type=F32,
        )
        for z in range(members):
            stage_both[t % 2, z] = value[:, z * 256 : z * 256 + 256].astype(BF16)
        store_both(t).start()
        return carry

    load_tile(0).start()
    reduce.add_side(0)
    reduce.corners[0].start()
    reduce.corners[1].start()
    lax.fori_loop(0, tiles, down_tile, 0)
    store_down.start()
    lax.fori_loop(0, 2, weight_tile, 0)
    reduce.middle()
    lax.fori_loop(2, tiles, weight_tile, 0)
    reduce.end()
    store_middle.wait()
    load_own.wait()
    sums[...] = jnp.zeros_like(sums)

    def body(span):
        change = norm_back_rows(reduce.rows_of(span), middle_grad[span, :], gain[...], sums, span)
        total = cotangent[span, :].astype(F32) + change
        middle_grad[span, :] = total
        branch[span, :] = total.astype(BF16)

    each_chunk(rows, body)
    gather.sent()
    reduce.finish()
    for t in (tiles - 2, tiles - 1):
        store_both(t).wait()
    store_down.wait()
    store_activated.wait()


def feed(mixed, w_out, tokens, cotangent_all, gate_all, w_up, w_down, cotangent, gain):
    groups, rows, width = cotangent_all.shape
    members = gate_all.shape[0]
    dma = pltpu.SemaphoreType.DMA
    units = members * 128
    return pl.pallas_call(
        feed_kernel,
        out_shape=(
            jax.ShapeDtypeStruct((rows, width), F32),
            jax.ShapeDtypeStruct((rows, width), F32),
            jax.ShapeDtypeStruct((rows, width), BF16),
            jax.ShapeDtypeStruct((8, width), F32),
            jax.ShapeDtypeStruct((groups, rows, units), BF16),
            jax.ShapeDtypeStruct((members, width, 256), BF16),
            jax.ShapeDtypeStruct((units, width), BF16),
            jax.ShapeDtypeStruct((members, width, LANES), BF16),
            jax.ShapeDtypeStruct((members, LANES, width), BF16),
        ),
        in_specs=[anywhere()] * 8 + [on_chip()],
        out_specs=(anywhere(),) + (on_chip(),) * 3 + (anywhere(),) * 5,
        scratch_shapes=[
            pltpu.VMEM((groups, rows, width), BF16),
            pltpu.VMEM((groups, rows, 2 * units), BF16),
        ]
        + reduce_scratch(rows, width)
        + [
            dma((10,)),
            dma((10,)),
            dma((13,)),
            dma((13,)),
            pltpu.VMEM((2, rows, width), BF16),
            pltpu.VMEM((2, groups, rows, 256), BF16),
            pltpu.VMEM((2, members, 256, 256), BF16),
            pltpu.VMEM((units, width), BF16),
            pltpu.VMEM((width, 2 * units), BF16),
            pltpu.VMEM((units, width), BF16),
            pltpu.VMEM((rows, width), BF16),
            pltpu.VMEM((groups, rows, units), BF16),
            dma((6 + 4 * members,)),
            dma((6,)),
            pltpu.VMEM((width, LANES), BF16),
            pltpu.VMEM((LANES, width), BF16),
            dma((4,)),
            dma((4,)),
            dma((4,)),
            dma((4,)),
            dma((5,)),
        ],
        compiler_params=remote_params(5, 63 * 1024 * 1024),
        cost_estimate=pl.CostEstimate(flops=0, bytes_accessed=400_000_000, transcendentals=0),
        name="feed",
    )(mixed, w_out, tokens, cotangent_all, gate_all, w_up, w_down, cotangent, gain)


def input_kernel(
    qkv_in, w_in, hidden_all, branch_all, mixed_in, tokens_in, middle_in, gain, sums_two,
    both_sum, both_in,
    result, gains, both_all, heads_all,
    part, from_side, from_corner, from_near, send, recv, sums,
    stage, arrive, send_h, recv_s, recv_h, own, plane_sums, column_sums, send_p, recv_p,
    weight_sum, row_tile, tile_sem, send_b, recv_b, send_t, recv_t, both_found, heads_own, local,
    mixed, tokens, middle_grad, fetch_sem, qkv_grad, w_qkv,
):
    me, z = lax.axis_index("dp"), lax.axis_index("mp")
    barrier = greet_all()
    count = qkv_grad.shape[0]
    tiles = tokens.shape[1] // 256
    outer = (z == 0) | (z == 3)

    def columns_of(t):
        return pl.ds(pl.multiple_of(lax.rem(t, tiles) * 256, 256), 256)

    def load(t, source):
        return pltpu.make_async_copy(
            source.at[:, :, columns_of(t)], row_tile.at[t % 2], tile_sem.at[t % 2]
        )

    own_part = pltpu.make_async_copy(both_sum.at[z], both_found.at[0], local.at[0])
    own_part.start()
    ways = [(outer, 1, 1), (outer, 2, 2)]
    ways += [(z == 1, 0, 1), (z == 1, 2, 2), (z == 1, 3, 3)]
    ways += [(z == 2, 0, 1), (z == 2, 1, 2), (z == 2, 3, 3)]

    def came(source, place):
        return pltpu.make_async_copy(both_in.at[source], both_found.at[place], local.at[place])

    for here, source, place in ways:
        pl.when(here)(came(source, place).start)

    @pl.when(outer)
    def _():
        both_found[3] = jnp.zeros_like(both_found[3])

    load(0, hidden_all).start()
    fetches = start_all(
        [
            pltpu.make_async_copy(source, target, fetch_sem.at[number])
            for number, (source, target) in enumerate(
                (
                    (qkv_in, qkv_grad),
                    (w_in, w_qkv),
                    (mixed_in, mixed),
                    (tokens_in, tokens),
                    (middle_in, middle_grad),
                )
            )
        ]
    )
    pl.semaphore_wait(barrier, 13)
    both = Gather(both_found.at[0], both_all, send_b, recv_b, local.at[4])

    def weight_tile(t, carry):
        @pl.when(t < tiles - 1)
        def _():
            load(t + 1, hidden_all).start()

        @pl.when((t >= tiles - 1) & (t < 2 * tiles - 1))
        def _():
            load(t + 1, branch_all).start()

        load(t, hidden_all).wait()

        @pl.when(t < tiles)
        def _():
            weight_sum[pl.ds(0, 768), columns_of(t)] = lax.dot_general(
                qkv_grad[...], row_tile[t % 2].reshape(count, 256), TN, preferred_element_type=F32
            ).astype(BF16)

        @pl.when(t >= tiles)
        def _():
            weight_sum[pl.ds(768, 256), columns_of(t)] = lax.dot_general(
                mixed[...], row_tile[t % 2].reshape(count, 256), TN, preferred_element_type=F32
            ).astype(BF16)

        return carry

    heads = Heads(weight_sum, stage, arrive, send_h, recv_s, recv_h)
    reduce = Reduce(qkv_grad, w_qkv, False, part, from_side, from_corner, from_near, send, recv)
    own_part.wait()
    for here, source, place in ways:
        pl.when(here)(came(source, place).wait)

    def add(span):
        value = both_found[0, span, :].astype(F32) + both_found[1, span, :].astype(F32)
        value = value + both_found[2, span, :].astype(F32) + both_found[3, span, :].astype(F32)
        both_found[0, span, :] = value.astype(BF16)

    each_chunk(both_found.shape[1], add)
    both.start()
    wait_all(fetches[:2])
    lax.fori_loop(0, tiles, weight_tile, 0)
    heads.start((0, 1, 2))
    wait_all(fetches[2:])
    lax.fori_loop(tiles, 2 * tiles, weight_tile, 0)
    heads.start((3,))
    both.pass_on()
    reduce.begin()
    heads.add((0, 1))
    reduce.middle()
    heads.add((2, 3))
    reduce.end()
    sums[...] = jnp.zeros_like(sums)

    def body(span):
        values = tokens[span, :].astype(F32)
        change = norm_back_rows(reduce.rows_of(span), values, gain[...], sums, span)
        result[span, :] = (middle_grad[span, :] + change).astype(BF16)

    each_chunk(result.shape[0], body)
    own[...] = jnp.concatenate(
        [
            jnp.sum(sums[...], axis=0, keepdims=True),
            jnp.sum(sums_two[...], axis=0, keepdims=True),
        ],
        axis=0,
    )
    swaps = swap_all(own, plane_sums, send_p, recv_p)
    for copy in swaps:
        copy.start()
    plane_sums[me] = own[...]
    heads.total(heads_own)
    gather = Gather(heads_own, heads_all, send_t, recv_t, local.at[5])
    gather.start()
    for copy in swaps:
        copy.wait()
    found = plane_sums[0]
    for other in range(1, 8):
        found = found + plane_sums[other]
    column_sums[z] = found
    passes = [
        to_mp(
            column_sums.at[z],
            column_sums.at[z],
            send_p.at[6 + step],
            recv_p.at[6 + step],
            lax.rem(z + step, 4),
        )
        for step in range(1, 4)
    ]
    for copy in passes:
        copy.start()
    both.finish()
    for copy in passes:
        copy.wait()
    gains[...] = (column_sums[0] + column_sums[1]) + (column_sums[2] + column_sums[3])
    gather.pass_on()
    heads.finish_send()
    reduce.finish()
    gather.finish()


def project_input(
    qkv_grad, w_qkv, hidden_all, branch_all, mixed, tokens, middle_grad, gain, sums_two,
    both_sum, both_in,
):
    rows, width = tokens.shape
    groups = hidden_all.shape[0]
    dma = pltpu.SemaphoreType.DMA
    shape = jax.ShapeDtypeStruct
    return pl.pallas_call(
        input_kernel,
        out_shape=(
            shape((rows, width), BF16),
            shape((2, width), F32),
            shape((groups, width, 256), BF16),
            shape((groups, 4 * HEAD_DIM, width // 2), BF16),
        ),
        in_specs=[anywhere()] * 7 + [on_chip()] * 2 + [anywhere()] * 2,
        out_specs=(on_chip(),) * 2 + (anywhere(),) * 2,
        scratch_shapes=reduce_scratch(rows, width)
        + [
            pltpu.VMEM((8, width), F32),
            pltpu.VMEM((2, 4, HEAD_DIM, width), BF16),
            pltpu.VMEM((3, 4, HEAD_DIM, width // 2), BF16),
            dma((16,)),
            dma((8,)),
            dma((12,)),
            pltpu.VMEM((2, width), F32),
            pltpu.VMEM((8, 2, width), F32),
            pltpu.VMEM((4, 2, width), F32),
            dma((10,)),
            dma((10,)),
            pltpu.VMEM((8 * LANES, width), BF16),
            pltpu.VMEM((2, groups, rows, 256), BF16),
            dma((2,)),
            dma((13,)),
            dma((13,)),
            dma((13,)),
            dma((13,)),
            pltpu.VMEM((4, width, 256), BF16),
            pltpu.VMEM((4 * HEAD_DIM, width // 2), BF16),
            dma((6,)),
            pltpu.VMEM(mixed.shape, BF16),
            pltpu.VMEM((rows, width), BF16),
            pltpu.VMEM((rows, width), F32),
            dma((5,)),
            pltpu.VMEM(qkv_grad.shape, BF16),
            pltpu.VMEM(w_qkv.shape, BF16),
        ],
        compiler_params=remote_params(6, 63 * 1024 * 1024),
        cost_estimate=pl.CostEstimate(flops=0, bytes_accessed=250_000_000, transcendentals=0),
        name="project_input",
    )(
        qkv_grad, w_qkv, hidden_all, branch_all, mixed, tokens, middle_grad, gain, sums_two,
        both_sum, both_in,
    )


def assemble_kernel(
    both, down, heads, order_column, output_b, input_b,
    output, inputs, query, keys, values, project, gate, upward, down_out,
):
    for d in range(both.shape[0]):
        gate[:, d * 128 : d * 128 + 128] = both[d, :, :128].astype(F32)
        upward[:, d * 128 : d * 128 + 128] = both[d, :, 128:].astype(F32)
    down_out[...] = down[0].astype(F32)
    for kind, out in enumerate((query, keys, values, project)):
        out[...] = heads[0, kind].astype(F32)
    place = lax.broadcasted_iota(jnp.int32, (order_column.shape[0], output_b.shape[0]), 1)
    unsort = (place.astype(F32) == order_column[...]).astype(BF16)
    output[...] = jnp.dot(unsort, output_b[...], preferred_element_type=F32).astype(BF16)
    inputs[...] = jnp.dot(unsort, input_b[...], preferred_element_type=F32).astype(BF16)


def assemble(both, down, heads, order_column, output_b, input_b):
    groups, width, wide = both.shape
    rows = output_b.shape[0]
    units = down.shape[1]
    chips = groups // 2
    columns = heads.shape[3]
    row_tile, tile = rows // groups, width // groups
    shape = jax.ShapeDtypeStruct
    head = shape((chips * HEAD_DIM, 2 * columns), F32)
    head_spec = pl.BlockSpec((HEAD_DIM, columns), lambda i: (i // 2, i % 2))
    wide_spec = pl.BlockSpec((tile, groups * units), lambda i: (i, 0))
    row_spec = pl.BlockSpec((row_tile, width), lambda i: (i, 0))
    whole_spec = pl.BlockSpec((rows, width), lambda i: (0, 0))
    return pl.pallas_call(
        assemble_kernel,
        grid=(groups,),
        out_shape=(
            shape((rows, width), BF16),
            shape((rows, width), BF16),
            head,
            head,
            head,
            head,
            shape((width, groups * units), F32),
            shape((width, groups * units), F32),
            shape((groups * units, width), F32),
        ),
        in_specs=[
            pl.BlockSpec((groups, tile, wide), lambda i: (0, i, 0)),
            pl.BlockSpec((1, units, width), lambda i: (i, 0, 0)),
            pl.BlockSpec((1, 4, HEAD_DIM, columns), lambda i: (i, 0, 0, 0)),
            pl.BlockSpec((row_tile, 1), lambda i: (i, 0)),
            whole_spec,
            whole_spec,
        ],
        out_specs=(
            row_spec, row_spec, head_spec, head_spec, head_spec, head_spec, wide_spec, wide_spec,
            pl.BlockSpec((units, width), lambda i: (i, 0)),
        ),
        compiler_params=pltpu.CompilerParams(vmem_limit_bytes=VMEM_LIMIT),
        cost_estimate=pl.CostEstimate(flops=0, bytes_accessed=58_000_000, transcendentals=0),
        name="assemble",
    )(both, down, heads, order_column, output_b, input_b)


def swapped(
    tokens, cotangent, route, lengths, key_mask, norm1_gain, norm2_gain,
    w_query, w_key, w_value, w_out, w_gate, w_up, w_down,
):
    groups = lax.axis_size("dp")
    members = lax.axis_size("mp")
    me = lax.axis_index("dp")
    z = lax.axis_index("mp")
    rows, width = tokens.shape
    bucket = rows // groups
    units = w_down.shape[0] // groups

    target = route // TOK_DEV
    earlier = jnp.arange(rows, dtype=jnp.int32)
    same = (target[:, None] == target[None, :]) & (earlier[None, :] < earlier[:, None])
    send_at = target * bucket + jnp.sum(same.astype(jnp.int32), axis=1)
    sorting = send_at[None, :] == earlier[:, None]
    slots_own = jnp.sum(jnp.where(sorting, (route % rows)[None, :], 0), axis=1)

    mask_window = lax.dynamic_slice_in_dim(
        jnp.concatenate([jnp.zeros((WINDOW,), jnp.int32), key_mask]), z * rows, rows + WINDOW
    )
    slot_rows = jnp.pad(slots_own.reshape(groups, bucket).T, ((0, 0), (0, LANES - groups)))
    mask_rows = jnp.pad(mask_window, (0, 4 * LANES - rows - WINDOW)).reshape(4, LANES)
    length_rows = jnp.pad(lengths, ((0, 3), (0, LANES - lengths.shape[1])))
    notes = jnp.concatenate([slot_rows, mask_rows, length_rows], axis=0).astype(F32)

    count = groups * rows
    scale = HEAD_DIM ** (-0.5)
    (
        hidden_one,
        w_qkv,
        w_proj,
        notes_all,
        gate_all,
        mixed,
        kept,
        tokens_b,
        cotangent_b,
        cotangent_all,
    ) = attend_ahead(
        tokens,
        cotangent,
        send_at.astype(F32)[None],
        norm1_gain[None],
        notes,
        w_query.T,
        w_key.T,
        w_value.T,
        w_out,
        w_gate,
        scale,
    )
    mixed = mixed.reshape(count, 2 * LANES)
    middle, middle_grad, branch, sums_two, activated, both_sum, down_sum, _, down_all = feed(
        mixed.reshape(groups, rows, 2 * LANES),
        w_proj,
        tokens_b,
        cotangent_all,
        gate_all,
        w_up,
        w_down,
        cotangent_b,
        norm2_gain[None],
    )
    qkv_grad, output_rows, branch_all, both_in, down_whole = attend_back(
        branch,
        notes_all,
        kept,
        w_proj,
        activated.reshape(count, units * members),
        down_all.reshape(members * units, width),
        middle,
        both_sum,
        down_sum,
        scale,
    )
    qkv_grad = qkv_grad.reshape(count, 6 * LANES)
    input_rows, gain_sums, both_whole, heads_whole = project_input(
        qkv_grad,
        w_qkv,
        hidden_one,
        branch_all,
        mixed,
        tokens_b,
        middle_grad,
        norm1_gain[None],
        sums_two,
        both_sum,
        both_in,
    )
    (
        output,
        input_grad,
        query_grad,
        key_grad,
        value_grad,
        proj_grad,
        gate_grad,
        up_grad,
        down_grad,
    ) = assemble(
        both_whole,
        down_whole,
        heads_whole.reshape(groups, 4, HEAD_DIM, width // 2),
        send_at.astype(F32)[:, None],
        output_rows,
        input_rows,
    )
    return (
        output,
        input_grad,
        gain_sums[0],
        gain_sums[1],
        query_grad.T,
        key_grad.T,
        value_grad.T,
        proj_grad,
        gate_grad,
        up_grad,
        down_grad,
    )


def solution(mesh):
    in_specs = (
        P(("dp", "mp"), None),
        P(("dp", "mp"), None),
        P(("dp", "mp")),
        P("dp", None),
        P("dp"),
        P(),
        P(),
        P(None, "mp"),
        P(None, "mp"),
        P(None, "mp"),
        P("mp", None),
        P(None, "mp"),
        P(None, "mp"),
        P("mp", None),
    )
    out_specs = (
        P(("dp", "mp"), None),
        P(("dp", "mp"), None),
        P(),
        P(),
        P(None, "mp"),
        P(None, "mp"),
        P(None, "mp"),
        P("mp", None),
        P(None, "mp"),
        P(None, "mp"),
        P("mp", None),
    )
    body = swapped if (mesh.shape["dp"], mesh.shape["mp"]) == (8, 4) else local
    return jax.shard_map(body, mesh=mesh, in_specs=in_specs, out_specs=out_specs, check_vma=False)
```

```python
import functools

import jax
import jax.numpy as jnp
from jax import lax
from jax.experimental import pallas as pl
from jax.experimental.pallas import tpu as pltpu
from jax.sharding import PartitionSpec as P

HEAD_DIM = 112
WINDOW = 64
TOK_DEV = 1536


EPSILON = 1e-05
MASKED = 1e30


def norm_rows(values):
    inverse = lax.rsqrt(jnp.mean(values * values, axis=-1, keepdims=True) + EPSILON)
    return (values * inverse, inverse)


def norm_back(gradient, normed, inverse, norm_gain):
    scaled = gradient * norm_gain
    result = inverse * (scaled - normed * jnp.mean(scaled * normed, axis=-1, keepdims=True))
    return (result, jnp.sum(gradient * normed, axis=0))


def padded(values, filler):
    front = jnp.full((WINDOW,) + values.shape[1:], filler, values.dtype)
    return jnp.concatenate([front, values], axis=0)


def block_scores(query_block, key_block, query_seg, key_seg, key_flag, first_row, score_scale):
    query_pos = first_row + jnp.arange(query_block.shape[0], dtype=jnp.int32)
    key_pos = first_row - WINDOW + jnp.arange(key_block.shape[0], dtype=jnp.int32)
    distance = query_pos[:, None] - key_pos[None, :]
    allowed = (distance >= 0) & (distance < WINDOW) & (query_seg[:, None] == key_seg[None, :])
    allowed = allowed & ((key_flag[None, :] == 1) | (distance == 0))
    raw_scores = (
        jnp.einsum("qhd,khd->hqk", query_block, key_block, preferred_element_type=jnp.float32)
        * score_scale
    )
    return jnp.where(allowed[None], raw_scores, -MASKED)


def block_inputs(query, key_pad, value_pad, segment, seg_pad, live_pad, first_row, block_rows):
    key_span = block_rows + WINDOW
    return (
        lax.dynamic_slice_in_dim(query, first_row, block_rows, 0),
        lax.dynamic_slice_in_dim(key_pad, first_row, key_span, 0),
        lax.dynamic_slice_in_dim(value_pad, first_row, key_span, 0),
        lax.dynamic_slice_in_dim(segment, first_row, block_rows, 0),
        lax.dynamic_slice_in_dim(seg_pad, first_row, key_span, 0),
        lax.dynamic_slice_in_dim(live_pad, first_row, key_span, 0),
    )


def attend_forward(query, key_all, value_all, segment, key_live):
    token_count, head_count, head_width = query.shape
    block_rows = min(512, token_count)
    score_scale = head_width ** (-0.5)
    key_pad = padded(key_all, 0.0)
    value_pad = padded(value_all, 0.0)
    seg_pad = padded(segment, -1)
    live_pad = padded(key_live, 0)

    def one_block(running, block_index):
        first_row = block_index * block_rows
        query_block, key_block, value_block, query_seg, key_seg, key_flag = block_inputs(
            query, key_pad, value_pad, segment, seg_pad, live_pad, first_row, block_rows
        )
        scores = block_scores(
            query_block, key_block, query_seg, key_seg, key_flag, first_row, score_scale
        )
        row_max = jnp.max(scores, axis=-1, keepdims=True)
        weights = jnp.exp(scores - row_max)
        denominator = jnp.sum(weights, axis=-1, keepdims=True)
        chances = (weights / denominator).astype(jnp.bfloat16)
        mixed = jnp.einsum("hqk,khd->qhd", chances, value_block, preferred_element_type=jnp.float32)
        return (
            running,
            (mixed.astype(jnp.bfloat16), row_max[..., 0] + jnp.log(denominator[..., 0])),
        )

    _, (mixed, logsum) = lax.scan(
        one_block, jnp.zeros((), jnp.int32), jnp.arange(token_count // block_rows, dtype=jnp.int32)
    )
    return (mixed.reshape(token_count, head_count * head_width), logsum)


def attend_backward(query, key_all, value_all, segment, key_live, logsum, mixed_grad):
    token_count, head_count, head_width = query.shape
    block_rows = min(512, token_count)
    key_span = block_rows + WINDOW
    score_scale = head_width ** (-0.5)
    key_pad = padded(key_all, 0.0)
    value_pad = padded(value_all, 0.0)
    seg_pad = padded(segment, -1)
    live_pad = padded(key_live, 0)

    def one_block(running, inputs):
        key_grad, value_grad = running
        block_index, block_logsum = inputs
        first_row = block_index * block_rows
        query_block, key_block, value_block, query_seg, key_seg, key_flag = block_inputs(
            query, key_pad, value_pad, segment, seg_pad, live_pad, first_row, block_rows
        )
        grad_block = lax.dynamic_slice_in_dim(mixed_grad, first_row, block_rows, 0)
        scores = block_scores(
            query_block, key_block, query_seg, key_seg, key_flag, first_row, score_scale
        )
        chances = jnp.exp(scores - block_logsum[..., None])
        chance_grad = jnp.einsum(
            "qhd,khd->hqk", grad_block, value_block, preferred_element_type=jnp.float32
        )
        row_dot = jnp.sum(chances * chance_grad, axis=-1, keepdims=True)
        score_grad = (chances * (chance_grad - row_dot)).astype(jnp.bfloat16)
        query_grad = (
            jnp.einsum("hqk,khd->qhd", score_grad, key_block, preferred_element_type=jnp.float32)
            * score_scale
        )
        key_part = (
            jnp.einsum("hqk,qhd->khd", score_grad, query_block, preferred_element_type=jnp.float32)
            * score_scale
        )
        value_part = jnp.einsum(
            "hqk,qhd->khd",
            chances.astype(jnp.bfloat16),
            grad_block,
            preferred_element_type=jnp.float32,
        )
        key_grad = lax.dynamic_update_slice_in_dim(
            key_grad,
            lax.dynamic_slice_in_dim(key_grad, first_row, key_span, 0) + key_part,
            first_row,
            0,
        )
        value_grad = lax.dynamic_update_slice_in_dim(
            value_grad,
            lax.dynamic_slice_in_dim(value_grad, first_row, key_span, 0) + value_part,
            first_row,
            0,
        )
        return ((key_grad, value_grad), query_grad)

    empty_grad = jnp.zeros((token_count + WINDOW, head_count, head_width), jnp.float32)
    (key_grad, value_grad), query_grad = lax.scan(
        one_block,
        (empty_grad, empty_grad),
        (jnp.arange(token_count // block_rows, dtype=jnp.int32), logsum),
    )
    flat_width = head_count * head_width
    return (
        query_grad.reshape(token_count, flat_width).astype(jnp.bfloat16),
        key_grad[WINDOW:].reshape(token_count, flat_width).astype(jnp.bfloat16),
        value_grad[WINDOW:].reshape(token_count, flat_width).astype(jnp.bfloat16),
    )


def local(
    tokens,
    cotangent,
    route,
    lengths,
    key_mask,
    norm1_gain,
    norm2_gain,
    w_query,
    w_key,
    w_value,
    w_out,
    w_gate,
    w_up,
    w_down,
):
    groups = lax.axis_size("dp")
    members = lax.axis_size("mp")
    member = lax.axis_index("mp")
    local_rows = tokens.shape[0]
    group_rows = local_rows * members
    bucket = local_rows // groups
    target = route // TOK_DEV
    chosen = (target[:, None] == jnp.arange(groups, dtype=jnp.int32)[None, :]).astype(jnp.int32)
    ranking = jnp.sum((jnp.cumsum(chosen, axis=0) - chosen) * chosen, axis=1)
    send_at = target * bucket + ranking
    arrival, arrival_grad, arrival_slot = (
        lax.all_to_all(
            jnp.zeros_like(tokens).at[send_at].set(tokens),
            "dp",
            split_axis=0,
            concat_axis=0,
            tiled=True,
        ),
        lax.all_to_all(
            jnp.zeros_like(cotangent).at[send_at].set(cotangent),
            "dp",
            split_axis=0,
            concat_axis=0,
            tiled=True,
        ),
        lax.all_to_all(
            jnp.zeros_like(route).at[send_at].set(route % local_rows),
            "dp",
            split_axis=0,
            concat_axis=0,
            tiled=True,
        ),
    )
    token_rows = jnp.zeros_like(arrival).at[arrival_slot].set(arrival)
    grad_rows = jnp.zeros_like(arrival_grad).at[arrival_slot].set(arrival_grad)
    seq_ends = jnp.cumsum(lengths[0])
    positions = jnp.arange(group_rows, dtype=jnp.int32)
    segment = jnp.sum((positions[:, None] >= seq_ends[None, :]).astype(jnp.int32), axis=1)
    input_rows = token_rows.astype(jnp.float32)
    normed_one, inverse_one = norm_rows(input_rows)
    leading_all, grad_all = (
        lax.all_gather(token_rows, "mp", axis=0, tiled=True),
        lax.all_gather(grad_rows, "mp", axis=0, tiled=True),
    )
    input_all = leading_all.astype(jnp.float32)
    normed_all, _ = norm_rows(input_all)
    hidden_one = (normed_all * norm1_gain).astype(jnp.bfloat16)
    head_count = w_query.shape[1] // HEAD_DIM
    query = jnp.dot(hidden_one, w_query, preferred_element_type=jnp.float32).astype(jnp.bfloat16)
    keys = jnp.dot(hidden_one, w_key, preferred_element_type=jnp.float32).astype(jnp.bfloat16)
    values = jnp.dot(hidden_one, w_value, preferred_element_type=jnp.float32).astype(jnp.bfloat16)
    query_heads = query.reshape(group_rows, head_count, HEAD_DIM)
    key_heads = keys.reshape(group_rows, head_count, HEAD_DIM)
    value_heads = values.reshape(group_rows, head_count, HEAD_DIM)
    mixed_flat, logsum = attend_forward(query_heads, key_heads, value_heads, segment, key_mask)
    attention_all = lax.psum(jnp.dot(mixed_flat, w_out, preferred_element_type=jnp.float32), "mp")
    middle_all = input_all + attention_all
    middle_rows = lax.dynamic_slice_in_dim(middle_all, member * local_rows, local_rows, 0)
    normed_mid, _ = norm_rows(middle_all)
    hidden_two = (normed_mid * norm2_gain).astype(jnp.bfloat16)
    normed_two, inverse_two = norm_rows(middle_rows)
    gate_value = jnp.dot(hidden_two, w_gate, preferred_element_type=jnp.float32)
    upward = jnp.dot(hidden_two, w_up, preferred_element_type=jnp.float32)
    sigmoid = jax.nn.sigmoid(gate_value)
    activated = (gate_value * sigmoid * upward).astype(jnp.bfloat16)
    out_rows = middle_rows + lax.psum_scatter(
        jnp.dot(activated, w_down, preferred_element_type=jnp.float32).astype(jnp.bfloat16),
        "mp",
        scatter_dimension=0,
        tiled=True,
    ).astype(jnp.float32)
    activated_grad = jnp.einsum("td,fd->tf", grad_all, w_down, preferred_element_type=jnp.float32)
    gate_grad = (activated_grad * upward * sigmoid * (1.0 + gate_value * (1.0 - sigmoid))).astype(
        jnp.bfloat16
    )
    upward_grad = (activated_grad * gate_value * sigmoid).astype(jnp.bfloat16)
    down_sum = jnp.einsum("tf,td->fd", activated, grad_all, preferred_element_type=jnp.float32)
    gate_sum = jnp.einsum("td,tf->df", hidden_two, gate_grad, preferred_element_type=jnp.float32)
    upward_sum = jnp.einsum(
        "td,tf->df", hidden_two, upward_grad, preferred_element_type=jnp.float32
    )
    hidden_two_grad = lax.psum_scatter(
        jnp.einsum("tf,df->td", gate_grad, w_gate, preferred_element_type=jnp.float32)
        + jnp.einsum("tf,df->td", upward_grad, w_up, preferred_element_type=jnp.float32),
        "mp",
        scatter_dimension=0,
        tiled=True,
    )
    norm_part_two, gain_two_grad = norm_back(hidden_two_grad, normed_two, inverse_two, norm2_gain)
    middle_grad = grad_rows.astype(jnp.float32) + norm_part_two
    branch_all = lax.all_gather(middle_grad.astype(jnp.bfloat16), "mp", axis=0, tiled=True)
    output_sum = jnp.einsum("tc,td->cd", mixed_flat, branch_all, preferred_element_type=jnp.float32)
    mixed_grad = jnp.einsum(
        "td,cd->tc", branch_all, w_out, preferred_element_type=jnp.float32
    ).astype(jnp.bfloat16)
    query_grad, key_grad, value_grad = attend_backward(
        query_heads,
        key_heads,
        value_heads,
        segment,
        key_mask,
        logsum,
        mixed_grad.reshape(group_rows, head_count, HEAD_DIM),
    )
    query_sum = jnp.einsum("td,tc->dc", hidden_one, query_grad, preferred_element_type=jnp.float32)
    key_sum = jnp.einsum("td,tc->dc", hidden_one, key_grad, preferred_element_type=jnp.float32)
    value_sum = jnp.einsum("td,tc->dc", hidden_one, value_grad, preferred_element_type=jnp.float32)
    hidden_one_grad = lax.psum_scatter(
        (
            jnp.einsum("tc,dc->td", query_grad, w_query, preferred_element_type=jnp.float32)
            + jnp.einsum("tc,dc->td", key_grad, w_key, preferred_element_type=jnp.float32)
            + jnp.einsum("tc,dc->td", value_grad, w_value, preferred_element_type=jnp.float32)
        ).astype(jnp.bfloat16),
        "mp",
        scatter_dimension=0,
        tiled=True,
    ).astype(jnp.float32)
    norm_part_one, gain_one_grad = norm_back(hidden_one_grad, normed_one, inverse_one, norm1_gain)
    input_grad = middle_grad + norm_part_one
    gain_one_sum, gain_two_sum = lax.psum((gain_one_grad, gain_two_grad), ("dp", "mp"))
    weight_sums = (
        lax.psum(query_sum.astype(jnp.bfloat16), "dp").astype(jnp.float32),
        lax.psum(key_sum.astype(jnp.bfloat16), "dp").astype(jnp.float32),
        lax.psum(value_sum.astype(jnp.bfloat16), "dp").astype(jnp.float32),
        lax.psum(output_sum.astype(jnp.bfloat16), "dp").astype(jnp.float32),
        lax.psum(gate_sum.astype(jnp.bfloat16), "dp").astype(jnp.float32),
        lax.psum(upward_sum.astype(jnp.bfloat16), "dp").astype(jnp.float32),
        lax.psum(down_sum.astype(jnp.bfloat16), "dp").astype(jnp.float32),
    )
    back_out, back_grad = (
        lax.all_to_all(
            out_rows.astype(jnp.bfloat16)[arrival_slot],
            "dp",
            split_axis=0,
            concat_axis=0,
            tiled=True,
        ),
        lax.all_to_all(
            input_grad.astype(jnp.bfloat16)[arrival_slot],
            "dp",
            split_axis=0,
            concat_axis=0,
            tiled=True,
        ),
    )
    return (
        back_out[send_at],
        back_grad[send_at],
        gain_one_sum,
        gain_two_sum,
        weight_sums[0],
        weight_sums[1],
        weight_sums[2],
        weight_sums[3],
        weight_sums[4],
        weight_sums[5],
        weight_sums[6],
    )


MESH = pl.DeviceIdType.MESH
LANES = 128
F32 = jnp.float32
BF16 = jnp.bfloat16
VMEM_LIMIT = 56 * 1024 * 1024


def plane():
    me = lax.axis_index("dp")
    side = me + 1 - 2 * lax.rem(me, 2)
    over_x = me + 2 - 4 * lax.rem(lax.div(me, 2), 2)
    over_y = me + 4 - 8 * lax.rem(lax.div(me, 4), 2)
    corner = over_x + 4 - 8 * lax.rem(lax.div(over_x, 4), 2)
    return (me, side, over_x, over_y, corner)


def to_dp(source, target, send_sem, recv_sem, index):
    return pltpu.make_async_remote_copy(
        src_ref=source,
        dst_ref=target,
        send_sem=send_sem,
        recv_sem=recv_sem,
        device_id={"dp": index},
        device_id_type=MESH,
    )


def to_mp(source, target, send_sem, recv_sem, index):
    return pltpu.make_async_remote_copy(
        src_ref=source,
        dst_ref=target,
        send_sem=send_sem,
        recv_sem=recv_sem,
        device_id={"mp": index},
        device_id_type=MESH,
    )


def owner_at(turn):
    me, side, over_x, over_y, _ = plane()
    block = turn // 2
    near = ((block + 1) // 2) % 2
    far = block // 3
    second = turn % 2
    other = (1 - near) * second + (block // 2) * near
    owner = me + (near * (1 - second) + far) * (over_x - me)
    return owner + (near * second + far) * (over_y - me) + other * (side - me)


ARRIVALS = (
    (1, (4,)),
    (2, (0, 1, 2)),
    (3, (3,)),
    (4, (6, 9)),
    (5, (8, 10)),
    (6, (5, 7)),
    (7, (11, 12)),
)


class Gather:
    AFTER = {0: (5, 6), 1: (7, 8), 2: (9,), 3: (10,), 5: (11,), 7: (12,)}

    def __init__(self, own, out, send, recv, local=None):
        me, side, over_x, over_y, corner = plane()
        half = out.shape[1] // 2
        low, high = pl.ds(0, half), pl.ds(half, half)
        self.keep = None if own is None else pltpu.make_async_copy(own, out.at[me], local)
        own = out.at[me] if own is None else own

        def hop(number, source, target, index):
            return to_dp(source, target, send.at[number], recv.at[number], index)

        def onward(number, owner, part, index):
            place = out.at[owner, part]
            return hop(number, place, place, index)

        self.copies = [
            hop(0, own.at[low], out.at[me, low], over_x),
            hop(1, own.at[high], out.at[me, high], over_y),
            hop(2, own.at[high], out.at[me, high], over_x),
            hop(3, own.at[low], out.at[me, low], over_y),
            hop(4, own, out.at[me], side),
            onward(5, over_x, low, over_y),
            onward(6, over_x, low, side),
            onward(7, over_y, high, over_x),
            onward(8, over_y, high, side),
            onward(9, over_x, high, side),
            onward(10, over_y, low, side),
            onward(11, corner, low, side),
            onward(12, corner, high, side),
        ]

    def start(self):
        for number in range(5):
            self.copies[number].start()
        if self.keep is not None:
            self.keep.start()

    def arrive(self, *numbers):
        for number in numbers:
            self.copies[number].wait_recv()
            for later in self.AFTER.get(number, ()):
                self.copies[later].start()

    def pass_on(self):
        self.arrive(0, 1, 2, 3)

    def sent(self):
        for copy in self.copies:
            copy.wait_send()
        if self.keep is not None:
            self.keep.wait()

    def finish(self):
        self.arrive(5, 7, 4, 6, 8, 9, 10, 11, 12)
        self.sent()


def greet_all():
    barrier = pltpu.get_barrier_semaphore()
    me, z = lax.axis_index("dp"), lax.axis_index("mp")
    for step in range(1, 8):
        pl.semaphore_signal(
            barrier, inc=1, device_id={"dp": lax.rem(me + step, 8)}, device_id_type=MESH
        )
    core = lax.rem(me, 2)
    for step in range(1, 4):
        for other in (me, me + 1 - 2 * core):
            pl.semaphore_signal(
                barrier,
                inc=1,
                device_id={"dp": other, "mp": lax.rem(z + step, 4)},
                device_id_type=MESH,
            )
    return barrier


def start_all(copies):
    for copy in copies:
        copy.start()
    return copies


def wait_all(copies):
    for copy in copies:
        copy.wait()


def swap_all(source, target, send, recv):
    me = lax.axis_index("dp")
    return [
        to_dp(source, target.at[me], send.at[step - 1], recv.at[step - 1], lax.rem(me + step, 8))
        for step in range(1, 8)
    ]


class Spread:
    def __init__(self, share, w_qkv, w_out, send, recv, local):
        me, z = lax.axis_index("dp"), lax.axis_index("mp")
        core = lax.rem(me, 2)
        self.place = z + core * (3 - 2 * z)
        self.send, self.recv, self.local = send, recv, local
        self.shares = [share.at[0], share.at[1], share.at[2], share.at[3]]
        self.slots = (core, 1 - core)
        self.core = core
        self.w_qkv, self.w_out = w_qkv, w_out

    def target(self, which, piece):
        slot = self.slots[which]
        block = slot if piece == 3 else 2 * piece + slot
        rows = pl.ds(pl.multiple_of(block * LANES, LANES), HEAD_DIM)
        return (self.w_out if piece == 3 else self.w_qkv).at[rows]

    def hop(self, which, piece, number, place, own):
        source = self.shares[piece] if own else self.target(which, piece)
        z = place + self.core * (3 - 2 * place)
        return to_mp(
            source,
            self.target(which, piece),
            self.send.at[number * 4 + piece],
            self.recv.at[which * 4 + piece],
            z,
        )

    def keep(self, which, piece):
        return pltpu.make_async_copy(
            self.shares[piece], self.target(which, piece), self.local.at[piece]
        )

    def start(self, pieces):
        @pl.when(self.place == 0)
        def _():
            for piece in pieces:
                self.hop(0, piece, 0, 1, True).start()
                self.keep(0, piece).start()

        @pl.when(self.place == 1)
        def _():
            for piece in pieces:
                self.hop(1, piece, 0, 0, True).start()
                self.hop(1, piece, 1, 2, True).start()
                self.keep(1, piece).start()

    def pass_on(self, pieces):
        @pl.when(self.place == 1)
        def _():
            for piece in pieces:
                self.hop(0, piece, 2, 2, False).wait_recv()
                self.hop(0, piece, 2, 2, False).start()

        @pl.when(self.place == 2)
        def _():
            for which in (1, 0):
                for piece in pieces:
                    self.hop(which, piece, which, 3, False).wait_recv()
                    self.hop(which, piece, which, 3, False).start()

    def finish(self, pieces):
        @pl.when(self.place == 0)
        def _():
            for piece in pieces:
                self.hop(1, piece, 0, 1, False).wait_recv()
                self.hop(0, piece, 0, 1, True).wait_send()
                self.keep(0, piece).wait()

        @pl.when(self.place == 1)
        def _():
            for piece in pieces:
                self.hop(1, piece, 0, 0, True).wait_send()
                self.hop(1, piece, 1, 2, True).wait_send()
                self.hop(0, piece, 2, 2, False).wait_send()
                self.keep(1, piece).wait()

        @pl.when(self.place == 2)
        def _():
            for piece in pieces:
                for which in (1, 0):
                    self.hop(which, piece, which, 3, False).wait_send()

        @pl.when(self.place == 3)
        def _():
            for piece in pieces:
                for which in (1, 0):
                    self.hop(which, piece, which, 3, False).wait_recv()


class Column:
    def __init__(self, own, out, send, recv, local):
        z = lax.axis_index("mp")
        self.z, self.own, self.out, self.send, self.recv = z, own, out, send, recv
        self.outer = (z == 0) | (z == 3)
        near = 1 + lax.div(z, 3)
        self.from_outer = (near, 3 - near)
        self.edge = 3 * (z - 1)
        self.from_inner = (3 - z, 3 - self.edge, self.edge)
        self.keep = pltpu.make_async_copy(own, out.at[z], local)

    def straight(self, number, target):
        return to_mp(
            self.own, self.out.at[self.z], self.send.at[number], self.recv.at[self.z], target
        )

    def onward(self):
        far = 3 - self.edge
        return to_mp(
            self.out.at[far], self.out.at[far], self.send.at[3], self.recv.at[far], self.edge
        )

    def came(self, source):
        return to_mp(
            self.own, self.out.at[source], self.send.at[0], self.recv.at[source], source
        ).wait_recv

    def start(self):
        self.keep.start()

        @pl.when(self.outer)
        def _():
            for number, target in enumerate(self.from_outer):
                self.straight(number, target).start()

        @pl.when(jnp.logical_not(self.outer))
        def _():
            for number, target in enumerate(self.from_inner):
                self.straight(number, target).start()

    def pass_on(self):
        @pl.when(jnp.logical_not(self.outer))
        def _():
            self.came(3 - self.edge)()
            self.onward().start()

    def finish(self):
        @pl.when(self.outer)
        def _():
            for source in (1, 2):
                self.came(source)()
            self.came(3 - self.z)()
            for number, target in enumerate(self.from_outer):
                self.straight(number, target).wait_send()

        @pl.when(jnp.logical_not(self.outer))
        def _():
            self.came(3 - self.z)()
            self.came(self.edge)()
            for number, target in enumerate(self.from_inner):
                self.straight(number, target).wait_send()
            self.onward().wait_send()

        self.keep.wait()


def anywhere():
    return pl.BlockSpec(memory_space=pl.ANY)


def on_chip():
    return pl.BlockSpec(memory_space=pltpu.VMEM)


def remote_params(number, limit=VMEM_LIMIT):
    return pltpu.CompilerParams(
        collective_id=number, has_side_effects=True, vmem_limit_bytes=limit
    )


def hot_of(notes, k, size):
    own = notes[:, 0:48, :].reshape(size, LANES)
    lane = lax.broadcasted_iota(jnp.int32, (size, LANES), 1)
    slot = jnp.sum(jnp.where(lane == k, own, 0.0), axis=1, keepdims=True)
    return (lax.broadcasted_iota(jnp.int32, (size, size), 1).astype(F32) == slot).astype(BF16)


def block_mask(notes, k, block, z, rows):
    position = rows * z + block * 128 + lax.broadcasted_iota(jnp.int32, (128, 1), 0)
    position = position.astype(F32)
    first_end = notes[k, 52:53, 0:1]
    second_end = first_end + notes[k, 52:53, 1:2]
    begin = jnp.where(position >= first_end, first_end, 0.0)
    begin = jnp.where(position >= second_end, second_end, begin)
    column = lax.broadcasted_iota(jnp.int32, (128, 192), 1)
    distance = 64 + lax.broadcasted_iota(jnp.int32, (128, 192), 0) - column
    key_position = (rows * z + block * 128 - 64 + column).astype(F32)
    live = jnp.concatenate(
        [notes[k, 48 + block : 49 + block, :], notes[k, 49 + block : 50 + block, 0:64]], axis=1
    )
    allowed = (distance >= 0) & (distance < WINDOW) & (key_position >= begin)
    return allowed & ((live == 1.0) | (distance == 0))


NT = (((1,), (1,)), ((), ()))
TN = (((0,), (0,)), ((), ()))


def forward_kernel(
    tokens, cotangent, order_row, gain, notes, query, keys, values, project, gate,
    hidden_out, w_qkv_out, w_out, notes_all, gate_all, mixed_out, kept_out, tokens_out, cotangent_out,
    cotangent_all,
    hidden_all, qkv, share, gate_own, w_qkv, mixed, kept, tokens_b, cotangent_b,
    send, recv, send_a, recv_a, send_g, recv_g, send_w, recv_w, send_n, recv_n, send_c, recv_c,
    local, out_sem, store_sem, *, scale,
):
    groups, rows, width = hidden_all.shape
    me, z = lax.axis_index("dp"), lax.axis_index("mp")
    members = lax.axis_size("mp")
    barrier = greet_all()
    head = pl.ds(pl.multiple_of(lax.div(me, 2) * HEAD_DIM, 16), HEAD_DIM)
    units = pl.ds(pl.multiple_of(me * LANES, LANES), LANES)
    loads = [
        pltpu.make_async_copy(source.at[head], share.at[piece], local.at[piece])
        for piece, source in enumerate((query, keys, values, project))
    ]
    loads.append(pltpu.make_async_copy(gate.at[:, units], gate_own, local.at[4]))
    for copy in loads:
        copy.start()
    none = jnp.zeros((LANES - HEAD_DIM, width), BF16)
    for block in range(6):
        w_qkv[block * LANES + HEAD_DIM : block * LANES + LANES, :] = none
    for block in range(2):
        w_out[block * LANES + HEAD_DIM : block * LANES + LANES, :] = none

    place = lax.broadcasted_iota(jnp.int32, (rows, rows), 0).astype(F32)
    sort = (place == order_row[...]).astype(BF16)
    tokens_b[...] = jnp.dot(sort, tokens[...], preferred_element_type=F32).astype(BF16)

    def normalise(span):
        value = tokens_b[span, :].astype(F32)
        inverse = lax.rsqrt(mean_rows(value * value) + EPSILON)
        hidden_all[me, span, :] = (value * inverse * gain[...]).astype(BF16)

    each_chunk(rows, normalise)
    notes_all[me] = notes[...]
    stores = start_all([pltpu.make_async_copy(tokens_b, tokens_out, store_sem.at[0])])
    pl.semaphore_wait(barrier, 13)
    gather = Gather(None, hidden_all, send_a, recv_a)
    gather.start()
    swaps = swap_all(notes, notes_all, send_n, recv_n)
    for copy in swaps:
        copy.start()
    for copy in loads[:4]:
        copy.wait()
    spread = Spread(share, w_qkv, w_out, send_w, recv_w, local)
    spread.start((0, 1, 2))
    cotangent_b[...] = jnp.dot(sort, cotangent[...], preferred_element_type=F32).astype(BF16)
    stores += start_all([pltpu.make_async_copy(cotangent_b, cotangent_out, store_sem.at[1])])
    wait_all(loads[4:])
    column = Column(gate_own, gate_all, send_c, recv_c, local.at[4])
    second = Gather(cotangent_b, cotangent_all, send_g, recv_g, local.at[5])
    spread.pass_on((0, 1, 2))
    gather.arrive(0, 1)
    second.start()
    column.start()
    gather.arrive(2, 3)
    spread.finish((0, 1, 2))
    spread.start((3,))
    stores += start_all([pltpu.make_async_copy(w_qkv, w_qkv_out, store_sem.at[2])])
    for copy in swaps:
        copy.wait()

    def keep(turn):
        owner = owner_at(turn)
        return pltpu.make_async_copy(hidden_all.at[owner], hidden_out.at[owner], out_sem.at[turn])

    def multiply(turn, carry):
        for number, numbers in ARRIVALS:
            left = tuple(n for n in numbers if n > 3)
            if left:
                pl.when(turn == number)(functools.partial(gather.arrive, *left))
        owner = owner_at(turn)
        keep(turn).start()
        product = lax.dot_general(
            hidden_all[owner], w_qkv[...], NT, preferred_element_type=F32
        ).astype(BF16)
        qkv[owner] = product.reshape(groups, rows // groups, 768)
        return carry

    lax.fori_loop(0, groups, multiply, 0)

    def halo(k, other):
        return to_mp(
            kept.at[k, pl.ds(rows, 64), pl.ds(256, 512)],
            kept.at[k, pl.ds(0, 64), pl.ds(256, 512)],
            send.at[k],
            recv.at[k],
            other,
        )

    def store_kept(k):
        return pltpu.make_async_copy(kept.at[k], kept_out.at[k], store_sem.at[3 + k])

    def store_mixed(k):
        span = pl.ds(k, 1)
        return pltpu.make_async_copy(
            mixed.at[:, span], mixed_out.at[:, span], store_sem.at[3 + groups + k]
        )

    def order(k, carry):
        hot = hot_of(notes_all, k, rows)
        given = qkv[:, pl.ds(k, 1)].reshape(rows, 768)
        kept[k, pl.ds(64, rows), :] = lax.dot_general(
            hot, given, TN, preferred_element_type=F32
        ).astype(BF16)
        kept[k, pl.ds(0, 64), pl.ds(0, 256)] = jnp.zeros((64, 256), BF16)

        @pl.when(z < members - 1)
        def _():
            halo(k, z + 1).start()

        @pl.when(z == 0)
        def _():
            kept[k, pl.ds(0, 64), pl.ds(256, 512)] = jnp.zeros((64, 512), BF16)

        return carry

    lax.fori_loop(0, groups, order, 0)

    def attend(k, carry):
        @pl.when(z > 0)
        def _():
            halo(k, z).wait_recv()

        store_kept(k).start()
        hot = hot_of(notes_all, k, rows)
        pairs = [(block, head) for block in range(rows // 128) for head in range(2)]
        masks = [block_mask(notes_all, k, block, z, rows) for block in range(rows // 128)]
        scores = []
        for block, head in pairs:
            query = kept[k, pl.ds(64 + block * 128, 128), pl.ds(head * 128, 128)]
            keys = kept[k, pl.ds(block * 128, 192), pl.ds(256 + head * 128, 128)]
            value = lax.dot_general(query, keys, NT, preferred_element_type=F32) * scale
            scores.append(jnp.where(masks[block], value, -MASKED))
        chances = []
        for value in scores:
            weights = jnp.exp(value - jnp.max(value, axis=-1, keepdims=True))
            total = jnp.sum(weights, axis=-1, keepdims=True)
            chances.append((weights / total).astype(BF16))
        parts = []
        for (block, head), chance in zip(pairs, chances):
            values = kept[k, pl.ds(block * 128, 192), pl.ds(512 + head * 128, 128)]
            parts.append(jnp.dot(chance, values, preferred_element_type=F32).astype(BF16))
        found = [
            jnp.concatenate(parts[2 * block : 2 * block + 2], axis=1)
            for block in range(rows // 128)
        ]
        ordered = jnp.concatenate(found, axis=0)
        back = jnp.dot(hot, ordered, preferred_element_type=F32).astype(BF16)
        mixed[:, pl.ds(k, 1)] = back.reshape(groups, 1, rows // groups, 256)
        store_mixed(k).start()
        return carry

    spread.pass_on((3,))
    lax.fori_loop(0, 2, attend, 0)
    second.pass_on()
    column.pass_on()
    lax.fori_loop(2, groups, attend, 0)
    spread.finish((3,))
    second.finish()
    column.finish()
    gather.sent()

    wait_all(stores)

    def stored(turn, carry):
        keep(turn).wait()
        store_kept(turn).wait()
        store_mixed(turn).wait()
        return carry

    lax.fori_loop(0, groups, stored, 0)

    @pl.when(z < members - 1)
    def _():
        def done(k, carry):
            halo(k, z + 1).wait_send()
            return carry

        lax.fori_loop(0, groups, done, 0)


def attend_ahead(
    tokens, cotangent, order_row, gain, notes, query, keys, values, project, gate, scale
):
    rows, width = tokens.shape
    groups, members = lax.axis_size("dp"), lax.axis_size("mp")
    dma = pltpu.SemaphoreType.DMA
    shape = jax.ShapeDtypeStruct
    return pl.pallas_call(
        functools.partial(forward_kernel, scale=scale),
        out_shape=(
            shape((groups, rows, width), BF16),
            shape((6 * LANES, width), BF16),
            shape((2 * LANES, width), BF16),
            shape((groups,) + notes.shape, F32),
            shape((members, width, LANES), BF16),
            shape((groups, groups, rows // groups, 256), BF16),
            shape((groups, rows + 64, 768), BF16),
            shape((rows, width), BF16),
            shape((rows, width), BF16),
            shape((groups, rows, width), BF16),
        ),
        in_specs=[on_chip()] * 5 + [anywhere()] * 5,
        out_specs=(
            anywhere(), anywhere(), on_chip(), on_chip(), anywhere(),
            anywhere(), anywhere(), anywhere(), anywhere(), anywhere(),
        ),
        scratch_shapes=[
            pltpu.VMEM((groups, rows, width), BF16),
            pltpu.VMEM((groups, groups, rows // groups, 768), BF16),
            pltpu.VMEM((4, HEAD_DIM, width), BF16),
            pltpu.VMEM((width, LANES), BF16),
            pltpu.VMEM((6 * LANES, width), BF16),
            pltpu.VMEM((groups, groups, rows // groups, 256), BF16),
            pltpu.VMEM((groups, rows + 64, 768), BF16),
            pltpu.VMEM((rows, width), BF16),
            pltpu.VMEM((rows, width), BF16),
            dma((groups,)),
            dma((groups,)),
            dma((13,)),
            dma((13,)),
            dma((13,)),
            dma((13,)),
            dma((12,)),
            dma((8,)),
            dma((7,)),
            dma((7,)),
            dma((4,)),
            dma((4,)),
            dma((6,)),
            dma((groups,)),
            dma((3 + 2 * groups,)),
        ],
        compiler_params=remote_params(2, 60 * 1024 * 1024),
        cost_estimate=pl.CostEstimate(flops=0, bytes_accessed=300_000_000, transcendentals=0),
        name="attend_ahead",
    )(tokens, cotangent, order_row, gain, notes, query, keys, values, project, gate)


CHUNK = 32


def each_chunk(rows, body, chunk=CHUNK):
    def step(i, carry):
        body(pl.ds(pl.multiple_of(i * chunk, chunk), chunk))
        return carry

    lax.fori_loop(0, rows // chunk, step, 0)


class Units:
    def __init__(self, part, came_in, stage, send, recv, local):
        self.z = lax.axis_index("mp")
        self.part_of = part
        self.inputs = (came_in,)
        self.stages = (stage,)
        self.send, self.recv, self.local = send, recv, local
        z = self.z
        self.outer = (z == 0) | (z == 3)
        self.far = 3 - z
        self.near = 1 + lax.div(z, 3)
        self.second = 3 - self.near
        self.edge = 3 * (z - 1)

    def part(self, kind, z):
        return self.part_of(z)

    def straight(self, kind, number, target):
        return to_mp(
            self.part(kind, target),
            self.inputs[kind].at[self.z],
            self.send.at[number * 2 + kind],
            self.recv.at[self.z * 2 + kind],
            target,
        )

    def staged(self, kind):
        return to_mp(
            self.part(kind, self.far),
            self.stages[kind].at[0],
            self.send.at[4 + kind],
            self.recv.at[8 + kind],
            self.near,
        )

    def summed(self, kind):
        return to_mp(
            self.stages[kind].at[1],
            self.inputs[kind].at[self.z],
            self.send.at[4 + kind],
            self.recv.at[self.z * 2 + kind],
            3 - self.edge,
        )

    def mine(self, kind):
        return pltpu.make_async_copy(
            self.part(kind, 3 - self.edge), self.stages[kind].at[1], self.local.at[kind]
        )

    def start(self):
        @pl.when(self.outer)
        def _():
            for kind in range(1):
                self.staged(kind).start()
            for kind in range(1):
                self.straight(kind, 0, self.near).start()
                self.straight(kind, 1, self.second).start()

        @pl.when(jnp.logical_not(self.outer))
        def _():
            for kind in range(1):
                self.mine(kind).start()
                self.straight(kind, 0, 3 - self.z).start()
                self.straight(kind, 1, self.edge).start()

    def add(self):
        @pl.when(jnp.logical_not(self.outer))
        def _():
            for kind in range(1):
                stage = self.stages[kind]
                self.mine(kind).wait()
                to_mp(
                    self.part(kind, 0),
                    stage.at[0],
                    self.send.at[4 + kind],
                    self.recv.at[8 + kind],
                    self.edge,
                ).wait_recv()

                def body(span):
                    stage[1, span, :] = (
                        stage[0, span, :].astype(F32) + stage[1, span, :].astype(F32)
                    ).astype(BF16)

                each_chunk(stage.shape[1], body)
                self.summed(kind).start()

    def arrived(self, kind, source):
        to_mp(
            self.part(kind, 0),
            self.inputs[kind].at[source],
            self.send.at[kind],
            self.recv.at[source * 2 + kind],
            source,
        ).wait_recv()

    def finish(self):
        @pl.when(self.outer)
        def _():
            for kind in range(1):
                self.arrived(kind, 1)
                self.arrived(kind, 2)
                self.straight(kind, 0, self.near).wait_send()
                self.straight(kind, 1, self.second).wait_send()
                self.staged(kind).wait_send()

        @pl.when(jnp.logical_not(self.outer))
        def _():
            for kind in range(1):
                self.arrived(kind, 0)
                self.arrived(kind, 3)
                self.arrived(kind, 3 - self.z)
                self.straight(kind, 0, 3 - self.z).wait_send()
                self.straight(kind, 1, self.edge).wait_send()
                self.summed(kind).wait_send()


class Reduce:
    COUNT = 10

    def __init__(self, left, right, across, part, from_side, from_corner, from_near, send, recv):
        self.left, self.right, self.across, self.part = left, right, across, part
        self.from_side, self.from_corner, self.from_near = from_side, from_corner, from_near
        self.send, self.recv = send, recv
        self.rows = part.shape[1]

    def product(self, owner, slot):
        rows, width = self.rows, self.part.shape[2]
        picked = pl.ds(pl.multiple_of(owner * rows, rows), rows)

        def tile(t, carry):
            columns = pl.ds(pl.multiple_of(t * 256, 256), 256)
            if callable(self.left):
                value = jnp.dot(
                    self.left(owner), self.right[:, columns], preferred_element_type=F32
                )
            elif self.across:
                value = lax.dot_general(
                    self.left[picked, :], self.right[columns, :], NT, preferred_element_type=F32
                )
            else:
                value = jnp.dot(
                    self.left[picked, :], self.right[:, columns], preferred_element_type=F32
                )
            self.part[slot, :, columns] = value.astype(BF16)
            return carry

        lax.fori_loop(0, width // 256, tile, 0)

    def prepare(self):
        _, side, over_x, over_y, corner = plane()
        part, near = self.part, self.from_near
        half = self.rows // 2
        low, high = pl.ds(0, half), pl.ds(half, half)

        def hop(number, source, target, index):
            return to_dp(source, target, self.send.at[number], self.recv.at[number], index)

        self.shares = [hop(i, part.at[4 + i], self.from_side.at[i], side) for i in range(4)]
        self.corners = [
            hop(4, part.at[0, low], self.from_corner.at[0], over_x),
            hop(5, part.at[0, high], self.from_corner.at[1], over_y),
        ]
        self.nears = [
            hop(6, part.at[1, low], near.at[0, low], over_x),
            hop(7, part.at[1, high], near.at[0, high], over_x),
            hop(8, part.at[2, high], near.at[1, high], over_y),
            hop(9, part.at[2, low], near.at[1, low], over_y),
        ]

    def add_side(self, slot):
        self.shares[slot].wait_recv()

        def body(span):
            self.part[slot, span, :] = (
                self.part[slot, span, :].astype(F32) + self.from_side[slot, span, :].astype(F32)
            ).astype(BF16)

        each_chunk(self.rows, body)

    def add_corner(self, slot, offset, which):
        self.corners[which].wait_recv()

        def body(span):
            target = pl.ds(pl.multiple_of(offset + span.start, CHUNK), CHUNK)
            self.part[slot, target, :] = (
                self.part[slot, target, :].astype(F32)
                + self.from_corner[which, span, :].astype(F32)
            ).astype(BF16)

        each_chunk(self.rows // 2, body)

    def products(self):
        self.prepare()
        me, _, over_x, over_y, corner = plane()
        turn = 1 - 2 * lax.rem(me, 2)
        for slot, owner in enumerate((corner, over_x, over_y, me)):
            self.product(owner + turn, 4 + slot)
            self.shares[slot].start()
        for slot, owner in enumerate((corner, over_x, over_y, me)):
            self.product(owner, slot)

    def launch(self):
        self.add_side(0)
        self.corners[0].start()
        self.corners[1].start()
        self.add_side(1)
        self.nears[0].start()
        self.add_side(2)
        self.nears[2].start()

    def begin(self):
        self.prepare()
        me, _, over_x, over_y, corner = plane()
        turn = 1 - 2 * lax.rem(me, 2)
        self.product(corner + turn, 4)
        self.shares[0].start()
        self.product(corner, 0)
        self.product(over_x + turn, 5)
        self.shares[1].start()
        self.add_side(0)
        self.corners[0].start()
        self.corners[1].start()
        self.product(over_x, 1)
        self.product(over_y + turn, 6)
        self.shares[2].start()
        self.add_side(1)
        self.nears[0].start()
        self.product(over_y, 2)
        self.product(me + turn, 7)
        self.shares[3].start()
        self.add_side(2)
        self.nears[2].start()
        self.product(me, 3)

    def middle(self):
        self.add_corner(2, 0, 0)
        self.nears[3].start()
        self.add_corner(1, self.rows // 2, 1)
        self.nears[1].start()

    def end(self):
        self.shares[3].wait_recv()
        for copy in self.nears:
            copy.wait_recv()

    def run(self):
        self.begin()
        self.middle()
        self.end()

    def rows_of(self, span):
        return (
            self.part[3, span, :].astype(F32)
            + self.from_side[3, span, :].astype(F32)
            + self.from_near[0, span, :].astype(F32)
            + self.from_near[1, span, :].astype(F32)
        )

    def finish(self):
        for copy in self.shares + self.corners + self.nears:
            copy.wait_send()


def reduce_scratch(rows, width):
    dma = pltpu.SemaphoreType.DMA
    return [
        pltpu.VMEM((8, rows, width), BF16),
        pltpu.VMEM((4, rows, width), BF16),
        pltpu.VMEM((2, rows // 2, width), BF16),
        pltpu.VMEM((2, rows, width), BF16),
        dma((10,)),
        dma((10,)),
    ]


def gather_scratch(rows, width):
    dma = pltpu.SemaphoreType.DMA
    return [pltpu.VMEM((rows, width), BF16), dma((13,)), dma((13,)), dma(())]


def mean_rows(values):
    return jnp.mean(values, axis=-1, keepdims=True)


class Heads:
    def __init__(self, source, stage, arrive, send, recv_stage, recv):
        me, z = lax.axis_index("dp"), lax.axis_index("mp")
        self.me, self.z = me, z
        self.core = lax.rem(me, 2)
        self.source, self.stage, self.arrive = source, stage, arrive
        self.send, self.recv_stage, self.recv = send, recv_stage, recv
        self.place = z + self.core * (3 - 2 * z)
        self.columns = source.shape[1] // 2

    def z_of(self, place):
        return place + self.core * (3 - 2 * place)

    def slot_of(self, place):
        return self.core if place == 0 else 1 - self.core

    def rows_of(self, place, kind):
        block = 2 * kind + self.slot_of(place)
        return self.source.at[pl.ds(pl.multiple_of(block * LANES, LANES), HEAD_DIM)]

    def half_of(self, ref, half):
        return ref.at[:, pl.ds(pl.multiple_of(half * self.columns, LANES), self.columns)]

    def to_stage(self, place, kind):
        return to_at(
            self.rows_of(place, kind),
            self.stage.at[place, kind],
            self.send.at[place * 4 + kind],
            self.recv_stage.at[place * 4 + kind],
            self.me,
            self.z_of(2),
        )

    def to_owner(self, place, kind, half, way, ref, number):
        return to_at(
            self.half_of(ref, half),
            self.arrive.at[way, kind],
            self.send.at[number],
            self.recv.at[way * 4 + kind],
            self.me - self.core + half,
            self.z_of(place),
        )

    def sums(self, kind):
        return [
            self.to_owner(
                place, kind, half, 2, self.stage.at[place, kind], place * 8 + kind * 2 + half
            )
            for place in (0, 1)
            for half in (0, 1)
        ]

    def cross(self, own, kind):
        other = 1 - own
        copies = [
            self.to_owner(other, kind, half, 0, self.rows_of(other, kind), kind * 2 + half)
            for half in (0, 1)
        ]
        copies.append(
            to_at(
                self.half_of(self.rows_of(own, kind), 1 - self.core),
                self.arrive.at[1, kind],
                self.send.at[8 + kind],
                self.recv.at[4 + kind],
                self.me + 1 - 2 * self.core,
                self.z,
            )
        )
        return copies

    def start(self, kinds):
        @pl.when(self.place == 3)
        def _():
            for kind in kinds:
                self.to_stage(0, kind).start()
                self.to_stage(1, kind).start()

        for own in (0, 1):
            @pl.when(self.place == own)
            def _():
                for kind in kinds:
                    for copy in self.cross(own, kind):
                        copy.start()

    def add(self, kinds):
        @pl.when(self.place == 2)
        def _():
            for kind in kinds:
                for place in (0, 1):
                    self.to_stage(place, kind).wait_recv()
                    mine = self.rows_of(place, kind)

                    def body(span):
                        self.stage[place, kind, span, :] = (
                            self.stage[place, kind, span, :].astype(F32)
                            + mine[span, :].astype(F32)
                        ).astype(BF16)

                    each_chunk(HEAD_DIM, body, 16)
                for copy in self.sums(kind):
                    copy.start()

    def total(self, out):
        owner = lax.div(self.z, 2) == self.core
        for kind in range(4):
            for own in (0, 1):
                @pl.when(self.place == own)
                def _():
                    self.arrive[1, kind] = self.half_of(self.rows_of(own, kind), self.core)[...]

            for way in range(3):
                waiting = to_at(
                    self.half_of(self.rows_of(0, kind), 0),
                    self.arrive.at[way, kind],
                    self.send.at[0],
                    self.recv.at[way * 4 + kind],
                    self.me,
                    lax.rem(self.z + 1, 4),
                )
                if way == 1:
                    pl.when(jnp.logical_not(owner))(waiting.wait_recv)
                else:
                    waiting.wait_recv()

            def body(span):
                found = self.arrive[0, kind, span, :].astype(F32)
                found = found + self.arrive[1, kind, span, :].astype(F32)
                found = found + self.arrive[2, kind, span, :].astype(F32)
                target = pl.ds(pl.multiple_of(kind * HEAD_DIM + span.start, 16), 16)
                out[target, :] = found.astype(BF16)

            each_chunk(HEAD_DIM, body, 16)

    def finish_send(self):
        for kind in range(4):
            @pl.when(self.place == 3)
            def _():
                self.to_stage(0, kind).wait_send()
                self.to_stage(1, kind).wait_send()

            @pl.when(self.place == 2)
            def _():
                for copy in self.sums(kind):
                    copy.wait_send()

            for own in (0, 1):
                @pl.when(self.place == own)
                def _():
                    for copy in self.cross(own, kind):
                        copy.wait_send()


def to_at(source, target, send_sem, recv_sem, dp, mp):
    return pltpu.make_async_remote_copy(
        src_ref=source,
        dst_ref=target,
        send_sem=send_sem,
        recv_sem=recv_sem,
        device_id={"dp": dp, "mp": mp},
        device_id_type=MESH,
    )


def backward_kernel(
    branch, notes_all, kept_in, w_out_in, activated_in, w_down_in, middle_in, both_sum, down_sum,
    out, result, branch_all, both_in, down_all,
    totals, query_part, key_value, ending, leaving, arriving, send, recv,
    part, from_side, from_corner, from_near, send_r, recv_r,
    mixed_grad, shard, load_sem, send_g, recv_g,
    both_stage, send_u, recv_u, local, down_found, send_d, recv_d,
    kept, w_out, activated, w_down, middle, fetch_sem, down_stage, send_v, recv_v, local_v,
    *, scale, groups, rows,
):
    z = lax.axis_index("mp")
    members = lax.axis_size("mp")
    barrier = greet_all()
    pairs = ((activated_in, activated), (w_out_in, w_out), (kept_in, kept), (middle_in, middle))
    pairs += ((w_down_in, w_down),)
    fetches = [
        pltpu.make_async_copy(source, target, fetch_sem.at[number])
        for number, (source, target) in enumerate(pairs)
    ]

    def down_rows(owner):
        return down_sum.at[pl.ds(pl.multiple_of(owner * LANES, LANES), LANES)]

    down_units = Units(down_rows, down_found, down_stage, send_v, recv_v, local_v)
    load_down = pltpu.make_async_copy(down_rows(z), down_found.at[z], load_sem.at[2])
    pl.semaphore_wait(barrier, 13)
    units = Units(lambda owner: both_sum.at[owner], both_in, both_stage, send_u, recv_u, local)
    gather = Gather(branch, branch_all, send_g, recv_g, local.at[2])
    gather.start()
    down_units.start()
    units.start()
    start_all(fetches)
    load_down.start()
    wait_all((fetches[0], fetches[4]))
    reduce = Reduce(activated, w_down, False, part, from_side, from_corner, from_near, send_r, recv_r)
    reduce.products()
    down_units.add()
    down = Gather(down_found.at[0], down_all, send_d, recv_d, local.at[1])

    def load_shard(turn):
        slot = turn % 2
        return pltpu.make_async_copy(branch_all.at[owner_at(turn)], shard.at[slot], load_sem.at[slot])

    def spread_back(turn, carry):
        for number, numbers in ARRIVALS:
            pl.when(turn == number)(functools.partial(gather.arrive, *numbers))

        @pl.when(turn == 0)
        def _():
            gather.keep.wait()

        load_shard(turn).start()
        load_shard(turn).wait()
        mixed_grad[owner_at(turn)] = (
            lax.dot_general(shard[turn % 2], w_out[...], NT, preferred_element_type=F32)
            .astype(BF16)
            .reshape(groups, rows // groups, 256)
        )
        return carry

    fetches[1].wait()
    lax.fori_loop(0, 4, spread_back, 0)
    reduce.launch()
    lax.fori_loop(4, 8, spread_back, 0)
    units.add()


    def halo(k, other):
        return to_mp(leaving.at[k], arriving.at[k], send.at[k], recv.at[k], other)

    def attend(k, carry):
        hot = hot_of(notes_all, k, rows)
        given = mixed_grad[:, pl.ds(k, 1)].reshape(rows, 256)
        grad_ordered = lax.dot_general(hot, given, TN, preferred_element_type=F32).astype(BF16)
        totals[...] = jnp.zeros_like(totals)
        pairs = [(block, head) for block in range(rows // 128) for head in range(2)]
        masks = [block_mask(notes_all, k, block, z, rows) for block in range(rows // 128)]

        def query_of(block, head):
            return kept[k, pl.ds(64 + block * 128, 128), pl.ds(head * 128, 128)]

        def keys_of(block, head):
            return kept[k, pl.ds(block * 128, 192), pl.ds(256 + head * 128, 128)]

        def grad_of(block, head):
            return grad_ordered[block * 128 : block * 128 + 128, head * 128 : head * 128 + 128]

        scores, chance_grads = [], []
        for block, head in pairs:
            value = lax.dot_general(
                query_of(block, head), keys_of(block, head), NT, preferred_element_type=F32
            )
            scores.append(jnp.where(masks[block], value * scale, -MASKED))
            values = kept[k, pl.ds(block * 128, 192), pl.ds(512 + head * 128, 128)]
            chance_grads.append(
                lax.dot_general(grad_of(block, head), values, NT, preferred_element_type=F32)
            )
        agains, score_grads = [], []
        for value, chance_grad in zip(scores, chance_grads):
            weights = jnp.exp(value - jnp.max(value, axis=-1, keepdims=True))
            again = weights / jnp.sum(weights, axis=-1, keepdims=True)
            row_dot = jnp.sum(again * chance_grad, axis=-1, keepdims=True)
            agains.append(again.astype(BF16))
            score_grads.append((again * (chance_grad - row_dot)).astype(BF16))
        for (block, head), again, score_grad in zip(pairs, agains, score_grads):
            query_part[k, pl.ds(block * 128, 128), pl.ds(head * 128, 128)] = (
                jnp.dot(score_grad, keys_of(block, head), preferred_element_type=F32) * scale
            ).astype(BF16)
            totals[pl.ds(block * 128, 192), pl.ds(head * 128, 128)] += (
                lax.dot_general(score_grad, query_of(block, head), TN, preferred_element_type=F32)
                * scale
            )
            totals[pl.ds(block * 128, 192), pl.ds(256 + head * 128, 128)] += lax.dot_general(
                again, grad_of(block, head), TN, preferred_element_type=F32
            )
        key_value[k] = totals[pl.ds(64, rows), :].astype(BF16)
        ending[k] = totals[pl.ds(rows, 64), :]

        @pl.when(z > 0)
        def _():
            leaving[k] = totals[pl.ds(0, 64), :].astype(BF16)
            halo(k, z - 1).start()

        return carry

    wait_all(fetches[2:4])
    lax.fori_loop(0, 2, attend, 0)
    reduce.middle()
    load_down.wait()
    down_units.finish()

    @pl.when((z == 0) | (z == members - 1))
    def _():
        down_found[members - 1 - z] = jnp.zeros_like(down_found[0])

    def add_down(span):
        value = down_found[0, span, :].astype(F32) + down_found[1, span, :].astype(F32)
        value = value + down_found[2, span, :].astype(F32) + down_found[3, span, :].astype(F32)
        down_found[0, span, :] = value.astype(BF16)

    each_chunk(down_found.shape[1], add_down)
    down.start()
    lax.fori_loop(2, groups, attend, 0)
    down.pass_on()

    def restore(k, carry):
        @pl.when(z < members - 1)
        def _():
            halo(k, z).wait_recv()
            key_value[k, pl.ds(rows - 64, 64), :] = (
                ending[k] + arriving[k].astype(F32)
            ).astype(BF16)

        hot = hot_of(notes_all, k, rows)
        ordered = jnp.concatenate([query_part[k], key_value[k]], axis=1)
        back = jnp.dot(hot, ordered, preferred_element_type=F32).astype(BF16)
        out[:, pl.ds(k, 1)] = back.reshape(groups, 1, rows // groups, 768)
        return carry

    lax.fori_loop(0, groups, restore, 0)
    reduce.end()

    def body(span):
        result[span, :] = (middle[span, :] + reduce.rows_of(span)).astype(BF16)

    each_chunk(rows, body)
    down.finish()
    units.finish()
    for copy in gather.copies:
        copy.wait_send()
    reduce.finish()

    @pl.when(z > 0)
    def _():
        def done(k, carry):
            halo(k, z - 1).wait_send()
            return carry

        lax.fori_loop(0, groups, done, 0)


def attend_back(
    branch, notes_all, kept, w_out, activated, w_down, middle, both_sum, down_sum, scale
):
    groups = kept.shape[0]
    rows, width = middle.shape
    members = both_sum.shape[0]
    dma = pltpu.SemaphoreType.DMA
    shape = jax.ShapeDtypeStruct
    return pl.pallas_call(
        functools.partial(backward_kernel, scale=scale, groups=groups, rows=rows),
        out_shape=(
            shape((groups, groups, rows // groups, 768), BF16),
            shape((rows, width), BF16),
            shape((groups, rows, width), BF16),
            shape((members, width, 256), BF16),
            shape((groups, LANES, width), BF16),
        ),
        in_specs=[on_chip()] * 2 + [anywhere()] * 7,
        out_specs=(on_chip(),) * 2 + (anywhere(),) * 3,
        scratch_shapes=[
            pltpu.VMEM((rows + 64, 512), F32),
            pltpu.VMEM((groups, rows, 256), BF16),
            pltpu.VMEM((groups, rows, 512), BF16),
            pltpu.VMEM((groups, 64, 512), F32),
            pltpu.VMEM((groups, 64, 512), BF16),
            pltpu.VMEM((groups, 64, 512), BF16),
            dma((groups,)),
            dma((groups,)),
        ]
        + reduce_scratch(rows, width)
        + [
            pltpu.VMEM((groups, groups, rows // groups, 256), BF16),
            pltpu.VMEM((2, rows, width), BF16),
            dma((3,)),
            dma((13,)),
            dma((13,)),
            pltpu.VMEM((2, width, 256), BF16),
            dma((6,)),
            dma((10,)),
            dma((3,)),
            pltpu.VMEM((members, LANES, width), BF16),
            dma((13,)),
            dma((13,)),
            pltpu.VMEM(kept.shape, BF16),
            pltpu.VMEM(w_out.shape, BF16),
            pltpu.VMEM(activated.shape, BF16),
            pltpu.VMEM((members * LANES, width), BF16),
            pltpu.VMEM((rows, width), F32),
            dma((5,)),
            pltpu.VMEM((2, LANES, width), BF16),
            dma((6,)),
            dma((10,)),
            dma((1,)),
        ],
        compiler_params=remote_params(3, 63 * 1024 * 1024),
        cost_estimate=pl.CostEstimate(flops=0, bytes_accessed=300_000_000, transcendentals=0),
        name="attend_back",
    )(branch, notes_all, kept, w_out, activated, w_down, middle, both_sum, down_sum)


def norm_back_rows(gradient, values, gain, sums, span):
    inverse = lax.rsqrt(mean_rows(values * values) + EPSILON)
    normed = values * inverse
    product = gradient * normed
    folded = product[0:8]
    for step in range(1, CHUNK // 8):
        folded = folded + product[step * 8 : step * 8 + 8]
    sums[...] += folded
    scaled = gradient * gain
    return inverse * (scaled - normed * mean_rows(scaled * normed))


def feed_kernel(
    mixed, w_out, tokens, cotangent_all, gate_all, w_up, down_weight, cotangent_own, gain,
    middle, middle_grad, branch, sums, activated_out, both_sum, down_out, up_all, down_all,
    hidden_all, both_grad, part, from_side, from_corner, from_near, send_r, recv_r,
    send_m, recv_m, send_n, recv_n, send_a, recv_a, send_b, recv_b, cot_shard, cot_tile, stage_both, down_sum, w_both, w_down,
    cotangent, activated, load_sem, local,
    up_own, down_own, send_u, recv_u, send_d, recv_d, first_sem,
):
    groups, rows, width = hidden_all.shape
    members = gate_all.shape[0]
    me = lax.axis_index("dp")
    barrier = greet_all()
    units_own = pl.ds(pl.multiple_of(me * LANES, LANES), LANES)
    first = start_all(
        [
            pltpu.make_async_copy(source, target, first_sem.at[number])
            for number, (source, target) in enumerate(
                (
                    (mixed, activated.at[:, :, pl.ds(0, 256)]),
                    (w_out, down_sum.at[pl.ds(0, 256)]),
                    (w_up.at[:, units_own], up_own),
                    (down_weight.at[units_own], down_own),
                    (tokens, cotangent),
                )
            )
        ]
    )
    gates = start_all(
        [
            pltpu.make_async_copy(
                gate_all.at[z], w_both.at[:, pl.ds(z * 256, 128)], load_sem.at[6 + z]
            )
            for z in range(members)
        ]
    )

    def slot_of(turn):
        block = turn // 2
        near = ((block + 1) // 2) % 2
        far = block // 3
        second = turn % 2
        other = (1 - near) * second + (block // 2) * near
        return 4 * other + 3 * (1 - near) * (1 - far) + near * (1 + second)

    def load_cotangent(turn):
        return pltpu.make_async_copy(
            cotangent_all.at[owner_at(turn)], cot_shard.at[turn % 2], load_sem.at[turn % 2]
        )

    load_cotangent(0).start()
    wait_all(first)
    pl.semaphore_wait(barrier, 13)
    columns_up = Column(up_own, up_all, send_u, recv_u, local.at[0])
    columns_down = Column(down_own, down_all, send_d, recv_d, local.at[2])
    columns_up.start()
    columns_down.start()
    half_rows = rows // 2

    def half(number, sends, recvs):
        span = pl.ds(number * half_rows, half_rows)
        quarter = pl.ds(number * (half_rows // 2), half_rows // 2)
        return Reduce(
            lambda owner: activated[owner, span, 0:256], down_sum.at[pl.ds(0, 256)], False,
            part.at[:, span], from_side.at[:, span], from_corner.at[:, quarter],
            from_near.at[:, span], sends, recvs,
        )

    projects = (half(0, send_m, recv_m), half(1, send_n, recv_n))
    gathers = [
        Gather(None, hidden_all.at[:, pl.ds(number * half_rows, half_rows)], sends, recvs)
        for number, (sends, recvs) in enumerate(((send_a, recv_a), (send_b, recv_b)))
    ]
    for project in projects:
        project.begin()
    for project in projects:
        project.middle()
    columns_up.pass_on()
    columns_down.pass_on()
    for number, project in enumerate(projects):
        project.end()

        def normalise(span):
            own = pl.ds(pl.multiple_of(number * half_rows + span.start, CHUNK), CHUNK)
            values = cotangent[own, :].astype(F32) + project.rows_of(span)
            middle_grad[own, :] = values
            inverse = lax.rsqrt(mean_rows(values * values) + EPSILON)
            hidden_all[me, own, :] = (values * inverse * gain[...]).astype(BF16)

        each_chunk(half_rows, normalise)
        gathers[number].start()

    for project in projects:
        project.finish()
    store_middle = pltpu.make_async_copy(middle_grad, middle, local.at[1])
    load_own = pltpu.make_async_copy(cotangent_own, cotangent, local.at[3])
    store_middle.start()
    load_own.start()
    columns_up.finish()
    columns_down.finish()
    ups = start_all(
        [
            pltpu.make_async_copy(
                up_all.at[z], w_both.at[:, pl.ds(z * 256 + 128, 128)], load_sem.at[10 + z]
            )
            for z in range(members)
        ]
    )
    ups += start_all(
        [
            pltpu.make_async_copy(
                down_all.at[z], w_down.at[pl.ds(z * LANES, LANES)], load_sem.at[14 + z]
            )
            for z in range(members)
        ]
    )
    reduce = Reduce(None, None, False, part, from_side, from_corner, from_near, send_r, recv_r)
    reduce.prepare()

    def nears():
        reduce.add_side(1)
        reduce.nears[0].start()
        reduce.add_side(2)
        reduce.nears[2].start()

    early = [
        (turn, functools.partial(gather.arrive, *numbers))
        for turn, numbers in ARRIVALS
        for gather in gathers
    ]
    early += [(6, nears)]
    late = [(1, 3), (4, 1), (5, 2), (7, 0)]
    wait_all(gates + ups)

    def unit(turn, carry):
        for number, action in early:
            pl.when(turn == number)(action)

        @pl.when(turn < 7)
        def _():
            load_cotangent(turn + 1).start()

        load_cotangent(turn).wait()
        owner, slot = owner_at(turn), slot_of(turn)
        mine = hidden_all[owner]
        grads = cot_shard[turn % 2]
        for z in range(members):
            raw = jnp.dot(mine, w_both[:, z * 256 : z * 256 + 256], preferred_element_type=F32)
            units = pl.ds(z * 128, 128)
            if z % 2 == 0:
                pair = lax.dot_general(
                    grads, w_down[pl.ds(z * 128, 256), :], NT, preferred_element_type=F32
                )
            active_grad = pair[:, 128 * (z % 2) : 128 * (z % 2) + 128]
            gate, upward = raw[:, :128], raw[:, 128:]
            sigmoid = jax.nn.sigmoid(gate)
            activated[owner, :, units] = (gate * sigmoid * upward).astype(BF16)
            both_grad[owner, :, pl.ds(z * 256, 128)] = (
                active_grad * upward * sigmoid * (1.0 + gate * (1.0 - sigmoid))
            ).astype(BF16)
            both_grad[owner, :, pl.ds(z * 256 + 128, 128)] = (
                active_grad * gate * sigmoid
            ).astype(BF16)

        def tile(t, inner):
            columns = pl.ds(pl.multiple_of(t * 256, 256), 256)
            part[slot, :, columns] = lax.dot_general(
                both_grad[owner], w_both[columns, :], NT, preferred_element_type=F32
            ).astype(BF16)
            return inner

        lax.fori_loop(0, width // 256, tile, 0)
        for number, share in late:
            pl.when(turn == number)(reduce.shares[share].start)
        return carry

    lax.fori_loop(0, 8, unit, 0)
    store_activated = pltpu.make_async_copy(activated, activated_out, local.at[4])
    store_activated.start()

    def load_tile(t):
        columns = pl.ds(pl.multiple_of(t * 256, 256), 256)
        return pltpu.make_async_copy(
            cotangent_all.at[:, :, columns], cot_tile.at[t % 2], load_sem.at[2 + t % 2]
        )

    def store_both(t):
        columns = pl.ds(pl.multiple_of(t * 256, 256), 256)
        return pltpu.make_async_copy(
            stage_both.at[t % 2], both_sum.at[:, columns], load_sem.at[4 + t % 2]
        )

    tiles = width // 256
    count = groups * rows

    def down_tile(t, carry):
        columns = pl.ds(pl.multiple_of(t * 256, 256), 256)

        @pl.when(t < tiles - 1)
        def _():
            load_tile(t + 1).start()

        load_tile(t).wait()
        down_sum[:, columns] = lax.dot_general(
            activated[...].reshape(count, members * 128),
            cot_tile[t % 2].reshape(count, 256),
            TN,
            preferred_element_type=F32,
        ).astype(BF16)
        return carry

    store_down = pltpu.make_async_copy(down_sum, down_out, local.at[5])

    def weight_tile(t, carry):
        columns = pl.ds(pl.multiple_of(t * 256, 256), 256)

        @pl.when(t >= 2)
        def _():
            store_both(t - 2).wait()

        value = lax.dot_general(
            hidden_all[:, :, columns].reshape(count, 256),
            both_grad[...].reshape(count, members * 256),
            TN,
            preferred_element_type=F32,
        )
        for z in range(members):
            stage_both[t % 2, z] = value[:, z * 256 : z * 256 + 256].astype(BF16)
        store_both(t).start()
        return carry

    load_tile(0).start()
    reduce.add_side(0)
    reduce.corners[0].start()
    reduce.corners[1].start()
    lax.fori_loop(0, tiles, down_tile, 0)
    store_down.start()
    lax.fori_loop(0, 2, weight_tile, 0)
    reduce.middle()
    lax.fori_loop(2, tiles, weight_tile, 0)
    reduce.end()
    store_middle.wait()
    load_own.wait()
    sums[...] = jnp.zeros_like(sums)

    def body(span):
        change = norm_back_rows(reduce.rows_of(span), middle_grad[span, :], gain[...], sums, span)
        total = cotangent[span, :].astype(F32) + change
        middle_grad[span, :] = total
        branch[span, :] = total.astype(BF16)

    each_chunk(rows, body)
    for gather in gathers:
        gather.sent()
    reduce.finish()
    for t in (tiles - 2, tiles - 1):
        store_both(t).wait()
    store_down.wait()
    store_activated.wait()


def feed(mixed, w_out, tokens, cotangent_all, gate_all, w_up, w_down, cotangent, gain):
    groups, rows, width = cotangent_all.shape
    members = gate_all.shape[0]
    dma = pltpu.SemaphoreType.DMA
    units = members * 128
    return pl.pallas_call(
        feed_kernel,
        out_shape=(
            jax.ShapeDtypeStruct((rows, width), F32),
            jax.ShapeDtypeStruct((rows, width), F32),
            jax.ShapeDtypeStruct((rows, width), BF16),
            jax.ShapeDtypeStruct((8, width), F32),
            jax.ShapeDtypeStruct((groups, rows, units), BF16),
            jax.ShapeDtypeStruct((members, width, 256), BF16),
            jax.ShapeDtypeStruct((units, width), BF16),
            jax.ShapeDtypeStruct((members, width, LANES), BF16),
            jax.ShapeDtypeStruct((members, LANES, width), BF16),
        ),
        in_specs=[anywhere()] * 8 + [on_chip()],
        out_specs=(anywhere(),) + (on_chip(),) * 3 + (anywhere(),) * 5,
        scratch_shapes=[
            pltpu.VMEM((groups, rows, width), BF16),
            pltpu.VMEM((groups, rows, 2 * units), BF16),
        ]
        + reduce_scratch(rows, width)
        + [
            dma((10,)),
            dma((10,)),
            dma((10,)),
            dma((10,)),
            dma((13,)),
            dma((13,)),
            dma((13,)),
            dma((13,)),
            pltpu.VMEM((2, rows, width), BF16),
            pltpu.VMEM((2, groups, rows, 256), BF16),
            pltpu.VMEM((2, members, 256, 256), BF16),
            pltpu.VMEM((units, width), BF16),
            pltpu.VMEM((width, 2 * units), BF16),
            pltpu.VMEM((units, width), BF16),
            pltpu.VMEM((rows, width), BF16),
            pltpu.VMEM((groups, rows, units), BF16),
            dma((6 + 4 * members,)),
            dma((6,)),
            pltpu.VMEM((width, LANES), BF16),
            pltpu.VMEM((LANES, width), BF16),
            dma((4,)),
            dma((4,)),
            dma((4,)),
            dma((4,)),
            dma((5,)),
        ],
        compiler_params=remote_params(5, 63 * 1024 * 1024),
        cost_estimate=pl.CostEstimate(flops=0, bytes_accessed=400_000_000, transcendentals=0),
        name="feed",
    )(mixed, w_out, tokens, cotangent_all, gate_all, w_up, w_down, cotangent, gain)


def input_kernel(
    qkv_in, w_in, hidden_all, branch_all, mixed_in, tokens_in, middle_in, gain, sums_two,
    both_sum, both_in,
    result, gains, both_all, heads_all,
    part, from_side, from_corner, from_near, send, recv, sums,
    stage, arrive, send_h, recv_s, recv_h, own, plane_sums, column_sums, send_p, recv_p,
    weight_sum, row_tile, tile_sem, send_b, recv_b, send_t, recv_t, both_found, heads_own, local,
    mixed, tokens, middle_grad, fetch_sem, qkv_grad, w_qkv,
):
    me, z = lax.axis_index("dp"), lax.axis_index("mp")
    barrier = greet_all()
    count = qkv_grad.shape[0]
    tiles = tokens.shape[1] // 256
    outer = (z == 0) | (z == 3)

    def columns_of(t):
        return pl.ds(pl.multiple_of(lax.rem(t, tiles) * 256, 256), 256)

    def load(t, source):
        return pltpu.make_async_copy(
            source.at[:, :, columns_of(t)], row_tile.at[t % 2], tile_sem.at[t % 2]
        )

    own_part = pltpu.make_async_copy(both_sum.at[z], both_found.at[0], local.at[0])
    own_part.start()
    ways = [(outer, 1, 1), (outer, 2, 2)]
    ways += [(z == 1, 0, 1), (z == 1, 2, 2), (z == 1, 3, 3)]
    ways += [(z == 2, 0, 1), (z == 2, 1, 2), (z == 2, 3, 3)]

    def came(source, place):
        return pltpu.make_async_copy(both_in.at[source], both_found.at[place], local.at[place])

    for here, source, place in ways:
        pl.when(here)(came(source, place).start)

    @pl.when(outer)
    def _():
        both_found[3] = jnp.zeros_like(both_found[3])

    load(0, hidden_all).start()
    fetches = start_all(
        [
            pltpu.make_async_copy(source, target, fetch_sem.at[number])
            for number, (source, target) in enumerate(
                (
                    (qkv_in, qkv_grad),
                    (w_in, w_qkv),
                    (mixed_in, mixed),
                    (tokens_in, tokens),
                    (middle_in, middle_grad),
                )
            )
        ]
    )
    pl.semaphore_wait(barrier, 13)
    both = Gather(both_found.at[0], both_all, send_b, recv_b, local.at[4])

    def weight_tile(t, carry):
        @pl.when(t < tiles - 1)
        def _():
            load(t + 1, hidden_all).start()

        @pl.when((t >= tiles - 1) & (t < 2 * tiles - 1))
        def _():
            load(t + 1, branch_all).start()

        load(t, hidden_all).wait()

        @pl.when(t < tiles)
        def _():
            weight_sum[pl.ds(0, 768), columns_of(t)] = lax.dot_general(
                qkv_grad[...], row_tile[t % 2].reshape(count, 256), TN, preferred_element_type=F32
            ).astype(BF16)

        @pl.when(t >= tiles)
        def _():
            weight_sum[pl.ds(768, 256), columns_of(t)] = lax.dot_general(
                mixed[...], row_tile[t % 2].reshape(count, 256), TN, preferred_element_type=F32
            ).astype(BF16)

        return carry

    heads = Heads(weight_sum, stage, arrive, send_h, recv_s, recv_h)
    reduce = Reduce(qkv_grad, w_qkv, False, part, from_side, from_corner, from_near, send, recv)
    own_part.wait()
    for here, source, place in ways:
        pl.when(here)(came(source, place).wait)

    def add(span):
        value = both_found[0, span, :].astype(F32) + both_found[1, span, :].astype(F32)
        value = value + both_found[2, span, :].astype(F32) + both_found[3, span, :].astype(F32)
        both_found[0, span, :] = value.astype(BF16)

    each_chunk(both_found.shape[1], add)
    both.start()
    wait_all(fetches[:2])
    lax.fori_loop(0, tiles, weight_tile, 0)
    heads.start((0, 1, 2))
    wait_all(fetches[2:])
    lax.fori_loop(tiles, 2 * tiles, weight_tile, 0)
    heads.start((3,))
    both.pass_on()
    reduce.begin()
    heads.add((0, 1))
    reduce.middle()
    heads.add((2, 3))
    reduce.end()
    sums[...] = jnp.zeros_like(sums)

    def body(span):
        values = tokens[span, :].astype(F32)
        change = norm_back_rows(reduce.rows_of(span), values, gain[...], sums, span)
        result[span, :] = (middle_grad[span, :] + change).astype(BF16)

    each_chunk(result.shape[0], body)
    own[...] = jnp.concatenate(
        [
            jnp.sum(sums[...], axis=0, keepdims=True),
            jnp.sum(sums_two[...], axis=0, keepdims=True),
        ],
        axis=0,
    )
    swaps = swap_all(own, plane_sums, send_p, recv_p)
    for copy in swaps:
        copy.start()
    plane_sums[me] = own[...]
    heads.total(heads_own)
    gather = Gather(heads_own, heads_all, send_t, recv_t, local.at[5])
    gather.start()
    for copy in swaps:
        copy.wait()
    found = plane_sums[0]
    for other in range(1, 8):
        found = found + plane_sums[other]
    column_sums[z] = found
    passes = [
        to_mp(
            column_sums.at[z],
            column_sums.at[z],
            send_p.at[6 + step],
            recv_p.at[6 + step],
            lax.rem(z + step, 4),
        )
        for step in range(1, 4)
    ]
    for copy in passes:
        copy.start()
    both.finish()
    for copy in passes:
        copy.wait()
    gains[...] = (column_sums[0] + column_sums[1]) + (column_sums[2] + column_sums[3])
    gather.pass_on()
    heads.finish_send()
    reduce.finish()
    gather.finish()


def project_input(
    qkv_grad, w_qkv, hidden_all, branch_all, mixed, tokens, middle_grad, gain, sums_two,
    both_sum, both_in,
):
    rows, width = tokens.shape
    groups = hidden_all.shape[0]
    dma = pltpu.SemaphoreType.DMA
    shape = jax.ShapeDtypeStruct
    return pl.pallas_call(
        input_kernel,
        out_shape=(
            shape((rows, width), BF16),
            shape((2, width), F32),
            shape((groups, width, 256), BF16),
            shape((groups, 4 * HEAD_DIM, width // 2), BF16),
        ),
        in_specs=[anywhere()] * 7 + [on_chip()] * 2 + [anywhere()] * 2,
        out_specs=(on_chip(),) * 2 + (anywhere(),) * 2,
        scratch_shapes=reduce_scratch(rows, width)
        + [
            pltpu.VMEM((8, width), F32),
            pltpu.VMEM((2, 4, HEAD_DIM, width), BF16),
            pltpu.VMEM((3, 4, HEAD_DIM, width // 2), BF16),
            dma((16,)),
            dma((8,)),
            dma((12,)),
            pltpu.VMEM((2, width), F32),
            pltpu.VMEM((8, 2, width), F32),
            pltpu.VMEM((4, 2, width), F32),
            dma((10,)),
            dma((10,)),
            pltpu.VMEM((8 * LANES, width), BF16),
            pltpu.VMEM((2, groups, rows, 256), BF16),
            dma((2,)),
            dma((13,)),
            dma((13,)),
            dma((13,)),
            dma((13,)),
            pltpu.VMEM((4, width, 256), BF16),
            pltpu.VMEM((4 * HEAD_DIM, width // 2), BF16),
            dma((6,)),
            pltpu.VMEM(mixed.shape, BF16),
            pltpu.VMEM((rows, width), BF16),
            pltpu.VMEM((rows, width), F32),
            dma((5,)),
            pltpu.VMEM(qkv_grad.shape, BF16),
            pltpu.VMEM(w_qkv.shape, BF16),
        ],
        compiler_params=remote_params(6, 63 * 1024 * 1024),
        cost_estimate=pl.CostEstimate(flops=0, bytes_accessed=250_000_000, transcendentals=0),
        name="project_input",
    )(
        qkv_grad, w_qkv, hidden_all, branch_all, mixed, tokens, middle_grad, gain, sums_two,
        both_sum, both_in,
    )


def assemble_kernel(
    both, down, heads, order_column, output_b, input_b,
    output, inputs, query, keys, values, project, gate, upward, down_out,
):
    for d in range(both.shape[0]):
        gate[:, d * 128 : d * 128 + 128] = both[d, :, :128].astype(F32)
        upward[:, d * 128 : d * 128 + 128] = both[d, :, 128:].astype(F32)
    down_out[...] = down[0].astype(F32)
    for kind, out in enumerate((query, keys, values, project)):
        out[...] = heads[0, kind].astype(F32)
    place = lax.broadcasted_iota(jnp.int32, (order_column.shape[0], output_b.shape[0]), 1)
    unsort = (place.astype(F32) == order_column[...]).astype(BF16)
    output[...] = jnp.dot(unsort, output_b[...], preferred_element_type=F32).astype(BF16)
    inputs[...] = jnp.dot(unsort, input_b[...], preferred_element_type=F32).astype(BF16)


def assemble(both, down, heads, order_column, output_b, input_b):
    groups, width, wide = both.shape
    rows = output_b.shape[0]
    units = down.shape[1]
    chips = groups // 2
    columns = heads.shape[3]
    row_tile, tile = rows // groups, width // groups
    shape = jax.ShapeDtypeStruct
    head = shape((chips * HEAD_DIM, 2 * columns), F32)
    head_spec = pl.BlockSpec((HEAD_DIM, columns), lambda i: (i // 2, i % 2))
    wide_spec = pl.BlockSpec((tile, groups * units), lambda i: (i, 0))
    row_spec = pl.BlockSpec((row_tile, width), lambda i: (i, 0))
    whole_spec = pl.BlockSpec((rows, width), lambda i: (0, 0))
    return pl.pallas_call(
        assemble_kernel,
        grid=(groups,),
        out_shape=(
            shape((rows, width), BF16),
            shape((rows, width), BF16),
            head,
            head,
            head,
            head,
            shape((width, groups * units), F32),
            shape((width, groups * units), F32),
            shape((groups * units, width), F32),
        ),
        in_specs=[
            pl.BlockSpec((groups, tile, wide), lambda i: (0, i, 0)),
            pl.BlockSpec((1, units, width), lambda i: (i, 0, 0)),
            pl.BlockSpec((1, 4, HEAD_DIM, columns), lambda i: (i, 0, 0, 0)),
            pl.BlockSpec((row_tile, 1), lambda i: (i, 0)),
            whole_spec,
            whole_spec,
        ],
        out_specs=(
            row_spec, row_spec, head_spec, head_spec, head_spec, head_spec, wide_spec, wide_spec,
            pl.BlockSpec((units, width), lambda i: (i, 0)),
        ),
        compiler_params=pltpu.CompilerParams(vmem_limit_bytes=VMEM_LIMIT),
        cost_estimate=pl.CostEstimate(flops=0, bytes_accessed=58_000_000, transcendentals=0),
        name="assemble",
    )(both, down, heads, order_column, output_b, input_b)


def swapped(
    tokens, cotangent, route, lengths, key_mask, norm1_gain, norm2_gain,
    w_query, w_key, w_value, w_out, w_gate, w_up, w_down,
):
    groups = lax.axis_size("dp")
    members = lax.axis_size("mp")
    me = lax.axis_index("dp")
    z = lax.axis_index("mp")
    rows, width = tokens.shape
    bucket = rows // groups
    units = w_down.shape[0] // groups

    target = route // TOK_DEV
    earlier = jnp.arange(rows, dtype=jnp.int32)
    same = (target[:, None] == target[None, :]) & (earlier[None, :] < earlier[:, None])
    send_at = target * bucket + jnp.sum(same.astype(jnp.int32), axis=1)
    sorting = send_at[None, :] == earlier[:, None]
    slots_own = jnp.sum(jnp.where(sorting, (route % rows)[None, :], 0), axis=1)

    mask_window = lax.dynamic_slice_in_dim(
        jnp.concatenate([jnp.zeros((WINDOW,), jnp.int32), key_mask]), z * rows, rows + WINDOW
    )
    slot_rows = jnp.pad(slots_own.reshape(groups, bucket).T, ((0, 0), (0, LANES - groups)))
    mask_rows = jnp.pad(mask_window, (0, 4 * LANES - rows - WINDOW)).reshape(4, LANES)
    length_rows = jnp.pad(lengths, ((0, 3), (0, LANES - lengths.shape[1])))
    notes = jnp.concatenate([slot_rows, mask_rows, length_rows], axis=0).astype(F32)

    count = groups * rows
    scale = HEAD_DIM ** (-0.5)
    (
        hidden_one,
        w_qkv,
        w_proj,
        notes_all,
        gate_all,
        mixed,
        kept,
        tokens_b,
        cotangent_b,
        cotangent_all,
    ) = attend_ahead(
        tokens,
        cotangent,
        send_at.astype(F32)[None],
        norm1_gain[None],
        notes,
        w_query.T,
        w_key.T,
        w_value.T,
        w_out,
        w_gate,
        scale,
    )
    mixed = mixed.reshape(count, 2 * LANES)
    middle, middle_grad, branch, sums_two, activated, both_sum, down_sum, _, down_all = feed(
        mixed.reshape(groups, rows, 2 * LANES),
        w_proj,
        tokens_b,
        cotangent_all,
        gate_all,
        w_up,
        w_down,
        cotangent_b,
        norm2_gain[None],
    )
    qkv_grad, output_rows, branch_all, both_in, down_whole = attend_back(
        branch,
        notes_all,
        kept,
        w_proj,
        activated.reshape(count, units * members),
        down_all.reshape(members * units, width),
        middle,
        both_sum,
        down_sum,
        scale,
    )
    qkv_grad = qkv_grad.reshape(count, 6 * LANES)
    input_rows, gain_sums, both_whole, heads_whole = project_input(
        qkv_grad,
        w_qkv,
        hidden_one,
        branch_all,
        mixed,
        tokens_b,
        middle_grad,
        norm1_gain[None],
        sums_two,
        both_sum,
        both_in,
    )
    (
        output,
        input_grad,
        query_grad,
        key_grad,
        value_grad,
        proj_grad,
        gate_grad,
        up_grad,
        down_grad,
    ) = assemble(
        both_whole,
        down_whole,
        heads_whole.reshape(groups, 4, HEAD_DIM, width // 2),
        send_at.astype(F32)[:, None],
        output_rows,
        input_rows,
    )
    return (
        output,
        input_grad,
        gain_sums[0],
        gain_sums[1],
        query_grad.T,
        key_grad.T,
        value_grad.T,
        proj_grad,
        gate_grad,
        up_grad,
        down_grad,
    )


def solution(mesh):
    in_specs = (
        P(("dp", "mp"), None),
        P(("dp", "mp"), None),
        P(("dp", "mp")),
        P("dp", None),
        P("dp"),
        P(),
        P(),
        P(None, "mp"),
        P(None, "mp"),
        P(None, "mp"),
        P("mp", None),
        P(None, "mp"),
        P(None, "mp"),
        P("mp", None),
    )
    out_specs = (
        P(("dp", "mp"), None),
        P(("dp", "mp"), None),
        P(),
        P(),
        P(None, "mp"),
        P(None, "mp"),
        P(None, "mp"),
        P("mp", None),
        P(None, "mp"),
        P(None, "mp"),
        P("mp", None),
    )
    body = swapped if (mesh.shape["dp"], mesh.shape["mp"]) == (8, 4) else local
    return jax.shard_map(body, mesh=mesh, in_specs=in_specs, out_specs=out_specs, check_vma=False)
```

```python
import functools

import jax
import jax.numpy as jnp
from jax import lax
from jax.experimental import pallas as pl
from jax.experimental.pallas import tpu as pltpu
from jax.sharding import PartitionSpec as P

HEAD_DIM = 112
WINDOW = 64
TOK_DEV = 1536


EPSILON = 1e-05
MASKED = 1e30


def norm_rows(values):
    inverse = lax.rsqrt(jnp.mean(values * values, axis=-1, keepdims=True) + EPSILON)
    return (values * inverse, inverse)


def norm_back(gradient, normed, inverse, norm_gain):
    scaled = gradient * norm_gain
    result = inverse * (scaled - normed * jnp.mean(scaled * normed, axis=-1, keepdims=True))
    return (result, jnp.sum(gradient * normed, axis=0))


def padded(values, filler):
    front = jnp.full((WINDOW,) + values.shape[1:], filler, values.dtype)
    return jnp.concatenate([front, values], axis=0)


def block_scores(query_block, key_block, query_seg, key_seg, key_flag, first_row, score_scale):
    query_pos = first_row + jnp.arange(query_block.shape[0], dtype=jnp.int32)
    key_pos = first_row - WINDOW + jnp.arange(key_block.shape[0], dtype=jnp.int32)
    distance = query_pos[:, None] - key_pos[None, :]
    allowed = (distance >= 0) & (distance < WINDOW) & (query_seg[:, None] == key_seg[None, :])
    allowed = allowed & ((key_flag[None, :] == 1) | (distance == 0))
    raw_scores = (
        jnp.einsum("qhd,khd->hqk", query_block, key_block, preferred_element_type=jnp.float32)
        * score_scale
    )
    return jnp.where(allowed[None], raw_scores, -MASKED)


def block_inputs(query, key_pad, value_pad, segment, seg_pad, live_pad, first_row, block_rows):
    key_span = block_rows + WINDOW
    return (
        lax.dynamic_slice_in_dim(query, first_row, block_rows, 0),
        lax.dynamic_slice_in_dim(key_pad, first_row, key_span, 0),
        lax.dynamic_slice_in_dim(value_pad, first_row, key_span, 0),
        lax.dynamic_slice_in_dim(segment, first_row, block_rows, 0),
        lax.dynamic_slice_in_dim(seg_pad, first_row, key_span, 0),
        lax.dynamic_slice_in_dim(live_pad, first_row, key_span, 0),
    )


def attend_forward(query, key_all, value_all, segment, key_live):
    token_count, head_count, head_width = query.shape
    block_rows = min(512, token_count)
    score_scale = head_width ** (-0.5)
    key_pad = padded(key_all, 0.0)
    value_pad = padded(value_all, 0.0)
    seg_pad = padded(segment, -1)
    live_pad = padded(key_live, 0)

    def one_block(running, block_index):
        first_row = block_index * block_rows
        query_block, key_block, value_block, query_seg, key_seg, key_flag = block_inputs(
            query, key_pad, value_pad, segment, seg_pad, live_pad, first_row, block_rows
        )
        scores = block_scores(
            query_block, key_block, query_seg, key_seg, key_flag, first_row, score_scale
        )
        row_max = jnp.max(scores, axis=-1, keepdims=True)
        weights = jnp.exp(scores - row_max)
        denominator = jnp.sum(weights, axis=-1, keepdims=True)
        chances = (weights / denominator).astype(jnp.bfloat16)
        mixed = jnp.einsum("hqk,khd->qhd", chances, value_block, preferred_element_type=jnp.float32)
        return (
            running,
            (mixed.astype(jnp.bfloat16), row_max[..., 0] + jnp.log(denominator[..., 0])),
        )

    _, (mixed, logsum) = lax.scan(
        one_block, jnp.zeros((), jnp.int32), jnp.arange(token_count // block_rows, dtype=jnp.int32)
    )
    return (mixed.reshape(token_count, head_count * head_width), logsum)


def attend_backward(query, key_all, value_all, segment, key_live, logsum, mixed_grad):
    token_count, head_count, head_width = query.shape
    block_rows = min(512, token_count)
    key_span = block_rows + WINDOW
    score_scale = head_width ** (-0.5)
    key_pad = padded(key_all, 0.0)
    value_pad = padded(value_all, 0.0)
    seg_pad = padded(segment, -1)
    live_pad = padded(key_live, 0)

    def one_block(running, inputs):
        key_grad, value_grad = running
        block_index, block_logsum = inputs
        first_row = block_index * block_rows
        query_block, key_block, value_block, query_seg, key_seg, key_flag = block_inputs(
            query, key_pad, value_pad, segment, seg_pad, live_pad, first_row, block_rows
        )
        grad_block = lax.dynamic_slice_in_dim(mixed_grad, first_row, block_rows, 0)
        scores = block_scores(
            query_block, key_block, query_seg, key_seg, key_flag, first_row, score_scale
        )
        chances = jnp.exp(scores - block_logsum[..., None])
        chance_grad = jnp.einsum(
            "qhd,khd->hqk", grad_block, value_block, preferred_element_type=jnp.float32
        )
        row_dot = jnp.sum(chances * chance_grad, axis=-1, keepdims=True)
        score_grad = (chances * (chance_grad - row_dot)).astype(jnp.bfloat16)
        query_grad = (
            jnp.einsum("hqk,khd->qhd", score_grad, key_block, preferred_element_type=jnp.float32)
            * score_scale
        )
        key_part = (
            jnp.einsum("hqk,qhd->khd", score_grad, query_block, preferred_element_type=jnp.float32)
            * score_scale
        )
        value_part = jnp.einsum(
            "hqk,qhd->khd",
            chances.astype(jnp.bfloat16),
            grad_block,
            preferred_element_type=jnp.float32,
        )
        key_grad = lax.dynamic_update_slice_in_dim(
            key_grad,
            lax.dynamic_slice_in_dim(key_grad, first_row, key_span, 0) + key_part,
            first_row,
            0,
        )
        value_grad = lax.dynamic_update_slice_in_dim(
            value_grad,
            lax.dynamic_slice_in_dim(value_grad, first_row, key_span, 0) + value_part,
            first_row,
            0,
        )
        return ((key_grad, value_grad), query_grad)

    empty_grad = jnp.zeros((token_count + WINDOW, head_count, head_width), jnp.float32)
    (key_grad, value_grad), query_grad = lax.scan(
        one_block,
        (empty_grad, empty_grad),
        (jnp.arange(token_count // block_rows, dtype=jnp.int32), logsum),
    )
    flat_width = head_count * head_width
    return (
        query_grad.reshape(token_count, flat_width).astype(jnp.bfloat16),
        key_grad[WINDOW:].reshape(token_count, flat_width).astype(jnp.bfloat16),
        value_grad[WINDOW:].reshape(token_count, flat_width).astype(jnp.bfloat16),
    )


def local(
    tokens,
    cotangent,
    route,
    lengths,
    key_mask,
    norm1_gain,
    norm2_gain,
    w_query,
    w_key,
    w_value,
    w_out,
    w_gate,
    w_up,
    w_down,
):
    groups = lax.axis_size("dp")
    members = lax.axis_size("mp")
    member = lax.axis_index("mp")
    local_rows = tokens.shape[0]
    group_rows = local_rows * members
    bucket = local_rows // groups
    target = route // TOK_DEV
    chosen = (target[:, None] == jnp.arange(groups, dtype=jnp.int32)[None, :]).astype(jnp.int32)
    ranking = jnp.sum((jnp.cumsum(chosen, axis=0) - chosen) * chosen, axis=1)
    send_at = target * bucket + ranking
    arrival, arrival_grad, arrival_slot = (
        lax.all_to_all(
            jnp.zeros_like(tokens).at[send_at].set(tokens),
            "dp",
            split_axis=0,
            concat_axis=0,
            tiled=True,
        ),
        lax.all_to_all(
            jnp.zeros_like(cotangent).at[send_at].set(cotangent),
            "dp",
            split_axis=0,
            concat_axis=0,
            tiled=True,
        ),
        lax.all_to_all(
            jnp.zeros_like(route).at[send_at].set(route % local_rows),
            "dp",
            split_axis=0,
            concat_axis=0,
            tiled=True,
        ),
    )
    token_rows = jnp.zeros_like(arrival).at[arrival_slot].set(arrival)
    grad_rows = jnp.zeros_like(arrival_grad).at[arrival_slot].set(arrival_grad)
    seq_ends = jnp.cumsum(lengths[0])
    positions = jnp.arange(group_rows, dtype=jnp.int32)
    segment = jnp.sum((positions[:, None] >= seq_ends[None, :]).astype(jnp.int32), axis=1)
    input_rows = token_rows.astype(jnp.float32)
    normed_one, inverse_one = norm_rows(input_rows)
    leading_all, grad_all = (
        lax.all_gather(token_rows, "mp", axis=0, tiled=True),
        lax.all_gather(grad_rows, "mp", axis=0, tiled=True),
    )
    input_all = leading_all.astype(jnp.float32)
    normed_all, _ = norm_rows(input_all)
    hidden_one = (normed_all * norm1_gain).astype(jnp.bfloat16)
    head_count = w_query.shape[1] // HEAD_DIM
    query = jnp.dot(hidden_one, w_query, preferred_element_type=jnp.float32).astype(jnp.bfloat16)
    keys = jnp.dot(hidden_one, w_key, preferred_element_type=jnp.float32).astype(jnp.bfloat16)
    values = jnp.dot(hidden_one, w_value, preferred_element_type=jnp.float32).astype(jnp.bfloat16)
    query_heads = query.reshape(group_rows, head_count, HEAD_DIM)
    key_heads = keys.reshape(group_rows, head_count, HEAD_DIM)
    value_heads = values.reshape(group_rows, head_count, HEAD_DIM)
    mixed_flat, logsum = attend_forward(query_heads, key_heads, value_heads, segment, key_mask)
    attention_all = lax.psum(jnp.dot(mixed_flat, w_out, preferred_element_type=jnp.float32), "mp")
    middle_all = input_all + attention_all
    middle_rows = lax.dynamic_slice_in_dim(middle_all, member * local_rows, local_rows, 0)
    normed_mid, _ = norm_rows(middle_all)
    hidden_two = (normed_mid * norm2_gain).astype(jnp.bfloat16)
    normed_two, inverse_two = norm_rows(middle_rows)
    gate_value = jnp.dot(hidden_two, w_gate, preferred_element_type=jnp.float32)
    upward = jnp.dot(hidden_two, w_up, preferred_element_type=jnp.float32)
    sigmoid = jax.nn.sigmoid(gate_value)
    activated = (gate_value * sigmoid * upward).astype(jnp.bfloat16)
    out_rows = middle_rows + lax.psum_scatter(
        jnp.dot(activated, w_down, preferred_element_type=jnp.float32).astype(jnp.bfloat16),
        "mp",
        scatter_dimension=0,
        tiled=True,
    ).astype(jnp.float32)
    activated_grad = jnp.einsum("td,fd->tf", grad_all, w_down, preferred_element_type=jnp.float32)
    gate_grad = (activated_grad * upward * sigmoid * (1.0 + gate_value * (1.0 - sigmoid))).astype(
        jnp.bfloat16
    )
    upward_grad = (activated_grad * gate_value * sigmoid).astype(jnp.bfloat16)
    down_sum = jnp.einsum("tf,td->fd", activated, grad_all, preferred_element_type=jnp.float32)
    gate_sum = jnp.einsum("td,tf->df", hidden_two, gate_grad, preferred_element_type=jnp.float32)
    upward_sum = jnp.einsum(
        "td,tf->df", hidden_two, upward_grad, preferred_element_type=jnp.float32
    )
    hidden_two_grad = lax.psum_scatter(
        jnp.einsum("tf,df->td", gate_grad, w_gate, preferred_element_type=jnp.float32)
        + jnp.einsum("tf,df->td", upward_grad, w_up, preferred_element_type=jnp.float32),
        "mp",
        scatter_dimension=0,
        tiled=True,
    )
    norm_part_two, gain_two_grad = norm_back(hidden_two_grad, normed_two, inverse_two, norm2_gain)
    middle_grad = grad_rows.astype(jnp.float32) + norm_part_two
    branch_all = lax.all_gather(middle_grad.astype(jnp.bfloat16), "mp", axis=0, tiled=True)
    output_sum = jnp.einsum("tc,td->cd", mixed_flat, branch_all, preferred_element_type=jnp.float32)
    mixed_grad = jnp.einsum(
        "td,cd->tc", branch_all, w_out, preferred_element_type=jnp.float32
    ).astype(jnp.bfloat16)
    query_grad, key_grad, value_grad = attend_backward(
        query_heads,
        key_heads,
        value_heads,
        segment,
        key_mask,
        logsum,
        mixed_grad.reshape(group_rows, head_count, HEAD_DIM),
    )
    query_sum = jnp.einsum("td,tc->dc", hidden_one, query_grad, preferred_element_type=jnp.float32)
    key_sum = jnp.einsum("td,tc->dc", hidden_one, key_grad, preferred_element_type=jnp.float32)
    value_sum = jnp.einsum("td,tc->dc", hidden_one, value_grad, preferred_element_type=jnp.float32)
    hidden_one_grad = lax.psum_scatter(
        (
            jnp.einsum("tc,dc->td", query_grad, w_query, preferred_element_type=jnp.float32)
            + jnp.einsum("tc,dc->td", key_grad, w_key, preferred_element_type=jnp.float32)
            + jnp.einsum("tc,dc->td", value_grad, w_value, preferred_element_type=jnp.float32)
        ).astype(jnp.bfloat16),
        "mp",
        scatter_dimension=0,
        tiled=True,
    ).astype(jnp.float32)
    norm_part_one, gain_one_grad = norm_back(hidden_one_grad, normed_one, inverse_one, norm1_gain)
    input_grad = middle_grad + norm_part_one
    gain_one_sum, gain_two_sum = lax.psum((gain_one_grad, gain_two_grad), ("dp", "mp"))
    weight_sums = (
        lax.psum(query_sum.astype(jnp.bfloat16), "dp").astype(jnp.float32),
        lax.psum(key_sum.astype(jnp.bfloat16), "dp").astype(jnp.float32),
        lax.psum(value_sum.astype(jnp.bfloat16), "dp").astype(jnp.float32),
        lax.psum(output_sum.astype(jnp.bfloat16), "dp").astype(jnp.float32),
        lax.psum(gate_sum.astype(jnp.bfloat16), "dp").astype(jnp.float32),
        lax.psum(upward_sum.astype(jnp.bfloat16), "dp").astype(jnp.float32),
        lax.psum(down_sum.astype(jnp.bfloat16), "dp").astype(jnp.float32),
    )
    back_out, back_grad = (
        lax.all_to_all(
            out_rows.astype(jnp.bfloat16)[arrival_slot],
            "dp",
            split_axis=0,
            concat_axis=0,
            tiled=True,
        ),
        lax.all_to_all(
            input_grad.astype(jnp.bfloat16)[arrival_slot],
            "dp",
            split_axis=0,
            concat_axis=0,
            tiled=True,
        ),
    )
    return (
        back_out[send_at],
        back_grad[send_at],
        gain_one_sum,
        gain_two_sum,
        weight_sums[0],
        weight_sums[1],
        weight_sums[2],
        weight_sums[3],
        weight_sums[4],
        weight_sums[5],
        weight_sums[6],
    )


MESH = pl.DeviceIdType.MESH
LANES = 128
F32 = jnp.float32
BF16 = jnp.bfloat16
VMEM_LIMIT = 56 * 1024 * 1024


def plane():
    me = lax.axis_index("dp")
    side = me + 1 - 2 * lax.rem(me, 2)
    over_x = me + 2 - 4 * lax.rem(lax.div(me, 2), 2)
    over_y = me + 4 - 8 * lax.rem(lax.div(me, 4), 2)
    corner = over_x + 4 - 8 * lax.rem(lax.div(over_x, 4), 2)
    return (me, side, over_x, over_y, corner)


def to_dp(source, target, send_sem, recv_sem, index):
    return pltpu.make_async_remote_copy(
        src_ref=source,
        dst_ref=target,
        send_sem=send_sem,
        recv_sem=recv_sem,
        device_id={"dp": index},
        device_id_type=MESH,
    )


def to_mp(source, target, send_sem, recv_sem, index):
    return pltpu.make_async_remote_copy(
        src_ref=source,
        dst_ref=target,
        send_sem=send_sem,
        recv_sem=recv_sem,
        device_id={"mp": index},
        device_id_type=MESH,
    )


def owner_at(turn):
    me, side, over_x, over_y, _ = plane()
    block = turn // 2
    near = ((block + 1) // 2) % 2
    far = block // 3
    second = turn % 2
    other = (1 - near) * second + (block // 2) * near
    owner = me + (near * (1 - second) + far) * (over_x - me)
    return owner + (near * second + far) * (over_y - me) + other * (side - me)


ARRIVALS = (
    (1, (4,)),
    (2, (0, 1, 2)),
    (3, (3,)),
    (4, (6, 9)),
    (5, (8, 10)),
    (6, (5, 7)),
    (7, (11, 12)),
)


class Gather:
    AFTER = {0: (5, 6), 1: (7, 8), 2: (9,), 3: (10,), 5: (11,), 7: (12,)}

    def __init__(self, own, out, send, recv, local=None):
        me, side, over_x, over_y, corner = plane()
        half = out.shape[1] // 2
        low, high = pl.ds(0, half), pl.ds(half, half)
        self.keep = None if own is None else pltpu.make_async_copy(own, out.at[me], local)
        own = out.at[me] if own is None else own

        def hop(number, source, target, index):
            return to_dp(source, target, send.at[number], recv.at[number], index)

        def onward(number, owner, part, index):
            place = out.at[owner, part]
            return hop(number, place, place, index)

        self.copies = [
            hop(0, own.at[low], out.at[me, low], over_x),
            hop(1, own.at[high], out.at[me, high], over_y),
            hop(2, own.at[high], out.at[me, high], over_x),
            hop(3, own.at[low], out.at[me, low], over_y),
            hop(4, own, out.at[me], side),
            onward(5, over_x, low, over_y),
            onward(6, over_x, low, side),
            onward(7, over_y, high, over_x),
            onward(8, over_y, high, side),
            onward(9, over_x, high, side),
            onward(10, over_y, low, side),
            onward(11, corner, low, side),
            onward(12, corner, high, side),
        ]

    def start(self):
        for number in range(5):
            self.copies[number].start()
        if self.keep is not None:
            self.keep.start()

    def arrive(self, *numbers):
        for number in numbers:
            self.copies[number].wait_recv()
            for later in self.AFTER.get(number, ()):
                self.copies[later].start()

    def pass_on(self):
        self.arrive(0, 1, 2, 3)

    def sent(self):
        for copy in self.copies:
            copy.wait_send()
        if self.keep is not None:
            self.keep.wait()

    def finish(self):
        self.arrive(5, 7, 4, 6, 8, 9, 10, 11, 12)
        self.sent()


def greet_all():
    barrier = pltpu.get_barrier_semaphore()
    me, z = lax.axis_index("dp"), lax.axis_index("mp")
    for step in range(1, 8):
        pl.semaphore_signal(
            barrier, inc=1, device_id={"dp": lax.rem(me + step, 8)}, device_id_type=MESH
        )
    core = lax.rem(me, 2)
    for step in range(1, 4):
        for other in (me, me + 1 - 2 * core):
            pl.semaphore_signal(
                barrier,
                inc=1,
                device_id={"dp": other, "mp": lax.rem(z + step, 4)},
                device_id_type=MESH,
            )
    return barrier


def start_all(copies):
    for copy in copies:
        copy.start()
    return copies


def wait_all(copies):
    for copy in copies:
        copy.wait()


def swap_all(source, target, send, recv):
    me = lax.axis_index("dp")
    return [
        to_dp(source, target.at[me], send.at[step - 1], recv.at[step - 1], lax.rem(me + step, 8))
        for step in range(1, 8)
    ]


class Spread:
    def __init__(self, share, w_qkv, w_out, send, recv, local):
        me, z = lax.axis_index("dp"), lax.axis_index("mp")
        core = lax.rem(me, 2)
        self.place = z + core * (3 - 2 * z)
        self.send, self.recv, self.local = send, recv, local
        self.shares = [share.at[0], share.at[1], share.at[2], share.at[3]]
        self.slots = (core, 1 - core)
        self.core = core
        self.w_qkv, self.w_out = w_qkv, w_out

    def target(self, which, piece):
        slot = self.slots[which]
        block = slot if piece == 3 else 2 * piece + slot
        rows = pl.ds(pl.multiple_of(block * LANES, LANES), HEAD_DIM)
        return (self.w_out if piece == 3 else self.w_qkv).at[rows]

    def hop(self, which, piece, number, place, own):
        source = self.shares[piece] if own else self.target(which, piece)
        z = place + self.core * (3 - 2 * place)
        return to_mp(
            source,
            self.target(which, piece),
            self.send.at[number * 4 + piece],
            self.recv.at[which * 4 + piece],
            z,
        )

    def keep(self, which, piece):
        return pltpu.make_async_copy(
            self.shares[piece], self.target(which, piece), self.local.at[piece]
        )

    def start(self, pieces):
        @pl.when(self.place == 0)
        def _():
            for piece in pieces:
                self.hop(0, piece, 0, 1, True).start()
                self.keep(0, piece).start()

        @pl.when(self.place == 1)
        def _():
            for piece in pieces:
                self.hop(1, piece, 0, 0, True).start()
                self.hop(1, piece, 1, 2, True).start()
                self.keep(1, piece).start()

    def pass_on(self, pieces):
        @pl.when(self.place == 1)
        def _():
            for piece in pieces:
                self.hop(0, piece, 2, 2, False).wait_recv()
                self.hop(0, piece, 2, 2, False).start()

        @pl.when(self.place == 2)
        def _():
            for which in (1, 0):
                for piece in pieces:
                    self.hop(which, piece, which, 3, False).wait_recv()
                    self.hop(which, piece, which, 3, False).start()

    def finish(self, pieces):
        @pl.when(self.place == 0)
        def _():
            for piece in pieces:
                self.hop(1, piece, 0, 1, False).wait_recv()
                self.hop(0, piece, 0, 1, True).wait_send()
                self.keep(0, piece).wait()

        @pl.when(self.place == 1)
        def _():
            for piece in pieces:
                self.hop(1, piece, 0, 0, True).wait_send()
                self.hop(1, piece, 1, 2, True).wait_send()
                self.hop(0, piece, 2, 2, False).wait_send()
                self.keep(1, piece).wait()

        @pl.when(self.place == 2)
        def _():
            for piece in pieces:
                for which in (1, 0):
                    self.hop(which, piece, which, 3, False).wait_send()

        @pl.when(self.place == 3)
        def _():
            for piece in pieces:
                for which in (1, 0):
                    self.hop(which, piece, which, 3, False).wait_recv()


class Column:
    def __init__(self, own, out, send, recv, local):
        z = lax.axis_index("mp")
        self.z, self.own, self.out, self.send, self.recv = z, own, out, send, recv
        self.outer = (z == 0) | (z == 3)
        near = 1 + lax.div(z, 3)
        self.from_outer = (near, 3 - near)
        self.edge = 3 * (z - 1)
        self.from_inner = (3 - z, 3 - self.edge, self.edge)
        self.keep = pltpu.make_async_copy(own, out.at[z], local)

    def straight(self, number, target):
        return to_mp(
            self.own, self.out.at[self.z], self.send.at[number], self.recv.at[self.z], target
        )

    def onward(self):
        far = 3 - self.edge
        return to_mp(
            self.out.at[far], self.out.at[far], self.send.at[3], self.recv.at[far], self.edge
        )

    def came(self, source):
        return to_mp(
            self.own, self.out.at[source], self.send.at[0], self.recv.at[source], source
        ).wait_recv

    def start(self):
        self.keep.start()

        @pl.when(self.outer)
        def _():
            for number, target in enumerate(self.from_outer):
                self.straight(number, target).start()

        @pl.when(jnp.logical_not(self.outer))
        def _():
            for number, target in enumerate(self.from_inner):
                self.straight(number, target).start()

    def pass_on(self):
        @pl.when(jnp.logical_not(self.outer))
        def _():
            self.came(3 - self.edge)()
            self.onward().start()

    def finish(self):
        @pl.when(self.outer)
        def _():
            for source in (1, 2):
                self.came(source)()
            self.came(3 - self.z)()
            for number, target in enumerate(self.from_outer):
                self.straight(number, target).wait_send()

        @pl.when(jnp.logical_not(self.outer))
        def _():
            self.came(3 - self.z)()
            self.came(self.edge)()
            for number, target in enumerate(self.from_inner):
                self.straight(number, target).wait_send()
            self.onward().wait_send()

        self.keep.wait()


def anywhere():
    return pl.BlockSpec(memory_space=pl.ANY)


def on_chip():
    return pl.BlockSpec(memory_space=pltpu.VMEM)


def remote_params(number, limit=VMEM_LIMIT):
    return pltpu.CompilerParams(
        collective_id=number, has_side_effects=True, vmem_limit_bytes=limit
    )


def hot_of(notes, k, size):
    own = notes[:, 0:48, :].reshape(size, LANES)
    lane = lax.broadcasted_iota(jnp.int32, (size, LANES), 1)
    slot = jnp.sum(jnp.where(lane == k, own, 0.0), axis=1, keepdims=True)
    return (lax.broadcasted_iota(jnp.int32, (size, size), 1).astype(F32) == slot).astype(BF16)


def block_mask(notes, k, block, z, rows):
    position = rows * z + block * 128 + lax.broadcasted_iota(jnp.int32, (128, 1), 0)
    position = position.astype(F32)
    first_end = notes[k, 52:53, 0:1]
    second_end = first_end + notes[k, 52:53, 1:2]
    begin = jnp.where(position >= first_end, first_end, 0.0)
    begin = jnp.where(position >= second_end, second_end, begin)
    column = lax.broadcasted_iota(jnp.int32, (128, 192), 1)
    distance = 64 + lax.broadcasted_iota(jnp.int32, (128, 192), 0) - column
    key_position = (rows * z + block * 128 - 64 + column).astype(F32)
    live = jnp.concatenate(
        [notes[k, 48 + block : 49 + block, :], notes[k, 49 + block : 50 + block, 0:64]], axis=1
    )
    allowed = (distance >= 0) & (distance < WINDOW) & (key_position >= begin)
    return allowed & ((live == 1.0) | (distance == 0))


NT = (((1,), (1,)), ((), ()))
TN = (((0,), (0,)), ((), ()))


def forward_kernel(
    tokens, cotangent, order_row, gain, notes, query, keys, values, project, gate,
    hidden_out, w_qkv_out, w_out, notes_all, gate_all, mixed_out, kept_out, tokens_out, cotangent_out,
    cotangent_all,
    hidden_all, qkv, share, gate_own, w_qkv, mixed, kept, tokens_b, cotangent_b,
    send, recv, send_a, recv_a, send_g, recv_g, send_w, recv_w, send_n, recv_n, send_c, recv_c,
    local, out_sem, store_sem, *, scale,
):
    groups, rows, width = hidden_all.shape
    me, z = lax.axis_index("dp"), lax.axis_index("mp")
    members = lax.axis_size("mp")
    barrier = greet_all()
    head = pl.ds(pl.multiple_of(lax.div(me, 2) * HEAD_DIM, 16), HEAD_DIM)
    units = pl.ds(pl.multiple_of(me * LANES, LANES), LANES)
    loads = [
        pltpu.make_async_copy(source.at[head], share.at[piece], local.at[piece])
        for piece, source in enumerate((query, keys, values, project))
    ]
    loads.append(pltpu.make_async_copy(gate.at[:, units], gate_own, local.at[4]))
    for copy in loads:
        copy.start()
    none = jnp.zeros((LANES - HEAD_DIM, width), BF16)
    for block in range(6):
        w_qkv[block * LANES + HEAD_DIM : block * LANES + LANES, :] = none
    for block in range(2):
        w_out[block * LANES + HEAD_DIM : block * LANES + LANES, :] = none

    place = lax.broadcasted_iota(jnp.int32, (rows, rows), 0).astype(F32)
    sort = (place == order_row[...]).astype(BF16)
    tokens_b[...] = jnp.dot(sort, tokens[...], preferred_element_type=F32).astype(BF16)

    def normalise(span):
        value = tokens_b[span, :].astype(F32)
        inverse = lax.rsqrt(mean_rows(value * value) + EPSILON)
        hidden_all[me, span, :] = (value * inverse * gain[...].reshape(1, -1)).astype(BF16)

    each_chunk(rows, normalise)
    notes_all[me] = notes[...]
    stores = start_all([pltpu.make_async_copy(tokens_b, tokens_out, store_sem.at[0])])
    pl.semaphore_wait(barrier, 13)
    gather = Gather(None, hidden_all, send_a, recv_a)
    gather.start()
    swaps = swap_all(notes, notes_all, send_n, recv_n)
    for copy in swaps:
        copy.start()
    for copy in loads[:4]:
        copy.wait()
    spread = Spread(share, w_qkv, w_out, send_w, recv_w, local)
    spread.start((0, 1, 2))
    cotangent_b[...] = jnp.dot(sort, cotangent[...], preferred_element_type=F32).astype(BF16)
    stores += start_all([pltpu.make_async_copy(cotangent_b, cotangent_out, store_sem.at[1])])
    wait_all(loads[4:])
    column = Column(gate_own, gate_all, send_c, recv_c, local.at[4])
    second = Gather(cotangent_b, cotangent_all, send_g, recv_g, local.at[5])
    spread.pass_on((0, 1, 2))
    gather.arrive(0, 1)
    second.start()
    column.start()
    gather.arrive(2, 3)
    spread.finish((0, 1, 2))
    spread.start((3,))
    stores += start_all([pltpu.make_async_copy(w_qkv, w_qkv_out, store_sem.at[2])])
    for copy in swaps:
        copy.wait()

    def keep(turn):
        owner = owner_at(turn)
        return pltpu.make_async_copy(hidden_all.at[owner], hidden_out.at[owner], out_sem.at[turn])

    def multiply(turn, carry):
        for number, numbers in ARRIVALS:
            left = tuple(n for n in numbers if n > 3)
            if left:
                pl.when(turn == number)(functools.partial(gather.arrive, *left))
        owner = owner_at(turn)
        keep(turn).start()
        product = lax.dot_general(
            hidden_all[owner], w_qkv[...], NT, preferred_element_type=F32
        ).astype(BF16)
        qkv[owner] = product.reshape(groups, rows // groups, 768)
        return carry

    lax.fori_loop(0, groups, multiply, 0)

    def halo(k, other):
        return to_mp(
            kept.at[k, pl.ds(rows, 64), pl.ds(256, 512)],
            kept.at[k, pl.ds(0, 64), pl.ds(256, 512)],
            send.at[k],
            recv.at[k],
            other,
        )

    def store_kept(k):
        return pltpu.make_async_copy(kept.at[k], kept_out.at[k], store_sem.at[3 + k])

    def store_mixed(k):
        span = pl.ds(k, 1)
        return pltpu.make_async_copy(
            mixed.at[:, span], mixed_out.at[:, span], store_sem.at[3 + groups + k]
        )

    def order(k, carry):
        hot = hot_of(notes_all, k, rows)
        given = qkv[:, pl.ds(k, 1)].reshape(rows, 768)
        kept[k, pl.ds(64, rows), :] = lax.dot_general(
            hot, given, TN, preferred_element_type=F32
        ).astype(BF16)
        kept[k, pl.ds(0, 64), pl.ds(0, 256)] = jnp.zeros((64, 256), BF16)

        @pl.when(z < members - 1)
        def _():
            halo(k, z + 1).start()

        @pl.when(z == 0)
        def _():
            kept[k, pl.ds(0, 64), pl.ds(256, 512)] = jnp.zeros((64, 512), BF16)

        return carry

    lax.fori_loop(0, groups, order, 0)

    def attend(k, carry):
        @pl.when(z > 0)
        def _():
            halo(k, z).wait_recv()

        store_kept(k).start()
        hot = hot_of(notes_all, k, rows)
        pairs = [(block, head) for block in range(rows // 128) for head in range(2)]
        masks = [block_mask(notes_all, k, block, z, rows) for block in range(rows // 128)]
        scores = []
        for block, head in pairs:
            query = kept[k, pl.ds(64 + block * 128, 128), pl.ds(head * 128, 128)]
            keys = kept[k, pl.ds(block * 128, 192), pl.ds(256 + head * 128, 128)]
            value = lax.dot_general(query, keys, NT, preferred_element_type=F32) * scale
            scores.append(jnp.where(masks[block], value, -MASKED))
        chances = []
        for value in scores:
            weights = jnp.exp(value - jnp.max(value, axis=-1, keepdims=True))
            total = jnp.sum(weights, axis=-1, keepdims=True)
            chances.append((weights / total).astype(BF16))
        parts = []
        for (block, head), chance in zip(pairs, chances):
            values = kept[k, pl.ds(block * 128, 192), pl.ds(512 + head * 128, 128)]
            parts.append(jnp.dot(chance, values, preferred_element_type=F32).astype(BF16))
        found = [
            jnp.concatenate(parts[2 * block : 2 * block + 2], axis=1)
            for block in range(rows // 128)
        ]
        ordered = jnp.concatenate(found, axis=0)
        back = jnp.dot(hot, ordered, preferred_element_type=F32).astype(BF16)
        mixed[:, pl.ds(k, 1)] = back.reshape(groups, 1, rows // groups, 256)
        store_mixed(k).start()
        return carry

    spread.pass_on((3,))
    lax.fori_loop(0, 2, attend, 0)
    second.pass_on()
    column.pass_on()
    lax.fori_loop(2, groups, attend, 0)
    spread.finish((3,))
    second.finish()
    column.finish()
    gather.sent()

    wait_all(stores)

    def stored(turn, carry):
        keep(turn).wait()
        store_kept(turn).wait()
        store_mixed(turn).wait()
        return carry

    lax.fori_loop(0, groups, stored, 0)

    @pl.when(z < members - 1)
    def _():
        def done(k, carry):
            halo(k, z + 1).wait_send()
            return carry

        lax.fori_loop(0, groups, done, 0)


def attend_ahead(
    tokens, cotangent, order_row, gain, notes, query, keys, values, project, gate, scale
):
    rows, width = tokens.shape
    groups, members = lax.axis_size("dp"), lax.axis_size("mp")
    dma = pltpu.SemaphoreType.DMA
    shape = jax.ShapeDtypeStruct
    return pl.pallas_call(
        functools.partial(forward_kernel, scale=scale),
        out_shape=(
            shape((groups, rows, width), BF16),
            shape((6 * LANES, width), BF16),
            shape((2 * LANES, width), BF16),
            shape((groups,) + notes.shape, F32),
            shape((members, width, LANES), BF16),
            shape((groups, groups, rows // groups, 256), BF16),
            shape((groups, rows + 64, 768), BF16),
            shape((rows, width), BF16),
            shape((rows, width), BF16),
            shape((groups, rows, width), BF16),
        ),
        in_specs=[on_chip()] * 5 + [anywhere()] * 5,
        out_specs=(
            anywhere(), anywhere(), on_chip(), on_chip(), anywhere(),
            anywhere(), anywhere(), anywhere(), anywhere(), anywhere(),
        ),
        scratch_shapes=[
            pltpu.VMEM((groups, rows, width), BF16),
            pltpu.VMEM((groups, groups, rows // groups, 768), BF16),
            pltpu.VMEM((4, HEAD_DIM, width), BF16),
            pltpu.VMEM((width, LANES), BF16),
            pltpu.VMEM((6 * LANES, width), BF16),
            pltpu.VMEM((groups, groups, rows // groups, 256), BF16),
            pltpu.VMEM((groups, rows + 64, 768), BF16),
            pltpu.VMEM((rows, width), BF16),
            pltpu.VMEM((rows, width), BF16),
            dma((groups,)),
            dma((groups,)),
            dma((13,)),
            dma((13,)),
            dma((13,)),
            dma((13,)),
            dma((12,)),
            dma((8,)),
            dma((7,)),
            dma((7,)),
            dma((4,)),
            dma((4,)),
            dma((6,)),
            dma((groups,)),
            dma((3 + 2 * groups,)),
        ],
        compiler_params=remote_params(2, 60 * 1024 * 1024),
        cost_estimate=pl.CostEstimate(flops=0, bytes_accessed=300_000_000, transcendentals=0),
        name="attend_ahead",
    )(tokens, cotangent, order_row, gain, notes, query, keys, values, project, gate)


CHUNK = 32


def each_chunk(rows, body, chunk=CHUNK):
    def step(i, carry):
        body(pl.ds(pl.multiple_of(i * chunk, chunk), chunk))
        return carry

    lax.fori_loop(0, rows // chunk, step, 0)


class Units:
    def __init__(self, part, came_in, stage, send, recv, local):
        self.z = lax.axis_index("mp")
        self.part_of = part
        self.inputs = (came_in,)
        self.stages = (stage,)
        self.send, self.recv, self.local = send, recv, local
        z = self.z
        self.outer = (z == 0) | (z == 3)
        self.far = 3 - z
        self.near = 1 + lax.div(z, 3)
        self.second = 3 - self.near
        self.edge = 3 * (z - 1)

    def part(self, kind, z):
        return self.part_of(z)

    def straight(self, kind, number, target):
        return to_mp(
            self.part(kind, target),
            self.inputs[kind].at[self.z],
            self.send.at[number * 2 + kind],
            self.recv.at[self.z * 2 + kind],
            target,
        )

    def staged(self, kind):
        return to_mp(
            self.part(kind, self.far),
            self.stages[kind].at[0],
            self.send.at[4 + kind],
            self.recv.at[8 + kind],
            self.near,
        )

    def summed(self, kind):
        return to_mp(
            self.stages[kind].at[1],
            self.inputs[kind].at[self.z],
            self.send.at[4 + kind],
            self.recv.at[self.z * 2 + kind],
            3 - self.edge,
        )

    def mine(self, kind):
        return pltpu.make_async_copy(
            self.part(kind, 3 - self.edge), self.stages[kind].at[1], self.local.at[kind]
        )

    def start(self):
        @pl.when(self.outer)
        def _():
            for kind in range(1):
                self.staged(kind).start()
            for kind in range(1):
                self.straight(kind, 0, self.near).start()
                self.straight(kind, 1, self.second).start()

        @pl.when(jnp.logical_not(self.outer))
        def _():
            for kind in range(1):
                self.mine(kind).start()
                self.straight(kind, 0, 3 - self.z).start()
                self.straight(kind, 1, self.edge).start()

    def add(self):
        @pl.when(jnp.logical_not(self.outer))
        def _():
            for kind in range(1):
                stage = self.stages[kind]
                self.mine(kind).wait()
                to_mp(
                    self.part(kind, 0),
                    stage.at[0],
                    self.send.at[4 + kind],
                    self.recv.at[8 + kind],
                    self.edge,
                ).wait_recv()

                def body(span):
                    stage[1, span, :] = (
                        stage[0, span, :].astype(F32) + stage[1, span, :].astype(F32)
                    ).astype(BF16)

                each_chunk(stage.shape[1], body)
                self.summed(kind).start()

    def arrived(self, kind, source):
        to_mp(
            self.part(kind, 0),
            self.inputs[kind].at[source],
            self.send.at[kind],
            self.recv.at[source * 2 + kind],
            source,
        ).wait_recv()

    def finish(self):
        @pl.when(self.outer)
        def _():
            for kind in range(1):
                self.arrived(kind, 1)
                self.arrived(kind, 2)
                self.straight(kind, 0, self.near).wait_send()
                self.straight(kind, 1, self.second).wait_send()
                self.staged(kind).wait_send()

        @pl.when(jnp.logical_not(self.outer))
        def _():
            for kind in range(1):
                self.arrived(kind, 0)
                self.arrived(kind, 3)
                self.arrived(kind, 3 - self.z)
                self.straight(kind, 0, 3 - self.z).wait_send()
                self.straight(kind, 1, self.edge).wait_send()
                self.summed(kind).wait_send()


class Reduce:
    COUNT = 10

    def __init__(self, left, right, across, part, from_side, from_corner, from_near, send, recv):
        self.left, self.right, self.across, self.part = left, right, across, part
        self.from_side, self.from_corner, self.from_near = from_side, from_corner, from_near
        self.send, self.recv = send, recv
        self.rows = part.shape[1]

    def product(self, owner, slot):
        rows, width = self.rows, self.part.shape[2]
        picked = pl.ds(pl.multiple_of(owner * rows, rows), rows)

        def tile(t, carry):
            columns = pl.ds(pl.multiple_of(t * 256, 256), 256)
            if callable(self.left):
                value = jnp.dot(
                    self.left(owner), self.right[:, columns], preferred_element_type=F32
                )
            elif self.across:
                value = lax.dot_general(
                    self.left[picked, :], self.right[columns, :], NT, preferred_element_type=F32
                )
            else:
                value = jnp.dot(
                    self.left[picked, :], self.right[:, columns], preferred_element_type=F32
                )
            self.part[slot, :, columns] = value.astype(BF16)
            return carry

        lax.fori_loop(0, width // 256, tile, 0)

    def prepare(self):
        _, side, over_x, over_y, corner = plane()
        part, near = self.part, self.from_near
        half = self.rows // 2
        low, high = pl.ds(0, half), pl.ds(half, half)

        def hop(number, source, target, index):
            return to_dp(source, target, self.send.at[number], self.recv.at[number], index)

        self.shares = [hop(i, part.at[4 + i], self.from_side.at[i], side) for i in range(4)]
        self.corners = [
            hop(4, part.at[0, low], self.from_corner.at[0], over_x),
            hop(5, part.at[0, high], self.from_corner.at[1], over_y),
        ]
        self.nears = [
            hop(6, part.at[1, low], near.at[0, low], over_x),
            hop(7, part.at[1, high], near.at[0, high], over_x),
            hop(8, part.at[2, high], near.at[1, high], over_y),
            hop(9, part.at[2, low], near.at[1, low], over_y),
        ]

    def add_side(self, slot):
        self.shares[slot].wait_recv()

        def body(span):
            self.part[slot, span, :] = (
                self.part[slot, span, :].astype(F32) + self.from_side[slot, span, :].astype(F32)
            ).astype(BF16)

        each_chunk(self.rows, body)

    def add_corner(self, slot, offset, which):
        self.corners[which].wait_recv()

        def body(span):
            target = pl.ds(pl.multiple_of(offset + span.start, CHUNK), CHUNK)
            self.part[slot, target, :] = (
                self.part[slot, target, :].astype(F32)
                + self.from_corner[which, span, :].astype(F32)
            ).astype(BF16)

        each_chunk(self.rows // 2, body)

    def products(self):
        self.prepare()
        me, _, over_x, over_y, corner = plane()
        turn = 1 - 2 * lax.rem(me, 2)
        for slot, owner in enumerate((corner, over_x, over_y, me)):
            self.product(owner + turn, 4 + slot)
            self.shares[slot].start()
        for slot, owner in enumerate((corner, over_x, over_y, me)):
            self.product(owner, slot)

    def launch(self):
        self.add_side(0)
        self.corners[0].start()
        self.corners[1].start()
        self.add_side(1)
        self.nears[0].start()
        self.add_side(2)
        self.nears[2].start()

    def begin(self):
        self.prepare()
        me, _, over_x, over_y, corner = plane()
        turn = 1 - 2 * lax.rem(me, 2)
        self.product(corner + turn, 4)
        self.shares[0].start()
        self.product(corner, 0)
        self.product(over_x + turn, 5)
        self.shares[1].start()
        self.add_side(0)
        self.corners[0].start()
        self.corners[1].start()
        self.product(over_x, 1)
        self.product(over_y + turn, 6)
        self.shares[2].start()
        self.add_side(1)
        self.nears[0].start()
        self.product(over_y, 2)
        self.product(me + turn, 7)
        self.shares[3].start()
        self.add_side(2)
        self.nears[2].start()
        self.product(me, 3)

    def middle(self):
        self.add_corner(2, 0, 0)
        self.nears[3].start()
        self.add_corner(1, self.rows // 2, 1)
        self.nears[1].start()

    def end(self):
        self.shares[3].wait_recv()
        for copy in self.nears:
            copy.wait_recv()

    def run(self):
        self.begin()
        self.middle()
        self.end()

    def rows_of(self, span):
        return (
            self.part[3, span, :].astype(F32)
            + self.from_side[3, span, :].astype(F32)
            + self.from_near[0, span, :].astype(F32)
            + self.from_near[1, span, :].astype(F32)
        )

    def finish(self):
        for copy in self.shares + self.corners + self.nears:
            copy.wait_send()


def reduce_scratch(rows, width):
    dma = pltpu.SemaphoreType.DMA
    return [
        pltpu.VMEM((8, rows, width), BF16),
        pltpu.VMEM((4, rows, width), BF16),
        pltpu.VMEM((2, rows // 2, width), BF16),
        pltpu.VMEM((2, rows, width), BF16),
        dma((10,)),
        dma((10,)),
    ]


def gather_scratch(rows, width):
    dma = pltpu.SemaphoreType.DMA
    return [pltpu.VMEM((rows, width), BF16), dma((13,)), dma((13,)), dma(())]


def mean_rows(values):
    return jnp.mean(values, axis=-1, keepdims=True)


class Heads:
    def __init__(self, source, stage, arrive, send, recv_stage, recv):
        me, z = lax.axis_index("dp"), lax.axis_index("mp")
        self.me, self.z = me, z
        self.core = lax.rem(me, 2)
        self.source, self.stage, self.arrive = source, stage, arrive
        self.send, self.recv_stage, self.recv = send, recv_stage, recv
        self.place = z + self.core * (3 - 2 * z)
        self.columns = source.shape[1] // 2

    def z_of(self, place):
        return place + self.core * (3 - 2 * place)

    def slot_of(self, place):
        return self.core if place == 0 else 1 - self.core

    def rows_of(self, place, kind):
        block = 2 * kind + self.slot_of(place)
        return self.source.at[pl.ds(pl.multiple_of(block * LANES, LANES), HEAD_DIM)]

    def half_of(self, ref, half):
        return ref.at[:, pl.ds(pl.multiple_of(half * self.columns, LANES), self.columns)]

    def to_stage(self, place, kind):
        return to_at(
            self.rows_of(place, kind),
            self.stage.at[place, kind],
            self.send.at[place * 4 + kind],
            self.recv_stage.at[place * 4 + kind],
            self.me,
            self.z_of(2),
        )

    def to_owner(self, place, kind, half, way, ref, number):
        return to_at(
            self.half_of(ref, half),
            self.arrive.at[way, kind],
            self.send.at[number],
            self.recv.at[way * 4 + kind],
            self.me - self.core + half,
            self.z_of(place),
        )

    def sums(self, kind):
        return [
            self.to_owner(
                place, kind, half, 2, self.stage.at[place, kind], place * 8 + kind * 2 + half
            )
            for place in (0, 1)
            for half in (0, 1)
        ]

    def cross(self, own, kind):
        other = 1 - own
        copies = [
            self.to_owner(other, kind, half, 0, self.rows_of(other, kind), kind * 2 + half)
            for half in (0, 1)
        ]
        copies.append(
            to_at(
                self.half_of(self.rows_of(own, kind), 1 - self.core),
                self.arrive.at[1, kind],
                self.send.at[8 + kind],
                self.recv.at[4 + kind],
                self.me + 1 - 2 * self.core,
                self.z,
            )
        )
        return copies

    def start(self, kinds):
        @pl.when(self.place == 3)
        def _():
            for kind in kinds:
                self.to_stage(0, kind).start()
                self.to_stage(1, kind).start()

        for own in (0, 1):
            @pl.when(self.place == own)
            def _():
                for kind in kinds:
                    for copy in self.cross(own, kind):
                        copy.start()

    def add(self, kinds):
        @pl.when(self.place == 2)
        def _():
            for kind in kinds:
                for place in (0, 1):
                    self.to_stage(place, kind).wait_recv()
                    mine = self.rows_of(place, kind)

                    def body(span):
                        self.stage[place, kind, span, :] = (
                            self.stage[place, kind, span, :].astype(F32)
                            + mine[span, :].astype(F32)
                        ).astype(BF16)

                    each_chunk(HEAD_DIM, body, 16)
                for copy in self.sums(kind):
                    copy.start()

    def total(self, out):
        owner = lax.div(self.z, 2) == self.core
        for kind in range(4):
            for own in (0, 1):
                @pl.when(self.place == own)
                def _():
                    self.arrive[1, kind] = self.half_of(self.rows_of(own, kind), self.core)[...]

            for way in range(3):
                waiting = to_at(
                    self.half_of(self.rows_of(0, kind), 0),
                    self.arrive.at[way, kind],
                    self.send.at[0],
                    self.recv.at[way * 4 + kind],
                    self.me,
                    lax.rem(self.z + 1, 4),
                )
                if way == 1:
                    pl.when(jnp.logical_not(owner))(waiting.wait_recv)
                else:
                    waiting.wait_recv()

            def body(span):
                found = self.arrive[0, kind, span, :].astype(F32)
                found = found + self.arrive[1, kind, span, :].astype(F32)
                found = found + self.arrive[2, kind, span, :].astype(F32)
                target = pl.ds(pl.multiple_of(kind * HEAD_DIM + span.start, 16), 16)
                out[target, :] = found.astype(BF16)

            each_chunk(HEAD_DIM, body, 16)

    def finish_send(self):
        for kind in range(4):
            @pl.when(self.place == 3)
            def _():
                self.to_stage(0, kind).wait_send()
                self.to_stage(1, kind).wait_send()

            @pl.when(self.place == 2)
            def _():
                for copy in self.sums(kind):
                    copy.wait_send()

            for own in (0, 1):
                @pl.when(self.place == own)
                def _():
                    for copy in self.cross(own, kind):
                        copy.wait_send()


def to_at(source, target, send_sem, recv_sem, dp, mp):
    return pltpu.make_async_remote_copy(
        src_ref=source,
        dst_ref=target,
        send_sem=send_sem,
        recv_sem=recv_sem,
        device_id={"dp": dp, "mp": mp},
        device_id_type=MESH,
    )


def backward_kernel(
    branch, notes_all, kept_in, w_out_in, activated_in, w_down_in, middle_in, both_sum, down_sum,
    out, result, branch_all, both_in, down_all,
    totals, query_part, key_value, ending, leaving, arriving, send, recv,
    part, from_side, from_corner, from_near, send_r, recv_r,
    mixed_grad, shard, load_sem, send_g, recv_g,
    both_stage, send_u, recv_u, local, down_found, send_d, recv_d,
    kept, w_out, activated, w_down, middle, fetch_sem, down_stage, send_v, recv_v, local_v,
    *, scale, groups, rows,
):
    z = lax.axis_index("mp")
    members = lax.axis_size("mp")
    barrier = greet_all()
    pairs = ((activated_in, activated), (w_out_in, w_out), (kept_in, kept), (middle_in, middle))
    pairs += ((w_down_in, w_down),)
    fetches = [
        pltpu.make_async_copy(source, target, fetch_sem.at[number])
        for number, (source, target) in enumerate(pairs)
    ]

    def down_rows(owner):
        return down_sum.at[pl.ds(pl.multiple_of(owner * LANES, LANES), LANES)]

    down_units = Units(down_rows, down_found, down_stage, send_v, recv_v, local_v)
    load_down = pltpu.make_async_copy(down_rows(z), down_found.at[z], load_sem.at[2])
    pl.semaphore_wait(barrier, 13)
    units = Units(lambda owner: both_sum.at[owner], both_in, both_stage, send_u, recv_u, local)
    gather = Gather(branch, branch_all, send_g, recv_g, local.at[2])
    gather.start()
    down_units.start()
    units.start()
    start_all(fetches)
    load_down.start()
    wait_all((fetches[0], fetches[4]))
    reduce = Reduce(activated, w_down, False, part, from_side, from_corner, from_near, send_r, recv_r)
    reduce.products()
    down_units.add()
    down = Gather(down_found.at[0], down_all, send_d, recv_d, local.at[1])

    def load_shard(turn):
        slot = turn % 2
        return pltpu.make_async_copy(branch_all.at[owner_at(turn)], shard.at[slot], load_sem.at[slot])

    def spread_back(turn, carry):
        for number, numbers in ARRIVALS:
            pl.when(turn == number)(functools.partial(gather.arrive, *numbers))

        @pl.when(turn == 0)
        def _():
            gather.keep.wait()

        load_shard(turn).start()
        load_shard(turn).wait()
        mixed_grad[owner_at(turn)] = (
            lax.dot_general(shard[turn % 2], w_out[...], NT, preferred_element_type=F32)
            .astype(BF16)
            .reshape(groups, rows // groups, 256)
        )
        return carry

    fetches[1].wait()
    lax.fori_loop(0, 4, spread_back, 0)
    reduce.launch()
    lax.fori_loop(4, 8, spread_back, 0)
    units.add()


    def halo(k, other):
        return to_mp(leaving.at[k], arriving.at[k], send.at[k], recv.at[k], other)

    def attend(k, carry):
        hot = hot_of(notes_all, k, rows)
        given = mixed_grad[:, pl.ds(k, 1)].reshape(rows, 256)
        grad_ordered = lax.dot_general(hot, given, TN, preferred_element_type=F32).astype(BF16)
        totals[...] = jnp.zeros_like(totals)
        pairs = [(block, head) for block in range(rows // 128) for head in range(2)]
        masks = [block_mask(notes_all, k, block, z, rows) for block in range(rows // 128)]

        def query_of(block, head):
            return kept[k, pl.ds(64 + block * 128, 128), pl.ds(head * 128, 128)]

        def keys_of(block, head):
            return kept[k, pl.ds(block * 128, 192), pl.ds(256 + head * 128, 128)]

        def grad_of(block, head):
            return grad_ordered[block * 128 : block * 128 + 128, head * 128 : head * 128 + 128]

        scores, chance_grads = [], []
        for block, head in pairs:
            value = lax.dot_general(
                query_of(block, head), keys_of(block, head), NT, preferred_element_type=F32
            )
            scores.append(jnp.where(masks[block], value * scale, -MASKED))
            values = kept[k, pl.ds(block * 128, 192), pl.ds(512 + head * 128, 128)]
            chance_grads.append(
                lax.dot_general(grad_of(block, head), values, NT, preferred_element_type=F32)
            )
        agains, score_grads = [], []
        for value, chance_grad in zip(scores, chance_grads):
            weights = jnp.exp(value - jnp.max(value, axis=-1, keepdims=True))
            again = weights / jnp.sum(weights, axis=-1, keepdims=True)
            row_dot = jnp.sum(again * chance_grad, axis=-1, keepdims=True)
            agains.append(again.astype(BF16))
            score_grads.append((again * (chance_grad - row_dot)).astype(BF16))
        for (block, head), again, score_grad in zip(pairs, agains, score_grads):
            query_part[k, pl.ds(block * 128, 128), pl.ds(head * 128, 128)] = (
                jnp.dot(score_grad, keys_of(block, head), preferred_element_type=F32) * scale
            ).astype(BF16)
            totals[pl.ds(block * 128, 192), pl.ds(head * 128, 128)] += (
                lax.dot_general(score_grad, query_of(block, head), TN, preferred_element_type=F32)
                * scale
            )
            totals[pl.ds(block * 128, 192), pl.ds(256 + head * 128, 128)] += lax.dot_general(
                again, grad_of(block, head), TN, preferred_element_type=F32
            )
        key_value[k] = totals[pl.ds(64, rows), :].astype(BF16)
        ending[k] = totals[pl.ds(rows, 64), :]

        @pl.when(z > 0)
        def _():
            leaving[k] = totals[pl.ds(0, 64), :].astype(BF16)
            halo(k, z - 1).start()

        return carry

    wait_all(fetches[2:4])
    lax.fori_loop(0, 2, attend, 0)
    reduce.middle()
    load_down.wait()
    down_units.finish()

    @pl.when((z == 0) | (z == members - 1))
    def _():
        down_found[members - 1 - z] = jnp.zeros_like(down_found[0])

    def add_down(span):
        value = down_found[0, span, :].astype(F32) + down_found[1, span, :].astype(F32)
        value = value + down_found[2, span, :].astype(F32) + down_found[3, span, :].astype(F32)
        down_found[0, span, :] = value.astype(BF16)

    each_chunk(down_found.shape[1], add_down)
    down.start()
    lax.fori_loop(2, groups, attend, 0)
    down.pass_on()

    def restore(k, carry):
        @pl.when(z < members - 1)
        def _():
            halo(k, z).wait_recv()
            key_value[k, pl.ds(rows - 64, 64), :] = (
                ending[k] + arriving[k].astype(F32)
            ).astype(BF16)

        hot = hot_of(notes_all, k, rows)
        ordered = jnp.concatenate([query_part[k], key_value[k]], axis=1)
        back = jnp.dot(hot, ordered, preferred_element_type=F32).astype(BF16)
        out[:, pl.ds(k, 1)] = back.reshape(groups, 1, rows // groups, 768)
        return carry

    lax.fori_loop(0, groups, restore, 0)
    reduce.end()

    def body(span):
        result[span, :] = (middle[span, :] + reduce.rows_of(span)).astype(BF16)

    each_chunk(rows, body)
    down.finish()
    units.finish()
    for copy in gather.copies:
        copy.wait_send()
    reduce.finish()

    @pl.when(z > 0)
    def _():
        def done(k, carry):
            halo(k, z - 1).wait_send()
            return carry

        lax.fori_loop(0, groups, done, 0)


def attend_back(
    branch, notes_all, kept, w_out, activated, w_down, middle, both_sum, down_sum, scale
):
    groups = kept.shape[0]
    rows, width = middle.shape
    members = both_sum.shape[0]
    dma = pltpu.SemaphoreType.DMA
    shape = jax.ShapeDtypeStruct
    return pl.pallas_call(
        functools.partial(backward_kernel, scale=scale, groups=groups, rows=rows),
        out_shape=(
            shape((groups, groups, rows // groups, 768), BF16),
            shape((rows, width), BF16),
            shape((groups, rows, width), BF16),
            shape((members, width, 256), BF16),
            shape((groups, LANES, width), BF16),
        ),
        in_specs=[on_chip()] * 2 + [anywhere()] * 7,
        out_specs=(on_chip(),) * 2 + (anywhere(),) * 3,
        scratch_shapes=[
            pltpu.VMEM((rows + 64, 512), F32),
            pltpu.VMEM((groups, rows, 256), BF16),
            pltpu.VMEM((groups, rows, 512), BF16),
            pltpu.VMEM((groups, 64, 512), F32),
            pltpu.VMEM((groups, 64, 512), BF16),
            pltpu.VMEM((groups, 64, 512), BF16),
            dma((groups,)),
            dma((groups,)),
        ]
        + reduce_scratch(rows, width)
        + [
            pltpu.VMEM((groups, groups, rows // groups, 256), BF16),
            pltpu.VMEM((2, rows, width), BF16),
            dma((3,)),
            dma((13,)),
            dma((13,)),
            pltpu.VMEM((2, width, 256), BF16),
            dma((6,)),
            dma((10,)),
            dma((3,)),
            pltpu.VMEM((members, LANES, width), BF16),
            dma((13,)),
            dma((13,)),
            pltpu.VMEM(kept.shape, BF16),
            pltpu.VMEM(w_out.shape, BF16),
            pltpu.VMEM(activated.shape, BF16),
            pltpu.VMEM((members * LANES, width), BF16),
            pltpu.VMEM((rows, width), F32),
            dma((5,)),
            pltpu.VMEM((2, LANES, width), BF16),
            dma((6,)),
            dma((10,)),
            dma((1,)),
        ],
        compiler_params=remote_params(3, 63 * 1024 * 1024),
        cost_estimate=pl.CostEstimate(flops=0, bytes_accessed=300_000_000, transcendentals=0),
        name="attend_back",
    )(branch, notes_all, kept, w_out, activated, w_down, middle, both_sum, down_sum)


def norm_back_rows(gradient, values, gain, sums, span):
    inverse = lax.rsqrt(mean_rows(values * values) + EPSILON)
    normed = values * inverse
    product = gradient * normed
    folded = product[0:8]
    for step in range(1, CHUNK // 8):
        folded = folded + product[step * 8 : step * 8 + 8]
    sums[...] += folded
    scaled = gradient * gain
    return inverse * (scaled - normed * mean_rows(scaled * normed))


def feed_kernel(
    mixed, w_out, tokens, cotangent_all, gate_all, w_up, down_weight, cotangent_own, gain,
    middle, middle_grad, branch, sums, activated_out, both_sum, down_out, up_all, down_all,
    hidden_all, both_grad, part, from_side, from_corner, from_near, send_r, recv_r,
    send_m, recv_m, send_n, recv_n, send_a, recv_a, send_b, recv_b, cot_shard, cot_tile, stage_both, down_sum, w_both, w_down,
    cotangent, activated, load_sem, local,
    up_own, down_own, send_u, recv_u, send_d, recv_d, first_sem,
):
    groups, rows, width = hidden_all.shape
    members = gate_all.shape[0]
    me = lax.axis_index("dp")
    barrier = greet_all()
    units_own = pl.ds(pl.multiple_of(me * LANES, LANES), LANES)
    first = start_all(
        [
            pltpu.make_async_copy(source, target, first_sem.at[number])
            for number, (source, target) in enumerate(
                (
                    (mixed, activated.at[:, :, pl.ds(0, 256)]),
                    (w_out, down_sum.at[pl.ds(0, 256)]),
                    (w_up.at[:, units_own], up_own),
                    (down_weight.at[units_own], down_own),
                    (tokens, cotangent),
                )
            )
        ]
    )
    gates = start_all(
        [
            pltpu.make_async_copy(
                gate_all.at[z], w_both.at[:, pl.ds(z * 256, 128)], load_sem.at[6 + z]
            )
            for z in range(members)
        ]
    )

    def slot_of(turn):
        block = turn // 2
        near = ((block + 1) // 2) % 2
        far = block // 3
        second = turn % 2
        other = (1 - near) * second + (block // 2) * near
        return 4 * other + 3 * (1 - near) * (1 - far) + near * (1 + second)

    def load_cotangent(turn):
        return pltpu.make_async_copy(
            cotangent_all.at[owner_at(turn)], cot_shard.at[turn % 2], load_sem.at[turn % 2]
        )

    load_cotangent(0).start()
    wait_all(first)
    pl.semaphore_wait(barrier, 13)
    columns_up = Column(up_own, up_all, send_u, recv_u, local.at[0])
    columns_down = Column(down_own, down_all, send_d, recv_d, local.at[2])
    columns_up.start()
    columns_down.start()
    half_rows = rows // 2

    def half(number, sends, recvs):
        span = pl.ds(number * half_rows, half_rows)
        quarter = pl.ds(number * (half_rows // 2), half_rows // 2)
        return Reduce(
            lambda owner: activated[owner, span, 0:256], down_sum.at[pl.ds(0, 256)], False,
            part.at[:, span], from_side.at[:, span], from_corner.at[:, quarter],
            from_near.at[:, span], sends, recvs,
        )

    projects = (half(0, send_m, recv_m), half(1, send_n, recv_n))
    gathers = [
        Gather(None, hidden_all.at[:, pl.ds(number * half_rows, half_rows)], sends, recvs)
        for number, (sends, recvs) in enumerate(((send_a, recv_a), (send_b, recv_b)))
    ]
    for project in projects:
        project.begin()
    for project in projects:
        project.middle()
    columns_up.pass_on()
    columns_down.pass_on()
    for number, project in enumerate(projects):
        project.end()

        def normalise(span):
            own = pl.ds(pl.multiple_of(number * half_rows + span.start, CHUNK), CHUNK)
            values = cotangent[own, :].astype(F32) + project.rows_of(span)
            middle_grad[own, :] = values
            inverse = lax.rsqrt(mean_rows(values * values) + EPSILON)
            hidden_all[me, own, :] = (values * inverse * gain[...].reshape(1, -1)).astype(BF16)

        each_chunk(half_rows, normalise)
        gathers[number].start()

    for project in projects:
        project.finish()
    store_middle = pltpu.make_async_copy(middle_grad, middle, local.at[1])
    load_own = pltpu.make_async_copy(cotangent_own, cotangent, local.at[3])
    store_middle.start()
    load_own.start()
    columns_up.finish()
    columns_down.finish()
    ups = start_all(
        [
            pltpu.make_async_copy(
                up_all.at[z], w_both.at[:, pl.ds(z * 256 + 128, 128)], load_sem.at[10 + z]
            )
            for z in range(members)
        ]
    )
    ups += start_all(
        [
            pltpu.make_async_copy(
                down_all.at[z], w_down.at[pl.ds(z * LANES, LANES)], load_sem.at[14 + z]
            )
            for z in range(members)
        ]
    )
    reduce = Reduce(None, None, False, part, from_side, from_corner, from_near, send_r, recv_r)
    reduce.prepare()

    def nears():
        reduce.add_side(1)
        reduce.nears[0].start()
        reduce.add_side(2)
        reduce.nears[2].start()

    early = [
        (turn, functools.partial(gather.arrive, *numbers))
        for turn, numbers in ARRIVALS
        for gather in gathers
    ]
    early += [(6, nears)]
    late = [(1, 3), (4, 1), (5, 2), (7, 0)]
    wait_all(gates + ups)

    def unit(turn, carry):
        for number, action in early:
            pl.when(turn == number)(action)

        @pl.when(turn < 7)
        def _():
            load_cotangent(turn + 1).start()

        load_cotangent(turn).wait()
        owner, slot = owner_at(turn), slot_of(turn)
        mine = hidden_all[owner]
        grads = cot_shard[turn % 2]
        for z in range(members):
            raw = jnp.dot(mine, w_both[:, z * 256 : z * 256 + 256], preferred_element_type=F32)
            units = pl.ds(z * 128, 128)
            if z % 2 == 0:
                pair = lax.dot_general(
                    grads, w_down[pl.ds(z * 128, 256), :], NT, preferred_element_type=F32
                )
            active_grad = pair[:, 128 * (z % 2) : 128 * (z % 2) + 128]
            gate, upward = raw[:, :128], raw[:, 128:]
            sigmoid = jax.nn.sigmoid(gate)
            activated[owner, :, units] = (gate * sigmoid * upward).astype(BF16)
            both_grad[owner, :, pl.ds(z * 256, 128)] = (
                active_grad * upward * sigmoid * (1.0 + gate * (1.0 - sigmoid))
            ).astype(BF16)
            both_grad[owner, :, pl.ds(z * 256 + 128, 128)] = (
                active_grad * gate * sigmoid
            ).astype(BF16)

        def tile(t, inner):
            columns = pl.ds(pl.multiple_of(t * 256, 256), 256)
            part[slot, :, columns] = lax.dot_general(
                both_grad[owner], w_both[columns, :], NT, preferred_element_type=F32
            ).astype(BF16)
            return inner

        lax.fori_loop(0, width // 256, tile, 0)
        for number, share in late:
            pl.when(turn == number)(reduce.shares[share].start)
        return carry

    lax.fori_loop(0, 8, unit, 0)
    store_activated = pltpu.make_async_copy(activated, activated_out, local.at[4])
    store_activated.start()

    def load_tile(t):
        columns = pl.ds(pl.multiple_of(t * 256, 256), 256)
        return pltpu.make_async_copy(
            cotangent_all.at[:, :, columns], cot_tile.at[t % 2], load_sem.at[2 + t % 2]
        )

    def store_both(t):
        columns = pl.ds(pl.multiple_of(t * 256, 256), 256)
        return pltpu.make_async_copy(
            stage_both.at[t % 2], both_sum.at[:, columns], load_sem.at[4 + t % 2]
        )

    tiles = width // 256
    count = groups * rows

    def down_tile(t, carry):
        columns = pl.ds(pl.multiple_of(t * 256, 256), 256)

        @pl.when(t < tiles - 1)
        def _():
            load_tile(t + 1).start()

        load_tile(t).wait()
        down_sum[:, columns] = lax.dot_general(
            activated[...].reshape(count, members * 128),
            cot_tile[t % 2].reshape(count, 256),
            TN,
            preferred_element_type=F32,
        ).astype(BF16)
        return carry

    store_down = pltpu.make_async_copy(down_sum, down_out, local.at[5])

    def weight_tile(t, carry):
        columns = pl.ds(pl.multiple_of(t * 256, 256), 256)

        @pl.when(t >= 2)
        def _():
            store_both(t - 2).wait()

        value = lax.dot_general(
            hidden_all[:, :, columns].reshape(count, 256),
            both_grad[...].reshape(count, members * 256),
            TN,
            preferred_element_type=F32,
        )
        for z in range(members):
            stage_both[t % 2, z] = value[:, z * 256 : z * 256 + 256].astype(BF16)
        store_both(t).start()
        return carry

    load_tile(0).start()
    reduce.add_side(0)
    reduce.corners[0].start()
    reduce.corners[1].start()
    lax.fori_loop(0, tiles, down_tile, 0)
    store_down.start()
    lax.fori_loop(0, 2, weight_tile, 0)
    reduce.middle()
    lax.fori_loop(2, tiles, weight_tile, 0)
    reduce.end()
    store_middle.wait()
    load_own.wait()
    sums[...] = jnp.zeros_like(sums)

    def body(span):
        change = norm_back_rows(reduce.rows_of(span), middle_grad[span, :], gain[...].reshape(1, -1), sums, span)
        total = cotangent[span, :].astype(F32) + change
        middle_grad[span, :] = total
        branch[span, :] = total.astype(BF16)

    each_chunk(rows, body)
    for gather in gathers:
        gather.sent()
    reduce.finish()
    for t in (tiles - 2, tiles - 1):
        store_both(t).wait()
    store_down.wait()
    store_activated.wait()


def feed(mixed, w_out, tokens, cotangent_all, gate_all, w_up, w_down, cotangent, gain):
    groups, rows, width = cotangent_all.shape
    members = gate_all.shape[0]
    dma = pltpu.SemaphoreType.DMA
    units = members * 128
    return pl.pallas_call(
        feed_kernel,
        out_shape=(
            jax.ShapeDtypeStruct((rows, width), F32),
            jax.ShapeDtypeStruct((rows, width), F32),
            jax.ShapeDtypeStruct((rows, width), BF16),
            jax.ShapeDtypeStruct((8, width), F32),
            jax.ShapeDtypeStruct((groups, rows, units), BF16),
            jax.ShapeDtypeStruct((members, width, 256), BF16),
            jax.ShapeDtypeStruct((units, width), BF16),
            jax.ShapeDtypeStruct((members, width, LANES), BF16),
            jax.ShapeDtypeStruct((members, LANES, width), BF16),
        ),
        in_specs=[anywhere()] * 8 + [on_chip()],
        out_specs=(anywhere(),) + (on_chip(),) * 3 + (anywhere(),) * 5,
        scratch_shapes=[
            pltpu.VMEM((groups, rows, width), BF16),
            pltpu.VMEM((groups, rows, 2 * units), BF16),
        ]
        + reduce_scratch(rows, width)
        + [
            dma((10,)),
            dma((10,)),
            dma((10,)),
            dma((10,)),
            dma((13,)),
            dma((13,)),
            dma((13,)),
            dma((13,)),
            pltpu.VMEM((2, rows, width), BF16),
            pltpu.VMEM((2, groups, rows, 256), BF16),
            pltpu.VMEM((2, members, 256, 256), BF16),
            pltpu.VMEM((units, width), BF16),
            pltpu.VMEM((width, 2 * units), BF16),
            pltpu.VMEM((units, width), BF16),
            pltpu.VMEM((rows, width), BF16),
            pltpu.VMEM((groups, rows, units), BF16),
            dma((6 + 4 * members,)),
            dma((6,)),
            pltpu.VMEM((width, LANES), BF16),
            pltpu.VMEM((LANES, width), BF16),
            dma((4,)),
            dma((4,)),
            dma((4,)),
            dma((4,)),
            dma((5,)),
        ],
        compiler_params=remote_params(5, 63 * 1024 * 1024),
        cost_estimate=pl.CostEstimate(flops=0, bytes_accessed=400_000_000, transcendentals=0),
        name="feed",
    )(mixed, w_out, tokens, cotangent_all, gate_all, w_up, w_down, cotangent, gain)


def input_kernel(
    qkv_in, w_in, hidden_all, branch_all, mixed_in, tokens_in, middle_in, gain, sums_two,
    both_sum, both_in,
    result, gains, both_all, heads_all,
    part, from_side, from_corner, from_near, send, recv, sums,
    stage, arrive, send_h, recv_s, recv_h, own, plane_sums, column_sums, send_p, recv_p,
    weight_sum, row_tile, tile_sem, send_b, recv_b, send_t, recv_t, both_found, heads_own, local,
    mixed, tokens, middle_grad, fetch_sem, qkv_grad, w_qkv,
):
    me, z = lax.axis_index("dp"), lax.axis_index("mp")
    barrier = greet_all()
    count = qkv_grad.shape[0]
    tiles = tokens.shape[1] // 256
    outer = (z == 0) | (z == 3)

    def columns_of(t):
        return pl.ds(pl.multiple_of(lax.rem(t, tiles) * 256, 256), 256)

    def load(t, source):
        return pltpu.make_async_copy(
            source.at[:, :, columns_of(t)], row_tile.at[t % 2], tile_sem.at[t % 2]
        )

    own_part = pltpu.make_async_copy(both_sum.at[z], both_found.at[0], local.at[0])
    own_part.start()
    ways = [(outer, 1, 1), (outer, 2, 2)]
    ways += [(z == 1, 0, 1), (z == 1, 2, 2), (z == 1, 3, 3)]
    ways += [(z == 2, 0, 1), (z == 2, 1, 2), (z == 2, 3, 3)]

    def came(source, place):
        return pltpu.make_async_copy(both_in.at[source], both_found.at[place], local.at[place])

    for here, source, place in ways:
        pl.when(here)(came(source, place).start)

    @pl.when(outer)
    def _():
        both_found[3] = jnp.zeros_like(both_found[3])

    load(0, hidden_all).start()
    fetches = start_all(
        [
            pltpu.make_async_copy(source, target, fetch_sem.at[number])
            for number, (source, target) in enumerate(
                (
                    (qkv_in, qkv_grad),
                    (w_in, w_qkv),
                    (mixed_in, mixed),
                    (tokens_in, tokens),
                    (middle_in, middle_grad),
                )
            )
        ]
    )
    pl.semaphore_wait(barrier, 13)
    both = Gather(both_found.at[0], both_all, send_b, recv_b, local.at[4])

    def weight_tile(t, carry):
        @pl.when(t < tiles - 1)
        def _():
            load(t + 1, hidden_all).start()

        @pl.when((t >= tiles - 1) & (t < 2 * tiles - 1))
        def _():
            load(t + 1, branch_all).start()

        load(t, hidden_all).wait()

        @pl.when(t < tiles)
        def _():
            weight_sum[pl.ds(0, 768), columns_of(t)] = lax.dot_general(
                qkv_grad[...], row_tile[t % 2].reshape(count, 256), TN, preferred_element_type=F32
            ).astype(BF16)

        @pl.when(t >= tiles)
        def _():
            weight_sum[pl.ds(768, 256), columns_of(t)] = lax.dot_general(
                mixed[...], row_tile[t % 2].reshape(count, 256), TN, preferred_element_type=F32
            ).astype(BF16)

        return carry

    heads = Heads(weight_sum, stage, arrive, send_h, recv_s, recv_h)
    reduce = Reduce(qkv_grad, w_qkv, False, part, from_side, from_corner, from_near, send, recv)
    own_part.wait()
    for here, source, place in ways:
        pl.when(here)(came(source, place).wait)

    def add(span):
        value = both_found[0, span, :].astype(F32) + both_found[1, span, :].astype(F32)
        value = value + both_found[2, span, :].astype(F32) + both_found[3, span, :].astype(F32)
        both_found[0, span, :] = value.astype(BF16)

    each_chunk(both_found.shape[1], add)
    both.start()
    wait_all(fetches[:2])
    lax.fori_loop(0, tiles, weight_tile, 0)
    heads.start((0, 1, 2))
    wait_all(fetches[2:])
    lax.fori_loop(tiles, 2 * tiles, weight_tile, 0)
    heads.start((3,))
    both.pass_on()
    reduce.begin()
    heads.add((0, 1))
    reduce.middle()
    heads.add((2, 3))
    reduce.end()
    sums[...] = jnp.zeros_like(sums)

    def body(span):
        values = tokens[span, :].astype(F32)
        change = norm_back_rows(reduce.rows_of(span), values, gain[...].reshape(1, -1), sums, span)
        result[span, :] = (middle_grad[span, :] + change).astype(BF16)

    each_chunk(result.shape[0], body)
    own[...] = jnp.concatenate(
        [
            jnp.sum(sums[...], axis=0, keepdims=True),
            jnp.sum(sums_two[...], axis=0, keepdims=True),
        ],
        axis=0,
    )
    swaps = swap_all(own, plane_sums, send_p, recv_p)
    for copy in swaps:
        copy.start()
    plane_sums[me] = own[...]
    heads.total(heads_own)
    gather = Gather(heads_own, heads_all, send_t, recv_t, local.at[5])
    gather.start()
    for copy in swaps:
        copy.wait()
    found = plane_sums[0]
    for other in range(1, 8):
        found = found + plane_sums[other]
    column_sums[z] = found
    passes = [
        to_mp(
            column_sums.at[z],
            column_sums.at[z],
            send_p.at[6 + step],
            recv_p.at[6 + step],
            lax.rem(z + step, 4),
        )
        for step in range(1, 4)
    ]
    for copy in passes:
        copy.start()
    both.finish()
    for copy in passes:
        copy.wait()
    gains[...] = (column_sums[0] + column_sums[1]) + (column_sums[2] + column_sums[3])
    gather.pass_on()
    heads.finish_send()
    reduce.finish()
    gather.finish()


def project_input(
    qkv_grad, w_qkv, hidden_all, branch_all, mixed, tokens, middle_grad, gain, sums_two,
    both_sum, both_in,
):
    rows, width = tokens.shape
    groups = hidden_all.shape[0]
    dma = pltpu.SemaphoreType.DMA
    shape = jax.ShapeDtypeStruct
    return pl.pallas_call(
        input_kernel,
        out_shape=(
            shape((rows, width), BF16),
            shape((2, width), F32),
            shape((groups, width, 256), BF16),
            shape((groups, 4 * HEAD_DIM, width // 2), BF16),
        ),
        in_specs=[anywhere()] * 7 + [on_chip()] * 2 + [anywhere()] * 2,
        out_specs=(on_chip(),) * 2 + (anywhere(),) * 2,
        scratch_shapes=reduce_scratch(rows, width)
        + [
            pltpu.VMEM((8, width), F32),
            pltpu.VMEM((2, 4, HEAD_DIM, width), BF16),
            pltpu.VMEM((3, 4, HEAD_DIM, width // 2), BF16),
            dma((16,)),
            dma((8,)),
            dma((12,)),
            pltpu.VMEM((2, width), F32),
            pltpu.VMEM((8, 2, width), F32),
            pltpu.VMEM((4, 2, width), F32),
            dma((10,)),
            dma((10,)),
            pltpu.VMEM((8 * LANES, width), BF16),
            pltpu.VMEM((2, groups, rows, 256), BF16),
            dma((2,)),
            dma((13,)),
            dma((13,)),
            dma((13,)),
            dma((13,)),
            pltpu.VMEM((4, width, 256), BF16),
            pltpu.VMEM((4 * HEAD_DIM, width // 2), BF16),
            dma((6,)),
            pltpu.VMEM(mixed.shape, BF16),
            pltpu.VMEM((rows, width), BF16),
            pltpu.VMEM((rows, width), F32),
            dma((5,)),
            pltpu.VMEM(qkv_grad.shape, BF16),
            pltpu.VMEM(w_qkv.shape, BF16),
        ],
        compiler_params=remote_params(6, 63 * 1024 * 1024),
        cost_estimate=pl.CostEstimate(flops=0, bytes_accessed=250_000_000, transcendentals=0),
        name="project_input",
    )(
        qkv_grad, w_qkv, hidden_all, branch_all, mixed, tokens, middle_grad, gain, sums_two,
        both_sum, both_in,
    )


def assemble_kernel(
    both, down, heads, order_row, output_b, input_b,
    output, inputs, query, keys, values, project, gate, upward, down_out, *, tiles,
):
    for d in range(both.shape[0]):
        gate[:, d * 128 : d * 128 + 128] = both[d, :, :128].astype(F32)
        upward[:, d * 128 : d * 128 + 128] = both[d, :, 128:].astype(F32)
    down_out[...] = down[0].astype(F32)
    for kind, out in enumerate((query, keys, values, project)):
        out[...] = heads[0, kind].astype(F32)
    rows = output_b.shape[0]

    @pl.when(pl.program_id(0) < tiles)
    def _():
        place = lax.broadcasted_iota(jnp.int32, (rows, rows), 0).astype(F32)
        sort = (place == order_row[...]).astype(BF16)
        for ordered, out in ((output_b, output), (input_b, inputs)):
            out[...] = lax.dot_general(
                sort, ordered[...], TN, preferred_element_type=F32
            ).astype(BF16)


def assemble(both, down, heads, order_row, output_b, input_b):
    groups, width, wide = both.shape
    rows = output_b.shape[0]
    units = down.shape[1]
    chips = groups // 2
    columns = heads.shape[3]
    tile = width // groups
    shape = jax.ShapeDtypeStruct
    head = shape((chips * HEAD_DIM, 2 * columns), F32)
    head_spec = pl.BlockSpec((HEAD_DIM, columns), lambda i: (i // 2, i % 2))
    wide_spec = pl.BlockSpec((tile, groups * units), lambda i: (i, 0))
    tiles = width // 256
    row_spec = pl.BlockSpec((rows, 256), lambda i: (0, jnp.minimum(i, tiles - 1)))
    return pl.pallas_call(
        functools.partial(assemble_kernel, tiles=tiles),
        grid=(groups,),
        out_shape=(
            shape((rows, width), BF16),
            shape((rows, width), BF16),
            head,
            head,
            head,
            head,
            shape((width, groups * units), F32),
            shape((width, groups * units), F32),
            shape((groups * units, width), F32),
        ),
        in_specs=[
            pl.BlockSpec((groups, tile, wide), lambda i: (0, i, 0)),
            pl.BlockSpec((1, units, width), lambda i: (i, 0, 0)),
            pl.BlockSpec((1, 4, HEAD_DIM, columns), lambda i: (i, 0, 0, 0)),
            pl.BlockSpec((1, rows), lambda i: (0, 0)),
            row_spec,
            row_spec,
        ],
        out_specs=(
            row_spec, row_spec, head_spec, head_spec, head_spec, head_spec, wide_spec, wide_spec,
            pl.BlockSpec((units, width), lambda i: (i, 0)),
        ),
        compiler_params=pltpu.CompilerParams(vmem_limit_bytes=VMEM_LIMIT),
        cost_estimate=pl.CostEstimate(flops=0, bytes_accessed=58_000_000, transcendentals=0),
        name="assemble",
    )(both, down, heads, order_row, output_b, input_b)


def swapped(
    tokens, cotangent, route, lengths, key_mask, norm1_gain, norm2_gain,
    w_query, w_key, w_value, w_out, w_gate, w_up, w_down,
):
    groups = lax.axis_size("dp")
    members = lax.axis_size("mp")
    me = lax.axis_index("dp")
    z = lax.axis_index("mp")
    rows, width = tokens.shape
    bucket = rows // groups
    units = w_down.shape[0] // groups

    target = route // TOK_DEV
    earlier = jnp.arange(rows, dtype=jnp.int32)
    same = (target[:, None] == target[None, :]) & (earlier[None, :] < earlier[:, None])
    send_at = target * bucket + jnp.sum(same.astype(jnp.int32), axis=1)
    sorting = send_at[None, :] == earlier[:, None]
    slots_own = jnp.sum(jnp.where(sorting, (route % rows)[None, :], 0), axis=1)

    mask_window = lax.dynamic_slice_in_dim(
        jnp.concatenate([jnp.zeros((WINDOW,), jnp.int32), key_mask]), z * rows, rows + WINDOW
    )
    slot_rows = jnp.pad(slots_own.reshape(groups, bucket).T, ((0, 0), (0, LANES - groups)))
    mask_rows = jnp.pad(mask_window, (0, 4 * LANES - rows - WINDOW)).reshape(4, LANES)
    length_rows = jnp.pad(lengths, ((0, 3), (0, LANES - lengths.shape[1])))
    notes = jnp.concatenate([slot_rows, mask_rows, length_rows], axis=0).astype(F32)

    count = groups * rows
    scale = HEAD_DIM ** (-0.5)
    order_row = send_at.astype(F32)[None]
    (
        hidden_one,
        w_qkv,
        w_proj,
        notes_all,
        gate_all,
        mixed,
        kept,
        tokens_b,
        cotangent_b,
        cotangent_all,
    ) = attend_ahead(
        tokens,
        cotangent,
        order_row,
        norm1_gain,
        notes,
        w_query.T,
        w_key.T,
        w_value.T,
        w_out,
        w_gate,
        scale,
    )
    mixed = mixed.reshape(count, 2 * LANES)
    middle, middle_grad, branch, sums_two, activated, both_sum, down_sum, _, down_all = feed(
        mixed.reshape(groups, rows, 2 * LANES),
        w_proj,
        tokens_b,
        cotangent_all,
        gate_all,
        w_up,
        w_down,
        cotangent_b,
        norm2_gain,
    )
    qkv_grad, output_rows, branch_all, both_in, down_whole = attend_back(
        branch,
        notes_all,
        kept,
        w_proj,
        activated.reshape(count, units * members),
        down_all.reshape(members * units, width),
        middle,
        both_sum,
        down_sum,
        scale,
    )
    qkv_grad = qkv_grad.reshape(count, 6 * LANES)
    input_rows, gain_sums, both_whole, heads_whole = project_input(
        qkv_grad,
        w_qkv,
        hidden_one,
        branch_all,
        mixed,
        tokens_b,
        middle_grad,
        norm1_gain,
        sums_two,
        both_sum,
        both_in,
    )
    (
        output,
        input_grad,
        query_grad,
        key_grad,
        value_grad,
        proj_grad,
        gate_grad,
        up_grad,
        down_grad,
    ) = assemble(
        both_whole,
        down_whole,
        heads_whole.reshape(groups, 4, HEAD_DIM, width // 2),
        order_row,
        output_rows,
        input_rows,
    )
    return (
        output,
        input_grad,
        gain_sums[0],
        gain_sums[1],
        query_grad.T,
        key_grad.T,
        value_grad.T,
        proj_grad,
        gate_grad,
        up_grad,
        down_grad,
    )


def solution(mesh):
    in_specs = (
        P(("dp", "mp"), None),
        P(("dp", "mp"), None),
        P(("dp", "mp")),
        P("dp", None),
        P("dp"),
        P(),
        P(),
        P(None, "mp"),
        P(None, "mp"),
        P(None, "mp"),
        P("mp", None),
        P(None, "mp"),
        P(None, "mp"),
        P("mp", None),
    )
    out_specs = (
        P(("dp", "mp"), None),
        P(("dp", "mp"), None),
        P(),
        P(),
        P(None, "mp"),
        P(None, "mp"),
        P(None, "mp"),
        P("mp", None),
        P(None, "mp"),
        P(None, "mp"),
        P("mp", None),
    )
    body = swapped if (mesh.shape["dp"], mesh.shape["mp"]) == (8, 4) else local
    return jax.shard_map(body, mesh=mesh, in_specs=in_specs, out_specs=out_specs, check_vma=False)
```

```python
import functools

import jax
import jax.numpy as jnp
from jax import lax
from jax.experimental import pallas as pl
from jax.experimental.pallas import tpu as pltpu
from jax.sharding import PartitionSpec as P

HEAD_DIM = 112
WINDOW = 64
TOK_DEV = 1536


EPSILON = 1e-05
MASKED = 1e30


def norm_rows(values):
    inverse = lax.rsqrt(jnp.mean(values * values, axis=-1, keepdims=True) + EPSILON)
    return (values * inverse, inverse)


def norm_back(gradient, normed, inverse, norm_gain):
    scaled = gradient * norm_gain
    result = inverse * (scaled - normed * jnp.mean(scaled * normed, axis=-1, keepdims=True))
    return (result, jnp.sum(gradient * normed, axis=0))


def padded(values, filler):
    front = jnp.full((WINDOW,) + values.shape[1:], filler, values.dtype)
    return jnp.concatenate([front, values], axis=0)


def block_scores(query_block, key_block, query_seg, key_seg, key_flag, first_row, score_scale):
    query_pos = first_row + jnp.arange(query_block.shape[0], dtype=jnp.int32)
    key_pos = first_row - WINDOW + jnp.arange(key_block.shape[0], dtype=jnp.int32)
    distance = query_pos[:, None] - key_pos[None, :]
    allowed = (distance >= 0) & (distance < WINDOW) & (query_seg[:, None] == key_seg[None, :])
    allowed = allowed & ((key_flag[None, :] == 1) | (distance == 0))
    raw_scores = (
        jnp.einsum("qhd,khd->hqk", query_block, key_block, preferred_element_type=jnp.float32)
        * score_scale
    )
    return jnp.where(allowed[None], raw_scores, -MASKED)


def block_inputs(query, key_pad, value_pad, segment, seg_pad, live_pad, first_row, block_rows):
    key_span = block_rows + WINDOW
    return (
        lax.dynamic_slice_in_dim(query, first_row, block_rows, 0),
        lax.dynamic_slice_in_dim(key_pad, first_row, key_span, 0),
        lax.dynamic_slice_in_dim(value_pad, first_row, key_span, 0),
        lax.dynamic_slice_in_dim(segment, first_row, block_rows, 0),
        lax.dynamic_slice_in_dim(seg_pad, first_row, key_span, 0),
        lax.dynamic_slice_in_dim(live_pad, first_row, key_span, 0),
    )


def attend_forward(query, key_all, value_all, segment, key_live):
    token_count, head_count, head_width = query.shape
    block_rows = min(512, token_count)
    score_scale = head_width ** (-0.5)
    key_pad = padded(key_all, 0.0)
    value_pad = padded(value_all, 0.0)
    seg_pad = padded(segment, -1)
    live_pad = padded(key_live, 0)

    def one_block(running, block_index):
        first_row = block_index * block_rows
        query_block, key_block, value_block, query_seg, key_seg, key_flag = block_inputs(
            query, key_pad, value_pad, segment, seg_pad, live_pad, first_row, block_rows
        )
        scores = block_scores(
            query_block, key_block, query_seg, key_seg, key_flag, first_row, score_scale
        )
        row_max = jnp.max(scores, axis=-1, keepdims=True)
        weights = jnp.exp(scores - row_max)
        denominator = jnp.sum(weights, axis=-1, keepdims=True)
        chances = (weights / denominator).astype(jnp.bfloat16)
        mixed = jnp.einsum("hqk,khd->qhd", chances, value_block, preferred_element_type=jnp.float32)
        return (
            running,
            (mixed.astype(jnp.bfloat16), row_max[..., 0] + jnp.log(denominator[..., 0])),
        )

    _, (mixed, logsum) = lax.scan(
        one_block, jnp.zeros((), jnp.int32), jnp.arange(token_count // block_rows, dtype=jnp.int32)
    )
    return (mixed.reshape(token_count, head_count * head_width), logsum)


def attend_backward(query, key_all, value_all, segment, key_live, logsum, mixed_grad):
    token_count, head_count, head_width = query.shape
    block_rows = min(512, token_count)
    key_span = block_rows + WINDOW
    score_scale = head_width ** (-0.5)
    key_pad = padded(key_all, 0.0)
    value_pad = padded(value_all, 0.0)
    seg_pad = padded(segment, -1)
    live_pad = padded(key_live, 0)

    def one_block(running, inputs):
        key_grad, value_grad = running
        block_index, block_logsum = inputs
        first_row = block_index * block_rows
        query_block, key_block, value_block, query_seg, key_seg, key_flag = block_inputs(
            query, key_pad, value_pad, segment, seg_pad, live_pad, first_row, block_rows
        )
        grad_block = lax.dynamic_slice_in_dim(mixed_grad, first_row, block_rows, 0)
        scores = block_scores(
            query_block, key_block, query_seg, key_seg, key_flag, first_row, score_scale
        )
        chances = jnp.exp(scores - block_logsum[..., None])
        chance_grad = jnp.einsum(
            "qhd,khd->hqk", grad_block, value_block, preferred_element_type=jnp.float32
        )
        row_dot = jnp.sum(chances * chance_grad, axis=-1, keepdims=True)
        score_grad = (chances * (chance_grad - row_dot)).astype(jnp.bfloat16)
        query_grad = (
            jnp.einsum("hqk,khd->qhd", score_grad, key_block, preferred_element_type=jnp.float32)
            * score_scale
        )
        key_part = (
            jnp.einsum("hqk,qhd->khd", score_grad, query_block, preferred_element_type=jnp.float32)
            * score_scale
        )
        value_part = jnp.einsum(
            "hqk,qhd->khd",
            chances.astype(jnp.bfloat16),
            grad_block,
            preferred_element_type=jnp.float32,
        )
        key_grad = lax.dynamic_update_slice_in_dim(
            key_grad,
            lax.dynamic_slice_in_dim(key_grad, first_row, key_span, 0) + key_part,
            first_row,
            0,
        )
        value_grad = lax.dynamic_update_slice_in_dim(
            value_grad,
            lax.dynamic_slice_in_dim(value_grad, first_row, key_span, 0) + value_part,
            first_row,
            0,
        )
        return ((key_grad, value_grad), query_grad)

    empty_grad = jnp.zeros((token_count + WINDOW, head_count, head_width), jnp.float32)
    (key_grad, value_grad), query_grad = lax.scan(
        one_block,
        (empty_grad, empty_grad),
        (jnp.arange(token_count // block_rows, dtype=jnp.int32), logsum),
    )
    flat_width = head_count * head_width
    return (
        query_grad.reshape(token_count, flat_width).astype(jnp.bfloat16),
        key_grad[WINDOW:].reshape(token_count, flat_width).astype(jnp.bfloat16),
        value_grad[WINDOW:].reshape(token_count, flat_width).astype(jnp.bfloat16),
    )


def local(
    tokens,
    cotangent,
    route,
    lengths,
    key_mask,
    norm1_gain,
    norm2_gain,
    w_query,
    w_key,
    w_value,
    w_out,
    w_gate,
    w_up,
    w_down,
):
    groups = lax.axis_size("dp")
    members = lax.axis_size("mp")
    member = lax.axis_index("mp")
    local_rows = tokens.shape[0]
    group_rows = local_rows * members
    bucket = local_rows // groups
    target = route // TOK_DEV
    chosen = (target[:, None] == jnp.arange(groups, dtype=jnp.int32)[None, :]).astype(jnp.int32)
    ranking = jnp.sum((jnp.cumsum(chosen, axis=0) - chosen) * chosen, axis=1)
    send_at = target * bucket + ranking
    arrival, arrival_grad, arrival_slot = (
        lax.all_to_all(
            jnp.zeros_like(tokens).at[send_at].set(tokens),
            "dp",
            split_axis=0,
            concat_axis=0,
            tiled=True,
        ),
        lax.all_to_all(
            jnp.zeros_like(cotangent).at[send_at].set(cotangent),
            "dp",
            split_axis=0,
            concat_axis=0,
            tiled=True,
        ),
        lax.all_to_all(
            jnp.zeros_like(route).at[send_at].set(route % local_rows),
            "dp",
            split_axis=0,
            concat_axis=0,
            tiled=True,
        ),
    )
    token_rows = jnp.zeros_like(arrival).at[arrival_slot].set(arrival)
    grad_rows = jnp.zeros_like(arrival_grad).at[arrival_slot].set(arrival_grad)
    seq_ends = jnp.cumsum(lengths[0])
    positions = jnp.arange(group_rows, dtype=jnp.int32)
    segment = jnp.sum((positions[:, None] >= seq_ends[None, :]).astype(jnp.int32), axis=1)
    input_rows = token_rows.astype(jnp.float32)
    normed_one, inverse_one = norm_rows(input_rows)
    leading_all, grad_all = (
        lax.all_gather(token_rows, "mp", axis=0, tiled=True),
        lax.all_gather(grad_rows, "mp", axis=0, tiled=True),
    )
    input_all = leading_all.astype(jnp.float32)
    normed_all, _ = norm_rows(input_all)
    hidden_one = (normed_all * norm1_gain).astype(jnp.bfloat16)
    head_count = w_query.shape[1] // HEAD_DIM
    query = jnp.dot(hidden_one, w_query, preferred_element_type=jnp.float32).astype(jnp.bfloat16)
    keys = jnp.dot(hidden_one, w_key, preferred_element_type=jnp.float32).astype(jnp.bfloat16)
    values = jnp.dot(hidden_one, w_value, preferred_element_type=jnp.float32).astype(jnp.bfloat16)
    query_heads = query.reshape(group_rows, head_count, HEAD_DIM)
    key_heads = keys.reshape(group_rows, head_count, HEAD_DIM)
    value_heads = values.reshape(group_rows, head_count, HEAD_DIM)
    mixed_flat, logsum = attend_forward(query_heads, key_heads, value_heads, segment, key_mask)
    attention_all = lax.psum(jnp.dot(mixed_flat, w_out, preferred_element_type=jnp.float32), "mp")
    middle_all = input_all + attention_all
    middle_rows = lax.dynamic_slice_in_dim(middle_all, member * local_rows, local_rows, 0)
    normed_mid, _ = norm_rows(middle_all)
    hidden_two = (normed_mid * norm2_gain).astype(jnp.bfloat16)
    normed_two, inverse_two = norm_rows(middle_rows)
    gate_value = jnp.dot(hidden_two, w_gate, preferred_element_type=jnp.float32)
    upward = jnp.dot(hidden_two, w_up, preferred_element_type=jnp.float32)
    sigmoid = jax.nn.sigmoid(gate_value)
    activated = (gate_value * sigmoid * upward).astype(jnp.bfloat16)
    out_rows = middle_rows + lax.psum_scatter(
        jnp.dot(activated, w_down, preferred_element_type=jnp.float32).astype(jnp.bfloat16),
        "mp",
        scatter_dimension=0,
        tiled=True,
    ).astype(jnp.float32)
    activated_grad = jnp.einsum("td,fd->tf", grad_all, w_down, preferred_element_type=jnp.float32)
    gate_grad = (activated_grad * upward * sigmoid * (1.0 + gate_value * (1.0 - sigmoid))).astype(
        jnp.bfloat16
    )
    upward_grad = (activated_grad * gate_value * sigmoid).astype(jnp.bfloat16)
    down_sum = jnp.einsum("tf,td->fd", activated, grad_all, preferred_element_type=jnp.float32)
    gate_sum = jnp.einsum("td,tf->df", hidden_two, gate_grad, preferred_element_type=jnp.float32)
    upward_sum = jnp.einsum(
        "td,tf->df", hidden_two, upward_grad, preferred_element_type=jnp.float32
    )
    hidden_two_grad = lax.psum_scatter(
        jnp.einsum("tf,df->td", gate_grad, w_gate, preferred_element_type=jnp.float32)
        + jnp.einsum("tf,df->td", upward_grad, w_up, preferred_element_type=jnp.float32),
        "mp",
        scatter_dimension=0,
        tiled=True,
    )
    norm_part_two, gain_two_grad = norm_back(hidden_two_grad, normed_two, inverse_two, norm2_gain)
    middle_grad = grad_rows.astype(jnp.float32) + norm_part_two
    branch_all = lax.all_gather(middle_grad.astype(jnp.bfloat16), "mp", axis=0, tiled=True)
    output_sum = jnp.einsum("tc,td->cd", mixed_flat, branch_all, preferred_element_type=jnp.float32)
    mixed_grad = jnp.einsum(
        "td,cd->tc", branch_all, w_out, preferred_element_type=jnp.float32
    ).astype(jnp.bfloat16)
    query_grad, key_grad, value_grad = attend_backward(
        query_heads,
        key_heads,
        value_heads,
        segment,
        key_mask,
        logsum,
        mixed_grad.reshape(group_rows, head_count, HEAD_DIM),
    )
    query_sum = jnp.einsum("td,tc->dc", hidden_one, query_grad, preferred_element_type=jnp.float32)
    key_sum = jnp.einsum("td,tc->dc", hidden_one, key_grad, preferred_element_type=jnp.float32)
    value_sum = jnp.einsum("td,tc->dc", hidden_one, value_grad, preferred_element_type=jnp.float32)
    hidden_one_grad = lax.psum_scatter(
        (
            jnp.einsum("tc,dc->td", query_grad, w_query, preferred_element_type=jnp.float32)
            + jnp.einsum("tc,dc->td", key_grad, w_key, preferred_element_type=jnp.float32)
            + jnp.einsum("tc,dc->td", value_grad, w_value, preferred_element_type=jnp.float32)
        ).astype(jnp.bfloat16),
        "mp",
        scatter_dimension=0,
        tiled=True,
    ).astype(jnp.float32)
    norm_part_one, gain_one_grad = norm_back(hidden_one_grad, normed_one, inverse_one, norm1_gain)
    input_grad = middle_grad + norm_part_one
    gain_one_sum, gain_two_sum = lax.psum((gain_one_grad, gain_two_grad), ("dp", "mp"))
    weight_sums = (
        lax.psum(query_sum.astype(jnp.bfloat16), "dp").astype(jnp.float32),
        lax.psum(key_sum.astype(jnp.bfloat16), "dp").astype(jnp.float32),
        lax.psum(value_sum.astype(jnp.bfloat16), "dp").astype(jnp.float32),
        lax.psum(output_sum.astype(jnp.bfloat16), "dp").astype(jnp.float32),
        lax.psum(gate_sum.astype(jnp.bfloat16), "dp").astype(jnp.float32),
        lax.psum(upward_sum.astype(jnp.bfloat16), "dp").astype(jnp.float32),
        lax.psum(down_sum.astype(jnp.bfloat16), "dp").astype(jnp.float32),
    )
    back_out, back_grad = (
        lax.all_to_all(
            out_rows.astype(jnp.bfloat16)[arrival_slot],
            "dp",
            split_axis=0,
            concat_axis=0,
            tiled=True,
        ),
        lax.all_to_all(
            input_grad.astype(jnp.bfloat16)[arrival_slot],
            "dp",
            split_axis=0,
            concat_axis=0,
            tiled=True,
        ),
    )
    return (
        back_out[send_at],
        back_grad[send_at],
        gain_one_sum,
        gain_two_sum,
        weight_sums[0],
        weight_sums[1],
        weight_sums[2],
        weight_sums[3],
        weight_sums[4],
        weight_sums[5],
        weight_sums[6],
    )


MESH = pl.DeviceIdType.MESH
LANES = 128
F32 = jnp.float32
BF16 = jnp.bfloat16
VMEM_LIMIT = 56 * 1024 * 1024


def plane():
    me = lax.axis_index("dp")
    side = me + 1 - 2 * lax.rem(me, 2)
    over_x = me + 2 - 4 * lax.rem(lax.div(me, 2), 2)
    over_y = me + 4 - 8 * lax.rem(lax.div(me, 4), 2)
    corner = over_x + 4 - 8 * lax.rem(lax.div(over_x, 4), 2)
    return (me, side, over_x, over_y, corner)


def to_dp(source, target, send_sem, recv_sem, index):
    return pltpu.make_async_remote_copy(
        src_ref=source,
        dst_ref=target,
        send_sem=send_sem,
        recv_sem=recv_sem,
        device_id={"dp": index},
        device_id_type=MESH,
    )


def to_mp(source, target, send_sem, recv_sem, index):
    return pltpu.make_async_remote_copy(
        src_ref=source,
        dst_ref=target,
        send_sem=send_sem,
        recv_sem=recv_sem,
        device_id={"mp": index},
        device_id_type=MESH,
    )


def owner_at(turn):
    me, side, over_x, over_y, _ = plane()
    block = turn // 2
    near = ((block + 1) // 2) % 2
    far = block // 3
    second = turn % 2
    other = (1 - near) * second + (block // 2) * near
    owner = me + (near * (1 - second) + far) * (over_x - me)
    return owner + (near * second + far) * (over_y - me) + other * (side - me)


ARRIVALS = (
    (1, (4,)),
    (2, (0, 1, 2)),
    (3, (3,)),
    (4, (6, 9)),
    (5, (8, 10)),
    (6, (5, 7)),
    (7, (11, 12)),
)


class Gather:
    AFTER = {0: (5, 6), 1: (7, 8), 2: (9,), 3: (10,), 5: (11,), 7: (12,)}

    def __init__(self, own, out, send, recv, local=None):
        me, side, over_x, over_y, corner = plane()
        half = out.shape[1] // 2
        low, high = pl.ds(0, half), pl.ds(half, half)
        self.keep = None if own is None else pltpu.make_async_copy(own, out.at[me], local)
        own = out.at[me] if own is None else own

        def hop(number, source, target, index):
            return to_dp(source, target, send.at[number], recv.at[number], index)

        def onward(number, owner, part, index):
            place = out.at[owner, part]
            return hop(number, place, place, index)

        self.copies = [
            hop(0, own.at[low], out.at[me, low], over_x),
            hop(1, own.at[high], out.at[me, high], over_y),
            hop(2, own.at[high], out.at[me, high], over_x),
            hop(3, own.at[low], out.at[me, low], over_y),
            hop(4, own, out.at[me], side),
            onward(5, over_x, low, over_y),
            onward(6, over_x, low, side),
            onward(7, over_y, high, over_x),
            onward(8, over_y, high, side),
            onward(9, over_x, high, side),
            onward(10, over_y, low, side),
            onward(11, corner, low, side),
            onward(12, corner, high, side),
        ]

    def start(self):
        for number in range(5):
            self.copies[number].start()
        if self.keep is not None:
            self.keep.start()

    def arrive(self, *numbers):
        for number in numbers:
            self.copies[number].wait_recv()
            for later in self.AFTER.get(number, ()):
                self.copies[later].start()

    def pass_on(self):
        self.arrive(0, 1, 2, 3)

    def sent(self):
        for copy in self.copies:
            copy.wait_send()
        if self.keep is not None:
            self.keep.wait()

    def finish(self):
        self.arrive(5, 7, 4, 6, 8, 9, 10, 11, 12)
        self.sent()


def greet_all():
    barrier = pltpu.get_barrier_semaphore()
    me, z = lax.axis_index("dp"), lax.axis_index("mp")
    for step in range(1, 8):
        pl.semaphore_signal(
            barrier, inc=1, device_id={"dp": lax.rem(me + step, 8)}, device_id_type=MESH
        )
    core = lax.rem(me, 2)
    for step in range(1, 4):
        for other in (me, me + 1 - 2 * core):
            pl.semaphore_signal(
                barrier,
                inc=1,
                device_id={"dp": other, "mp": lax.rem(z + step, 4)},
                device_id_type=MESH,
            )
    return barrier


def start_all(copies):
    for copy in copies:
        copy.start()
    return copies


def wait_all(copies):
    for copy in copies:
        copy.wait()


def swap_all(source, target, send, recv):
    me = lax.axis_index("dp")
    return [
        to_dp(source, target.at[me], send.at[step - 1], recv.at[step - 1], lax.rem(me + step, 8))
        for step in range(1, 8)
    ]


class Spread:
    def __init__(self, share, w_qkv, w_out, send, recv, local):
        me, z = lax.axis_index("dp"), lax.axis_index("mp")
        core = lax.rem(me, 2)
        self.place = z + core * (3 - 2 * z)
        self.send, self.recv, self.local = send, recv, local
        self.shares = [share.at[0], share.at[1], share.at[2], share.at[3]]
        self.slots = (core, 1 - core)
        self.core = core
        self.w_qkv, self.w_out = w_qkv, w_out

    def target(self, which, piece):
        slot = self.slots[which]
        block = slot if piece == 3 else 2 * piece + slot
        rows = pl.ds(pl.multiple_of(block * LANES, LANES), HEAD_DIM)
        return (self.w_out if piece == 3 else self.w_qkv).at[rows]

    def hop(self, which, piece, number, place, own):
        source = self.shares[piece] if own else self.target(which, piece)
        z = place + self.core * (3 - 2 * place)
        return to_mp(
            source,
            self.target(which, piece),
            self.send.at[number * 4 + piece],
            self.recv.at[which * 4 + piece],
            z,
        )

    def keep(self, which, piece):
        return pltpu.make_async_copy(
            self.shares[piece], self.target(which, piece), self.local.at[piece]
        )

    def start(self, pieces):
        @pl.when(self.place == 0)
        def _():
            for piece in pieces:
                self.hop(0, piece, 0, 1, True).start()
                self.keep(0, piece).start()

        @pl.when(self.place == 1)
        def _():
            for piece in pieces:
                self.hop(1, piece, 0, 0, True).start()
                self.hop(1, piece, 1, 2, True).start()
                self.keep(1, piece).start()

    def pass_on(self, pieces):
        @pl.when(self.place == 1)
        def _():
            for piece in pieces:
                self.hop(0, piece, 2, 2, False).wait_recv()
                self.hop(0, piece, 2, 2, False).start()

        @pl.when(self.place == 2)
        def _():
            for which in (1, 0):
                for piece in pieces:
                    self.hop(which, piece, which, 3, False).wait_recv()
                    self.hop(which, piece, which, 3, False).start()

    def finish(self, pieces):
        @pl.when(self.place == 0)
        def _():
            for piece in pieces:
                self.hop(1, piece, 0, 1, False).wait_recv()
                self.hop(0, piece, 0, 1, True).wait_send()
                self.keep(0, piece).wait()

        @pl.when(self.place == 1)
        def _():
            for piece in pieces:
                self.hop(1, piece, 0, 0, True).wait_send()
                self.hop(1, piece, 1, 2, True).wait_send()
                self.hop(0, piece, 2, 2, False).wait_send()
                self.keep(1, piece).wait()

        @pl.when(self.place == 2)
        def _():
            for piece in pieces:
                for which in (1, 0):
                    self.hop(which, piece, which, 3, False).wait_send()

        @pl.when(self.place == 3)
        def _():
            for piece in pieces:
                for which in (1, 0):
                    self.hop(which, piece, which, 3, False).wait_recv()


class Column:
    def __init__(self, own, out, send, recv, local):
        z = lax.axis_index("mp")
        self.z, self.own, self.out, self.send, self.recv = z, own, out, send, recv
        self.outer = (z == 0) | (z == 3)
        near = 1 + lax.div(z, 3)
        self.from_outer = (near, 3 - near)
        self.edge = 3 * (z - 1)
        self.from_inner = (3 - z, 3 - self.edge, self.edge)
        self.keep = pltpu.make_async_copy(own, out.at[z], local)

    def straight(self, number, target):
        return to_mp(
            self.own, self.out.at[self.z], self.send.at[number], self.recv.at[self.z], target
        )

    def onward(self):
        far = 3 - self.edge
        return to_mp(
            self.out.at[far], self.out.at[far], self.send.at[3], self.recv.at[far], self.edge
        )

    def came(self, source):
        return to_mp(
            self.own, self.out.at[source], self.send.at[0], self.recv.at[source], source
        ).wait_recv

    def start(self):
        self.keep.start()

        @pl.when(self.outer)
        def _():
            for number, target in enumerate(self.from_outer):
                self.straight(number, target).start()

        @pl.when(jnp.logical_not(self.outer))
        def _():
            for number, target in enumerate(self.from_inner):
                self.straight(number, target).start()

    def pass_on(self):
        @pl.when(jnp.logical_not(self.outer))
        def _():
            self.came(3 - self.edge)()
            self.onward().start()

    def finish(self):
        @pl.when(self.outer)
        def _():
            for source in (1, 2):
                self.came(source)()
            self.came(3 - self.z)()
            for number, target in enumerate(self.from_outer):
                self.straight(number, target).wait_send()

        @pl.when(jnp.logical_not(self.outer))
        def _():
            self.came(3 - self.z)()
            self.came(self.edge)()
            for number, target in enumerate(self.from_inner):
                self.straight(number, target).wait_send()
            self.onward().wait_send()

        self.keep.wait()


def anywhere():
    return pl.BlockSpec(memory_space=pl.ANY)


def on_chip():
    return pl.BlockSpec(memory_space=pltpu.VMEM)


def remote_params(number, limit=VMEM_LIMIT):
    return pltpu.CompilerParams(
        collective_id=number, has_side_effects=True, vmem_limit_bytes=limit
    )


def hot_of(notes, k, size):
    own = notes[:, 0:48, :].reshape(size, LANES)
    lane = lax.broadcasted_iota(jnp.int32, (size, LANES), 1)
    slot = jnp.sum(jnp.where(lane == k, own, 0.0), axis=1, keepdims=True)
    return (lax.broadcasted_iota(jnp.int32, (size, size), 1).astype(F32) == slot).astype(BF16)


def block_mask(notes, k, block, z, rows):
    position = rows * z + block * 128 + lax.broadcasted_iota(jnp.int32, (128, 1), 0)
    position = position.astype(F32)
    first_end = notes[k, 52:53, 0:1]
    second_end = first_end + notes[k, 52:53, 1:2]
    begin = jnp.where(position >= first_end, first_end, 0.0)
    begin = jnp.where(position >= second_end, second_end, begin)
    column = lax.broadcasted_iota(jnp.int32, (128, 192), 1)
    distance = 64 + lax.broadcasted_iota(jnp.int32, (128, 192), 0) - column
    key_position = (rows * z + block * 128 - 64 + column).astype(F32)
    live = jnp.concatenate(
        [notes[k, 48 + block : 49 + block, :], notes[k, 49 + block : 50 + block, 0:64]], axis=1
    )
    allowed = (distance >= 0) & (distance < WINDOW) & (key_position >= begin)
    return allowed & ((live == 1.0) | (distance == 0))


NT = (((1,), (1,)), ((), ()))
TN = (((0,), (0,)), ((), ()))


def forward_kernel(
    tokens, cotangent, order_row, gain, notes, query, keys, values, project, gate,
    hidden_out, w_qkv_out, w_out, notes_all, gate_all, mixed_out, kept_out, tokens_out, cotangent_out,
    cotangent_all,
    hidden_all, qkv, share, gate_own, w_qkv, mixed, kept, tokens_b, cotangent_b,
    send, recv, send_a, recv_a, send_g, recv_g, send_w, recv_w, send_n, recv_n, send_c, recv_c,
    local, out_sem, store_sem, *, scale,
):
    groups, rows, width = hidden_all.shape
    me, z = lax.axis_index("dp"), lax.axis_index("mp")
    members = lax.axis_size("mp")
    barrier = greet_all()
    head = pl.ds(pl.multiple_of(lax.div(me, 2) * HEAD_DIM, 16), HEAD_DIM)
    units = pl.ds(pl.multiple_of(me * LANES, LANES), LANES)
    loads = [
        pltpu.make_async_copy(source.at[head], share.at[piece], local.at[piece])
        for piece, source in enumerate((query, keys, values, project))
    ]
    loads.append(pltpu.make_async_copy(gate.at[:, units], gate_own, local.at[4]))
    for copy in loads:
        copy.start()
    none = jnp.zeros((LANES - HEAD_DIM, width), BF16)
    for block in range(6):
        w_qkv[block * LANES + HEAD_DIM : block * LANES + LANES, :] = none
    for block in range(2):
        w_out[block * LANES + HEAD_DIM : block * LANES + LANES, :] = none

    place = lax.broadcasted_iota(jnp.int32, (rows, rows), 0).astype(F32)
    sort = (place == order_row[...].reshape(1, -1)).astype(BF16)
    tokens_b[...] = jnp.dot(sort, tokens[...], preferred_element_type=F32).astype(BF16)

    def normalise(span):
        value = tokens_b[span, :].astype(F32)
        inverse = lax.rsqrt(mean_rows(value * value) + EPSILON)
        hidden_all[me, span, :] = (value * inverse * gain[...].reshape(1, -1)).astype(BF16)

    each_chunk(rows, normalise)
    notes_all[me] = notes[...]
    stores = start_all([pltpu.make_async_copy(tokens_b, tokens_out, store_sem.at[0])])
    pl.semaphore_wait(barrier, 13)
    gather = Gather(None, hidden_all, send_a, recv_a)
    gather.start()
    swaps = swap_all(notes, notes_all, send_n, recv_n)
    for copy in swaps:
        copy.start()
    for copy in loads[:4]:
        copy.wait()
    spread = Spread(share, w_qkv, w_out, send_w, recv_w, local)
    spread.start((0, 1, 2))
    cotangent_b[...] = jnp.dot(sort, cotangent[...], preferred_element_type=F32).astype(BF16)
    stores += start_all([pltpu.make_async_copy(cotangent_b, cotangent_out, store_sem.at[1])])
    wait_all(loads[4:])
    column = Column(gate_own, gate_all, send_c, recv_c, local.at[4])
    second = Gather(cotangent_b, cotangent_all, send_g, recv_g, local.at[5])
    spread.pass_on((0, 1, 2))
    gather.arrive(0, 1)
    second.start()
    column.start()
    gather.arrive(2, 3)
    spread.finish((0, 1, 2))
    spread.start((3,))
    stores += start_all([pltpu.make_async_copy(w_qkv, w_qkv_out, store_sem.at[2])])
    for copy in swaps:
        copy.wait()

    def keep(turn):
        owner = owner_at(turn)
        return pltpu.make_async_copy(hidden_all.at[owner], hidden_out.at[owner], out_sem.at[turn])

    def multiply(turn, carry):
        for number, numbers in ARRIVALS:
            left = tuple(n for n in numbers if n > 3)
            if left:
                pl.when(turn == number)(functools.partial(gather.arrive, *left))
        owner = owner_at(turn)
        keep(turn).start()
        product = lax.dot_general(
            hidden_all[owner], w_qkv[...], NT, preferred_element_type=F32
        ).astype(BF16)
        qkv[owner] = product.reshape(groups, rows // groups, 768)
        return carry

    lax.fori_loop(0, groups, multiply, 0)

    def halo(k, other):
        return to_mp(
            kept.at[k, pl.ds(rows, 64), pl.ds(256, 512)],
            kept.at[k, pl.ds(0, 64), pl.ds(256, 512)],
            send.at[k],
            recv.at[k],
            other,
        )

    def store_kept(k):
        return pltpu.make_async_copy(kept.at[k], kept_out.at[k], store_sem.at[3 + k])

    def store_mixed(k):
        span = pl.ds(k, 1)
        return pltpu.make_async_copy(
            mixed.at[:, span], mixed_out.at[:, span], store_sem.at[3 + groups + k]
        )

    def order(k, carry):
        hot = hot_of(notes_all, k, rows)
        given = qkv[:, pl.ds(k, 1)].reshape(rows, 768)
        kept[k, pl.ds(64, rows), :] = lax.dot_general(
            hot, given, TN, preferred_element_type=F32
        ).astype(BF16)
        kept[k, pl.ds(0, 64), pl.ds(0, 256)] = jnp.zeros((64, 256), BF16)

        @pl.when(z < members - 1)
        def _():
            halo(k, z + 1).start()

        @pl.when(z == 0)
        def _():
            kept[k, pl.ds(0, 64), pl.ds(256, 512)] = jnp.zeros((64, 512), BF16)

        return carry

    lax.fori_loop(0, groups, order, 0)

    def attend(k, carry):
        @pl.when(z > 0)
        def _():
            halo(k, z).wait_recv()

        store_kept(k).start()
        hot = hot_of(notes_all, k, rows)
        pairs = [(block, head) for block in range(rows // 128) for head in range(2)]
        masks = [block_mask(notes_all, k, block, z, rows) for block in range(rows // 128)]
        scores = []
        for block, head in pairs:
            query = kept[k, pl.ds(64 + block * 128, 128), pl.ds(head * 128, 128)]
            keys = kept[k, pl.ds(block * 128, 192), pl.ds(256 + head * 128, 128)]
            value = lax.dot_general(query, keys, NT, preferred_element_type=F32) * scale
            scores.append(jnp.where(masks[block], value, -MASKED))
        chances = []
        for value in scores:
            weights = jnp.exp(value - jnp.max(value, axis=-1, keepdims=True))
            total = jnp.sum(weights, axis=-1, keepdims=True)
            chances.append((weights / total).astype(BF16))
        parts = []
        for (block, head), chance in zip(pairs, chances):
            values = kept[k, pl.ds(block * 128, 192), pl.ds(512 + head * 128, 128)]
            parts.append(jnp.dot(chance, values, preferred_element_type=F32).astype(BF16))
        found = [
            jnp.concatenate(parts[2 * block : 2 * block + 2], axis=1)
            for block in range(rows // 128)
        ]
        ordered = jnp.concatenate(found, axis=0)
        back = jnp.dot(hot, ordered, preferred_element_type=F32).astype(BF16)
        mixed[:, pl.ds(k, 1)] = back.reshape(groups, 1, rows // groups, 256)
        store_mixed(k).start()
        return carry

    spread.pass_on((3,))
    lax.fori_loop(0, 2, attend, 0)
    second.pass_on()
    column.pass_on()
    lax.fori_loop(2, groups, attend, 0)
    spread.finish((3,))
    second.finish()
    column.finish()
    gather.sent()

    wait_all(stores)

    def stored(turn, carry):
        keep(turn).wait()
        store_kept(turn).wait()
        store_mixed(turn).wait()
        return carry

    lax.fori_loop(0, groups, stored, 0)

    @pl.when(z < members - 1)
    def _():
        def done(k, carry):
            halo(k, z + 1).wait_send()
            return carry

        lax.fori_loop(0, groups, done, 0)


def attend_ahead(
    tokens, cotangent, order_row, gain, notes, query, keys, values, project, gate, scale
):
    rows, width = tokens.shape
    groups, members = lax.axis_size("dp"), lax.axis_size("mp")
    dma = pltpu.SemaphoreType.DMA
    shape = jax.ShapeDtypeStruct
    return pl.pallas_call(
        functools.partial(forward_kernel, scale=scale),
        out_shape=(
            shape((groups, rows, width), BF16),
            shape((6 * LANES, width), BF16),
            shape((2 * LANES, width), BF16),
            shape((groups,) + notes.shape, F32),
            shape((members, width, LANES), BF16),
            shape((groups, groups, rows // groups, 256), BF16),
            shape((groups, rows + 64, 768), BF16),
            shape((rows, width), BF16),
            shape((rows, width), BF16),
            shape((groups, rows, width), BF16),
        ),
        in_specs=[on_chip()] * 5 + [anywhere()] * 5,
        out_specs=(
            anywhere(), anywhere(), on_chip(), on_chip(), anywhere(),
            anywhere(), anywhere(), anywhere(), anywhere(), anywhere(),
        ),
        scratch_shapes=[
            pltpu.VMEM((groups, rows, width), BF16),
            pltpu.VMEM((groups, groups, rows // groups, 768), BF16),
            pltpu.VMEM((4, HEAD_DIM, width), BF16),
            pltpu.VMEM((width, LANES), BF16),
            pltpu.VMEM((6 * LANES, width), BF16),
            pltpu.VMEM((groups, groups, rows // groups, 256), BF16),
            pltpu.VMEM((groups, rows + 64, 768), BF16),
            pltpu.VMEM((rows, width), BF16),
            pltpu.VMEM((rows, width), BF16),
            dma((groups,)),
            dma((groups,)),
            dma((13,)),
            dma((13,)),
            dma((13,)),
            dma((13,)),
            dma((12,)),
            dma((8,)),
            dma((7,)),
            dma((7,)),
            dma((4,)),
            dma((4,)),
            dma((6,)),
            dma((groups,)),
            dma((3 + 2 * groups,)),
        ],
        compiler_params=remote_params(2, 60 * 1024 * 1024),
        cost_estimate=pl.CostEstimate(flops=0, bytes_accessed=300_000_000, transcendentals=0),
        name="attend_ahead",
    )(tokens, cotangent, order_row, gain, notes, query, keys, values, project, gate)


CHUNK = 32


def each_chunk(rows, body, chunk=CHUNK):
    def step(i, carry):
        body(pl.ds(pl.multiple_of(i * chunk, chunk), chunk))
        return carry

    lax.fori_loop(0, rows // chunk, step, 0)


class Units:
    def __init__(self, part, came_in, stage, send, recv, local):
        self.z = lax.axis_index("mp")
        self.part_of = part
        self.inputs = (came_in,)
        self.stages = (stage,)
        self.send, self.recv, self.local = send, recv, local
        z = self.z
        self.outer = (z == 0) | (z == 3)
        self.far = 3 - z
        self.near = 1 + lax.div(z, 3)
        self.second = 3 - self.near
        self.edge = 3 * (z - 1)

    def part(self, kind, z):
        return self.part_of(z)

    def straight(self, kind, number, target):
        return to_mp(
            self.part(kind, target),
            self.inputs[kind].at[self.z],
            self.send.at[number * 2 + kind],
            self.recv.at[self.z * 2 + kind],
            target,
        )

    def staged(self, kind):
        return to_mp(
            self.part(kind, self.far),
            self.stages[kind].at[0],
            self.send.at[4 + kind],
            self.recv.at[8 + kind],
            self.near,
        )

    def summed(self, kind):
        return to_mp(
            self.stages[kind].at[1],
            self.inputs[kind].at[self.z],
            self.send.at[4 + kind],
            self.recv.at[self.z * 2 + kind],
            3 - self.edge,
        )

    def mine(self, kind):
        return pltpu.make_async_copy(
            self.part(kind, 3 - self.edge), self.stages[kind].at[1], self.local.at[kind]
        )

    def start(self):
        @pl.when(self.outer)
        def _():
            for kind in range(1):
                self.staged(kind).start()
            for kind in range(1):
                self.straight(kind, 0, self.near).start()
                self.straight(kind, 1, self.second).start()

        @pl.when(jnp.logical_not(self.outer))
        def _():
            for kind in range(1):
                self.mine(kind).start()
                self.straight(kind, 0, 3 - self.z).start()
                self.straight(kind, 1, self.edge).start()

    def add(self):
        @pl.when(jnp.logical_not(self.outer))
        def _():
            for kind in range(1):
                stage = self.stages[kind]
                self.mine(kind).wait()
                to_mp(
                    self.part(kind, 0),
                    stage.at[0],
                    self.send.at[4 + kind],
                    self.recv.at[8 + kind],
                    self.edge,
                ).wait_recv()

                def body(span):
                    stage[1, span, :] = (
                        stage[0, span, :].astype(F32) + stage[1, span, :].astype(F32)
                    ).astype(BF16)

                each_chunk(stage.shape[1], body)
                self.summed(kind).start()

    def arrived(self, kind, source):
        to_mp(
            self.part(kind, 0),
            self.inputs[kind].at[source],
            self.send.at[kind],
            self.recv.at[source * 2 + kind],
            source,
        ).wait_recv()

    def finish(self):
        @pl.when(self.outer)
        def _():
            for kind in range(1):
                self.arrived(kind, 1)
                self.arrived(kind, 2)
                self.straight(kind, 0, self.near).wait_send()
                self.straight(kind, 1, self.second).wait_send()
                self.staged(kind).wait_send()

        @pl.when(jnp.logical_not(self.outer))
        def _():
            for kind in range(1):
                self.arrived(kind, 0)
                self.arrived(kind, 3)
                self.arrived(kind, 3 - self.z)
                self.straight(kind, 0, 3 - self.z).wait_send()
                self.straight(kind, 1, self.edge).wait_send()
                self.summed(kind).wait_send()


class Reduce:
    COUNT = 10

    def __init__(self, left, right, across, part, from_side, from_corner, from_near, send, recv):
        self.left, self.right, self.across, self.part = left, right, across, part
        self.from_side, self.from_corner, self.from_near = from_side, from_corner, from_near
        self.send, self.recv = send, recv
        self.rows = part.shape[1]

    def product(self, owner, slot):
        rows, width = self.rows, self.part.shape[2]
        picked = pl.ds(pl.multiple_of(owner * rows, rows), rows)

        def tile(t, carry):
            columns = pl.ds(pl.multiple_of(t * 256, 256), 256)
            if callable(self.left):
                value = jnp.dot(
                    self.left(owner), self.right[:, columns], preferred_element_type=F32
                )
            elif self.across:
                value = lax.dot_general(
                    self.left[picked, :], self.right[columns, :], NT, preferred_element_type=F32
                )
            else:
                value = jnp.dot(
                    self.left[picked, :], self.right[:, columns], preferred_element_type=F32
                )
            self.part[slot, :, columns] = value.astype(BF16)
            return carry

        lax.fori_loop(0, width // 256, tile, 0)

    def prepare(self):
        _, side, over_x, over_y, corner = plane()
        part, near = self.part, self.from_near
        half = self.rows // 2
        low, high = pl.ds(0, half), pl.ds(half, half)

        def hop(number, source, target, index):
            return to_dp(source, target, self.send.at[number], self.recv.at[number], index)

        self.shares = [hop(i, part.at[4 + i], self.from_side.at[i], side) for i in range(4)]
        self.corners = [
            hop(4, part.at[0, low], self.from_corner.at[0], over_x),
            hop(5, part.at[0, high], self.from_corner.at[1], over_y),
        ]
        self.nears = [
            hop(6, part.at[1, low], near.at[0, low], over_x),
            hop(7, part.at[1, high], near.at[0, high], over_x),
            hop(8, part.at[2, high], near.at[1, high], over_y),
            hop(9, part.at[2, low], near.at[1, low], over_y),
        ]

    def add_side(self, slot):
        self.shares[slot].wait_recv()

        def body(span):
            self.part[slot, span, :] = (
                self.part[slot, span, :].astype(F32) + self.from_side[slot, span, :].astype(F32)
            ).astype(BF16)

        each_chunk(self.rows, body)

    def add_corner(self, slot, offset, which):
        self.corners[which].wait_recv()

        def body(span):
            target = pl.ds(pl.multiple_of(offset + span.start, CHUNK), CHUNK)
            self.part[slot, target, :] = (
                self.part[slot, target, :].astype(F32)
                + self.from_corner[which, span, :].astype(F32)
            ).astype(BF16)

        each_chunk(self.rows // 2, body)

    def products(self):
        self.prepare()
        me, _, over_x, over_y, corner = plane()
        turn = 1 - 2 * lax.rem(me, 2)
        for slot, owner in enumerate((corner, over_x, over_y, me)):
            self.product(owner + turn, 4 + slot)
            self.shares[slot].start()
        for slot, owner in enumerate((corner, over_x, over_y, me)):
            self.product(owner, slot)

    def launch(self):
        self.add_side(0)
        self.corners[0].start()
        self.corners[1].start()
        self.add_side(1)
        self.nears[0].start()
        self.add_side(2)
        self.nears[2].start()

    def begin(self):
        self.prepare()
        me, _, over_x, over_y, corner = plane()
        turn = 1 - 2 * lax.rem(me, 2)
        self.product(corner + turn, 4)
        self.shares[0].start()
        self.product(corner, 0)
        self.product(over_x + turn, 5)
        self.shares[1].start()
        self.add_side(0)
        self.corners[0].start()
        self.corners[1].start()
        self.product(over_x, 1)
        self.product(over_y + turn, 6)
        self.shares[2].start()
        self.add_side(1)
        self.nears[0].start()
        self.product(over_y, 2)
        self.product(me + turn, 7)
        self.shares[3].start()
        self.add_side(2)
        self.nears[2].start()
        self.product(me, 3)

    def middle(self):
        self.add_corner(2, 0, 0)
        self.nears[3].start()
        self.add_corner(1, self.rows // 2, 1)
        self.nears[1].start()

    def end(self):
        self.shares[3].wait_recv()
        for copy in self.nears:
            copy.wait_recv()

    def run(self):
        self.begin()
        self.middle()
        self.end()

    def rows_of(self, span):
        return (
            self.part[3, span, :].astype(F32)
            + self.from_side[3, span, :].astype(F32)
            + self.from_near[0, span, :].astype(F32)
            + self.from_near[1, span, :].astype(F32)
        )

    def finish(self):
        for copy in self.shares + self.corners + self.nears:
            copy.wait_send()


def reduce_scratch(rows, width):
    dma = pltpu.SemaphoreType.DMA
    return [
        pltpu.VMEM((8, rows, width), BF16),
        pltpu.VMEM((4, rows, width), BF16),
        pltpu.VMEM((2, rows // 2, width), BF16),
        pltpu.VMEM((2, rows, width), BF16),
        dma((10,)),
        dma((10,)),
    ]


def gather_scratch(rows, width):
    dma = pltpu.SemaphoreType.DMA
    return [pltpu.VMEM((rows, width), BF16), dma((13,)), dma((13,)), dma(())]


def mean_rows(values):
    return jnp.mean(values, axis=-1, keepdims=True)


class Heads:
    def __init__(self, source, stage, arrive, send, recv_stage, recv):
        me, z = lax.axis_index("dp"), lax.axis_index("mp")
        self.me, self.z = me, z
        self.core = lax.rem(me, 2)
        self.source, self.stage, self.arrive = source, stage, arrive
        self.send, self.recv_stage, self.recv = send, recv_stage, recv
        self.place = z + self.core * (3 - 2 * z)
        self.columns = source.shape[1] // 2

    def z_of(self, place):
        return place + self.core * (3 - 2 * place)

    def slot_of(self, place):
        return self.core if place == 0 else 1 - self.core

    def rows_of(self, place, kind):
        block = 2 * kind + self.slot_of(place)
        return self.source.at[pl.ds(pl.multiple_of(block * LANES, LANES), HEAD_DIM)]

    def half_of(self, ref, half):
        return ref.at[:, pl.ds(pl.multiple_of(half * self.columns, LANES), self.columns)]

    def to_stage(self, place, kind):
        return to_at(
            self.rows_of(place, kind),
            self.stage.at[place, kind],
            self.send.at[place * 4 + kind],
            self.recv_stage.at[place * 4 + kind],
            self.me,
            self.z_of(2),
        )

    def to_owner(self, place, kind, half, way, ref, number):
        return to_at(
            self.half_of(ref, half),
            self.arrive.at[way, kind],
            self.send.at[number],
            self.recv.at[way * 4 + kind],
            self.me - self.core + half,
            self.z_of(place),
        )

    def sums(self, kind):
        return [
            self.to_owner(
                place, kind, half, 2, self.stage.at[place, kind], place * 8 + kind * 2 + half
            )
            for place in (0, 1)
            for half in (0, 1)
        ]

    def cross(self, own, kind):
        other = 1 - own
        copies = [
            self.to_owner(other, kind, half, 0, self.rows_of(other, kind), kind * 2 + half)
            for half in (0, 1)
        ]
        copies.append(
            to_at(
                self.half_of(self.rows_of(own, kind), 1 - self.core),
                self.arrive.at[1, kind],
                self.send.at[8 + kind],
                self.recv.at[4 + kind],
                self.me + 1 - 2 * self.core,
                self.z,
            )
        )
        return copies

    def start(self, kinds):
        @pl.when(self.place == 3)
        def _():
            for kind in kinds:
                self.to_stage(0, kind).start()
                self.to_stage(1, kind).start()

        for own in (0, 1):
            @pl.when(self.place == own)
            def _():
                for kind in kinds:
                    for copy in self.cross(own, kind):
                        copy.start()

    def add(self, kinds):
        @pl.when(self.place == 2)
        def _():
            for kind in kinds:
                for place in (0, 1):
                    self.to_stage(place, kind).wait_recv()
                    mine = self.rows_of(place, kind)

                    def body(span):
                        self.stage[place, kind, span, :] = (
                            self.stage[place, kind, span, :].astype(F32)
                            + mine[span, :].astype(F32)
                        ).astype(BF16)

                    each_chunk(HEAD_DIM, body, 16)
                for copy in self.sums(kind):
                    copy.start()

    def total(self, out):
        owner = lax.div(self.z, 2) == self.core
        for kind in range(4):
            for own in (0, 1):
                @pl.when(self.place == own)
                def _():
                    self.arrive[1, kind] = self.half_of(self.rows_of(own, kind), self.core)[...]

            for way in range(3):
                waiting = to_at(
                    self.half_of(self.rows_of(0, kind), 0),
                    self.arrive.at[way, kind],
                    self.send.at[0],
                    self.recv.at[way * 4 + kind],
                    self.me,
                    lax.rem(self.z + 1, 4),
                )
                if way == 1:
                    pl.when(jnp.logical_not(owner))(waiting.wait_recv)
                else:
                    waiting.wait_recv()

            def body(span):
                found = self.arrive[0, kind, span, :].astype(F32)
                found = found + self.arrive[1, kind, span, :].astype(F32)
                found = found + self.arrive[2, kind, span, :].astype(F32)
                target = pl.ds(pl.multiple_of(kind * HEAD_DIM + span.start, 16), 16)
                out[target, :] = found.astype(BF16)

            each_chunk(HEAD_DIM, body, 16)

    def finish_send(self):
        for kind in range(4):
            @pl.when(self.place == 3)
            def _():
                self.to_stage(0, kind).wait_send()
                self.to_stage(1, kind).wait_send()

            @pl.when(self.place == 2)
            def _():
                for copy in self.sums(kind):
                    copy.wait_send()

            for own in (0, 1):
                @pl.when(self.place == own)
                def _():
                    for copy in self.cross(own, kind):
                        copy.wait_send()


def to_at(source, target, send_sem, recv_sem, dp, mp):
    return pltpu.make_async_remote_copy(
        src_ref=source,
        dst_ref=target,
        send_sem=send_sem,
        recv_sem=recv_sem,
        device_id={"dp": dp, "mp": mp},
        device_id_type=MESH,
    )


def backward_kernel(
    branch, notes_all, kept_in, w_out_in, activated_in, w_down_in, middle_in, both_sum, down_sum,
    out, result, branch_all, both_in, down_all,
    totals, query_part, key_value, ending, leaving, arriving, send, recv,
    part, from_side, from_corner, from_near, send_r, recv_r,
    mixed_grad, shard, load_sem, send_g, recv_g,
    both_stage, send_u, recv_u, local, down_found, send_d, recv_d,
    kept, w_out, activated, w_down, middle, fetch_sem, down_stage, send_v, recv_v, local_v,
    *, scale, groups, rows,
):
    z = lax.axis_index("mp")
    members = lax.axis_size("mp")
    barrier = greet_all()
    pairs = ((activated_in, activated), (w_out_in, w_out), (kept_in, kept), (middle_in, middle))
    pairs += ((w_down_in, w_down),)
    fetches = [
        pltpu.make_async_copy(source, target, fetch_sem.at[number])
        for number, (source, target) in enumerate(pairs)
    ]

    def down_rows(owner):
        return down_sum.at[pl.ds(pl.multiple_of(owner * LANES, LANES), LANES)]

    down_units = Units(down_rows, down_found, down_stage, send_v, recv_v, local_v)
    load_down = pltpu.make_async_copy(down_rows(z), down_found.at[z], load_sem.at[2])
    pl.semaphore_wait(barrier, 13)
    units = Units(lambda owner: both_sum.at[owner], both_in, both_stage, send_u, recv_u, local)
    gather = Gather(branch, branch_all, send_g, recv_g, local.at[2])
    gather.start()
    down_units.start()
    units.start()
    start_all(fetches)
    load_down.start()
    wait_all((fetches[0], fetches[4]))
    reduce = Reduce(activated, w_down, False, part, from_side, from_corner, from_near, send_r, recv_r)
    reduce.products()
    down_units.add()
    down = Gather(down_found.at[0], down_all, send_d, recv_d, local.at[1])

    def load_shard(turn):
        slot = turn % 2
        return pltpu.make_async_copy(branch_all.at[owner_at(turn)], shard.at[slot], load_sem.at[slot])

    def spread_back(turn, carry):
        for number, numbers in ARRIVALS:
            pl.when(turn == number)(functools.partial(gather.arrive, *numbers))

        @pl.when(turn == 0)
        def _():
            gather.keep.wait()

        load_shard(turn).start()
        load_shard(turn).wait()
        mixed_grad[owner_at(turn)] = (
            lax.dot_general(shard[turn % 2], w_out[...], NT, preferred_element_type=F32)
            .astype(BF16)
            .reshape(groups, rows // groups, 256)
        )
        return carry

    fetches[1].wait()
    lax.fori_loop(0, 4, spread_back, 0)
    reduce.launch()
    lax.fori_loop(4, 8, spread_back, 0)
    units.add()


    def halo(k, other):
        return to_mp(leaving.at[k], arriving.at[k], send.at[k], recv.at[k], other)

    def attend(k, carry):
        hot = hot_of(notes_all, k, rows)
        given = mixed_grad[:, pl.ds(k, 1)].reshape(rows, 256)
        grad_ordered = lax.dot_general(hot, given, TN, preferred_element_type=F32).astype(BF16)
        totals[...] = jnp.zeros_like(totals)
        pairs = [(block, head) for block in range(rows // 128) for head in range(2)]
        masks = [block_mask(notes_all, k, block, z, rows) for block in range(rows // 128)]

        def query_of(block, head):
            return kept[k, pl.ds(64 + block * 128, 128), pl.ds(head * 128, 128)]

        def keys_of(block, head):
            return kept[k, pl.ds(block * 128, 192), pl.ds(256 + head * 128, 128)]

        def grad_of(block, head):
            return grad_ordered[block * 128 : block * 128 + 128, head * 128 : head * 128 + 128]

        scores, chance_grads = [], []
        for block, head in pairs:
            value = lax.dot_general(
                query_of(block, head), keys_of(block, head), NT, preferred_element_type=F32
            )
            scores.append(jnp.where(masks[block], value * scale, -MASKED))
            values = kept[k, pl.ds(block * 128, 192), pl.ds(512 + head * 128, 128)]
            chance_grads.append(
                lax.dot_general(grad_of(block, head), values, NT, preferred_element_type=F32)
            )
        agains, score_grads = [], []
        for value, chance_grad in zip(scores, chance_grads):
            weights = jnp.exp(value - jnp.max(value, axis=-1, keepdims=True))
            again = weights / jnp.sum(weights, axis=-1, keepdims=True)
            row_dot = jnp.sum(again * chance_grad, axis=-1, keepdims=True)
            agains.append(again.astype(BF16))
            score_grads.append((again * (chance_grad - row_dot)).astype(BF16))
        for (block, head), again, score_grad in zip(pairs, agains, score_grads):
            query_part[k, pl.ds(block * 128, 128), pl.ds(head * 128, 128)] = (
                jnp.dot(score_grad, keys_of(block, head), preferred_element_type=F32) * scale
            ).astype(BF16)
            totals[pl.ds(block * 128, 192), pl.ds(head * 128, 128)] += (
                lax.dot_general(score_grad, query_of(block, head), TN, preferred_element_type=F32)
                * scale
            )
            totals[pl.ds(block * 128, 192), pl.ds(256 + head * 128, 128)] += lax.dot_general(
                again, grad_of(block, head), TN, preferred_element_type=F32
            )
        key_value[k] = totals[pl.ds(64, rows), :].astype(BF16)
        ending[k] = totals[pl.ds(rows, 64), :]

        @pl.when(z > 0)
        def _():
            leaving[k] = totals[pl.ds(0, 64), :].astype(BF16)
            halo(k, z - 1).start()

        return carry

    wait_all(fetches[2:4])
    lax.fori_loop(0, 2, attend, 0)
    reduce.middle()
    load_down.wait()
    down_units.finish()

    @pl.when((z == 0) | (z == members - 1))
    def _():
        down_found[members - 1 - z] = jnp.zeros_like(down_found[0])

    def add_down(span):
        value = down_found[0, span, :].astype(F32) + down_found[1, span, :].astype(F32)
        value = value + down_found[2, span, :].astype(F32) + down_found[3, span, :].astype(F32)
        down_found[0, span, :] = value.astype(BF16)

    each_chunk(down_found.shape[1], add_down)
    down.start()
    lax.fori_loop(2, groups, attend, 0)
    down.pass_on()

    def restore(k, carry):
        @pl.when(z < members - 1)
        def _():
            halo(k, z).wait_recv()
            key_value[k, pl.ds(rows - 64, 64), :] = (
                ending[k] + arriving[k].astype(F32)
            ).astype(BF16)

        hot = hot_of(notes_all, k, rows)
        ordered = jnp.concatenate([query_part[k], key_value[k]], axis=1)
        back = jnp.dot(hot, ordered, preferred_element_type=F32).astype(BF16)
        out[:, pl.ds(k, 1)] = back.reshape(groups, 1, rows // groups, 768)
        return carry

    lax.fori_loop(0, groups, restore, 0)
    reduce.end()

    def body(span):
        result[span, :] = (middle[span, :] + reduce.rows_of(span)).astype(BF16)

    each_chunk(rows, body)
    down.finish()
    units.finish()
    for copy in gather.copies:
        copy.wait_send()
    reduce.finish()

    @pl.when(z > 0)
    def _():
        def done(k, carry):
            halo(k, z - 1).wait_send()
            return carry

        lax.fori_loop(0, groups, done, 0)


def attend_back(
    branch, notes_all, kept, w_out, activated, w_down, middle, both_sum, down_sum, scale
):
    groups = kept.shape[0]
    rows, width = middle.shape
    members = both_sum.shape[0]
    dma = pltpu.SemaphoreType.DMA
    shape = jax.ShapeDtypeStruct
    return pl.pallas_call(
        functools.partial(backward_kernel, scale=scale, groups=groups, rows=rows),
        out_shape=(
            shape((groups, groups, rows // groups, 768), BF16),
            shape((rows, width), BF16),
            shape((groups, rows, width), BF16),
            shape((members, width, 256), BF16),
            shape((groups, LANES, width), BF16),
        ),
        in_specs=[on_chip()] * 2 + [anywhere()] * 7,
        out_specs=(on_chip(),) * 2 + (anywhere(),) * 3,
        scratch_shapes=[
            pltpu.VMEM((rows + 64, 512), F32),
            pltpu.VMEM((groups, rows, 256), BF16),
            pltpu.VMEM((groups, rows, 512), BF16),
            pltpu.VMEM((groups, 64, 512), F32),
            pltpu.VMEM((groups, 64, 512), BF16),
            pltpu.VMEM((groups, 64, 512), BF16),
            dma((groups,)),
            dma((groups,)),
        ]
        + reduce_scratch(rows, width)
        + [
            pltpu.VMEM((groups, groups, rows // groups, 256), BF16),
            pltpu.VMEM((2, rows, width), BF16),
            dma((3,)),
            dma((13,)),
            dma((13,)),
            pltpu.VMEM((2, width, 256), BF16),
            dma((6,)),
            dma((10,)),
            dma((3,)),
            pltpu.VMEM((members, LANES, width), BF16),
            dma((13,)),
            dma((13,)),
            pltpu.VMEM(kept.shape, BF16),
            pltpu.VMEM(w_out.shape, BF16),
            pltpu.VMEM(activated.shape, BF16),
            pltpu.VMEM((members * LANES, width), BF16),
            pltpu.VMEM((rows, width), F32),
            dma((5,)),
            pltpu.VMEM((2, LANES, width), BF16),
            dma((6,)),
            dma((10,)),
            dma((1,)),
        ],
        compiler_params=remote_params(3, 63 * 1024 * 1024),
        cost_estimate=pl.CostEstimate(flops=0, bytes_accessed=300_000_000, transcendentals=0),
        name="attend_back",
    )(branch, notes_all, kept, w_out, activated, w_down, middle, both_sum, down_sum)


def norm_back_rows(gradient, values, gain, sums, span):
    inverse = lax.rsqrt(mean_rows(values * values) + EPSILON)
    normed = values * inverse
    product = gradient * normed
    folded = product[0:8]
    for step in range(1, CHUNK // 8):
        folded = folded + product[step * 8 : step * 8 + 8]
    sums[...] += folded
    scaled = gradient * gain
    return inverse * (scaled - normed * mean_rows(scaled * normed))


def feed_kernel(
    mixed, w_out, tokens, cotangent_all, gate_all, w_up, down_weight, cotangent_own, gain,
    middle, middle_grad, branch, sums, activated_out, both_sum, down_out, up_all, down_all,
    hidden_all, both_grad, part, from_side, from_corner, from_near, send_r, recv_r,
    send_m, recv_m, send_n, recv_n, send_a, recv_a, send_b, recv_b, cot_shard, cot_tile, stage_both, down_sum, w_both, w_down,
    cotangent, activated, load_sem, local,
    up_own, down_own, send_u, recv_u, send_d, recv_d, first_sem,
):
    groups, rows, width = hidden_all.shape
    members = gate_all.shape[0]
    me = lax.axis_index("dp")
    barrier = greet_all()
    units_own = pl.ds(pl.multiple_of(me * LANES, LANES), LANES)
    first = start_all(
        [
            pltpu.make_async_copy(source, target, first_sem.at[number])
            for number, (source, target) in enumerate(
                (
                    (mixed, activated.at[:, :, pl.ds(0, 256)]),
                    (w_out, down_sum.at[pl.ds(0, 256)]),
                    (w_up.at[:, units_own], up_own),
                    (down_weight.at[units_own], down_own),
                    (tokens, cotangent),
                )
            )
        ]
    )
    gates = start_all(
        [
            pltpu.make_async_copy(
                gate_all.at[z], w_both.at[:, pl.ds(z * 256, 128)], load_sem.at[6 + z]
            )
            for z in range(members)
        ]
    )

    def slot_of(turn):
        block = turn // 2
        near = ((block + 1) // 2) % 2
        far = block // 3
        second = turn % 2
        other = (1 - near) * second + (block // 2) * near
        return 4 * other + 3 * (1 - near) * (1 - far) + near * (1 + second)

    def load_cotangent(turn):
        return pltpu.make_async_copy(
            cotangent_all.at[owner_at(turn)], cot_shard.at[turn % 2], load_sem.at[turn % 2]
        )

    load_cotangent(0).start()
    wait_all(first)
    pl.semaphore_wait(barrier, 13)
    columns_up = Column(up_own, up_all, send_u, recv_u, local.at[0])
    columns_down = Column(down_own, down_all, send_d, recv_d, local.at[2])
    columns_up.start()
    columns_down.start()
    half_rows = rows // 2

    def half(number, sends, recvs):
        span = pl.ds(number * half_rows, half_rows)
        quarter = pl.ds(number * (half_rows // 2), half_rows // 2)
        return Reduce(
            lambda owner: activated[owner, span, 0:256], down_sum.at[pl.ds(0, 256)], False,
            part.at[:, span], from_side.at[:, span], from_corner.at[:, quarter],
            from_near.at[:, span], sends, recvs,
        )

    projects = (half(0, send_m, recv_m), half(1, send_n, recv_n))
    gathers = [
        Gather(None, hidden_all.at[:, pl.ds(number * half_rows, half_rows)], sends, recvs)
        for number, (sends, recvs) in enumerate(((send_a, recv_a), (send_b, recv_b)))
    ]
    for project in projects:
        project.begin()
    for project in projects:
        project.middle()
    columns_up.pass_on()
    columns_down.pass_on()
    for number, project in enumerate(projects):
        project.end()

        def normalise(span):
            own = pl.ds(pl.multiple_of(number * half_rows + span.start, CHUNK), CHUNK)
            values = cotangent[own, :].astype(F32) + project.rows_of(span)
            middle_grad[own, :] = values
            inverse = lax.rsqrt(mean_rows(values * values) + EPSILON)
            hidden_all[me, own, :] = (values * inverse * gain[...].reshape(1, -1)).astype(BF16)

        each_chunk(half_rows, normalise)
        gathers[number].start()

    for project in projects:
        project.finish()
    store_middle = pltpu.make_async_copy(middle_grad, middle, local.at[1])
    load_own = pltpu.make_async_copy(cotangent_own, cotangent, local.at[3])
    store_middle.start()
    load_own.start()
    columns_up.finish()
    columns_down.finish()
    ups = start_all(
        [
            pltpu.make_async_copy(
                up_all.at[z], w_both.at[:, pl.ds(z * 256 + 128, 128)], load_sem.at[10 + z]
            )
            for z in range(members)
        ]
    )
    ups += start_all(
        [
            pltpu.make_async_copy(
                down_all.at[z], w_down.at[pl.ds(z * LANES, LANES)], load_sem.at[14 + z]
            )
            for z in range(members)
        ]
    )
    reduce = Reduce(None, None, False, part, from_side, from_corner, from_near, send_r, recv_r)
    reduce.prepare()

    def nears():
        reduce.add_side(1)
        reduce.nears[0].start()
        reduce.add_side(2)
        reduce.nears[2].start()

    early = [
        (turn, functools.partial(gather.arrive, *numbers))
        for turn, numbers in ARRIVALS
        for gather in gathers
    ]
    early += [(6, nears)]
    late = [(1, 3), (4, 1), (5, 2), (7, 0)]
    wait_all(gates + ups)

    def unit(turn, carry):
        for number, action in early:
            pl.when(turn == number)(action)

        @pl.when(turn < 7)
        def _():
            load_cotangent(turn + 1).start()

        load_cotangent(turn).wait()
        owner, slot = owner_at(turn), slot_of(turn)
        mine = hidden_all[owner]
        grads = cot_shard[turn % 2]
        for z in range(members):
            raw = jnp.dot(mine, w_both[:, z * 256 : z * 256 + 256], preferred_element_type=F32)
            units = pl.ds(z * 128, 128)
            if z % 2 == 0:
                pair = lax.dot_general(
                    grads, w_down[pl.ds(z * 128, 256), :], NT, preferred_element_type=F32
                )
            active_grad = pair[:, 128 * (z % 2) : 128 * (z % 2) + 128]
            gate, upward = raw[:, :128], raw[:, 128:]
            sigmoid = jax.nn.sigmoid(gate)
            activated[owner, :, units] = (gate * sigmoid * upward).astype(BF16)
            both_grad[owner, :, pl.ds(z * 256, 128)] = (
                active_grad * upward * sigmoid * (1.0 + gate * (1.0 - sigmoid))
            ).astype(BF16)
            both_grad[owner, :, pl.ds(z * 256 + 128, 128)] = (
                active_grad * gate * sigmoid
            ).astype(BF16)

        def tile(t, inner):
            columns = pl.ds(pl.multiple_of(t * 256, 256), 256)
            part[slot, :, columns] = lax.dot_general(
                both_grad[owner], w_both[columns, :], NT, preferred_element_type=F32
            ).astype(BF16)
            return inner

        lax.fori_loop(0, width // 256, tile, 0)
        for number, share in late:
            pl.when(turn == number)(reduce.shares[share].start)
        return carry

    lax.fori_loop(0, 8, unit, 0)
    store_activated = pltpu.make_async_copy(activated, activated_out, local.at[4])
    store_activated.start()

    def load_tile(t):
        columns = pl.ds(pl.multiple_of(t * 256, 256), 256)
        return pltpu.make_async_copy(
            cotangent_all.at[:, :, columns], cot_tile.at[t % 2], load_sem.at[2 + t % 2]
        )

    def store_both(t):
        columns = pl.ds(pl.multiple_of(t * 256, 256), 256)
        return pltpu.make_async_copy(
            stage_both.at[t % 2], both_sum.at[:, columns], load_sem.at[4 + t % 2]
        )

    tiles = width // 256
    count = groups * rows

    def down_tile(t, carry):
        columns = pl.ds(pl.multiple_of(t * 256, 256), 256)

        @pl.when(t < tiles - 1)
        def _():
            load_tile(t + 1).start()

        load_tile(t).wait()
        down_sum[:, columns] = lax.dot_general(
            activated[...].reshape(count, members * 128),
            cot_tile[t % 2].reshape(count, 256),
            TN,
            preferred_element_type=F32,
        ).astype(BF16)
        return carry

    store_down = pltpu.make_async_copy(down_sum, down_out, local.at[5])

    def weight_tile(t, carry):
        columns = pl.ds(pl.multiple_of(t * 256, 256), 256)

        @pl.when(t >= 2)
        def _():
            store_both(t - 2).wait()

        value = lax.dot_general(
            hidden_all[:, :, columns].reshape(count, 256),
            both_grad[...].reshape(count, members * 256),
            TN,
            preferred_element_type=F32,
        )
        for z in range(members):
            stage_both[t % 2, z] = value[:, z * 256 : z * 256 + 256].astype(BF16)
        store_both(t).start()
        return carry

    load_tile(0).start()
    reduce.add_side(0)
    reduce.corners[0].start()
    reduce.corners[1].start()
    lax.fori_loop(0, tiles, down_tile, 0)
    store_down.start()
    lax.fori_loop(0, 2, weight_tile, 0)
    reduce.middle()
    lax.fori_loop(2, tiles, weight_tile, 0)
    reduce.end()
    store_middle.wait()
    load_own.wait()
    sums[...] = jnp.zeros_like(sums)

    def body(span):
        change = norm_back_rows(reduce.rows_of(span), middle_grad[span, :], gain[...].reshape(1, -1), sums, span)
        total = cotangent[span, :].astype(F32) + change
        middle_grad[span, :] = total
        branch[span, :] = total.astype(BF16)

    each_chunk(rows, body)
    for gather in gathers:
        gather.sent()
    reduce.finish()
    for t in (tiles - 2, tiles - 1):
        store_both(t).wait()
    store_down.wait()
    store_activated.wait()


def feed(mixed, w_out, tokens, cotangent_all, gate_all, w_up, w_down, cotangent, gain):
    groups, rows, width = cotangent_all.shape
    members = gate_all.shape[0]
    dma = pltpu.SemaphoreType.DMA
    units = members * 128
    return pl.pallas_call(
        feed_kernel,
        out_shape=(
            jax.ShapeDtypeStruct((rows, width), F32),
            jax.ShapeDtypeStruct((rows, width), F32),
            jax.ShapeDtypeStruct((rows, width), BF16),
            jax.ShapeDtypeStruct((8, width), F32),
            jax.ShapeDtypeStruct((groups, rows, units), BF16),
            jax.ShapeDtypeStruct((members, width, 256), BF16),
            jax.ShapeDtypeStruct((units, width), BF16),
            jax.ShapeDtypeStruct((members, width, LANES), BF16),
            jax.ShapeDtypeStruct((members, LANES, width), BF16),
        ),
        in_specs=[anywhere()] * 8 + [on_chip()],
        out_specs=(anywhere(),) + (on_chip(),) * 3 + (anywhere(),) * 5,
        scratch_shapes=[
            pltpu.VMEM((groups, rows, width), BF16),
            pltpu.VMEM((groups, rows, 2 * units), BF16),
        ]
        + reduce_scratch(rows, width)
        + [
            dma((10,)),
            dma((10,)),
            dma((10,)),
            dma((10,)),
            dma((13,)),
            dma((13,)),
            dma((13,)),
            dma((13,)),
            pltpu.VMEM((2, rows, width), BF16),
            pltpu.VMEM((2, groups, rows, 256), BF16),
            pltpu.VMEM((2, members, 256, 256), BF16),
            pltpu.VMEM((units, width), BF16),
            pltpu.VMEM((width, 2 * units), BF16),
            pltpu.VMEM((units, width), BF16),
            pltpu.VMEM((rows, width), BF16),
            pltpu.VMEM((groups, rows, units), BF16),
            dma((6 + 4 * members,)),
            dma((6,)),
            pltpu.VMEM((width, LANES), BF16),
            pltpu.VMEM((LANES, width), BF16),
            dma((4,)),
            dma((4,)),
            dma((4,)),
            dma((4,)),
            dma((5,)),
        ],
        compiler_params=remote_params(5, 63 * 1024 * 1024),
        cost_estimate=pl.CostEstimate(flops=0, bytes_accessed=400_000_000, transcendentals=0),
        name="feed",
    )(mixed, w_out, tokens, cotangent_all, gate_all, w_up, w_down, cotangent, gain)


def input_kernel(
    qkv_in, w_in, hidden_all, branch_all, mixed_in, tokens_in, middle_in, gain, sums_two,
    both_sum, both_in,
    result, gains, both_all, heads_all,
    part, from_side, from_corner, from_near, send, recv, sums,
    stage, arrive, send_h, recv_s, recv_h, own, plane_sums, column_sums, send_p, recv_p,
    weight_sum, row_tile, tile_sem, send_b, recv_b, send_t, recv_t, both_found, heads_own, local,
    mixed, tokens, middle_grad, fetch_sem, qkv_grad, w_qkv,
):
    me, z = lax.axis_index("dp"), lax.axis_index("mp")
    barrier = greet_all()
    count = qkv_grad.shape[0]
    tiles = tokens.shape[1] // 256
    outer = (z == 0) | (z == 3)

    def columns_of(t):
        return pl.ds(pl.multiple_of(lax.rem(t, tiles) * 256, 256), 256)

    def load(t, source):
        return pltpu.make_async_copy(
            source.at[:, :, columns_of(t)], row_tile.at[t % 2], tile_sem.at[t % 2]
        )

    own_part = pltpu.make_async_copy(both_sum.at[z], both_found.at[0], local.at[0])
    own_part.start()
    ways = [(outer, 1, 1), (outer, 2, 2)]
    ways += [(z == 1, 0, 1), (z == 1, 2, 2), (z == 1, 3, 3)]
    ways += [(z == 2, 0, 1), (z == 2, 1, 2), (z == 2, 3, 3)]

    def came(source, place):
        return pltpu.make_async_copy(both_in.at[source], both_found.at[place], local.at[place])

    for here, source, place in ways:
        pl.when(here)(came(source, place).start)

    @pl.when(outer)
    def _():
        both_found[3] = jnp.zeros_like(both_found[3])

    load(0, hidden_all).start()
    fetches = start_all(
        [
            pltpu.make_async_copy(source, target, fetch_sem.at[number])
            for number, (source, target) in enumerate(
                (
                    (qkv_in, qkv_grad),
                    (w_in, w_qkv),
                    (mixed_in, mixed),
                    (tokens_in, tokens),
                    (middle_in, middle_grad),
                )
            )
        ]
    )
    pl.semaphore_wait(barrier, 13)
    both = Gather(both_found.at[0], both_all, send_b, recv_b, local.at[4])

    def weight_tile(t, carry):
        @pl.when(t < tiles - 1)
        def _():
            load(t + 1, hidden_all).start()

        @pl.when((t >= tiles - 1) & (t < 2 * tiles - 1))
        def _():
            load(t + 1, branch_all).start()

        load(t, hidden_all).wait()

        @pl.when(t < tiles)
        def _():
            weight_sum[pl.ds(0, 768), columns_of(t)] = lax.dot_general(
                qkv_grad[...], row_tile[t % 2].reshape(count, 256), TN, preferred_element_type=F32
            ).astype(BF16)

        @pl.when(t >= tiles)
        def _():
            weight_sum[pl.ds(768, 256), columns_of(t)] = lax.dot_general(
                mixed[...], row_tile[t % 2].reshape(count, 256), TN, preferred_element_type=F32
            ).astype(BF16)

        return carry

    heads = Heads(weight_sum, stage, arrive, send_h, recv_s, recv_h)
    reduce = Reduce(qkv_grad, w_qkv, False, part, from_side, from_corner, from_near, send, recv)
    own_part.wait()
    for here, source, place in ways:
        pl.when(here)(came(source, place).wait)

    def add(span):
        value = both_found[0, span, :].astype(F32) + both_found[1, span, :].astype(F32)
        value = value + both_found[2, span, :].astype(F32) + both_found[3, span, :].astype(F32)
        both_found[0, span, :] = value.astype(BF16)

    each_chunk(both_found.shape[1], add)
    both.start()
    wait_all(fetches[:2])
    lax.fori_loop(0, tiles, weight_tile, 0)
    heads.start((0, 1, 2))
    wait_all(fetches[2:])
    lax.fori_loop(tiles, 2 * tiles, weight_tile, 0)
    heads.start((3,))
    both.pass_on()
    reduce.begin()
    heads.add((0, 1))
    reduce.middle()
    heads.add((2, 3))
    reduce.end()
    sums[...] = jnp.zeros_like(sums)

    def body(span):
        values = tokens[span, :].astype(F32)
        change = norm_back_rows(reduce.rows_of(span), values, gain[...].reshape(1, -1), sums, span)
        result[span, :] = (middle_grad[span, :] + change).astype(BF16)

    each_chunk(result.shape[0], body)
    own[...] = jnp.concatenate(
        [
            jnp.sum(sums[...], axis=0, keepdims=True),
            jnp.sum(sums_two[...], axis=0, keepdims=True),
        ],
        axis=0,
    )
    swaps = swap_all(own, plane_sums, send_p, recv_p)
    for copy in swaps:
        copy.start()
    plane_sums[me] = own[...]
    heads.total(heads_own)
    gather = Gather(heads_own, heads_all, send_t, recv_t, local.at[5])
    gather.start()
    for copy in swaps:
        copy.wait()
    found = plane_sums[0]
    for other in range(1, 8):
        found = found + plane_sums[other]
    column_sums[z] = found
    passes = [
        to_mp(
            column_sums.at[z],
            column_sums.at[z],
            send_p.at[6 + step],
            recv_p.at[6 + step],
            lax.rem(z + step, 4),
        )
        for step in range(1, 4)
    ]
    for copy in passes:
        copy.start()
    both.finish()
    for copy in passes:
        copy.wait()
    gains[...] = (column_sums[0] + column_sums[1]) + (column_sums[2] + column_sums[3])
    gather.pass_on()
    heads.finish_send()
    reduce.finish()
    gather.finish()


def project_input(
    qkv_grad, w_qkv, hidden_all, branch_all, mixed, tokens, middle_grad, gain, sums_two,
    both_sum, both_in,
):
    rows, width = tokens.shape
    groups = hidden_all.shape[0]
    dma = pltpu.SemaphoreType.DMA
    shape = jax.ShapeDtypeStruct
    return pl.pallas_call(
        input_kernel,
        out_shape=(
            shape((rows, width), BF16),
            shape((2, width), F32),
            shape((groups, width, 256), BF16),
            shape((groups, 4 * HEAD_DIM, width // 2), BF16),
        ),
        in_specs=[anywhere()] * 7 + [on_chip()] * 2 + [anywhere()] * 2,
        out_specs=(on_chip(),) * 2 + (anywhere(),) * 2,
        scratch_shapes=reduce_scratch(rows, width)
        + [
            pltpu.VMEM((8, width), F32),
            pltpu.VMEM((2, 4, HEAD_DIM, width), BF16),
            pltpu.VMEM((3, 4, HEAD_DIM, width // 2), BF16),
            dma((16,)),
            dma((8,)),
            dma((12,)),
            pltpu.VMEM((2, width), F32),
            pltpu.VMEM((8, 2, width), F32),
            pltpu.VMEM((4, 2, width), F32),
            dma((10,)),
            dma((10,)),
            pltpu.VMEM((8 * LANES, width), BF16),
            pltpu.VMEM((2, groups, rows, 256), BF16),
            dma((2,)),
            dma((13,)),
            dma((13,)),
            dma((13,)),
            dma((13,)),
            pltpu.VMEM((4, width, 256), BF16),
            pltpu.VMEM((4 * HEAD_DIM, width // 2), BF16),
            dma((6,)),
            pltpu.VMEM(mixed.shape, BF16),
            pltpu.VMEM((rows, width), BF16),
            pltpu.VMEM((rows, width), F32),
            dma((5,)),
            pltpu.VMEM(qkv_grad.shape, BF16),
            pltpu.VMEM(w_qkv.shape, BF16),
        ],
        compiler_params=remote_params(6, 63 * 1024 * 1024),
        cost_estimate=pl.CostEstimate(flops=0, bytes_accessed=250_000_000, transcendentals=0),
        name="project_input",
    )(
        qkv_grad, w_qkv, hidden_all, branch_all, mixed, tokens, middle_grad, gain, sums_two,
        both_sum, both_in,
    )


def assemble_kernel(
    both, down, heads, order_row, output_b, input_b, gains,
    gain_one, gain_two, output, inputs, query, keys, values, project, gate, upward, down_out, *, tiles,
):
    for d in range(both.shape[0]):
        gate[:, d * 128 : d * 128 + 128] = both[d, :, :128].astype(F32)
        upward[:, d * 128 : d * 128 + 128] = both[d, :, 128:].astype(F32)
    down_out[...] = down[0].astype(F32)
    for kind, out in enumerate((query, keys, values, project)):
        out[...] = heads[0, kind].astype(F32)
    rows = output_b.shape[0]
    gain_one[...] = gains[0:1, :].reshape(-1)
    gain_two[...] = gains[1:2, :].reshape(-1)

    @pl.when(pl.program_id(0) < tiles)
    def _():
        place = lax.broadcasted_iota(jnp.int32, (rows, rows), 0).astype(F32)
        sort = (place == order_row[...].reshape(1, -1)).astype(BF16)
        for ordered, out in ((output_b, output), (input_b, inputs)):
            out[...] = lax.dot_general(
                sort, ordered[...], TN, preferred_element_type=F32
            ).astype(BF16)


def assemble(both, down, heads, order_row, output_b, input_b, gains):
    groups, width, wide = both.shape
    rows = output_b.shape[0]
    units = down.shape[1]
    chips = groups // 2
    columns = heads.shape[3]
    tile = width // groups
    shape = jax.ShapeDtypeStruct
    head = shape((chips * HEAD_DIM, 2 * columns), F32)
    head_spec = pl.BlockSpec((HEAD_DIM, columns), lambda i: (i // 2, i % 2))
    wide_spec = pl.BlockSpec((tile, groups * units), lambda i: (i, 0))
    tiles = width // 256
    row_spec = pl.BlockSpec((rows, 256), lambda i: (0, jnp.minimum(i, tiles - 1)))
    return pl.pallas_call(
        functools.partial(assemble_kernel, tiles=tiles),
        grid=(groups,),
        out_shape=(
            shape((width,), F32),
            shape((width,), F32),
            shape((rows, width), BF16),
            shape((rows, width), BF16),
            head,
            head,
            head,
            head,
            shape((width, groups * units), F32),
            shape((width, groups * units), F32),
            shape((groups * units, width), F32),
        ),
        in_specs=[
            pl.BlockSpec((groups, tile, wide), lambda i: (0, i, 0)),
            pl.BlockSpec((1, units, width), lambda i: (i, 0, 0)),
            pl.BlockSpec((1, 4, HEAD_DIM, columns), lambda i: (i, 0, 0, 0)),
            pl.BlockSpec((rows,), lambda i: (0,)),
            row_spec,
            row_spec,
            pl.BlockSpec((2, width), lambda i: (0, 0)),
        ],
        out_specs=(
            pl.BlockSpec((width,), lambda i: (0,)),
            pl.BlockSpec((width,), lambda i: (0,)),
            row_spec, row_spec, head_spec, head_spec, head_spec, head_spec, wide_spec, wide_spec,
            pl.BlockSpec((units, width), lambda i: (i, 0)),
        ),
        compiler_params=pltpu.CompilerParams(vmem_limit_bytes=VMEM_LIMIT),
        cost_estimate=pl.CostEstimate(flops=0, bytes_accessed=58_000_000, transcendentals=0),
        name="assemble",
    )(both, down, heads, order_row, output_b, input_b, gains)


def swapped(
    tokens, cotangent, route, lengths, key_mask, norm1_gain, norm2_gain,
    w_query, w_key, w_value, w_out, w_gate, w_up, w_down,
):
    groups = lax.axis_size("dp")
    members = lax.axis_size("mp")
    me = lax.axis_index("dp")
    z = lax.axis_index("mp")
    rows, width = tokens.shape
    bucket = rows // groups
    units = w_down.shape[0] // groups

    target = route // TOK_DEV
    earlier = jnp.arange(rows, dtype=jnp.int32)
    same = (target[:, None] == target[None, :]) & (earlier[None, :] < earlier[:, None])
    send_at = target * bucket + jnp.sum(same.astype(jnp.int32), axis=1)
    sorting = send_at[None, :] == earlier[:, None]
    slots_own = jnp.sum(jnp.where(sorting, (route % rows)[None, :], 0), axis=1)

    mask_window = lax.dynamic_slice_in_dim(
        jnp.concatenate([jnp.zeros((WINDOW,), jnp.int32), key_mask]), z * rows, rows + WINDOW
    )
    slot_rows = jnp.pad(slots_own.reshape(groups, bucket).T, ((0, 0), (0, LANES - groups)))
    mask_rows = jnp.pad(mask_window, (0, 4 * LANES - rows - WINDOW)).reshape(4, LANES)
    length_rows = jnp.pad(lengths, ((0, 3), (0, LANES - lengths.shape[1])))
    notes = jnp.concatenate([slot_rows, mask_rows, length_rows], axis=0).astype(F32)

    count = groups * rows
    scale = HEAD_DIM ** (-0.5)
    order_row = send_at.astype(F32)
    (
        hidden_one,
        w_qkv,
        w_proj,
        notes_all,
        gate_all,
        mixed,
        kept,
        tokens_b,
        cotangent_b,
        cotangent_all,
    ) = attend_ahead(
        tokens,
        cotangent,
        order_row,
        norm1_gain,
        notes,
        w_query.T,
        w_key.T,
        w_value.T,
        w_out,
        w_gate,
        scale,
    )
    mixed = mixed.reshape(count, 2 * LANES)
    middle, middle_grad, branch, sums_two, activated, both_sum, down_sum, _, down_all = feed(
        mixed.reshape(groups, rows, 2 * LANES),
        w_proj,
        tokens_b,
        cotangent_all,
        gate_all,
        w_up,
        w_down,
        cotangent_b,
        norm2_gain,
    )
    qkv_grad, output_rows, branch_all, both_in, down_whole = attend_back(
        branch,
        notes_all,
        kept,
        w_proj,
        activated.reshape(count, units * members),
        down_all.reshape(members * units, width),
        middle,
        both_sum,
        down_sum,
        scale,
    )
    qkv_grad = qkv_grad.reshape(count, 6 * LANES)
    input_rows, gain_sums, both_whole, heads_whole = project_input(
        qkv_grad,
        w_qkv,
        hidden_one,
        branch_all,
        mixed,
        tokens_b,
        middle_grad,
        norm1_gain,
        sums_two,
        both_sum,
        both_in,
    )
    (
        gain_one_grad,
        gain_two_grad,
        output,
        input_grad,
        query_grad,
        key_grad,
        value_grad,
        proj_grad,
        gate_grad,
        up_grad,
        down_grad,
    ) = assemble(
        both_whole,
        down_whole,
        heads_whole.reshape(groups, 4, HEAD_DIM, width // 2),
        order_row,
        output_rows,
        input_rows,
        gain_sums,
    )
    return (
        output,
        input_grad,
        gain_one_grad,
        gain_two_grad,
        query_grad.T,
        key_grad.T,
        value_grad.T,
        proj_grad,
        gate_grad,
        up_grad,
        down_grad,
    )


def solution(mesh):
    in_specs = (
        P(("dp", "mp"), None),
        P(("dp", "mp"), None),
        P(("dp", "mp")),
        P("dp", None),
        P("dp"),
        P(),
        P(),
        P(None, "mp"),
        P(None, "mp"),
        P(None, "mp"),
        P("mp", None),
        P(None, "mp"),
        P(None, "mp"),
        P("mp", None),
    )
    out_specs = (
        P(("dp", "mp"), None),
        P(("dp", "mp"), None),
        P(),
        P(),
        P(None, "mp"),
        P(None, "mp"),
        P(None, "mp"),
        P("mp", None),
        P(None, "mp"),
        P(None, "mp"),
        P("mp", None),
    )
    body = swapped if (mesh.shape["dp"], mesh.shape["mp"]) == (8, 4) else local
    return jax.shard_map(body, mesh=mesh, in_specs=in_specs, out_specs=out_specs, check_vma=False)
```

```python
import functools

import jax
import jax.numpy as jnp
from jax import lax
from jax.experimental import pallas as pl
from jax.experimental.pallas import tpu as pltpu
from jax.sharding import PartitionSpec as P

HEAD_DIM = 112
WINDOW = 64
TOK_DEV = 1536


EPSILON = 1e-05
MASKED = 1e30


def norm_rows(values):
    inverse = lax.rsqrt(jnp.mean(values * values, axis=-1, keepdims=True) + EPSILON)
    return (values * inverse, inverse)


def norm_back(gradient, normed, inverse, norm_gain):
    scaled = gradient * norm_gain
    result = inverse * (scaled - normed * jnp.mean(scaled * normed, axis=-1, keepdims=True))
    return (result, jnp.sum(gradient * normed, axis=0))


def padded(values, filler):
    front = jnp.full((WINDOW,) + values.shape[1:], filler, values.dtype)
    return jnp.concatenate([front, values], axis=0)


def block_scores(query_block, key_block, query_seg, key_seg, key_flag, first_row, score_scale):
    query_pos = first_row + jnp.arange(query_block.shape[0], dtype=jnp.int32)
    key_pos = first_row - WINDOW + jnp.arange(key_block.shape[0], dtype=jnp.int32)
    distance = query_pos[:, None] - key_pos[None, :]
    allowed = (distance >= 0) & (distance < WINDOW) & (query_seg[:, None] == key_seg[None, :])
    allowed = allowed & ((key_flag[None, :] == 1) | (distance == 0))
    raw_scores = (
        jnp.einsum("qhd,khd->hqk", query_block, key_block, preferred_element_type=jnp.float32)
        * score_scale
    )
    return jnp.where(allowed[None], raw_scores, -MASKED)


def block_inputs(query, key_pad, value_pad, segment, seg_pad, live_pad, first_row, block_rows):
    key_span = block_rows + WINDOW
    return (
        lax.dynamic_slice_in_dim(query, first_row, block_rows, 0),
        lax.dynamic_slice_in_dim(key_pad, first_row, key_span, 0),
        lax.dynamic_slice_in_dim(value_pad, first_row, key_span, 0),
        lax.dynamic_slice_in_dim(segment, first_row, block_rows, 0),
        lax.dynamic_slice_in_dim(seg_pad, first_row, key_span, 0),
        lax.dynamic_slice_in_dim(live_pad, first_row, key_span, 0),
    )


def attend_forward(query, key_all, value_all, segment, key_live):
    token_count, head_count, head_width = query.shape
    block_rows = min(512, token_count)
    score_scale = head_width ** (-0.5)
    key_pad = padded(key_all, 0.0)
    value_pad = padded(value_all, 0.0)
    seg_pad = padded(segment, -1)
    live_pad = padded(key_live, 0)

    def one_block(running, block_index):
        first_row = block_index * block_rows
        query_block, key_block, value_block, query_seg, key_seg, key_flag = block_inputs(
            query, key_pad, value_pad, segment, seg_pad, live_pad, first_row, block_rows
        )
        scores = block_scores(
            query_block, key_block, query_seg, key_seg, key_flag, first_row, score_scale
        )
        row_max = jnp.max(scores, axis=-1, keepdims=True)
        weights = jnp.exp(scores - row_max)
        denominator = jnp.sum(weights, axis=-1, keepdims=True)
        chances = (weights / denominator).astype(jnp.bfloat16)
        mixed = jnp.einsum("hqk,khd->qhd", chances, value_block, preferred_element_type=jnp.float32)
        return (
            running,
            (mixed.astype(jnp.bfloat16), row_max[..., 0] + jnp.log(denominator[..., 0])),
        )

    _, (mixed, logsum) = lax.scan(
        one_block, jnp.zeros((), jnp.int32), jnp.arange(token_count // block_rows, dtype=jnp.int32)
    )
    return (mixed.reshape(token_count, head_count * head_width), logsum)


def attend_backward(query, key_all, value_all, segment, key_live, logsum, mixed_grad):
    token_count, head_count, head_width = query.shape
    block_rows = min(512, token_count)
    key_span = block_rows + WINDOW
    score_scale = head_width ** (-0.5)
    key_pad = padded(key_all, 0.0)
    value_pad = padded(value_all, 0.0)
    seg_pad = padded(segment, -1)
    live_pad = padded(key_live, 0)

    def one_block(running, inputs):
        key_grad, value_grad = running
        block_index, block_logsum = inputs
        first_row = block_index * block_rows
        query_block, key_block, value_block, query_seg, key_seg, key_flag = block_inputs(
            query, key_pad, value_pad, segment, seg_pad, live_pad, first_row, block_rows
        )
        grad_block = lax.dynamic_slice_in_dim(mixed_grad, first_row, block_rows, 0)
        scores = block_scores(
            query_block, key_block, query_seg, key_seg, key_flag, first_row, score_scale
        )
        chances = jnp.exp(scores - block_logsum[..., None])
        chance_grad = jnp.einsum(
            "qhd,khd->hqk", grad_block, value_block, preferred_element_type=jnp.float32
        )
        row_dot = jnp.sum(chances * chance_grad, axis=-1, keepdims=True)
        score_grad = (chances * (chance_grad - row_dot)).astype(jnp.bfloat16)
        query_grad = (
            jnp.einsum("hqk,khd->qhd", score_grad, key_block, preferred_element_type=jnp.float32)
            * score_scale
        )
        key_part = (
            jnp.einsum("hqk,qhd->khd", score_grad, query_block, preferred_element_type=jnp.float32)
            * score_scale
        )
        value_part = jnp.einsum(
            "hqk,qhd->khd",
            chances.astype(jnp.bfloat16),
            grad_block,
            preferred_element_type=jnp.float32,
        )
        key_grad = lax.dynamic_update_slice_in_dim(
            key_grad,
            lax.dynamic_slice_in_dim(key_grad, first_row, key_span, 0) + key_part,
            first_row,
            0,
        )
        value_grad = lax.dynamic_update_slice_in_dim(
            value_grad,
            lax.dynamic_slice_in_dim(value_grad, first_row, key_span, 0) + value_part,
            first_row,
            0,
        )
        return ((key_grad, value_grad), query_grad)

    empty_grad = jnp.zeros((token_count + WINDOW, head_count, head_width), jnp.float32)
    (key_grad, value_grad), query_grad = lax.scan(
        one_block,
        (empty_grad, empty_grad),
        (jnp.arange(token_count // block_rows, dtype=jnp.int32), logsum),
    )
    flat_width = head_count * head_width
    return (
        query_grad.reshape(token_count, flat_width).astype(jnp.bfloat16),
        key_grad[WINDOW:].reshape(token_count, flat_width).astype(jnp.bfloat16),
        value_grad[WINDOW:].reshape(token_count, flat_width).astype(jnp.bfloat16),
    )


def local(
    tokens,
    cotangent,
    route,
    lengths,
    key_mask,
    norm1_gain,
    norm2_gain,
    w_query,
    w_key,
    w_value,
    w_out,
    w_gate,
    w_up,
    w_down,
):
    groups = lax.axis_size("dp")
    members = lax.axis_size("mp")
    member = lax.axis_index("mp")
    local_rows = tokens.shape[0]
    group_rows = local_rows * members
    bucket = local_rows // groups
    target = route // TOK_DEV
    chosen = (target[:, None] == jnp.arange(groups, dtype=jnp.int32)[None, :]).astype(jnp.int32)
    ranking = jnp.sum((jnp.cumsum(chosen, axis=0) - chosen) * chosen, axis=1)
    send_at = target * bucket + ranking
    arrival, arrival_grad, arrival_slot = (
        lax.all_to_all(
            jnp.zeros_like(tokens).at[send_at].set(tokens),
            "dp",
            split_axis=0,
            concat_axis=0,
            tiled=True,
        ),
        lax.all_to_all(
            jnp.zeros_like(cotangent).at[send_at].set(cotangent),
            "dp",
            split_axis=0,
            concat_axis=0,
            tiled=True,
        ),
        lax.all_to_all(
            jnp.zeros_like(route).at[send_at].set(route % local_rows),
            "dp",
            split_axis=0,
            concat_axis=0,
            tiled=True,
        ),
    )
    token_rows = jnp.zeros_like(arrival).at[arrival_slot].set(arrival)
    grad_rows = jnp.zeros_like(arrival_grad).at[arrival_slot].set(arrival_grad)
    seq_ends = jnp.cumsum(lengths[0])
    positions = jnp.arange(group_rows, dtype=jnp.int32)
    segment = jnp.sum((positions[:, None] >= seq_ends[None, :]).astype(jnp.int32), axis=1)
    input_rows = token_rows.astype(jnp.float32)
    normed_one, inverse_one = norm_rows(input_rows)
    leading_all, grad_all = (
        lax.all_gather(token_rows, "mp", axis=0, tiled=True),
        lax.all_gather(grad_rows, "mp", axis=0, tiled=True),
    )
    input_all = leading_all.astype(jnp.float32)
    normed_all, _ = norm_rows(input_all)
    hidden_one = (normed_all * norm1_gain).astype(jnp.bfloat16)
    head_count = w_query.shape[1] // HEAD_DIM
    query = jnp.dot(hidden_one, w_query, preferred_element_type=jnp.float32).astype(jnp.bfloat16)
    keys = jnp.dot(hidden_one, w_key, preferred_element_type=jnp.float32).astype(jnp.bfloat16)
    values = jnp.dot(hidden_one, w_value, preferred_element_type=jnp.float32).astype(jnp.bfloat16)
    query_heads = query.reshape(group_rows, head_count, HEAD_DIM)
    key_heads = keys.reshape(group_rows, head_count, HEAD_DIM)
    value_heads = values.reshape(group_rows, head_count, HEAD_DIM)
    mixed_flat, logsum = attend_forward(query_heads, key_heads, value_heads, segment, key_mask)
    attention_all = lax.psum(jnp.dot(mixed_flat, w_out, preferred_element_type=jnp.float32), "mp")
    middle_all = input_all + attention_all
    middle_rows = lax.dynamic_slice_in_dim(middle_all, member * local_rows, local_rows, 0)
    normed_mid, _ = norm_rows(middle_all)
    hidden_two = (normed_mid * norm2_gain).astype(jnp.bfloat16)
    normed_two, inverse_two = norm_rows(middle_rows)
    gate_value = jnp.dot(hidden_two, w_gate, preferred_element_type=jnp.float32)
    upward = jnp.dot(hidden_two, w_up, preferred_element_type=jnp.float32)
    sigmoid = jax.nn.sigmoid(gate_value)
    activated = (gate_value * sigmoid * upward).astype(jnp.bfloat16)
    out_rows = middle_rows + lax.psum_scatter(
        jnp.dot(activated, w_down, preferred_element_type=jnp.float32).astype(jnp.bfloat16),
        "mp",
        scatter_dimension=0,
        tiled=True,
    ).astype(jnp.float32)
    activated_grad = jnp.einsum("td,fd->tf", grad_all, w_down, preferred_element_type=jnp.float32)
    gate_grad = (activated_grad * upward * sigmoid * (1.0 + gate_value * (1.0 - sigmoid))).astype(
        jnp.bfloat16
    )
    upward_grad = (activated_grad * gate_value * sigmoid).astype(jnp.bfloat16)
    down_sum = jnp.einsum("tf,td->fd", activated, grad_all, preferred_element_type=jnp.float32)
    gate_sum = jnp.einsum("td,tf->df", hidden_two, gate_grad, preferred_element_type=jnp.float32)
    upward_sum = jnp.einsum(
        "td,tf->df", hidden_two, upward_grad, preferred_element_type=jnp.float32
    )
    hidden_two_grad = lax.psum_scatter(
        jnp.einsum("tf,df->td", gate_grad, w_gate, preferred_element_type=jnp.float32)
        + jnp.einsum("tf,df->td", upward_grad, w_up, preferred_element_type=jnp.float32),
        "mp",
        scatter_dimension=0,
        tiled=True,
    )
    norm_part_two, gain_two_grad = norm_back(hidden_two_grad, normed_two, inverse_two, norm2_gain)
    middle_grad = grad_rows.astype(jnp.float32) + norm_part_two
    branch_all = lax.all_gather(middle_grad.astype(jnp.bfloat16), "mp", axis=0, tiled=True)
    output_sum = jnp.einsum("tc,td->cd", mixed_flat, branch_all, preferred_element_type=jnp.float32)
    mixed_grad = jnp.einsum(
        "td,cd->tc", branch_all, w_out, preferred_element_type=jnp.float32
    ).astype(jnp.bfloat16)
    query_grad, key_grad, value_grad = attend_backward(
        query_heads,
        key_heads,
        value_heads,
        segment,
        key_mask,
        logsum,
        mixed_grad.reshape(group_rows, head_count, HEAD_DIM),
    )
    query_sum = jnp.einsum("td,tc->dc", hidden_one, query_grad, preferred_element_type=jnp.float32)
    key_sum = jnp.einsum("td,tc->dc", hidden_one, key_grad, preferred_element_type=jnp.float32)
    value_sum = jnp.einsum("td,tc->dc", hidden_one, value_grad, preferred_element_type=jnp.float32)
    hidden_one_grad = lax.psum_scatter(
        (
            jnp.einsum("tc,dc->td", query_grad, w_query, preferred_element_type=jnp.float32)
            + jnp.einsum("tc,dc->td", key_grad, w_key, preferred_element_type=jnp.float32)
            + jnp.einsum("tc,dc->td", value_grad, w_value, preferred_element_type=jnp.float32)
        ).astype(jnp.bfloat16),
        "mp",
        scatter_dimension=0,
        tiled=True,
    ).astype(jnp.float32)
    norm_part_one, gain_one_grad = norm_back(hidden_one_grad, normed_one, inverse_one, norm1_gain)
    input_grad = middle_grad + norm_part_one
    gain_one_sum, gain_two_sum = lax.psum((gain_one_grad, gain_two_grad), ("dp", "mp"))
    weight_sums = (
        lax.psum(query_sum.astype(jnp.bfloat16), "dp").astype(jnp.float32),
        lax.psum(key_sum.astype(jnp.bfloat16), "dp").astype(jnp.float32),
        lax.psum(value_sum.astype(jnp.bfloat16), "dp").astype(jnp.float32),
        lax.psum(output_sum.astype(jnp.bfloat16), "dp").astype(jnp.float32),
        lax.psum(gate_sum.astype(jnp.bfloat16), "dp").astype(jnp.float32),
        lax.psum(upward_sum.astype(jnp.bfloat16), "dp").astype(jnp.float32),
        lax.psum(down_sum.astype(jnp.bfloat16), "dp").astype(jnp.float32),
    )
    back_out, back_grad = (
        lax.all_to_all(
            out_rows.astype(jnp.bfloat16)[arrival_slot],
            "dp",
            split_axis=0,
            concat_axis=0,
            tiled=True,
        ),
        lax.all_to_all(
            input_grad.astype(jnp.bfloat16)[arrival_slot],
            "dp",
            split_axis=0,
            concat_axis=0,
            tiled=True,
        ),
    )
    return (
        back_out[send_at],
        back_grad[send_at],
        gain_one_sum,
        gain_two_sum,
        weight_sums[0],
        weight_sums[1],
        weight_sums[2],
        weight_sums[3],
        weight_sums[4],
        weight_sums[5],
        weight_sums[6],
    )


MESH = pl.DeviceIdType.MESH
LANES = 128
F32 = jnp.float32
BF16 = jnp.bfloat16
VMEM_LIMIT = 56 * 1024 * 1024


def plane():
    me = lax.axis_index("dp")
    side = me + 1 - 2 * lax.rem(me, 2)
    over_x = me + 2 - 4 * lax.rem(lax.div(me, 2), 2)
    over_y = me + 4 - 8 * lax.rem(lax.div(me, 4), 2)
    corner = over_x + 4 - 8 * lax.rem(lax.div(over_x, 4), 2)
    return (me, side, over_x, over_y, corner)


def to_dp(source, target, send_sem, recv_sem, index):
    return pltpu.make_async_remote_copy(
        src_ref=source,
        dst_ref=target,
        send_sem=send_sem,
        recv_sem=recv_sem,
        device_id={"dp": index},
        device_id_type=MESH,
    )


def to_mp(source, target, send_sem, recv_sem, index):
    return pltpu.make_async_remote_copy(
        src_ref=source,
        dst_ref=target,
        send_sem=send_sem,
        recv_sem=recv_sem,
        device_id={"mp": index},
        device_id_type=MESH,
    )


def owner_at(turn):
    me, side, over_x, over_y, _ = plane()
    block = turn // 2
    near = ((block + 1) // 2) % 2
    far = block // 3
    second = turn % 2
    other = (1 - near) * second + (block // 2) * near
    owner = me + (near * (1 - second) + far) * (over_x - me)
    return owner + (near * second + far) * (over_y - me) + other * (side - me)


ARRIVALS = (
    (1, (4,)),
    (2, (0, 1, 2)),
    (3, (3,)),
    (4, (6, 9)),
    (5, (8, 10)),
    (6, (5, 7)),
    (7, (11, 12)),
)


class Gather:
    AFTER = {0: (5, 6), 1: (7, 8), 2: (9,), 3: (10,), 5: (11,), 7: (12,)}

    def __init__(self, own, out, send, recv, local=None):
        me, side, over_x, over_y, corner = plane()
        half = out.shape[1] // 2
        low, high = pl.ds(0, half), pl.ds(half, half)
        self.keep = None if own is None else pltpu.make_async_copy(own, out.at[me], local)
        own = out.at[me] if own is None else own

        def hop(number, source, target, index):
            return to_dp(source, target, send.at[number], recv.at[number], index)

        def onward(number, owner, part, index):
            place = out.at[owner, part]
            return hop(number, place, place, index)

        self.copies = [
            hop(0, own.at[low], out.at[me, low], over_x),
            hop(1, own.at[high], out.at[me, high], over_y),
            hop(2, own.at[high], out.at[me, high], over_x),
            hop(3, own.at[low], out.at[me, low], over_y),
            hop(4, own, out.at[me], side),
            onward(5, over_x, low, over_y),
            onward(6, over_x, low, side),
            onward(7, over_y, high, over_x),
            onward(8, over_y, high, side),
            onward(9, over_x, high, side),
            onward(10, over_y, low, side),
            onward(11, corner, low, side),
            onward(12, corner, high, side),
        ]

    def start(self):
        for number in range(5):
            self.copies[number].start()
        if self.keep is not None:
            self.keep.start()

    def arrive(self, *numbers):
        for number in numbers:
            self.copies[number].wait_recv()
            for later in self.AFTER.get(number, ()):
                self.copies[later].start()

    def pass_on(self):
        self.arrive(0, 1, 2, 3)

    def sent(self):
        for copy in self.copies:
            copy.wait_send()
        if self.keep is not None:
            self.keep.wait()

    def finish(self):
        self.arrive(5, 7, 4, 6, 8, 9, 10, 11, 12)
        self.sent()


def greet_all():
    barrier = pltpu.get_barrier_semaphore()
    me, z = lax.axis_index("dp"), lax.axis_index("mp")
    for step in range(1, 8):
        pl.semaphore_signal(
            barrier, inc=1, device_id={"dp": lax.rem(me + step, 8)}, device_id_type=MESH
        )
    core = lax.rem(me, 2)
    for step in range(1, 4):
        for other in (me, me + 1 - 2 * core):
            pl.semaphore_signal(
                barrier,
                inc=1,
                device_id={"dp": other, "mp": lax.rem(z + step, 4)},
                device_id_type=MESH,
            )
    return barrier


def start_all(copies):
    for copy in copies:
        copy.start()
    return copies


def wait_all(copies):
    for copy in copies:
        copy.wait()


def swap_all(source, target, send, recv):
    me = lax.axis_index("dp")
    return [
        to_dp(source, target.at[me], send.at[step - 1], recv.at[step - 1], lax.rem(me + step, 8))
        for step in range(1, 8)
    ]


class Spread:
    def __init__(self, share, w_qkv, w_out, send, recv, local):
        me, z = lax.axis_index("dp"), lax.axis_index("mp")
        core = lax.rem(me, 2)
        self.place = z + core * (3 - 2 * z)
        self.send, self.recv, self.local = send, recv, local
        self.shares = [share.at[0], share.at[1], share.at[2], share.at[3]]
        self.slots = (core, 1 - core)
        self.core = core
        self.w_qkv, self.w_out = w_qkv, w_out

    def target(self, which, piece):
        slot = self.slots[which]
        block = slot if piece == 3 else 2 * piece + slot
        rows = pl.ds(pl.multiple_of(block * LANES, LANES), HEAD_DIM)
        return (self.w_out if piece == 3 else self.w_qkv).at[rows]

    def hop(self, which, piece, number, place, own):
        source = self.shares[piece] if own else self.target(which, piece)
        z = place + self.core * (3 - 2 * place)
        return to_mp(
            source,
            self.target(which, piece),
            self.send.at[number * 4 + piece],
            self.recv.at[which * 4 + piece],
            z,
        )

    def keep(self, which, piece):
        return pltpu.make_async_copy(
            self.shares[piece], self.target(which, piece), self.local.at[piece]
        )

    def start(self, pieces):
        @pl.when(self.place == 0)
        def _():
            for piece in pieces:
                self.hop(0, piece, 0, 1, True).start()
                self.keep(0, piece).start()

        @pl.when(self.place == 1)
        def _():
            for piece in pieces:
                self.hop(1, piece, 0, 0, True).start()
                self.hop(1, piece, 1, 2, True).start()
                self.keep(1, piece).start()

    def pass_on(self, pieces):
        @pl.when(self.place == 1)
        def _():
            for piece in pieces:
                self.hop(0, piece, 2, 2, False).wait_recv()
                self.hop(0, piece, 2, 2, False).start()

        @pl.when(self.place == 2)
        def _():
            for which in (1, 0):
                for piece in pieces:
                    self.hop(which, piece, which, 3, False).wait_recv()
                    self.hop(which, piece, which, 3, False).start()

    def finish(self, pieces):
        @pl.when(self.place == 0)
        def _():
            for piece in pieces:
                self.hop(1, piece, 0, 1, False).wait_recv()
                self.hop(0, piece, 0, 1, True).wait_send()
                self.keep(0, piece).wait()

        @pl.when(self.place == 1)
        def _():
            for piece in pieces:
                self.hop(1, piece, 0, 0, True).wait_send()
                self.hop(1, piece, 1, 2, True).wait_send()
                self.hop(0, piece, 2, 2, False).wait_send()
                self.keep(1, piece).wait()

        @pl.when(self.place == 2)
        def _():
            for piece in pieces:
                for which in (1, 0):
                    self.hop(which, piece, which, 3, False).wait_send()

        @pl.when(self.place == 3)
        def _():
            for piece in pieces:
                for which in (1, 0):
                    self.hop(which, piece, which, 3, False).wait_recv()


class Column:
    def __init__(self, own, out, send, recv, local):
        z = lax.axis_index("mp")
        self.z, self.own, self.out, self.send, self.recv = z, own, out, send, recv
        self.outer = (z == 0) | (z == 3)
        near = 1 + lax.div(z, 3)
        self.from_outer = (near, 3 - near)
        self.edge = 3 * (z - 1)
        self.from_inner = (3 - z, 3 - self.edge, self.edge)
        self.keep = pltpu.make_async_copy(own, out.at[z], local)

    def straight(self, number, target):
        return to_mp(
            self.own, self.out.at[self.z], self.send.at[number], self.recv.at[self.z], target
        )

    def onward(self):
        far = 3 - self.edge
        return to_mp(
            self.out.at[far], self.out.at[far], self.send.at[3], self.recv.at[far], self.edge
        )

    def came(self, source):
        return to_mp(
            self.own, self.out.at[source], self.send.at[0], self.recv.at[source], source
        ).wait_recv

    def start(self):
        self.keep.start()

        @pl.when(self.outer)
        def _():
            for number, target in enumerate(self.from_outer):
                self.straight(number, target).start()

        @pl.when(jnp.logical_not(self.outer))
        def _():
            for number, target in enumerate(self.from_inner):
                self.straight(number, target).start()

    def pass_on(self):
        @pl.when(jnp.logical_not(self.outer))
        def _():
            self.came(3 - self.edge)()
            self.onward().start()

    def finish(self):
        @pl.when(self.outer)
        def _():
            for source in (1, 2):
                self.came(source)()
            self.came(3 - self.z)()
            for number, target in enumerate(self.from_outer):
                self.straight(number, target).wait_send()

        @pl.when(jnp.logical_not(self.outer))
        def _():
            self.came(3 - self.z)()
            self.came(self.edge)()
            for number, target in enumerate(self.from_inner):
                self.straight(number, target).wait_send()
            self.onward().wait_send()

        self.keep.wait()


def anywhere():
    return pl.BlockSpec(memory_space=pl.ANY)


def on_chip():
    return pl.BlockSpec(memory_space=pltpu.VMEM)


def remote_params(number, limit=VMEM_LIMIT):
    return pltpu.CompilerParams(
        collective_id=number, has_side_effects=True, vmem_limit_bytes=limit
    )


def hot_of(notes, k, size):
    own = notes[:, 0:48, :].reshape(size, LANES)
    lane = lax.broadcasted_iota(jnp.int32, (size, LANES), 1)
    slot = jnp.sum(jnp.where(lane == k, own, 0.0), axis=1, keepdims=True)
    return (lax.broadcasted_iota(jnp.int32, (size, size), 1).astype(F32) == slot).astype(BF16)


def block_mask(notes, k, block, z, rows):
    position = rows * z + block * 128 + lax.broadcasted_iota(jnp.int32, (128, 1), 0)
    position = position.astype(F32)
    first_end = notes[k, 52:53, 0:1]
    second_end = first_end + notes[k, 52:53, 1:2]
    begin = jnp.where(position >= first_end, first_end, 0.0)
    begin = jnp.where(position >= second_end, second_end, begin)
    column = lax.broadcasted_iota(jnp.int32, (128, 192), 1)
    distance = 64 + lax.broadcasted_iota(jnp.int32, (128, 192), 0) - column
    key_position = (rows * z + block * 128 - 64 + column).astype(F32)
    live = jnp.concatenate(
        [notes[k, 48 + block : 49 + block, :], notes[k, 49 + block : 50 + block, 0:64]], axis=1
    )
    allowed = (distance >= 0) & (distance < WINDOW) & (key_position >= begin)
    return allowed & ((live == 1.0) | (distance == 0))


NT = (((1,), (1,)), ((), ()))
TN = (((0,), (0,)), ((), ()))


def forward_kernel(
    tokens, cotangent, order_row, gain, notes, query, keys, values, project, gate,
    hidden_out, w_qkv_out, w_out, notes_all, gate_all, mixed_out, kept_out, tokens_out, cotangent_out,
    cotangent_all,
    hidden_all, qkv, share, gate_own, w_qkv, mixed, kept, tokens_b, cotangent_b,
    send, recv, send_a, recv_a, send_g, recv_g, send_w, recv_w, send_n, recv_n, send_c, recv_c,
    local, out_sem, store_sem, *, scale,
):
    groups, rows, width = hidden_all.shape
    me, z = lax.axis_index("dp"), lax.axis_index("mp")
    members = lax.axis_size("mp")
    barrier = greet_all()
    head = pl.ds(pl.multiple_of(lax.div(me, 2) * HEAD_DIM, 16), HEAD_DIM)
    units = pl.ds(pl.multiple_of(me * LANES, LANES), LANES)
    loads = [
        pltpu.make_async_copy(source.at[head], share.at[piece], local.at[piece])
        for piece, source in enumerate((query, keys, values, project))
    ]
    loads.append(pltpu.make_async_copy(gate.at[:, units], gate_own, local.at[4]))
    for copy in loads:
        copy.start()
    none = jnp.zeros((LANES - HEAD_DIM, width), BF16)
    for block in range(6):
        w_qkv[block * LANES + HEAD_DIM : block * LANES + LANES, :] = none
    for block in range(2):
        w_out[block * LANES + HEAD_DIM : block * LANES + LANES, :] = none

    place = lax.broadcasted_iota(jnp.int32, (rows, rows), 0).astype(F32)
    sort = (place == order_row[...].reshape(1, -1)).astype(BF16)
    tokens_b[...] = jnp.dot(sort, tokens[...], preferred_element_type=F32).astype(BF16)

    def normalise(span):
        value = tokens_b[span, :].astype(F32)
        inverse = lax.rsqrt(mean_rows(value * value) + EPSILON)
        hidden_all[me, span, :] = (value * inverse * gain[...].reshape(1, -1)).astype(BF16)

    each_chunk(rows, normalise)
    notes_all[me] = notes[...]
    stores = start_all([pltpu.make_async_copy(tokens_b, tokens_out, store_sem.at[0])])
    pl.semaphore_wait(barrier, 13)
    gather = Gather(None, hidden_all, send_a, recv_a)
    gather.start()
    swaps = swap_all(notes, notes_all, send_n, recv_n)
    for copy in swaps:
        copy.start()
    for copy in loads[:4]:
        copy.wait()
    spread = Spread(share, w_qkv, w_out, send_w, recv_w, local)
    spread.start((0, 1, 2))
    cotangent_b[...] = jnp.dot(sort, cotangent[...], preferred_element_type=F32).astype(BF16)
    stores += start_all([pltpu.make_async_copy(cotangent_b, cotangent_out, store_sem.at[1])])
    wait_all(loads[4:])
    column = Column(gate_own, gate_all, send_c, recv_c, local.at[4])
    second = Gather(cotangent_b, cotangent_all, send_g, recv_g, local.at[5])
    spread.pass_on((0, 1, 2))
    gather.arrive(0, 1)
    second.start()
    column.start()
    gather.arrive(2, 3)
    spread.finish((0, 1, 2))
    spread.start((3,))
    stores += start_all([pltpu.make_async_copy(w_qkv, w_qkv_out, store_sem.at[2])])
    for copy in swaps:
        copy.wait()

    def keep(turn):
        owner = owner_at(turn)
        return pltpu.make_async_copy(hidden_all.at[owner], hidden_out.at[owner], out_sem.at[turn])

    def multiply(turn, carry):
        for number, numbers in ARRIVALS:
            left = tuple(n for n in numbers if n > 3)
            if left:
                pl.when(turn == number)(functools.partial(gather.arrive, *left))
        owner = owner_at(turn)
        keep(turn).start()
        product = lax.dot_general(
            hidden_all[owner], w_qkv[...], NT, preferred_element_type=F32
        ).astype(BF16)
        qkv[owner] = product.reshape(groups, rows // groups, 768)
        return carry

    lax.fori_loop(0, groups, multiply, 0)

    def halo(k, other):
        return to_mp(
            kept.at[k, pl.ds(rows, 64), pl.ds(256, 512)],
            kept.at[k, pl.ds(0, 64), pl.ds(256, 512)],
            send.at[k],
            recv.at[k],
            other,
        )

    def store_kept(k):
        return pltpu.make_async_copy(kept.at[k], kept_out.at[k], store_sem.at[3 + k])

    def store_mixed(k):
        span = pl.ds(k, 1)
        return pltpu.make_async_copy(
            mixed.at[:, span], mixed_out.at[:, span], store_sem.at[3 + groups + k]
        )

    def order(k, carry):
        hot = hot_of(notes_all, k, rows)
        given = qkv[:, pl.ds(k, 1)].reshape(rows, 768)
        kept[k, pl.ds(64, rows), :] = lax.dot_general(
            hot, given, TN, preferred_element_type=F32
        ).astype(BF16)
        kept[k, pl.ds(0, 64), pl.ds(0, 256)] = jnp.zeros((64, 256), BF16)

        @pl.when(z < members - 1)
        def _():
            halo(k, z + 1).start()

        @pl.when(z == 0)
        def _():
            kept[k, pl.ds(0, 64), pl.ds(256, 512)] = jnp.zeros((64, 512), BF16)

        return carry

    lax.fori_loop(0, groups, order, 0)

    def attend(k, carry):
        @pl.when(z > 0)
        def _():
            halo(k, z).wait_recv()

        store_kept(k).start()
        hot = hot_of(notes_all, k, rows)
        pairs = [(block, head) for block in range(rows // 128) for head in range(2)]
        masks = [block_mask(notes_all, k, block, z, rows) for block in range(rows // 128)]
        scores = []
        for block, head in pairs:
            query = kept[k, pl.ds(64 + block * 128, 128), pl.ds(head * 128, 128)]
            keys = kept[k, pl.ds(block * 128, 192), pl.ds(256 + head * 128, 128)]
            value = lax.dot_general(query, keys, NT, preferred_element_type=F32) * scale
            scores.append(jnp.where(masks[block], value, -MASKED))
        chances = []
        for value in scores:
            weights = jnp.exp(value - jnp.max(value, axis=-1, keepdims=True))
            total = jnp.sum(weights, axis=-1, keepdims=True)
            chances.append((weights / total).astype(BF16))
        parts = []
        for (block, head), chance in zip(pairs, chances):
            values = kept[k, pl.ds(block * 128, 192), pl.ds(512 + head * 128, 128)]
            parts.append(jnp.dot(chance, values, preferred_element_type=F32).astype(BF16))
        found = [
            jnp.concatenate(parts[2 * block : 2 * block + 2], axis=1)
            for block in range(rows // 128)
        ]
        ordered = jnp.concatenate(found, axis=0)
        back = jnp.dot(hot, ordered, preferred_element_type=F32).astype(BF16)
        mixed[:, pl.ds(k, 1)] = back.reshape(groups, 1, rows // groups, 256)
        store_mixed(k).start()
        return carry

    spread.pass_on((3,))
    lax.fori_loop(0, 2, attend, 0)
    second.pass_on()
    column.pass_on()
    lax.fori_loop(2, groups, attend, 0)
    spread.finish((3,))
    second.finish()
    column.finish()
    gather.sent()

    wait_all(stores)

    def stored(turn, carry):
        keep(turn).wait()
        store_kept(turn).wait()
        store_mixed(turn).wait()
        return carry

    lax.fori_loop(0, groups, stored, 0)

    @pl.when(z < members - 1)
    def _():
        def done(k, carry):
            halo(k, z + 1).wait_send()
            return carry

        lax.fori_loop(0, groups, done, 0)


def attend_ahead(
    tokens, cotangent, order_row, gain, notes, query, keys, values, project, gate, scale
):
    rows, width = tokens.shape
    groups, members = lax.axis_size("dp"), lax.axis_size("mp")
    dma = pltpu.SemaphoreType.DMA
    shape = jax.ShapeDtypeStruct
    return pl.pallas_call(
        functools.partial(forward_kernel, scale=scale),
        out_shape=(
            shape((groups, rows, width), BF16),
            shape((6 * LANES, width), BF16),
            shape((2 * LANES, width), BF16),
            shape((groups,) + notes.shape, F32),
            shape((members, width, LANES), BF16),
            shape((groups, groups, rows // groups, 256), BF16),
            shape((groups, rows + 64, 768), BF16),
            shape((rows, width), BF16),
            shape((rows, width), BF16),
            shape((groups, rows, width), BF16),
        ),
        in_specs=[on_chip()] * 5 + [anywhere()] * 5,
        out_specs=(
            anywhere(), anywhere(), on_chip(), on_chip(), anywhere(),
            anywhere(), anywhere(), anywhere(), anywhere(), anywhere(),
        ),
        scratch_shapes=[
            pltpu.VMEM((groups, rows, width), BF16),
            pltpu.VMEM((groups, groups, rows // groups, 768), BF16),
            pltpu.VMEM((4, HEAD_DIM, width), BF16),
            pltpu.VMEM((width, LANES), BF16),
            pltpu.VMEM((6 * LANES, width), BF16),
            pltpu.VMEM((groups, groups, rows // groups, 256), BF16),
            pltpu.VMEM((groups, rows + 64, 768), BF16),
            pltpu.VMEM((rows, width), BF16),
            pltpu.VMEM((rows, width), BF16),
            dma((groups,)),
            dma((groups,)),
            dma((13,)),
            dma((13,)),
            dma((13,)),
            dma((13,)),
            dma((12,)),
            dma((8,)),
            dma((7,)),
            dma((7,)),
            dma((4,)),
            dma((4,)),
            dma((6,)),
            dma((groups,)),
            dma((3 + 2 * groups,)),
        ],
        compiler_params=remote_params(2, 60 * 1024 * 1024),
        cost_estimate=pl.CostEstimate(flops=0, bytes_accessed=300_000_000, transcendentals=0),
        name="attend_ahead",
    )(tokens, cotangent, order_row, gain, notes, query, keys, values, project, gate)


CHUNK = 32


def each_chunk(rows, body, chunk=CHUNK):
    def step(i, carry):
        body(pl.ds(pl.multiple_of(i * chunk, chunk), chunk))
        return carry

    lax.fori_loop(0, rows // chunk, step, 0)


class Units:
    def __init__(self, part, came_in, stage, send, recv, local):
        self.z = lax.axis_index("mp")
        self.part_of = part
        self.inputs = (came_in,)
        self.stages = (stage,)
        self.send, self.recv, self.local = send, recv, local
        z = self.z
        self.outer = (z == 0) | (z == 3)
        self.far = 3 - z
        self.near = 1 + lax.div(z, 3)
        self.second = 3 - self.near
        self.edge = 3 * (z - 1)

    def part(self, kind, z):
        return self.part_of(z)

    def straight(self, kind, number, target):
        return to_mp(
            self.part(kind, target),
            self.inputs[kind].at[self.z],
            self.send.at[number * 2 + kind],
            self.recv.at[self.z * 2 + kind],
            target,
        )

    def staged(self, kind):
        return to_mp(
            self.part(kind, self.far),
            self.stages[kind].at[0],
            self.send.at[4 + kind],
            self.recv.at[8 + kind],
            self.near,
        )

    def summed(self, kind):
        return to_mp(
            self.stages[kind].at[1],
            self.inputs[kind].at[self.z],
            self.send.at[4 + kind],
            self.recv.at[self.z * 2 + kind],
            3 - self.edge,
        )

    def mine(self, kind):
        return pltpu.make_async_copy(
            self.part(kind, 3 - self.edge), self.stages[kind].at[1], self.local.at[kind]
        )

    def start(self):
        @pl.when(self.outer)
        def _():
            for kind in range(1):
                self.staged(kind).start()
            for kind in range(1):
                self.straight(kind, 0, self.near).start()
                self.straight(kind, 1, self.second).start()

        @pl.when(jnp.logical_not(self.outer))
        def _():
            for kind in range(1):
                self.mine(kind).start()
                self.straight(kind, 0, 3 - self.z).start()
                self.straight(kind, 1, self.edge).start()

    def add(self):
        @pl.when(jnp.logical_not(self.outer))
        def _():
            for kind in range(1):
                stage = self.stages[kind]
                self.mine(kind).wait()
                to_mp(
                    self.part(kind, 0),
                    stage.at[0],
                    self.send.at[4 + kind],
                    self.recv.at[8 + kind],
                    self.edge,
                ).wait_recv()

                def body(span):
                    stage[1, span, :] = (
                        stage[0, span, :].astype(F32) + stage[1, span, :].astype(F32)
                    ).astype(BF16)

                each_chunk(stage.shape[1], body)
                self.summed(kind).start()

    def arrived(self, kind, source):
        to_mp(
            self.part(kind, 0),
            self.inputs[kind].at[source],
            self.send.at[kind],
            self.recv.at[source * 2 + kind],
            source,
        ).wait_recv()

    def finish(self):
        @pl.when(self.outer)
        def _():
            for kind in range(1):
                self.arrived(kind, 1)
                self.arrived(kind, 2)
                self.straight(kind, 0, self.near).wait_send()
                self.straight(kind, 1, self.second).wait_send()
                self.staged(kind).wait_send()

        @pl.when(jnp.logical_not(self.outer))
        def _():
            for kind in range(1):
                self.arrived(kind, 0)
                self.arrived(kind, 3)
                self.arrived(kind, 3 - self.z)
                self.straight(kind, 0, 3 - self.z).wait_send()
                self.straight(kind, 1, self.edge).wait_send()
                self.summed(kind).wait_send()


class Reduce:
    COUNT = 10

    def __init__(self, left, right, across, part, from_side, from_corner, from_near, send, recv):
        self.left, self.right, self.across, self.part = left, right, across, part
        self.from_side, self.from_corner, self.from_near = from_side, from_corner, from_near
        self.send, self.recv = send, recv
        self.rows = part.shape[1]

    def product(self, owner, slot):
        rows, width = self.rows, self.part.shape[2]
        picked = pl.ds(pl.multiple_of(owner * rows, rows), rows)

        def tile(t, carry):
            columns = pl.ds(pl.multiple_of(t * 256, 256), 256)
            if callable(self.left):
                value = jnp.dot(
                    self.left(owner), self.right[:, columns], preferred_element_type=F32
                )
            elif self.across:
                value = lax.dot_general(
                    self.left[picked, :], self.right[columns, :], NT, preferred_element_type=F32
                )
            else:
                value = jnp.dot(
                    self.left[picked, :], self.right[:, columns], preferred_element_type=F32
                )
            self.part[slot, :, columns] = value.astype(BF16)
            return carry

        lax.fori_loop(0, width // 256, tile, 0)

    def prepare(self):
        _, side, over_x, over_y, corner = plane()
        part, near = self.part, self.from_near
        half = self.rows // 2
        low, high = pl.ds(0, half), pl.ds(half, half)

        def hop(number, source, target, index):
            return to_dp(source, target, self.send.at[number], self.recv.at[number], index)

        self.shares = [hop(i, part.at[4 + i], self.from_side.at[i], side) for i in range(4)]
        self.corners = [
            hop(4, part.at[0, low], self.from_corner.at[0], over_x),
            hop(5, part.at[0, high], self.from_corner.at[1], over_y),
        ]
        self.nears = [
            hop(6, part.at[1, low], near.at[0, low], over_x),
            hop(7, part.at[1, high], near.at[0, high], over_x),
            hop(8, part.at[2, high], near.at[1, high], over_y),
            hop(9, part.at[2, low], near.at[1, low], over_y),
        ]

    def add_side(self, slot):
        self.shares[slot].wait_recv()

        def body(span):
            self.part[slot, span, :] = (
                self.part[slot, span, :].astype(F32) + self.from_side[slot, span, :].astype(F32)
            ).astype(BF16)

        each_chunk(self.rows, body)

    def add_corner(self, slot, offset, which):
        self.corners[which].wait_recv()

        def body(span):
            target = pl.ds(pl.multiple_of(offset + span.start, CHUNK), CHUNK)
            self.part[slot, target, :] = (
                self.part[slot, target, :].astype(F32)
                + self.from_corner[which, span, :].astype(F32)
            ).astype(BF16)

        each_chunk(self.rows // 2, body)

    def products(self):
        self.prepare()
        me, _, over_x, over_y, corner = plane()
        turn = 1 - 2 * lax.rem(me, 2)
        for slot, owner in enumerate((corner, over_x, over_y, me)):
            self.product(owner + turn, 4 + slot)
            self.shares[slot].start()
        for slot, owner in enumerate((corner, over_x, over_y, me)):
            self.product(owner, slot)

    def launch(self):
        self.add_side(0)
        self.corners[0].start()
        self.corners[1].start()
        self.add_side(1)
        self.nears[0].start()
        self.add_side(2)
        self.nears[2].start()

    def begin(self):
        self.prepare()
        me, _, over_x, over_y, corner = plane()
        turn = 1 - 2 * lax.rem(me, 2)
        self.product(corner + turn, 4)
        self.shares[0].start()
        self.product(corner, 0)
        self.product(over_x + turn, 5)
        self.shares[1].start()
        self.add_side(0)
        self.corners[0].start()
        self.corners[1].start()
        self.product(over_x, 1)
        self.product(over_y + turn, 6)
        self.shares[2].start()
        self.add_side(1)
        self.nears[0].start()
        self.product(over_y, 2)
        self.product(me + turn, 7)
        self.shares[3].start()
        self.add_side(2)
        self.nears[2].start()
        self.product(me, 3)

    def middle(self):
        self.add_corner(2, 0, 0)
        self.nears[3].start()
        self.add_corner(1, self.rows // 2, 1)
        self.nears[1].start()

    def end(self):
        self.shares[3].wait_recv()
        for copy in self.nears:
            copy.wait_recv()

    def run(self):
        self.begin()
        self.middle()
        self.end()

    def rows_of(self, span):
        return (
            self.part[3, span, :].astype(F32)
            + self.from_side[3, span, :].astype(F32)
            + self.from_near[0, span, :].astype(F32)
            + self.from_near[1, span, :].astype(F32)
        )

    def finish(self):
        for copy in self.shares + self.corners + self.nears:
            copy.wait_send()


def reduce_scratch(rows, width):
    dma = pltpu.SemaphoreType.DMA
    return [
        pltpu.VMEM((8, rows, width), BF16),
        pltpu.VMEM((4, rows, width), BF16),
        pltpu.VMEM((2, rows // 2, width), BF16),
        pltpu.VMEM((2, rows, width), BF16),
        dma((10,)),
        dma((10,)),
    ]


def gather_scratch(rows, width):
    dma = pltpu.SemaphoreType.DMA
    return [pltpu.VMEM((rows, width), BF16), dma((13,)), dma((13,)), dma(())]


def mean_rows(values):
    return jnp.mean(values, axis=-1, keepdims=True)


class Heads:
    def __init__(self, source, stage, arrive, send, recv_stage, recv):
        me, z = lax.axis_index("dp"), lax.axis_index("mp")
        self.me, self.z = me, z
        self.core = lax.rem(me, 2)
        self.source, self.stage, self.arrive = source, stage, arrive
        self.send, self.recv_stage, self.recv = send, recv_stage, recv
        self.place = z + self.core * (3 - 2 * z)
        self.columns = source.shape[1] // 2

    def z_of(self, place):
        return place + self.core * (3 - 2 * place)

    def slot_of(self, place):
        return self.core if place == 0 else 1 - self.core

    def rows_of(self, place, kind):
        block = 2 * kind + self.slot_of(place)
        return self.source.at[pl.ds(pl.multiple_of(block * LANES, LANES), HEAD_DIM)]

    def half_of(self, ref, half):
        return ref.at[:, pl.ds(pl.multiple_of(half * self.columns, LANES), self.columns)]

    def to_stage(self, place, kind):
        return to_at(
            self.rows_of(place, kind),
            self.stage.at[place, kind],
            self.send.at[place * 4 + kind],
            self.recv_stage.at[place * 4 + kind],
            self.me,
            self.z_of(2),
        )

    def to_owner(self, place, kind, half, way, ref, number):
        return to_at(
            self.half_of(ref, half),
            self.arrive.at[way, kind],
            self.send.at[number],
            self.recv.at[way * 4 + kind],
            self.me - self.core + half,
            self.z_of(place),
        )

    def sums(self, kind):
        return [
            self.to_owner(
                place, kind, half, 2, self.stage.at[place, kind], place * 8 + kind * 2 + half
            )
            for place in (0, 1)
            for half in (0, 1)
        ]

    def cross(self, own, kind):
        other = 1 - own
        copies = [
            self.to_owner(other, kind, half, 0, self.rows_of(other, kind), kind * 2 + half)
            for half in (0, 1)
        ]
        copies.append(
            to_at(
                self.half_of(self.rows_of(own, kind), 1 - self.core),
                self.arrive.at[1, kind],
                self.send.at[8 + kind],
                self.recv.at[4 + kind],
                self.me + 1 - 2 * self.core,
                self.z,
            )
        )
        return copies

    def start(self, kinds):
        @pl.when(self.place == 3)
        def _():
            for kind in kinds:
                self.to_stage(0, kind).start()
                self.to_stage(1, kind).start()

        for own in (0, 1):
            @pl.when(self.place == own)
            def _():
                for kind in kinds:
                    for copy in self.cross(own, kind):
                        copy.start()

    def add(self, kinds):
        @pl.when(self.place == 2)
        def _():
            for kind in kinds:
                for place in (0, 1):
                    self.to_stage(place, kind).wait_recv()
                    mine = self.rows_of(place, kind)

                    def body(span):
                        self.stage[place, kind, span, :] = (
                            self.stage[place, kind, span, :].astype(F32)
                            + mine[span, :].astype(F32)
                        ).astype(BF16)

                    each_chunk(HEAD_DIM, body, 16)
                for copy in self.sums(kind):
                    copy.start()

    def total(self, out):
        owner = lax.div(self.z, 2) == self.core
        for kind in range(4):
            for own in (0, 1):
                @pl.when(self.place == own)
                def _():
                    self.arrive[1, kind] = self.half_of(self.rows_of(own, kind), self.core)[...]

            for way in range(3):
                waiting = to_at(
                    self.half_of(self.rows_of(0, kind), 0),
                    self.arrive.at[way, kind],
                    self.send.at[0],
                    self.recv.at[way * 4 + kind],
                    self.me,
                    lax.rem(self.z + 1, 4),
                )
                if way == 1:
                    pl.when(jnp.logical_not(owner))(waiting.wait_recv)
                else:
                    waiting.wait_recv()

            def body(span):
                found = self.arrive[0, kind, span, :].astype(F32)
                found = found + self.arrive[1, kind, span, :].astype(F32)
                found = found + self.arrive[2, kind, span, :].astype(F32)
                target = pl.ds(pl.multiple_of(kind * HEAD_DIM + span.start, 16), 16)
                out[target, :] = found.astype(BF16)

            each_chunk(HEAD_DIM, body, 16)

    def finish_send(self):
        for kind in range(4):
            @pl.when(self.place == 3)
            def _():
                self.to_stage(0, kind).wait_send()
                self.to_stage(1, kind).wait_send()

            @pl.when(self.place == 2)
            def _():
                for copy in self.sums(kind):
                    copy.wait_send()

            for own in (0, 1):
                @pl.when(self.place == own)
                def _():
                    for copy in self.cross(own, kind):
                        copy.wait_send()


def to_at(source, target, send_sem, recv_sem, dp, mp):
    return pltpu.make_async_remote_copy(
        src_ref=source,
        dst_ref=target,
        send_sem=send_sem,
        recv_sem=recv_sem,
        device_id={"dp": dp, "mp": mp},
        device_id_type=MESH,
    )


def backward_kernel(
    branch, notes_all, kept_in, w_out_in, activated_in, w_down_in, middle_in, both_sum, down_sum,
    out, result, branch_all, both_in, down_all,
    totals, query_part, key_value, ending, leaving, arriving, send, recv,
    part, from_side, from_corner, from_near, send_r, recv_r,
    mixed_grad, shard, load_sem, send_g, recv_g,
    both_stage, send_u, recv_u, local, down_found, send_d, recv_d,
    kept, w_out, activated, w_down, middle, fetch_sem, down_stage, send_v, recv_v, local_v,
    *, scale, groups, rows,
):
    z = lax.axis_index("mp")
    members = lax.axis_size("mp")
    barrier = greet_all()
    pairs = ((activated_in, activated), (w_out_in, w_out), (kept_in, kept), (middle_in, middle))
    pairs += ((w_down_in, w_down),)
    fetches = [
        pltpu.make_async_copy(source, target, fetch_sem.at[number])
        for number, (source, target) in enumerate(pairs)
    ]

    def down_rows(owner):
        return down_sum.at[pl.ds(pl.multiple_of(owner * LANES, LANES), LANES)]

    down_units = Units(down_rows, down_found, down_stage, send_v, recv_v, local_v)
    load_down = pltpu.make_async_copy(down_rows(z), down_found.at[z], load_sem.at[2])
    pl.semaphore_wait(barrier, 13)
    units = Units(lambda owner: both_sum.at[owner], both_in, both_stage, send_u, recv_u, local)
    gather = Gather(branch, branch_all, send_g, recv_g, local.at[2])
    gather.start()
    down_units.start()
    units.start()
    start_all(fetches)
    load_down.start()
    wait_all((fetches[0], fetches[4]))
    reduce = Reduce(activated, w_down, False, part, from_side, from_corner, from_near, send_r, recv_r)
    reduce.products()
    down_units.add()
    down = Gather(down_found.at[0], down_all, send_d, recv_d, local.at[1])

    def load_shard(turn):
        slot = turn % 2
        return pltpu.make_async_copy(branch_all.at[owner_at(turn)], shard.at[slot], load_sem.at[slot])

    def spread_back(turn, carry):
        for number, numbers in ARRIVALS:
            pl.when(turn == number)(functools.partial(gather.arrive, *numbers))

        @pl.when(turn == 0)
        def _():
            gather.keep.wait()

        load_shard(turn).start()
        load_shard(turn).wait()
        mixed_grad[owner_at(turn)] = (
            lax.dot_general(shard[turn % 2], w_out[...], NT, preferred_element_type=F32)
            .astype(BF16)
            .reshape(groups, rows // groups, 256)
        )
        return carry

    fetches[1].wait()
    lax.fori_loop(0, 4, spread_back, 0)
    reduce.launch()
    lax.fori_loop(4, 8, spread_back, 0)
    units.add()


    def halo(k, other):
        return to_mp(leaving.at[k], arriving.at[k], send.at[k], recv.at[k], other)

    def attend(k, carry):
        hot = hot_of(notes_all, k, rows)
        given = mixed_grad[:, pl.ds(k, 1)].reshape(rows, 256)
        grad_ordered = lax.dot_general(hot, given, TN, preferred_element_type=F32).astype(BF16)
        totals[...] = jnp.zeros_like(totals)
        pairs = [(block, head) for block in range(rows // 128) for head in range(2)]
        masks = [block_mask(notes_all, k, block, z, rows) for block in range(rows // 128)]

        def query_of(block, head):
            return kept[k, pl.ds(64 + block * 128, 128), pl.ds(head * 128, 128)]

        def keys_of(block, head):
            return kept[k, pl.ds(block * 128, 192), pl.ds(256 + head * 128, 128)]

        def grad_of(block, head):
            return grad_ordered[block * 128 : block * 128 + 128, head * 128 : head * 128 + 128]

        scores, chance_grads = [], []
        for block, head in pairs:
            value = lax.dot_general(
                query_of(block, head), keys_of(block, head), NT, preferred_element_type=F32
            )
            scores.append(jnp.where(masks[block], value * scale, -MASKED))
            values = kept[k, pl.ds(block * 128, 192), pl.ds(512 + head * 128, 128)]
            chance_grads.append(
                lax.dot_general(grad_of(block, head), values, NT, preferred_element_type=F32)
            )
        agains, score_grads = [], []
        for value, chance_grad in zip(scores, chance_grads):
            weights = jnp.exp(value - jnp.max(value, axis=-1, keepdims=True))
            again = weights / jnp.sum(weights, axis=-1, keepdims=True)
            row_dot = jnp.sum(again * chance_grad, axis=-1, keepdims=True)
            agains.append(again.astype(BF16))
            score_grads.append((again * (chance_grad - row_dot)).astype(BF16))
        for (block, head), again, score_grad in zip(pairs, agains, score_grads):
            query_part[k, pl.ds(block * 128, 128), pl.ds(head * 128, 128)] = (
                jnp.dot(score_grad, keys_of(block, head), preferred_element_type=F32) * scale
            ).astype(BF16)
            totals[pl.ds(block * 128, 192), pl.ds(head * 128, 128)] += (
                lax.dot_general(score_grad, query_of(block, head), TN, preferred_element_type=F32)
                * scale
            )
            totals[pl.ds(block * 128, 192), pl.ds(256 + head * 128, 128)] += lax.dot_general(
                again, grad_of(block, head), TN, preferred_element_type=F32
            )
        key_value[k] = totals[pl.ds(64, rows), :].astype(BF16)
        ending[k] = totals[pl.ds(rows, 64), :]

        @pl.when(z > 0)
        def _():
            leaving[k] = totals[pl.ds(0, 64), :].astype(BF16)
            halo(k, z - 1).start()

        return carry

    wait_all(fetches[2:4])
    lax.fori_loop(0, 3, attend, 0)
    reduce.middle()
    load_down.wait()
    down_units.finish()

    @pl.when((z == 0) | (z == members - 1))
    def _():
        down_found[members - 1 - z] = jnp.zeros_like(down_found[0])

    def add_down(span):
        value = down_found[0, span, :].astype(F32) + down_found[1, span, :].astype(F32)
        value = value + down_found[2, span, :].astype(F32) + down_found[3, span, :].astype(F32)
        down_found[0, span, :] = value.astype(BF16)

    each_chunk(down_found.shape[1], add_down)
    down.start()
    lax.fori_loop(3, groups, attend, 0)
    down.pass_on()

    def restore(k, carry):
        @pl.when(z < members - 1)
        def _():
            halo(k, z).wait_recv()
            key_value[k, pl.ds(rows - 64, 64), :] = (
                ending[k] + arriving[k].astype(F32)
            ).astype(BF16)

        hot = hot_of(notes_all, k, rows)
        ordered = jnp.concatenate([query_part[k], key_value[k]], axis=1)
        back = jnp.dot(hot, ordered, preferred_element_type=F32).astype(BF16)
        out[:, pl.ds(k, 1)] = back.reshape(groups, 1, rows // groups, 768)
        return carry

    lax.fori_loop(0, groups, restore, 0)
    reduce.end()

    def body(span):
        result[span, :] = (middle[span, :] + reduce.rows_of(span)).astype(BF16)

    each_chunk(rows, body)
    down.finish()
    units.finish()
    for copy in gather.copies:
        copy.wait_send()
    reduce.finish()

    @pl.when(z > 0)
    def _():
        def done(k, carry):
            halo(k, z - 1).wait_send()
            return carry

        lax.fori_loop(0, groups, done, 0)


def attend_back(
    branch, notes_all, kept, w_out, activated, w_down, middle, both_sum, down_sum, scale
):
    groups = kept.shape[0]
    rows, width = middle.shape
    members = both_sum.shape[0]
    dma = pltpu.SemaphoreType.DMA
    shape = jax.ShapeDtypeStruct
    return pl.pallas_call(
        functools.partial(backward_kernel, scale=scale, groups=groups, rows=rows),
        out_shape=(
            shape((groups, groups, rows // groups, 768), BF16),
            shape((rows, width), BF16),
            shape((groups, rows, width), BF16),
            shape((members, width, 256), BF16),
            shape((groups, LANES, width), BF16),
        ),
        in_specs=[on_chip()] * 2 + [anywhere()] * 7,
        out_specs=(on_chip(),) * 2 + (anywhere(),) * 3,
        scratch_shapes=[
            pltpu.VMEM((rows + 64, 512), F32),
            pltpu.VMEM((groups, rows, 256), BF16),
            pltpu.VMEM((groups, rows, 512), BF16),
            pltpu.VMEM((groups, 64, 512), F32),
            pltpu.VMEM((groups, 64, 512), BF16),
            pltpu.VMEM((groups, 64, 512), BF16),
            dma((groups,)),
            dma((groups,)),
        ]
        + reduce_scratch(rows, width)
        + [
            pltpu.VMEM((groups, groups, rows // groups, 256), BF16),
            pltpu.VMEM((2, rows, width), BF16),
            dma((3,)),
            dma((13,)),
            dma((13,)),
            pltpu.VMEM((2, width, 256), BF16),
            dma((6,)),
            dma((10,)),
            dma((3,)),
            pltpu.VMEM((members, LANES, width), BF16),
            dma((13,)),
            dma((13,)),
            pltpu.VMEM(kept.shape, BF16),
            pltpu.VMEM(w_out.shape, BF16),
            pltpu.VMEM(activated.shape, BF16),
            pltpu.VMEM((members * LANES, width), BF16),
            pltpu.VMEM((rows, width), F32),
            dma((5,)),
            pltpu.VMEM((2, LANES, width), BF16),
            dma((6,)),
            dma((10,)),
            dma((1,)),
        ],
        compiler_params=remote_params(3, 63 * 1024 * 1024),
        cost_estimate=pl.CostEstimate(flops=0, bytes_accessed=300_000_000, transcendentals=0),
        name="attend_back",
    )(branch, notes_all, kept, w_out, activated, w_down, middle, both_sum, down_sum)


def norm_back_rows(gradient, values, gain, sums, span):
    inverse = lax.rsqrt(mean_rows(values * values) + EPSILON)
    normed = values * inverse
    product = gradient * normed
    folded = product[0:8]
    for step in range(1, CHUNK // 8):
        folded = folded + product[step * 8 : step * 8 + 8]
    sums[...] += folded
    scaled = gradient * gain
    return inverse * (scaled - normed * mean_rows(scaled * normed))


def feed_kernel(
    mixed, w_out, tokens, cotangent_all, gate_all, w_up, down_weight, cotangent_own, gain,
    middle, middle_grad, branch, sums, activated_out, both_sum, down_out, up_all, down_all,
    hidden_all, both_grad, part, from_side, from_corner, from_near, send_r, recv_r,
    send_m, recv_m, send_n, recv_n, send_a, recv_a, send_b, recv_b, cot_shard, cot_tile, stage_both, down_sum, w_both, w_down,
    cotangent, activated, load_sem, local,
    up_own, down_own, send_u, recv_u, send_d, recv_d, first_sem,
):
    groups, rows, width = hidden_all.shape
    members = gate_all.shape[0]
    me = lax.axis_index("dp")
    barrier = greet_all()
    units_own = pl.ds(pl.multiple_of(me * LANES, LANES), LANES)
    first = start_all(
        [
            pltpu.make_async_copy(source, target, first_sem.at[number])
            for number, (source, target) in enumerate(
                (
                    (mixed, activated.at[:, :, pl.ds(0, 256)]),
                    (w_out, down_sum.at[pl.ds(0, 256)]),
                    (w_up.at[:, units_own], up_own),
                    (down_weight.at[units_own], down_own),
                    (tokens, cotangent),
                )
            )
        ]
    )
    gates = start_all(
        [
            pltpu.make_async_copy(
                gate_all.at[z], w_both.at[:, pl.ds(z * 256, 128)], load_sem.at[6 + z]
            )
            for z in range(members)
        ]
    )

    def slot_of(turn):
        block = turn // 2
        near = ((block + 1) // 2) % 2
        far = block // 3
        second = turn % 2
        other = (1 - near) * second + (block // 2) * near
        return 4 * other + 3 * (1 - near) * (1 - far) + near * (1 + second)

    def load_cotangent(turn):
        return pltpu.make_async_copy(
            cotangent_all.at[owner_at(turn)], cot_shard.at[turn % 2], load_sem.at[turn % 2]
        )

    load_cotangent(0).start()
    wait_all(first)
    pl.semaphore_wait(barrier, 13)
    columns_up = Column(up_own, up_all, send_u, recv_u, local.at[0])
    columns_down = Column(down_own, down_all, send_d, recv_d, local.at[2])
    columns_up.start()
    columns_down.start()
    half_rows = rows // 2

    def half(number, sends, recvs):
        span = pl.ds(number * half_rows, half_rows)
        quarter = pl.ds(number * (half_rows // 2), half_rows // 2)
        return Reduce(
            lambda owner: activated[owner, span, 0:256], down_sum.at[pl.ds(0, 256)], False,
            part.at[:, span], from_side.at[:, span], from_corner.at[:, quarter],
            from_near.at[:, span], sends, recvs,
        )

    projects = (half(0, send_m, recv_m), half(1, send_n, recv_n))
    gathers = [
        Gather(None, hidden_all.at[:, pl.ds(number * half_rows, half_rows)], sends, recvs)
        for number, (sends, recvs) in enumerate(((send_a, recv_a), (send_b, recv_b)))
    ]
    for project in projects:
        project.begin()
    for project in projects:
        project.middle()
    columns_up.pass_on()
    columns_down.pass_on()
    for number, project in enumerate(projects):
        project.end()

        def normalise(span):
            own = pl.ds(pl.multiple_of(number * half_rows + span.start, CHUNK), CHUNK)
            values = cotangent[own, :].astype(F32) + project.rows_of(span)
            middle_grad[own, :] = values
            inverse = lax.rsqrt(mean_rows(values * values) + EPSILON)
            hidden_all[me, own, :] = (values * inverse * gain[...].reshape(1, -1)).astype(BF16)

        each_chunk(half_rows, normalise)
        gathers[number].start()

    for project in projects:
        project.finish()
    store_middle = pltpu.make_async_copy(middle_grad, middle, local.at[1])
    load_own = pltpu.make_async_copy(cotangent_own, cotangent, local.at[3])
    store_middle.start()
    load_own.start()
    columns_up.finish()
    columns_down.finish()
    ups = start_all(
        [
            pltpu.make_async_copy(
                up_all.at[z], w_both.at[:, pl.ds(z * 256 + 128, 128)], load_sem.at[10 + z]
            )
            for z in range(members)
        ]
    )
    ups += start_all(
        [
            pltpu.make_async_copy(
                down_all.at[z], w_down.at[pl.ds(z * LANES, LANES)], load_sem.at[14 + z]
            )
            for z in range(members)
        ]
    )
    reduce = Reduce(None, None, False, part, from_side, from_corner, from_near, send_r, recv_r)
    reduce.prepare()

    def nears():
        reduce.add_side(1)
        reduce.nears[0].start()
        reduce.add_side(2)
        reduce.nears[2].start()

    early = [
        (turn, functools.partial(gather.arrive, *numbers))
        for turn, numbers in ARRIVALS
        for gather in gathers
    ]
    early += [(6, nears)]
    late = [(1, 3), (4, 1), (5, 2), (7, 0)]
    wait_all(gates + ups)

    def unit(turn, carry):
        for number, action in early:
            pl.when(turn == number)(action)

        @pl.when(turn < 7)
        def _():
            load_cotangent(turn + 1).start()

        load_cotangent(turn).wait()
        owner, slot = owner_at(turn), slot_of(turn)
        mine = hidden_all[owner]
        grads = cot_shard[turn % 2]
        for z in range(members):
            raw = jnp.dot(mine, w_both[:, z * 256 : z * 256 + 256], preferred_element_type=F32)
            units = pl.ds(z * 128, 128)
            if z % 2 == 0:
                pair = lax.dot_general(
                    grads, w_down[pl.ds(z * 128, 256), :], NT, preferred_element_type=F32
                )
            active_grad = pair[:, 128 * (z % 2) : 128 * (z % 2) + 128]
            gate, upward = raw[:, :128], raw[:, 128:]
            sigmoid = jax.nn.sigmoid(gate)
            activated[owner, :, units] = (gate * sigmoid * upward).astype(BF16)
            both_grad[owner, :, pl.ds(z * 256, 128)] = (
                active_grad * upward * sigmoid * (1.0 + gate * (1.0 - sigmoid))
            ).astype(BF16)
            both_grad[owner, :, pl.ds(z * 256 + 128, 128)] = (
                active_grad * gate * sigmoid
            ).astype(BF16)

        def tile(t, inner):
            columns = pl.ds(pl.multiple_of(t * 256, 256), 256)
            part[slot, :, columns] = lax.dot_general(
                both_grad[owner], w_both[columns, :], NT, preferred_element_type=F32
            ).astype(BF16)
            return inner

        lax.fori_loop(0, width // 256, tile, 0)
        for number, share in late:
            pl.when(turn == number)(reduce.shares[share].start)
        return carry

    lax.fori_loop(0, 8, unit, 0)
    store_activated = pltpu.make_async_copy(activated, activated_out, local.at[4])
    store_activated.start()

    def load_tile(t):
        columns = pl.ds(pl.multiple_of(t * 256, 256), 256)
        return pltpu.make_async_copy(
            cotangent_all.at[:, :, columns], cot_tile.at[t % 2], load_sem.at[2 + t % 2]
        )

    def store_both(t):
        columns = pl.ds(pl.multiple_of(t * 256, 256), 256)
        return pltpu.make_async_copy(
            stage_both.at[t % 2], both_sum.at[:, columns], load_sem.at[4 + t % 2]
        )

    tiles = width // 256
    count = groups * rows

    def down_tile(t, carry):
        columns = pl.ds(pl.multiple_of(t * 256, 256), 256)

        @pl.when(t < tiles - 1)
        def _():
            load_tile(t + 1).start()

        load_tile(t).wait()
        down_sum[:, columns] = lax.dot_general(
            activated[...].reshape(count, members * 128),
            cot_tile[t % 2].reshape(count, 256),
            TN,
            preferred_element_type=F32,
        ).astype(BF16)
        return carry

    store_down = pltpu.make_async_copy(down_sum, down_out, local.at[5])

    def weight_tile(t, carry):
        columns = pl.ds(pl.multiple_of(t * 256, 256), 256)

        @pl.when(t >= 2)
        def _():
            store_both(t - 2).wait()

        value = lax.dot_general(
            hidden_all[:, :, columns].reshape(count, 256),
            both_grad[...].reshape(count, members * 256),
            TN,
            preferred_element_type=F32,
        )
        for z in range(members):
            stage_both[t % 2, z] = value[:, z * 256 : z * 256 + 256].astype(BF16)
        store_both(t).start()
        return carry

    load_tile(0).start()
    reduce.add_side(0)
    reduce.corners[0].start()
    reduce.corners[1].start()
    lax.fori_loop(0, tiles, down_tile, 0)
    store_down.start()
    lax.fori_loop(0, 2, weight_tile, 0)
    reduce.middle()
    lax.fori_loop(2, tiles, weight_tile, 0)
    reduce.end()
    store_middle.wait()
    load_own.wait()
    sums[...] = jnp.zeros_like(sums)

    def body(span):
        change = norm_back_rows(reduce.rows_of(span), middle_grad[span, :], gain[...].reshape(1, -1), sums, span)
        total = cotangent[span, :].astype(F32) + change
        middle_grad[span, :] = total
        branch[span, :] = total.astype(BF16)

    each_chunk(rows, body)
    for gather in gathers:
        gather.sent()
    reduce.finish()
    for t in (tiles - 2, tiles - 1):
        store_both(t).wait()
    store_down.wait()
    store_activated.wait()


def feed(mixed, w_out, tokens, cotangent_all, gate_all, w_up, w_down, cotangent, gain):
    groups, rows, width = cotangent_all.shape
    members = gate_all.shape[0]
    dma = pltpu.SemaphoreType.DMA
    units = members * 128
    return pl.pallas_call(
        feed_kernel,
        out_shape=(
            jax.ShapeDtypeStruct((rows, width), F32),
            jax.ShapeDtypeStruct((rows, width), F32),
            jax.ShapeDtypeStruct((rows, width), BF16),
            jax.ShapeDtypeStruct((8, width), F32),
            jax.ShapeDtypeStruct((groups, rows, units), BF16),
            jax.ShapeDtypeStruct((members, width, 256), BF16),
            jax.ShapeDtypeStruct((units, width), BF16),
            jax.ShapeDtypeStruct((members, width, LANES), BF16),
            jax.ShapeDtypeStruct((members, LANES, width), BF16),
        ),
        in_specs=[anywhere()] * 8 + [on_chip()],
        out_specs=(anywhere(),) + (on_chip(),) * 3 + (anywhere(),) * 5,
        scratch_shapes=[
            pltpu.VMEM((groups, rows, width), BF16),
            pltpu.VMEM((groups, rows, 2 * units), BF16),
        ]
        + reduce_scratch(rows, width)
        + [
            dma((10,)),
            dma((10,)),
            dma((10,)),
            dma((10,)),
            dma((13,)),
            dma((13,)),
            dma((13,)),
            dma((13,)),
            pltpu.VMEM((2, rows, width), BF16),
            pltpu.VMEM((2, groups, rows, 256), BF16),
            pltpu.VMEM((2, members, 256, 256), BF16),
            pltpu.VMEM((units, width), BF16),
            pltpu.VMEM((width, 2 * units), BF16),
            pltpu.VMEM((units, width), BF16),
            pltpu.VMEM((rows, width), BF16),
            pltpu.VMEM((groups, rows, units), BF16),
            dma((6 + 4 * members,)),
            dma((6,)),
            pltpu.VMEM((width, LANES), BF16),
            pltpu.VMEM((LANES, width), BF16),
            dma((4,)),
            dma((4,)),
            dma((4,)),
            dma((4,)),
            dma((5,)),
        ],
        compiler_params=remote_params(5, 63 * 1024 * 1024),
        cost_estimate=pl.CostEstimate(flops=0, bytes_accessed=400_000_000, transcendentals=0),
        name="feed",
    )(mixed, w_out, tokens, cotangent_all, gate_all, w_up, w_down, cotangent, gain)


def input_kernel(
    qkv_in, w_in, hidden_all, branch_all, mixed_in, tokens_in, middle_in, gain, sums_two,
    both_sum, both_in,
    result, gains, both_all, heads_all,
    part, from_side, from_corner, from_near, send, recv, sums,
    stage, arrive, send_h, recv_s, recv_h, own, plane_sums, column_sums, send_p, recv_p,
    weight_sum, row_tile, tile_sem, send_b, recv_b, send_t, recv_t, both_found, heads_own, local,
    mixed, tokens, middle_grad, fetch_sem, qkv_grad, w_qkv,
):
    me, z = lax.axis_index("dp"), lax.axis_index("mp")
    barrier = greet_all()
    count = qkv_grad.shape[0]
    tiles = tokens.shape[1] // 256
    outer = (z == 0) | (z == 3)

    def columns_of(t):
        return pl.ds(pl.multiple_of(lax.rem(t, tiles) * 256, 256), 256)

    def load(t, source):
        return pltpu.make_async_copy(
            source.at[:, :, columns_of(t)], row_tile.at[t % 2], tile_sem.at[t % 2]
        )

    own_part = pltpu.make_async_copy(both_sum.at[z], both_found.at[0], local.at[0])
    own_part.start()
    ways = [(outer, 1, 1), (outer, 2, 2)]
    ways += [(z == 1, 0, 1), (z == 1, 2, 2), (z == 1, 3, 3)]
    ways += [(z == 2, 0, 1), (z == 2, 1, 2), (z == 2, 3, 3)]

    def came(source, place):
        return pltpu.make_async_copy(both_in.at[source], both_found.at[place], local.at[place])

    for here, source, place in ways:
        pl.when(here)(came(source, place).start)

    @pl.when(outer)
    def _():
        both_found[3] = jnp.zeros_like(both_found[3])

    load(0, hidden_all).start()
    fetches = start_all(
        [
            pltpu.make_async_copy(source, target, fetch_sem.at[number])
            for number, (source, target) in enumerate(
                (
                    (qkv_in, qkv_grad),
                    (w_in, w_qkv),
                    (mixed_in, mixed),
                    (tokens_in, tokens),
                    (middle_in, middle_grad),
                )
            )
        ]
    )
    pl.semaphore_wait(barrier, 13)
    both = Gather(both_found.at[0], both_all, send_b, recv_b, local.at[4])

    def weight_tile(t, carry):
        @pl.when(t < tiles - 1)
        def _():
            load(t + 1, hidden_all).start()

        @pl.when((t >= tiles - 1) & (t < 2 * tiles - 1))
        def _():
            load(t + 1, branch_all).start()

        load(t, hidden_all).wait()

        @pl.when(t < tiles)
        def _():
            weight_sum[pl.ds(0, 768), columns_of(t)] = lax.dot_general(
                qkv_grad[...], row_tile[t % 2].reshape(count, 256), TN, preferred_element_type=F32
            ).astype(BF16)

        @pl.when(t >= tiles)
        def _():
            weight_sum[pl.ds(768, 256), columns_of(t)] = lax.dot_general(
                mixed[...], row_tile[t % 2].reshape(count, 256), TN, preferred_element_type=F32
            ).astype(BF16)

        return carry

    heads = Heads(weight_sum, stage, arrive, send_h, recv_s, recv_h)
    reduce = Reduce(qkv_grad, w_qkv, False, part, from_side, from_corner, from_near, send, recv)
    own_part.wait()
    for here, source, place in ways:
        pl.when(here)(came(source, place).wait)

    def add(span):
        value = both_found[0, span, :].astype(F32) + both_found[1, span, :].astype(F32)
        value = value + both_found[2, span, :].astype(F32) + both_found[3, span, :].astype(F32)
        both_found[0, span, :] = value.astype(BF16)

    each_chunk(both_found.shape[1], add)
    both.start()
    wait_all(fetches[:2])
    lax.fori_loop(0, tiles, weight_tile, 0)
    heads.start((0, 1, 2))
    wait_all(fetches[2:])
    lax.fori_loop(tiles, 2 * tiles, weight_tile, 0)
    heads.start((3,))
    both.pass_on()
    reduce.begin()
    heads.add((0, 1))
    reduce.middle()
    heads.add((2, 3))
    reduce.end()
    sums[...] = jnp.zeros_like(sums)

    def body(span):
        values = tokens[span, :].astype(F32)
        change = norm_back_rows(reduce.rows_of(span), values, gain[...].reshape(1, -1), sums, span)
        result[span, :] = (middle_grad[span, :] + change).astype(BF16)

    each_chunk(result.shape[0], body)
    own[...] = jnp.concatenate(
        [
            jnp.sum(sums[...], axis=0, keepdims=True),
            jnp.sum(sums_two[...], axis=0, keepdims=True),
        ],
        axis=0,
    )
    swaps = swap_all(own, plane_sums, send_p, recv_p)
    for copy in swaps:
        copy.start()
    plane_sums[me] = own[...]
    heads.total(heads_own)
    gather = Gather(heads_own, heads_all, send_t, recv_t, local.at[5])
    gather.start()
    for copy in swaps:
        copy.wait()
    found = plane_sums[0]
    for other in range(1, 8):
        found = found + plane_sums[other]
    column_sums[z] = found
    passes = [
        to_mp(
            column_sums.at[z],
            column_sums.at[z],
            send_p.at[6 + step],
            recv_p.at[6 + step],
            lax.rem(z + step, 4),
        )
        for step in range(1, 4)
    ]
    for copy in passes:
        copy.start()
    both.finish()
    for copy in passes:
        copy.wait()
    gains[...] = (column_sums[0] + column_sums[1]) + (column_sums[2] + column_sums[3])
    gather.pass_on()
    heads.finish_send()
    reduce.finish()
    gather.finish()


def project_input(
    qkv_grad, w_qkv, hidden_all, branch_all, mixed, tokens, middle_grad, gain, sums_two,
    both_sum, both_in,
):
    rows, width = tokens.shape
    groups = hidden_all.shape[0]
    dma = pltpu.SemaphoreType.DMA
    shape = jax.ShapeDtypeStruct
    return pl.pallas_call(
        input_kernel,
        out_shape=(
            shape((rows, width), BF16),
            shape((2, width), F32),
            shape((groups, width, 256), BF16),
            shape((groups, 4 * HEAD_DIM, width // 2), BF16),
        ),
        in_specs=[anywhere()] * 7 + [on_chip()] * 2 + [anywhere()] * 2,
        out_specs=(on_chip(),) * 2 + (anywhere(),) * 2,
        scratch_shapes=reduce_scratch(rows, width)
        + [
            pltpu.VMEM((8, width), F32),
            pltpu.VMEM((2, 4, HEAD_DIM, width), BF16),
            pltpu.VMEM((3, 4, HEAD_DIM, width // 2), BF16),
            dma((16,)),
            dma((8,)),
            dma((12,)),
            pltpu.VMEM((2, width), F32),
            pltpu.VMEM((8, 2, width), F32),
            pltpu.VMEM((4, 2, width), F32),
            dma((10,)),
            dma((10,)),
            pltpu.VMEM((8 * LANES, width), BF16),
            pltpu.VMEM((2, groups, rows, 256), BF16),
            dma((2,)),
            dma((13,)),
            dma((13,)),
            dma((13,)),
            dma((13,)),
            pltpu.VMEM((4, width, 256), BF16),
            pltpu.VMEM((4 * HEAD_DIM, width // 2), BF16),
            dma((6,)),
            pltpu.VMEM(mixed.shape, BF16),
            pltpu.VMEM((rows, width), BF16),
            pltpu.VMEM((rows, width), F32),
            dma((5,)),
            pltpu.VMEM(qkv_grad.shape, BF16),
            pltpu.VMEM(w_qkv.shape, BF16),
        ],
        compiler_params=remote_params(6, 63 * 1024 * 1024),
        cost_estimate=pl.CostEstimate(flops=0, bytes_accessed=250_000_000, transcendentals=0),
        name="project_input",
    )(
        qkv_grad, w_qkv, hidden_all, branch_all, mixed, tokens, middle_grad, gain, sums_two,
        both_sum, both_in,
    )


def assemble_kernel(
    both, down, heads, order_row, output_b, input_b, gains,
    gain_one, gain_two, output, inputs, query, keys, values, project, gate, upward, down_out, *, tiles,
):
    for d in range(both.shape[0]):
        gate[:, d * 128 : d * 128 + 128] = both[d, :, :128].astype(F32)
        upward[:, d * 128 : d * 128 + 128] = both[d, :, 128:].astype(F32)
    down_out[...] = down[0].astype(F32)
    for kind, out in enumerate((query, keys, values, project)):
        out[...] = heads[0, kind].astype(F32)
    rows = output_b.shape[0]
    gain_one[...] = gains[0:1, :].reshape(-1)
    gain_two[...] = gains[1:2, :].reshape(-1)

    @pl.when(pl.program_id(0) < tiles)
    def _():
        place = lax.broadcasted_iota(jnp.int32, (rows, rows), 0).astype(F32)
        sort = (place == order_row[...].reshape(1, -1)).astype(BF16)
        for ordered, out in ((output_b, output), (input_b, inputs)):
            out[...] = lax.dot_general(
                sort, ordered[...], TN, preferred_element_type=F32
            ).astype(BF16)


def assemble(both, down, heads, order_row, output_b, input_b, gains):
    groups, width, wide = both.shape
    rows = output_b.shape[0]
    units = down.shape[1]
    chips = groups // 2
    columns = heads.shape[3]
    tile = width // groups
    shape = jax.ShapeDtypeStruct
    head = shape((chips * HEAD_DIM, 2 * columns), F32)
    head_spec = pl.BlockSpec((HEAD_DIM, columns), lambda i: (i // 2, i % 2))
    wide_spec = pl.BlockSpec((tile, groups * units), lambda i: (i, 0))
    tiles = width // 256
    row_spec = pl.BlockSpec((rows, 256), lambda i: (0, jnp.minimum(i, tiles - 1)))
    return pl.pallas_call(
        functools.partial(assemble_kernel, tiles=tiles),
        grid=(groups,),
        out_shape=(
            shape((width,), F32),
            shape((width,), F32),
            shape((rows, width), BF16),
            shape((rows, width), BF16),
            head,
            head,
            head,
            head,
            shape((width, groups * units), F32),
            shape((width, groups * units), F32),
            shape((groups * units, width), F32),
        ),
        in_specs=[
            pl.BlockSpec((groups, tile, wide), lambda i: (0, i, 0)),
            pl.BlockSpec((1, units, width), lambda i: (i, 0, 0)),
            pl.BlockSpec((1, 4, HEAD_DIM, columns), lambda i: (i, 0, 0, 0)),
            pl.BlockSpec((rows,), lambda i: (0,)),
            row_spec,
            row_spec,
            pl.BlockSpec((2, width), lambda i: (0, 0)),
        ],
        out_specs=(
            pl.BlockSpec((width,), lambda i: (0,)),
            pl.BlockSpec((width,), lambda i: (0,)),
            row_spec, row_spec, head_spec, head_spec, head_spec, head_spec, wide_spec, wide_spec,
            pl.BlockSpec((units, width), lambda i: (i, 0)),
        ),
        compiler_params=pltpu.CompilerParams(vmem_limit_bytes=VMEM_LIMIT),
        cost_estimate=pl.CostEstimate(flops=0, bytes_accessed=58_000_000, transcendentals=0),
        name="assemble",
    )(both, down, heads, order_row, output_b, input_b, gains)


def swapped(
    tokens, cotangent, route, lengths, key_mask, norm1_gain, norm2_gain,
    w_query, w_key, w_value, w_out, w_gate, w_up, w_down,
):
    groups = lax.axis_size("dp")
    members = lax.axis_size("mp")
    me = lax.axis_index("dp")
    z = lax.axis_index("mp")
    rows, width = tokens.shape
    bucket = rows // groups
    units = w_down.shape[0] // groups

    target = route // TOK_DEV
    earlier = jnp.arange(rows, dtype=jnp.int32)
    same = (target[:, None] == target[None, :]) & (earlier[None, :] < earlier[:, None])
    send_at = target * bucket + jnp.sum(same.astype(jnp.int32), axis=1)
    sorting = send_at[None, :] == earlier[:, None]
    slots_own = jnp.sum(jnp.where(sorting, (route % rows)[None, :], 0), axis=1)

    mask_window = lax.dynamic_slice_in_dim(
        jnp.concatenate([jnp.zeros((WINDOW,), jnp.int32), key_mask]), z * rows, rows + WINDOW
    )
    slot_rows = jnp.pad(slots_own.reshape(groups, bucket).T, ((0, 0), (0, LANES - groups)))
    mask_rows = jnp.pad(mask_window, (0, 4 * LANES - rows - WINDOW)).reshape(4, LANES)
    length_rows = jnp.pad(lengths, ((0, 3), (0, LANES - lengths.shape[1])))
    notes = jnp.concatenate([slot_rows, mask_rows, length_rows], axis=0).astype(F32)

    count = groups * rows
    scale = HEAD_DIM ** (-0.5)
    order_row = send_at.astype(F32)
    (
        hidden_one,
        w_qkv,
        w_proj,
        notes_all,
        gate_all,
        mixed,
        kept,
        tokens_b,
        cotangent_b,
        cotangent_all,
    ) = attend_ahead(
        tokens,
        cotangent,
        order_row,
        norm1_gain,
        notes,
        w_query.T,
        w_key.T,
        w_value.T,
        w_out,
        w_gate,
        scale,
    )
    mixed = mixed.reshape(count, 2 * LANES)
    middle, middle_grad, branch, sums_two, activated, both_sum, down_sum, _, down_all = feed(
        mixed.reshape(groups, rows, 2 * LANES),
        w_proj,
        tokens_b,
        cotangent_all,
        gate_all,
        w_up,
        w_down,
        cotangent_b,
        norm2_gain,
    )
    qkv_grad, output_rows, branch_all, both_in, down_whole = attend_back(
        branch,
        notes_all,
        kept,
        w_proj,
        activated.reshape(count, units * members),
        down_all.reshape(members * units, width),
        middle,
        both_sum,
        down_sum,
        scale,
    )
    qkv_grad = qkv_grad.reshape(count, 6 * LANES)
    input_rows, gain_sums, both_whole, heads_whole = project_input(
        qkv_grad,
        w_qkv,
        hidden_one,
        branch_all,
        mixed,
        tokens_b,
        middle_grad,
        norm1_gain,
        sums_two,
        both_sum,
        both_in,
    )
    (
        gain_one_grad,
        gain_two_grad,
        output,
        input_grad,
        query_grad,
        key_grad,
        value_grad,
        proj_grad,
        gate_grad,
        up_grad,
        down_grad,
    ) = assemble(
        both_whole,
        down_whole,
        heads_whole.reshape(groups, 4, HEAD_DIM, width // 2),
        order_row,
        output_rows,
        input_rows,
        gain_sums,
    )
    return (
        output,
        input_grad,
        gain_one_grad,
        gain_two_grad,
        query_grad.T,
        key_grad.T,
        value_grad.T,
        proj_grad,
        gate_grad,
        up_grad,
        down_grad,
    )


def solution(mesh):
    in_specs = (
        P(("dp", "mp"), None),
        P(("dp", "mp"), None),
        P(("dp", "mp")),
        P("dp", None),
        P("dp"),
        P(),
        P(),
        P(None, "mp"),
        P(None, "mp"),
        P(None, "mp"),
        P("mp", None),
        P(None, "mp"),
        P(None, "mp"),
        P("mp", None),
    )
    out_specs = (
        P(("dp", "mp"), None),
        P(("dp", "mp"), None),
        P(),
        P(),
        P(None, "mp"),
        P(None, "mp"),
        P(None, "mp"),
        P("mp", None),
        P(None, "mp"),
        P(None, "mp"),
        P("mp", None),
    )
    body = swapped if (mesh.shape["dp"], mesh.shape["mp"]) == (8, 4) else local
    return jax.shard_map(body, mesh=mesh, in_specs=in_specs, out_specs=out_specs, check_vma=False)
```
